32 devices in a mesh: dp: 8 (over y, x, core), mp: 4 (over z).
Axes of the slice: x: 2, y: 2, z: 4, core: 2. Of those that a mesh axis runs over, the one named last changes fastest.
Arguments:
- tokens_in: bfloat16 [16384, 768], P(('dp', 'mp')), may hold values from -5 to 5
- timesteps: int32 [8], replicated, may hold values from 0 to 999
- lengths: int32 [8], replicated, may hold values from 512 to 2048, as said below
- time_table: bfloat16 [1000, 768], replicated, may hold values from -0.8984375 to 0.8984375
- norm_gains: float32 [2, 768], replicated, may hold values from 0.5 to 1.5
- norm_biases: float32 [2, 768], replicated, may hold values from -0.6 to 0.6
- w_qkv: bfloat16 [3, 768, 768], P(None, 'dp', 'mp'), may hold values from -0.3125 to 0.3125
- qv_bias: float32 [2, 768], replicated, may hold values from -0.42 to 0.42
- w_out: bfloat16 [768, 768], P('mp', 'dp'), may hold values from -0.21875 to 0.21875
- out_bias: float32 [768], replicated, may hold values from -0.6 to 0.6
- w_up: bfloat16 [768, 3072], P('dp', 'mp'), may hold values from -0.21875 to 0.21875
- up_bias: float32 [3072], replicated, may hold values from -0.8 to 0
- w_down: bfloat16 [3072, 768], P('mp', 'dp'), may hold values from -0.109375 to 0.109375
- down_bias: float32 [768], replicated, may hold values from -0.6 to 0.6
- cotangent: bfloat16 [16384, 768], P(('dp', 'mp')), may hold values from -50 to 50
- teacher: bfloat16 [16384, 768], P(('dp', 'mp')), may hold values from -5 to 5
Outputs:
- output: bfloat16 [16384, 768], P(('dp', 'mp'))
- input_grad: float32 [16384, 768], P(('dp', 'mp'))
- table_grad: float32 [1000, 768], replicated
- norm_gain_grad: float32 [2, 768], replicated
- norm_bias_grad: float32 [2, 768], replicated
- w_qkv_grad: float32 [3, 768, 768], P(None, 'dp', 'mp')
- qv_bias_grad: float32 [2, 768], replicated
- w_out_grad: float32 [768, 768], P('mp', 'dp')
- out_bias_grad: float32 [768], replicated
- w_up_grad: float32 [768, 3072], P('dp', 'mp')
- up_bias_grad: float32 [3072], replicated
- w_down_grad: float32 [3072, 768], P('mp', 'dp')
- down_bias_grad: float32 [768], replicated
The draws below stay inside these ranges and needn't reach their ends.
Inputs may be any that keep to these rules, and one draw needn't show every extreme that they name: Sequence s holds its valid tokens in its first lengths[s] slots and padding after them; some sequence fills all 2048 slots.
All inputs are finite; a program needn't handle non-finite values.
Results may differ from the reference program's by a relative error of at most 0.0095.
The reference program's roundings to bfloat16 on the way count: a program that leaves them out, or rounds other values in their place, can miss the bound.
Values may be sent and summed in bfloat16 or wider, within the bound.
No kernel may reach another device: no remote copies, remote signals or barrier semaphores. Data moves between devices by JAX's collectives and lax.ppermute only.
A program may use at most 128 MiB of HBM per device.

```python
from functools import partial
import jax
import jax.numpy as jnp
from jax import lax

D = 768
HEADS = 12
HEAD_DIM = 64
FF = 3072
NT = 1000
MAXLEN = 2048
SEQS = 8
TOKENS = 16384


def draw_lengths(key, part):
    first_key, second_key = jax.random.split(jax.random.fold_in(key, 11))
    drawn_values = jax.random.randint(first_key, (SEQS,), MAXLEN // 4, MAXLEN + 1)
    chosen_seq = jax.random.randint(second_key, (), 0, SEQS)
    return jnp.where(jnp.arange(SEQS) == chosen_seq, MAXLEN, drawn_values).astype(jnp.int32)


def state_rows(key):
    base_key = jax.random.fold_in(key, 0)
    base = jnp.clip(jax.random.normal(base_key, (TOKENS, D), jnp.float32), -5.0, 5.0)
    return base.astype(jnp.bfloat16)


def draw_tokens_in(key, part):
    return state_rows(jax.random.fold_in(key, 31))


def draw_teacher(key, part):
    return state_rows(jax.random.fold_in(key, 47))


def draw_cotangent(key, part):
    base_key, scale_key, pair_key = jax.random.split(jax.random.fold_in(key, 23), 3)
    base = jnp.clip(jax.random.normal(base_key, (TOKENS, D), jnp.float32), -4.0, 4.0)
    row_scale = jnp.exp(jax.random.uniform(scale_key, (TOKENS, 1), jnp.float32) * jnp.log(5.0))
    block_width = max(D // SEQS, 1)
    paired = jax.random.permutation(pair_key, SEQS)
    row_seq = jnp.arange(TOKENS) // MAXLEN
    col_block = jnp.arange(D) // block_width
    marked = paired[row_seq][:, None] == col_block[None, :]
    factor = jnp.where(marked, 2.5, 1.0)
    return (base * row_scale * factor).astype(jnp.bfloat16)


def place_ends(result, rng, smallest, high):
    longest = result.shape.index(max(result.shape))
    spots = []
    for shift in (0, 1):
        where = [jax.random.randint(jax.random.fold_in(rng, axis), (), 0, length) for axis, length in enumerate(result.shape)]
        where[longest] = (where[longest] + shift) % result.shape[longest]
        spots.append(tuple(where))
    return result.at[spots[0]].set(smallest).at[spots[1]].set(high)


def block_scale(stream_key, shape, pieces, least, top_value):
    def one(axis_at, parts):
        heights = jax.random.uniform(jax.random.fold_in(jax.random.fold_in(stream_key, 6), axis_at), (parts,), jnp.float32, least / len(pieces), top_value / len(pieces))
        return jnp.repeat(jnp.exp(heights), shape[axis_at] // parts).reshape((-1,) + (1,) * (len(shape) - axis_at - 1))

    level = one(*pieces[0])
    for cut in pieces[1:]:
        level = level * one(*cut)
    return level


def scatter_about(own_key, extent, scale, bound, pieces=(), dtype=jnp.bfloat16):
    loudness = block_scale(own_key, extent, pieces, -0.22, 0.18) if pieces else 1.0
    result = jax.random.normal(own_key, extent, jnp.float32) * scale * loudness
    return jnp.minimum(jnp.maximum(result, -bound), bound).astype(dtype)


def setup_inputs(seed: int = 0) -> dict:
    streams_of = jax.random.split(jax.random.key(seed), 17)
    return {
        "tokens_in": draw_tokens_in(jax.random.fold_in(streams_of[16], 71), 0),
        "timesteps": place_ends(jax.random.randint(streams_of[1], (SEQS,), 0, NT), jax.random.fold_in(streams_of[1], 1), 0, NT - 1).astype(jnp.int32),
        "lengths": draw_lengths(jax.random.fold_in(streams_of[16], 71), 0),
        "time_table": scatter_about(streams_of[3], (NT, D), 0.15, 0.8984375),
        "norm_gains": jnp.clip(1.0 + 0.1 * jax.random.normal(streams_of[4], (2, D), jnp.float32), 0.5, 1.5),
        "norm_biases": scatter_about(streams_of[5], (2, D), 0.1, 0.6, (), jnp.float32),
        "w_qkv": scatter_about(streams_of[6], (3, D, D), (D * 2 // 5) ** -0.5, 0.3125, ((1, 8), (2, 4))),
        "qv_bias": scatter_about(streams_of[7], (2, D), 0.07, 0.42, (), jnp.float32),
        "w_out": scatter_about(streams_of[8], (D, D), D ** -0.5, 0.21875, ((0, 4), (1, 8))),
        "out_bias": scatter_about(streams_of[9], (D,), 0.1, 0.6, (), jnp.float32),
        "w_up": scatter_about(streams_of[10], (D, FF), D ** -0.5, 0.21875, ((0, 8), (1, 4))),
        "up_bias": jnp.clip(jax.random.uniform(streams_of[11], (FF,), jnp.float32, -0.8, 0.0), -0.8, 0.0),
        "w_down": scatter_about(streams_of[12], (FF, D), FF ** -0.5, 0.109375, ((0, 4), (1, 8))),
        "down_bias": scatter_about(streams_of[13], (D,), 0.1, 0.6, (), jnp.float32),
        "cotangent": draw_cotangent(jax.random.fold_in(streams_of[16], 71), 0),
        "teacher": draw_teacher(jax.random.fold_in(streams_of[16], 71), 0),
    }


far_below = -1e+30
epsilon = 1e-05
highest = lax.Precision.HIGHEST

@jax.custom_vjp
def low(v):
    return lax.optimization_barrier(v.astype(jnp.bfloat16)).astype(jnp.float32)

@jax.custom_vjp
def low_back(v):
    return v

def low_keep(v):
    return (low(v), None)

def low_pass(kept, grad):
    return (grad,)

def back_keep(v):
    return (v, None)

def back_low(kept, grad):
    return (low(grad),)
low.defvjp(low_keep, low_pass)
low_back.defvjp(back_keep, back_low)

def norm_rows(values, gain_row, shift_row):
    center = values - lax.optimization_barrier(jnp.mean(values, axis=-1, keepdims=True))
    spread = lax.optimization_barrier(jnp.mean(center * center, axis=-1, keepdims=True))
    return center * lax.rsqrt(spread + epsilon) * gain_row + shift_row

def attend_sequence(inputs):
    queries, keys_seq, values_seq, length = inputs
    score_scale = HEAD_DIM ** (-0.5)
    scores = jnp.einsum('qhd,khd->hqk', queries, keys_seq, precision=highest) * score_scale
    scores = low_back(scores)
    key_kept = jnp.arange(MAXLEN) < length
    scores = jnp.where(key_kept[None, None, :], scores, far_below)
    prob_rows = jax.nn.softmax(scores, axis=-1)
    return jnp.einsum('hqk,khd->qhd', low(prob_rows), values_seq, precision=highest)

def block_forward(start_in, time_table, norm_gains, norm_biases, w_qkv, qv_bias, w_out, out_bias, w_up, up_bias, w_down, down_bias, timesteps=None, lengths=None):
    row_seq = jnp.arange(TOKENS) // MAXLEN
    start_state = start_in + time_table[timesteps[row_seq]]
    first_norm = low(norm_rows(start_state, norm_gains[0], norm_biases[0]))
    bias_stack = jnp.stack([qv_bias[0], jnp.zeros((D,), jnp.float32), qv_bias[1]])
    projected = jnp.einsum('td,cde->cte', first_norm, w_qkv, precision=highest) + bias_stack[:, None, :]
    projected = low(low_back(projected))
    heads_all = projected.reshape(3, SEQS, MAXLEN, HEADS, HEAD_DIM)
    attended = lax.map(jax.checkpoint(attend_sequence), (heads_all[0], heads_all[1], heads_all[2], lengths))
    attended = low(low_back(attended.reshape(TOKENS, D)))
    attn_sum = low_back(jnp.dot(attended, w_out, precision=highest))
    middle_state = start_state + attn_sum + out_bias
    second_norm = low(norm_rows(middle_state, norm_gains[1], norm_biases[1]))
    hidden_pre = low_back(jnp.dot(second_norm, w_up, precision=highest) + up_bias)
    hidden_act = low(jax.nn.gelu(hidden_pre, approximate=False))
    ffn_sum = low_back(jnp.dot(hidden_act, w_down, precision=highest))
    return middle_state + ffn_sum + down_bias

def reference(tokens_in, timesteps, lengths, time_table, norm_gains, norm_biases, w_qkv, qv_bias, w_out, out_bias, w_up, up_bias, w_down, down_bias, cotangent, teacher):
    forward = partial(block_forward, timesteps=timesteps, lengths=lengths)
    final_state, backward = jax.vjp(forward, tokens_in.astype(jnp.float32), time_table.astype(jnp.float32), norm_gains, norm_biases, w_qkv.astype(jnp.float32), qv_bias, w_out.astype(jnp.float32), out_bias, w_up.astype(jnp.float32), up_bias, w_down.astype(jnp.float32), down_bias)
    row_index = jnp.arange(TOKENS)
    row_valid = row_index % MAXLEN < lengths[row_index // MAXLEN]
    loss_weight = TOKENS / jnp.sum(lengths).astype(jnp.float32)
    final_grad = jnp.where(row_valid[:, None], cotangent.astype(jnp.float32) + loss_weight * (final_state - teacher.astype(jnp.float32)), 0.0)
    gradients = backward(final_grad)
    return (final_state.astype(jnp.bfloat16), gradients[0], gradients[1], gradients[2], gradients[3], gradients[4], gradients[5], gradients[6], gradients[7], gradients[8], gradients[9], gradients[10], gradients[11])
```

```python
import functools

import jax
import jax.numpy as jnp
from jax import lax
from jax.experimental import pallas as pl
from jax.experimental.pallas import tpu as pltpu
from jax.sharding import PartitionSpec as P

D = 768
HEADS = 12
HEAD_DIM = 64
FF = 3072
MAXLEN = 2048
PAIR = 2 * HEAD_DIM
PAIRS = HEADS // 2
KEY_BLOCK = 512

far_below = -1e30
epsilon = 1e-05
score_scale = HEAD_DIM ** (-0.5)
low = jnp.bfloat16
full = jnp.float32
both = ("dp", "mp")


def norm_stats(values):
    center = values - jnp.mean(values, axis=-1, keepdims=True)
    spread = jnp.mean(center * center, axis=-1, keepdims=True)
    inverse = lax.rsqrt(spread + epsilon)
    return center * inverse, inverse


def norm_back(unit, inverse, gain_row, grad):
    scaled = grad * gain_row
    mean_scaled = jnp.mean(scaled, axis=-1, keepdims=True)
    mean_unit = jnp.mean(scaled * unit, axis=-1, keepdims=True)
    return (
        inverse * (scaled - mean_scaled - unit * mean_unit),
        jnp.sum(grad * unit, axis=0),
        jnp.sum(grad, axis=0),
    )


def dot_of(left_side, right_side, left_dim, right_dim):
    return lax.dot_general(
        left_side,
        right_side,
        (((left_dim,), (right_dim,)), ((), ())),
        preferred_element_type=full,
    )


def first_half(shape):
    return lax.broadcasted_iota(jnp.int32, shape, len(shape) - 1) < HEAD_DIM


def forward_kernel(length_ref, q_ref, k_ref, v_ref, out_ref, log_ref):
    rows = q_ref.shape[0]
    keys = k_ref.shape[0]
    length = length_ref[0]
    bias = jnp.where(
        lax.broadcasted_iota(jnp.int32, (1, keys), 1) < length, 0.0, far_below
    )
    q_pair = q_ref[...]
    k_pair = k_ref[...]
    v_pair = v_ref[...]
    lower = first_half((rows, PAIR))
    mixed = []
    logs = []
    for half in range(2):
        kept = lower if half == 0 else jnp.logical_not(lower)
        q_half = jnp.where(kept, q_pair, jnp.zeros_like(q_pair))
        scores = dot_of(q_half, k_pair, 1, 1) + bias
        highest = jnp.max(scores, axis=-1, keepdims=True)
        exp_scores = jnp.exp(scores - highest)
        totals = jnp.sum(exp_scores, axis=-1, keepdims=True)
        mixed.append(dot_of(exp_scores.astype(low), v_pair, 1, 0) / totals)
        logs.append(highest + jnp.log(totals))
    out_ref[...] = jnp.where(lower, mixed[0], mixed[1])
    lane = lax.broadcasted_iota(jnp.int32, (rows, PAIR), 1)
    log_ref[...] = jnp.where(lower, logs[0], logs[1])


def attend_forward(queries, keys, values, length):
    rows, total = queries.shape[0], keys.shape[0]
    pair_rows = lambda count: pl.BlockSpec((count, PAIR), lambda i, n: (0, i))
    return pl.pallas_call(
        forward_kernel,
        out_shape=(
            jax.ShapeDtypeStruct((rows, D), full),
            jax.ShapeDtypeStruct((rows, D), full),
        ),
        grid_spec=pltpu.PrefetchScalarGridSpec(
            num_scalar_prefetch=1,
            grid=(PAIRS,),
            in_specs=[pair_rows(rows), pair_rows(total), pair_rows(total)],
            out_specs=[pair_rows(rows), pair_rows(rows)],
        ),
        compiler_params=pltpu.CompilerParams(vmem_limit_bytes=56 << 20),
        cost_estimate=pl.CostEstimate(
            flops=4 * rows * total * D * 4,
            bytes_accessed=12 * total * D,
            transcendentals=rows * total * HEADS,
        ),
        name="attend_forward",
    )(length, queries, keys, values)


def backward_kernel(
    length_ref, q_ref, k_ref, v_ref, g_ref, log_ref, delta_ref, dq_ref, dk_ref, dv_ref
):
    rows = q_ref.shape[0]
    keys = k_ref.shape[0]
    length = length_ref[0]
    q_pair = q_ref[...]
    g_pair = g_ref[...]
    lower = first_half((rows, PAIR))
    lower_keys = first_half((KEY_BLOCK, PAIR))
    dq = [jnp.zeros((rows, PAIR), full), jnp.zeros((rows, PAIR), full)]
    for block in range(keys // KEY_BLOCK):
        span = slice(block * KEY_BLOCK, (block + 1) * KEY_BLOCK)
        k_pair = k_ref[span, :]
        v_pair = v_ref[span, :]
        place = block * KEY_BLOCK + lax.broadcasted_iota(
            jnp.int32, (KEY_BLOCK, 1), 0
        )
        bias = jnp.where(place < length, 0.0, far_below)
        dk = []
        dv = []
        for half in range(2):
            kept = lower if half == 0 else jnp.logical_not(lower)
            q_half = jnp.where(kept, q_pair, jnp.zeros_like(q_pair))
            g_half = jnp.where(kept, g_pair, jnp.zeros_like(g_pair))
            log_row = log_ref[0, half : half + 1, :]
            delta_row = delta_ref[0, half : half + 1, :]
            scores = dot_of(k_pair, q_half, 1, 1) + bias
            probs = jnp.exp(scores - log_row)
            dv.append(dot_of(probs.astype(low), g_pair, 1, 0))
            prob_grad = dot_of(v_pair, g_half, 1, 1)
            score_grad = (probs * (prob_grad - delta_row)).astype(low)
            dk.append(dot_of(score_grad, q_pair, 1, 0))
            dq[half] = dq[half] + dot_of(score_grad, k_pair, 0, 0)
        dk_ref[span, :] = jnp.where(lower_keys, dk[0], dk[1]).astype(low)
        dv_ref[span, :] = jnp.where(lower_keys, dv[0], dv[1]).astype(low)
    dq_ref[...] = (jnp.where(lower, dq[0], dq[1]) * score_scale).astype(low)


def attend_backward(queries, keys, values, grads, logs, deltas, length):
    rows, total = queries.shape[0], keys.shape[0]
    pair_rows = lambda count: pl.BlockSpec((count, PAIR), lambda i, n: (0, i))
    stats = pl.BlockSpec((1, 2, rows), lambda i, n: (i, 0, 0))
    return pl.pallas_call(
        backward_kernel,
        out_shape=(
            jax.ShapeDtypeStruct((rows, D), low),
            jax.ShapeDtypeStruct((total, D), low),
            jax.ShapeDtypeStruct((total, D), low),
        ),
        grid_spec=pltpu.PrefetchScalarGridSpec(
            num_scalar_prefetch=1,
            grid=(PAIRS,),
            in_specs=[
                pair_rows(rows),
                pair_rows(total),
                pair_rows(total),
                pair_rows(rows),
                stats,
                stats,
            ],
            out_specs=[pair_rows(rows), pair_rows(total), pair_rows(total)],
        ),
        compiler_params=pltpu.CompilerParams(vmem_limit_bytes=56 << 20),
        cost_estimate=pl.CostEstimate(
            flops=10 * rows * total * D * 4,
            bytes_accessed=16 * total * D,
            transcendentals=rows * total * HEADS,
        ),
        name="attend_backward",
    )(length, queries, keys, values, grads, logs, deltas)


def shards(
    tokens_in,
    timesteps,
    lengths,
    time_table,
    norm_gains,
    norm_biases,
    w_qkv,
    qv_bias,
    w_out,
    out_bias,
    w_up,
    up_bias,
    w_down,
    down_bias,
    cotangent,
    teacher,
):
    model_rank = lax.axis_index("mp")
    data_rank = lax.axis_index("dp")
    mp = lax.axis_size("mp")
    dp = lax.axis_size("dp")
    own_rows = tokens_in.shape[0]
    length = lax.dynamic_slice_in_dim(lengths, data_rank, 1)
    own_time = lax.dynamic_slice_in_dim(timesteps, data_rank, 1)
    position = model_rank * own_rows + jnp.arange(own_rows)
    row_valid = position < length[0]
    table_row = lax.dynamic_slice_in_dim(time_table, own_time[0], 1)
    start_state = tokens_in.astype(full) + table_row.astype(full)

    gather_all = functools.partial(lax.all_gather, axis_name=("mp", "dp"), axis=0, tiled=True)
    qkv_weight = lax.all_gather(w_qkv, "mp", axis=2, tiled=True)
    qkv_weight = lax.all_gather(qkv_weight, "dp", axis=1, tiled=True)
    up_weight = gather_all(w_up).reshape(mp, D, -1)
    down_weight = gather_all(w_down.T).reshape(mp, D, -1)
    out_weight = lax.all_gather(w_out, "dp", axis=1, tiled=True)
    out_weight = lax.all_gather(out_weight, "mp", axis=0, tiled=True)

    unit_one, inverse_one = norm_stats(start_state)
    first_norm = (unit_one * norm_gains[0] + norm_biases[0]).astype(low)
    first_all = lax.all_gather(first_norm, "mp", axis=0, tiled=True)

    queries = ((dot_of(first_norm, qkv_weight[0], 1, 0) + qv_bias[0]).astype(low) * score_scale).astype(low)
    keys = dot_of(first_all, qkv_weight[1], 1, 0).astype(low)
    values = (dot_of(first_all, qkv_weight[2], 1, 0) + qv_bias[1]).astype(low)
    mixed, logs = attend_forward(queries, keys, values, length)
    attended = mixed.astype(low)

    middle_state = start_state + dot_of(attended, out_weight, 1, 0) + out_bias
    unit_two, inverse_two = norm_stats(middle_state)
    second_norm = (unit_two * norm_gains[1] + norm_biases[1]).astype(low)
    hidden_pre = jnp.einsum(
        "td,mdf->mtf", second_norm, up_weight, preferred_element_type=full
    ) + up_bias.reshape(mp, 1, -1)
    error = lax.erf(hidden_pre * (0.5**0.5))
    cumulative = 0.5 * (1.0 + error)
    hidden_act = (hidden_pre * cumulative).astype(low)
    act_slope = cumulative + hidden_pre * jnp.exp(-0.5 * hidden_pre * hidden_pre) * (
        (2.0 * jnp.pi) ** -0.5
    )
    final_state = (
        middle_state
        + jnp.einsum("mtf,mdf->td", hidden_act, down_weight, preferred_element_type=full)
        + down_bias
    )
    output = final_state.astype(low)
    loss_weight = lengths.shape[0] * MAXLEN / jnp.sum(lengths).astype(full)
    final_grad = jnp.where(
        row_valid[:, None],
        cotangent.astype(full) + loss_weight * (final_state - teacher.astype(full)),
        0.0,
    )
    final_low = final_grad.astype(low)
    down_part = jnp.einsum(
        "td,mtf->mdf", final_low, hidden_act, preferred_element_type=full
    )
    act_grad = jnp.einsum("td,mdf->mtf", final_low, down_weight, preferred_element_type=full)
    pre_grad = (act_slope * act_grad).astype(low)
    up_part = jnp.einsum("td,mtf->mdf", second_norm, pre_grad, preferred_element_type=full)
    up_bias_part = jnp.sum(pre_grad, axis=1, dtype=full).reshape(FF)
    second_grad = jnp.einsum("mtf,mdf->td", pre_grad, up_weight, preferred_element_type=full)
    middle_part, gain_two, shift_two = norm_back(
        unit_two, inverse_two, norm_gains[1], second_grad
    )
    middle_grad = final_grad + middle_part
    middle_low = middle_grad.astype(low)
    out_part = dot_of(middle_low, attended, 0, 0)
    attended_grad = dot_of(middle_low, out_weight, 1, 1).astype(low)

    scatter_all = functools.partial(
        lax.psum_scatter, axis_name=("mp", "dp"), scatter_dimension=0, tiled=True
    )
    down_grad = scatter_all(down_part.astype(low).reshape(mp * D, -1)).astype(full).T
    up_grad = scatter_all(up_part.astype(low).reshape(mp * D, -1)).astype(full)

    deltas = jnp.sum(
        (attended_grad.astype(full) * mixed).reshape(own_rows, HEADS, HEAD_DIM), axis=-1
    )
    deltas = deltas.T.reshape(PAIRS, 2, own_rows)
    logs = logs.reshape(own_rows, HEADS, HEAD_DIM)[:, :, 0].T.reshape(PAIRS, 2, own_rows)
    query_grad, key_grad, value_grad = attend_backward(
        queries, keys, values, attended_grad, logs, deltas, length
    )
    first_part = dot_of(key_grad, qkv_weight[1], 1, 1) + dot_of(value_grad, qkv_weight[2], 1, 1)
    first_query = dot_of(query_grad, qkv_weight[0], 1, 1)
    first_grad = first_query + lax.psum_scatter(
        first_part.astype(low), "mp", scatter_dimension=0, tiled=True
    ).astype(full)
    qkv_part = jnp.stack(
        [
            dot_of(first_norm, query_grad, 0, 0),
            dot_of(first_all, key_grad, 0, 0),
            dot_of(first_all, value_grad, 0, 0),
        ]
    ).astype(low)
    qv_bias_part = jnp.stack(
        [jnp.sum(query_grad, axis=0, dtype=full), jnp.sum(value_grad, axis=0, dtype=full)]
    )
    qkv_grad = lax.psum_scatter(qkv_part, "mp", scatter_dimension=2, tiled=True)
    qkv_grad = lax.psum_scatter(qkv_grad, "dp", scatter_dimension=1, tiled=True).astype(full)
    out_grad = lax.psum_scatter(out_part.T.astype(low), "mp", scatter_dimension=0, tiled=True)
    out_grad = lax.psum_scatter(out_grad, "dp", scatter_dimension=1, tiled=True).astype(full)

    start_part, gain_one, shift_one = norm_back(
        unit_one, inverse_one, norm_gains[0], first_grad
    )
    input_grad = middle_grad + start_part
    sequence_sum = jnp.sum(input_grad, axis=0)
    own_slot = (jnp.arange(dp) == data_rank).astype(full)
    packed = jnp.concatenate(
        [
            jnp.stack([gain_one, gain_two, shift_one, shift_two]),
            qv_bias_part,
            jnp.stack([jnp.sum(middle_grad, axis=0), jnp.sum(final_grad, axis=0)]),
            up_bias_part.reshape(-1, D),
            own_slot[:, None] * sequence_sum[None, :],
        ]
    )
    total = lax.psum(packed, both)
    fixed = 8 + FF // D
    chosen = (timesteps[None, :] == jnp.arange(time_table.shape[0])[:, None]).astype(full)
    table_grad = lax.dot_general(
        chosen,
        total[fixed:],
        (((1,), (0,)), ((), ())),
        precision=lax.Precision.HIGHEST,
        preferred_element_type=full,
    )
    return (
        output,
        input_grad,
        table_grad,
        total[0:2],
        total[2:4],
        qkv_grad,
        total[4:6],
        out_grad,
        total[6],
        up_grad,
        total[8:fixed].reshape(FF),
        down_grad,
        total[7],
    )


def solution(mesh):
    rows = P(both, None)
    placed = (
        rows,
        P(),
        P(),
        P(),
        P(),
        P(),
        P(None, "dp", "mp"),
        P(),
        P("mp", "dp"),
        P(),
        P("dp", "mp"),
        P(),
        P("mp", "dp"),
        P(),
        rows,
        rows,
    )
    return jax.shard_map(
        shards,
        mesh=mesh,
        in_specs=placed,
        out_specs=(
            rows,
            rows,
            P(),
            P(),
            P(),
            P(None, "dp", "mp"),
            P(),
            P("mp", "dp"),
            P(),
            P("dp", "mp"),
            P(),
            P("mp", "dp"),
            P(),
        ),
        check_vma=False,
    )
```

```python
import functools

import jax
import jax.numpy as jnp
from jax import lax
from jax.experimental import pallas as pl
from jax.experimental.pallas import tpu as pltpu
from jax.sharding import PartitionSpec as P

D = 768
HEADS = 12
HEAD_DIM = 64
FF = 3072
MAXLEN = 2048
PAIR = 2 * HEAD_DIM
PAIRS = HEADS // 2
KEY_BLOCK = 512

far_below = -1e30
epsilon = 1e-05
score_scale = HEAD_DIM ** (-0.5)
low = jnp.bfloat16
full = jnp.float32
both = ("dp", "mp")


def norm_stats(values):
    center = values - jnp.mean(values, axis=-1, keepdims=True)
    spread = jnp.mean(center * center, axis=-1, keepdims=True)
    inverse = lax.rsqrt(spread + epsilon)
    return center * inverse, inverse


def norm_back(unit, inverse, gain_row, grad):
    scaled = grad * gain_row
    mean_scaled = jnp.mean(scaled, axis=-1, keepdims=True)
    mean_unit = jnp.mean(scaled * unit, axis=-1, keepdims=True)
    return (
        inverse * (scaled - mean_scaled - unit * mean_unit),
        jnp.sum(grad * unit, axis=0),
        jnp.sum(grad, axis=0),
    )


def dot_of(left_side, right_side, left_dim, right_dim):
    return lax.dot_general(
        left_side,
        right_side,
        (((left_dim,), (right_dim,)), ((), ())),
        preferred_element_type=full,
    )


def first_half(shape):
    return lax.broadcasted_iota(jnp.int32, shape, len(shape) - 1) < HEAD_DIM


def forward_kernel(
    first, last, scalars, q_ref, k_ref, v_ref, *refs
):
    if first:
        outs = refs
    else:
        top_in, sum_in, acc_in = refs[:3]
        outs = refs[3:]
    rows = q_ref.shape[0]
    keys = k_ref.shape[0]
    limit = scalars[1] - scalars[0] * keys
    place = lax.broadcasted_iota(jnp.int32, (1, keys), 1)
    bias = jnp.where(place < limit, 0.0, far_below)
    q_pair = q_ref[...]
    k_pair = k_ref[...]
    v_pair = v_ref[...]
    lower = first_half((rows, PAIR))
    parts = []
    for half in range(2):
        kept = lower if half == 0 else jnp.logical_not(lower)
        lane = half * HEAD_DIM
        q_half = jnp.where(kept, q_pair, jnp.zeros_like(q_pair))
        scores = dot_of(q_half, k_pair, 1, 1) + bias
        highest = jnp.max(scores, axis=-1, keepdims=True)
        if first:
            highest = jnp.maximum(highest, far_below)
            exp_scores = jnp.exp(scores - highest)
            totals = jnp.sum(exp_scores, axis=-1, keepdims=True)
            mixed = dot_of(exp_scores.astype(low), v_pair, 1, 0)
        else:
            before = top_in[:, lane : lane + 1]
            highest = jnp.maximum(highest, before)
            shrink = jnp.exp(before - highest)
            exp_scores = jnp.exp(scores - highest)
            totals = sum_in[:, lane : lane + 1] * shrink + jnp.sum(
                exp_scores, axis=-1, keepdims=True
            )
            mixed = acc_in[...] * shrink + dot_of(exp_scores.astype(low), v_pair, 1, 0)
        parts.append((highest, totals, mixed))
    top = jnp.where(lower, parts[0][0], parts[1][0])
    total = jnp.where(lower, parts[0][1], parts[1][1])
    mixed = jnp.where(lower, parts[0][2], parts[1][2])
    if last:
        out_ref, log_ref = outs
        out_ref[...] = mixed / total
        log_ref[...] = top + jnp.log(total)
    else:
        top_ref, sum_ref, acc_ref = outs
        top_ref[...] = top
        sum_ref[...] = total
        acc_ref[...] = mixed


def attend_forward(queries, keys, values, scalars, state, last):
    rows, total = queries.shape[0], keys.shape[0]
    first = state is None
    pair_rows = lambda count: pl.BlockSpec((count, PAIR), lambda i, n: (0, i))
    wide = jax.ShapeDtypeStruct((rows, D), full)
    carried = () if first else state
    return pl.pallas_call(
        functools.partial(forward_kernel, first, last),
        out_shape=(wide,) * (2 if last else 3),
        grid_spec=pltpu.PrefetchScalarGridSpec(
            num_scalar_prefetch=1,
            grid=(PAIRS,),
            in_specs=[pair_rows(rows), pair_rows(total), pair_rows(total)]
            + [pair_rows(rows)] * len(carried),
            out_specs=[pair_rows(rows)] * (2 if last else 3),
        ),
        compiler_params=pltpu.CompilerParams(vmem_limit_bytes=40 << 20),
        cost_estimate=pl.CostEstimate(
            flops=4 * rows * total * D * 4,
            bytes_accessed=12 * total * D,
            transcendentals=rows * total * HEADS,
        ),
        name="attend_forward",
    )(scalars, queries, keys, values, *carried)


def backward_kernel(
    first, last, scalars, q_ref, k_ref, v_ref, g_ref, log_ref, delta_ref, *refs
):
    if first:
        dq_ref, dk_ref, dv_ref = refs
    else:
        dq_in, dq_ref, dk_ref, dv_ref = refs
    rows = q_ref.shape[0]
    keys = k_ref.shape[0]
    limit = scalars[1] - scalars[0] * keys
    q_pair = q_ref[...]
    g_pair = g_ref[...]
    k_pair = k_ref[...]
    v_pair = v_ref[...]
    lower = first_half((rows, PAIR))
    lower_keys = first_half((keys, PAIR))
    place = lax.broadcasted_iota(jnp.int32, (keys, 1), 0)
    bias = jnp.where(place < limit, 0.0, far_below)
    dq = []
    dk = []
    dv = []
    for half in range(2):
        kept = lower if half == 0 else jnp.logical_not(lower)
        q_half = jnp.where(kept, q_pair, jnp.zeros_like(q_pair))
        g_half = jnp.where(kept, g_pair, jnp.zeros_like(g_pair))
        log_row = log_ref[0, half : half + 1, :]
        delta_row = delta_ref[0, half : half + 1, :]
        scores = dot_of(k_pair, q_half, 1, 1) + bias
        probs = jnp.exp(scores - log_row)
        dv.append(dot_of(probs.astype(low), g_pair, 1, 0))
        prob_grad = dot_of(v_pair, g_half, 1, 1)
        score_grad = (probs * (prob_grad - delta_row)).astype(low)
        dk.append(dot_of(score_grad, q_pair, 1, 0))
        dq.append(dot_of(score_grad, k_pair, 0, 0))
    dk_ref[...] = jnp.where(lower_keys, dk[0], dk[1]).astype(low)
    dv_ref[...] = jnp.where(lower_keys, dv[0], dv[1]).astype(low)
    dq_all = jnp.where(lower, dq[0], dq[1])
    if not first:
        dq_all = dq_all + dq_in[...]
    if last:
        dq_ref[...] = (dq_all * score_scale).astype(low)
    else:
        dq_ref[...] = dq_all


def attend_backward(queries, keys, values, grads, logs, deltas, scalars, carried, last):
    rows, total = queries.shape[0], keys.shape[0]
    first = carried is None
    extra = () if first else (carried,)
    pair_rows = lambda count: pl.BlockSpec((count, PAIR), lambda i, n: (0, i))
    stats = pl.BlockSpec((1, 2, rows), lambda i, n: (i, 0, 0))
    return pl.pallas_call(
        functools.partial(backward_kernel, first, last),
        out_shape=(
            jax.ShapeDtypeStruct((rows, D), low if last else full),
            jax.ShapeDtypeStruct((total, D), low),
            jax.ShapeDtypeStruct((total, D), low),
        ),
        grid_spec=pltpu.PrefetchScalarGridSpec(
            num_scalar_prefetch=1,
            grid=(PAIRS,),
            in_specs=[
                pair_rows(rows),
                pair_rows(total),
                pair_rows(total),
                pair_rows(rows),
                stats,
                stats,
            ]
            + [pair_rows(rows)] * len(extra),
            out_specs=[pair_rows(rows), pair_rows(total), pair_rows(total)],
        ),
        compiler_params=pltpu.CompilerParams(vmem_limit_bytes=40 << 20),
        cost_estimate=pl.CostEstimate(
            flops=10 * rows * total * D * 4,
            bytes_accessed=16 * total * D,
            transcendentals=rows * total * HEADS,
        ),
        name="attend_backward",
    )(scalars, queries, keys, values, grads, logs, deltas, *extra)


def swap(value, axis, bit):
    count = lax.axis_size(axis)
    return lax.ppermute(value, axis, [(i, i ^ bit) for i in range(count)])


def outer_bits():
    bits = []
    bit = 2
    while bit < lax.axis_size("dp"):
        bits.append(bit)
        bit *= 2
    return bits


def gather_dp(parts):
    bits = outer_bits()
    half = len(bits) // 2
    orders = [bits[half * (n % 2) :] + bits[: half * (n % 2)] for n in range(len(parts))]
    held = [[([0], part)] for part in parts]
    for step in range(len(bits)):
        arrived = []
        for n in range(len(parts)):
            bit = orders[n][step]
            masks = [m for mask, _ in held[n] for m in mask]
            block = jnp.concatenate([array for _, array in held[n]]) if len(held[n]) > 1 else held[n][0][1]
            arrived.append([(masks, block), ([m ^ bit for m in masks], swap(block, "dp", bit))])
        held = arrived
    return [
        pieces + [([m ^ 1 for m in masks], swap(block, "dp", 1)) for masks, block in pieces]
        for pieces in held
    ]


def place_kernel(plan, *refs):
    count = len(plan)
    ins = refs[:count]
    outs = refs[count:-1]
    sems = refs[-1]
    me = lax.axis_index("dp")
    rank = lax.axis_index("mp")
    copies = []
    for ref, moves in zip(ins, plan):
        for start, size, which, mask, rank_mask, stride, offset in moves:
            row = (me ^ mask) * 96 + offset
            if stride:
                row = row + (rank ^ rank_mask) * stride
            copy = pltpu.make_async_copy(
                ref.at[pl.ds(start, size), :],
                outs[which].at[pl.ds(pl.multiple_of(row, 16), size), :],
                sems.at[len(copies)],
            )
            copy.start()
            copies.append(copy)
    for copy in copies:
        copy.wait()


def place(gathered, layouts, shapes):
    arrays = []
    plan = []
    for pieces, layout in zip(gathered, layouts):
        rows = sum(size for _, size, *_ in layout)
        for masks, array in pieces:
            moves = []
            for j, mask in enumerate(masks):
                for start, size, which, rank_mask, stride, offset in layout:
                    moves.append((j * rows + start, size, which, mask, rank_mask, stride, offset))
            arrays.append(array)
            plan.append(moves)
    moved = sum(array.size for array in arrays) * 4
    return pl.pallas_call(
        functools.partial(place_kernel, plan),
        out_shape=[jax.ShapeDtypeStruct(shape, low) for shape in shapes],
        in_specs=[pl.BlockSpec(memory_space=pl.ANY)] * len(arrays),
        out_specs=[pl.BlockSpec(memory_space=pl.ANY)] * len(shapes),
        scratch_shapes=[pltpu.SemaphoreType.DMA((sum(len(moves) for moves in plan),))],
        cost_estimate=pl.CostEstimate(flops=0, bytes_accessed=moved, transcendentals=0),
        name="place",
    )(*arrays)


def scatter_dp(values):
    bits = outer_bits()
    half = len(bits) // 2
    orders = [[1] + bits[half * (n % 2) :] + bits[: half * (n % 2)] for n in range(len(values))]
    me = lax.axis_index("dp")
    held = []
    for value in values:
        lead, dp = value.shape[0], value.shape[1]
        dims = (2,) * (len(bits) + 1)
        held.append(value.reshape((lead,) + dims + value.shape[2:]))
    axes = [list(reversed([1] + bits)) for _ in values]
    for step in range(len(bits) + 1):
        sends = []
        keeps = []
        for n, value in enumerate(held):
            bit = orders[n][step]
            axis = 1 + axes[n].index(bit)
            axes[n].remove(bit)
            mine = (me // bit) % 2
            keeps.append(lax.dynamic_index_in_dim(value, mine, axis, keepdims=False))
            sends.append(lax.dynamic_index_in_dim(value, 1 - mine, axis, keepdims=False))
        got = [swap(send.astype(low), "dp", orders[n][step]) for n, send in enumerate(sends)]
        held = [keep.astype(full) + other.astype(full) for keep, other in zip(keeps, got)]
        if step < len(bits):
            held = [value.astype(low) for value in held]
    return held


def scatter_mp(value):
    rank = lax.axis_index("mp")
    for bit in (2, 1):
        mine = (rank // bit) % 2
        pair = value.reshape((2, value.shape[0] // 2) + value.shape[1:])
        keep = lax.dynamic_index_in_dim(pair, mine, 0, keepdims=False)
        send = lax.dynamic_index_in_dim(pair, 1 - mine, 0, keepdims=False)
        value = keep.astype(full) + swap(send.astype(low), "mp", bit).astype(full)
    return value[0]


def shards(
    tokens_in,
    timesteps,
    lengths,
    time_table,
    norm_gains,
    norm_biases,
    w_qkv,
    qv_bias,
    w_out,
    out_bias,
    w_up,
    up_bias,
    w_down,
    down_bias,
    cotangent,
    teacher,
):
    rank = lax.axis_index("mp")
    data_rank = lax.axis_index("dp")
    mp = lax.axis_size("mp")
    dp = lax.axis_size("dp")
    own_rows = tokens_in.shape[0]
    length = lax.dynamic_index_in_dim(lengths, data_rank, keepdims=False)
    own_time = lax.dynamic_index_in_dim(timesteps, data_rank, keepdims=False)
    position = rank * own_rows + jnp.arange(own_rows)
    row_valid = position < length
    odd = rank % 2 == 1
    upper = rank >= 2
    middle = jnp.logical_or(rank == 1, rank == 2)

    block = w_qkv.shape[1]
    narrow = jnp.concatenate([w_qkv.reshape(3 * block, -1), w_out.T])
    other = swap(narrow, "mp", 1)
    pair = jnp.concatenate(
        [jnp.where(odd, other, narrow), jnp.where(odd, narrow, other)], axis=1
    )
    other = swap(pair, "mp", 2)
    wide = jnp.concatenate(
        [jnp.where(upper, other, pair), jnp.where(upper, pair, other)], axis=1
    )
    qkv_rows, out_rows = wide[: 3 * block], wide[3 * block :]
    aligned = block % 32 == 0
    if aligned:
        split = 3 * block // 2
        gathered = gather_dp([qkv_rows[:split], qkv_rows[split:]])
        (qkv_weight,) = place(
            gathered,
            [
                [(0, block, 0, 0, 0, 0), (block, split - block, 0, 0, 0, D)],
                [
                    (0, 2 * block - split, 0, 0, 0, D + split - block),
                    (2 * block - split, block, 0, 0, 0, 2 * D),
                ],
            ],
            [(3 * D, D)],
        )
        qkv_weight = qkv_weight.reshape(3, D, D)
    else:
        qkv_weight = lax.all_gather(
            qkv_rows.reshape(3, block, D), "dp", axis=1, tiled=True
        )

    table_row = lax.dynamic_slice_in_dim(time_table, own_time, 1)
    start_state = tokens_in.astype(full) + table_row.astype(full)
    unit_one, inverse_one = norm_stats(start_state)
    first_norm = (unit_one * norm_gains[0] + norm_biases[0]).astype(low)
    rightward = lambda value, pairs: lax.ppermute(value, "mp", pairs)
    from_left = rightward(first_norm, [(0, 1), (1, 2), (2, 3)])
    from_right = rightward(first_norm, [(1, 0), (2, 1), (3, 2)])
    near = jnp.where(rank == 0, from_right, from_left)
    second = jnp.where(
        upper,
        rightward(from_left, [(1, 2), (2, 3)]),
        rightward(from_right, [(1, 0), (2, 1)]),
    )
    last = jnp.where(middle, from_right, rightward(second, [(1, 0), (2, 3)]))
    chunks = [first_norm, near, second, last]
    indices = [
        rank,
        jnp.where(rank == 0, 1, rank - 1),
        jnp.where(upper, rank - 2, rank + 2),
        jnp.where(middle, rank + 1, 3 - rank),
    ]
    scalars = [jnp.stack([index, length]).astype(jnp.int32) for index in indices]

    if aligned:
        tall = jnp.concatenate([w_up, w_down.T])
        pair = jnp.concatenate([tall, swap(tall, "mp", 1)])
        other = swap(pair, "mp", 2)
        parts = [
            jnp.concatenate([pair, out_rows[: block // 2]]),
            jnp.concatenate([other, out_rows[block // 2 :]]),
        ]
        gathered = gather_dp(parts)
        layout = lambda masks, shift: [
            (0, block, 0, masks[0], D, 0),
            (block, block, 1, masks[0], D, 0),
            (2 * block, block, 0, masks[1], D, 0),
            (3 * block, block, 1, masks[1], D, 0),
            (4 * block, block // 2, 2, 0, 0, shift),
        ]
        up_weight, down_weight, out_weight = place(
            gathered,
            [layout((0, 1), 0), layout((2, 3), block // 2)],
            [(mp * D, D), (mp * D, D), (D, D)],
        )
    else:
        out_weight = lax.all_gather(out_rows, "dp", axis=0, tiled=True)
        up_weight = lax.all_gather(w_up, ("mp", "dp"), axis=0, tiled=True)
        down_weight = lax.all_gather(w_down.T, ("mp", "dp"), axis=0, tiled=True)
    up_weight = up_weight.reshape(mp, D, D)
    down_weight = down_weight.reshape(mp, D, D)

    queries = dot_of(first_norm, qkv_weight[0], 1, 0) + qv_bias[0]
    queries = (queries.astype(low) * score_scale).astype(low)
    keys = []
    values = []
    state = None
    for n, chunk in enumerate(chunks):
        keys.append(dot_of(chunk, qkv_weight[1], 1, 0).astype(low))
        values.append((dot_of(chunk, qkv_weight[2], 1, 0) + qv_bias[1]).astype(low))
        state = attend_forward(queries, keys[n], values[n], scalars[n], state, n == 3)
    mixed, logs = state
    attended = mixed.astype(low)

    middle_state = start_state + dot_of(attended, out_weight, 1, 1) + out_bias
    unit_two, inverse_two = norm_stats(middle_state)
    second_norm = (unit_two * norm_gains[1] + norm_biases[1]).astype(low)
    hidden_pre = jnp.einsum(
        "td,mdf->mtf", second_norm, up_weight, preferred_element_type=full
    ) + up_bias.reshape(mp, 1, -1)
    error = lax.erf(hidden_pre * (0.5**0.5))
    cumulative = 0.5 * (1.0 + error)
    hidden_act = (hidden_pre * cumulative).astype(low)
    act_slope = cumulative + hidden_pre * jnp.exp(-0.5 * hidden_pre * hidden_pre) * (
        (2.0 * jnp.pi) ** -0.5
    )
    final_state = (
        middle_state
        + jnp.einsum("mtf,mdf->td", hidden_act, down_weight, preferred_element_type=full)
        + down_bias
    )
    output = final_state.astype(low)
    loss_weight = lengths.shape[0] * MAXLEN / jnp.sum(lengths).astype(full)
    final_grad = jnp.where(
        row_valid[:, None],
        cotangent.astype(full) + loss_weight * (final_state - teacher.astype(full)),
        0.0,
    )
    final_low = final_grad.astype(low)
    down_part = jnp.einsum("td,mtf->mdf", final_low, hidden_act, preferred_element_type=full)
    act_grad = jnp.einsum("td,mdf->mtf", final_low, down_weight, preferred_element_type=full)
    pre_grad = (act_slope * act_grad).astype(low)
    up_part = jnp.einsum("td,mtf->mdf", second_norm, pre_grad, preferred_element_type=full)
    up_bias_part = jnp.sum(pre_grad, axis=1, dtype=full).reshape(FF)
    second_grad = jnp.einsum("mtf,mdf->td", pre_grad, up_weight, preferred_element_type=full)
    middle_part, gain_two, shift_two = norm_back(
        unit_two, inverse_two, norm_gains[1], second_grad
    )
    middle_grad = final_grad + middle_part
    middle_low = middle_grad.astype(low)
    out_part = dot_of(middle_low, attended, 0, 0)
    attended_grad = dot_of(middle_low, out_weight, 1, 0).astype(low)

    deltas = jnp.sum(
        (attended_grad.astype(full) * mixed).reshape(own_rows, HEADS, HEAD_DIM), axis=-1
    )
    deltas = deltas.T.reshape(PAIRS, 2, own_rows)
    logs = logs.reshape(own_rows, HEADS, HEAD_DIM)[:, :, 0].T.reshape(PAIRS, 2, own_rows)
    key_grads = [None] * 4
    value_grads = [None] * 4
    firsts = [None] * 4
    query_grad = None
    sent_last = sent_right = sent_left = None
    for n in (3, 2, 1, 0):
        query_grad, key_grads[n], value_grads[n] = attend_backward(
            queries,
            keys[n],
            values[n],
            attended_grad,
            logs,
            deltas,
            scalars[n],
            query_grad,
            n == 0,
        )
        firsts[n] = dot_of(key_grads[n], qkv_weight[1], 1, 1) + dot_of(
            value_grads[n], qkv_weight[2], 1, 1
        )
        if n == 3:
            back_last = rightward(firsts[3].astype(low), [(0, 1), (3, 2)]).astype(full)
        elif n == 2:
            payload = (firsts[2] + back_last).astype(low)
            back_right = rightward(payload, [(0, 1), (1, 2)]).astype(full)
            back_left = rightward(payload, [(3, 2), (2, 1)]).astype(full)
        elif n == 1:
            to_right = jnp.where(rank == 0, firsts[1], firsts[3] + back_right).astype(low)
            to_left = (firsts[1] + back_left).astype(low)
            final_right = rightward(to_right, [(0, 1), (1, 2), (2, 3)])
            final_left = rightward(to_left, [(3, 2), (2, 1), (1, 0)])
    first_grad = (
        firsts[0]
        + dot_of(query_grad, qkv_weight[0], 1, 1)
        + final_right.astype(full)
        + final_left.astype(full)
    )
    chunk_all = jnp.concatenate(chunks)
    qkv_part = jnp.stack(
        [
            dot_of(first_norm, query_grad, 0, 0).astype(low),
            dot_of(chunk_all, jnp.concatenate(key_grads), 0, 0).astype(low),
            dot_of(chunk_all, jnp.concatenate(value_grads), 0, 0).astype(low),
        ]
    ).reshape(3, dp, block, D)
    qv_bias_part = jnp.stack(
        [
            jnp.sum(query_grad, axis=0, dtype=full),
            sum(jnp.sum(grad, axis=0, dtype=full) for grad in value_grads),
        ]
    )

    up_own, down_own = scatter_dp(
        [
            jnp.concatenate([up_part.astype(low).reshape(mp, dp, block, D), out_part.astype(low).reshape(1, dp, block, D)]),
            down_part.astype(low).reshape(mp, dp, block, D),
        ]
    )
    out_own = up_own[mp].reshape(block, mp, -1).transpose(1, 0, 2)
    tall = scatter_mp(jnp.concatenate([up_own[:mp], down_own], axis=1))
    up_grad = tall[:block]
    down_grad = tall[block:].T
    out_grad = scatter_mp(out_own).T
    left_part, right_part = scatter_dp([qkv_part[..., : D // 2], qkv_part[..., D // 2 :]])
    keep = jnp.where(upper, right_part, left_part)
    keep = keep + swap(jnp.where(upper, left_part, right_part).astype(low), "mp", 2).astype(full)
    width = D // mp
    here = jnp.where(odd, keep[..., width:], keep[..., :width])
    there = jnp.where(odd, keep[..., :width], keep[..., width:])
    qkv_grad = here + swap(there.astype(low), "mp", 1).astype(full)

    start_part, gain_one, shift_one = norm_back(
        unit_one, inverse_one, norm_gains[0], first_grad
    )
    input_grad = middle_grad + start_part
    sequence_sum = jnp.sum(input_grad, axis=0)
    own_slot = (jnp.arange(dp) == data_rank).astype(full)
    total = jnp.concatenate(
        [
            jnp.stack([gain_one, gain_two, shift_one, shift_two]),
            qv_bias_part,
            jnp.stack([jnp.sum(middle_grad, axis=0), jnp.sum(final_grad, axis=0)]),
            up_bias_part.reshape(-1, D),
            own_slot[:, None] * sequence_sum[None, :],
        ]
    )
    for bit in [1] + outer_bits():
        total = total + swap(total, "dp", bit)
    for bit in (1, 2):
        total = total + swap(total, "mp", bit)
    fixed = 8 + FF // D
    chosen = (timesteps[None, :] == jnp.arange(time_table.shape[0])[:, None]).astype(full)
    table_grad = lax.dot_general(
        chosen,
        total[fixed:],
        (((1,), (0,)), ((), ())),
        precision=lax.Precision.HIGHEST,
        preferred_element_type=full,
    )
    return (
        output,
        input_grad,
        table_grad,
        total[0:2],
        total[2:4],
        qkv_grad,
        total[4:6],
        out_grad,
        total[6],
        up_grad,
        total[8:fixed].reshape(FF),
        down_grad,
        total[7],
    )


def solution(mesh):
    rows = P(both, None)
    placed = (
        rows,
        P(),
        P(),
        P(),
        P(),
        P(),
        P(None, "dp", "mp"),
        P(),
        P("mp", "dp"),
        P(),
        P("dp", "mp"),
        P(),
        P("mp", "dp"),
        P(),
        rows,
        rows,
    )
    return jax.shard_map(
        shards,
        mesh=mesh,
        in_specs=placed,
        out_specs=(
            rows,
            rows,
            P(),
            P(),
            P(),
            P(None, "dp", "mp"),
            P(),
            P("mp", "dp"),
            P(),
            P("dp", "mp"),
            P(),
            P("mp", "dp"),
            P(),
        ),
        check_vma=False,
    )
```

```python
import functools

import jax
import jax.numpy as jnp
from jax import lax
from jax.experimental import pallas as pl
from jax.experimental.pallas import tpu as pltpu
from jax.sharding import PartitionSpec as P

D = 768
HEADS = 12
HEAD_DIM = 64
FF = 3072
MAXLEN = 2048
PAIR = 2 * HEAD_DIM
PAIRS = HEADS // 2
VMEM_LIMIT = 58 << 20

far_below = -1e30
epsilon = 1e-05
score_scale = HEAD_DIM ** (-0.5)
low = jnp.bfloat16
full = jnp.float32
both = ("dp", "mp")


def norm_stats(values):
    center = values - jnp.mean(values, axis=-1, keepdims=True)
    spread = jnp.mean(center * center, axis=-1, keepdims=True)
    inverse = lax.rsqrt(spread + epsilon)
    return center * inverse, inverse


def norm_back(unit, inverse, gain_row, grad):
    scaled = grad * gain_row
    mean_scaled = jnp.mean(scaled, axis=-1, keepdims=True)
    mean_unit = jnp.mean(scaled * unit, axis=-1, keepdims=True)
    return (
        inverse * (scaled - mean_scaled - unit * mean_unit),
        jnp.sum(grad * unit, axis=0),
        jnp.sum(grad, axis=0),
    )


def dot_of(left_side, right_side, left_dim, right_dim):
    return lax.dot_general(
        left_side,
        right_side,
        (((left_dim,), (right_dim,)), ((), ())),
        preferred_element_type=full,
    )


def first_half(shape):
    return lax.broadcasted_iota(jnp.int32, shape, len(shape) - 1) < HEAD_DIM


def forward_kernel(first, scalars, q_ref, *refs):
    count = 2
    key_refs, value_refs = refs[:count], refs[count : 2 * count]
    refs = refs[2 * count :]
    if not first:
        top_in, sum_in, acc_in = refs[:3]
        refs = refs[3:]
    rows = q_ref.shape[0]
    keys = key_refs[0].shape[0]
    place = lax.broadcasted_iota(jnp.int32, (1, keys), 1)
    q_pair = q_ref[...]
    lower = first_half((rows, PAIR))
    parts = []
    for half in range(2):
        kept = lower if half == 0 else jnp.logical_not(lower)
        q_half = jnp.where(kept, q_pair, jnp.zeros_like(q_pair))
        scores = []
        for n in range(count):
            bias = jnp.where(place + scalars[n] * keys < scalars[count], 0.0, far_below)
            scores.append(dot_of(q_half, key_refs[n][...], 1, 1) + bias)
        highest = functools.reduce(
            jnp.maximum, [jnp.max(score, axis=-1, keepdims=True) for score in scores]
        )
        totals = jnp.zeros_like(highest)
        mixed = jnp.zeros((rows, PAIR), full)
        for n in range(count):
            exp_scores = jnp.exp(scores[n] - highest)
            totals = totals + jnp.sum(exp_scores, axis=-1, keepdims=True)
            mixed = mixed + dot_of(exp_scores.astype(low), value_refs[n][...], 1, 0)
        parts.append((highest, totals, mixed))
    top = jnp.where(lower, parts[0][0], parts[1][0])
    total = jnp.where(lower, parts[0][1], parts[1][1])
    mixed = jnp.where(lower, parts[0][2], parts[1][2])
    if first:
        top_ref, sum_ref, acc_ref = refs
        top_ref[...] = top
        sum_ref[...] = total
        acc_ref[...] = mixed
    else:
        out_ref, log_ref = refs
        highest = jnp.maximum(top, top_in[...])
        here = jnp.exp(top - highest)
        before = jnp.exp(top_in[...] - highest)
        total = total * here + sum_in[...] * before
        out_ref[...] = (mixed * here + acc_in[...] * before) / total
        log_ref[...] = highest + jnp.log(total)


def attend_forward(queries, keys, values, scalars, state):
    rows, total = queries.shape[0], keys[0].shape[0]
    first = state is None
    pair_rows = lambda count: pl.BlockSpec((count, PAIR), lambda i, n: (0, i))
    wide = jax.ShapeDtypeStruct((rows, D), full)
    carried = () if first else state
    return pl.pallas_call(
        functools.partial(forward_kernel, first),
        out_shape=(wide,) * (3 if first else 2),
        grid_spec=pltpu.PrefetchScalarGridSpec(
            num_scalar_prefetch=1,
            grid=(PAIRS,),
            in_specs=[pair_rows(rows)]
            + [pair_rows(total)] * (len(keys) + len(values))
            + [pair_rows(rows)] * len(carried),
            out_specs=[pair_rows(rows)] * (3 if first else 2),
        ),
        compiler_params=pltpu.CompilerParams(vmem_limit_bytes=VMEM_LIMIT),
        cost_estimate=pl.CostEstimate(
            flops=8 * rows * total * D * 4,
            bytes_accessed=24 * total * D,
            transcendentals=2 * rows * total * HEADS,
        ),
        name="attend_forward",
    )(scalars, queries, *keys, *values, *carried)


def backward_kernel(
    first,
    last,
    scalars,
    q_ref,
    k_ref,
    v_ref,
    g_ref,
    log_ref,
    delta_ref,
    wk_ref,
    wv_ref,
    *refs
):
    if last:
        wq_ref = refs[0]
        refs = refs[1:]
    if not first:
        dq_in = refs[0]
        refs = refs[1:]
    dq_ref, dk_ref, dv_ref, back_ref, accum = refs
    step = pl.program_id(0)
    rows = q_ref.shape[0]
    keys = k_ref.shape[0]
    limit = scalars[1] - scalars[0] * keys
    q_pair = q_ref[...]
    g_pair = g_ref[...]
    k_pair = k_ref[...]
    v_pair = v_ref[...]
    lower = first_half((rows, PAIR))
    lower_keys = first_half((keys, PAIR))
    place = lax.broadcasted_iota(jnp.int32, (keys, 1), 0)
    bias = jnp.where(place < limit, 0.0, far_below)
    dq = []
    dk = []
    dv = []
    for half in range(2):
        kept = lower if half == 0 else jnp.logical_not(lower)
        q_half = jnp.where(kept, q_pair, jnp.zeros_like(q_pair))
        g_half = jnp.where(kept, g_pair, jnp.zeros_like(g_pair))
        log_row = log_ref[0, half : half + 1, :]
        delta_row = delta_ref[0, half : half + 1, :]
        scores = dot_of(k_pair, q_half, 1, 1) + bias
        probs = jnp.exp(scores - log_row)
        dv.append(dot_of(probs.astype(low), g_pair, 1, 0))
        prob_grad = dot_of(v_pair, g_half, 1, 1)
        score_grad = (probs * (prob_grad - delta_row)).astype(low)
        dk.append(dot_of(score_grad, q_pair, 1, 0))
        dq.append(dot_of(score_grad, k_pair, 0, 0))
    dk_low = jnp.where(lower_keys, dk[0], dk[1]).astype(low)
    dv_low = jnp.where(lower_keys, dv[0], dv[1]).astype(low)
    dk_ref[...] = dk_low
    dv_ref[...] = dv_low
    grads = [dk_low, dv_low]
    weights = [wk_ref[0], wv_ref[0]]
    dq_all = jnp.where(lower, dq[0], dq[1])
    if not first:
        dq_all = dq_all + dq_in[...]
    back = dot_of(jnp.concatenate(grads, axis=1), jnp.concatenate(weights, axis=1), 1, 1)
    if last:
        dq_low = (dq_all * score_scale).astype(low)
        dq_ref[...] = dq_low
        back = back + dot_of(dq_low, wq_ref[0], 1, 1)
    else:
        dq_ref[...] = dq_all

    @pl.when(step == 0)
    def _():
        accum[...] = back

    @pl.when(step > 0)
    def _():
        accum[...] += back

    @pl.when(step == PAIRS - 1)
    def _():
        back_ref[...] = accum[...].astype(back_ref.dtype)


def attend_backward(
    queries, keys, values, grads, logs, deltas, weights, scalars, carried, last
):
    rows, total = queries.shape[0], keys.shape[0]
    first = carried is None
    pair_rows = lambda count: pl.BlockSpec((count, PAIR), lambda i, n: (0, i))
    stats = pl.BlockSpec((1, 2, rows), lambda i, n: (i, 0, 0))
    weight = lambda c: pl.BlockSpec((1, D, PAIR), lambda i, n: (c, 0, i))
    extra = (weights,) * last + (() if first else (carried,))
    extra_specs = [weight(0)] * last + ([] if first else [pair_rows(rows)])
    return pl.pallas_call(
        functools.partial(backward_kernel, first, last),
        out_shape=(
            jax.ShapeDtypeStruct((rows, D), low if last else full),
            jax.ShapeDtypeStruct((total, D), low),
            jax.ShapeDtypeStruct((total, D), low),
            jax.ShapeDtypeStruct((total, D), low if first else full),
        ),
        grid_spec=pltpu.PrefetchScalarGridSpec(
            num_scalar_prefetch=1,
            grid=(PAIRS,),
            in_specs=[
                pair_rows(rows),
                pair_rows(total),
                pair_rows(total),
                pair_rows(rows),
                stats,
                stats,
                weight(1),
                weight(2),
            ]
            + extra_specs,
            out_specs=[
                pair_rows(rows),
                pair_rows(total),
                pair_rows(total),
                pl.BlockSpec((total, D), lambda i, n: (0, 0)),
            ],
            scratch_shapes=[pltpu.VMEM((total, D), full)],
        ),
        compiler_params=pltpu.CompilerParams(vmem_limit_bytes=VMEM_LIMIT),
        cost_estimate=pl.CostEstimate(
            flops=10 * rows * total * D * 4,
            bytes_accessed=16 * total * D,
            transcendentals=rows * total * HEADS,
        ),
        name="attend_backward",
    )(scalars, queries, keys, values, grads, logs, deltas, weights, weights, *extra)


def swap(value, axis, bit):
    count = lax.axis_size(axis)
    return lax.ppermute(value, axis, [(i, i ^ bit) for i in range(count)])


def after(value, *waits):
    return lax.optimization_barrier((value,) + waits)[0]


def outer_bits():
    bits = []
    bit = 2
    while bit < lax.axis_size("dp"):
        bits.append(bit)
        bit *= 2
    return bits


def gather_dp(parts, waits=()):
    bits = outer_bits()
    half = len(bits) // 2
    orders = [bits[half * (n % 2) :] + bits[: half * (n % 2)] for n in range(len(parts))]
    held = [[([0], part)] for part in parts]
    for step in range(len(bits)):
        arrived = []
        for n in range(len(parts)):
            bit = orders[n][step]
            masks = [m for mask, _ in held[n] for m in mask]
            arrays = [array for _, array in held[n]]
            block = jnp.concatenate(arrays) if step else after(arrays[0], *waits)
            arrived.append([(masks, block), ([m ^ bit for m in masks], swap(block, "dp", bit))])
        held = arrived
    return [
        pieces + [([m ^ 1 for m in masks], swap(block, "dp", 1)) for masks, block in pieces]
        for pieces in held
    ]


def canonical_row(me, rank, block, mask, rank_mask, stride, offset):
    if mask is None:
        return offset
    row = (me ^ mask) * block + offset
    if stride:
        row = row + (rank ^ rank_mask) * stride
    return pl.multiple_of(row, 16)


def place_kernel(plan, block, *refs):
    count = len(plan)
    ins = refs[:count]
    outs = refs[count:-1]
    sems = refs[-1]
    me = lax.axis_index("dp")
    rank = lax.axis_index("mp")
    copies = []
    for ref, moves in zip(ins, plan):
        for start, size, which, mask, rank_mask, stride, offset in moves:
            row = canonical_row(me, rank, block, mask, rank_mask, stride, offset)
            copy = pltpu.make_async_copy(
                ref.at[pl.ds(start, size), :],
                outs[which].at[pl.ds(row, size), :],
                sems.at[len(copies)],
            )
            copy.start()
            copies.append(copy)
    for copy in copies:
        copy.wait()


def plan_of(gathered, layouts):
    arrays = []
    plan = []
    for pieces, layout in zip(gathered, layouts):
        rows = sum(size for _, size, *_ in layout)
        for masks, array in pieces:
            moves = []
            for j, mask in enumerate(masks):
                for start, size, which, rank_mask, stride, offset in layout:
                    moves.append((j * rows + start, size, which, mask, rank_mask, stride, offset))
            arrays.append(array)
            plan.append(moves)
    return arrays, plan


def place(arrays, plan, block, shapes):
    moved = sum(array.size for array in arrays) * 4
    return pl.pallas_call(
        functools.partial(place_kernel, plan, block),
        out_shape=[jax.ShapeDtypeStruct(shape, low) for shape in shapes],
        in_specs=[pl.BlockSpec(memory_space=pl.ANY)] * len(arrays),
        out_specs=[pl.BlockSpec(memory_space=pltpu.VMEM)] * len(shapes),
        scratch_shapes=[pltpu.SemaphoreType.DMA((sum(len(moves) for moves in plan),))],
        compiler_params=pltpu.CompilerParams(vmem_limit_bytes=VMEM_LIMIT),
        cost_estimate=pl.CostEstimate(flops=0, bytes_accessed=moved, transcendentals=0),
        name="place",
    )(*arrays)


def middle_kernel(plan, block, total, *refs):
    limit_ref, vector_ref = refs[:2]
    token_hbm, mixed_hbm, log_hbm, cot_hbm, teach_hbm = refs[2:7]
    pieces = refs[7 : 7 + total]
    (
        out_hbm,
        final_hbm,
        act_hbm,
        pre_hbm,
        second_hbm,
        middle_low_hbm,
        attended_hbm,
        middle_hbm,
        grad_hbm,
        delta_ref,
        log_ref,
        sum_ref,
    ) = refs[7 + total : 19 + total]
    (
        token,
        mixed,
        logs,
        cot,
        teach,
        up,
        down,
        proj,
        act,
        pre,
        slope,
        second,
        attended,
        middle,
        final,
        out,
        final_low,
        middle_low,
        grad,
        accum,
        in_sems,
        weight_sems,
        out_sems,
    ) = refs[19 + total :]
    targets = (up, down, proj)
    rows = token.shape[0]
    me = lax.axis_index("dp")
    rank = lax.axis_index("mp")

    def fetch(ref, scratch, n):
        copy = pltpu.make_async_copy(ref, scratch, in_sems.at[n])
        copy.start()
        return copy

    def send(scratch, ref, n):
        copy = pltpu.make_async_copy(scratch, ref, out_sems.at[n])
        copy.start()
        return copy

    gets = [
        fetch(token_hbm, token, 0),
        fetch(mixed_hbm, mixed, 1),
        fetch(log_hbm, logs, 2),
        fetch(cot_hbm, cot, 3),
        fetch(teach_hbm, teach, 4),
    ]
    loads = {0: [], 1: [], 2: []}
    number = 0
    for want in (2, 0, 1):
        for ref, moves in zip(pieces, plan):
            for start, size, which, mask, rank_mask, stride, offset in moves:
                if which != want:
                    continue
                row = canonical_row(me, rank, block, mask, rank_mask, stride, offset)
                copy = pltpu.make_async_copy(
                    ref.at[pl.ds(start, size), :],
                    targets[which].at[pl.ds(row, size), :],
                    weight_sems.at[number],
                )
                copy.start()
                loads[which].append(copy)
                number += 1

    table_row = vector_ref[0:1, :]
    out_bias = vector_ref[1:2, :]
    gain = vector_ref[2:3, :]
    shift = vector_ref[3:4, :]
    down_bias = vector_ref[4:5, :]
    weight = vector_ref[5:6, :]
    gets[0].wait()
    gets[1].wait()
    attended[...] = mixed[...].astype(low)
    puts = [send(attended, attended_hbm, 0)]
    for copy in loads[2]:
        copy.wait()
    state = token[...].astype(full) + table_row + out_bias
    state = state + dot_of(attended[...], proj[...], 1, 1)
    middle[...] = state
    unit, _ = norm_stats(state)
    second[...] = (unit * gain + shift).astype(low)
    puts.append(send(second, second_hbm, 1))
    accum[...] = jnp.zeros((rows, D), full)
    for copy in loads[0]:
        copy.wait()
    for copy in loads[1]:
        copy.wait()

    def forward(m, _):
        place = pl.ds(pl.multiple_of(m * D, D), D)
        value = dot_of(second[...], up[place, :], 1, 0) + vector_ref[pl.ds(8 + m, 1), :]
        cumulative = 0.5 + 0.5 * lax.erf(value * (0.5**0.5))
        act[m] = (value * cumulative).astype(low)
        slope[m] = cumulative + value * jnp.exp(-0.5 * value * value) * 0.3989422804014327
        accum[...] += dot_of(act[m], down[place, :], 1, 1)
        return 0

    lax.fori_loop(0, FF // D, forward, 0)
    puts.append(send(act, act_hbm, 2))
    final_state = middle[...] + accum[...] + down_bias
    out[...] = final_state.astype(low)
    puts.append(send(out, out_hbm, 3))
    gets[3].wait()
    gets[4].wait()
    place = lax.broadcasted_iota(jnp.int32, (rows, 1), 0)
    grads = cot[...].astype(full) + weight * (final_state - teach[...].astype(full))
    grads = jnp.where(place < limit_ref[0], grads, 0.0)
    final[...] = grads
    final_low[...] = grads.astype(low)
    puts.append(send(final_low, final_hbm, 4))
    sum_ref[3:4, :] = jnp.sum(grads, axis=0, keepdims=True)
    accum[...] = jnp.zeros((rows, D), full)

    def backward(m, _):
        place = pl.ds(pl.multiple_of(m * D, D), D)
        value = slope[m] * dot_of(final_low[...], down[place, :], 1, 0)
        value = value.astype(low)
        pre[m] = value
        sum_ref[pl.ds(8 + m, 1), :] = jnp.sum(value.astype(full), axis=0, keepdims=True)
        accum[...] += dot_of(value, up[place, :], 1, 1)
        return 0

    lax.fori_loop(0, FF // D, backward, 0)
    puts.append(send(pre, pre_hbm, 5))
    unit, inverse = norm_stats(middle[...])
    second_grad = accum[...]
    sum_ref[0:1, :] = jnp.sum(second_grad * unit, axis=0, keepdims=True)
    sum_ref[1:2, :] = jnp.sum(second_grad, axis=0, keepdims=True)
    scaled = second_grad * gain
    mean_scaled = jnp.mean(scaled, axis=-1, keepdims=True)
    mean_unit = jnp.mean(scaled * unit, axis=-1, keepdims=True)
    total_grad = final[...] + inverse * (scaled - mean_scaled - unit * mean_unit)
    middle[...] = total_grad
    puts.append(send(middle, middle_hbm, 6))
    middle_low[...] = total_grad.astype(low)
    puts.append(send(middle_low, middle_low_hbm, 7))
    sum_ref[2:3, :] = jnp.sum(total_grad, axis=0, keepdims=True)
    attended_grad = dot_of(middle_low[...], proj[...], 1, 0).astype(low)
    grad[...] = attended_grad
    puts.append(send(grad, grad_hbm, 8))
    gets[2].wait()
    head = lax.broadcasted_iota(jnp.int32, (16, D), 0)
    lane = lax.broadcasted_iota(jnp.int32, (16, D), 1)
    member = jnp.where(lane // HEAD_DIM == head, 1.0, 0.0)
    leader = jnp.where(lane == head * HEAD_DIM, 1.0, 0.0)
    exact = functools.partial(
        lax.dot_general,
        dimension_numbers=(((1,), (1,)), ((), ())),
        precision=lax.Precision.HIGHEST,
        preferred_element_type=full,
    )
    deltas = exact(member, attended_grad.astype(full) * mixed[...])
    tops = exact(leader, logs[...])
    for pair in range(PAIRS):
        delta_ref[pair] = deltas[2 * pair : 2 * pair + 2]
        log_ref[pair] = tops[2 * pair : 2 * pair + 2]
    for copy in puts:
        copy.wait()


def middle_call(limit, vectors, tokens, mixed, logs, cot, teach, arrays, plan, block):
    rows = tokens.shape[0]
    hidden = FF // D
    narrow = jax.ShapeDtypeStruct((rows, D), low)
    wide = jax.ShapeDtypeStruct((rows, D), full)
    many = jax.ShapeDtypeStruct((hidden, rows, D), low)
    stats = jax.ShapeDtypeStruct((PAIRS, 2, rows), full)
    anywhere = pl.BlockSpec(memory_space=pl.ANY)
    inside = pl.BlockSpec(memory_space=pltpu.VMEM)
    moves = sum(len(part) for part in plan)
    return pl.pallas_call(
        functools.partial(middle_kernel, plan, block, len(arrays)),
        out_shape=(
            narrow,
            narrow,
            many,
            many,
            narrow,
            narrow,
            narrow,
            wide,
            narrow,
            stats,
            stats,
            jax.ShapeDtypeStruct((8 + 8, D), full),
        ),
        in_specs=[pl.BlockSpec(memory_space=pltpu.SMEM), inside]
        + [anywhere] * (5 + len(arrays)),
        out_specs=[anywhere] * 9 + [inside] * 3,
        scratch_shapes=[
            pltpu.VMEM((rows, D), low),
            pltpu.VMEM((rows, D), full),
            pltpu.VMEM((rows, D), full),
            pltpu.VMEM((rows, D), low),
            pltpu.VMEM((rows, D), low),
            pltpu.VMEM((FF, D), low),
            pltpu.VMEM((FF, D), low),
            pltpu.VMEM((D, D), low),
            pltpu.VMEM((hidden, rows, D), low),
            pltpu.VMEM((hidden, rows, D), low),
            pltpu.VMEM((hidden, rows, D), full),
            pltpu.VMEM((rows, D), low),
            pltpu.VMEM((rows, D), low),
            pltpu.VMEM((rows, D), full),
            pltpu.VMEM((rows, D), full),
            pltpu.VMEM((rows, D), low),
            pltpu.VMEM((rows, D), low),
            pltpu.VMEM((rows, D), low),
            pltpu.VMEM((rows, D), low),
            pltpu.VMEM((rows, D), full),
            pltpu.SemaphoreType.DMA((5,)),
            pltpu.SemaphoreType.DMA((moves,)),
            pltpu.SemaphoreType.DMA((9,)),
        ],
        compiler_params=pltpu.CompilerParams(vmem_limit_bytes=VMEM_LIMIT),
        cost_estimate=pl.CostEstimate(
            flops=20 * rows * D * FF, bytes_accessed=30 << 20, transcendentals=2 * rows * FF
        ),
        name="middle",
    )(limit, vectors, tokens, mixed, logs, cot, teach, *arrays)


def feed_grad_kernel(
    final_ref, act_ref, second_ref, pre_ref, middle_ref, attended_ref, *refs
):
    down_keep, down_send, up_keep, up_send, left, right = refs
    block = down_keep.shape[2]
    m = pl.program_id(0)
    even = lax.axis_index("dp") % 2 == 0

    @pl.when(m == 0)
    def _():
        left[...] = final_ref[...].T
        right[...] = second_ref[...].T

    def store(value, keep, send, index):
        for outer in range(down_keep.shape[1]):
            first = value[2 * outer * block : (2 * outer + 1) * block]
            other = value[(2 * outer + 1) * block : (2 * outer + 2) * block]
            keep[index, outer] = jnp.where(even, first, other).astype(low)
            send[index, outer] = jnp.where(even, other, first).astype(low)

    @pl.when(m < FF // D)
    def _():
        store(dot_of(left[...], act_ref[0], 1, 0), down_keep, down_send, 0)
        store(dot_of(right[...], pre_ref[0], 1, 0), up_keep, up_send, 0)

    @pl.when(m == FF // D)
    def _():
        store(dot_of(middle_ref[...].T, attended_ref[...], 1, 0), up_keep, up_send, 0)


def feed_grads(final_low, act, second, pre, middle_low, attended, dp):
    rows = final_low.shape[0]
    hidden = FF // D
    whole = pl.BlockSpec((rows, D), lambda m: (0, 0))
    last = hidden - 1
    slice_of = pl.BlockSpec((1, rows, D), lambda m: (jnp.minimum(m, last), 0, 0))
    shape = (hidden, dp // 2, D // dp, D)
    longer = (hidden + 1,) + shape[1:]
    down_spec = pl.BlockSpec((1,) + shape[1:], lambda m: (jnp.minimum(m, last), 0, 0, 0))
    up_spec = pl.BlockSpec((1,) + shape[1:], lambda m: (m, 0, 0, 0))
    return pl.pallas_call(
        feed_grad_kernel,
        out_shape=[jax.ShapeDtypeStruct(shape, low)] * 2
        + [jax.ShapeDtypeStruct(longer, low)] * 2,
        grid=(hidden + 1,),
        in_specs=[whole, slice_of, whole, slice_of, whole, whole],
        out_specs=[down_spec, down_spec, up_spec, up_spec],
        scratch_shapes=[pltpu.VMEM((D, rows), low)] * 2,
        compiler_params=pltpu.CompilerParams(vmem_limit_bytes=VMEM_LIMIT),
        cost_estimate=pl.CostEstimate(
            flops=10 * rows * D * FF, bytes_accessed=20 << 20, transcendentals=0
        ),
        name="feed_grads",
    )(final_low, act, second, pre, middle_low, attended)


def qkv_grad_kernel(count, *refs):
    chunk_refs = refs[:count]
    query_ref = refs[count]
    key_refs = refs[count + 1 : 2 * count + 1]
    value_refs = refs[2 * count + 1 : 3 * count + 1]
    keep_ref, send_ref, sum_ref, turned = refs[3 * count + 1 :]
    block = keep_ref.shape[2]
    rows = query_ref.shape[0]
    c = pl.program_id(0)
    even = lax.axis_index("dp") % 2 == 0
    ones = jnp.ones((16, rows), low)

    def store(value):
        for outer in range(keep_ref.shape[1]):
            first = value[2 * outer * block : (2 * outer + 1) * block]
            other = value[(2 * outer + 1) * block : (2 * outer + 2) * block]
            keep_ref[0, outer] = jnp.where(even, first, other).astype(low)
            send_ref[0, outer] = jnp.where(even, other, first).astype(low)

    @pl.when(c == 0)
    def _():
        for n in range(count):
            turned[n] = chunk_refs[n][...].T
        store(dot_of(turned[0], query_ref[...], 1, 0))
        sum_ref[0:8, :] = dot_of(ones, query_ref[...], 1, 0)[0:8]

    def many(sources):
        value = dot_of(turned[0], sources[0][...], 1, 0)
        for n in range(1, count):
            value = value + dot_of(turned[n], sources[n][...], 1, 0)
        store(value)

    @pl.when(c == 1)
    def _():
        many(key_refs)

    @pl.when(c == 2)
    def _():
        many(value_refs)
        value = dot_of(ones, value_refs[0][...], 1, 0)
        for n in range(1, count):
            value = value + dot_of(ones, value_refs[n][...], 1, 0)
        sum_ref[8:16, :] = value[0:8]


def qkv_grads(chunks, query_grad, key_grads, value_grads, dp):
    rows = query_grad.shape[0]
    count = len(chunks)
    whole = pl.BlockSpec((rows, D), lambda c: (0, 0))
    shape = (3, dp // 2, D // dp, D)
    part = pl.BlockSpec((1,) + shape[1:], lambda c: (c, 0, 0, 0))
    return pl.pallas_call(
        functools.partial(qkv_grad_kernel, count),
        out_shape=[jax.ShapeDtypeStruct(shape, low)] * 2
        + [jax.ShapeDtypeStruct((16, D), full)],
        grid=(3,),
        in_specs=[whole] * (3 * count + 1),
        out_specs=[part, part, pl.BlockSpec((16, D), lambda c: (0, 0))],
        scratch_shapes=[pltpu.VMEM((count, D, rows), low)],
        compiler_params=pltpu.CompilerParams(vmem_limit_bytes=VMEM_LIMIT),
        cost_estimate=pl.CostEstimate(
            flops=18 * rows * D * D, bytes_accessed=18 << 20, transcendentals=0
        ),
        name="qkv_grads",
    )(*chunks, query_grad, *key_grads, *value_grads)


def two_parts(value, axis, mine):
    keep = lax.dynamic_index_in_dim(value, mine, axis, keepdims=False)
    send = lax.dynamic_index_in_dim(value, 1 - mine, axis, keepdims=False)
    return keep, send.astype(low)


def scatter_dp(parts):
    bits = outer_bits()
    half = len(bits) // 2
    orders = [bits[half * (n % 2) :] + bits[: half * (n % 2)] for n in range(len(parts))]
    me = lax.axis_index("dp")
    yield [send for _, send in parts]
    held = [keep.astype(full) + swap(send, "dp", 1).astype(full) for keep, send in parts]
    held = [
        value.astype(low).reshape(value.shape[:1] + (2,) * len(bits) + value.shape[2:])
        for value in held
    ]
    axes = [list(reversed(bits)) for _ in parts]
    for step in range(len(bits)):
        parts = []
        for n, value in enumerate(held):
            bit = orders[n][step]
            axis = 1 + axes[n].index(bit)
            axes[n].remove(bit)
            parts.append(two_parts(value, axis, (me // bit) % 2))
        yield [send for _, send in parts]
        held = [
            keep.astype(full) + swap(send, "dp", orders[n][step]).astype(full)
            for n, (keep, send) in enumerate(parts)
        ]
        if step < len(bits) - 1:
            held = [value.astype(low) for value in held]
    return held


def scatter_mp(value):
    rank = lax.axis_index("mp")
    for bit in (2, 1):
        pair = value.reshape((2, value.shape[0] // 2) + value.shape[1:])
        keep, send = two_parts(pair, 0, (rank // bit) % 2)
        yield [send]
        value = keep.astype(full) + swap(send, "mp", bit).astype(full)
    return value[0]


def scatter_feed(up_parts, down_parts):
    mp = lax.axis_size("mp")
    up_own, down_own = yield from scatter_dp([up_parts, down_parts])
    block = down_own.shape[1]
    out_own = up_own[mp].reshape(block, mp, -1).transpose(1, 0, 2)
    tall = yield from scatter_mp(jnp.concatenate([up_own[:mp], down_own], axis=1))
    out_grad = yield from scatter_mp(out_own)
    return tall[:block], tall[block:].T, out_grad.T


def scatter_qkv(keep, send):
    rank = lax.axis_index("mp")
    left_part, right_part = yield from scatter_dp(
        [(keep[..., : D // 2], send[..., : D // 2]), (keep[..., D // 2 :], send[..., D // 2 :])]
    )
    upper = rank >= 2
    odd = rank % 2 == 1
    send = jnp.where(upper, left_part, right_part).astype(low)
    yield [send]
    keep = jnp.where(upper, right_part, left_part) + swap(send, "mp", 2).astype(full)
    width = D // lax.axis_size("mp")
    send = jnp.where(odd, keep[..., :width], keep[..., width:]).astype(low)
    yield [send]
    return jnp.where(odd, keep[..., width:], keep[..., :width]) + swap(
        send, "mp", 1
    ).astype(full)


class Steps:
    def __init__(self, steps):
        self.steps = steps
        self.result = None
        self.done = False

    def next(self):
        try:
            return next(self.steps)
        except StopIteration as stop:
            self.result = stop.value
            self.done = True
            return []

    def finish(self):
        while not self.done:
            self.next()
        return self.result


def shards(
    tokens_in,
    timesteps,
    lengths,
    time_table,
    norm_gains,
    norm_biases,
    w_qkv,
    qv_bias,
    w_out,
    out_bias,
    w_up,
    up_bias,
    w_down,
    down_bias,
    cotangent,
    teacher,
):
    rank = lax.axis_index("mp")
    data_rank = lax.axis_index("dp")
    mp = lax.axis_size("mp")
    dp = lax.axis_size("dp")
    own_rows = tokens_in.shape[0]
    length = lax.dynamic_index_in_dim(lengths, data_rank, keepdims=False)
    own_time = lax.dynamic_index_in_dim(timesteps, data_rank, keepdims=False)
    odd = rank % 2 == 1
    upper = rank >= 2
    middle = jnp.logical_or(rank == 1, rank == 2)

    block = w_qkv.shape[1]
    aligned = block % 32 == 0
    narrow = jnp.concatenate([w_qkv.reshape(3 * block, -1), w_out.T])
    first_swap = swap(narrow, "mp", 1)
    pair = jnp.concatenate(
        [jnp.where(odd, first_swap, narrow), jnp.where(odd, narrow, first_swap)], axis=1
    )
    second_swap = swap(pair, "mp", 2)
    wide = jnp.concatenate(
        [jnp.where(upper, second_swap, pair), jnp.where(upper, pair, second_swap)], axis=1
    )
    qkv_rows, out_rows = wide[: 3 * block], wide[3 * block :]
    up_swap = swap(after(w_up, first_swap), "mp", 1)

    table_row = lax.dynamic_slice_in_dim(time_table, own_time, 1).astype(full)
    start_state = tokens_in.astype(full) + table_row
    unit_one, inverse_one = norm_stats(start_state)
    first_norm = (unit_one * norm_gains[0] + norm_biases[0]).astype(low)
    sent = after(first_norm, second_swap)
    along = lambda value, pairs: lax.ppermute(value, "mp", pairs)
    from_left = along(sent, [(0, 1), (1, 2), (2, 3)])
    from_right = along(sent, [(1, 0), (2, 1), (3, 2)])
    near = jnp.where(rank == 0, from_right, from_left)

    up_pair = jnp.concatenate([w_up, up_swap])
    up_other = swap(after(up_pair, second_swap), "mp", 2)
    down_own = w_down.T
    down_swap = swap(after(down_own, second_swap), "mp", 1)
    down_pair = jnp.concatenate([down_own, down_swap])
    down_other = swap(after(down_pair, up_other), "mp", 2)

    if aligned:
        split = 3 * block // 2
        gathered = gather_dp([qkv_rows[:split], qkv_rows[split:]])
        arrived = [array for pieces in gathered for _, array in pieces]
        arrays, plan = plan_of(
            gathered,
            [
                [(0, block, 0, 0, 0, 0), (block, split - block, 0, 0, 0, D)],
                [
                    (0, 2 * block - split, 0, 0, 0, D + split - block),
                    (2 * block - split, block, 0, 0, 0, 2 * D),
                ],
            ],
        )
        (qkv_weight,) = place(arrays, plan, block, [(3 * D, D)])
        qkv_weight = qkv_weight.reshape(3, D, D)
        early = [gathered[0][0][1], gathered[1][0][1]]
        ups = gather_dp([up_pair, up_other], early)
        lates = [ups[0][0][1], ups[1][0][1]]
        downs = gather_dp(
            [
                jnp.concatenate([down_pair, out_rows[: block // 2]]),
                jnp.concatenate([down_other, out_rows[block // 2 :]]),
            ],
            lates,
        )
        up_arrays, up_plan = plan_of(
            ups,
            [
                [(0, block, 0, 0, D, 0), (block, block, 0, 1, D, 0)],
                [(0, block, 0, 2, D, 0), (block, block, 0, 3, D, 0)],
            ],
        )
        down_arrays, down_plan = plan_of(
            downs,
            [
                [
                    (0, block, 1, 0, D, 0),
                    (block, block, 1, 1, D, 0),
                    (2 * block, block // 2, 2, 0, 0, 0),
                ],
                [
                    (0, block, 1, 2, D, 0),
                    (block, block, 1, 3, D, 0),
                    (2 * block, block // 2, 2, 0, 0, block // 2),
                ],
            ],
        )
        arrays, plan = up_arrays + down_arrays, up_plan + down_plan
    else:
        early = []
        qkv_weight = lax.all_gather(
            qkv_rows.reshape(3, block, D), "dp", axis=1, tiled=True
        )
        arrays = [
            lax.all_gather(w_up, ("mp", "dp"), axis=0, tiled=True),
            lax.all_gather(down_own, ("mp", "dp"), axis=0, tiled=True),
            lax.all_gather(out_rows, "dp", axis=0, tiled=True),
        ]
        plan = [[(0, array.shape[0], n, None, 0, 0, 0)] for n, array in enumerate(arrays)]

    queries = dot_of(first_norm, qkv_weight[0], 1, 0) + qv_bias[0]
    queries = (queries.astype(low) * score_scale).astype(low)
    hop_right = after(from_left, *early)
    hop_left = after(from_right, *early)
    second = jnp.where(
        upper,
        along(hop_right, [(1, 2), (2, 3)]),
        along(hop_left, [(1, 0), (2, 1)]),
    )
    indices = [
        rank,
        jnp.where(rank == 0, 1, rank - 1),
        jnp.where(upper, rank - 2, rank + 2),
        jnp.where(middle, rank + 1, 3 - rank),
    ]
    scalars = [jnp.stack([index, length]).astype(jnp.int32) for index in indices]

    def project(chunk):
        return (
            dot_of(chunk, qkv_weight[1], 1, 0).astype(low),
            (dot_of(chunk, qkv_weight[2], 1, 0) + qv_bias[1]).astype(low),
        )

    keys, values = map(list, zip(*[project(first_norm), project(near)]))
    state = attend_forward(
        after(queries, hop_right, hop_left),
        keys,
        values,
        jnp.stack(indices[:2] + [length]),
        None,
    )
    second = after(second, state[0])
    last = jnp.where(middle, from_right, along(second, [(1, 0), (2, 3)]))
    chunks = [first_norm, near, second, last]
    for chunk in chunks[2:]:
        key, value = project(chunk)
        keys.append(key)
        values.append(value)
    mixed, logs = attend_forward(
        queries, keys[2:], values[2:], jnp.stack(indices[2:] + [length]), state
    )

    loss_weight = lengths.shape[0] * MAXLEN / jnp.sum(lengths).astype(full)
    vectors = jnp.concatenate(
        [
            table_row,
            out_bias[None],
            norm_gains[1:2],
            norm_biases[1:2],
            down_bias[None],
            jnp.full((3, D), loss_weight),
            up_bias.reshape(-1, D),
            jnp.zeros((4, D), full),
        ]
    )
    limit = (length - rank * own_rows).reshape(1)
    (
        output,
        final_low,
        hidden_act,
        pre_grad,
        second_norm,
        middle_low,
        attended,
        middle_grad,
        attended_grad,
        deltas,
        log_rows,
        sums,
    ) = middle_call(
        limit, vectors, tokens_in, mixed, logs, cotangent, teacher, arrays, plan, block
    )
    gain_two, shift_two, middle_sum, final_sum = sums[0], sums[1], sums[2], sums[3]
    down_keep, down_send, up_keep, up_send = feed_grads(
        final_low, hidden_act, second_norm, pre_grad, middle_low, attended, dp
    )

    feed = Steps(scatter_feed((up_keep, up_send), (down_keep, down_send)))
    key_grads = [None] * 4
    value_grads = [None] * 4
    firsts = [None] * 4
    query_grad = None
    for n in (3, 2, 1, 0):
        waits = feed.next()
        if n == 1:
            waits = waits + [payload]
        query_grad, key_grads[n], value_grads[n], firsts[n] = attend_backward(
            queries,
            keys[n],
            values[n],
            after(attended_grad, *waits),
            log_rows,
            deltas,
            qkv_weight,
            scalars[n],
            query_grad,
            n == 0,
        )
        if n == 3:
            back_last = along(firsts[3], [(0, 1), (3, 2)]).astype(full)
        elif n == 2:
            payload = (firsts[2] + back_last).astype(low)
            back_right = along(payload, [(0, 1), (1, 2)]).astype(full)
            back_left = along(payload, [(3, 2), (2, 1)]).astype(full)
        elif n == 1:
            to_right = jnp.where(
                rank == 0, firsts[1], firsts[3].astype(full) + back_right
            ).astype(low)
            to_left = (firsts[1] + back_left).astype(low)
            final_right = along(to_right, [(0, 1), (1, 2), (2, 3)])
            final_left = along(to_left, [(3, 2), (2, 1), (1, 0)])
    first_grad = firsts[0] + final_right.astype(full) + final_left.astype(full)
    qkv_keep, qkv_send, bias_sums = qkv_grads(chunks, query_grad, key_grads, value_grads, dp)
    qv_bias_part = jnp.stack([bias_sums[0], bias_sums[8]])
    qkv_grad = Steps(scatter_qkv(qkv_keep, qkv_send)).finish()
    up_grad, down_grad, out_grad = feed.finish()

    start_part, gain_one, shift_one = norm_back(
        unit_one, inverse_one, norm_gains[0], first_grad
    )
    input_grad = middle_grad + start_part
    sequence_sum = jnp.sum(input_grad, axis=0)
    own_slot = (jnp.arange(dp) == data_rank).astype(full)
    total = jnp.concatenate(
        [
            jnp.stack([gain_one, gain_two, shift_one, shift_two]),
            qv_bias_part,
            jnp.stack([middle_sum, final_sum]),
            sums[8 : 8 + FF // D],
            own_slot[:, None] * sequence_sum[None, :],
        ]
    )
    for bit in [1] + outer_bits():
        total = total + swap(total, "dp", bit)
    for bit in (1, 2):
        total = total + swap(total, "mp", bit)
    fixed = 8 + FF // D
    chosen = (timesteps[None, :] == jnp.arange(time_table.shape[0])[:, None]).astype(full)
    table_grad = lax.dot_general(
        chosen,
        total[fixed:],
        (((1,), (0,)), ((), ())),
        precision=lax.Precision.HIGHEST,
        preferred_element_type=full,
    )
    return (
        output,
        input_grad,
        table_grad,
        total[0:2],
        total[2:4],
        qkv_grad,
        total[4:6],
        out_grad,
        total[6],
        up_grad,
        total[8:fixed].reshape(FF),
        down_grad,
        total[7],
    )


def solution(mesh):
    rows = P(both, None)
    placed = (
        rows,
        P(),
        P(),
        P(),
        P(),
        P(),
        P(None, "dp", "mp"),
        P(),
        P("mp", "dp"),
        P(),
        P("dp", "mp"),
        P(),
        P("mp", "dp"),
        P(),
        rows,
        rows,
    )
    return jax.shard_map(
        shards,
        mesh=mesh,
        in_specs=placed,
        out_specs=(
            rows,
            rows,
            P(),
            P(),
            P(),
            P(None, "dp", "mp"),
            P(),
            P("mp", "dp"),
            P(),
            P("dp", "mp"),
            P(),
            P("mp", "dp"),
            P(),
        ),
        check_vma=False,
    )
```

```python
import functools

import jax
import jax.numpy as jnp
from jax import lax
from jax.experimental import pallas as pl
from jax.experimental.pallas import tpu as pltpu
from jax.sharding import PartitionSpec as P

D = 768
HEADS = 12
HEAD_DIM = 64
FF = 3072
MAXLEN = 2048
PAIR = 2 * HEAD_DIM
PAIRS = HEADS // 2
VMEM_LIMIT = 58 << 20
SMALL_COST = pl.CostEstimate(flops=1 << 20, bytes_accessed=1 << 16, transcendentals=0)

far_below = -1e30
epsilon = 1e-05
score_scale = HEAD_DIM ** (-0.5)
low = jnp.bfloat16
full = jnp.float32
both = ("dp", "mp")


def norm_stats(values):
    center = values - jnp.mean(values, axis=-1, keepdims=True)
    spread = jnp.mean(center * center, axis=-1, keepdims=True)
    inverse = lax.rsqrt(spread + epsilon)
    return center * inverse, inverse


def norm_back(unit, inverse, gain_row, grad):
    scaled = grad * gain_row
    mean_scaled = jnp.mean(scaled, axis=-1, keepdims=True)
    mean_unit = jnp.mean(scaled * unit, axis=-1, keepdims=True)
    return (
        inverse * (scaled - mean_scaled - unit * mean_unit),
        jnp.sum(grad * unit, axis=0),
        jnp.sum(grad, axis=0),
    )


def dot_of(left_side, right_side, left_dim, right_dim):
    return lax.dot_general(
        left_side,
        right_side,
        (((left_dim,), (right_dim,)), ((), ())),
        preferred_element_type=full,
    )


def first_half(shape):
    return lax.broadcasted_iota(jnp.int32, shape, len(shape) - 1) < HEAD_DIM


def forward_kernel(numbers, first, scalars, q_ref, *refs):
    count = len(numbers)
    key_refs, value_refs = refs[:count], refs[count : 2 * count]
    refs = refs[2 * count :]
    if not first:
        top_in, sum_in, acc_in = refs[:3]
        refs = refs[3:]
    rows = q_ref.shape[0]
    keys = key_refs[0].shape[0]
    place = lax.broadcasted_iota(jnp.int32, (1, keys), 1)
    q_pair = q_ref[...]
    lower = first_half((rows, PAIR))
    parts = []
    for half in range(2):
        kept = lower if half == 0 else jnp.logical_not(lower)
        q_half = jnp.where(kept, q_pair, jnp.zeros_like(q_pair))
        scores = []
        for n in range(count):
            bias = jnp.where(place + scalars[numbers[n]] * keys < scalars[4], 0.0, far_below)
            scores.append(dot_of(q_half, key_refs[n][...], 1, 1) + bias)
        highest = functools.reduce(
            jnp.maximum, [jnp.max(score, axis=-1, keepdims=True) for score in scores]
        )
        totals = jnp.zeros_like(highest)
        mixed = jnp.zeros((rows, PAIR), full)
        for n in range(count):
            exp_scores = jnp.exp(scores[n] - highest)
            totals = totals + jnp.sum(exp_scores, axis=-1, keepdims=True)
            mixed = mixed + dot_of(exp_scores.astype(low), value_refs[n][...], 1, 0)
        parts.append((highest, totals, mixed))
    top = jnp.where(lower, parts[0][0], parts[1][0])
    total = jnp.where(lower, parts[0][1], parts[1][1])
    mixed = jnp.where(lower, parts[0][2], parts[1][2])
    if first:
        top_ref, sum_ref, acc_ref = refs
        top_ref[...] = top
        sum_ref[...] = total
        acc_ref[...] = mixed
    else:
        out_ref, log_ref = refs
        highest = jnp.maximum(top, top_in[...])
        here = jnp.exp(top - highest)
        before = jnp.exp(top_in[...] - highest)
        total = total * here + sum_in[...] * before
        out_ref[...] = (mixed * here + acc_in[...] * before) / total
        log_ref[...] = highest + jnp.log(total)


def attend_forward(queries, pairs, scalars, numbers, state):
    rows, total = queries.shape[0], pairs[0].shape[0]
    first = state is None
    column = lambda count, c: pl.BlockSpec((count, PAIR), lambda i, n: (0, c * PAIRS + i))
    wide = jax.ShapeDtypeStruct((rows, D), full)
    carried = () if first else state
    return pl.pallas_call(
        functools.partial(forward_kernel, numbers, first),
        out_shape=(wide,) * (3 if first else 2),
        grid_spec=pltpu.PrefetchScalarGridSpec(
            num_scalar_prefetch=1,
            grid=(PAIRS,),
            in_specs=[column(rows, 0)]
            + [column(total, 0)] * len(pairs)
            + [column(total, 1)] * len(pairs)
            + [column(rows, 0)] * len(carried),
            out_specs=[column(rows, 0)] * (3 if first else 2),
        ),
        compiler_params=pltpu.CompilerParams(vmem_limit_bytes=VMEM_LIMIT),
        cost_estimate=SMALL_COST,
        name="attend_forward",
    )(scalars, queries, *pairs, *pairs, *carried)


def backward_kernel(
    number,
    first,
    last,
    scalars,
    q_ref,
    k_ref,
    v_ref,
    g_ref,
    log_ref,
    delta_ref,
    wk_ref,
    wv_ref,
    *refs
):
    if last:
        wq_ref = refs[0]
        refs = refs[1:]
    if not first:
        dq_in = refs[0]
        refs = refs[1:]
    dq_ref, dk_ref, dv_ref, back_ref, accum = refs
    step = pl.program_id(0)
    rows = q_ref.shape[0]
    keys = k_ref.shape[0]
    limit = scalars[4] - scalars[number] * keys
    q_pair = q_ref[...]
    g_pair = g_ref[...]
    k_pair = k_ref[...]
    v_pair = v_ref[...]
    lower = first_half((rows, PAIR))
    lower_keys = first_half((keys, PAIR))
    place = lax.broadcasted_iota(jnp.int32, (keys, 1), 0)
    bias = jnp.where(place < limit, 0.0, far_below)
    dq = []
    dk = []
    dv = []
    for half in range(2):
        kept = lower if half == 0 else jnp.logical_not(lower)
        q_half = jnp.where(kept, q_pair, jnp.zeros_like(q_pair))
        g_half = jnp.where(kept, g_pair, jnp.zeros_like(g_pair))
        log_row = log_ref[0, half : half + 1, :]
        delta_row = delta_ref[0, half : half + 1, :]
        scores = dot_of(k_pair, q_half, 1, 1) + bias
        probs = jnp.exp(scores - log_row)
        dv.append(dot_of(probs.astype(low), g_pair, 1, 0))
        prob_grad = dot_of(v_pair, g_half, 1, 1)
        score_grad = (probs * (prob_grad - delta_row)).astype(low)
        dk.append(dot_of(score_grad, q_pair, 1, 0))
        dq.append(dot_of(score_grad, k_pair, 0, 0))
    dk_low = jnp.where(lower_keys, dk[0], dk[1]).astype(low)
    dv_low = jnp.where(lower_keys, dv[0], dv[1]).astype(low)
    dk_ref[...] = dk_low
    dv_ref[...] = dv_low
    grads = [dk_low, dv_low]
    weights = [wk_ref[...], wv_ref[...]]
    dq_all = jnp.where(lower, dq[0], dq[1])
    if not first:
        dq_all = dq_all + dq_in[...]
    back = dot_of(jnp.concatenate(grads, axis=1), jnp.concatenate(weights, axis=1), 1, 1)
    if last:
        dq_low = (dq_all * score_scale).astype(low)
        dq_ref[...] = dq_low
        back = back + dot_of(dq_low, wq_ref[...], 1, 1)
    else:
        dq_ref[...] = dq_all

    @pl.when(step == 0)
    def _():
        accum[...] = back

    @pl.when(step > 0)
    def _():
        accum[...] += back

    @pl.when(step == PAIRS - 1)
    def _():
        back_ref[...] = accum[...].astype(back_ref.dtype)


def attend_backward(
    number, queries, pair, grads, logs, deltas, query_weight, pair_weight, scalars, carried, last
):
    rows, total = queries.shape[0], pair.shape[0]
    first = carried is None
    column = lambda count, c: pl.BlockSpec((count, PAIR), lambda i, n: (0, c * PAIRS + i))
    stats = pl.BlockSpec((1, 2, rows), lambda i, n: (i, 0, 0))
    extra = (query_weight,) * last + (() if first else (carried,))
    extra_specs = [column(D, 0)] * last + ([] if first else [column(rows, 0)])
    return pl.pallas_call(
        functools.partial(backward_kernel, number, first, last),
        out_shape=(
            jax.ShapeDtypeStruct((rows, D), low if last else full),
            jax.ShapeDtypeStruct((total, D), low),
            jax.ShapeDtypeStruct((total, D), low),
            jax.ShapeDtypeStruct((total, D), low if first else full),
        ),
        grid_spec=pltpu.PrefetchScalarGridSpec(
            num_scalar_prefetch=1,
            grid=(PAIRS,),
            in_specs=[
                column(rows, 0),
                column(total, 0),
                column(total, 1),
                column(rows, 0),
                stats,
                stats,
                column(D, 0),
                column(D, 1),
            ]
            + extra_specs,
            out_specs=[
                column(rows, 0),
                column(total, 0),
                column(total, 0),
                pl.BlockSpec((total, D), lambda i, n: (0, 0)),
            ],
            scratch_shapes=[pltpu.VMEM((total, D), full)],
        ),
        compiler_params=pltpu.CompilerParams(vmem_limit_bytes=VMEM_LIMIT),
        cost_estimate=SMALL_COST,
        name="attend_backward",
    )(
        scalars,
        queries,
        pair,
        pair,
        grads,
        logs,
        deltas,
        pair_weight,
        pair_weight,
        *extra,
    )


def swap(value, axis, bit):
    count = lax.axis_size(axis)
    return lax.ppermute(value, axis, [(i, i ^ bit) for i in range(count)])


class Order:
    def __init__(self):
        self.marks = ()

    def __call__(self, *values):
        values = lax.optimization_barrier(values + self.marks)[: len(values)]
        self.marks = values
        return values[0] if len(values) == 1 else values


def outer_bits():
    bits = []
    bit = 2
    while bit < lax.axis_size("dp"):
        bits.append(bit)
        bit *= 2
    return bits


class Gather:
    def __init__(self, parts):
        self.bits = outer_bits()
        half = len(self.bits) // 2
        self.orders = [
            self.bits[half * (n % 2) :] + self.bits[: half * (n % 2)] for n in range(len(parts))
        ]
        self.result = [[([0], part)] for part in parts]
        self.step = 0

    def advance(self, order):
        held = self.result
        if self.step < len(self.bits):
            masks = [[m for mask, _ in pieces for m in mask] for pieces in held]
            blocks = [
                jnp.concatenate([array for _, array in pieces]) if self.step else pieces[0][1]
                for pieces in held
            ]
            blocks = order(*blocks)
            bits = [turn[self.step] for turn in self.orders]
            self.result = [
                [(mask, block), ([m ^ bit for m in mask], swap(block, "dp", bit))]
                for mask, block, bit in zip(masks, blocks, bits)
            ]
        else:
            arrays = order(*[array for pieces in held for _, array in pieces])
            arrays = iter(arrays)
            self.result = []
            for pieces in held:
                kept = [(masks, next(arrays)) for masks, _ in pieces]
                self.result.append(
                    kept + [([m ^ 1 for m in masks], swap(array, "dp", 1)) for masks, array in kept]
                )
        self.step += 1


def canonical_row(me, rank, block, mask, rank_mask, stride, offset):
    if mask is None:
        return offset
    row = (me ^ mask) * block + offset
    if stride:
        row = row + (rank ^ rank_mask) * stride
    return pl.multiple_of(row, 16)


def place_kernel(plan, block, *refs):
    count = len(plan)
    ins = refs[:count]
    outs = refs[count:-1]
    sems = refs[-1]
    me = lax.axis_index("dp")
    rank = lax.axis_index("mp")
    copies = []
    for ref, moves in zip(ins, plan):
        for start, size, which, mask, column, _, offset in moves:
            row = canonical_row(me, rank, block, mask, 0, 0, offset)
            copy = pltpu.make_async_copy(
                ref.at[pl.ds(start, size), :],
                outs[which].at[pl.ds(row, size), pl.ds(column * D, D)],
                sems.at[len(copies)],
            )
            copy.start()
            copies.append(copy)
    for copy in copies:
        copy.wait()


def plan_of(gathered, layouts):
    arrays = []
    plan = []
    for pieces, layout in zip(gathered, layouts):
        rows = sum(size for _, size, *_ in layout)
        for masks, array in pieces:
            moves = []
            for j, mask in enumerate(masks):
                for start, size, which, rank_mask, stride, offset in layout:
                    moves.append((j * rows + start, size, which, mask, rank_mask, stride, offset))
            arrays.append(array)
            plan.append(moves)
    return arrays, plan


def place(arrays, plan, block, shapes):
    return pl.pallas_call(
        functools.partial(place_kernel, plan, block),
        out_shape=[jax.ShapeDtypeStruct(shape, low) for shape in shapes],
        in_specs=[pl.BlockSpec(memory_space=pl.ANY)] * len(arrays),
        out_specs=[pl.BlockSpec(memory_space=pltpu.VMEM)] * len(shapes),
        scratch_shapes=[pltpu.SemaphoreType.DMA((sum(len(moves) for moves in plan),))],
        compiler_params=pltpu.CompilerParams(vmem_limit_bytes=VMEM_LIMIT),
        cost_estimate=SMALL_COST,
        name="place",
    )(*arrays)


def middle_kernel(plan, block, total, *refs):
    limit_ref, vector_ref = refs[:2]
    token_hbm, mixed_hbm, log_hbm, cot_hbm, teach_hbm = refs[2:7]
    pieces = refs[7 : 7 + total]
    (
        out_hbm,
        final_hbm,
        act_hbm,
        pre_hbm,
        second_hbm,
        middle_low_hbm,
        attended_hbm,
        middle_hbm,
        grad_hbm,
        delta_ref,
        log_ref,
        sum_ref,
    ) = refs[7 + total : 19 + total]
    (
        token,
        mixed,
        logs,
        cot,
        teach,
        up,
        down,
        proj,
        act,
        pre,
        slope,
        second,
        attended,
        middle,
        final,
        out,
        final_low,
        middle_low,
        grad,
        accum,
        in_sems,
        weight_sems,
        out_sems,
    ) = refs[19 + total :]
    targets = (up, down, proj)
    rows = token.shape[0]
    me = lax.axis_index("dp")
    rank = lax.axis_index("mp")

    def fetch(ref, scratch, n):
        copy = pltpu.make_async_copy(ref, scratch, in_sems.at[n])
        copy.start()
        return copy

    def send(scratch, ref, n):
        copy = pltpu.make_async_copy(scratch, ref, out_sems.at[n])
        copy.start()
        return copy

    gets = [
        fetch(token_hbm, token, 0),
        fetch(mixed_hbm, mixed, 1),
        fetch(log_hbm, logs, 2),
        fetch(cot_hbm, cot, 3),
        fetch(teach_hbm, teach, 4),
    ]
    loads = {0: [], 1: [], 2: []}
    number = 0
    for want in (2, 0, 1):
        for ref, moves in zip(pieces, plan):
            for start, size, which, mask, rank_mask, stride, offset in moves:
                if which != want:
                    continue
                row = canonical_row(me, rank, block, mask, rank_mask, stride, offset)
                copy = pltpu.make_async_copy(
                    ref.at[pl.ds(start, size), :],
                    targets[which].at[pl.ds(row, size), :],
                    weight_sems.at[number],
                )
                copy.start()
                loads[which].append(copy)
                number += 1

    table_row = vector_ref[0:1, :]
    out_bias = vector_ref[1:2, :]
    gain = vector_ref[2:3, :]
    shift = vector_ref[3:4, :]
    down_bias = vector_ref[4:5, :]
    weight = vector_ref[5:6, :]
    gets[0].wait()
    gets[1].wait()
    attended[...] = mixed[...].astype(low)
    puts = [send(attended, attended_hbm, 0)]
    for copy in loads[2]:
        copy.wait()
    state = token[...].astype(full) + table_row + out_bias
    state = state + dot_of(attended[...], proj[...], 1, 1)
    middle[...] = state
    unit, _ = norm_stats(state)
    second[...] = (unit * gain + shift).astype(low)
    puts.append(send(second, second_hbm, 1))
    accum[...] = jnp.zeros((rows, D), full)
    for copy in loads[0]:
        copy.wait()
    for copy in loads[1]:
        copy.wait()

    def forward(m, _):
        place = pl.ds(pl.multiple_of(m * D, D), D)
        value = dot_of(second[...], up[place, :], 1, 0) + vector_ref[pl.ds(8 + m, 1), :]
        cumulative = 0.5 + 0.5 * lax.erf(value * (0.5**0.5))
        act[m] = (value * cumulative).astype(low)
        slope[m] = cumulative + value * jnp.exp(-0.5 * value * value) * 0.3989422804014327
        accum[...] += dot_of(act[m], down[place, :], 1, 1)
        return 0

    lax.fori_loop(0, FF // D, forward, 0)
    puts.append(send(act, act_hbm, 2))
    final_state = middle[...] + accum[...] + down_bias
    out[...] = final_state.astype(low)
    puts.append(send(out, out_hbm, 3))
    gets[3].wait()
    gets[4].wait()
    place = lax.broadcasted_iota(jnp.int32, (rows, 1), 0)
    grads = cot[...].astype(full) + weight * (final_state - teach[...].astype(full))
    grads = jnp.where(place < limit_ref[5], grads, 0.0)
    final[...] = grads
    final_low[...] = grads.astype(low)
    puts.append(send(final_low, final_hbm, 4))
    sum_ref[3:4, :] = jnp.sum(grads, axis=0, keepdims=True)
    accum[...] = jnp.zeros((rows, D), full)

    def backward(m, _):
        place = pl.ds(pl.multiple_of(m * D, D), D)
        value = slope[m] * dot_of(final_low[...], down[place, :], 1, 0)
        value = value.astype(low)
        pre[m] = value
        sum_ref[pl.ds(8 + m, 1), :] = jnp.sum(value.astype(full), axis=0, keepdims=True)
        accum[...] += dot_of(value, up[place, :], 1, 1)
        return 0

    lax.fori_loop(0, FF // D, backward, 0)
    puts.append(send(pre, pre_hbm, 5))
    unit, inverse = norm_stats(middle[...])
    second_grad = accum[...]
    sum_ref[0:1, :] = jnp.sum(second_grad * unit, axis=0, keepdims=True)
    sum_ref[1:2, :] = jnp.sum(second_grad, axis=0, keepdims=True)
    scaled = second_grad * gain
    mean_scaled = jnp.mean(scaled, axis=-1, keepdims=True)
    mean_unit = jnp.mean(scaled * unit, axis=-1, keepdims=True)
    total_grad = final[...] + inverse * (scaled - mean_scaled - unit * mean_unit)
    middle[...] = total_grad
    puts.append(send(middle, middle_hbm, 6))
    middle_low[...] = total_grad.astype(low)
    puts.append(send(middle_low, middle_low_hbm, 7))
    sum_ref[2:3, :] = jnp.sum(total_grad, axis=0, keepdims=True)
    attended_grad = dot_of(middle_low[...], proj[...], 1, 0).astype(low)
    grad[...] = attended_grad
    puts.append(send(grad, grad_hbm, 8))
    gets[2].wait()
    head = lax.broadcasted_iota(jnp.int32, (16, D), 0)
    lane = lax.broadcasted_iota(jnp.int32, (16, D), 1)
    member = jnp.where(lane // HEAD_DIM == head, 1.0, 0.0)
    leader = jnp.where(lane == head * HEAD_DIM, 1.0, 0.0)
    exact = functools.partial(
        lax.dot_general,
        dimension_numbers=(((1,), (1,)), ((), ())),
        precision=lax.Precision.HIGHEST,
        preferred_element_type=full,
    )
    deltas = exact(member, attended_grad.astype(full) * mixed[...])
    tops = exact(leader, logs[...])
    for pair in range(PAIRS):
        delta_ref[pair] = deltas[2 * pair : 2 * pair + 2]
        log_ref[pair] = tops[2 * pair : 2 * pair + 2]
    for copy in puts:
        copy.wait()


def middle_call(limit, vectors, tokens, mixed, logs, cot, teach, arrays, plan, block):
    rows = tokens.shape[0]
    hidden = FF // D
    narrow = jax.ShapeDtypeStruct((rows, D), low)
    wide = jax.ShapeDtypeStruct((rows, D), full)
    many = jax.ShapeDtypeStruct((hidden, rows, D), low)
    stats = jax.ShapeDtypeStruct((PAIRS, 2, rows), full)
    anywhere = pl.BlockSpec(memory_space=pl.ANY)
    inside = pl.BlockSpec(memory_space=pltpu.VMEM)
    moves = sum(len(part) for part in plan)
    return pl.pallas_call(
        functools.partial(middle_kernel, plan, block, len(arrays)),
        out_shape=(
            narrow,
            narrow,
            many,
            many,
            narrow,
            narrow,
            narrow,
            wide,
            narrow,
            stats,
            stats,
            jax.ShapeDtypeStruct((8 + 8, D), full),
        ),
        in_specs=[pl.BlockSpec(memory_space=pltpu.SMEM), inside]
        + [anywhere] * (5 + len(arrays)),
        out_specs=[anywhere] * 9 + [inside] * 3,
        scratch_shapes=[
            pltpu.VMEM((rows, D), low),
            pltpu.VMEM((rows, D), full),
            pltpu.VMEM((rows, D), full),
            pltpu.VMEM((rows, D), low),
            pltpu.VMEM((rows, D), low),
            pltpu.VMEM((FF, D), low),
            pltpu.VMEM((FF, D), low),
            pltpu.VMEM((D, D), low),
            pltpu.VMEM((hidden, rows, D), low),
            pltpu.VMEM((hidden, rows, D), low),
            pltpu.VMEM((hidden, rows, D), full),
            pltpu.VMEM((rows, D), low),
            pltpu.VMEM((rows, D), low),
            pltpu.VMEM((rows, D), full),
            pltpu.VMEM((rows, D), full),
            pltpu.VMEM((rows, D), low),
            pltpu.VMEM((rows, D), low),
            pltpu.VMEM((rows, D), low),
            pltpu.VMEM((rows, D), low),
            pltpu.VMEM((rows, D), full),
            pltpu.SemaphoreType.DMA((5,)),
            pltpu.SemaphoreType.DMA((moves,)),
            pltpu.SemaphoreType.DMA((9,)),
        ],
        compiler_params=pltpu.CompilerParams(vmem_limit_bytes=VMEM_LIMIT),
        cost_estimate=SMALL_COST,
        name="middle",
    )(limit, vectors, tokens, mixed, logs, cot, teach, *arrays)


def feed_grad_kernel(
    final_ref, act_ref, second_ref, pre_ref, middle_ref, attended_ref, *refs
):
    down_keep, down_send, up_keep, up_send, left, right = refs
    block = down_keep.shape[2]
    m = pl.program_id(0)
    even = lax.axis_index("dp") % 2 == 0

    @pl.when(m == 0)
    def _():
        left[...] = final_ref[...].T
        right[...] = second_ref[...].T

    def store(value, keep, send, index):
        for outer in range(down_keep.shape[1]):
            first = value[2 * outer * block : (2 * outer + 1) * block]
            other = value[(2 * outer + 1) * block : (2 * outer + 2) * block]
            keep[index, outer] = jnp.where(even, first, other).astype(low)
            send[index, outer] = jnp.where(even, other, first).astype(low)

    @pl.when(m < FF // D)
    def _():
        store(dot_of(left[...], act_ref[0], 1, 0), down_keep, down_send, 0)
        store(dot_of(right[...], pre_ref[0], 1, 0), up_keep, up_send, 0)

    @pl.when(m == FF // D)
    def _():
        store(dot_of(middle_ref[...].T, attended_ref[...], 1, 0), up_keep, up_send, 0)


def feed_grads(final_low, act, second, pre, middle_low, attended, dp):
    rows = final_low.shape[0]
    hidden = FF // D
    whole = pl.BlockSpec((rows, D), lambda m: (0, 0))
    last = hidden - 1
    slice_of = pl.BlockSpec((1, rows, D), lambda m: (jnp.minimum(m, last), 0, 0))
    shape = (hidden, dp // 2, D // dp, D)
    longer = (hidden + 1,) + shape[1:]
    down_spec = pl.BlockSpec((1,) + shape[1:], lambda m: (jnp.minimum(m, last), 0, 0, 0))
    up_spec = pl.BlockSpec((1,) + shape[1:], lambda m: (m, 0, 0, 0))
    return pl.pallas_call(
        feed_grad_kernel,
        out_shape=[jax.ShapeDtypeStruct(shape, low)] * 2
        + [jax.ShapeDtypeStruct(longer, low)] * 2,
        grid=(hidden + 1,),
        in_specs=[whole, slice_of, whole, slice_of, whole, whole],
        out_specs=[down_spec, down_spec, up_spec, up_spec],
        scratch_shapes=[pltpu.VMEM((D, rows), low)] * 2,
        compiler_params=pltpu.CompilerParams(vmem_limit_bytes=VMEM_LIMIT),
        cost_estimate=SMALL_COST,
        name="feed_grads",
    )(final_low, act, second, pre, middle_low, attended)


def qkv_grad_kernel(count, *refs):
    chunk_refs = refs[:count]
    query_ref = refs[count]
    key_refs = refs[count + 1 : 2 * count + 1]
    value_refs = refs[2 * count + 1 : 3 * count + 1]
    keep_ref, send_ref, sum_ref, turned = refs[3 * count + 1 :]
    block = keep_ref.shape[2]
    rows = query_ref.shape[0]
    c = pl.program_id(0)
    even = lax.axis_index("dp") % 2 == 0
    ones = jnp.ones((16, rows), low)

    def store(value):
        for outer in range(keep_ref.shape[1]):
            first = value[2 * outer * block : (2 * outer + 1) * block]
            other = value[(2 * outer + 1) * block : (2 * outer + 2) * block]
            keep_ref[0, outer] = jnp.where(even, first, other).astype(low)
            send_ref[0, outer] = jnp.where(even, other, first).astype(low)

    @pl.when(c == 0)
    def _():
        for n in range(count):
            turned[n] = chunk_refs[n][...].T
        store(dot_of(turned[0], query_ref[...], 1, 0))
        sum_ref[0:8, :] = dot_of(ones, query_ref[...], 1, 0)[0:8]

    def many(sources):
        value = dot_of(turned[0], sources[0][...], 1, 0)
        for n in range(1, count):
            value = value + dot_of(turned[n], sources[n][...], 1, 0)
        store(value)

    @pl.when(c == 1)
    def _():
        many(key_refs)

    @pl.when(c == 2)
    def _():
        many(value_refs)
        value = dot_of(ones, value_refs[0][...], 1, 0)
        for n in range(1, count):
            value = value + dot_of(ones, value_refs[n][...], 1, 0)
        sum_ref[8:16, :] = value[0:8]


def qkv_grads(chunks, query_grad, key_grads, value_grads, dp):
    rows = query_grad.shape[0]
    count = len(chunks)
    whole = pl.BlockSpec((rows, D), lambda c: (0, 0))
    shape = (3, dp // 2, D // dp, D)
    part = pl.BlockSpec((1,) + shape[1:], lambda c: (c, 0, 0, 0))
    return pl.pallas_call(
        functools.partial(qkv_grad_kernel, count),
        out_shape=[jax.ShapeDtypeStruct(shape, low)] * 2
        + [jax.ShapeDtypeStruct((16, D), full)],
        grid=(3,),
        in_specs=[whole] * (3 * count + 1),
        out_specs=[part, part, pl.BlockSpec((16, D), lambda c: (0, 0))],
        scratch_shapes=[pltpu.VMEM((count, D, rows), low)],
        compiler_params=pltpu.CompilerParams(vmem_limit_bytes=VMEM_LIMIT),
        cost_estimate=SMALL_COST,
        name="qkv_grads",
    )(*chunks, query_grad, *key_grads, *value_grads)


def two_parts(value, axis, mine):
    keep = lax.dynamic_index_in_dim(value, mine, axis, keepdims=False)
    send = lax.dynamic_index_in_dim(value, 1 - mine, axis, keepdims=False)
    return keep, send.astype(low)


def scatter_dp(parts):
    bits = outer_bits()
    half = len(bits) // 2
    orders = [bits[half * (n % 2) :] + bits[: half * (n % 2)] for n in range(len(parts))]
    me = lax.axis_index("dp")
    sends = yield [send for _, send in parts]
    held = [
        (keep.astype(full) + swap(send, "dp", 1).astype(full)).astype(low)
        for (keep, _), send in zip(parts, sends)
    ]
    held = [
        value.reshape(value.shape[:1] + (2,) * len(bits) + value.shape[2:]) for value in held
    ]
    axes = [list(reversed(bits)) for _ in parts]
    for step in range(len(bits)):
        parts = []
        for n, value in enumerate(held):
            bit = orders[n][step]
            axis = 1 + axes[n].index(bit)
            axes[n].remove(bit)
            parts.append(two_parts(value, axis, (me // bit) % 2))
        sends = yield [send for _, send in parts]
        held = [
            keep.astype(full) + swap(sends[n], "dp", orders[n][step]).astype(full)
            for n, (keep, _) in enumerate(parts)
        ]
        if step < len(bits) - 1:
            held = [value.astype(low) for value in held]
    return held


def scatter_mp(values):
    rank = lax.axis_index("mp")
    for bit in (2, 1):
        parts = []
        for value in values:
            pair = value.reshape((2, value.shape[0] // 2) + value.shape[1:])
            parts.append(two_parts(pair, 0, (rank // bit) % 2))
        sends = yield [send for _, send in parts]
        values = [
            keep.astype(full) + swap(send, "mp", bit).astype(full)
            for (keep, _), send in zip(parts, sends)
        ]
    return [value[0] for value in values]


def scatter_feed(up_parts, down_parts):
    mp = lax.axis_size("mp")
    up_own, down_own = yield from scatter_dp([up_parts, down_parts])
    block = down_own.shape[1]
    out_own = up_own[mp].reshape(block, mp, -1).transpose(1, 0, 2)
    tall, out_grad = yield from scatter_mp(
        [jnp.concatenate([up_own[:mp], down_own], axis=1), out_own]
    )
    return tall[:block], tall[block:].T, out_grad.T


def scatter_qkv(keep, send):
    rank = lax.axis_index("mp")
    left_part, right_part = yield from scatter_dp(
        [(keep[..., : D // 2], send[..., : D // 2]), (keep[..., D // 2 :], send[..., D // 2 :])]
    )
    upper = rank >= 2
    odd = rank % 2 == 1
    (send,) = yield [jnp.where(upper, left_part, right_part).astype(low)]
    keep = jnp.where(upper, right_part, left_part) + swap(send, "mp", 2).astype(full)
    width = D // lax.axis_size("mp")
    (send,) = yield [jnp.where(odd, keep[..., :width], keep[..., width:]).astype(low)]
    return jnp.where(odd, keep[..., width:], keep[..., :width]) + swap(
        send, "mp", 1
    ).astype(full)


def butterfly(value):
    for bit in [1] + outer_bits():
        (value,) = yield [value]
        value = value + swap(value, "dp", bit)
    for bit in (1, 2):
        (value,) = yield [value]
        value = value + swap(value, "mp", bit)
    return value


class Steps:
    def __init__(self, steps):
        self.steps = steps
        self.pending = next(steps)
        self.result = None

    def advance(self, order):
        if self.pending is None:
            return
        sends = order(*self.pending)
        sends = [sends] if len(self.pending) == 1 else list(sends)
        try:
            self.pending = self.steps.send(sends)
        except StopIteration as stop:
            self.pending = None
            self.result = stop.value

    def finish(self, order):
        while self.pending is not None:
            self.advance(order)
        return self.result


def shards(
    tokens_in,
    timesteps,
    lengths,
    time_table,
    norm_gains,
    norm_biases,
    w_qkv,
    qv_bias,
    w_out,
    out_bias,
    w_up,
    up_bias,
    w_down,
    down_bias,
    cotangent,
    teacher,
):
    rank = lax.axis_index("mp")
    data_rank = lax.axis_index("dp")
    mp = lax.axis_size("mp")
    dp = lax.axis_size("dp")
    own_rows = tokens_in.shape[0]
    length = lax.dynamic_index_in_dim(lengths, data_rank, keepdims=False)
    own_time = lax.dynamic_index_in_dim(timesteps, data_rank, keepdims=False)
    odd = rank % 2 == 1
    upper = rank >= 2
    middle = jnp.logical_or(rank == 1, rank == 2)
    order = Order()
    along = lambda value, pairs: lax.ppermute(value, "mp", pairs)

    block = w_qkv.shape[1]
    aligned = block % 32 == 0
    narrow = order(jnp.concatenate([w_qkv.reshape(3 * block, -1), w_out.T]))
    first_swap = swap(narrow, "mp", 1)
    up_own = order(w_up)
    up_swap = swap(up_own, "mp", 1)
    pair = order(
        jnp.concatenate(
            [jnp.where(odd, first_swap, narrow), jnp.where(odd, narrow, first_swap)], axis=1
        )
    )
    second_swap = swap(pair, "mp", 2)
    tokens = order(tokens_in)
    table_row = lax.dynamic_slice_in_dim(time_table, own_time, 1).astype(full)
    unit_one, _ = norm_stats(tokens.astype(full) + table_row)
    first_norm = (unit_one * norm_gains[0] + norm_biases[0]).astype(low)
    loss_weight = lengths.shape[0] * MAXLEN / jnp.sum(lengths).astype(full)
    vectors = jnp.concatenate(
        [
            table_row,
            out_bias[None],
            norm_gains[1:2],
            norm_biases[1:2],
            down_bias[None],
            jnp.full((3, D), loss_weight),
            up_bias.reshape(-1, D),
            jnp.zeros((4, D), full),
        ]
    )
    scalars = jnp.stack(
        [
            rank,
            jnp.where(rank == 0, 1, rank - 1),
            jnp.where(upper, rank - 2, rank + 2),
            jnp.where(middle, rank + 1, 3 - rank),
            length,
            length - rank * own_rows,
        ]
    ).astype(jnp.int32)
    first_norm, vectors, scalars = order(first_norm, vectors, scalars)
    wide = jnp.concatenate(
        [jnp.where(upper, second_swap, pair), jnp.where(upper, pair, second_swap)], axis=1
    )
    qkv_rows, out_rows = wide[: 3 * block], wide[3 * block :]
    if aligned:
        split = 3 * block // 2
        qkv_gather = Gather([qkv_rows[:split], qkv_rows[split:]])
        qkv_gather.advance(order)
    sent, up_pair = order(first_norm, jnp.concatenate([up_own, up_swap]))
    from_left = along(sent, [(0, 1), (1, 2), (2, 3)])
    from_right = along(sent, [(1, 0), (2, 1), (3, 2)])
    up_other = swap(up_pair, "mp", 2)
    down_own = order(w_down.T)
    down_swap = swap(down_own, "mp", 1)

    if aligned:
        while qkv_gather.step <= len(qkv_gather.bits):
            qkv_gather.advance(order)
        arrays, plan = plan_of(
            qkv_gather.result,
            [
                [(0, block, 0, 0, 0, 0), (block, split - block, 1, 0, 0, 0)],
                [
                    (0, 2 * block - split, 1, 0, 0, split - block),
                    (2 * block - split, block, 1, 1, 0, 0),
                ],
            ],
        )
        query_weight, pair_weight = place(arrays, plan, block, [(D, D), (D, 2 * D)])
    else:
        weights = lax.all_gather(qkv_rows.reshape(3, block, D), "dp", axis=1, tiled=True)
        query_weight = weights[0]
        pair_weight = jnp.concatenate([weights[1], weights[2]], axis=1)
    pair_bias = jnp.concatenate([jnp.zeros((D,), full), qv_bias[1]])

    def project(chunk):
        return (dot_of(chunk, pair_weight, 1, 0) + pair_bias).astype(low)

    queries = dot_of(first_norm, query_weight, 1, 0) + qv_bias[0]
    queries = (queries.astype(low) * score_scale).astype(low)
    queries, pair_own = order(queries, project(first_norm))

    hop_right, hop_left = order(from_left, from_right)
    second_right = along(hop_right, [(1, 2), (2, 3)])
    second_left = along(hop_left, [(1, 0), (2, 1)])
    down_pair, up_other = order(jnp.concatenate([down_own, down_swap]), up_other)
    down_other = swap(down_pair, "mp", 2)
    if aligned:
        ups = Gather([up_pair, up_other])
        ups.advance(order)
    near = jnp.where(rank == 0, hop_left, hop_right)
    pair_near = order(project(near))
    state = attend_forward(queries, [pair_own, pair_near], scalars, (0, 1), None)
    state = order(*state)
    if aligned:
        while ups.step < len(ups.bits):
            ups.advance(order)
    second = order(jnp.where(upper, second_right, second_left))
    third = along(second, [(1, 0), (2, 3)])
    if aligned:
        downs = Gather(
            [
                jnp.concatenate([down_pair, out_rows[: block // 2]]),
                jnp.concatenate([down_other, out_rows[block // 2 :]]),
            ]
        )
        downs.advance(order)
    pair_second = order(project(second))
    if aligned:
        ups.advance(order)
        while downs.step < len(downs.bits):
            downs.advance(order)
    last = order(jnp.where(middle, hop_left, third))
    pair_last = project(last)
    mixed, logs = order(
        *attend_forward(queries, [pair_second, pair_last], scalars, (2, 3), state)
    )
    if aligned:
        downs.advance(order)
        up_arrays, up_plan = plan_of(
            ups.result,
            [
                [(0, block, 0, 0, D, 0), (block, block, 0, 1, D, 0)],
                [(0, block, 0, 2, D, 0), (block, block, 0, 3, D, 0)],
            ],
        )
        down_arrays, down_plan = plan_of(
            downs.result,
            [
                [
                    (0, block, 1, 0, D, 0),
                    (block, block, 1, 1, D, 0),
                    (2 * block, block // 2, 2, 0, 0, 0),
                ],
                [
                    (0, block, 1, 2, D, 0),
                    (block, block, 1, 3, D, 0),
                    (2 * block, block // 2, 2, 0, 0, block // 2),
                ],
            ],
        )
        arrays, plan = up_arrays + down_arrays, up_plan + down_plan
    else:
        arrays = [
            lax.all_gather(w_up, ("mp", "dp"), axis=0, tiled=True),
            lax.all_gather(w_down.T, ("mp", "dp"), axis=0, tiled=True),
            lax.all_gather(out_rows, "dp", axis=0, tiled=True),
        ]
        plan = [[(0, array.shape[0], n, None, 0, 0, 0)] for n, array in enumerate(arrays)]
    chunks = [first_norm, near, second, last]
    pairs = [pair_own, pair_near, pair_second, pair_last]

    (
        output,
        final_low,
        hidden_act,
        pre_grad,
        second_norm,
        middle_low,
        attended,
        middle_grad,
        attended_grad,
        deltas,
        log_rows,
        sums,
    ) = middle_call(
        scalars, vectors, tokens, mixed, logs, cotangent, teacher, arrays, plan, block
    )
    gain_two, shift_two, middle_sum, final_sum = sums[0], sums[1], sums[2], sums[3]
    down_keep, down_send, up_keep, up_send = feed_grads(
        final_low, hidden_act, second_norm, pre_grad, middle_low, attended, dp
    )

    feed = Steps(scatter_feed((up_keep, up_send), (down_keep, down_send)))
    key_grads = [None] * 4
    value_grads = [None] * 4
    firsts = [None] * 4
    query_grad = None
    feed.advance(order)
    for n in (3, 2, 1, 0):
        query_grad, key_grads[n], value_grads[n], firsts[n] = attend_backward(
            n,
            queries,
            pairs[n],
            order(attended_grad),
            log_rows,
            deltas,
            query_weight,
            pair_weight,
            scalars,
            query_grad,
            n == 0,
        )
        firsts[n] = order(firsts[n])
        if n == 3:
            back_last = along(firsts[3], [(0, 1), (3, 2)]).astype(full)
            feed.advance(order)
        elif n == 2:
            payload = order((firsts[2] + back_last).astype(low))
            back_right = along(payload, [(0, 1), (1, 2)]).astype(full)
            back_left = along(payload, [(3, 2), (2, 1)]).astype(full)
        elif n == 1:
            feed.advance(order)
            to_right = jnp.where(
                rank == 0, firsts[1], firsts[3].astype(full) + back_right
            ).astype(low)
            to_left = (firsts[1] + back_left).astype(low)
            to_right, to_left = order(to_right, to_left)
            final_right = along(to_right, [(0, 1), (1, 2), (2, 3)])
            final_left = along(to_left, [(3, 2), (2, 1), (1, 0)])
    feed.advance(order)
    qkv_keep, qkv_send, bias_sums = qkv_grads(chunks, query_grad, key_grads, value_grads, dp)
    qkv = Steps(scatter_qkv(qkv_keep, qkv_send))
    qkv.advance(order)
    first_grad = firsts[0] + final_right.astype(full) + final_left.astype(full)
    unit_one, inverse_one = norm_stats(tokens.astype(full) + table_row)
    start_part, gain_one, shift_one = norm_back(
        unit_one, inverse_one, norm_gains[0], first_grad
    )
    input_grad = middle_grad + start_part
    sequence_sum = jnp.sum(input_grad, axis=0)
    own_slot = (jnp.arange(dp) == data_rank).astype(full)
    packed = jnp.concatenate(
        [
            jnp.stack([gain_one, gain_two, shift_one, shift_two]),
            jnp.stack([bias_sums[0], bias_sums[8]]),
            jnp.stack([middle_sum, final_sum]),
            sums[8 : 8 + FF // D],
            own_slot[:, None] * sequence_sum[None, :],
        ]
    )
    qkv.advance(order)
    small = Steps(butterfly(packed))
    for _ in range(3):
        small.advance(order)
    qkv.advance(order)
    feed.advance(order)
    small.advance(order)
    qkv.advance(order)
    small.advance(order)
    qkv_grad = qkv.finish(order)
    total = small.finish(order)
    up_grad, down_grad, out_grad = feed.finish(order)
    fixed = 8 + FF // D
    chosen = (timesteps[None, :] == jnp.arange(time_table.shape[0])[:, None]).astype(full)
    table_grad = lax.dot_general(
        chosen,
        total[fixed:],
        (((1,), (0,)), ((), ())),
        precision=lax.Precision.HIGHEST,
        preferred_element_type=full,
    )
    return (
        output,
        input_grad,
        table_grad,
        total[0:2],
        total[2:4],
        qkv_grad,
        total[4:6],
        out_grad,
        total[6],
        up_grad,
        total[8:fixed].reshape(FF),
        down_grad,
        total[7],
    )


def solution(mesh):
    rows = P(both, None)
    placed = (
        rows,
        P(),
        P(),
        P(),
        P(),
        P(),
        P(None, "dp", "mp"),
        P(),
        P("mp", "dp"),
        P(),
        P("dp", "mp"),
        P(),
        P("mp", "dp"),
        P(),
        rows,
        rows,
    )
    return jax.shard_map(
        shards,
        mesh=mesh,
        in_specs=placed,
        out_specs=(
            rows,
            rows,
            P(),
            P(),
            P(),
            P(None, "dp", "mp"),
            P(),
            P("mp", "dp"),
            P(),
            P("dp", "mp"),
            P(),
            P("mp", "dp"),
            P(),
        ),
        check_vma=False,
    )
```

```python
import functools

import jax
import jax.numpy as jnp
from jax import lax
from jax.experimental import pallas as pl
from jax.experimental.pallas import tpu as pltpu
from jax.sharding import PartitionSpec as P

D = 768
HEADS = 12
HEAD_DIM = 64
FF = 3072
MAXLEN = 2048
PAIR = 2 * HEAD_DIM
PAIRS = HEADS // 2
VMEM_LIMIT = 58 << 20
SMALL_COST = pl.CostEstimate(flops=1 << 20, bytes_accessed=1 << 16, transcendentals=0)

far_below = -1e30
epsilon = 1e-05
score_scale = HEAD_DIM ** (-0.5)
low = jnp.bfloat16
full = jnp.float32
both = ("dp", "mp")


def norm_stats(values):
    center = values - jnp.mean(values, axis=-1, keepdims=True)
    spread = jnp.mean(center * center, axis=-1, keepdims=True)
    inverse = lax.rsqrt(spread + epsilon)
    return center * inverse, inverse


def norm_back(unit, inverse, gain_row, grad):
    scaled = grad * gain_row
    mean_scaled = jnp.mean(scaled, axis=-1, keepdims=True)
    mean_unit = jnp.mean(scaled * unit, axis=-1, keepdims=True)
    return (
        inverse * (scaled - mean_scaled - unit * mean_unit),
        jnp.sum(grad * unit, axis=0),
        jnp.sum(grad, axis=0),
    )


def dot_of(left_side, right_side, left_dim, right_dim):
    return lax.dot_general(
        left_side,
        right_side,
        (((left_dim,), (right_dim,)), ((), ())),
        preferred_element_type=full,
    )


def first_half(shape):
    return lax.broadcasted_iota(jnp.int32, shape, len(shape) - 1) < HEAD_DIM


def forward_kernel(numbers, first, scalars, *refs):
    count = len(numbers)
    chunk_refs = refs[:count]
    wk_ref, wv_ref, value_bias_ref = refs[count : count + 3]
    refs = refs[count + 3 :]
    if first:
        wq_ref, query_bias_ref = refs[:2]
        key_outs, value_outs = refs[2 : 2 + count], refs[2 + count : 2 + 2 * count]
        query_out, top_ref, sum_ref, acc_ref = refs[2 + 2 * count :]
        q_pair = (dot_of(chunk_refs[0][...], wq_ref[...], 1, 0) + query_bias_ref[...]).astype(low)
        q_pair = q_pair * jnp.asarray(score_scale, low)
        query_out[...] = q_pair
    else:
        q_ref, top_in, sum_in, acc_in = refs[:4]
        key_outs, value_outs = refs[4 : 4 + count], refs[4 + count : 4 + 2 * count]
        out_ref, log_ref = refs[4 + 2 * count :]
        q_pair = q_ref[...]
    weight = jnp.concatenate([wk_ref[...], wv_ref[...]], axis=1)
    keys = []
    values = []
    for n in range(count):
        both_parts = dot_of(chunk_refs[n][...], weight, 1, 0)
        keys.append(both_parts[:, :PAIR].astype(low))
        values.append((both_parts[:, PAIR:] + value_bias_ref[...]).astype(low))
        key_outs[n][...] = keys[n]
        value_outs[n][...] = values[n]
    rows = q_pair.shape[0]
    size = keys[0].shape[0]
    place = lax.broadcasted_iota(jnp.int32, (1, size), 1)
    lower = first_half((rows, PAIR))
    parts = []
    for half in range(2):
        kept = lower if half == 0 else jnp.logical_not(lower)
        q_half = jnp.where(kept, q_pair, jnp.zeros_like(q_pair))
        scores = []
        for n in range(count):
            bias = jnp.where(place + scalars[numbers[n]] * size < scalars[4], 0.0, far_below)
            scores.append(dot_of(q_half, keys[n], 1, 1) + bias)
        highest = functools.reduce(
            jnp.maximum, [jnp.max(score, axis=-1, keepdims=True) for score in scores]
        )
        totals = jnp.zeros_like(highest)
        mixed = jnp.zeros((rows, PAIR), full)
        for n in range(count):
            exp_scores = jnp.exp(scores[n] - highest)
            totals = totals + jnp.sum(exp_scores, axis=-1, keepdims=True)
            mixed = mixed + dot_of(exp_scores.astype(low), values[n], 1, 0)
        parts.append((highest, totals, mixed))
    top = jnp.where(lower, parts[0][0], parts[1][0])
    total = jnp.where(lower, parts[0][1], parts[1][1])
    mixed = jnp.where(lower, parts[0][2], parts[1][2])
    if first:
        top_ref[...] = top
        sum_ref[...] = total
        acc_ref[...] = mixed
    else:
        highest = jnp.maximum(top, top_in[...])
        here = jnp.exp(top - highest)
        before = jnp.exp(top_in[...] - highest)
        total = total * here + sum_in[...] * before
        out_ref[...] = (mixed * here + acc_in[...] * before) / total
        log_ref[...] = highest + jnp.log(total)


def attend_forward(chunks, numbers, scalars, query_weight, pair_weight, query_bias, value_bias, carried):
    rows = chunks[0].shape[0]
    count = len(chunks)
    first = carried is None
    column = lambda height, c: pl.BlockSpec((height, PAIR), lambda i, n: (0, c * PAIRS + i))
    whole = pl.BlockSpec((rows, D), lambda i, n: (0, 0))
    wide = jax.ShapeDtypeStruct((rows, D), full)
    narrow = jax.ShapeDtypeStruct((rows, D), low)
    extra = (query_weight, query_bias) if first else carried
    results = (narrow, wide, wide, wide) if first else (wide, wide)
    return pl.pallas_call(
        functools.partial(forward_kernel, numbers, first),
        out_shape=(narrow,) * (2 * count) + results,
        grid_spec=pltpu.PrefetchScalarGridSpec(
            num_scalar_prefetch=1,
            grid=(PAIRS,),
            in_specs=[whole] * count
            + [column(D, 0), column(D, 1), column(1, 0)]
            + ([column(D, 0), column(1, 0)] if first else [column(rows, 0)] * 4),
            out_specs=[column(rows, 0)] * (2 * count + len(results)),
        ),
        compiler_params=pltpu.CompilerParams(vmem_limit_bytes=VMEM_LIMIT),
        cost_estimate=SMALL_COST,
        name="attend_forward",
    )(scalars, *chunks, pair_weight, pair_weight, value_bias, *extra)


def backward_kernel(
    number,
    first,
    last,
    scalars,
    q_ref,
    k_ref,
    v_ref,
    g_ref,
    log_ref,
    delta_ref,
    wk_ref,
    wv_ref,
    *refs
):
    if last:
        wq_ref = refs[0]
        refs = refs[1:]
    if not first:
        dq_in = refs[0]
        refs = refs[1:]
    dq_ref, dk_ref, dv_ref, back_ref, accum = refs
    step = pl.program_id(0)
    rows = q_ref.shape[0]
    keys = k_ref.shape[0]
    limit = scalars[4] - scalars[number] * keys
    q_pair = q_ref[...]
    g_pair = g_ref[...]
    k_pair = k_ref[...]
    v_pair = v_ref[...]
    lower = first_half((rows, PAIR))
    lower_keys = first_half((keys, PAIR))
    place = lax.broadcasted_iota(jnp.int32, (keys, 1), 0)
    bias = jnp.where(place < limit, 0.0, far_below)
    dq = []
    dk = []
    dv = []
    for half in range(2):
        kept = lower if half == 0 else jnp.logical_not(lower)
        q_half = jnp.where(kept, q_pair, jnp.zeros_like(q_pair))
        g_half = jnp.where(kept, g_pair, jnp.zeros_like(g_pair))
        log_row = log_ref[0, half : half + 1, :]
        delta_row = delta_ref[0, half : half + 1, :]
        scores = dot_of(k_pair, q_half, 1, 1) + bias
        probs = jnp.exp(scores - log_row)
        dv.append(dot_of(probs.astype(low), g_pair, 1, 0))
        prob_grad = dot_of(v_pair, g_half, 1, 1)
        score_grad = (probs * (prob_grad - delta_row)).astype(low)
        dk.append(dot_of(score_grad, q_pair, 1, 0))
        dq.append(dot_of(score_grad, k_pair, 0, 0))
    dk_low = jnp.where(lower_keys, dk[0], dk[1]).astype(low)
    dv_low = jnp.where(lower_keys, dv[0], dv[1]).astype(low)
    dk_ref[...] = dk_low
    dv_ref[...] = dv_low
    grads = [dk_low, dv_low]
    weights = [wk_ref[...], wv_ref[...]]
    dq_all = jnp.where(lower, dq[0], dq[1])
    if not first:
        dq_all = dq_all + dq_in[...]
    back = dot_of(jnp.concatenate(grads, axis=1), jnp.concatenate(weights, axis=1), 1, 1)
    if last:
        dq_low = (dq_all * score_scale).astype(low)
        dq_ref[...] = dq_low
        back = back + dot_of(dq_low, wq_ref[...], 1, 1)
    else:
        dq_ref[...] = dq_all

    @pl.when(step == 0)
    def _():
        accum[...] = back

    @pl.when(step > 0)
    def _():
        accum[...] += back

    @pl.when(step == PAIRS - 1)
    def _():
        back_ref[...] = accum[...].astype(back_ref.dtype)


def attend_backward(
    number,
    queries,
    keys,
    values,
    grads,
    logs,
    deltas,
    query_weight,
    pair_weight,
    scalars,
    carried,
    last,
):
    rows, total = queries.shape[0], keys.shape[0]
    first = carried is None
    column = lambda count, c: pl.BlockSpec((count, PAIR), lambda i, n: (0, c * PAIRS + i))
    stats = pl.BlockSpec((1, 2, rows), lambda i, n: (i, 0, 0))
    extra = (query_weight,) * last + (() if first else (carried,))
    extra_specs = [column(D, 0)] * last + ([] if first else [column(rows, 0)])
    return pl.pallas_call(
        functools.partial(backward_kernel, number, first, last),
        out_shape=(
            jax.ShapeDtypeStruct((rows, D), low if last else full),
            jax.ShapeDtypeStruct((total, D), low),
            jax.ShapeDtypeStruct((total, D), low),
            jax.ShapeDtypeStruct((total, D), low if first else full),
        ),
        grid_spec=pltpu.PrefetchScalarGridSpec(
            num_scalar_prefetch=1,
            grid=(PAIRS,),
            in_specs=[
                column(rows, 0),
                column(total, 0),
                column(total, 0),
                column(rows, 0),
                stats,
                stats,
                column(D, 0),
                column(D, 1),
            ]
            + extra_specs,
            out_specs=[
                column(rows, 0),
                column(total, 0),
                column(total, 0),
                pl.BlockSpec((total, D), lambda i, n: (0, 0)),
            ],
            scratch_shapes=[pltpu.VMEM((total, D), full)],
        ),
        compiler_params=pltpu.CompilerParams(vmem_limit_bytes=VMEM_LIMIT),
        cost_estimate=SMALL_COST,
        name="attend_backward",
    )(
        scalars,
        queries,
        keys,
        values,
        grads,
        logs,
        deltas,
        pair_weight,
        pair_weight,
        *extra,
    )


def swap(value, axis, bit):
    count = lax.axis_size(axis)
    return lax.ppermute(value, axis, [(i, i ^ bit) for i in range(count)])


class Order:
    def __init__(self):
        self.marks = ()

    def __call__(self, *values):
        values = lax.optimization_barrier(values + self.marks)[: len(values)]
        self.marks = values
        return values[0] if len(values) == 1 else values


def outer_bits():
    bits = []
    bit = 2
    while bit < lax.axis_size("dp"):
        bits.append(bit)
        bit *= 2
    return bits


class Gather:
    def __init__(self, parts):
        self.bits = outer_bits()
        half = len(self.bits) // 2
        self.orders = [
            self.bits[half * (n % 2) :] + self.bits[: half * (n % 2)] for n in range(len(parts))
        ]
        self.result = [[([0], part)] for part in parts]
        self.step = 0

    def advance(self, order):
        held = self.result
        if self.step < len(self.bits):
            masks = [[m for mask, _ in pieces for m in mask] for pieces in held]
            blocks = [
                jnp.concatenate([array for _, array in pieces]) if self.step else pieces[0][1]
                for pieces in held
            ]
            blocks = order(*blocks)
            bits = [turn[self.step] for turn in self.orders]
            self.result = [
                [(mask, block), ([m ^ bit for m in mask], swap(block, "dp", bit))]
                for mask, block, bit in zip(masks, blocks, bits)
            ]
        else:
            arrays = order(*[array for pieces in held for _, array in pieces])
            arrays = iter(arrays)
            self.result = []
            for pieces in held:
                kept = [(masks, next(arrays)) for masks, _ in pieces]
                self.result.append(
                    kept + [([m ^ 1 for m in masks], swap(array, "dp", 1)) for masks, array in kept]
                )
        self.step += 1


def canonical_row(me, rank, block, mask, rank_mask, stride, offset):
    if mask is None:
        return offset
    row = (me ^ mask) * block + offset
    if stride:
        row = row + (rank ^ rank_mask) * stride
    return pl.multiple_of(row, 16)


def place_kernel(plan, block, *refs):
    count = len(plan)
    ins = refs[:count]
    outs = refs[count:-1]
    sems = refs[-1]
    me = lax.axis_index("dp")
    rank = lax.axis_index("mp")
    copies = []
    for ref, moves in zip(ins, plan):
        for start, size, which, mask, column, _, offset in moves:
            row = canonical_row(me, rank, block, mask, 0, 0, offset)
            copy = pltpu.make_async_copy(
                ref.at[pl.ds(start, size), :],
                outs[which].at[pl.ds(row, size), pl.ds(column * D, D)],
                sems.at[len(copies)],
            )
            copy.start()
            copies.append(copy)
    for copy in copies:
        copy.wait()


def plan_of(gathered, layouts):
    arrays = []
    plan = []
    for pieces, layout in zip(gathered, layouts):
        rows = sum(size for _, size, *_ in layout)
        for masks, array in pieces:
            moves = []
            for j, mask in enumerate(masks):
                for start, size, which, rank_mask, stride, offset in layout:
                    moves.append((j * rows + start, size, which, mask, rank_mask, stride, offset))
            arrays.append(array)
            plan.append(moves)
    return arrays, plan


def place(arrays, plan, block, shapes):
    return pl.pallas_call(
        functools.partial(place_kernel, plan, block),
        out_shape=[jax.ShapeDtypeStruct(shape, low) for shape in shapes],
        in_specs=[pl.BlockSpec(memory_space=pl.ANY)] * len(arrays),
        out_specs=[pl.BlockSpec(memory_space=pltpu.VMEM)] * len(shapes),
        scratch_shapes=[pltpu.SemaphoreType.DMA((sum(len(moves) for moves in plan),))],
        compiler_params=pltpu.CompilerParams(vmem_limit_bytes=VMEM_LIMIT),
        cost_estimate=SMALL_COST,
        name="place",
    )(*arrays)


def middle_kernel(plan, block, total, *refs):
    limit_ref, vector_ref = refs[:2]
    token_hbm, mixed_hbm, log_hbm, cot_hbm, teach_hbm = refs[2:7]
    pieces = refs[7 : 7 + total]
    (
        out_hbm,
        final_hbm,
        act_hbm,
        pre_hbm,
        second_hbm,
        middle_low_hbm,
        attended_hbm,
        middle_hbm,
        grad_hbm,
        delta_ref,
        log_ref,
        sum_ref,
    ) = refs[7 + total : 19 + total]
    (
        token,
        mixed,
        logs,
        cot,
        teach,
        up,
        down,
        proj,
        act,
        pre,
        slope,
        second,
        attended,
        middle,
        final,
        out,
        final_low,
        middle_low,
        grad,
        accum,
        in_sems,
        weight_sems,
        out_sems,
    ) = refs[19 + total :]
    targets = (up, down, proj)
    rows = token.shape[0]
    me = lax.axis_index("dp")
    rank = lax.axis_index("mp")

    def fetch(ref, scratch, n):
        copy = pltpu.make_async_copy(ref, scratch, in_sems.at[n])
        copy.start()
        return copy

    def send(scratch, ref, n):
        copy = pltpu.make_async_copy(scratch, ref, out_sems.at[n])
        copy.start()
        return copy

    gets = [
        fetch(token_hbm, token, 0),
        fetch(mixed_hbm, mixed, 1),
        fetch(log_hbm, logs, 2),
        fetch(cot_hbm, cot, 3),
        fetch(teach_hbm, teach, 4),
    ]
    loads = {0: [], 1: [], 2: []}
    number = 0
    for want in (2, 0, 1):
        for ref, moves in zip(pieces, plan):
            for start, size, which, mask, rank_mask, stride, offset in moves:
                if which != want:
                    continue
                row = canonical_row(me, rank, block, mask, rank_mask, stride, offset)
                copy = pltpu.make_async_copy(
                    ref.at[pl.ds(start, size), :],
                    targets[which].at[pl.ds(row, size), :],
                    weight_sems.at[number],
                )
                copy.start()
                loads[which].append(copy)
                number += 1

    table_row = vector_ref[0:1, :]
    out_bias = vector_ref[1:2, :]
    gain = vector_ref[2:3, :]
    shift = vector_ref[3:4, :]
    down_bias = vector_ref[4:5, :]
    weight = vector_ref[5:6, :]
    gets[0].wait()
    gets[1].wait()
    attended[...] = mixed[...].astype(low)
    puts = [send(attended, attended_hbm, 0)]
    for copy in loads[2]:
        copy.wait()
    state = token[...].astype(full) + table_row + out_bias
    state = state + dot_of(attended[...], proj[...], 1, 1)
    middle[...] = state
    unit, _ = norm_stats(state)
    second[...] = (unit * gain + shift).astype(low)
    puts.append(send(second, second_hbm, 1))
    accum[...] = jnp.zeros((rows, D), full)
    for copy in loads[0]:
        copy.wait()
    for copy in loads[1]:
        copy.wait()

    def forward(m, _):
        place = pl.ds(pl.multiple_of(m * D, D), D)
        value = dot_of(second[...], up[place, :], 1, 0) + vector_ref[pl.ds(8 + m, 1), :]
        cumulative = 0.5 + 0.5 * lax.erf(value * (0.5**0.5))
        act[m] = (value * cumulative).astype(low)
        slope[m] = cumulative + value * jnp.exp(-0.5 * value * value) * 0.3989422804014327
        accum[...] += dot_of(act[m], down[place, :], 1, 1)
        return 0

    lax.fori_loop(0, FF // D, forward, 0)
    puts.append(send(act, act_hbm, 2))
    final_state = middle[...] + accum[...] + down_bias
    out[...] = final_state.astype(low)
    puts.append(send(out, out_hbm, 3))
    gets[3].wait()
    gets[4].wait()
    place = lax.broadcasted_iota(jnp.int32, (rows, 1), 0)
    grads = cot[...].astype(full) + weight * (final_state - teach[...].astype(full))
    grads = jnp.where(place < limit_ref[5], grads, 0.0)
    final[...] = grads
    final_low[...] = grads.astype(low)
    puts.append(send(final_low, final_hbm, 4))
    sum_ref[3:4, :] = jnp.sum(grads, axis=0, keepdims=True)
    accum[...] = jnp.zeros((rows, D), full)

    def backward(m, _):
        place = pl.ds(pl.multiple_of(m * D, D), D)
        value = slope[m] * dot_of(final_low[...], down[place, :], 1, 0)
        value = value.astype(low)
        pre[m] = value
        sum_ref[pl.ds(8 + m, 1), :] = jnp.sum(value.astype(full), axis=0, keepdims=True)
        accum[...] += dot_of(value, up[place, :], 1, 1)
        return 0

    lax.fori_loop(0, FF // D, backward, 0)
    puts.append(send(pre, pre_hbm, 5))
    unit, inverse = norm_stats(middle[...])
    second_grad = accum[...]
    sum_ref[0:1, :] = jnp.sum(second_grad * unit, axis=0, keepdims=True)
    sum_ref[1:2, :] = jnp.sum(second_grad, axis=0, keepdims=True)
    scaled = second_grad * gain
    mean_scaled = jnp.mean(scaled, axis=-1, keepdims=True)
    mean_unit = jnp.mean(scaled * unit, axis=-1, keepdims=True)
    total_grad = final[...] + inverse * (scaled - mean_scaled - unit * mean_unit)
    middle[...] = total_grad
    puts.append(send(middle, middle_hbm, 6))
    middle_low[...] = total_grad.astype(low)
    puts.append(send(middle_low, middle_low_hbm, 7))
    sum_ref[2:3, :] = jnp.sum(total_grad, axis=0, keepdims=True)
    attended_grad = dot_of(middle_low[...], proj[...], 1, 0).astype(low)
    grad[...] = attended_grad
    puts.append(send(grad, grad_hbm, 8))
    gets[2].wait()
    head = lax.broadcasted_iota(jnp.int32, (16, D), 0)
    lane = lax.broadcasted_iota(jnp.int32, (16, D), 1)
    member = jnp.where(lane // HEAD_DIM == head, 1.0, 0.0)
    leader = jnp.where(lane == head * HEAD_DIM, 1.0, 0.0)
    exact = functools.partial(
        lax.dot_general,
        dimension_numbers=(((1,), (1,)), ((), ())),
        precision=lax.Precision.HIGHEST,
        preferred_element_type=full,
    )
    deltas = exact(member, attended_grad.astype(full) * mixed[...])
    tops = exact(leader, logs[...])
    for pair in range(PAIRS):
        delta_ref[pair] = deltas[2 * pair : 2 * pair + 2]
        log_ref[pair] = tops[2 * pair : 2 * pair + 2]
    for copy in puts:
        copy.wait()


def middle_call(limit, vectors, tokens, mixed, logs, cot, teach, arrays, plan, block):
    rows = tokens.shape[0]
    hidden = FF // D
    narrow = jax.ShapeDtypeStruct((rows, D), low)
    wide = jax.ShapeDtypeStruct((rows, D), full)
    many = jax.ShapeDtypeStruct((hidden, rows, D), low)
    stats = jax.ShapeDtypeStruct((PAIRS, 2, rows), full)
    anywhere = pl.BlockSpec(memory_space=pl.ANY)
    inside = pl.BlockSpec(memory_space=pltpu.VMEM)
    moves = sum(len(part) for part in plan)
    return pl.pallas_call(
        functools.partial(middle_kernel, plan, block, len(arrays)),
        out_shape=(
            narrow,
            narrow,
            many,
            many,
            narrow,
            narrow,
            narrow,
            wide,
            narrow,
            stats,
            stats,
            jax.ShapeDtypeStruct((8 + 8, D), full),
        ),
        in_specs=[pl.BlockSpec(memory_space=pltpu.SMEM), inside]
        + [anywhere] * (5 + len(arrays)),
        out_specs=[anywhere] * 9 + [inside] * 3,
        scratch_shapes=[
            pltpu.VMEM((rows, D), low),
            pltpu.VMEM((rows, D), full),
            pltpu.VMEM((rows, D), full),
            pltpu.VMEM((rows, D), low),
            pltpu.VMEM((rows, D), low),
            pltpu.VMEM((FF, D), low),
            pltpu.VMEM((FF, D), low),
            pltpu.VMEM((D, D), low),
            pltpu.VMEM((hidden, rows, D), low),
            pltpu.VMEM((hidden, rows, D), low),
            pltpu.VMEM((hidden, rows, D), full),
            pltpu.VMEM((rows, D), low),
            pltpu.VMEM((rows, D), low),
            pltpu.VMEM((rows, D), full),
            pltpu.VMEM((rows, D), full),
            pltpu.VMEM((rows, D), low),
            pltpu.VMEM((rows, D), low),
            pltpu.VMEM((rows, D), low),
            pltpu.VMEM((rows, D), low),
            pltpu.VMEM((rows, D), full),
            pltpu.SemaphoreType.DMA((5,)),
            pltpu.SemaphoreType.DMA((moves,)),
            pltpu.SemaphoreType.DMA((9,)),
        ],
        compiler_params=pltpu.CompilerParams(vmem_limit_bytes=VMEM_LIMIT),
        cost_estimate=SMALL_COST,
        name="middle",
    )(limit, vectors, tokens, mixed, logs, cot, teach, *arrays)


def feed_grad_kernel(
    final_ref, act_ref, second_ref, pre_ref, middle_ref, attended_ref, *refs
):
    down_keep, down_send, up_keep, up_send, left, right = refs
    block = down_keep.shape[2]
    m = pl.program_id(0)
    even = lax.axis_index("dp") % 2 == 0

    @pl.when(m == 0)
    def _():
        left[...] = final_ref[...].T
        right[...] = second_ref[...].T

    def store(value, keep, send, index):
        for outer in range(down_keep.shape[1]):
            first = value[2 * outer * block : (2 * outer + 1) * block]
            other = value[(2 * outer + 1) * block : (2 * outer + 2) * block]
            keep[index, outer] = jnp.where(even, first, other).astype(low)
            send[index, outer] = jnp.where(even, other, first).astype(low)

    @pl.when(m < FF // D)
    def _():
        store(dot_of(left[...], act_ref[0], 1, 0), down_keep, down_send, 0)
        store(dot_of(right[...], pre_ref[0], 1, 0), up_keep, up_send, 0)

    @pl.when(m == FF // D)
    def _():
        store(dot_of(middle_ref[...].T, attended_ref[...], 1, 0), up_keep, up_send, 0)


def feed_grads(final_low, act, second, pre, middle_low, attended, dp):
    rows = final_low.shape[0]
    hidden = FF // D
    whole = pl.BlockSpec((rows, D), lambda m: (0, 0))
    last = hidden - 1
    slice_of = pl.BlockSpec((1, rows, D), lambda m: (jnp.minimum(m, last), 0, 0))
    shape = (hidden, dp // 2, D // dp, D)
    longer = (hidden + 1,) + shape[1:]
    down_spec = pl.BlockSpec((1,) + shape[1:], lambda m: (jnp.minimum(m, last), 0, 0, 0))
    up_spec = pl.BlockSpec((1,) + shape[1:], lambda m: (m, 0, 0, 0))
    return pl.pallas_call(
        feed_grad_kernel,
        out_shape=[jax.ShapeDtypeStruct(shape, low)] * 2
        + [jax.ShapeDtypeStruct(longer, low)] * 2,
        grid=(hidden + 1,),
        in_specs=[whole, slice_of, whole, slice_of, whole, whole],
        out_specs=[down_spec, down_spec, up_spec, up_spec],
        scratch_shapes=[pltpu.VMEM((D, rows), low)] * 2,
        compiler_params=pltpu.CompilerParams(vmem_limit_bytes=VMEM_LIMIT),
        cost_estimate=SMALL_COST,
        name="feed_grads",
    )(final_low, act, second, pre, middle_low, attended)


def qkv_grad_kernel(count, *refs):
    chunk_refs = refs[:count]
    query_ref = refs[count]
    key_refs = refs[count + 1 : 2 * count + 1]
    value_refs = refs[2 * count + 1 : 3 * count + 1]
    keep_ref, send_ref, sum_ref, turned = refs[3 * count + 1 :]
    block = keep_ref.shape[2]
    rows = query_ref.shape[0]
    c = pl.program_id(0)
    even = lax.axis_index("dp") % 2 == 0
    ones = jnp.ones((16, rows), low)

    def store(value):
        for outer in range(keep_ref.shape[1]):
            first = value[2 * outer * block : (2 * outer + 1) * block]
            other = value[(2 * outer + 1) * block : (2 * outer + 2) * block]
            keep_ref[0, outer] = jnp.where(even, first, other).astype(low)
            send_ref[0, outer] = jnp.where(even, other, first).astype(low)

    @pl.when(c == 0)
    def _():
        for n in range(count):
            turned[n] = chunk_refs[n][...].T
        store(dot_of(turned[0], query_ref[...], 1, 0))
        sum_ref[0:8, :] = dot_of(ones, query_ref[...], 1, 0)[0:8]

    def many(sources):
        value = dot_of(turned[0], sources[0][...], 1, 0)
        for n in range(1, count):
            value = value + dot_of(turned[n], sources[n][...], 1, 0)
        store(value)

    @pl.when(c == 1)
    def _():
        many(key_refs)

    @pl.when(c == 2)
    def _():
        many(value_refs)
        value = dot_of(ones, value_refs[0][...], 1, 0)
        for n in range(1, count):
            value = value + dot_of(ones, value_refs[n][...], 1, 0)
        sum_ref[8:16, :] = value[0:8]


def qkv_grads(chunks, query_grad, key_grads, value_grads, dp):
    rows = query_grad.shape[0]
    count = len(chunks)
    whole = pl.BlockSpec((rows, D), lambda c: (0, 0))
    shape = (3, dp // 2, D // dp, D)
    part = pl.BlockSpec((1,) + shape[1:], lambda c: (c, 0, 0, 0))
    return pl.pallas_call(
        functools.partial(qkv_grad_kernel, count),
        out_shape=[jax.ShapeDtypeStruct(shape, low)] * 2
        + [jax.ShapeDtypeStruct((16, D), full)],
        grid=(3,),
        in_specs=[whole] * (3 * count + 1),
        out_specs=[part, part, pl.BlockSpec((16, D), lambda c: (0, 0))],
        scratch_shapes=[pltpu.VMEM((count, D, rows), low)],
        compiler_params=pltpu.CompilerParams(vmem_limit_bytes=VMEM_LIMIT),
        cost_estimate=SMALL_COST,
        name="qkv_grads",
    )(*chunks, query_grad, *key_grads, *value_grads)


def two_parts(value, axis, mine):
    keep = lax.dynamic_index_in_dim(value, mine, axis, keepdims=False)
    send = lax.dynamic_index_in_dim(value, 1 - mine, axis, keepdims=False)
    return keep, send.astype(low)


def scatter_dp(parts):
    bits = outer_bits()
    half = len(bits) // 2
    orders = [bits[half * (n % 2) :] + bits[: half * (n % 2)] for n in range(len(parts))]
    me = lax.axis_index("dp")
    sends = yield [send for _, send in parts]
    held = [
        (keep.astype(full) + swap(send, "dp", 1).astype(full)).astype(low)
        for (keep, _), send in zip(parts, sends)
    ]
    held = [
        value.reshape(value.shape[:1] + (2,) * len(bits) + value.shape[2:]) for value in held
    ]
    axes = [list(reversed(bits)) for _ in parts]
    for step in range(len(bits)):
        parts = []
        for n, value in enumerate(held):
            bit = orders[n][step]
            axis = 1 + axes[n].index(bit)
            axes[n].remove(bit)
            parts.append(two_parts(value, axis, (me // bit) % 2))
        sends = yield [send for _, send in parts]
        held = [
            keep.astype(full) + swap(sends[n], "dp", orders[n][step]).astype(full)
            for n, (keep, _) in enumerate(parts)
        ]
        if step < len(bits) - 1:
            held = [value.astype(low) for value in held]
    return held


def scatter_mp(values):
    rank = lax.axis_index("mp")
    for bit in (2, 1):
        parts = []
        for value in values:
            pair = value.reshape((2, value.shape[0] // 2) + value.shape[1:])
            parts.append(two_parts(pair, 0, (rank // bit) % 2))
        sends = yield [send for _, send in parts]
        values = [
            keep.astype(full) + swap(send, "mp", bit).astype(full)
            for (keep, _), send in zip(parts, sends)
        ]
    return [value[0] for value in values]


def scatter_feed(up_parts, down_parts):
    mp = lax.axis_size("mp")
    up_own, down_own = yield from scatter_dp([up_parts, down_parts])
    block = down_own.shape[1]
    out_own = up_own[mp].reshape(block, mp, -1).transpose(1, 0, 2)
    tall, out_grad = yield from scatter_mp(
        [jnp.concatenate([up_own[:mp], down_own], axis=1), out_own]
    )
    return tall[:block], tall[block:].T, out_grad.T


def scatter_qkv(keep, send):
    rank = lax.axis_index("mp")
    left_part, right_part = yield from scatter_dp(
        [(keep[..., : D // 2], send[..., : D // 2]), (keep[..., D // 2 :], send[..., D // 2 :])]
    )
    upper = rank >= 2
    odd = rank % 2 == 1
    (send,) = yield [jnp.where(upper, left_part, right_part).astype(low)]
    keep = jnp.where(upper, right_part, left_part) + swap(send, "mp", 2).astype(full)
    width = D // lax.axis_size("mp")
    (send,) = yield [jnp.where(odd, keep[..., :width], keep[..., width:]).astype(low)]
    return jnp.where(odd, keep[..., width:], keep[..., :width]) + swap(
        send, "mp", 1
    ).astype(full)


def butterfly(value):
    for bit in [1] + outer_bits():
        (value,) = yield [value]
        value = value + swap(value, "dp", bit)
    for bit in (1, 2):
        (value,) = yield [value]
        value = value + swap(value, "mp", bit)
    return value


class Steps:
    def __init__(self, steps):
        self.steps = steps
        self.pending = next(steps)
        self.result = None

    def advance(self, order):
        if self.pending is None:
            return
        sends = order(*self.pending)
        sends = [sends] if len(self.pending) == 1 else list(sends)
        try:
            self.pending = self.steps.send(sends)
        except StopIteration as stop:
            self.pending = None
            self.result = stop.value

    def finish(self, order):
        while self.pending is not None:
            self.advance(order)
        return self.result


def shards(
    tokens_in,
    timesteps,
    lengths,
    time_table,
    norm_gains,
    norm_biases,
    w_qkv,
    qv_bias,
    w_out,
    out_bias,
    w_up,
    up_bias,
    w_down,
    down_bias,
    cotangent,
    teacher,
):
    rank = lax.axis_index("mp")
    data_rank = lax.axis_index("dp")
    mp = lax.axis_size("mp")
    dp = lax.axis_size("dp")
    own_rows = tokens_in.shape[0]
    length = lax.dynamic_index_in_dim(lengths, data_rank, keepdims=False)
    own_time = lax.dynamic_index_in_dim(timesteps, data_rank, keepdims=False)
    odd = rank % 2 == 1
    upper = rank >= 2
    middle = jnp.logical_or(rank == 1, rank == 2)
    order = Order()
    along = lambda value, pairs: lax.ppermute(value, "mp", pairs)

    block = w_qkv.shape[1]
    aligned = block % 32 == 0
    narrow = order(jnp.concatenate([w_qkv.reshape(3 * block, -1), w_out.T]))
    first_swap = swap(narrow, "mp", 1)
    up_own = order(w_up)
    up_swap = swap(up_own, "mp", 1)
    pair = order(
        jnp.concatenate(
            [jnp.where(odd, first_swap, narrow), jnp.where(odd, narrow, first_swap)], axis=1
        )
    )
    second_swap = swap(pair, "mp", 2)
    tokens, lengths, own_time, norm_gains, norm_biases, out_bias, down_bias, up_bias, length = order(
        tokens_in, lengths, own_time, norm_gains, norm_biases, out_bias, down_bias, up_bias, length
    )
    table_row = lax.dynamic_slice_in_dim(time_table, own_time, 1).astype(full)
    unit_one, _ = norm_stats(tokens.astype(full) + table_row)
    first_norm = (unit_one * norm_gains[0] + norm_biases[0]).astype(low)
    loss_weight = lengths.shape[0] * MAXLEN / jnp.sum(lengths).astype(full)
    vectors = jnp.concatenate(
        [
            table_row,
            out_bias[None],
            norm_gains[1:2],
            norm_biases[1:2],
            down_bias[None],
            jnp.full((3, D), loss_weight),
            up_bias.reshape(-1, D),
            jnp.zeros((4, D), full),
        ]
    )
    scalars = jnp.stack(
        [
            rank,
            jnp.where(rank == 0, 1, rank - 1),
            jnp.where(upper, rank - 2, rank + 2),
            jnp.where(middle, rank + 1, 3 - rank),
            length,
            length - rank * own_rows,
        ]
    ).astype(jnp.int32)
    first_norm, vectors, scalars = order(first_norm, vectors, scalars)
    wide = jnp.concatenate(
        [jnp.where(upper, second_swap, pair), jnp.where(upper, pair, second_swap)], axis=1
    )
    qkv_rows, out_rows = wide[: 3 * block], wide[3 * block :]
    if aligned:
        split = 3 * block // 2
        qkv_gather = Gather([qkv_rows[:split], qkv_rows[split:]])
        qkv_gather.advance(order)
    sent, up_pair = order(first_norm, jnp.concatenate([up_own, up_swap]))
    from_left = along(sent, [(0, 1), (1, 2), (2, 3)])
    from_right = along(sent, [(1, 0), (2, 1), (3, 2)])
    down_own = order(w_down.T)
    down_swap = swap(down_own, "mp", 1)
    up_other = swap(up_pair, "mp", 2)

    if aligned:
        while qkv_gather.step < len(qkv_gather.bits):
            qkv_gather.advance(order)
    hop_right, hop_left = order(from_left, from_right)
    second_right = along(hop_right, [(1, 2), (2, 3)])
    second_left = along(hop_left, [(1, 0), (2, 1)])
    near = jnp.where(rank == 0, hop_left, hop_right)
    if aligned:
        qkv_gather.advance(order)
        arrays, plan = plan_of(
            qkv_gather.result,
            [
                [(0, block, 0, 0, 0, 0), (block, split - block, 1, 0, 0, 0)],
                [
                    (0, 2 * block - split, 1, 0, 0, split - block),
                    (2 * block - split, block, 1, 1, 0, 0),
                ],
            ],
        )
        query_weight, pair_weight = place(arrays, plan, block, [(D, D), (D, 2 * D)])
    else:
        weights = lax.all_gather(qkv_rows.reshape(3, block, D), "dp", axis=1, tiled=True)
        query_weight = weights[0]
        pair_weight = jnp.concatenate([weights[1], weights[2]], axis=1)
    down_pair, up_other, query_weight, pair_weight = order(
        jnp.concatenate([down_own, down_swap]), up_other, query_weight, pair_weight
    )
    down_other = swap(down_pair, "mp", 2)

    if aligned:
        ups = Gather([up_pair, up_other])
        ups.advance(order)
    attend = lambda chunks, numbers, carried: order(
        *attend_forward(
            chunks,
            numbers,
            scalars,
            query_weight,
            pair_weight,
            qv_bias[0:1],
            qv_bias[1:2],
            carried,
        )
    )
    key_own, key_near, value_own, value_near, queries, *state = attend(
        [first_norm, near], (0, 1), None
    )
    if aligned:
        while ups.step < len(ups.bits):
            ups.advance(order)
    second = order(jnp.where(upper, second_right, second_left))
    third = along(second, [(1, 0), (2, 3)])
    if aligned:
        downs = Gather(
            [
                jnp.concatenate([down_pair, out_rows[: block // 2]]),
                jnp.concatenate([down_other, out_rows[block // 2 :]]),
            ]
        )
        downs.advance(order)
        ups.advance(order)
        while downs.step < len(downs.bits):
            downs.advance(order)
    last = order(jnp.where(middle, hop_left, third))
    key_second, key_last, value_second, value_last, mixed, logs = attend(
        [second, last], (2, 3), (queries, *state)
    )
    if aligned:
        downs.advance(order)
        up_arrays, up_plan = plan_of(
            ups.result,
            [
                [(0, block, 0, 0, D, 0), (block, block, 0, 1, D, 0)],
                [(0, block, 0, 2, D, 0), (block, block, 0, 3, D, 0)],
            ],
        )
        down_arrays, down_plan = plan_of(
            downs.result,
            [
                [
                    (0, block, 1, 0, D, 0),
                    (block, block, 1, 1, D, 0),
                    (2 * block, block // 2, 2, 0, 0, 0),
                ],
                [
                    (0, block, 1, 2, D, 0),
                    (block, block, 1, 3, D, 0),
                    (2 * block, block // 2, 2, 0, 0, block // 2),
                ],
            ],
        )
        arrays, plan = up_arrays + down_arrays, up_plan + down_plan
    else:
        arrays = [
            lax.all_gather(w_up, ("mp", "dp"), axis=0, tiled=True),
            lax.all_gather(w_down.T, ("mp", "dp"), axis=0, tiled=True),
            lax.all_gather(out_rows, "dp", axis=0, tiled=True),
        ]
        plan = [[(0, array.shape[0], n, None, 0, 0, 0)] for n, array in enumerate(arrays)]
    chunks = [first_norm, near, second, last]
    keys = [key_own, key_near, key_second, key_last]
    values = [value_own, value_near, value_second, value_last]

    (
        output,
        final_low,
        hidden_act,
        pre_grad,
        second_norm,
        middle_low,
        attended,
        middle_grad,
        attended_grad,
        deltas,
        log_rows,
        sums,
    ) = middle_call(
        scalars, vectors, tokens, mixed, logs, cotangent, teacher, arrays, plan, block
    )
    gain_two, shift_two, middle_sum, final_sum = sums[0], sums[1], sums[2], sums[3]
    down_keep, down_send, up_keep, up_send = feed_grads(
        final_low, hidden_act, second_norm, pre_grad, middle_low, attended, dp
    )

    feed = Steps(scatter_feed((up_keep, up_send), (down_keep, down_send)))
    key_grads = [None] * 4
    value_grads = [None] * 4
    firsts = [None] * 4
    query_grad = None
    feed.advance(order)
    for n in (3, 2, 1, 0):
        query_grad, key_grads[n], value_grads[n], firsts[n] = attend_backward(
            n,
            queries,
            keys[n],
            values[n],
            order(attended_grad),
            log_rows,
            deltas,
            query_weight,
            pair_weight,
            scalars,
            query_grad,
            n == 0,
        )
        firsts[n] = order(firsts[n])
        if n == 3:
            back_last = along(firsts[3], [(0, 1), (3, 2)]).astype(full)
            feed.advance(order)
        elif n == 2:
            payload = order((firsts[2] + back_last).astype(low))
            back_right = along(payload, [(0, 1), (1, 2)]).astype(full)
            back_left = along(payload, [(3, 2), (2, 1)]).astype(full)
        elif n == 1:
            feed.advance(order)
            to_right = jnp.where(
                rank == 0, firsts[1], firsts[3].astype(full) + back_right
            ).astype(low)
            to_left = (firsts[1] + back_left).astype(low)
            to_right, to_left = order(to_right, to_left)
            final_right = along(to_right, [(0, 1), (1, 2), (2, 3)])
            final_left = along(to_left, [(3, 2), (2, 1), (1, 0)])
    query_grad, final_right, final_left = order(query_grad, final_right, final_left)
    qkv_keep, qkv_send, bias_sums = qkv_grads(chunks, query_grad, key_grads, value_grads, dp)
    qkv = Steps(scatter_qkv(qkv_keep, qkv_send))
    qkv.advance(order)
    feed.advance(order)
    qkv.advance(order)
    tokens, first_own = order(tokens, firsts[0])
    first_grad = first_own + final_right.astype(full) + final_left.astype(full)
    unit_one, inverse_one = norm_stats(tokens.astype(full) + table_row)
    start_part, gain_one, shift_one = norm_back(
        unit_one, inverse_one, norm_gains[0], first_grad
    )
    input_grad = middle_grad + start_part
    sequence_sum = jnp.sum(input_grad, axis=0)
    own_slot = (jnp.arange(dp) == data_rank).astype(full)
    packed = jnp.concatenate(
        [
            jnp.stack([gain_one, gain_two, shift_one, shift_two]),
            jnp.stack([bias_sums[0], bias_sums[8]]),
            jnp.stack([middle_sum, final_sum]),
            sums[8 : 8 + FF // D],
            own_slot[:, None] * sequence_sum[None, :],
        ]
    )
    small = Steps(butterfly(packed))
    small.advance(order)
    small.advance(order)
    qkv.advance(order)
    small.advance(order)
    feed.advance(order)
    small.advance(order)
    qkv.advance(order)
    small.advance(order)
    qkv_grad = qkv.finish(order)
    total = small.finish(order)
    up_grad, down_grad, out_grad = feed.finish(order)
    fixed = 8 + FF // D
    chosen = (timesteps[None, :] == jnp.arange(time_table.shape[0])[:, None]).astype(full)
    table_grad = lax.dot_general(
        chosen,
        total[fixed:],
        (((1,), (0,)), ((), ())),
        precision=lax.Precision.HIGHEST,
        preferred_element_type=full,
    )
    return (
        output,
        input_grad,
        table_grad,
        total[0:2],
        total[2:4],
        qkv_grad,
        total[4:6],
        out_grad,
        total[6],
        up_grad,
        total[8:fixed].reshape(FF),
        down_grad,
        total[7],
    )


def solution(mesh):
    rows = P(both, None)
    placed = (
        rows,
        P(),
        P(),
        P(),
        P(),
        P(),
        P(None, "dp", "mp"),
        P(),
        P("mp", "dp"),
        P(),
        P("dp", "mp"),
        P(),
        P("mp", "dp"),
        P(),
        rows,
        rows,
    )
    return jax.shard_map(
        shards,
        mesh=mesh,
        in_specs=placed,
        out_specs=(
            rows,
            rows,
            P(),
            P(),
            P(),
            P(None, "dp", "mp"),
            P(),
            P("mp", "dp"),
            P(),
            P("dp", "mp"),
            P(),
            P("mp", "dp"),
            P(),
        ),
        check_vma=False,
    )
```

```python
import functools

import jax
import jax.numpy as jnp
from jax import lax
from jax.experimental import pallas as pl
from jax.experimental.pallas import tpu as pltpu
from jax.sharding import PartitionSpec as P

D = 768
HEADS = 12
HEAD_DIM = 64
FF = 3072
MAXLEN = 2048
PAIR = 2 * HEAD_DIM
PAIRS = HEADS // 2
VMEM_LIMIT = 58 << 20
SMALL_COST = pl.CostEstimate(flops=1 << 20, bytes_accessed=1 << 16, transcendentals=0)

far_below = -1e30
epsilon = 1e-05
score_scale = HEAD_DIM ** (-0.5)
low = jnp.bfloat16
full = jnp.float32
both = ("dp", "mp")


def norm_stats(values):
    center = values - jnp.mean(values, axis=-1, keepdims=True)
    spread = jnp.mean(center * center, axis=-1, keepdims=True)
    inverse = lax.rsqrt(spread + epsilon)
    return center * inverse, inverse


def norm_back(unit, inverse, gain_row, grad):
    scaled = grad * gain_row
    mean_scaled = jnp.mean(scaled, axis=-1, keepdims=True)
    mean_unit = jnp.mean(scaled * unit, axis=-1, keepdims=True)
    return (
        inverse * (scaled - mean_scaled - unit * mean_unit),
        jnp.sum(grad * unit, axis=0),
        jnp.sum(grad, axis=0),
    )


def dot_of(left_side, right_side, left_dim, right_dim):
    return lax.dot_general(
        left_side,
        right_side,
        (((left_dim,), (right_dim,)), ((), ())),
        preferred_element_type=full,
    )


def first_half(shape):
    return lax.broadcasted_iota(jnp.int32, shape, len(shape) - 1) < HEAD_DIM


def forward_kernel(numbers, first, final, scalars, *refs):
    count = len(numbers)
    chunk_refs = refs[:count]
    wk_ref, wv_ref, value_bias_ref = refs[count : count + 3]
    refs = refs[count + 3 :]
    if first:
        wq_ref, query_bias_ref = refs[:2]
        key_outs, value_outs = refs[2 : 2 + count], refs[2 + count : 2 + 2 * count]
        query_out, top_ref, sum_ref, acc_ref = refs[2 + 2 * count :]
        q_pair = (dot_of(chunk_refs[0][...], wq_ref[...], 1, 0) + query_bias_ref[...]).astype(low)
        q_pair = q_pair * jnp.asarray(score_scale, low)
        query_out[...] = q_pair
    else:
        q_ref, top_in, sum_in, acc_in = refs[:4]
        key_outs, value_outs = refs[4 : 4 + count], refs[4 + count : 4 + 2 * count]
        results = refs[4 + 2 * count :]
        q_pair = q_ref[...]
    weight = jnp.concatenate([wk_ref[...], wv_ref[...]], axis=1)
    keys = []
    values = []
    for n in range(count):
        both_parts = dot_of(chunk_refs[n][...], weight, 1, 0)
        keys.append(both_parts[:, :PAIR].astype(low))
        values.append((both_parts[:, PAIR:] + value_bias_ref[...]).astype(low))
        key_outs[n][...] = keys[n]
        value_outs[n][...] = values[n]
    rows = q_pair.shape[0]
    size = keys[0].shape[0]
    place = lax.broadcasted_iota(jnp.int32, (1, size), 1)
    lower = first_half((rows, PAIR))
    parts = []
    for half in range(2):
        kept = lower if half == 0 else jnp.logical_not(lower)
        q_half = jnp.where(kept, q_pair, jnp.zeros_like(q_pair))
        scores = []
        for n in range(count):
            bias = jnp.where(place + scalars[numbers[n]] * size < scalars[4], 0.0, far_below)
            scores.append(dot_of(q_half, keys[n], 1, 1) + bias)
        highest = functools.reduce(
            jnp.maximum, [jnp.max(score, axis=-1, keepdims=True) for score in scores]
        )
        totals = jnp.zeros_like(highest)
        mixed = jnp.zeros((rows, PAIR), full)
        for n in range(count):
            exp_scores = jnp.exp(scores[n] - highest)
            totals = totals + jnp.sum(exp_scores, axis=-1, keepdims=True)
            mixed = mixed + dot_of(exp_scores.astype(low), values[n], 1, 0)
        parts.append((highest, totals, mixed))
    top = jnp.where(lower, parts[0][0], parts[1][0])
    total = jnp.where(lower, parts[0][1], parts[1][1])
    mixed = jnp.where(lower, parts[0][2], parts[1][2])
    if first:
        top_ref[...] = top
        sum_ref[...] = total
        acc_ref[...] = mixed
    else:
        highest = jnp.maximum(top, top_in[...])
        here = jnp.exp(top - highest)
        before = jnp.exp(top_in[...] - highest)
        total = total * here + sum_in[...] * before
        mixed = mixed * here + acc_in[...] * before
        if final:
            results[0][...] = mixed / total
            results[1][...] = highest + jnp.log(total)
        else:
            results[0][...] = highest
            results[1][...] = total
            results[2][...] = mixed


def attend_forward(chunks, numbers, scalars, query_weight, pair_weight, query_bias, value_bias, carried):
    rows = chunks[0].shape[0]
    count = len(chunks)
    first = carried is None
    final = 3 in numbers
    column = lambda height, c: pl.BlockSpec((height, PAIR), lambda i, n: (0, c * PAIRS + i))
    whole = pl.BlockSpec((rows, D), lambda i, n: (0, 0))
    wide = jax.ShapeDtypeStruct((rows, D), full)
    narrow = jax.ShapeDtypeStruct((rows, D), low)
    extra = (query_weight, query_bias) if first else carried
    results = (narrow,) * first + (wide,) * (2 if final else 3)
    return pl.pallas_call(
        functools.partial(forward_kernel, numbers, first, final),
        out_shape=(narrow,) * (2 * count) + results,
        grid_spec=pltpu.PrefetchScalarGridSpec(
            num_scalar_prefetch=1,
            grid=(PAIRS,),
            in_specs=[whole] * count
            + [column(D, 0), column(D, 1), column(1, 0)]
            + ([column(D, 0), column(1, 0)] if first else [column(rows, 0)] * 4),
            out_specs=[column(rows, 0)] * (2 * count + len(results)),
        ),
        compiler_params=pltpu.CompilerParams(vmem_limit_bytes=VMEM_LIMIT),
        cost_estimate=SMALL_COST,
        name="attend_forward",
    )(scalars, *chunks, pair_weight, pair_weight, value_bias, *extra)


def backward_kernel(
    number,
    first,
    last,
    scalars,
    q_ref,
    k_ref,
    v_ref,
    g_ref,
    log_ref,
    delta_ref,
    wk_ref,
    wv_ref,
    *refs
):
    if last:
        wq_ref = refs[0]
        refs = refs[1:]
    if not first:
        dq_in = refs[0]
        refs = refs[1:]
    dq_ref, dk_ref, dv_ref, back_ref, accum = refs
    step = pl.program_id(0)
    rows = q_ref.shape[0]
    keys = k_ref.shape[0]
    limit = scalars[4] - scalars[number] * keys
    q_pair = q_ref[...]
    g_pair = g_ref[...]
    k_pair = k_ref[...]
    v_pair = v_ref[...]
    lower = first_half((rows, PAIR))
    lower_keys = first_half((keys, PAIR))
    place = lax.broadcasted_iota(jnp.int32, (keys, 1), 0)
    bias = jnp.where(place < limit, 0.0, far_below)
    dq = []
    dk = []
    dv = []
    for half in range(2):
        kept = lower if half == 0 else jnp.logical_not(lower)
        q_half = jnp.where(kept, q_pair, jnp.zeros_like(q_pair))
        g_half = jnp.where(kept, g_pair, jnp.zeros_like(g_pair))
        log_row = log_ref[0, half : half + 1, :]
        delta_row = delta_ref[0, half : half + 1, :]
        scores = dot_of(k_pair, q_half, 1, 1) + bias
        probs = jnp.exp(scores - log_row)
        dv.append(dot_of(probs.astype(low), g_pair, 1, 0))
        prob_grad = dot_of(v_pair, g_half, 1, 1)
        score_grad = (probs * (prob_grad - delta_row)).astype(low)
        dk.append(dot_of(score_grad, q_pair, 1, 0))
        dq.append(dot_of(score_grad, k_pair, 0, 0))
    dk_low = jnp.where(lower_keys, dk[0], dk[1]).astype(low)
    dv_low = jnp.where(lower_keys, dv[0], dv[1]).astype(low)
    dk_ref[...] = dk_low
    dv_ref[...] = dv_low
    grads = [dk_low, dv_low]
    weights = [wk_ref[...], wv_ref[...]]
    dq_all = jnp.where(lower, dq[0], dq[1])
    if not first:
        dq_all = dq_all + dq_in[...]
    back = dot_of(jnp.concatenate(grads, axis=1), jnp.concatenate(weights, axis=1), 1, 1)
    if last:
        dq_low = (dq_all * score_scale).astype(low)
        dq_ref[...] = dq_low
        back = back + dot_of(dq_low, wq_ref[...], 1, 1)
    else:
        dq_ref[...] = dq_all

    @pl.when(step == 0)
    def _():
        accum[...] = back

    @pl.when(step > 0)
    def _():
        accum[...] += back

    @pl.when(step == PAIRS - 1)
    def _():
        back_ref[...] = accum[...].astype(back_ref.dtype)


def attend_backward(
    number,
    queries,
    keys,
    values,
    grads,
    logs,
    deltas,
    query_weight,
    pair_weight,
    scalars,
    carried,
    last,
):
    rows, total = queries.shape[0], keys.shape[0]
    first = carried is None
    column = lambda count, c: pl.BlockSpec((count, PAIR), lambda i, n: (0, c * PAIRS + i))
    stats = pl.BlockSpec((1, 2, rows), lambda i, n: (i, 0, 0))
    extra = (query_weight,) * last + (() if first else (carried,))
    extra_specs = [column(D, 0)] * last + ([] if first else [column(rows, 0)])
    return pl.pallas_call(
        functools.partial(backward_kernel, number, first, last),
        out_shape=(
            jax.ShapeDtypeStruct((rows, D), low if last else full),
            jax.ShapeDtypeStruct((total, D), low),
            jax.ShapeDtypeStruct((total, D), low),
            jax.ShapeDtypeStruct((total, D), low if first else full),
        ),
        grid_spec=pltpu.PrefetchScalarGridSpec(
            num_scalar_prefetch=1,
            grid=(PAIRS,),
            in_specs=[
                column(rows, 0),
                column(total, 0),
                column(total, 0),
                column(rows, 0),
                stats,
                stats,
                column(D, 0),
                column(D, 1),
            ]
            + extra_specs,
            out_specs=[
                column(rows, 0),
                column(total, 0),
                column(total, 0),
                pl.BlockSpec((total, D), lambda i, n: (0, 0)),
            ],
            scratch_shapes=[pltpu.VMEM((total, D), full)],
        ),
        compiler_params=pltpu.CompilerParams(vmem_limit_bytes=VMEM_LIMIT),
        cost_estimate=SMALL_COST,
        name="attend_backward",
    )(
        scalars,
        queries,
        keys,
        values,
        grads,
        logs,
        deltas,
        pair_weight,
        pair_weight,
        *extra,
    )


def swap(value, axis, bit):
    count = lax.axis_size(axis)
    return lax.ppermute(value, axis, [(i, i ^ bit) for i in range(count)])


class Order:
    def __init__(self):
        self.marks = ()

    def __call__(self, *values):
        values = lax.optimization_barrier(values + self.marks)[: len(values)]
        self.marks = values
        return values[0] if len(values) == 1 else values


def outer_bits():
    bits = []
    bit = 2
    while bit < lax.axis_size("dp"):
        bits.append(bit)
        bit *= 2
    return bits


class Gather:
    def __init__(self, parts):
        self.bits = outer_bits()
        half = len(self.bits) // 2
        self.orders = [
            self.bits[half * (n % 2) :] + self.bits[: half * (n % 2)] for n in range(len(parts))
        ]
        self.result = [[([0], part)] for part in parts]
        self.step = 0

    def advance(self, order):
        held = self.result
        if self.step < len(self.bits):
            masks = [[m for mask, _ in pieces for m in mask] for pieces in held]
            blocks = [
                jnp.concatenate([array for _, array in pieces]) if self.step else pieces[0][1]
                for pieces in held
            ]
            blocks = order(*blocks)
            bits = [turn[self.step] for turn in self.orders]
            self.result = [
                [(mask, block), ([m ^ bit for m in mask], swap(block, "dp", bit))]
                for mask, block, bit in zip(masks, blocks, bits)
            ]
        else:
            arrays = order(*[array for pieces in held for _, array in pieces])
            arrays = iter(arrays)
            self.result = []
            for pieces in held:
                kept = [(masks, next(arrays)) for masks, _ in pieces]
                self.result.append(
                    kept + [([m ^ 1 for m in masks], swap(array, "dp", 1)) for masks, array in kept]
                )
        self.step += 1


def canonical_row(me, rank, block, mask, rank_mask, stride, offset):
    if mask is None:
        return offset
    row = (me ^ mask) * block + offset
    if stride:
        row = row + (rank ^ rank_mask) * stride
    return pl.multiple_of(row, 16)


def place_kernel(plan, block, *refs):
    count = len(plan)
    ins = refs[:count]
    outs = refs[count:-1]
    sems = refs[-1]
    me = lax.axis_index("dp")
    rank = lax.axis_index("mp")
    copies = []
    for ref, moves in zip(ins, plan):
        for start, size, which, mask, column, _, offset in moves:
            row = canonical_row(me, rank, block, mask, 0, 0, offset)
            copy = pltpu.make_async_copy(
                ref.at[pl.ds(start, size), :],
                outs[which].at[pl.ds(row, size), pl.ds(column * D, D)],
                sems.at[len(copies)],
            )
            copy.start()
            copies.append(copy)
    for copy in copies:
        copy.wait()


def plan_of(gathered, layouts):
    arrays = []
    plan = []
    for pieces, layout in zip(gathered, layouts):
        rows = sum(size for _, size, *_ in layout)
        for masks, array in pieces:
            moves = []
            for j, mask in enumerate(masks):
                for start, size, which, rank_mask, stride, offset in layout:
                    moves.append((j * rows + start, size, which, mask, rank_mask, stride, offset))
            arrays.append(array)
            plan.append(moves)
    return arrays, plan


def place(arrays, plan, block, shapes):
    return pl.pallas_call(
        functools.partial(place_kernel, plan, block),
        out_shape=[jax.ShapeDtypeStruct(shape, low) for shape in shapes],
        in_specs=[pl.BlockSpec(memory_space=pl.ANY)] * len(arrays),
        out_specs=[pl.BlockSpec(memory_space=pltpu.VMEM)] * len(shapes),
        scratch_shapes=[pltpu.SemaphoreType.DMA((sum(len(moves) for moves in plan),))],
        compiler_params=pltpu.CompilerParams(vmem_limit_bytes=VMEM_LIMIT),
        cost_estimate=SMALL_COST,
        name="place",
    )(*arrays)


def middle_kernel(plan, block, total, *refs):
    limit_ref, vector_ref = refs[:2]
    token_hbm, mixed_hbm, log_hbm, cot_hbm, teach_hbm = refs[2:7]
    pieces = refs[7 : 7 + total]
    (
        out_hbm,
        final_hbm,
        act_hbm,
        pre_hbm,
        second_hbm,
        middle_low_hbm,
        attended_hbm,
        middle_hbm,
        grad_hbm,
        delta_ref,
        log_ref,
        sum_ref,
    ) = refs[7 + total : 19 + total]
    (
        token,
        mixed,
        logs,
        cot,
        teach,
        up,
        down,
        proj,
        act,
        pre,
        slope,
        second,
        attended,
        middle,
        final,
        out,
        final_low,
        middle_low,
        grad,
        accum,
        in_sems,
        weight_sems,
        out_sems,
    ) = refs[19 + total :]
    targets = (up, down, proj)
    rows = token.shape[0]
    me = lax.axis_index("dp")
    rank = lax.axis_index("mp")

    def fetch(ref, scratch, n):
        copy = pltpu.make_async_copy(ref, scratch, in_sems.at[n])
        copy.start()
        return copy

    def send(scratch, ref, n):
        copy = pltpu.make_async_copy(scratch, ref, out_sems.at[n])
        copy.start()
        return copy

    gets = [
        fetch(token_hbm, token, 0),
        fetch(mixed_hbm, mixed, 1),
        fetch(log_hbm, logs, 2),
        fetch(cot_hbm, cot, 3),
        fetch(teach_hbm, teach, 4),
    ]
    loads = {0: [], 1: [], 2: []}
    number = 0
    for want in (2, 0, 1):
        for ref, moves in zip(pieces, plan):
            for start, size, which, mask, rank_mask, stride, offset in moves:
                if which != want:
                    continue
                row = canonical_row(me, rank, block, mask, rank_mask, stride, offset)
                copy = pltpu.make_async_copy(
                    ref.at[pl.ds(start, size), :],
                    targets[which].at[pl.ds(row, size), :],
                    weight_sems.at[number],
                )
                copy.start()
                loads[which].append(copy)
                number += 1

    table_row = vector_ref[0:1, :]
    out_bias = vector_ref[1:2, :]
    gain = vector_ref[2:3, :]
    shift = vector_ref[3:4, :]
    down_bias = vector_ref[4:5, :]
    weight = vector_ref[5:6, :]
    gets[0].wait()
    gets[1].wait()
    attended[...] = mixed[...].astype(low)
    puts = [send(attended, attended_hbm, 0)]
    for copy in loads[2]:
        copy.wait()
    state = token[...].astype(full) + table_row + out_bias
    state = state + dot_of(attended[...], proj[...], 1, 1)
    middle[...] = state
    unit, _ = norm_stats(state)
    second[...] = (unit * gain + shift).astype(low)
    puts.append(send(second, second_hbm, 1))
    accum[...] = jnp.zeros((rows, D), full)
    for copy in loads[0]:
        copy.wait()
    for copy in loads[1]:
        copy.wait()

    def forward(m, _):
        place = pl.ds(pl.multiple_of(m * D, D), D)
        value = dot_of(second[...], up[place, :], 1, 0) + vector_ref[pl.ds(8 + m, 1), :]
        cumulative = 0.5 + 0.5 * lax.erf(value * (0.5**0.5))
        act[m] = (value * cumulative).astype(low)
        slope[m] = cumulative + value * jnp.exp(-0.5 * value * value) * 0.3989422804014327
        accum[...] += dot_of(act[m], down[place, :], 1, 1)
        return 0

    lax.fori_loop(0, FF // D, forward, 0)
    puts.append(send(act, act_hbm, 2))
    final_state = middle[...] + accum[...] + down_bias
    out[...] = final_state.astype(low)
    puts.append(send(out, out_hbm, 3))
    gets[3].wait()
    gets[4].wait()
    place = lax.broadcasted_iota(jnp.int32, (rows, 1), 0)
    grads = cot[...].astype(full) + weight * (final_state - teach[...].astype(full))
    grads = jnp.where(place < limit_ref[5], grads, 0.0)
    final[...] = grads
    final_low[...] = grads.astype(low)
    puts.append(send(final_low, final_hbm, 4))
    sum_ref[3:4, :] = jnp.sum(grads, axis=0, keepdims=True)
    accum[...] = jnp.zeros((rows, D), full)

    def backward(m, _):
        place = pl.ds(pl.multiple_of(m * D, D), D)
        value = slope[m] * dot_of(final_low[...], down[place, :], 1, 0)
        value = value.astype(low)
        pre[m] = value
        sum_ref[pl.ds(8 + m, 1), :] = jnp.sum(value.astype(full), axis=0, keepdims=True)
        accum[...] += dot_of(value, up[place, :], 1, 1)
        return 0

    lax.fori_loop(0, FF // D, backward, 0)
    puts.append(send(pre, pre_hbm, 5))
    unit, inverse = norm_stats(middle[...])
    second_grad = accum[...]
    sum_ref[0:1, :] = jnp.sum(second_grad * unit, axis=0, keepdims=True)
    sum_ref[1:2, :] = jnp.sum(second_grad, axis=0, keepdims=True)
    scaled = second_grad * gain
    mean_scaled = jnp.mean(scaled, axis=-1, keepdims=True)
    mean_unit = jnp.mean(scaled * unit, axis=-1, keepdims=True)
    total_grad = final[...] + inverse * (scaled - mean_scaled - unit * mean_unit)
    middle[...] = total_grad
    puts.append(send(middle, middle_hbm, 6))
    middle_low[...] = total_grad.astype(low)
    puts.append(send(middle_low, middle_low_hbm, 7))
    sum_ref[2:3, :] = jnp.sum(total_grad, axis=0, keepdims=True)
    attended_grad = dot_of(middle_low[...], proj[...], 1, 0).astype(low)
    grad[...] = attended_grad
    puts.append(send(grad, grad_hbm, 8))
    gets[2].wait()
    head = lax.broadcasted_iota(jnp.int32, (16, D), 0)
    lane = lax.broadcasted_iota(jnp.int32, (16, D), 1)
    member = jnp.where(lane // HEAD_DIM == head, 1.0, 0.0)
    leader = jnp.where(lane == head * HEAD_DIM, 1.0, 0.0)
    exact = functools.partial(
        lax.dot_general,
        dimension_numbers=(((1,), (1,)), ((), ())),
        precision=lax.Precision.HIGHEST,
        preferred_element_type=full,
    )
    deltas = exact(member, attended_grad.astype(full) * mixed[...])
    tops = exact(leader, logs[...])
    for pair in range(PAIRS):
        delta_ref[pair] = deltas[2 * pair : 2 * pair + 2]
        log_ref[pair] = tops[2 * pair : 2 * pair + 2]
    for copy in puts:
        copy.wait()


def middle_call(limit, vectors, tokens, mixed, logs, cot, teach, arrays, plan, block):
    rows = tokens.shape[0]
    hidden = FF // D
    narrow = jax.ShapeDtypeStruct((rows, D), low)
    wide = jax.ShapeDtypeStruct((rows, D), full)
    many = jax.ShapeDtypeStruct((hidden, rows, D), low)
    stats = jax.ShapeDtypeStruct((PAIRS, 2, rows), full)
    anywhere = pl.BlockSpec(memory_space=pl.ANY)
    inside = pl.BlockSpec(memory_space=pltpu.VMEM)
    moves = sum(len(part) for part in plan)
    return pl.pallas_call(
        functools.partial(middle_kernel, plan, block, len(arrays)),
        out_shape=(
            narrow,
            narrow,
            many,
            many,
            narrow,
            narrow,
            narrow,
            wide,
            narrow,
            stats,
            stats,
            jax.ShapeDtypeStruct((8 + 8, D), full),
        ),
        in_specs=[pl.BlockSpec(memory_space=pltpu.SMEM), inside]
        + [anywhere] * (5 + len(arrays)),
        out_specs=[anywhere] * 9 + [inside] * 3,
        scratch_shapes=[
            pltpu.VMEM((rows, D), low),
            pltpu.VMEM((rows, D), full),
            pltpu.VMEM((rows, D), full),
            pltpu.VMEM((rows, D), low),
            pltpu.VMEM((rows, D), low),
            pltpu.VMEM((FF, D), low),
            pltpu.VMEM((FF, D), low),
            pltpu.VMEM((D, D), low),
            pltpu.VMEM((hidden, rows, D), low),
            pltpu.VMEM((hidden, rows, D), low),
            pltpu.VMEM((hidden, rows, D), full),
            pltpu.VMEM((rows, D), low),
            pltpu.VMEM((rows, D), low),
            pltpu.VMEM((rows, D), full),
            pltpu.VMEM((rows, D), full),
            pltpu.VMEM((rows, D), low),
            pltpu.VMEM((rows, D), low),
            pltpu.VMEM((rows, D), low),
            pltpu.VMEM((rows, D), low),
            pltpu.VMEM((rows, D), full),
            pltpu.SemaphoreType.DMA((5,)),
            pltpu.SemaphoreType.DMA((moves,)),
            pltpu.SemaphoreType.DMA((9,)),
        ],
        compiler_params=pltpu.CompilerParams(vmem_limit_bytes=VMEM_LIMIT),
        cost_estimate=SMALL_COST,
        name="middle",
    )(limit, vectors, tokens, mixed, logs, cot, teach, *arrays)


def store_split(value, keep, send, index):
    block = keep.shape[2]
    even = lax.axis_index("dp") % 2 == 0
    for outer in range(keep.shape[1]):
        first = value[2 * outer * block : (2 * outer + 1) * block]
        other = value[(2 * outer + 1) * block : (2 * outer + 2) * block]
        keep[index, outer] = jnp.where(even, first, other).astype(low)
        send[index, outer] = jnp.where(even, other, first).astype(low)


def feed_grad_kernel(left_ref, right_ref, *refs):
    keep, send, turned = refs[-3:]
    m = pl.program_id(0)

    @pl.when(m == 0)
    def _():
        turned[...] = left_ref[...].T

    @pl.when(m < FF // D)
    def _():
        store_split(dot_of(turned[...], right_ref[0], 1, 0), keep, send, 0)

    if len(refs) > 3:

        @pl.when(m == FF // D)
        def _():
            store_split(dot_of(refs[0][...].T, refs[1][...], 1, 0), keep, send, 0)


def feed_grads(left, right, more, dp):
    rows = left.shape[0]
    hidden = FF // D
    count = hidden + (1 if more else 0)
    whole = pl.BlockSpec((rows, D), lambda m: (0, 0))
    shape = (count, dp // 2, D // dp, D)
    return pl.pallas_call(
        feed_grad_kernel,
        out_shape=[jax.ShapeDtypeStruct(shape, low)] * 2,
        grid=(count,),
        in_specs=[
            whole,
            pl.BlockSpec((1, rows, D), lambda m: (jnp.minimum(m, hidden - 1), 0, 0)),
        ]
        + [whole] * len(more),
        out_specs=[pl.BlockSpec((1,) + shape[1:], lambda m: (m, 0, 0, 0))] * 2,
        scratch_shapes=[pltpu.VMEM((D, rows), low)],
        compiler_params=pltpu.CompilerParams(vmem_limit_bytes=VMEM_LIMIT),
        cost_estimate=SMALL_COST,
        name="feed_grads",
    )(left, right, *more)


def fold_kernel(bits, places, *refs):
    count = len(bits)
    me = lax.axis_index("dp")
    for n in range(count):
        keep, got = refs[2 * n : 2 * n + 2]
        out_keep, out_send = refs[2 * count + 2 * n : 2 * count + 2 * n + 2]
        step = 1 << places[n]
        mine = (me // bits[n]) % 2 * step
        for j in range(keep.shape[1] // 2):
            base = (j // step) * 2 * step + j % step
            for out, shift in ((out_keep, mine), (out_send, step - mine)):
                value = keep[0, base + shift].astype(full) + got[0, base + shift].astype(full)
                out[0, j] = value.astype(low)


def fold(pairs, bits, places):
    lead = pairs[0][0].shape[0]
    block = lambda shape: pl.BlockSpec((1,) + shape[1:], lambda i: (i, 0, 0, 0))
    halves = [
        (keep.shape[0], keep.shape[1] // 2) + keep.shape[2:] for keep, _ in pairs for _ in range(2)
    ]
    outs = pl.pallas_call(
        functools.partial(fold_kernel, bits, places),
        out_shape=[jax.ShapeDtypeStruct(shape, low) for shape in halves],
        grid=(lead,),
        in_specs=[block(value.shape) for pair in pairs for value in pair],
        out_specs=[block(shape) for shape in halves],
        compiler_params=pltpu.CompilerParams(vmem_limit_bytes=VMEM_LIMIT),
        cost_estimate=pl.CostEstimate(flops=0, bytes_accessed=16 << 20, transcendentals=0),
        name="fold",
    )(*[value for pair in pairs for value in pair])
    return [(outs[2 * n], outs[2 * n + 1]) for n in range(len(pairs))]


def qkv_grad_kernel(count, *refs):
    chunk_refs = refs[:count]
    query_ref = refs[count]
    key_refs = refs[count + 1 : 2 * count + 1]
    value_refs = refs[2 * count + 1 : 3 * count + 1]
    keeps, sends = refs[3 * count + 1 : 3 * count + 3], refs[3 * count + 3 : 3 * count + 5]
    sum_ref, turned = refs[3 * count + 5 :]
    rows = query_ref.shape[0]
    c = pl.program_id(0)
    ones = jnp.ones((16, rows), low)

    def store(value):
        for n in range(2):
            store_split(value[:, n * D // 2 : (n + 1) * D // 2], keeps[n], sends[n], 0)

    @pl.when(c == 0)
    def _():
        for n in range(count):
            turned[n] = chunk_refs[n][...].T
        store(dot_of(turned[0], query_ref[...], 1, 0))
        sum_ref[0:8, :] = dot_of(ones, query_ref[...], 1, 0)[0:8]

    def many(sources):
        value = dot_of(turned[0], sources[0][...], 1, 0)
        for n in range(1, count):
            value = value + dot_of(turned[n], sources[n][...], 1, 0)
        store(value)

    @pl.when(c == 1)
    def _():
        many(key_refs)

    @pl.when(c == 2)
    def _():
        many(value_refs)
        value = dot_of(ones, value_refs[0][...], 1, 0)
        for n in range(1, count):
            value = value + dot_of(ones, value_refs[n][...], 1, 0)
        sum_ref[8:16, :] = value[0:8]


def qkv_grads(chunks, query_grad, key_grads, value_grads, dp):
    rows = query_grad.shape[0]
    count = len(chunks)
    whole = pl.BlockSpec((rows, D), lambda c: (0, 0))
    shape = (3, dp // 2, D // dp, D // 2)
    part = pl.BlockSpec((1,) + shape[1:], lambda c: (c, 0, 0, 0))
    return pl.pallas_call(
        functools.partial(qkv_grad_kernel, count),
        out_shape=[jax.ShapeDtypeStruct(shape, low)] * 4
        + [jax.ShapeDtypeStruct((16, D), full)],
        grid=(3,),
        in_specs=[whole] * (3 * count + 1),
        out_specs=[part] * 4 + [pl.BlockSpec((16, D), lambda c: (0, 0))],
        scratch_shapes=[pltpu.VMEM((count, D, rows), low)],
        compiler_params=pltpu.CompilerParams(vmem_limit_bytes=VMEM_LIMIT),
        cost_estimate=SMALL_COST,
        name="qkv_grads",
    )(*chunks, query_grad, *key_grads, *value_grads)


def two_parts(value, axis, mine):
    keep = lax.dynamic_index_in_dim(value, mine, axis, keepdims=False)
    send = lax.dynamic_index_in_dim(value, 1 - mine, axis, keepdims=False)
    return keep, send.astype(low)


def scatter_dp(parts, turns):
    bits = outer_bits()
    half = len(bits) // 2
    orders = [[1] + bits[half * (turn % 2) :] + bits[: half * (turn % 2)] for turn in turns]
    left = [list(bits) for _ in turns]
    for step in range(len(bits) + 1):
        sends = yield [send for _, send in parts]
        got = [swap(send, "dp", turn[step]) for send, turn in zip(sends, orders)]
        pairs = [(keep, other) for (keep, _), other in zip(parts, got)]
        if step < len(bits):
            places = []
            for n, turn in enumerate(orders):
                places.append(left[n].index(turn[step + 1]))
                left[n].remove(turn[step + 1])
            parts = fold(pairs, [turn[step + 1] for turn in orders], places)
    return [(keep.astype(full) + other.astype(full))[:, 0] for keep, other in pairs]


def scatter_mp(values):
    rank = lax.axis_index("mp")
    for bit in (2, 1):
        parts = []
        for value in values:
            pair = value.reshape((2, value.shape[0] // 2) + value.shape[1:])
            parts.append(two_parts(pair, 0, (rank // bit) % 2))
        sends = yield [send for _, send in parts]
        values = [
            keep.astype(full) + swap(send, "mp", bit).astype(full)
            for (keep, _), send in zip(parts, sends)
        ]
    return [value[0] for value in values]


def scatter_feed(up_own, down_own):
    mp = lax.axis_size("mp")
    block = down_own.shape[1]
    out_own = up_own[mp].reshape(block, mp, -1).transpose(1, 0, 2)
    tall, out_grad = yield from scatter_mp(
        [jnp.concatenate([up_own[:mp], down_own], axis=1), out_own]
    )
    return tall[:block], tall[block:].T, out_grad.T


def scatter_qkv(keep_left, keep_right, send_left, send_right):
    rank = lax.axis_index("mp")
    left_part, right_part = yield from scatter_dp(
        [(keep_left, send_left), (keep_right, send_right)], (0, 1)
    )
    upper = rank >= 2
    odd = rank % 2 == 1
    (send,) = yield [jnp.where(upper, left_part, right_part).astype(low)]
    keep = jnp.where(upper, right_part, left_part) + swap(send, "mp", 2).astype(full)
    width = D // lax.axis_size("mp")
    (send,) = yield [jnp.where(odd, keep[..., :width], keep[..., width:]).astype(low)]
    return jnp.where(odd, keep[..., width:], keep[..., :width]) + swap(
        send, "mp", 1
    ).astype(full)


def butterfly(value):
    for bit in [1] + outer_bits():
        (value,) = yield [value]
        value = value + swap(value, "dp", bit)
    for bit in (1, 2):
        (value,) = yield [value]
        value = value + swap(value, "mp", bit)
    return value


class Steps:
    def __init__(self, steps):
        self.steps = steps
        self.pending = next(steps)
        self.result = None

    def advance(self, order):
        if self.pending is None:
            return
        sends = order(*self.pending)
        sends = [sends] if len(self.pending) == 1 else list(sends)
        try:
            self.pending = self.steps.send(sends)
        except StopIteration as stop:
            self.pending = None
            self.result = stop.value

    def finish(self, order):
        while self.pending is not None:
            self.advance(order)
        return self.result


def shards(
    tokens_in,
    timesteps,
    lengths,
    time_table,
    norm_gains,
    norm_biases,
    w_qkv,
    qv_bias,
    w_out,
    out_bias,
    w_up,
    up_bias,
    w_down,
    down_bias,
    cotangent,
    teacher,
):
    rank = lax.axis_index("mp")
    data_rank = lax.axis_index("dp")
    mp = lax.axis_size("mp")
    dp = lax.axis_size("dp")
    own_rows = tokens_in.shape[0]
    length = lax.dynamic_index_in_dim(lengths, data_rank, keepdims=False)
    own_time = lax.dynamic_index_in_dim(timesteps, data_rank, keepdims=False)
    odd = rank % 2 == 1
    upper = rank >= 2
    middle = jnp.logical_or(rank == 1, rank == 2)
    order = Order()
    along = lambda value, pairs: lax.ppermute(value, "mp", pairs)

    block = w_qkv.shape[1]
    aligned = block % 32 == 0
    narrow = order(jnp.concatenate([w_qkv.reshape(3 * block, -1), w_out.T]))
    first_swap = swap(narrow, "mp", 1)
    tall = order(jnp.concatenate([w_up, w_down.T]))
    tall_swap = swap(tall, "mp", 1)
    pair = order(
        jnp.concatenate(
            [jnp.where(odd, first_swap, narrow), jnp.where(odd, narrow, first_swap)], axis=1
        )
    )
    second_swap = swap(pair, "mp", 2)
    tokens, lengths, own_time, norm_gains, norm_biases, out_bias, down_bias, up_bias, length = order(
        tokens_in, lengths, own_time, norm_gains, norm_biases, out_bias, down_bias, up_bias, length
    )
    table_row = lax.dynamic_slice_in_dim(time_table, own_time, 1).astype(full)
    unit_one, _ = norm_stats(tokens.astype(full) + table_row)
    first_norm = (unit_one * norm_gains[0] + norm_biases[0]).astype(low)
    loss_weight = lengths.shape[0] * MAXLEN / jnp.sum(lengths).astype(full)
    vectors = jnp.concatenate(
        [
            table_row,
            out_bias[None],
            norm_gains[1:2],
            norm_biases[1:2],
            down_bias[None],
            jnp.full((3, D), loss_weight),
            up_bias.reshape(-1, D),
            jnp.zeros((4, D), full),
        ]
    )
    scalars = jnp.stack(
        [
            rank,
            jnp.where(rank == 0, 1, rank - 1),
            jnp.where(upper, rank - 2, rank + 2),
            jnp.where(middle, rank + 1, 3 - rank),
            length,
            length - rank * own_rows,
        ]
    ).astype(jnp.int32)
    first_norm, vectors, scalars = order(first_norm, vectors, scalars)
    wide = jnp.concatenate(
        [jnp.where(upper, second_swap, pair), jnp.where(upper, pair, second_swap)], axis=1
    )
    qkv_rows, out_rows = wide[: 3 * block], wide[3 * block :]
    if aligned:
        split = 3 * block // 2
        qkv_gather = Gather([qkv_rows[:split], qkv_rows[split:]])
        qkv_gather.advance(order)
    tall = order(jnp.concatenate([tall, tall_swap]))
    tall_other = swap(tall, "mp", 2)

    if aligned:
        while qkv_gather.step < len(qkv_gather.bits):
            qkv_gather.advance(order)
    sent = order(first_norm)
    from_left = along(sent, [(0, 1), (1, 2), (2, 3)])
    from_right = along(sent, [(1, 0), (2, 1), (3, 2)])
    if aligned:
        feed_gather = Gather(
            [
                jnp.concatenate([tall, out_rows[: block // 2]]),
                jnp.concatenate([tall_other, out_rows[block // 2 :]]),
            ]
        )
        feed_gather.advance(order)
        qkv_gather.advance(order)
        arrays, plan = plan_of(
            qkv_gather.result,
            [
                [(0, block, 0, 0, 0, 0), (block, split - block, 1, 0, 0, 0)],
                [
                    (0, 2 * block - split, 1, 0, 0, split - block),
                    (2 * block - split, block, 1, 1, 0, 0),
                ],
            ],
        )
        query_weight, pair_weight = order(*place(arrays, plan, block, [(D, D), (D, 2 * D)]))
    else:
        weights = lax.all_gather(qkv_rows.reshape(3, block, D), "dp", axis=1, tiled=True)
        query_weight = weights[0]
        pair_weight = jnp.concatenate([weights[1], weights[2]], axis=1)
    hop_right, hop_left = order(from_left, from_right)
    second_right = along(hop_right, [(1, 2), (2, 3)])
    second_left = along(hop_left, [(1, 0), (2, 1)])
    near = jnp.where(rank == 0, hop_left, hop_right)
    if aligned:
        while feed_gather.step < len(feed_gather.bits):
            feed_gather.advance(order)
    attend = lambda chunks, numbers, carried: attend_forward(
        chunks,
        numbers,
        scalars,
        query_weight,
        pair_weight,
        qv_bias[0:1],
        qv_bias[1:2],
        carried,
    )
    key_own, key_near, value_own, value_near, queries, *state = order(
        *attend(order(first_norm, near), (0, 1), None)
    )
    second = order(jnp.where(upper, second_right, second_left))
    third = along(second, [(1, 0), (2, 3)])
    key_second, value_second, *state = attend([second], (2,), (queries, *state))
    key_second, value_second, *state = order(key_second, value_second, *state)
    last = order(jnp.where(middle, hop_left, third))
    if aligned:
        feed_gather.advance(order)
    key_last, value_last, mixed, logs = order(*attend([order(last)], (3,), (queries, *state)))
    if aligned:
        layout = lambda masks, shift: [
            (0, block, 0, masks[0], D, 0),
            (block, block, 1, masks[0], D, 0),
            (2 * block, block, 0, masks[1], D, 0),
            (3 * block, block, 1, masks[1], D, 0),
            (4 * block, block // 2, 2, 0, 0, shift),
        ]
        arrays, plan = plan_of(
            feed_gather.result, [layout((0, 1), 0), layout((2, 3), block // 2)]
        )
    else:
        arrays = [
            lax.all_gather(w_up, ("mp", "dp"), axis=0, tiled=True),
            lax.all_gather(w_down.T, ("mp", "dp"), axis=0, tiled=True),
            lax.all_gather(out_rows, "dp", axis=0, tiled=True),
        ]
        plan = [[(0, array.shape[0], n, None, 0, 0, 0)] for n, array in enumerate(arrays)]
    chunks = [first_norm, near, second, last]
    keys = [key_own, key_near, key_second, key_last]
    values = [value_own, value_near, value_second, value_last]

    (
        output,
        final_low,
        hidden_act,
        pre_grad,
        second_norm,
        middle_low,
        attended,
        middle_grad,
        attended_grad,
        deltas,
        log_rows,
        sums,
    ) = middle_call(
        scalars, vectors, tokens, mixed, logs, cotangent, teacher, arrays, plan, block
    )
    gain_two, shift_two, middle_sum, final_sum = sums[0], sums[1], sums[2], sums[3]
    down = Steps(scatter_dp([feed_grads(final_low, hidden_act, (), dp)], (1,)))
    down.advance(order)
    second_norm = order(second_norm)
    up = Steps(
        scatter_dp([feed_grads(second_norm, pre_grad, (middle_low, attended), dp)], (0,))
    )
    up.advance(order)
    down.advance(order)
    up.advance(order)

    key_grads = [None] * 4
    value_grads = [None] * 4
    firsts = [None] * 4
    query_grad = None
    for n in (3, 2, 1, 0):
        query_grad, key_grads[n], value_grads[n], firsts[n] = attend_backward(
            n,
            queries,
            keys[n],
            values[n],
            order(attended_grad),
            log_rows,
            deltas,
            query_weight,
            pair_weight,
            scalars,
            query_grad,
            n == 0,
        )
        firsts[n] = order(firsts[n])
        if n == 3:
            back_last = along(firsts[3], [(0, 1), (3, 2)]).astype(full)
        elif n == 2:
            down.advance(order)
            up.advance(order)
            payload = order((firsts[2] + back_last).astype(low))
            back_right = along(payload, [(0, 1), (1, 2)]).astype(full)
            back_left = along(payload, [(3, 2), (2, 1)]).astype(full)
        elif n == 1:
            to_right = jnp.where(
                rank == 0, firsts[1], firsts[3].astype(full) + back_right
            ).astype(low)
            to_left = (firsts[1] + back_left).astype(low)
            (up_own,) = up.finish(order)
            (down_own,) = down.finish(order)
            feed = Steps(scatter_feed(up_own, down_own))
            feed.advance(order)
            to_right, to_left = order(to_right, to_left)
            final_right = along(to_right, [(0, 1), (1, 2), (2, 3)])
            final_left = along(to_left, [(3, 2), (2, 1), (1, 0)])
    query_grad, final_right, final_left = order(query_grad, final_right, final_left)
    *halves, bias_sums = qkv_grads(chunks, query_grad, key_grads, value_grads, dp)
    qkv = Steps(scatter_qkv(*halves))
    qkv.advance(order)
    qkv.advance(order)
    feed.advance(order)
    tokens, first_own = order(tokens, firsts[0])
    first_grad = first_own + final_right.astype(full) + final_left.astype(full)
    unit_one, inverse_one = norm_stats(tokens.astype(full) + table_row)
    start_part, gain_one, shift_one = norm_back(
        unit_one, inverse_one, norm_gains[0], first_grad
    )
    input_grad = middle_grad + start_part
    sequence_sum = jnp.sum(input_grad, axis=0)
    own_slot = (jnp.arange(dp) == data_rank).astype(full)
    packed = jnp.concatenate(
        [
            jnp.stack([gain_one, gain_two, shift_one, shift_two]),
            jnp.stack([bias_sums[0], bias_sums[8]]),
            jnp.stack([middle_sum, final_sum]),
            sums[8 : 8 + FF // D],
            own_slot[:, None] * sequence_sum[None, :],
        ]
    )
    small = Steps(butterfly(packed))
    small.advance(order)
    qkv.advance(order)
    small.advance(order)
    small.advance(order)
    qkv.advance(order)
    small.advance(order)
    qkv.advance(order)
    small.advance(order)
    qkv_grad = qkv.finish(order)
    total = small.finish(order)
    up_grad, down_grad, out_grad = feed.finish(order)
    fixed = 8 + FF // D
    chosen = (timesteps[None, :] == jnp.arange(time_table.shape[0])[:, None]).astype(full)
    table_grad = lax.dot_general(
        chosen,
        total[fixed:],
        (((1,), (0,)), ((), ())),
        precision=lax.Precision.HIGHEST,
        preferred_element_type=full,
    )
    return (
        output,
        input_grad,
        table_grad,
        total[0:2],
        total[2:4],
        qkv_grad,
        total[4:6],
        out_grad,
        total[6],
        up_grad,
        total[8:fixed].reshape(FF),
        down_grad,
        total[7],
    )


def solution(mesh):
    rows = P(both, None)
    placed = (
        rows,
        P(),
        P(),
        P(),
        P(),
        P(),
        P(None, "dp", "mp"),
        P(),
        P("mp", "dp"),
        P(),
        P("dp", "mp"),
        P(),
        P("mp", "dp"),
        P(),
        rows,
        rows,
    )
    return jax.shard_map(
        shards,
        mesh=mesh,
        in_specs=placed,
        out_specs=(
            rows,
            rows,
            P(),
            P(),
            P(),
            P(None, "dp", "mp"),
            P(),
            P("mp", "dp"),
            P(),
            P("dp", "mp"),
            P(),
            P("mp", "dp"),
            P(),
        ),
        check_vma=False,
    )
```

```python
import functools

import jax
import jax.numpy as jnp
from jax import lax
from jax.experimental import pallas as pl
from jax.experimental.pallas import tpu as pltpu
from jax.sharding import PartitionSpec as P

D = 768
HEADS = 12
HEAD_DIM = 64
FF = 3072
MAXLEN = 2048
PAIR = 2 * HEAD_DIM
PAIRS = HEADS // 2
VMEM_LIMIT = 58 << 20
SMALL_COST = pl.CostEstimate(flops=1 << 20, bytes_accessed=1 << 16, transcendentals=0)

far_below = -1e30
epsilon = 1e-05
score_scale = HEAD_DIM ** (-0.5)
low = jnp.bfloat16
full = jnp.float32
both = ("dp", "mp")


def norm_stats(values):
    center = values - jnp.mean(values, axis=-1, keepdims=True)
    spread = jnp.mean(center * center, axis=-1, keepdims=True)
    inverse = lax.rsqrt(spread + epsilon)
    return center * inverse, inverse


def dot_of(left_side, right_side, left_dim, right_dim):
    return lax.dot_general(
        left_side,
        right_side,
        (((left_dim,), (right_dim,)), ((), ())),
        preferred_element_type=full,
    )


def first_half(shape):
    return lax.broadcasted_iota(jnp.int32, shape, len(shape) - 1) < HEAD_DIM


def forward_kernel(numbers, first, final, scalars, *refs):
    count = len(numbers)
    chunk_refs = refs[:count]
    wk_ref, wv_ref, value_bias_ref = refs[count : count + 3]
    refs = refs[count + 3 :]
    if first:
        wq_ref, query_bias_ref = refs[:2]
        key_outs, value_outs = refs[2 : 2 + count], refs[2 + count : 2 + 2 * count]
        query_out, top_ref, sum_ref, acc_ref = refs[2 + 2 * count :]
        q_pair = (dot_of(chunk_refs[0][...], wq_ref[...], 1, 0) + query_bias_ref[...]).astype(low)
        q_pair = q_pair * jnp.asarray(score_scale, low)
        query_out[...] = q_pair
    else:
        q_ref, top_in, sum_in, acc_in = refs[:4]
        key_outs, value_outs = refs[4 : 4 + count], refs[4 + count : 4 + 2 * count]
        results = refs[4 + 2 * count :]
        q_pair = q_ref[...]
    weight = jnp.concatenate([wk_ref[...], wv_ref[...]], axis=1)
    keys = []
    values = []
    for n in range(count):
        both_parts = dot_of(chunk_refs[n][...], weight, 1, 0)
        keys.append(both_parts[:, :PAIR].astype(low))
        values.append((both_parts[:, PAIR:] + value_bias_ref[...]).astype(low))
        key_outs[n][...] = keys[n]
        value_outs[n][...] = values[n]
    rows = q_pair.shape[0]
    size = keys[0].shape[0]
    place = lax.broadcasted_iota(jnp.int32, (1, size), 1)
    lower = first_half((rows, PAIR))
    parts = []
    for half in range(2):
        kept = lower if half == 0 else jnp.logical_not(lower)
        q_half = jnp.where(kept, q_pair, jnp.zeros_like(q_pair))
        scores = []
        for n in range(count):
            bias = jnp.where(place + scalars[numbers[n]] * size < scalars[4], 0.0, far_below)
            scores.append(dot_of(q_half, keys[n], 1, 1) + bias)
        highest = functools.reduce(
            jnp.maximum, [jnp.max(score, axis=-1, keepdims=True) for score in scores]
        )
        totals = jnp.zeros_like(highest)
        mixed = jnp.zeros((rows, PAIR), full)
        for n in range(count):
            exp_scores = jnp.exp(scores[n] - highest)
            totals = totals + jnp.sum(exp_scores, axis=-1, keepdims=True)
            mixed = mixed + dot_of(exp_scores.astype(low), values[n], 1, 0)
        parts.append((highest, totals, mixed))
    top = jnp.where(lower, parts[0][0], parts[1][0])
    total = jnp.where(lower, parts[0][1], parts[1][1])
    mixed = jnp.where(lower, parts[0][2], parts[1][2])
    if first:
        top_ref[...] = top
        sum_ref[...] = total
        acc_ref[...] = mixed
    else:
        highest = jnp.maximum(top, top_in[...])
        here = jnp.exp(top - highest)
        before = jnp.exp(top_in[...] - highest)
        total = total * here + sum_in[...] * before
        mixed = mixed * here + acc_in[...] * before
        if final:
            results[0][...] = mixed / total
            results[1][...] = highest + jnp.log(total)
        else:
            results[0][...] = highest
            results[1][...] = total
            results[2][...] = mixed


def attend_forward(chunks, numbers, scalars, query_weight, pair_weight, query_bias, value_bias, carried):
    rows = chunks[0].shape[0]
    count = len(chunks)
    first = carried is None
    final = 3 in numbers
    column = lambda height, c: pl.BlockSpec((height, PAIR), lambda i, n: (0, c * PAIRS + i))
    whole = pl.BlockSpec((rows, D), lambda i, n: (0, 0))
    wide = jax.ShapeDtypeStruct((rows, D), full)
    narrow = jax.ShapeDtypeStruct((rows, D), low)
    extra = (query_weight, query_bias) if first else carried
    results = (narrow,) * first + (wide,) * (2 if final else 3)
    return pl.pallas_call(
        functools.partial(forward_kernel, numbers, first, final),
        out_shape=(narrow,) * (2 * count) + results,
        grid_spec=pltpu.PrefetchScalarGridSpec(
            num_scalar_prefetch=1,
            grid=(PAIRS,),
            in_specs=[whole] * count
            + [column(D, 0), column(D, 1), column(1, 0)]
            + ([column(D, 0), column(1, 0)] if first else [column(rows, 0)] * 4),
            out_specs=[column(rows, 0)] * (2 * count + len(results)),
        ),
        compiler_params=pltpu.CompilerParams(vmem_limit_bytes=VMEM_LIMIT),
        cost_estimate=SMALL_COST,
        name="attend_forward",
    )(scalars, *chunks, pair_weight, pair_weight, value_bias, *extra)


def backward_kernel(
    number,
    first,
    last,
    scalars,
    q_ref,
    k_ref,
    v_ref,
    g_ref,
    log_ref,
    delta_ref,
    wk_ref,
    wv_ref,
    *refs
):
    if last:
        wq_ref = refs[0]
        refs = refs[1:]
    if not first:
        dq_in = refs[0]
        refs = refs[1:]
    dq_ref, dk_ref, dv_ref, back_ref, accum = refs
    step = pl.program_id(0)
    rows = q_ref.shape[0]
    keys = k_ref.shape[0]
    limit = scalars[4] - scalars[number] * keys
    q_pair = q_ref[...]
    g_pair = g_ref[...]
    k_pair = k_ref[...]
    v_pair = v_ref[...]
    lower = first_half((rows, PAIR))
    nothing = jnp.zeros((rows, PAIR), low)
    two_halves = lambda pair: jnp.concatenate(
        [jnp.where(lower, pair, nothing), jnp.where(lower, nothing, pair)]
    )
    queries = two_halves(q_pair)
    grads_out = two_halves(g_pair)
    row_of = lambda ref: jnp.concatenate([ref[0, 0:1, :], ref[0, 1:2, :]], axis=1)
    place = lax.broadcasted_iota(jnp.int32, (keys, 1), 0)
    bias = jnp.where(place < limit, 0.0, far_below)
    scores = dot_of(k_pair, queries, 1, 1) + bias
    prob_grad = dot_of(v_pair, grads_out, 1, 1)
    probs = jnp.exp(scores - row_of(log_ref))
    score_grad = (probs * (prob_grad - row_of(delta_ref))).astype(low)
    dv_low = dot_of(probs.astype(low), grads_out, 1, 0).astype(low)
    dk_low = dot_of(score_grad, queries, 1, 0).astype(low)
    turned = dot_of(k_pair.T, score_grad, 1, 0)
    upper_rows = lax.broadcasted_iota(jnp.int32, (PAIR, rows), 0) < HEAD_DIM
    dk_ref[...] = dk_low
    dv_ref[...] = dv_low
    grads = [dk_low, dv_low]
    weights = [wk_ref[...], wv_ref[...]]
    dq_all = jnp.where(upper_rows, turned[:, :rows], turned[:, rows:]).T
    if not first:
        dq_all = dq_all + dq_in[...]
    back = dot_of(jnp.concatenate(grads, axis=1), jnp.concatenate(weights, axis=1), 1, 1)
    if last:
        dq_low = (dq_all * score_scale).astype(low)
        dq_ref[...] = dq_low
        back = back + dot_of(dq_low, wq_ref[...], 1, 1)
    else:
        dq_ref[...] = dq_all

    @pl.when(step == 0)
    def _():
        accum[...] = back

    @pl.when(step > 0)
    def _():
        accum[...] += back

    @pl.when(step == PAIRS - 1)
    def _():
        back_ref[...] = accum[...].astype(back_ref.dtype)


def attend_backward(
    number,
    queries,
    keys,
    values,
    grads,
    logs,
    deltas,
    query_weight,
    pair_weight,
    scalars,
    carried,
    last,
):
    rows, total = queries.shape[0], keys.shape[0]
    first = carried is None
    column = lambda count, c: pl.BlockSpec((count, PAIR), lambda i, n: (0, c * PAIRS + i))
    stats = pl.BlockSpec((1, 2, rows), lambda i, n: (i, 0, 0))
    extra = (query_weight,) * last + (() if first else (carried,))
    extra_specs = [column(D, 0)] * last + ([] if first else [column(rows, 0)])
    return pl.pallas_call(
        functools.partial(backward_kernel, number, first, last),
        out_shape=(
            jax.ShapeDtypeStruct((rows, D), low if last else full),
            jax.ShapeDtypeStruct((total, D), low),
            jax.ShapeDtypeStruct((total, D), low),
            jax.ShapeDtypeStruct((total, D), low if first else full),
        ),
        grid_spec=pltpu.PrefetchScalarGridSpec(
            num_scalar_prefetch=1,
            grid=(PAIRS,),
            in_specs=[
                column(rows, 0),
                column(total, 0),
                column(total, 0),
                column(rows, 0),
                stats,
                stats,
                column(D, 0),
                column(D, 1),
            ]
            + extra_specs,
            out_specs=[
                column(rows, 0),
                column(total, 0),
                column(total, 0),
                pl.BlockSpec((total, D), lambda i, n: (0, 0)),
            ],
            scratch_shapes=[pltpu.VMEM((total, D), full)],
        ),
        compiler_params=pltpu.CompilerParams(vmem_limit_bytes=VMEM_LIMIT),
        cost_estimate=SMALL_COST,
        name="attend_backward",
    )(
        scalars,
        queries,
        keys,
        values,
        grads,
        logs,
        deltas,
        pair_weight,
        pair_weight,
        *extra,
    )


def swap(value, axis, bit):
    count = lax.axis_size(axis)
    return lax.ppermute(value, axis, [(i, i ^ bit) for i in range(count)])


class Order:
    def __init__(self):
        self.marks = ()

    def __call__(self, *values):
        values = lax.optimization_barrier(values + self.marks)[: len(values)]
        self.marks = values
        return values[0] if len(values) == 1 else values


def outer_bits():
    bits = []
    bit = 2
    while bit < lax.axis_size("dp"):
        bits.append(bit)
        bit *= 2
    return bits


class Gather:
    def __init__(self, parts):
        self.bits = outer_bits()
        half = len(self.bits) // 2
        self.orders = [
            self.bits[half * (n % 2) :] + self.bits[: half * (n % 2)] for n in range(len(parts))
        ]
        self.result = [[([0], part)] for part in parts]
        self.step = 0

    def advance(self, order):
        held = self.result
        if self.step < len(self.bits):
            masks = [[m for mask, _ in pieces for m in mask] for pieces in held]
            blocks = [
                jnp.concatenate([array for _, array in pieces]) if self.step else pieces[0][1]
                for pieces in held
            ]
            blocks = order(*blocks)
            bits = [turn[self.step] for turn in self.orders]
            self.result = [
                [(mask, block), ([m ^ bit for m in mask], swap(block, "dp", bit))]
                for mask, block, bit in zip(masks, blocks, bits)
            ]
        else:
            arrays = order(*[array for pieces in held for _, array in pieces])
            arrays = iter(arrays)
            self.result = []
            for pieces in held:
                kept = [(masks, next(arrays)) for masks, _ in pieces]
                self.result.append(
                    kept + [([m ^ 1 for m in masks], swap(array, "dp", 1)) for masks, array in kept]
                )
        self.step += 1


def canonical_row(me, rank, block, mask, rank_mask, stride, offset):
    if mask is None:
        return offset
    row = (me ^ mask) * block + offset
    if stride:
        if rank_mask >= 2:
            rank_mask = rank_mask ^ ((rank + 1) // 2 % 2)
        row = row + (rank ^ rank_mask) * stride
    return pl.multiple_of(row, 16)


def place_kernel(plan, block, *refs):
    count = len(plan)
    ins = refs[:count]
    outs = refs[count:-1]
    sems = refs[-1]
    me = lax.axis_index("dp")
    rank = lax.axis_index("mp")
    copies = []
    for ref, moves in zip(ins, plan):
        for start, size, which, mask, column, _, offset in moves:
            row = canonical_row(me, rank, block, mask, 0, 0, offset)
            copy = pltpu.make_async_copy(
                ref.at[pl.ds(start, size), :],
                outs[which].at[pl.ds(row, size), pl.ds(column * D, D)],
                sems.at[len(copies)],
            )
            copy.start()
            copies.append(copy)
    for copy in copies:
        copy.wait()


def plan_of(gathered, layouts):
    arrays = []
    plan = []
    for pieces, layout in zip(gathered, layouts):
        rows = sum(size for _, size, *_ in layout)
        for masks, array in pieces:
            moves = []
            for j, mask in enumerate(masks):
                for start, size, which, rank_mask, stride, offset in layout:
                    moves.append((j * rows + start, size, which, mask, rank_mask, stride, offset))
            arrays.append(array)
            plan.append(moves)
    return arrays, plan


def place(arrays, plan, block, shapes):
    return pl.pallas_call(
        functools.partial(place_kernel, plan, block),
        out_shape=[jax.ShapeDtypeStruct(shape, low) for shape in shapes],
        in_specs=[pl.BlockSpec(memory_space=pl.ANY)] * len(arrays),
        out_specs=[pl.BlockSpec(memory_space=pltpu.VMEM)] * len(shapes),
        scratch_shapes=[pltpu.SemaphoreType.DMA((sum(len(moves) for moves in plan),))],
        compiler_params=pltpu.CompilerParams(vmem_limit_bytes=VMEM_LIMIT),
        cost_estimate=SMALL_COST,
        name="place",
    )(*arrays)


def store_split(value, keep, send, index):
    block = keep.shape[2]
    even = lax.axis_index("dp") % 2 == 0
    for outer in range(keep.shape[1]):
        first = value[2 * outer * block : (2 * outer + 1) * block]
        other = value[(2 * outer + 1) * block : (2 * outer + 2) * block]
        keep[index, outer] = jnp.where(even, first, other).astype(low)
        send[index, outer] = jnp.where(even, other, first).astype(low)


def middle_kernel(plan, block, total, *refs):
    limit_ref, vector_ref = refs[:2]
    token_hbm, mixed_hbm, log_hbm, cot_hbm, teach_hbm = refs[2:7]
    pieces = refs[7 : 7 + total]
    (
        out_hbm,
        middle_hbm,
        grad_hbm,
        down_keep,
        down_send,
        up_keep,
        up_send,
        delta_ref,
        log_ref,
        sum_ref,
    ) = refs[7 + total : 17 + total]
    (
        token,
        mixed,
        logs,
        cot,
        teach,
        up,
        down,
        proj,
        right,
        slope,
        second,
        middle,
        final,
        out,
        final_low,
        middle_low,
        grad,
        accum,
        turned,
        stage_keep,
        stage_send,
        in_sems,
        weight_sems,
        out_sems,
        keep_sems,
        send_sems,
    ) = refs[17 + total :]
    hidden = FF // D
    targets = (up, down, proj)
    rows = token.shape[0]
    me = lax.axis_index("dp")
    rank = lax.axis_index("mp")

    def fetch(ref, scratch, n):
        copy = pltpu.make_async_copy(ref, scratch, in_sems.at[n])
        copy.start()
        return copy

    def send(scratch, ref, n):
        copy = pltpu.make_async_copy(scratch, ref, out_sems.at[n])
        copy.start()
        return copy

    gets = [
        fetch(token_hbm, token, 0),
        fetch(mixed_hbm, mixed, 1),
        fetch(log_hbm, logs, 2),
        fetch(cot_hbm, cot, 3),
        fetch(teach_hbm, teach, 4),
    ]
    loads = {0: [], 1: [], 2: []}
    number = 0
    for want in (2, 0, 1):
        for ref, moves in zip(pieces, plan):
            for start, size, which, mask, rank_mask, stride, offset in moves:
                if which != want:
                    continue
                row = canonical_row(me, rank, block, mask, rank_mask, stride, offset)
                copy = pltpu.make_async_copy(
                    ref.at[pl.ds(start, size), :],
                    targets[which].at[pl.ds(row, size), :],
                    weight_sems.at[number],
                )
                copy.start()
                loads[which].append(copy)
                number += 1

    table_row = vector_ref[0:1, :]
    out_bias = vector_ref[1:2, :]
    gain = vector_ref[2:3, :]
    shift = vector_ref[3:4, :]
    down_bias = vector_ref[4:5, :]
    weight = vector_ref[5:6, :]
    gets[0].wait()
    gets[1].wait()
    right[2 * hidden] = mixed[...].astype(low)
    for copy in loads[2]:
        copy.wait()
    state = token[...].astype(full) + table_row + out_bias
    state = state + dot_of(right[2 * hidden], proj[...], 1, 1)
    middle[...] = state
    unit, _ = norm_stats(state)
    second[...] = (unit * gain + shift).astype(low)
    accum[...] = jnp.zeros((rows, D), full)
    for copy in loads[0]:
        copy.wait()
    for copy in loads[1]:
        copy.wait()

    def forward(m, _):
        place = pl.ds(pl.multiple_of(m * D, D), D)
        value = dot_of(second[...], up[place, :], 1, 0) + vector_ref[pl.ds(8 + m, 1), :]
        cumulative = 0.5 + 0.5 * lax.erf(value * (0.5**0.5))
        right[m] = (value * cumulative).astype(low)
        slope[m] = cumulative + value * jnp.exp(-0.5 * value * value) * 0.3989422804014327
        accum[...] += dot_of(right[m], down[place, :], 1, 1)
        return 0

    lax.fori_loop(0, FF // D, forward, 0)
    final_state = middle[...] + accum[...] + down_bias
    out[...] = final_state.astype(low)
    puts = [send(out, out_hbm, 0)]
    gets[3].wait()
    gets[4].wait()
    place = lax.broadcasted_iota(jnp.int32, (rows, 1), 0)
    grads = cot[...].astype(full) + weight * (final_state - teach[...].astype(full))
    grads = jnp.where(place < limit_ref[5], grads, 0.0)
    final[...] = grads
    final_low[...] = grads.astype(low)
    sum_ref[3:4, :] = jnp.sum(grads, axis=0, keepdims=True)
    accum[...] = jnp.zeros((rows, D), full)

    def backward(m, _):
        place = pl.ds(pl.multiple_of(m * D, D), D)
        value = slope[m] * dot_of(final_low[...], down[place, :], 1, 0)
        value = value.astype(low)
        right[hidden + m] = value
        sum_ref[pl.ds(8 + m, 1), :] = jnp.sum(value.astype(full), axis=0, keepdims=True)
        accum[...] += dot_of(value, up[place, :], 1, 1)
        return 0

    lax.fori_loop(0, FF // D, backward, 0)
    unit, inverse = norm_stats(middle[...])
    second_grad = accum[...]
    sum_ref[0:1, :] = jnp.sum(second_grad * unit, axis=0, keepdims=True)
    sum_ref[1:2, :] = jnp.sum(second_grad, axis=0, keepdims=True)
    scaled = second_grad * gain
    mean_scaled = jnp.mean(scaled, axis=-1, keepdims=True)
    mean_unit = jnp.mean(scaled * unit, axis=-1, keepdims=True)
    total_grad = final[...] + inverse * (scaled - mean_scaled - unit * mean_unit)
    middle[...] = total_grad
    puts.append(send(middle, middle_hbm, 1))
    middle_low[...] = total_grad.astype(low)
    sum_ref[2:3, :] = jnp.sum(total_grad, axis=0, keepdims=True)
    attended_grad = dot_of(middle_low[...], proj[...], 1, 0).astype(low)
    grad[...] = attended_grad
    puts.append(send(grad, grad_hbm, 2))
    gets[2].wait()
    head = lax.broadcasted_iota(jnp.int32, (16, D), 0)
    lane = lax.broadcasted_iota(jnp.int32, (16, D), 1)
    member = jnp.where(lane // HEAD_DIM == head, 1.0, 0.0)
    leader = jnp.where(lane == head * HEAD_DIM, 1.0, 0.0)
    exact = functools.partial(
        lax.dot_general,
        dimension_numbers=(((1,), (1,)), ((), ())),
        precision=lax.Precision.HIGHEST,
        preferred_element_type=full,
    )
    deltas = exact(member, attended_grad.astype(full) * mixed[...])
    tops = exact(leader, logs[...])
    for pair in range(PAIRS):
        delta_ref[pair] = deltas[2 * pair : 2 * pair + 2]
        log_ref[pair] = tops[2 * pair : 2 * pair + 2]
    turned[0] = final_low[...].T
    turned[1] = second[...].T
    turned[2] = middle_low[...].T

    def weights(i, _):
        store_split(dot_of(turned[i // hidden], right[i], 1, 0), stage_keep, stage_send, i)

        @pl.when(i < hidden)
        def _():
            pltpu.make_async_copy(stage_keep.at[i], down_keep.at[i], keep_sems.at[i]).start()
            pltpu.make_async_copy(stage_send.at[i], down_send.at[i], send_sems.at[i]).start()

        @pl.when(i >= hidden)
        def _():
            row = i - hidden
            pltpu.make_async_copy(stage_keep.at[i], up_keep.at[row], keep_sems.at[i]).start()
            pltpu.make_async_copy(stage_send.at[i], up_send.at[row], send_sems.at[i]).start()

        return 0

    lax.fori_loop(0, 2 * hidden + 1, weights, 0)
    for copy in puts:
        copy.wait()
    for i in range(2 * hidden + 1):
        if i < hidden:
            keep, gone, row = down_keep, down_send, i
        else:
            keep, gone, row = up_keep, up_send, i - hidden
        pltpu.make_async_copy(stage_keep.at[i], keep.at[row], keep_sems.at[i]).wait()
        pltpu.make_async_copy(stage_send.at[i], gone.at[row], send_sems.at[i]).wait()


def middle_call(limit, vectors, tokens, mixed, logs, cot, teach, arrays, plan, block, dp):
    rows = tokens.shape[0]
    hidden = FF // D
    narrow = jax.ShapeDtypeStruct((rows, D), low)
    wide = jax.ShapeDtypeStruct((rows, D), full)
    shape = (dp // 2, D // dp, D)
    parts = [jax.ShapeDtypeStruct((count,) + shape, low) for count in (hidden, hidden + 1)]
    stats = jax.ShapeDtypeStruct((PAIRS, 2, rows), full)
    anywhere = pl.BlockSpec(memory_space=pl.ANY)
    inside = pl.BlockSpec(memory_space=pltpu.VMEM)
    moves = sum(len(part) for part in plan)
    return pl.pallas_call(
        functools.partial(middle_kernel, plan, block, len(arrays)),
        out_shape=(
            narrow,
            wide,
            narrow,
            parts[0],
            parts[0],
            parts[1],
            parts[1],
            stats,
            stats,
            jax.ShapeDtypeStruct((8 + 8, D), full),
        ),
        in_specs=[pl.BlockSpec(memory_space=pltpu.SMEM), inside]
        + [anywhere] * (5 + len(arrays)),
        out_specs=[anywhere] * 7 + [inside] * 3,
        scratch_shapes=[
            pltpu.VMEM((rows, D), low),
            pltpu.VMEM((rows, D), full),
            pltpu.VMEM((rows, D), full),
            pltpu.VMEM((rows, D), low),
            pltpu.VMEM((rows, D), low),
            pltpu.VMEM((FF, D), low),
            pltpu.VMEM((FF, D), low),
            pltpu.VMEM((D, D), low),
            pltpu.VMEM((2 * hidden + 1, rows, D), low),
            pltpu.VMEM((hidden, rows, D), full),
            pltpu.VMEM((rows, D), low),
            pltpu.VMEM((rows, D), full),
            pltpu.VMEM((rows, D), full),
            pltpu.VMEM((rows, D), low),
            pltpu.VMEM((rows, D), low),
            pltpu.VMEM((rows, D), low),
            pltpu.VMEM((rows, D), low),
            pltpu.VMEM((rows, D), full),
            pltpu.VMEM((3, D, rows), low),
            pltpu.VMEM((2 * hidden + 1,) + shape, low),
            pltpu.VMEM((2 * hidden + 1,) + shape, low),
            pltpu.SemaphoreType.DMA((5,)),
            pltpu.SemaphoreType.DMA((moves,)),
            pltpu.SemaphoreType.DMA((3,)),
            pltpu.SemaphoreType.DMA((2 * hidden + 1,)),
            pltpu.SemaphoreType.DMA((2 * hidden + 1,)),
        ],
        compiler_params=pltpu.CompilerParams(vmem_limit_bytes=VMEM_LIMIT),
        cost_estimate=SMALL_COST,
        name="middle",
    )(limit, vectors, tokens, mixed, logs, cot, teach, *arrays)


def fold_kernel(bits, places, *refs):
    count = len(bits)
    me = lax.axis_index("dp")
    for n in range(count):
        keep, got = refs[2 * n : 2 * n + 2]
        out_keep, out_send = refs[2 * count + 2 * n : 2 * count + 2 * n + 2]
        step = 1 << places[n]
        mine = (me // bits[n]) % 2 * step
        for j in range(keep.shape[1] // 2):
            base = (j // step) * 2 * step + j % step
            for out, shift in ((out_keep, mine), (out_send, step - mine)):
                value = keep[0, base + shift].astype(full) + got[0, base + shift].astype(full)
                out[0, j] = value.astype(low)


def fold(pairs, bits, places):
    lead = pairs[0][0].shape[0]
    block = lambda shape: pl.BlockSpec((1,) + shape[1:], lambda i: (i, 0, 0, 0))
    halves = [
        (keep.shape[0], keep.shape[1] // 2) + keep.shape[2:] for keep, _ in pairs for _ in range(2)
    ]
    outs = pl.pallas_call(
        functools.partial(fold_kernel, bits, places),
        out_shape=[jax.ShapeDtypeStruct(shape, low) for shape in halves],
        grid=(lead,),
        in_specs=[block(value.shape) for pair in pairs for value in pair],
        out_specs=[block(shape) for shape in halves],
        compiler_params=pltpu.CompilerParams(vmem_limit_bytes=VMEM_LIMIT),
        cost_estimate=pl.CostEstimate(flops=0, bytes_accessed=16 << 20, transcendentals=0),
        name="fold",
    )(*[value for pair in pairs for value in pair])
    return [(outs[2 * n], outs[2 * n + 1]) for n in range(len(pairs))]


def qkv_grad_kernel(count, *refs):
    sources = refs[: 3 * count + 1]
    outs = refs[3 * count + 1 : 3 * count + 5]
    sum_ref, held, turned, total, stage, in_sems, out_sems = refs[3 * count + 5 :]
    first_use = [0, count] + list(range(1, count)) + list(range(count + 1, 3 * count + 1))
    for n in first_use:
        pltpu.make_async_copy(sources[n], held.at[n], in_sems.at[n]).start()

    def wait(n):
        pltpu.make_async_copy(sources[0], held.at[n], in_sems.at[n]).wait()

    def turn(n, _):
        wait(n)
        turned[n] = held[n].T
        return 0

    lax.fori_loop(0, count, turn, 0)
    sum_ref[...] = jnp.zeros_like(sum_ref)

    def step(i, _):
        c = (i + count - 1) // count
        n = jnp.where(i == 0, 0, (i + count - 1) % count)
        wait(count + i)
        right = held[count + i]
        value = dot_of(turned[n], right, 1, 0)
        total[...] = value + jnp.where(n == 0, jnp.zeros_like(value), total[...])

        @pl.when(c != 1)
        def _():
            row = pl.ds(pl.multiple_of(c * 4, 8), 1)
            sum_ref[row, :] += jnp.sum(right.astype(full), axis=0, keepdims=True)

        @pl.when(i % count == 0)
        def _():
            for part in range(2):
                store_split(
                    total[:, part * D // 2 : (part + 1) * D // 2],
                    stage.at[part],
                    stage.at[2 + part],
                    c,
                )
            for k in range(4):
                pltpu.make_async_copy(
                    stage.at[k, c], outs[k].at[c], out_sems.at[k * 3 + c]
                ).start()

        return 0

    lax.fori_loop(0, 2 * count + 1, step, 0)
    for k in range(4):
        for c in range(3):
            pltpu.make_async_copy(stage.at[k, c], outs[k].at[c], out_sems.at[k * 3 + c]).wait()


def qkv_grads(chunks, query_grad, key_grads, value_grads, dp):
    rows = query_grad.shape[0]
    count = len(chunks)
    shape = (3, dp // 2, D // dp, D // 2)
    anywhere = pl.BlockSpec(memory_space=pl.ANY)
    return pl.pallas_call(
        functools.partial(qkv_grad_kernel, count),
        out_shape=[jax.ShapeDtypeStruct(shape, low)] * 4
        + [jax.ShapeDtypeStruct((16, D), full)],
        in_specs=[anywhere] * (3 * count + 1),
        out_specs=[anywhere] * 4 + [pl.BlockSpec(memory_space=pltpu.VMEM)],
        scratch_shapes=[
            pltpu.VMEM((3 * count + 1, rows, D), low),
            pltpu.VMEM((count, D, rows), low),
            pltpu.VMEM((D, D), full),
            pltpu.VMEM((4,) + shape, low),
            pltpu.SemaphoreType.DMA((3 * count + 1,)),
            pltpu.SemaphoreType.DMA((12,)),
        ],
        compiler_params=pltpu.CompilerParams(vmem_limit_bytes=VMEM_LIMIT),
        cost_estimate=SMALL_COST,
        name="qkv_grads",
    )(*chunks, query_grad, *key_grads, *value_grads)


def last_kernel(
    token_ref,
    first_ref,
    right_ref,
    left_ref,
    middle_ref,
    vector_ref,
    gain_ref,
    bias_ref,
    sum_ref,
    out_ref,
    pack_ref,
):
    @pl.when(pl.program_id(0) == 0)
    def _():
        pack_ref[...] = jnp.zeros_like(pack_ref)
        pack_ref[1:2, :] = sum_ref[0:1, :]
        pack_ref[3:4, :] = sum_ref[1:2, :]
        pack_ref[4:5, :] = bias_ref[0:1, :]
        pack_ref[5:6, :] = bias_ref[8:9, :]
        pack_ref[6:8, :] = sum_ref[2:4, :]
        pack_ref[8 : 8 + FF // D, :] = sum_ref[8 : 8 + FF // D, :]

    unit, inverse = norm_stats(token_ref[...].astype(full) + vector_ref[0:1, :])
    grad = first_ref[...] + right_ref[...].astype(full) + left_ref[...].astype(full)
    scaled = grad * gain_ref[0:1, :]
    mean_scaled = jnp.mean(scaled, axis=-1, keepdims=True)
    mean_unit = jnp.mean(scaled * unit, axis=-1, keepdims=True)
    result = middle_ref[...] + inverse * (scaled - mean_scaled - unit * mean_unit)
    out_ref[...] = result
    pack_ref[0:1, :] += jnp.sum(grad * unit, axis=0, keepdims=True)
    pack_ref[2:3, :] += jnp.sum(grad, axis=0, keepdims=True)
    pack_ref[pl.ds(16 + lax.axis_index("dp"), 1), :] += jnp.sum(result, axis=0, keepdims=True)


def last_norm(tokens, first, right, left, middle_grad, vectors, gains, bias_sums, sums, dp):
    rows = tokens.shape[0]
    part = pl.BlockSpec((rows // 4, D), lambda i: (i, 0))
    whole = lambda value: pl.BlockSpec(value.shape, lambda i: (0, 0))
    small = (vectors, gains, bias_sums, sums)
    return pl.pallas_call(
        last_kernel,
        out_shape=(
            jax.ShapeDtypeStruct((rows, D), full),
            jax.ShapeDtypeStruct((16 + dp, D), full),
        ),
        grid=(4,),
        in_specs=[part] * 5 + [whole(value) for value in small],
        out_specs=[part, pl.BlockSpec((16 + dp, D), lambda i: (0, 0))],
        compiler_params=pltpu.CompilerParams(vmem_limit_bytes=VMEM_LIMIT),
        cost_estimate=SMALL_COST,
        name="last_norm",
    )(tokens, first, right, left, middle_grad, *small)


def two_parts(value, axis, mine):
    keep = lax.dynamic_index_in_dim(value, mine, axis, keepdims=False)
    send = lax.dynamic_index_in_dim(value, 1 - mine, axis, keepdims=False)
    return keep, send.astype(low)


def scatter_dp(parts, turns):
    bits = outer_bits()
    half = len(bits) // 2
    orders = [[1] + bits[half * (turn % 2) :] + bits[: half * (turn % 2)] for turn in turns]
    left = [list(bits) for _ in turns]
    for step in range(len(bits) + 1):
        sends = yield [send for _, send in parts]
        got = [swap(send, "dp", turn[step]) for send, turn in zip(sends, orders)]
        pairs = [(keep, other) for (keep, _), other in zip(parts, got)]
        if step < len(bits):
            places = []
            for n, turn in enumerate(orders):
                places.append(left[n].index(turn[step + 1]))
                left[n].remove(turn[step + 1])
            parts = fold(pairs, [turn[step + 1] for turn in orders], places)
    got = yield [other for _, other in pairs]
    return [
        (keep.astype(full) + other.astype(full))[:, 0] for (keep, _), other in zip(pairs, got)
    ]


def scatter_mp(value):
    rank = lax.axis_index("mp")
    part = lambda index: lax.dynamic_index_in_dim(value, index, keepdims=False)
    sends = yield [part(rank ^ bit).astype(low) for bit in (1, 2, 3)]
    got = yield [swap(send, "mp", bit) for bit, send in zip((1, 2, 3), sends)]
    got = [other.astype(full) for other in got]
    return (part(rank) + got[0]) + (got[1] + got[2])


def scatter_feed(up_own, down_own):
    mp = lax.axis_size("mp")
    block = down_own.shape[1]
    out_own = up_own[mp].reshape(block, mp, -1).transpose(1, 0, 2)
    own = yield from scatter_mp(
        jnp.concatenate([up_own[:mp], down_own, out_own.reshape(mp, -1, D)], axis=1)
    )
    return own[:block], own[block : 2 * block].T, own[2 * block :].reshape(block, -1).T


def scatter_qkv(keep_left, keep_right, send_left, send_right):
    left_part, right_part = yield from scatter_dp(
        [(keep_left, send_left), (keep_right, send_right)], (0, 1)
    )
    width = D // lax.axis_size("mp")
    parts = [part[..., at : at + width] for part in (left_part, right_part) for at in (0, width)]
    return (yield from scatter_mp(jnp.stack(parts)))


def sum_small(value):
    (value,) = yield [value]
    value = value + swap(value, "dp", 1)
    bits = outer_bits()
    groups = [("dp", bits[n : n + 2]) for n in range(0, len(bits), 2)] + [("mp", [1, 2])]
    for axis, pair in groups:
        (value,) = yield [value]
        if len(pair) == 1:
            value = value + swap(value, axis, pair[0])
        else:
            one, two = pair
            got = [swap(value, axis, mask) for mask in (one, two, one + two)]
            if axis == "mp":
                got = yield got
            value = (value + got[0]) + (got[1] + got[2])
    return value


class Steps:
    def __init__(self, steps):
        self.steps = steps
        self.pending = next(steps)
        self.result = None

    def advance(self, order):
        if self.pending is None:
            return
        sends = order(*self.pending)
        sends = [sends] if len(self.pending) == 1 else list(sends)
        try:
            self.pending = self.steps.send(sends)
        except StopIteration as stop:
            self.pending = None
            self.result = stop.value

    def finish(self, order):
        while self.pending is not None:
            self.advance(order)
        return self.result


def shards(
    tokens_in,
    timesteps,
    lengths,
    time_table,
    norm_gains,
    norm_biases,
    w_qkv,
    qv_bias,
    w_out,
    out_bias,
    w_up,
    up_bias,
    w_down,
    down_bias,
    cotangent,
    teacher,
):
    rank = lax.axis_index("mp")
    data_rank = lax.axis_index("dp")
    mp = lax.axis_size("mp")
    dp = lax.axis_size("dp")
    own_rows = tokens_in.shape[0]
    length = lax.dynamic_index_in_dim(lengths, data_rank, keepdims=False)
    own_time = lax.dynamic_index_in_dim(timesteps, data_rank, keepdims=False)
    odd = rank % 2 == 1
    upper = rank >= 2
    middle = jnp.logical_or(rank == 1, rank == 2)
    order = Order()
    along = lambda value, pairs: lax.ppermute(value, "mp", pairs)

    block = w_qkv.shape[1]
    aligned = block % 32 == 0
    narrow = order(jnp.concatenate([w_qkv.reshape(3 * block, -1), w_out.T]))
    first_swap = swap(narrow, "mp", 1)
    tall = order(jnp.concatenate([w_up, w_down.T]))
    tall_swap = swap(tall, "mp", 1)
    pair = order(
        jnp.concatenate(
            [jnp.where(odd, first_swap, narrow), jnp.where(odd, narrow, first_swap)], axis=1
        )
    )
    second_swap = swap(pair, "mp", 2)
    tokens, lengths, own_time, norm_gains, norm_biases, out_bias, down_bias, up_bias, length = order(
        tokens_in, lengths, own_time, norm_gains, norm_biases, out_bias, down_bias, up_bias, length
    )
    table_row = lax.dynamic_slice_in_dim(time_table, own_time, 1).astype(full)
    unit_one, _ = norm_stats(tokens.astype(full) + table_row)
    first_norm = (unit_one * norm_gains[0] + norm_biases[0]).astype(low)
    loss_weight = lengths.shape[0] * MAXLEN / jnp.sum(lengths).astype(full)
    vectors = jnp.concatenate(
        [
            table_row,
            out_bias[None],
            norm_gains[1:2],
            norm_biases[1:2],
            down_bias[None],
            jnp.full((3, D), loss_weight),
            up_bias.reshape(-1, D),
            jnp.zeros((4, D), full),
        ]
    )
    scalars = jnp.stack(
        [
            rank,
            jnp.where(rank == 0, 1, rank - 1),
            jnp.where(upper, rank - 2, rank + 2),
            jnp.where(middle, rank + 1, 3 - rank),
            length,
            length - rank * own_rows,
        ]
    ).astype(jnp.int32)
    first_norm, vectors, scalars = order(first_norm, vectors, scalars)
    wide = jnp.concatenate(
        [jnp.where(upper, second_swap, pair), jnp.where(upper, pair, second_swap)], axis=1
    )
    qkv_rows, out_rows = wide[: 3 * block], wide[3 * block :]
    if aligned:
        split = 3 * block // 2
        qkv_gather = Gather([qkv_rows[:split], qkv_rows[split:]])
        qkv_gather.advance(order)
    tall = order(jnp.concatenate([tall, tall_swap]))
    tall_across = along(tall, [(1, 2), (2, 1)])

    if aligned:
        while qkv_gather.step < len(qkv_gather.bits):
            qkv_gather.advance(order)
    tall_across = order(tall_across)
    tall_other = jnp.where(middle, tall_across, along(tall_across, [(1, 0), (2, 3)]))
    sent = order(first_norm)
    from_left = along(sent, [(0, 1), (1, 2), (2, 3)])
    from_right = along(sent, [(1, 0), (2, 1), (3, 2)])
    if aligned:
        feed_gather = Gather(
            [
                jnp.concatenate([tall, out_rows[: block // 2]]),
                jnp.concatenate([tall_other, out_rows[block // 2 :]]),
            ]
        )
        qkv_gather.advance(order)
        arrays, plan = plan_of(
            qkv_gather.result,
            [
                [(0, block, 0, 0, 0, 0), (block, split - block, 1, 0, 0, 0)],
                [
                    (0, 2 * block - split, 1, 0, 0, split - block),
                    (2 * block - split, block, 1, 1, 0, 0),
                ],
            ],
        )
        query_weight, pair_weight = order(*place(arrays, plan, block, [(D, D), (D, 2 * D)]))
        feed_gather.advance(order)
    else:
        weights = lax.all_gather(qkv_rows.reshape(3, block, D), "dp", axis=1, tiled=True)
        query_weight = weights[0]
        pair_weight = jnp.concatenate([weights[1], weights[2]], axis=1)
    hop_right, hop_left = order(from_left, from_right)
    second_right = along(hop_right, [(1, 2), (2, 3)])
    second_left = along(hop_left, [(1, 0), (2, 1)])
    near = jnp.where(rank == 0, hop_left, hop_right)
    if aligned:
        while feed_gather.step < len(feed_gather.bits):
            feed_gather.advance(order)
    attend = lambda chunks, numbers, carried: attend_forward(
        chunks,
        numbers,
        scalars,
        query_weight,
        pair_weight,
        qv_bias[0:1],
        qv_bias[1:2],
        carried,
    )
    key_own, key_near, value_own, value_near, queries, *state = order(
        *attend(order(first_norm, near), (0, 1), None)
    )
    second = order(jnp.where(upper, second_right, second_left))
    third = along(second, [(1, 0), (2, 3)])
    key_second, value_second, *state = attend([second], (2,), (queries, *state))
    key_second, value_second, *state = order(key_second, value_second, *state)
    last = order(jnp.where(middle, hop_left, third))
    if aligned:
        feed_gather.advance(order)
    key_last, value_last, mixed, logs = order(*attend([order(last)], (3,), (queries, *state)))
    if aligned:
        layout = lambda masks, shift: [
            (0, block, 0, masks[0], D, 0),
            (block, block, 1, masks[0], D, 0),
            (2 * block, block, 0, masks[1], D, 0),
            (3 * block, block, 1, masks[1], D, 0),
            (4 * block, block // 2, 2, 0, 0, shift),
        ]
        arrays, plan = plan_of(
            feed_gather.result, [layout((0, 1), 0), layout((2, 3), block // 2)]
        )
    else:
        arrays = [
            lax.all_gather(w_up, ("mp", "dp"), axis=0, tiled=True),
            lax.all_gather(w_down.T, ("mp", "dp"), axis=0, tiled=True),
            lax.all_gather(out_rows, "dp", axis=0, tiled=True),
        ]
        plan = [[(0, array.shape[0], n, None, 0, 0, 0)] for n, array in enumerate(arrays)]
    chunks = [first_norm, near, second, last]
    keys = [key_own, key_near, key_second, key_last]
    values = [value_own, value_near, value_second, value_last]

    output, middle_grad, attended_grad, *parts, deltas, log_rows, sums = middle_call(
        scalars, vectors, tokens, mixed, logs, cotangent, teacher, arrays, plan, block, dp
    )
    down = Steps(scatter_dp([(parts[0], parts[1])], (1,)))
    down.advance(order)
    up = Steps(scatter_dp([(parts[2], parts[3])], (0,)))
    up.advance(order)

    key_grads = [None] * 4
    value_grads = [None] * 4
    firsts = [None] * 4
    query_grad = None
    for n in (3, 2, 1, 0):
        query_grad, key_grads[n], value_grads[n], firsts[n] = attend_backward(
            n,
            queries,
            keys[n],
            values[n],
            order(attended_grad),
            log_rows,
            deltas,
            query_weight,
            pair_weight,
            scalars,
            query_grad,
            n == 0,
        )
        firsts[n] = order(firsts[n])
        if n == 3:
            down.advance(order)
            up.advance(order)
            back_last = along(firsts[3], [(0, 1), (3, 2)]).astype(full)
        elif n == 2:
            payload = order((firsts[2] + back_last).astype(low))
            back_right = along(payload, [(0, 1), (1, 2)]).astype(full)
            back_left = along(payload, [(3, 2), (2, 1)]).astype(full)
        elif n == 1:
            down.advance(order)
            up.advance(order)
            to_right = jnp.where(
                rank == 0, firsts[1], firsts[3].astype(full) + back_right
            ).astype(low)
            to_left = (firsts[1] + back_left).astype(low)
            to_right, to_left = order(to_right, to_left)
            final_right = along(to_right, [(0, 1), (1, 2), (2, 3)])
            final_left = along(to_left, [(3, 2), (2, 1), (1, 0)])
    (up_own,) = up.finish(order)
    (down_own,) = down.finish(order)
    feed = Steps(scatter_feed(up_own, down_own))
    feed.advance(order)
    query_grad, final_right, final_left = order(query_grad, final_right, final_left)
    *halves, bias_sums = qkv_grads(chunks, query_grad, key_grads, value_grads, dp)
    qkv = Steps(scatter_qkv(*halves))
    qkv.advance(order)
    tokens, first_own = order(tokens, firsts[0])
    input_grad, packed = last_norm(
        tokens,
        first_own,
        final_right,
        final_left,
        middle_grad,
        vectors,
        norm_gains,
        bias_sums,
        sums,
        dp,
    )
    packed, input_grad = order(packed, input_grad)
    small = Steps(sum_small(packed))
    qkv.advance(order)
    small.advance(order)
    small.advance(order)
    feed.advance(order)
    qkv.advance(order)
    small.advance(order)
    qkv.advance(order)
    qkv.advance(order)
    total = small.finish(order)
    qkv_grad = qkv.finish(order)
    up_grad, down_grad, out_grad = feed.finish(order)
    fixed = 16
    chosen = (timesteps[None, :] == jnp.arange(time_table.shape[0])[:, None]).astype(full)
    table_grad = lax.dot_general(
        chosen,
        total[fixed:],
        (((1,), (0,)), ((), ())),
        precision=lax.Precision.HIGHEST,
        preferred_element_type=full,
    )
    return (
        output,
        input_grad,
        table_grad,
        total[0:2],
        total[2:4],
        qkv_grad,
        total[4:6],
        out_grad,
        total[6],
        up_grad,
        total[8 : 8 + FF // D].reshape(FF),
        down_grad,
        total[7],
    )


def solution(mesh):
    rows = P(both, None)
    placed = (
        rows,
        P(),
        P(),
        P(),
        P(),
        P(),
        P(None, "dp", "mp"),
        P(),
        P("mp", "dp"),
        P(),
        P("dp", "mp"),
        P(),
        P("mp", "dp"),
        P(),
        rows,
        rows,
    )
    return jax.shard_map(
        shards,
        mesh=mesh,
        in_specs=placed,
        out_specs=(
            rows,
            rows,
            P(),
            P(),
            P(),
            P(None, "dp", "mp"),
            P(),
            P("mp", "dp"),
            P(),
            P("dp", "mp"),
            P(),
            P("mp", "dp"),
            P(),
        ),
        check_vma=False,
    )
```

```python
import functools

import jax
import jax.numpy as jnp
from jax import lax
from jax.experimental import pallas as pl
from jax.experimental.pallas import tpu as pltpu
from jax.sharding import PartitionSpec as P

D = 768
HEADS = 12
HEAD_DIM = 64
FF = 3072
MAXLEN = 2048
PAIR = 2 * HEAD_DIM
PAIRS = HEADS // 2
VMEM_LIMIT = 58 << 20
SMALL_COST = pl.CostEstimate(flops=1 << 20, bytes_accessed=1 << 16, transcendentals=0)

far_below = -1e30
epsilon = 1e-05
score_scale = HEAD_DIM ** (-0.5)
low = jnp.bfloat16
full = jnp.float32
both = ("dp", "mp")


def norm_stats(values):
    center = values - jnp.mean(values, axis=-1, keepdims=True)
    spread = jnp.mean(center * center, axis=-1, keepdims=True)
    inverse = lax.rsqrt(spread + epsilon)
    return center * inverse, inverse


def dot_of(left_side, right_side, left_dim, right_dim):
    return lax.dot_general(
        left_side,
        right_side,
        (((left_dim,), (right_dim,)), ((), ())),
        preferred_element_type=full,
    )


def first_half(shape):
    return lax.broadcasted_iota(jnp.int32, shape, len(shape) - 1) < HEAD_DIM


def forward_kernel(numbers, first, final, scalars, *refs):
    count = len(numbers)
    chunk_refs = refs[:count]
    wk_ref, wv_ref, value_bias_ref = refs[count : count + 3]
    refs = refs[count + 3 :]
    if first:
        wq_ref, query_bias_ref = refs[:2]
        key_outs, value_outs = refs[2 : 2 + count], refs[2 + count : 2 + 2 * count]
        query_out, top_ref, sum_ref, acc_ref = refs[2 + 2 * count :]
        q_pair = (dot_of(chunk_refs[0][...], wq_ref[...], 1, 0) + query_bias_ref[...]).astype(low)
        q_pair = q_pair * jnp.asarray(score_scale, low)
        query_out[...] = q_pair
    else:
        q_ref, top_in, sum_in, acc_in = refs[:4]
        key_outs, value_outs = refs[4 : 4 + count], refs[4 + count : 4 + 2 * count]
        results = refs[4 + 2 * count :]
        q_pair = q_ref[...]
    weight = jnp.concatenate([wk_ref[...], wv_ref[...]], axis=1)
    keys = []
    values = []
    for n in range(count):
        both_parts = dot_of(chunk_refs[n][...], weight, 1, 0)
        keys.append(both_parts[:, :PAIR].astype(low))
        values.append((both_parts[:, PAIR:] + value_bias_ref[...]).astype(low))
        key_outs[n][...] = keys[n]
        value_outs[n][...] = values[n]
    rows = q_pair.shape[0]
    size = keys[0].shape[0]
    place = lax.broadcasted_iota(jnp.int32, (1, size), 1)
    lower = first_half((rows, PAIR))
    parts = []
    for half in range(2):
        kept = lower if half == 0 else jnp.logical_not(lower)
        q_half = jnp.where(kept, q_pair, jnp.zeros_like(q_pair))
        scores = []
        for n in range(count):
            bias = jnp.where(place + scalars[numbers[n]] * size < scalars[4], 0.0, far_below)
            scores.append(dot_of(q_half, keys[n], 1, 1) + bias)
        highest = functools.reduce(
            jnp.maximum, [jnp.max(score, axis=-1, keepdims=True) for score in scores]
        )
        totals = jnp.zeros_like(highest)
        mixed = jnp.zeros((rows, PAIR), full)
        for n in range(count):
            exp_scores = jnp.exp(scores[n] - highest)
            totals = totals + jnp.sum(exp_scores, axis=-1, keepdims=True)
            mixed = mixed + dot_of(exp_scores.astype(low), values[n], 1, 0)
        parts.append((highest, totals, mixed))
    top = jnp.where(lower, parts[0][0], parts[1][0])
    total = jnp.where(lower, parts[0][1], parts[1][1])
    mixed = jnp.where(lower, parts[0][2], parts[1][2])
    if first:
        top_ref[...] = top
        sum_ref[...] = total
        acc_ref[...] = mixed
    else:
        highest = jnp.maximum(top, top_in[...])
        here = jnp.exp(top - highest)
        before = jnp.exp(top_in[...] - highest)
        total = total * here + sum_in[...] * before
        mixed = mixed * here + acc_in[...] * before
        if final:
            results[0][...] = mixed / total
            results[1][...] = highest + jnp.log(total)
        else:
            results[0][...] = highest
            results[1][...] = total
            results[2][...] = mixed


def attend_forward(chunks, numbers, scalars, query_weight, pair_weight, query_bias, value_bias, carried):
    rows = chunks[0].shape[0]
    count = len(chunks)
    first = carried is None
    final = 3 in numbers
    column = lambda height, c: pl.BlockSpec((height, PAIR), lambda i, n: (0, c * PAIRS + i))
    whole = pl.BlockSpec((rows, D), lambda i, n: (0, 0))
    wide = jax.ShapeDtypeStruct((rows, D), full)
    narrow = jax.ShapeDtypeStruct((rows, D), low)
    extra = (query_weight, query_bias) if first else carried
    results = (narrow,) * first + (wide,) * (2 if final else 3)
    return pl.pallas_call(
        functools.partial(forward_kernel, numbers, first, final),
        out_shape=(narrow,) * (2 * count) + results,
        grid_spec=pltpu.PrefetchScalarGridSpec(
            num_scalar_prefetch=1,
            grid=(PAIRS,),
            in_specs=[whole] * count
            + [column(D, 0), column(D, 1), column(1, 0)]
            + ([column(D, 0), column(1, 0)] if first else [column(rows, 0)] * 4),
            out_specs=[column(rows, 0)] * (2 * count + len(results)),
        ),
        compiler_params=pltpu.CompilerParams(vmem_limit_bytes=VMEM_LIMIT),
        cost_estimate=SMALL_COST,
        name="attend_forward",
    )(scalars, *chunks, pair_weight, pair_weight, value_bias, *extra)


def backward_kernel(
    number,
    first,
    last,
    folds,
    scalars,
    q_ref,
    k_ref,
    v_ref,
    g_ref,
    log_ref,
    delta_ref,
    wk_ref,
    wv_ref,
    *refs
):
    if last:
        wq_ref = refs[0]
        refs = refs[1:]
    if not first:
        dq_in = refs[0]
        refs = refs[1:]
    count = len(folds)
    fold_ins, refs = refs[: 2 * count], refs[2 * count :]
    dq_ref, dk_ref, dv_ref, back_ref = refs[:4]
    fold_outs, accum = refs[4:-1], refs[-1]
    step = pl.program_id(0)
    for n, (lead, bit, at) in enumerate(folds):

        @pl.when(step < lead)
        def _():
            fold_block(
                *fold_ins[2 * n : 2 * n + 2], *fold_outs[2 * n : 2 * n + 2], bit, at
            )

    rows = q_ref.shape[0]
    keys = k_ref.shape[0]
    limit = scalars[4] - scalars[number] * keys
    q_pair = q_ref[...]
    g_pair = g_ref[...]
    k_pair = k_ref[...]
    v_pair = v_ref[...]
    lower = first_half((rows, PAIR))
    nothing = jnp.zeros((rows, PAIR), low)
    two_halves = lambda pair: jnp.concatenate(
        [jnp.where(lower, pair, nothing), jnp.where(lower, nothing, pair)]
    )
    queries = two_halves(q_pair)
    grads_out = two_halves(g_pair)
    row_of = lambda ref: jnp.concatenate([ref[0, 0:1, :], ref[0, 1:2, :]], axis=1)
    place = lax.broadcasted_iota(jnp.int32, (keys, 1), 0)
    bias = jnp.where(place < limit, 0.0, far_below)
    scores = dot_of(k_pair, queries, 1, 1) + bias
    prob_grad = dot_of(v_pair, grads_out, 1, 1)
    probs = jnp.exp(scores - row_of(log_ref))
    score_grad = (probs * (prob_grad - row_of(delta_ref))).astype(low)
    dv_low = dot_of(probs.astype(low), grads_out, 1, 0).astype(low)
    dk_low = dot_of(score_grad, queries, 1, 0).astype(low)
    turned = dot_of(k_pair.T, score_grad, 1, 0)
    upper_rows = lax.broadcasted_iota(jnp.int32, (PAIR, rows), 0) < HEAD_DIM
    dk_ref[...] = dk_low
    dv_ref[...] = dv_low
    grads = [dk_low, dv_low]
    weights = [wk_ref[...], wv_ref[...]]
    dq_all = jnp.where(upper_rows, turned[:, :rows], turned[:, rows:]).T
    if not first:
        dq_all = dq_all + dq_in[...]
    back = dot_of(jnp.concatenate(grads, axis=1), jnp.concatenate(weights, axis=1), 1, 1)
    if last:
        dq_low = (dq_all * score_scale).astype(low)
        dq_ref[...] = dq_low
        back = back + dot_of(dq_low, wq_ref[...], 1, 1)
    else:
        dq_ref[...] = dq_all

    @pl.when(step == 0)
    def _():
        accum[...] = back

    @pl.when(step > 0)
    def _():
        accum[...] += back

    @pl.when(step == PAIRS - 1)
    def _():
        back_ref[...] = accum[...].astype(back_ref.dtype)


def attend_backward(
    number,
    queries,
    keys,
    values,
    grads,
    logs,
    deltas,
    query_weight,
    pair_weight,
    scalars,
    carried,
    last,
    pairs,
    bits,
    places,
):
    rows, total = queries.shape[0], keys.shape[0]
    first = carried is None
    folds = [(keep.shape[0], bit, at) for (keep, _), bit, at in zip(pairs, bits, places)]
    halves = [
        (keep.shape[0], keep.shape[1] // 2) + keep.shape[2:] for keep, _ in pairs for _ in range(2)
    ]

    def by_lead(shape):
        end = shape[0] - 1
        return pl.BlockSpec((1,) + shape[1:], lambda i, n: (jnp.minimum(i, end), 0, 0, 0))

    column = lambda count, c: pl.BlockSpec((count, PAIR), lambda i, n: (0, c * PAIRS + i))
    stats = pl.BlockSpec((1, 2, rows), lambda i, n: (i, 0, 0))
    extra = (query_weight,) * last + (() if first else (carried,))
    extra_specs = [column(D, 0)] * last + ([] if first else [column(rows, 0)])
    return pl.pallas_call(
        functools.partial(backward_kernel, number, first, last, folds),
        out_shape=(
            jax.ShapeDtypeStruct((rows, D), low if last else full),
            jax.ShapeDtypeStruct((total, D), low),
            jax.ShapeDtypeStruct((total, D), low),
            jax.ShapeDtypeStruct((total, D), low if first else full),
            *[jax.ShapeDtypeStruct(shape, low) for shape in halves],
        ),
        grid_spec=pltpu.PrefetchScalarGridSpec(
            num_scalar_prefetch=1,
            grid=(PAIRS,),
            in_specs=[
                column(rows, 0),
                column(total, 0),
                column(total, 0),
                column(rows, 0),
                stats,
                stats,
                column(D, 0),
                column(D, 1),
            ]
            + extra_specs
            + [by_lead(value.shape) for pair in pairs for value in pair],
            out_specs=[
                column(rows, 0),
                column(total, 0),
                column(total, 0),
                pl.BlockSpec((total, D), lambda i, n: (0, 0)),
            ]
            + [by_lead(shape) for shape in halves],
            scratch_shapes=[pltpu.VMEM((total, D), full)],
        ),
        compiler_params=pltpu.CompilerParams(vmem_limit_bytes=VMEM_LIMIT),
        cost_estimate=SMALL_COST,
        name="attend_backward",
    )(
        scalars,
        queries,
        keys,
        values,
        grads,
        logs,
        deltas,
        pair_weight,
        pair_weight,
        *extra,
        *[value for pair in pairs for value in pair],
    )


def swap(value, axis, bit):
    count = lax.axis_size(axis)
    return lax.ppermute(value, axis, [(i, i ^ bit) for i in range(count)])


class Order:
    def __init__(self):
        self.marks = ()

    def __call__(self, *values):
        values = lax.optimization_barrier(values + self.marks)[: len(values)]
        self.marks = values
        return values[0] if len(values) == 1 else values


def outer_bits():
    bits = []
    bit = 2
    while bit < lax.axis_size("dp"):
        bits.append(bit)
        bit *= 2
    return bits


class Gather:
    def __init__(self, parts):
        self.bits = outer_bits()
        half = len(self.bits) // 2
        self.orders = [
            self.bits[half * (n % 2) :] + self.bits[: half * (n % 2)] for n in range(len(parts))
        ]
        self.result = [[([0], part)] for part in parts]
        self.step = 0

    def advance(self, order):
        held = self.result
        if self.step < len(self.bits):
            masks = [[m for mask, _ in pieces for m in mask] for pieces in held]
            blocks = [
                jnp.concatenate([array for _, array in pieces]) if self.step else pieces[0][1]
                for pieces in held
            ]
            blocks = order(*blocks)
            bits = [turn[self.step] for turn in self.orders]
            self.result = [
                [(mask, block), ([m ^ bit for m in mask], swap(block, "dp", bit))]
                for mask, block, bit in zip(masks, blocks, bits)
            ]
        else:
            arrays = order(*[array for pieces in held for _, array in pieces])
            arrays = iter(arrays)
            self.result = []
            for pieces in held:
                kept = [(masks, next(arrays)) for masks, _ in pieces]
                self.result.append(
                    kept + [([m ^ 1 for m in masks], swap(array, "dp", 1)) for masks, array in kept]
                )
        self.step += 1


def canonical_row(me, rank, block, mask, rank_mask, stride, offset):
    if mask is None:
        return offset
    row = (me ^ mask) * block + offset
    if stride:
        if rank_mask >= 2:
            rank_mask = rank_mask ^ ((rank + 1) // 2 % 2)
        row = row + (rank ^ rank_mask) * stride
    return pl.multiple_of(row, 16)


def place_kernel(plan, block, *refs):
    count = len(plan)
    ins = refs[:count]
    outs = refs[count:-1]
    sems = refs[-1]
    me = lax.axis_index("dp")
    rank = lax.axis_index("mp")
    copies = []
    for ref, moves in zip(ins, plan):
        for start, size, which, mask, column, _, offset in moves:
            row = canonical_row(me, rank, block, mask, 0, 0, offset)
            copy = pltpu.make_async_copy(
                ref.at[pl.ds(start, size), :],
                outs[which].at[pl.ds(row, size), pl.ds(column * D, D)],
                sems.at[len(copies)],
            )
            copy.start()
            copies.append(copy)
    for copy in copies:
        copy.wait()


def plan_of(gathered, layouts):
    arrays = []
    plan = []
    for pieces, layout in zip(gathered, layouts):
        rows = sum(size for _, size, *_ in layout)
        for masks, array in pieces:
            moves = []
            for j, mask in enumerate(masks):
                for start, size, which, rank_mask, stride, offset in layout:
                    moves.append((j * rows + start, size, which, mask, rank_mask, stride, offset))
            arrays.append(array)
            plan.append(moves)
    return arrays, plan


def place(arrays, plan, block, shapes):
    return pl.pallas_call(
        functools.partial(place_kernel, plan, block),
        out_shape=[jax.ShapeDtypeStruct(shape, low) for shape in shapes],
        in_specs=[pl.BlockSpec(memory_space=pl.ANY)] * len(arrays),
        out_specs=[pl.BlockSpec(memory_space=pltpu.VMEM)] * len(shapes),
        scratch_shapes=[pltpu.SemaphoreType.DMA((sum(len(moves) for moves in plan),))],
        compiler_params=pltpu.CompilerParams(vmem_limit_bytes=VMEM_LIMIT),
        cost_estimate=SMALL_COST,
        name="place",
    )(*arrays)


def store_split(value, keep, send, index):
    block = keep.shape[2]
    even = lax.axis_index("dp") % 2 == 0
    for outer in range(keep.shape[1]):
        first = value[2 * outer * block : (2 * outer + 1) * block]
        other = value[(2 * outer + 1) * block : (2 * outer + 2) * block]
        keep[index, outer] = jnp.where(even, first, other).astype(low)
        send[index, outer] = jnp.where(even, other, first).astype(low)


def middle_kernel(plan, block, total, *refs):
    limit_ref, vector_ref = refs[:2]
    token_hbm, mixed_hbm, log_hbm, cot_hbm, teach_hbm = refs[2:7]
    pieces = refs[7 : 7 + total]
    (
        out_hbm,
        middle_hbm,
        grad_hbm,
        down_keep,
        down_send,
        up_keep,
        up_send,
        delta_ref,
        log_ref,
        sum_ref,
    ) = refs[7 + total : 17 + total]
    (
        token,
        mixed,
        logs,
        cot,
        teach,
        up,
        down,
        proj,
        right,
        slope,
        second,
        middle,
        final,
        out,
        final_low,
        middle_low,
        grad,
        accum,
        turned,
        stage_keep,
        stage_send,
        in_sems,
        weight_sems,
        out_sems,
        keep_sems,
        send_sems,
    ) = refs[17 + total :]
    hidden = FF // D
    targets = (up, down, proj)
    rows = token.shape[0]
    me = lax.axis_index("dp")
    rank = lax.axis_index("mp")

    def fetch(ref, scratch, n):
        copy = pltpu.make_async_copy(ref, scratch, in_sems.at[n])
        copy.start()
        return copy

    def send(scratch, ref, n):
        copy = pltpu.make_async_copy(scratch, ref, out_sems.at[n])
        copy.start()
        return copy

    gets = [
        fetch(token_hbm, token, 0),
        fetch(mixed_hbm, mixed, 1),
        fetch(log_hbm, logs, 2),
        fetch(cot_hbm, cot, 3),
        fetch(teach_hbm, teach, 4),
    ]
    loads = {0: [], 1: [], 2: []}
    number = 0
    for want in (2, 0, 1):
        for ref, moves in zip(pieces, plan):
            for start, size, which, mask, rank_mask, stride, offset in moves:
                if which != want:
                    continue
                row = canonical_row(me, rank, block, mask, rank_mask, stride, offset)
                copy = pltpu.make_async_copy(
                    ref.at[pl.ds(start, size), :],
                    targets[which].at[pl.ds(row, size), :],
                    weight_sems.at[number],
                )
                copy.start()
                loads[which].append(copy)
                number += 1

    table_row = vector_ref[0:1, :]
    out_bias = vector_ref[1:2, :]
    gain = vector_ref[2:3, :]
    shift = vector_ref[3:4, :]
    down_bias = vector_ref[4:5, :]
    weight = vector_ref[5:6, :]
    gets[0].wait()
    gets[1].wait()
    right[2 * hidden] = mixed[...].astype(low)
    for copy in loads[2]:
        copy.wait()
    state = token[...].astype(full) + table_row + out_bias
    state = state + dot_of(right[2 * hidden], proj[...], 1, 1)
    middle[...] = state
    unit, _ = norm_stats(state)
    second[...] = (unit * gain + shift).astype(low)
    accum[...] = jnp.zeros((rows, D), full)
    for copy in loads[0]:
        copy.wait()
    for copy in loads[1]:
        copy.wait()

    def forward(m, _):
        place = pl.ds(pl.multiple_of(m * D, D), D)
        value = dot_of(second[...], up[place, :], 1, 0) + vector_ref[pl.ds(8 + m, 1), :]
        cumulative = 0.5 + 0.5 * lax.erf(value * (0.5**0.5))
        right[m] = (value * cumulative).astype(low)
        slope[m] = cumulative + value * jnp.exp(-0.5 * value * value) * 0.3989422804014327
        accum[...] += dot_of(right[m], down[place, :], 1, 1)
        return 0

    lax.fori_loop(0, FF // D, forward, 0)
    final_state = middle[...] + accum[...] + down_bias
    out[...] = final_state.astype(low)
    puts = [send(out, out_hbm, 0)]
    gets[3].wait()
    gets[4].wait()
    place = lax.broadcasted_iota(jnp.int32, (rows, 1), 0)
    grads = cot[...].astype(full) + weight * (final_state - teach[...].astype(full))
    grads = jnp.where(place < limit_ref[5], grads, 0.0)
    final[...] = grads
    final_low[...] = grads.astype(low)
    sum_ref[3:4, :] = jnp.sum(grads, axis=0, keepdims=True)
    accum[...] = jnp.zeros((rows, D), full)

    def backward(m, _):
        place = pl.ds(pl.multiple_of(m * D, D), D)
        value = slope[m] * dot_of(final_low[...], down[place, :], 1, 0)
        value = value.astype(low)
        right[hidden + m] = value
        sum_ref[pl.ds(8 + m, 1), :] = jnp.sum(value.astype(full), axis=0, keepdims=True)
        accum[...] += dot_of(value, up[place, :], 1, 1)
        return 0

    lax.fori_loop(0, FF // D, backward, 0)
    unit, inverse = norm_stats(middle[...])
    second_grad = accum[...]
    sum_ref[0:1, :] = jnp.sum(second_grad * unit, axis=0, keepdims=True)
    sum_ref[1:2, :] = jnp.sum(second_grad, axis=0, keepdims=True)
    scaled = second_grad * gain
    mean_scaled = jnp.mean(scaled, axis=-1, keepdims=True)
    mean_unit = jnp.mean(scaled * unit, axis=-1, keepdims=True)
    total_grad = final[...] + inverse * (scaled - mean_scaled - unit * mean_unit)
    middle[...] = total_grad
    puts.append(send(middle, middle_hbm, 1))
    middle_low[...] = total_grad.astype(low)
    sum_ref[2:3, :] = jnp.sum(total_grad, axis=0, keepdims=True)
    attended_grad = dot_of(middle_low[...], proj[...], 1, 0).astype(low)
    grad[...] = attended_grad
    puts.append(send(grad, grad_hbm, 2))
    gets[2].wait()
    head = lax.broadcasted_iota(jnp.int32, (16, D), 0)
    lane = lax.broadcasted_iota(jnp.int32, (16, D), 1)
    member = jnp.where(lane // HEAD_DIM == head, 1.0, 0.0)
    leader = jnp.where(lane == head * HEAD_DIM, 1.0, 0.0)
    exact = functools.partial(
        lax.dot_general,
        dimension_numbers=(((1,), (1,)), ((), ())),
        precision=lax.Precision.HIGHEST,
        preferred_element_type=full,
    )
    deltas = exact(member, attended_grad.astype(full) * mixed[...])
    tops = exact(leader, logs[...])
    for pair in range(PAIRS):
        delta_ref[pair] = deltas[2 * pair : 2 * pair + 2]
        log_ref[pair] = tops[2 * pair : 2 * pair + 2]
    turned[0] = final_low[...].T
    turned[1] = second[...].T
    turned[2] = middle_low[...].T

    def weights(i, _):
        store_split(dot_of(turned[i // hidden], right[i], 1, 0), stage_keep, stage_send, i)

        @pl.when(i < hidden)
        def _():
            pltpu.make_async_copy(stage_keep.at[i], down_keep.at[i], keep_sems.at[i]).start()
            pltpu.make_async_copy(stage_send.at[i], down_send.at[i], send_sems.at[i]).start()

        @pl.when(i >= hidden)
        def _():
            row = i - hidden
            pltpu.make_async_copy(stage_keep.at[i], up_keep.at[row], keep_sems.at[i]).start()
            pltpu.make_async_copy(stage_send.at[i], up_send.at[row], send_sems.at[i]).start()

        return 0

    lax.fori_loop(0, 2 * hidden + 1, weights, 0)
    for copy in puts:
        copy.wait()
    for i in range(2 * hidden + 1):
        if i < hidden:
            keep, gone, row = down_keep, down_send, i
        else:
            keep, gone, row = up_keep, up_send, i - hidden
        pltpu.make_async_copy(stage_keep.at[i], keep.at[row], keep_sems.at[i]).wait()
        pltpu.make_async_copy(stage_send.at[i], gone.at[row], send_sems.at[i]).wait()


def middle_call(limit, vectors, tokens, mixed, logs, cot, teach, arrays, plan, block, dp):
    rows = tokens.shape[0]
    hidden = FF // D
    narrow = jax.ShapeDtypeStruct((rows, D), low)
    wide = jax.ShapeDtypeStruct((rows, D), full)
    shape = (dp // 2, D // dp, D)
    parts = [jax.ShapeDtypeStruct((count,) + shape, low) for count in (hidden, hidden + 1)]
    stats = jax.ShapeDtypeStruct((PAIRS, 2, rows), full)
    anywhere = pl.BlockSpec(memory_space=pl.ANY)
    inside = pl.BlockSpec(memory_space=pltpu.VMEM)
    moves = sum(len(part) for part in plan)
    return pl.pallas_call(
        functools.partial(middle_kernel, plan, block, len(arrays)),
        out_shape=(
            narrow,
            wide,
            narrow,
            parts[0],
            parts[0],
            parts[1],
            parts[1],
            stats,
            stats,
            jax.ShapeDtypeStruct((8 + 8, D), full),
        ),
        in_specs=[pl.BlockSpec(memory_space=pltpu.SMEM), inside]
        + [anywhere] * (5 + len(arrays)),
        out_specs=[anywhere] * 7 + [inside] * 3,
        scratch_shapes=[
            pltpu.VMEM((rows, D), low),
            pltpu.VMEM((rows, D), full),
            pltpu.VMEM((rows, D), full),
            pltpu.VMEM((rows, D), low),
            pltpu.VMEM((rows, D), low),
            pltpu.VMEM((FF, D), low),
            pltpu.VMEM((FF, D), low),
            pltpu.VMEM((D, D), low),
            pltpu.VMEM((2 * hidden + 1, rows, D), low),
            pltpu.VMEM((hidden, rows, D), full),
            pltpu.VMEM((rows, D), low),
            pltpu.VMEM((rows, D), full),
            pltpu.VMEM((rows, D), full),
            pltpu.VMEM((rows, D), low),
            pltpu.VMEM((rows, D), low),
            pltpu.VMEM((rows, D), low),
            pltpu.VMEM((rows, D), low),
            pltpu.VMEM((rows, D), full),
            pltpu.VMEM((3, D, rows), low),
            pltpu.VMEM((2 * hidden + 1,) + shape, low),
            pltpu.VMEM((2 * hidden + 1,) + shape, low),
            pltpu.SemaphoreType.DMA((5,)),
            pltpu.SemaphoreType.DMA((moves,)),
            pltpu.SemaphoreType.DMA((3,)),
            pltpu.SemaphoreType.DMA((2 * hidden + 1,)),
            pltpu.SemaphoreType.DMA((2 * hidden + 1,)),
        ],
        compiler_params=pltpu.CompilerParams(vmem_limit_bytes=VMEM_LIMIT),
        cost_estimate=SMALL_COST,
        name="middle",
    )(limit, vectors, tokens, mixed, logs, cot, teach, *arrays)


def fold_block(keep, got, out_keep, out_send, bit, place):
    step = 1 << place
    mine = (lax.axis_index("dp") // bit) % 2 * step
    for j in range(keep.shape[1] // 2):
        base = (j // step) * 2 * step + j % step
        for out, shift in ((out_keep, mine), (out_send, step - mine)):
            value = keep[0, base + shift].astype(full) + got[0, base + shift].astype(full)
            out[0, j] = value.astype(low)


def fold_kernel(bits, places, *refs):
    count = len(bits)
    for n in range(count):
        fold_block(
            *refs[2 * n : 2 * n + 2],
            *refs[2 * count + 2 * n : 2 * count + 2 * n + 2],
            bits[n],
            places[n],
        )


def fold(pairs, bits, places):
    lead = pairs[0][0].shape[0]
    block = lambda shape: pl.BlockSpec((1,) + shape[1:], lambda i: (i, 0, 0, 0))
    halves = [
        (keep.shape[0], keep.shape[1] // 2) + keep.shape[2:] for keep, _ in pairs for _ in range(2)
    ]
    outs = pl.pallas_call(
        functools.partial(fold_kernel, bits, places),
        out_shape=[jax.ShapeDtypeStruct(shape, low) for shape in halves],
        grid=(lead,),
        in_specs=[block(value.shape) for pair in pairs for value in pair],
        out_specs=[block(shape) for shape in halves],
        compiler_params=pltpu.CompilerParams(vmem_limit_bytes=VMEM_LIMIT),
        cost_estimate=pl.CostEstimate(flops=0, bytes_accessed=16 << 20, transcendentals=0),
        name="fold",
    )(*[value for pair in pairs for value in pair])
    return [(outs[2 * n], outs[2 * n + 1]) for n in range(len(pairs))]


def qkv_grad_kernel(count, *refs):
    sources = refs[: 3 * count + 1]
    outs = refs[3 * count + 1 : 3 * count + 5]
    sum_ref, held, turned, total, stage, in_sems, out_sems = refs[3 * count + 5 :]
    first_use = [0, count] + list(range(1, count)) + list(range(count + 1, 3 * count + 1))
    for n in first_use:
        pltpu.make_async_copy(sources[n], held.at[n], in_sems.at[n]).start()

    def wait(n):
        pltpu.make_async_copy(sources[0], held.at[n], in_sems.at[n]).wait()

    def turn(n, _):
        wait(n)
        turned[n] = held[n].T
        return 0

    lax.fori_loop(0, count, turn, 0)
    sum_ref[...] = jnp.zeros_like(sum_ref)

    def step(i, _):
        c = (i + count - 1) // count
        n = jnp.where(i == 0, 0, (i + count - 1) % count)
        wait(count + i)
        right = held[count + i]
        value = dot_of(turned[n], right, 1, 0)
        total[...] = value + jnp.where(n == 0, jnp.zeros_like(value), total[...])

        @pl.when(c != 1)
        def _():
            row = pl.ds(pl.multiple_of(c * 4, 8), 1)
            sum_ref[row, :] += jnp.sum(right.astype(full), axis=0, keepdims=True)

        @pl.when(i % count == 0)
        def _():
            for part in range(2):
                store_split(
                    total[:, part * D // 2 : (part + 1) * D // 2],
                    stage.at[part],
                    stage.at[2 + part],
                    c,
                )
            for k in range(4):
                pltpu.make_async_copy(
                    stage.at[k, c], outs[k].at[c], out_sems.at[k * 3 + c]
                ).start()

        return 0

    lax.fori_loop(0, 2 * count + 1, step, 0)
    for k in range(4):
        for c in range(3):
            pltpu.make_async_copy(stage.at[k, c], outs[k].at[c], out_sems.at[k * 3 + c]).wait()


def qkv_grads(chunks, query_grad, key_grads, value_grads, dp):
    rows = query_grad.shape[0]
    count = len(chunks)
    shape = (3, dp // 2, D // dp, D // 2)
    anywhere = pl.BlockSpec(memory_space=pl.ANY)
    return pl.pallas_call(
        functools.partial(qkv_grad_kernel, count),
        out_shape=[jax.ShapeDtypeStruct(shape, low)] * 4
        + [jax.ShapeDtypeStruct((16, D), full)],
        in_specs=[anywhere] * (3 * count + 1),
        out_specs=[anywhere] * 4 + [pl.BlockSpec(memory_space=pltpu.VMEM)],
        scratch_shapes=[
            pltpu.VMEM((3 * count + 1, rows, D), low),
            pltpu.VMEM((count, D, rows), low),
            pltpu.VMEM((D, D), full),
            pltpu.VMEM((4,) + shape, low),
            pltpu.SemaphoreType.DMA((3 * count + 1,)),
            pltpu.SemaphoreType.DMA((12,)),
        ],
        compiler_params=pltpu.CompilerParams(vmem_limit_bytes=VMEM_LIMIT),
        cost_estimate=SMALL_COST,
        name="qkv_grads",
    )(*chunks, query_grad, *key_grads, *value_grads)


def last_kernel(
    token_ref,
    first_ref,
    right_ref,
    left_ref,
    middle_ref,
    vector_ref,
    gain_ref,
    bias_ref,
    sum_ref,
    out_ref,
    pack_ref,
):
    @pl.when(pl.program_id(0) == 0)
    def _():
        pack_ref[...] = jnp.zeros_like(pack_ref)
        pack_ref[1:2, :] = sum_ref[0:1, :]
        pack_ref[3:4, :] = sum_ref[1:2, :]
        pack_ref[4:5, :] = bias_ref[0:1, :]
        pack_ref[5:6, :] = bias_ref[8:9, :]
        pack_ref[6:8, :] = sum_ref[2:4, :]
        pack_ref[8 : 8 + FF // D, :] = sum_ref[8 : 8 + FF // D, :]

    unit, inverse = norm_stats(token_ref[...].astype(full) + vector_ref[0:1, :])
    grad = first_ref[...] + right_ref[...].astype(full) + left_ref[...].astype(full)
    scaled = grad * gain_ref[0:1, :]
    mean_scaled = jnp.mean(scaled, axis=-1, keepdims=True)
    mean_unit = jnp.mean(scaled * unit, axis=-1, keepdims=True)
    result = middle_ref[...] + inverse * (scaled - mean_scaled - unit * mean_unit)
    out_ref[...] = result
    pack_ref[0:1, :] += jnp.sum(grad * unit, axis=0, keepdims=True)
    pack_ref[2:3, :] += jnp.sum(grad, axis=0, keepdims=True)
    pack_ref[pl.ds(16 + lax.axis_index("dp"), 1), :] += jnp.sum(result, axis=0, keepdims=True)


def last_norm(tokens, first, right, left, middle_grad, vectors, gains, bias_sums, sums, dp):
    rows = tokens.shape[0]
    part = pl.BlockSpec((rows // 4, D), lambda i: (i, 0))
    whole = lambda value: pl.BlockSpec(value.shape, lambda i: (0, 0))
    small = (vectors, gains, bias_sums, sums)
    return pl.pallas_call(
        last_kernel,
        out_shape=(
            jax.ShapeDtypeStruct((rows, D), full),
            jax.ShapeDtypeStruct((16 + dp, D), full),
        ),
        grid=(4,),
        in_specs=[part] * 5 + [whole(value) for value in small],
        out_specs=[part, pl.BlockSpec((16 + dp, D), lambda i: (0, 0))],
        compiler_params=pltpu.CompilerParams(vmem_limit_bytes=VMEM_LIMIT),
        cost_estimate=SMALL_COST,
        name="last_norm",
    )(tokens, first, right, left, middle_grad, *small)


def two_parts(value, axis, mine):
    keep = lax.dynamic_index_in_dim(value, mine, axis, keepdims=False)
    send = lax.dynamic_index_in_dim(value, 1 - mine, axis, keepdims=False)
    return keep, send.astype(low)


class Scatter:
    def __init__(self, parts, turns):
        self.bits = outer_bits()
        half = len(self.bits) // 2
        self.orders = [
            [1] + self.bits[half * (turn % 2) :] + self.bits[: half * (turn % 2)] for turn in turns
        ]
        self.left = [list(self.bits) for _ in turns]
        self.step = 0
        self.parts = parts

    def sends(self):
        return [send for _, send in self.parts]

    def exchange(self, sends):
        self.pairs = [
            (keep, swap(send, "dp", turn[self.step]))
            for (keep, _), send, turn in zip(self.parts, sends, self.orders)
        ]
        self.step += 1

    def folds(self):
        if self.step > len(self.bits):
            return [], [], []
        bits = [turn[self.step] for turn in self.orders]
        places = []
        for left, bit in zip(self.left, bits):
            places.append(left.index(bit))
            left.remove(bit)
        return self.pairs, bits, places

    def give(self, outs):
        self.parts = [(outs[n], outs[n + 1]) for n in range(0, len(outs), 2)]

    def fold(self):
        outs = []
        for pair, bit, at in zip(*self.folds()):
            outs += fold([pair], [bit], [at])[0]
        self.give(outs)

    def advance(self, order):
        sends = order(*self.sends())
        self.exchange(list(sends) if len(self.parts) > 1 else [sends])

    def finish(self, order):
        while self.step <= len(self.bits):
            self.fold()
            self.advance(order)
        got = order(*[other for _, other in self.pairs])
        return [
            (keep.astype(full) + other.astype(full))[:, 0]
            for (keep, _), other in zip(self.pairs, got)
        ]


def scatter_dp(parts, turns):
    scatter = Scatter(parts, turns)
    while True:
        sends = yield scatter.sends()
        scatter.exchange(sends)
        if scatter.step > len(scatter.bits):
            break
        scatter.parts = fold(*scatter.folds())
    got = yield [other for _, other in scatter.pairs]
    return [
        (keep.astype(full) + other.astype(full))[:, 0]
        for (keep, _), other in zip(scatter.pairs, got)
    ]


def scatter_mp(value):
    rank = lax.axis_index("mp")
    part = lambda index: lax.dynamic_index_in_dim(value, index, keepdims=False)
    sends = yield [part(rank ^ bit).astype(low) for bit in (1, 2, 3)]
    got = yield [swap(send, "mp", bit) for bit, send in zip((1, 2, 3), sends)]
    got = [other.astype(full) for other in got]
    return (part(rank) + got[0]) + (got[1] + got[2])


def scatter_feed(up_own, down_own):
    mp = lax.axis_size("mp")
    block = down_own.shape[1]
    out_own = up_own[mp].reshape(block, mp, -1).transpose(1, 0, 2)
    own = yield from scatter_mp(
        jnp.concatenate([up_own[:mp], down_own, out_own.reshape(mp, -1, D)], axis=1)
    )
    return own[:block], own[block : 2 * block].T, own[2 * block :].reshape(block, -1).T


def scatter_qkv(keep_left, keep_right, send_left, send_right):
    left_part, right_part = yield from scatter_dp(
        [(keep_left, send_left), (keep_right, send_right)], (0, 1)
    )
    width = D // lax.axis_size("mp")
    parts = [part[..., at : at + width] for part in (left_part, right_part) for at in (0, width)]
    return (yield from scatter_mp(jnp.stack(parts)))


def sum_small(value):
    (value,) = yield [value]
    value = value + swap(value, "dp", 1)
    bits = outer_bits()
    groups = [("dp", bits[n : n + 2]) for n in range(0, len(bits), 2)] + [("mp", [1, 2])]
    for axis, pair in groups:
        (value,) = yield [value]
        if len(pair) == 1:
            value = value + swap(value, axis, pair[0])
        else:
            one, two = pair
            got = [swap(value, axis, mask) for mask in (one, two, one + two)]
            if axis == "mp":
                got = yield got
            value = (value + got[0]) + (got[1] + got[2])
    return value


class Steps:
    def __init__(self, steps):
        self.steps = steps
        self.pending = next(steps)
        self.result = None

    def advance(self, order):
        if self.pending is None:
            return
        sends = order(*self.pending)
        sends = [sends] if len(self.pending) == 1 else list(sends)
        try:
            self.pending = self.steps.send(sends)
        except StopIteration as stop:
            self.pending = None
            self.result = stop.value

    def finish(self, order):
        while self.pending is not None:
            self.advance(order)
        return self.result


def shards(
    tokens_in,
    timesteps,
    lengths,
    time_table,
    norm_gains,
    norm_biases,
    w_qkv,
    qv_bias,
    w_out,
    out_bias,
    w_up,
    up_bias,
    w_down,
    down_bias,
    cotangent,
    teacher,
):
    rank = lax.axis_index("mp")
    data_rank = lax.axis_index("dp")
    mp = lax.axis_size("mp")
    dp = lax.axis_size("dp")
    own_rows = tokens_in.shape[0]
    length = lax.dynamic_index_in_dim(lengths, data_rank, keepdims=False)
    own_time = lax.dynamic_index_in_dim(timesteps, data_rank, keepdims=False)
    odd = rank % 2 == 1
    upper = rank >= 2
    middle = jnp.logical_or(rank == 1, rank == 2)
    order = Order()
    along = lambda value, pairs: lax.ppermute(value, "mp", pairs)

    block = w_qkv.shape[1]
    aligned = block % 32 == 0
    narrow = order(jnp.concatenate([w_qkv.reshape(3 * block, -1), w_out.T]))
    first_swap = swap(narrow, "mp", 1)
    tall = order(jnp.concatenate([w_up, w_down.T]))
    tall_swap = swap(tall, "mp", 1)
    pair = order(
        jnp.concatenate(
            [jnp.where(odd, first_swap, narrow), jnp.where(odd, narrow, first_swap)], axis=1
        )
    )
    second_swap = swap(pair, "mp", 2)
    tokens, lengths, own_time, norm_gains, norm_biases, out_bias, down_bias, up_bias, length = order(
        tokens_in, lengths, own_time, norm_gains, norm_biases, out_bias, down_bias, up_bias, length
    )
    table_row = lax.dynamic_slice_in_dim(time_table, own_time, 1).astype(full)
    unit_one, _ = norm_stats(tokens.astype(full) + table_row)
    first_norm = (unit_one * norm_gains[0] + norm_biases[0]).astype(low)
    loss_weight = lengths.shape[0] * MAXLEN / jnp.sum(lengths).astype(full)
    vectors = jnp.concatenate(
        [
            table_row,
            out_bias[None],
            norm_gains[1:2],
            norm_biases[1:2],
            down_bias[None],
            jnp.full((3, D), loss_weight),
            up_bias.reshape(-1, D),
            jnp.zeros((4, D), full),
        ]
    )
    scalars = jnp.stack(
        [
            rank,
            jnp.where(rank == 0, 1, rank - 1),
            jnp.where(upper, rank - 2, rank + 2),
            jnp.where(middle, rank + 1, 3 - rank),
            length,
            length - rank * own_rows,
        ]
    ).astype(jnp.int32)
    first_norm, vectors, scalars = order(first_norm, vectors, scalars)
    wide = jnp.concatenate(
        [jnp.where(upper, second_swap, pair), jnp.where(upper, pair, second_swap)], axis=1
    )
    qkv_rows, out_rows = wide[: 3 * block], wide[3 * block :]
    if aligned:
        split = 3 * block // 2
        qkv_gather = Gather([qkv_rows[:split], qkv_rows[split:]])
        qkv_gather.advance(order)
    tall = order(jnp.concatenate([tall, tall_swap]))
    tall_across = along(tall, [(1, 2), (2, 1)])

    if aligned:
        while qkv_gather.step < len(qkv_gather.bits):
            qkv_gather.advance(order)
    tall_across = order(tall_across)
    tall_other = jnp.where(middle, tall_across, along(tall_across, [(1, 0), (2, 3)]))
    sent = order(first_norm)
    from_left = along(sent, [(0, 1), (1, 2), (2, 3)])
    from_right = along(sent, [(1, 0), (2, 1), (3, 2)])
    if aligned:
        feed_gather = Gather(
            [
                jnp.concatenate([tall, out_rows[: block // 2]]),
                jnp.concatenate([tall_other, out_rows[block // 2 :]]),
            ]
        )
        qkv_gather.advance(order)
        arrays, plan = plan_of(
            qkv_gather.result,
            [
                [(0, block, 0, 0, 0, 0), (block, split - block, 1, 0, 0, 0)],
                [
                    (0, 2 * block - split, 1, 0, 0, split - block),
                    (2 * block - split, block, 1, 1, 0, 0),
                ],
            ],
        )
        query_weight, pair_weight = order(*place(arrays, plan, block, [(D, D), (D, 2 * D)]))
        feed_gather.advance(order)
    else:
        weights = lax.all_gather(qkv_rows.reshape(3, block, D), "dp", axis=1, tiled=True)
        query_weight = weights[0]
        pair_weight = jnp.concatenate([weights[1], weights[2]], axis=1)
    hop_right, hop_left = order(from_left, from_right)
    second_right = along(hop_right, [(1, 2), (2, 3)])
    second_left = along(hop_left, [(1, 0), (2, 1)])
    near = jnp.where(rank == 0, hop_left, hop_right)
    if aligned:
        while feed_gather.step < len(feed_gather.bits):
            feed_gather.advance(order)
    attend = lambda chunks, numbers, carried: attend_forward(
        chunks,
        numbers,
        scalars,
        query_weight,
        pair_weight,
        qv_bias[0:1],
        qv_bias[1:2],
        carried,
    )
    key_own, key_near, value_own, value_near, queries, *state = order(
        *attend(order(first_norm, near), (0, 1), None)
    )
    second = order(jnp.where(upper, second_right, second_left))
    third = along(second, [(1, 0), (2, 3)])
    key_second, value_second, *state = attend([second], (2,), (queries, *state))
    key_second, value_second, *state = order(key_second, value_second, *state)
    last = order(jnp.where(middle, hop_left, third))
    if aligned:
        feed_gather.advance(order)
    key_last, value_last, mixed, logs = order(*attend([order(last)], (3,), (queries, *state)))
    if aligned:
        layout = lambda masks, shift: [
            (0, block, 0, masks[0], D, 0),
            (block, block, 1, masks[0], D, 0),
            (2 * block, block, 0, masks[1], D, 0),
            (3 * block, block, 1, masks[1], D, 0),
            (4 * block, block // 2, 2, 0, 0, shift),
        ]
        arrays, plan = plan_of(
            feed_gather.result, [layout((0, 1), 0), layout((2, 3), block // 2)]
        )
    else:
        arrays = [
            lax.all_gather(w_up, ("mp", "dp"), axis=0, tiled=True),
            lax.all_gather(w_down.T, ("mp", "dp"), axis=0, tiled=True),
            lax.all_gather(out_rows, "dp", axis=0, tiled=True),
        ]
        plan = [[(0, array.shape[0], n, None, 0, 0, 0)] for n, array in enumerate(arrays)]
    chunks = [first_norm, near, second, last]
    keys = [key_own, key_near, key_second, key_last]
    values = [value_own, value_near, value_second, value_last]

    output, middle_grad, attended_grad, *parts, deltas, log_rows, sums = middle_call(
        scalars, vectors, tokens, mixed, logs, cotangent, teacher, arrays, plan, block, dp
    )
    scatter = Scatter([(parts[0], parts[1]), (parts[2], parts[3])], (1, 0))
    scatter.advance(order)

    key_grads = [None] * 4
    value_grads = [None] * 4
    firsts = [None] * 4
    query_grad = None
    for n in (3, 2, 1, 0):
        pairs, bits, places = scatter.folds() if n % 2 == 0 else ([], [], [])
        query_grad, key_grads[n], value_grads[n], firsts[n], *folded = attend_backward(
            n,
            queries,
            keys[n],
            values[n],
            order(attended_grad),
            log_rows,
            deltas,
            query_weight,
            pair_weight,
            scalars,
            query_grad,
            n == 0,
            pairs,
            bits,
            places,
        )
        firsts[n] = order(firsts[n])
        if folded:
            scatter.give(folded)
        if n == 3:
            back_last = along(firsts[3], [(0, 1), (3, 2)]).astype(full)
        elif n == 2:
            scatter.advance(order)
            payload = order((firsts[2] + back_last).astype(low))
            back_right = along(payload, [(0, 1), (1, 2)]).astype(full)
            back_left = along(payload, [(3, 2), (2, 1)]).astype(full)
        elif n == 1:
            to_right = jnp.where(
                rank == 0, firsts[1], firsts[3].astype(full) + back_right
            ).astype(low)
            to_left = (firsts[1] + back_left).astype(low)
            to_right, to_left = order(to_right, to_left)
            final_right = along(to_right, [(0, 1), (1, 2), (2, 3)])
            final_left = along(to_left, [(3, 2), (2, 1), (1, 0)])
    scatter.advance(order)
    query_grad, final_right, final_left = order(query_grad, final_right, final_left)
    *halves, bias_sums = qkv_grads(chunks, query_grad, key_grads, value_grads, dp)
    qkv = Steps(scatter_qkv(*halves))
    qkv.advance(order)
    down_own, up_own = scatter.finish(order)
    feed = Steps(scatter_feed(up_own, down_own))
    feed.advance(order)
    tokens, first_own = order(tokens, firsts[0])
    input_grad, packed = last_norm(
        tokens,
        first_own,
        final_right,
        final_left,
        middle_grad,
        vectors,
        norm_gains,
        bias_sums,
        sums,
        dp,
    )
    packed, input_grad = order(packed, input_grad)
    small = Steps(sum_small(packed))
    qkv.advance(order)
    small.advance(order)
    small.advance(order)
    feed.advance(order)
    qkv.advance(order)
    small.advance(order)
    qkv.advance(order)
    qkv.advance(order)
    total = small.finish(order)
    qkv_grad = qkv.finish(order)
    up_grad, down_grad, out_grad = feed.finish(order)
    fixed = 16
    chosen = (timesteps[None, :] == jnp.arange(time_table.shape[0])[:, None]).astype(full)
    table_grad = lax.dot_general(
        chosen,
        total[fixed:],
        (((1,), (0,)), ((), ())),
        precision=lax.Precision.HIGHEST,
        preferred_element_type=full,
    )
    return (
        output,
        input_grad,
        table_grad,
        total[0:2],
        total[2:4],
        qkv_grad,
        total[4:6],
        out_grad,
        total[6],
        up_grad,
        total[8 : 8 + FF // D].reshape(FF),
        down_grad,
        total[7],
    )


def solution(mesh):
    rows = P(both, None)
    placed = (
        rows,
        P(),
        P(),
        P(),
        P(),
        P(),
        P(None, "dp", "mp"),
        P(),
        P("mp", "dp"),
        P(),
        P("dp", "mp"),
        P(),
        P("mp", "dp"),
        P(),
        rows,
        rows,
    )
    return jax.shard_map(
        shards,
        mesh=mesh,
        in_specs=placed,
        out_specs=(
            rows,
            rows,
            P(),
            P(),
            P(),
            P(None, "dp", "mp"),
            P(),
            P("mp", "dp"),
            P(),
            P("dp", "mp"),
            P(),
            P("mp", "dp"),
            P(),
        ),
        check_vma=False,
    )
```

```python
import functools

import jax
import jax.numpy as jnp
from jax import lax
from jax.experimental import pallas as pl
from jax.experimental.pallas import tpu as pltpu
from jax.sharding import PartitionSpec as P

D = 768
HEADS = 12
HEAD_DIM = 64
FF = 3072
MAXLEN = 2048
PAIR = 2 * HEAD_DIM
PAIRS = HEADS // 2
VMEM_LIMIT = 58 << 20
SMALL_COST = pl.CostEstimate(flops=1 << 20, bytes_accessed=1 << 16, transcendentals=0)

far_below = -1e30
epsilon = 1e-05
score_scale = HEAD_DIM ** (-0.5)
low = jnp.bfloat16
full = jnp.float32
both = ("dp", "mp")


def norm_stats(values):
    center = values - jnp.mean(values, axis=-1, keepdims=True)
    spread = jnp.mean(center * center, axis=-1, keepdims=True)
    inverse = lax.rsqrt(spread + epsilon)
    return center * inverse, inverse


def dot_of(left_side, right_side, left_dim, right_dim):
    return lax.dot_general(
        left_side,
        right_side,
        (((left_dim,), (right_dim,)), ((), ())),
        preferred_element_type=full,
    )


def first_half(shape):
    return lax.broadcasted_iota(jnp.int32, shape, len(shape) - 1) < HEAD_DIM


def forward_kernel(numbers, first, final, scalars, *refs):
    count = len(numbers)
    chunk_refs = refs[:count]
    wk_ref, wv_ref, value_bias_ref = refs[count : count + 3]
    refs = refs[count + 3 :]
    if first:
        wq_ref, query_bias_ref = refs[:2]
        key_outs, value_outs = refs[2 : 2 + count], refs[2 + count : 2 + 2 * count]
        query_out, top_ref, sum_ref, acc_ref = refs[2 + 2 * count :]
        q_pair = (dot_of(chunk_refs[0][...], wq_ref[...], 1, 0) + query_bias_ref[...]).astype(low)
        q_pair = q_pair * jnp.asarray(score_scale, low)
        query_out[...] = q_pair
    else:
        q_ref, top_in, sum_in, acc_in = refs[:4]
        key_outs, value_outs = refs[4 : 4 + count], refs[4 + count : 4 + 2 * count]
        results = refs[4 + 2 * count :]
        q_pair = q_ref[...]
    weight = jnp.concatenate([wk_ref[...], wv_ref[...]], axis=1)
    keys = []
    values = []
    for n in range(count):
        both_parts = dot_of(chunk_refs[n][...], weight, 1, 0)
        keys.append(both_parts[:, :PAIR].astype(low))
        values.append((both_parts[:, PAIR:] + value_bias_ref[...]).astype(low))
        key_outs[n][...] = keys[n]
        value_outs[n][...] = values[n]
    rows = q_pair.shape[0]
    size = keys[0].shape[0]
    place = lax.broadcasted_iota(jnp.int32, (1, size), 1)
    lower = first_half((rows, PAIR))
    parts = []
    for half in range(2):
        kept = lower if half == 0 else jnp.logical_not(lower)
        q_half = jnp.where(kept, q_pair, jnp.zeros_like(q_pair))
        scores = []
        for n in range(count):
            bias = jnp.where(place + scalars[numbers[n]] * size < scalars[4], 0.0, far_below)
            scores.append(dot_of(q_half, keys[n], 1, 1) + bias)
        highest = functools.reduce(
            jnp.maximum, [jnp.max(score, axis=-1, keepdims=True) for score in scores]
        )
        totals = jnp.zeros_like(highest)
        mixed = jnp.zeros((rows, PAIR), full)
        for n in range(count):
            exp_scores = jnp.exp(scores[n] - highest)
            totals = totals + jnp.sum(exp_scores, axis=-1, keepdims=True)
            mixed = mixed + dot_of(exp_scores.astype(low), values[n], 1, 0)
        parts.append((highest, totals, mixed))
    top = jnp.where(lower, parts[0][0], parts[1][0])
    total = jnp.where(lower, parts[0][1], parts[1][1])
    mixed = jnp.where(lower, parts[0][2], parts[1][2])
    if first:
        top_ref[...] = top
        sum_ref[...] = total
        acc_ref[...] = mixed
    else:
        highest = jnp.maximum(top, top_in[...])
        here = jnp.exp(top - highest)
        before = jnp.exp(top_in[...] - highest)
        total = total * here + sum_in[...] * before
        mixed = mixed * here + acc_in[...] * before
        if final:
            results[0][...] = mixed / total
            results[1][...] = highest + jnp.log(total)
        else:
            results[0][...] = highest
            results[1][...] = total
            results[2][...] = mixed


def attend_forward(chunks, numbers, scalars, query_weight, pair_weight, query_bias, value_bias, carried):
    rows = chunks[0].shape[0]
    count = len(chunks)
    first = carried is None
    final = 3 in numbers
    column = lambda height, c: pl.BlockSpec((height, PAIR), lambda i, n: (0, c * PAIRS + i))
    whole = pl.BlockSpec((rows, D), lambda i, n: (0, 0))
    wide = jax.ShapeDtypeStruct((rows, D), full)
    narrow = jax.ShapeDtypeStruct((rows, D), low)
    extra = (query_weight, query_bias) if first else carried
    results = (narrow,) * first + (wide,) * (2 if final else 3)
    return pl.pallas_call(
        functools.partial(forward_kernel, numbers, first, final),
        out_shape=(narrow,) * (2 * count) + results,
        grid_spec=pltpu.PrefetchScalarGridSpec(
            num_scalar_prefetch=1,
            grid=(PAIRS,),
            in_specs=[whole] * count
            + [column(D, 0), column(D, 1), column(1, 0)]
            + ([column(D, 0), column(1, 0)] if first else [column(rows, 0)] * 4),
            out_specs=[column(rows, 0)] * (2 * count + len(results)),
        ),
        compiler_params=pltpu.CompilerParams(vmem_limit_bytes=VMEM_LIMIT),
        cost_estimate=SMALL_COST,
        name="attend_forward",
    )(scalars, *chunks, pair_weight, pair_weight, value_bias, *extra)


def backward_kernel(
    number,
    first,
    last,
    folds,
    scalars,
    q_ref,
    k_ref,
    v_ref,
    g_ref,
    log_ref,
    delta_ref,
    wk_ref,
    wv_ref,
    *refs
):
    if last:
        wq_ref = refs[0]
        refs = refs[1:]
    if not first:
        dq_in = refs[0]
        refs = refs[1:]
    count = len(folds)
    fold_ins, refs = refs[: 2 * count], refs[2 * count :]
    dq_ref, dk_ref, dv_ref, back_ref = refs[:4]
    fold_outs, accum = refs[4:-1], refs[-1]
    step = pl.program_id(0)
    for n, (lead, bit, at) in enumerate(folds):

        @pl.when(step < lead)
        def _():
            fold_block(
                *fold_ins[2 * n : 2 * n + 2], *fold_outs[2 * n : 2 * n + 2], bit, at
            )

    rows = q_ref.shape[0]
    keys = k_ref.shape[0]
    limit = scalars[4] - scalars[number] * keys
    q_pair = q_ref[...]
    g_pair = g_ref[...]
    k_pair = k_ref[...]
    v_pair = v_ref[...]
    lower = first_half((rows, PAIR))
    nothing = jnp.zeros((rows, PAIR), low)
    two_halves = lambda pair: jnp.concatenate(
        [jnp.where(lower, pair, nothing), jnp.where(lower, nothing, pair)]
    )
    queries = two_halves(q_pair)
    grads_out = two_halves(g_pair)
    row_of = lambda ref: jnp.concatenate([ref[0, 0:1, :], ref[0, 1:2, :]], axis=1)
    place = lax.broadcasted_iota(jnp.int32, (keys, 1), 0)
    bias = jnp.where(place < limit, 0.0, far_below)
    scores = dot_of(k_pair, queries, 1, 1) + bias
    prob_grad = dot_of(v_pair, grads_out, 1, 1)
    probs = jnp.exp(scores - row_of(log_ref))
    score_grad = (probs * (prob_grad - row_of(delta_ref))).astype(low)
    dv_low = dot_of(probs.astype(low), grads_out, 1, 0).astype(low)
    dk_low = dot_of(score_grad, queries, 1, 0).astype(low)
    turned = dot_of(k_pair.T, score_grad, 1, 0)
    upper_rows = lax.broadcasted_iota(jnp.int32, (PAIR, rows), 0) < HEAD_DIM
    dk_ref[...] = dk_low
    dv_ref[...] = dv_low
    grads = [dk_low, dv_low]
    weights = [wk_ref[...], wv_ref[...]]
    dq_all = jnp.where(upper_rows, turned[:, :rows], turned[:, rows:]).T
    if not first:
        dq_all = dq_all + dq_in[...]
    back = dot_of(jnp.concatenate(grads, axis=1), jnp.concatenate(weights, axis=1), 1, 1)
    if last:
        dq_low = (dq_all * score_scale).astype(low)
        dq_ref[...] = dq_low
        back = back + dot_of(dq_low, wq_ref[...], 1, 1)
    else:
        dq_ref[...] = dq_all

    @pl.when(step == 0)
    def _():
        accum[...] = back

    @pl.when(step > 0)
    def _():
        accum[...] += back

    @pl.when(step == PAIRS - 1)
    def _():
        back_ref[...] = accum[...].astype(back_ref.dtype)


def attend_backward(
    number,
    queries,
    keys,
    values,
    grads,
    logs,
    deltas,
    query_weight,
    pair_weight,
    scalars,
    carried,
    last,
    pairs,
    bits,
    places,
):
    rows, total = queries.shape[0], keys.shape[0]
    first = carried is None
    folds = [(keep.shape[0], bit, at) for (keep, _), bit, at in zip(pairs, bits, places)]
    halves = [
        (keep.shape[0], keep.shape[1] // 2) + keep.shape[2:] for keep, _ in pairs for _ in range(2)
    ]

    def by_lead(shape):
        end = shape[0] - 1
        return pl.BlockSpec((1,) + shape[1:], lambda i, n: (jnp.minimum(i, end), 0, 0, 0))

    column = lambda count, c: pl.BlockSpec((count, PAIR), lambda i, n: (0, c * PAIRS + i))
    stats = pl.BlockSpec((1, 2, rows), lambda i, n: (i, 0, 0))
    extra = (query_weight,) * last + (() if first else (carried,))
    extra_specs = [column(D, 0)] * last + ([] if first else [column(rows, 0)])
    return pl.pallas_call(
        functools.partial(backward_kernel, number, first, last, folds),
        out_shape=(
            jax.ShapeDtypeStruct((rows, D), low if last else full),
            jax.ShapeDtypeStruct((total, D), low),
            jax.ShapeDtypeStruct((total, D), low),
            jax.ShapeDtypeStruct((total, D), low if first else full),
            *[jax.ShapeDtypeStruct(shape, low) for shape in halves],
        ),
        grid_spec=pltpu.PrefetchScalarGridSpec(
            num_scalar_prefetch=1,
            grid=(PAIRS,),
            in_specs=[
                column(rows, 0),
                column(total, 0),
                column(total, 0),
                column(rows, 0),
                stats,
                stats,
                column(D, 0),
                column(D, 1),
            ]
            + extra_specs
            + [by_lead(value.shape) for pair in pairs for value in pair],
            out_specs=[
                column(rows, 0),
                column(total, 0),
                column(total, 0),
                pl.BlockSpec((total, D), lambda i, n: (0, 0)),
            ]
            + [by_lead(shape) for shape in halves],
            scratch_shapes=[pltpu.VMEM((total, D), full)],
        ),
        compiler_params=pltpu.CompilerParams(vmem_limit_bytes=VMEM_LIMIT),
        cost_estimate=SMALL_COST,
        name="attend_backward",
    )(
        scalars,
        queries,
        keys,
        values,
        grads,
        logs,
        deltas,
        pair_weight,
        pair_weight,
        *extra,
        *[value for pair in pairs for value in pair],
    )


def swap(value, axis, bit):
    count = lax.axis_size(axis)
    return lax.ppermute(value, axis, [(i, i ^ bit) for i in range(count)])


class Order:
    def __init__(self):
        self.marks = ()

    def __call__(self, *values):
        values = lax.optimization_barrier(values + self.marks)[: len(values)]
        self.marks = values
        return values[0] if len(values) == 1 else values


def outer_bits():
    bits = []
    bit = 2
    while bit < lax.axis_size("dp"):
        bits.append(bit)
        bit *= 2
    return bits


class Gather:
    def __init__(self, parts):
        self.bits = outer_bits()
        half = len(self.bits) // 2
        self.orders = [
            self.bits[half * (n % 2) :] + self.bits[: half * (n % 2)] for n in range(len(parts))
        ]
        self.result = [[([0], part)] for part in parts]
        self.step = 0

    def advance(self, order):
        held = self.result
        if self.step < len(self.bits):
            masks = [[m for mask, _ in pieces for m in mask] for pieces in held]
            blocks = [
                jnp.concatenate([array for _, array in pieces]) if self.step else pieces[0][1]
                for pieces in held
            ]
            blocks = order(*blocks)
            bits = [turn[self.step] for turn in self.orders]
            self.result = [
                [(mask, block), ([m ^ bit for m in mask], swap(block, "dp", bit))]
                for mask, block, bit in zip(masks, blocks, bits)
            ]
        else:
            arrays = order(*[array for pieces in held for _, array in pieces])
            arrays = iter(arrays)
            self.result = []
            for pieces in held:
                kept = [(masks, next(arrays)) for masks, _ in pieces]
                self.result.append(
                    kept + [([m ^ 1 for m in masks], swap(array, "dp", 1)) for masks, array in kept]
                )
        self.step += 1


def canonical_row(me, rank, block, mask, rank_mask, stride, offset):
    if mask is None:
        return offset
    row = (me ^ mask) * block + offset
    if stride:
        if rank_mask >= 2:
            rank_mask = rank_mask ^ ((rank + 1) // 2 % 2)
        row = row + (rank ^ rank_mask) * stride
    return pl.multiple_of(row, 16)


def place_kernel(plan, block, *refs):
    count = len(plan)
    ins = refs[:count]
    outs = refs[count:-1]
    sems = refs[-1]
    me = lax.axis_index("dp")
    rank = lax.axis_index("mp")
    copies = []
    for ref, moves in zip(ins, plan):
        for start, size, which, mask, column, _, offset in moves:
            row = canonical_row(me, rank, block, mask, 0, 0, offset)
            copy = pltpu.make_async_copy(
                ref.at[pl.ds(start, size), :],
                outs[which].at[pl.ds(row, size), pl.ds(column * D, D)],
                sems.at[len(copies)],
            )
            copy.start()
            copies.append(copy)
    for copy in copies:
        copy.wait()


def plan_of(gathered, layouts):
    arrays = []
    plan = []
    for pieces, layout in zip(gathered, layouts):
        rows = sum(size for _, size, *_ in layout)
        for masks, array in pieces:
            moves = []
            for j, mask in enumerate(masks):
                for start, size, which, rank_mask, stride, offset in layout:
                    moves.append((j * rows + start, size, which, mask, rank_mask, stride, offset))
            arrays.append(array)
            plan.append(moves)
    return arrays, plan


def place(arrays, plan, block, shapes):
    return pl.pallas_call(
        functools.partial(place_kernel, plan, block),
        out_shape=[jax.ShapeDtypeStruct(shape, low) for shape in shapes],
        in_specs=[pl.BlockSpec(memory_space=pl.ANY)] * len(arrays),
        out_specs=[pl.BlockSpec(memory_space=pltpu.VMEM)] * len(shapes),
        scratch_shapes=[pltpu.SemaphoreType.DMA((sum(len(moves) for moves in plan),))],
        compiler_params=pltpu.CompilerParams(vmem_limit_bytes=VMEM_LIMIT),
        cost_estimate=SMALL_COST,
        name="place",
    )(*arrays)


def store_split(value, keep, send, index):
    block = keep.shape[2]
    even = lax.axis_index("dp") % 2 == 0
    for outer in range(keep.shape[1]):
        first = value[2 * outer * block : (2 * outer + 1) * block]
        other = value[(2 * outer + 1) * block : (2 * outer + 2) * block]
        keep[index, outer] = jnp.where(even, first, other).astype(low)
        send[index, outer] = jnp.where(even, other, first).astype(low)


def middle_kernel(plan, block, total, *refs):
    limit_ref, vector_ref = refs[:2]
    token_hbm, mixed_hbm, log_hbm, cot_hbm, teach_hbm = refs[2:7]
    pieces = refs[7 : 7 + total]
    (
        out_hbm,
        middle_hbm,
        grad_hbm,
        down_keep,
        down_send,
        up_keep,
        up_send,
        delta_ref,
        log_ref,
        sum_ref,
    ) = refs[7 + total : 17 + total]
    (
        token,
        mixed,
        logs,
        cot,
        teach,
        up,
        down,
        proj,
        right,
        slope,
        second,
        middle,
        final,
        out,
        final_low,
        middle_low,
        grad,
        accum,
        turned,
        stage_keep,
        stage_send,
        in_sems,
        weight_sems,
        out_sems,
        keep_sems,
        send_sems,
    ) = refs[17 + total :]
    hidden = FF // D
    targets = (up, down, proj)
    rows = token.shape[0]
    me = lax.axis_index("dp")
    rank = lax.axis_index("mp")

    def fetch(ref, scratch, n):
        copy = pltpu.make_async_copy(ref, scratch, in_sems.at[n])
        copy.start()
        return copy

    def send(scratch, ref, n):
        copy = pltpu.make_async_copy(scratch, ref, out_sems.at[n])
        copy.start()
        return copy

    gets = [
        fetch(token_hbm, token, 0),
        fetch(mixed_hbm, mixed, 1),
        fetch(log_hbm, logs, 2),
        fetch(cot_hbm, cot, 3),
        fetch(teach_hbm, teach, 4),
    ]
    loads = {0: [], 1: [], 2: []}
    number = 0
    for want in (2, 0, 1):
        for ref, moves in zip(pieces, plan):
            for start, size, which, mask, rank_mask, stride, offset in moves:
                if which != want:
                    continue
                row = canonical_row(me, rank, block, mask, rank_mask, stride, offset)
                copy = pltpu.make_async_copy(
                    ref.at[pl.ds(start, size), :],
                    targets[which].at[pl.ds(row, size), :],
                    weight_sems.at[number],
                )
                copy.start()
                loads[which].append(copy)
                number += 1

    table_row = vector_ref[0:1, :]
    out_bias = vector_ref[1:2, :]
    gain = vector_ref[2:3, :]
    shift = vector_ref[3:4, :]
    down_bias = vector_ref[4:5, :]
    weight = vector_ref[5:6, :]
    gets[0].wait()
    gets[1].wait()
    right[2 * hidden] = mixed[...].astype(low)
    for copy in loads[2]:
        copy.wait()
    state = token[...].astype(full) + table_row + out_bias
    state = state + dot_of(right[2 * hidden], proj[...], 1, 1)
    middle[...] = state
    unit, _ = norm_stats(state)
    second[...] = (unit * gain + shift).astype(low)
    accum[...] = jnp.zeros((rows, D), full)
    for copy in loads[0]:
        copy.wait()
    for copy in loads[1]:
        copy.wait()

    def forward(m, _):
        place = pl.ds(pl.multiple_of(m * D, D), D)
        value = dot_of(second[...], up[place, :], 1, 0) + vector_ref[pl.ds(8 + m, 1), :]
        cumulative = 0.5 + 0.5 * lax.erf(value * (0.5**0.5))
        right[m] = (value * cumulative).astype(low)
        slope[m] = cumulative + value * jnp.exp(-0.5 * value * value) * 0.3989422804014327
        accum[...] += dot_of(right[m], down[place, :], 1, 1)
        return 0

    lax.fori_loop(0, FF // D, forward, 0)
    final_state = middle[...] + accum[...] + down_bias
    out[...] = final_state.astype(low)
    puts = [send(out, out_hbm, 0)]
    gets[3].wait()
    gets[4].wait()
    place = lax.broadcasted_iota(jnp.int32, (rows, 1), 0)
    grads = cot[...].astype(full) + weight * (final_state - teach[...].astype(full))
    grads = jnp.where(place < limit_ref[5], grads, 0.0)
    final[...] = grads
    final_low[...] = grads.astype(low)
    sum_ref[3:4, :] = jnp.sum(grads, axis=0, keepdims=True)
    accum[...] = jnp.zeros((rows, D), full)

    def backward(m, _):
        place = pl.ds(pl.multiple_of(m * D, D), D)
        value = slope[m] * dot_of(final_low[...], down[place, :], 1, 0)
        value = value.astype(low)
        right[hidden + m] = value
        sum_ref[pl.ds(8 + m, 1), :] = jnp.sum(value.astype(full), axis=0, keepdims=True)
        accum[...] += dot_of(value, up[place, :], 1, 1)
        return 0

    lax.fori_loop(0, FF // D, backward, 0)
    unit, inverse = norm_stats(middle[...])
    second_grad = accum[...]
    sum_ref[0:1, :] = jnp.sum(second_grad * unit, axis=0, keepdims=True)
    sum_ref[1:2, :] = jnp.sum(second_grad, axis=0, keepdims=True)
    scaled = second_grad * gain
    mean_scaled = jnp.mean(scaled, axis=-1, keepdims=True)
    mean_unit = jnp.mean(scaled * unit, axis=-1, keepdims=True)
    total_grad = final[...] + inverse * (scaled - mean_scaled - unit * mean_unit)
    middle[...] = total_grad
    puts.append(send(middle, middle_hbm, 1))
    middle_low[...] = total_grad.astype(low)
    sum_ref[2:3, :] = jnp.sum(total_grad, axis=0, keepdims=True)
    attended_grad = dot_of(middle_low[...], proj[...], 1, 0).astype(low)
    grad[...] = attended_grad
    puts.append(send(grad, grad_hbm, 2))
    gets[2].wait()
    head = lax.broadcasted_iota(jnp.int32, (16, D), 0)
    lane = lax.broadcasted_iota(jnp.int32, (16, D), 1)
    member = jnp.where(lane // HEAD_DIM == head, 1.0, 0.0)
    leader = jnp.where(lane == head * HEAD_DIM, 1.0, 0.0)
    exact = functools.partial(
        lax.dot_general,
        dimension_numbers=(((1,), (1,)), ((), ())),
        precision=lax.Precision.HIGHEST,
        preferred_element_type=full,
    )
    deltas = exact(member, attended_grad.astype(full) * mixed[...])
    tops = exact(leader, logs[...])
    for pair in range(PAIRS):
        delta_ref[pair] = deltas[2 * pair : 2 * pair + 2]
        log_ref[pair] = tops[2 * pair : 2 * pair + 2]
    turned[0] = final_low[...].T
    turned[1] = second[...].T
    turned[2] = middle_low[...].T

    def weights(i, _):
        store_split(dot_of(turned[i // hidden], right[i], 1, 0), stage_keep, stage_send, i)

        @pl.when(i < hidden)
        def _():
            pltpu.make_async_copy(stage_keep.at[i], down_keep.at[i], keep_sems.at[i]).start()
            pltpu.make_async_copy(stage_send.at[i], down_send.at[i], send_sems.at[i]).start()

        @pl.when(i >= hidden)
        def _():
            row = i - hidden
            pltpu.make_async_copy(stage_keep.at[i], up_keep.at[row], keep_sems.at[i]).start()
            pltpu.make_async_copy(stage_send.at[i], up_send.at[row], send_sems.at[i]).start()

        return 0

    lax.fori_loop(0, 2 * hidden + 1, weights, 0)
    for copy in puts:
        copy.wait()
    for i in range(2 * hidden + 1):
        if i < hidden:
            keep, gone, row = down_keep, down_send, i
        else:
            keep, gone, row = up_keep, up_send, i - hidden
        pltpu.make_async_copy(stage_keep.at[i], keep.at[row], keep_sems.at[i]).wait()
        pltpu.make_async_copy(stage_send.at[i], gone.at[row], send_sems.at[i]).wait()


def middle_call(limit, vectors, tokens, mixed, logs, cot, teach, arrays, plan, block, dp):
    rows = tokens.shape[0]
    hidden = FF // D
    narrow = jax.ShapeDtypeStruct((rows, D), low)
    wide = jax.ShapeDtypeStruct((rows, D), full)
    shape = (dp // 2, D // dp, D)
    parts = [jax.ShapeDtypeStruct((count,) + shape, low) for count in (hidden, hidden + 1)]
    stats = jax.ShapeDtypeStruct((PAIRS, 2, rows), full)
    anywhere = pl.BlockSpec(memory_space=pl.ANY)
    inside = pl.BlockSpec(memory_space=pltpu.VMEM)
    moves = sum(len(part) for part in plan)
    return pl.pallas_call(
        functools.partial(middle_kernel, plan, block, len(arrays)),
        out_shape=(
            narrow,
            wide,
            narrow,
            parts[0],
            parts[0],
            parts[1],
            parts[1],
            stats,
            stats,
            jax.ShapeDtypeStruct((8 + 8, D), full),
        ),
        in_specs=[pl.BlockSpec(memory_space=pltpu.SMEM), inside]
        + [anywhere] * (5 + len(arrays)),
        out_specs=[anywhere] * 7 + [inside] * 3,
        scratch_shapes=[
            pltpu.VMEM((rows, D), low),
            pltpu.VMEM((rows, D), full),
            pltpu.VMEM((rows, D), full),
            pltpu.VMEM((rows, D), low),
            pltpu.VMEM((rows, D), low),
            pltpu.VMEM((FF, D), low),
            pltpu.VMEM((FF, D), low),
            pltpu.VMEM((D, D), low),
            pltpu.VMEM((2 * hidden + 1, rows, D), low),
            pltpu.VMEM((hidden, rows, D), full),
            pltpu.VMEM((rows, D), low),
            pltpu.VMEM((rows, D), full),
            pltpu.VMEM((rows, D), full),
            pltpu.VMEM((rows, D), low),
            pltpu.VMEM((rows, D), low),
            pltpu.VMEM((rows, D), low),
            pltpu.VMEM((rows, D), low),
            pltpu.VMEM((rows, D), full),
            pltpu.VMEM((3, D, rows), low),
            pltpu.VMEM((2 * hidden + 1,) + shape, low),
            pltpu.VMEM((2 * hidden + 1,) + shape, low),
            pltpu.SemaphoreType.DMA((5,)),
            pltpu.SemaphoreType.DMA((moves,)),
            pltpu.SemaphoreType.DMA((3,)),
            pltpu.SemaphoreType.DMA((2 * hidden + 1,)),
            pltpu.SemaphoreType.DMA((2 * hidden + 1,)),
        ],
        compiler_params=pltpu.CompilerParams(vmem_limit_bytes=VMEM_LIMIT),
        cost_estimate=SMALL_COST,
        name="middle",
    )(limit, vectors, tokens, mixed, logs, cot, teach, *arrays)


def fold_block(keep, got, out_keep, out_send, bit, place):
    step = 1 << place
    mine = (lax.axis_index("dp") // bit) % 2 * step
    for j in range(keep.shape[1] // 2):
        base = (j // step) * 2 * step + j % step
        for out, shift in ((out_keep, mine), (out_send, step - mine)):
            value = keep[0, base + shift].astype(full) + got[0, base + shift].astype(full)
            out[0, j] = value.astype(low)


def fold_kernel(bits, places, *refs):
    count = len(bits)
    for n in range(count):
        fold_block(
            *refs[2 * n : 2 * n + 2],
            *refs[2 * count + 2 * n : 2 * count + 2 * n + 2],
            bits[n],
            places[n],
        )


def fold(pairs, bits, places):
    lead = pairs[0][0].shape[0]
    block = lambda shape: pl.BlockSpec((1,) + shape[1:], lambda i: (i, 0, 0, 0))
    halves = [
        (keep.shape[0], keep.shape[1] // 2) + keep.shape[2:] for keep, _ in pairs for _ in range(2)
    ]
    outs = pl.pallas_call(
        functools.partial(fold_kernel, bits, places),
        out_shape=[jax.ShapeDtypeStruct(shape, low) for shape in halves],
        grid=(lead,),
        in_specs=[block(value.shape) for pair in pairs for value in pair],
        out_specs=[block(shape) for shape in halves],
        compiler_params=pltpu.CompilerParams(vmem_limit_bytes=VMEM_LIMIT),
        cost_estimate=pl.CostEstimate(flops=0, bytes_accessed=16 << 20, transcendentals=0),
        name="fold",
    )(*[value for pair in pairs for value in pair])
    return [(outs[2 * n], outs[2 * n + 1]) for n in range(len(pairs))]


def qkv_grad_kernel(count, *refs):
    sources = refs[: 3 * count + 1]
    outs = refs[3 * count + 1 : 3 * count + 5]
    sum_ref, held, turned, total, stage, in_sems, out_sems = refs[3 * count + 5 :]
    first_use = [0, count] + list(range(1, count)) + list(range(count + 1, 3 * count + 1))
    for n in first_use:
        pltpu.make_async_copy(sources[n], held.at[n], in_sems.at[n]).start()

    def wait(n):
        pltpu.make_async_copy(sources[0], held.at[n], in_sems.at[n]).wait()

    def turn(n, _):
        wait(n)
        turned[n] = held[n].T
        return 0

    lax.fori_loop(0, count, turn, 0)
    sum_ref[...] = jnp.zeros_like(sum_ref)

    def step(i, _):
        c = (i + count - 1) // count
        n = jnp.where(i == 0, 0, (i + count - 1) % count)
        wait(count + i)
        right = held[count + i]
        value = dot_of(turned[n], right, 1, 0)
        total[...] = value + jnp.where(n == 0, jnp.zeros_like(value), total[...])

        @pl.when(c != 1)
        def _():
            row = pl.ds(pl.multiple_of(c * 4, 8), 1)
            sum_ref[row, :] += jnp.sum(right.astype(full), axis=0, keepdims=True)

        @pl.when(i % count == 0)
        def _():
            for part in range(2):
                store_split(
                    total[:, part * D // 2 : (part + 1) * D // 2],
                    stage.at[part],
                    stage.at[2 + part],
                    c,
                )
            for k in range(4):
                pltpu.make_async_copy(
                    stage.at[k, c], outs[k].at[c], out_sems.at[k * 3 + c]
                ).start()

        return 0

    lax.fori_loop(0, 2 * count + 1, step, 0)
    for k in range(4):
        for c in range(3):
            pltpu.make_async_copy(stage.at[k, c], outs[k].at[c], out_sems.at[k * 3 + c]).wait()


def qkv_grads(chunks, query_grad, key_grads, value_grads, dp):
    rows = query_grad.shape[0]
    count = len(chunks)
    shape = (3, dp // 2, D // dp, D // 2)
    anywhere = pl.BlockSpec(memory_space=pl.ANY)
    return pl.pallas_call(
        functools.partial(qkv_grad_kernel, count),
        out_shape=[jax.ShapeDtypeStruct(shape, low)] * 4
        + [jax.ShapeDtypeStruct((16, D), full)],
        in_specs=[anywhere] * (3 * count + 1),
        out_specs=[anywhere] * 4 + [pl.BlockSpec(memory_space=pltpu.VMEM)],
        scratch_shapes=[
            pltpu.VMEM((3 * count + 1, rows, D), low),
            pltpu.VMEM((count, D, rows), low),
            pltpu.VMEM((D, D), full),
            pltpu.VMEM((4,) + shape, low),
            pltpu.SemaphoreType.DMA((3 * count + 1,)),
            pltpu.SemaphoreType.DMA((12,)),
        ],
        compiler_params=pltpu.CompilerParams(vmem_limit_bytes=VMEM_LIMIT),
        cost_estimate=SMALL_COST,
        name="qkv_grads",
    )(*chunks, query_grad, *key_grads, *value_grads)


def last_kernel(
    token_ref,
    first_ref,
    right_ref,
    left_ref,
    middle_ref,
    vector_ref,
    gain_ref,
    bias_ref,
    sum_ref,
    out_ref,
    pack_ref,
):
    @pl.when(pl.program_id(0) == 0)
    def _():
        pack_ref[...] = jnp.zeros_like(pack_ref)
        pack_ref[1:2, :] = sum_ref[0:1, :]
        pack_ref[3:4, :] = sum_ref[1:2, :]
        pack_ref[4:5, :] = bias_ref[0:1, :]
        pack_ref[5:6, :] = bias_ref[8:9, :]
        pack_ref[6:8, :] = sum_ref[2:4, :]
        pack_ref[8 : 8 + FF // D, :] = sum_ref[8 : 8 + FF // D, :]

    unit, inverse = norm_stats(token_ref[...].astype(full) + vector_ref[0:1, :])
    grad = first_ref[...] + right_ref[...].astype(full) + left_ref[...].astype(full)
    scaled = grad * gain_ref[0:1, :]
    mean_scaled = jnp.mean(scaled, axis=-1, keepdims=True)
    mean_unit = jnp.mean(scaled * unit, axis=-1, keepdims=True)
    result = middle_ref[...] + inverse * (scaled - mean_scaled - unit * mean_unit)
    out_ref[...] = result
    pack_ref[0:1, :] += jnp.sum(grad * unit, axis=0, keepdims=True)
    pack_ref[2:3, :] += jnp.sum(grad, axis=0, keepdims=True)
    pack_ref[pl.ds(16 + lax.axis_index("dp"), 1), :] += jnp.sum(result, axis=0, keepdims=True)


def last_norm(tokens, first, right, left, middle_grad, vectors, gains, bias_sums, sums, dp):
    rows = tokens.shape[0]
    part = pl.BlockSpec((rows // 4, D), lambda i: (i, 0))
    whole = lambda value: pl.BlockSpec(value.shape, lambda i: (0, 0))
    small = (vectors, gains, bias_sums, sums)
    return pl.pallas_call(
        last_kernel,
        out_shape=(
            jax.ShapeDtypeStruct((rows, D), full),
            jax.ShapeDtypeStruct((16 + dp, D), full),
        ),
        grid=(4,),
        in_specs=[part] * 5 + [whole(value) for value in small],
        out_specs=[part, pl.BlockSpec((16 + dp, D), lambda i: (0, 0))],
        compiler_params=pltpu.CompilerParams(vmem_limit_bytes=VMEM_LIMIT),
        cost_estimate=SMALL_COST,
        name="last_norm",
    )(tokens, first, right, left, middle_grad, *small)


def two_parts(value, axis, mine):
    keep = lax.dynamic_index_in_dim(value, mine, axis, keepdims=False)
    send = lax.dynamic_index_in_dim(value, 1 - mine, axis, keepdims=False)
    return keep, send.astype(low)


class Scatter:
    def __init__(self, parts, turns):
        self.bits = outer_bits()
        half = len(self.bits) // 2
        self.orders = [
            [1] + self.bits[half * (turn % 2) :] + self.bits[: half * (turn % 2)] for turn in turns
        ]
        self.left = [list(self.bits) for _ in turns]
        self.step = 0
        self.parts = parts

    def sends(self):
        return [send for _, send in self.parts]

    def exchange(self, sends):
        self.pairs = [
            (keep, swap(send, "dp", turn[self.step]))
            for (keep, _), send, turn in zip(self.parts, sends, self.orders)
        ]
        self.step += 1

    def folds(self):
        if self.step > len(self.bits):
            return [], [], []
        bits = [turn[self.step] for turn in self.orders]
        places = []
        for left, bit in zip(self.left, bits):
            places.append(left.index(bit))
            left.remove(bit)
        return self.pairs, bits, places

    def give(self, outs):
        self.parts = [(outs[n], outs[n + 1]) for n in range(0, len(outs), 2)]

    def fold(self):
        outs = []
        for pair, bit, at in zip(*self.folds()):
            outs += fold([pair], [bit], [at])[0]
        self.give(outs)

    def advance(self, order):
        sends = order(*self.sends())
        self.exchange(list(sends) if len(self.parts) > 1 else [sends])

    def finish(self, order):
        while self.step <= len(self.bits):
            self.fold()
            self.advance(order)
        got = order(*[other for _, other in self.pairs])
        return [
            (keep.astype(full) + other.astype(full))[:, 0]
            for (keep, _), other in zip(self.pairs, got)
        ]


def scatter_dp(parts, turns):
    scatter = Scatter(parts, turns)
    while True:
        sends = yield scatter.sends()
        scatter.exchange(sends)
        if scatter.step > len(scatter.bits):
            break
        scatter.parts = fold(*scatter.folds())
    got = yield [other for _, other in scatter.pairs]
    return [
        (keep.astype(full) + other.astype(full))[:, 0]
        for (keep, _), other in zip(scatter.pairs, got)
    ]


def scatter_mp(value):
    rank = lax.axis_index("mp")
    part = lambda index: lax.dynamic_index_in_dim(value, index, keepdims=False)
    sends = yield [part(rank ^ bit).astype(low) for bit in (1, 2, 3)]
    got = yield [swap(send, "mp", bit) for bit, send in zip((1, 2, 3), sends)]
    got = [other.astype(full) for other in got]
    return (part(rank) + got[0]) + (got[1] + got[2])


def halve_mp(value):
    rank = lax.axis_index("mp")
    pairs = value.reshape((2, 2) + value.shape[1:])
    keep, send = two_parts(pairs, 1, rank % 2)
    (send,) = yield [send]
    (got,) = yield [swap(send, "mp", 1)]
    keep, send = two_parts(keep.astype(full) + got.astype(full), 0, rank // 2)
    (send,) = yield [send]
    (got,) = yield [swap(send, "mp", 2)]
    return keep + got.astype(full)


def scatter_feed(up_own, down_own):
    mp = lax.axis_size("mp")
    block = down_own.shape[1]
    out_own = up_own[mp].reshape(block, mp, -1).transpose(1, 0, 2)
    own = yield from halve_mp(
        jnp.concatenate([up_own[:mp], down_own, out_own.reshape(mp, -1, D)], axis=1)
    )
    return own[:block], own[block : 2 * block].T, own[2 * block :].reshape(block, -1).T


def scatter_qkv(keep_left, keep_right, send_left, send_right):
    left_part, right_part = yield from scatter_dp(
        [(keep_left, send_left), (keep_right, send_right)], (0, 1)
    )
    width = D // lax.axis_size("mp")
    parts = [part[..., at : at + width] for part in (left_part, right_part) for at in (0, width)]
    return (yield from scatter_mp(jnp.stack(parts)))


def sum_small(value):
    (value,) = yield [value]
    value = value + swap(value, "dp", 1)
    bits = outer_bits()
    groups = [("dp", bits[n : n + 2]) for n in range(0, len(bits), 2)] + [("mp", [1, 2])]
    for axis, pair in groups:
        (value,) = yield [value]
        if len(pair) == 1:
            value = value + swap(value, axis, pair[0])
        else:
            one, two = pair
            got = [swap(value, axis, mask) for mask in (one, two, one + two)]
            if axis == "mp":
                got = yield got
            value = (value + got[0]) + (got[1] + got[2])
    return value


class Steps:
    def __init__(self, steps):
        self.steps = steps
        self.pending = next(steps)
        self.result = None

    def advance(self, order):
        if self.pending is None:
            return
        sends = order(*self.pending)
        sends = [sends] if len(self.pending) == 1 else list(sends)
        try:
            self.pending = self.steps.send(sends)
        except StopIteration as stop:
            self.pending = None
            self.result = stop.value

    def finish(self, order):
        while self.pending is not None:
            self.advance(order)
        return self.result


def shards(
    tokens_in,
    timesteps,
    lengths,
    time_table,
    norm_gains,
    norm_biases,
    w_qkv,
    qv_bias,
    w_out,
    out_bias,
    w_up,
    up_bias,
    w_down,
    down_bias,
    cotangent,
    teacher,
):
    rank = lax.axis_index("mp")
    data_rank = lax.axis_index("dp")
    mp = lax.axis_size("mp")
    dp = lax.axis_size("dp")
    own_rows = tokens_in.shape[0]
    length = lax.dynamic_index_in_dim(lengths, data_rank, keepdims=False)
    own_time = lax.dynamic_index_in_dim(timesteps, data_rank, keepdims=False)
    odd = rank % 2 == 1
    upper = rank >= 2
    middle = jnp.logical_or(rank == 1, rank == 2)
    order = Order()
    along = lambda value, pairs: lax.ppermute(value, "mp", pairs)

    block = w_qkv.shape[1]
    aligned = block % 32 == 0
    narrow = order(jnp.concatenate([w_qkv.reshape(3 * block, -1), w_out.T]))
    first_swap = swap(narrow, "mp", 1)
    tall = order(jnp.concatenate([w_up, w_down.T]))
    tall_swap = swap(tall, "mp", 1)
    pair = order(
        jnp.concatenate(
            [jnp.where(odd, first_swap, narrow), jnp.where(odd, narrow, first_swap)], axis=1
        )
    )
    second_swap = swap(pair, "mp", 2)
    tokens, lengths, own_time, norm_gains, norm_biases, out_bias, down_bias, up_bias, length = order(
        tokens_in, lengths, own_time, norm_gains, norm_biases, out_bias, down_bias, up_bias, length
    )
    table_row = lax.dynamic_slice_in_dim(time_table, own_time, 1).astype(full)
    unit_one, _ = norm_stats(tokens.astype(full) + table_row)
    first_norm = (unit_one * norm_gains[0] + norm_biases[0]).astype(low)
    loss_weight = lengths.shape[0] * MAXLEN / jnp.sum(lengths).astype(full)
    vectors = jnp.concatenate(
        [
            table_row,
            out_bias[None],
            norm_gains[1:2],
            norm_biases[1:2],
            down_bias[None],
            jnp.full((3, D), loss_weight),
            up_bias.reshape(-1, D),
            jnp.zeros((4, D), full),
        ]
    )
    scalars = jnp.stack(
        [
            rank,
            jnp.where(rank == 0, 1, rank - 1),
            jnp.where(upper, rank - 2, rank + 2),
            jnp.where(middle, rank + 1, 3 - rank),
            length,
            length - rank * own_rows,
        ]
    ).astype(jnp.int32)
    first_norm, vectors, scalars = order(first_norm, vectors, scalars)
    wide = jnp.concatenate(
        [jnp.where(upper, second_swap, pair), jnp.where(upper, pair, second_swap)], axis=1
    )
    qkv_rows, out_rows = wide[: 3 * block], wide[3 * block :]
    if aligned:
        split = 3 * block // 2
        qkv_gather = Gather([qkv_rows[:split], qkv_rows[split:]])
        qkv_gather.advance(order)
    tall = order(jnp.concatenate([tall, tall_swap]))
    tall_across = along(tall, [(1, 2), (2, 1)])

    if aligned:
        while qkv_gather.step < len(qkv_gather.bits):
            qkv_gather.advance(order)
    tall_across = order(tall_across)
    tall_other = jnp.where(middle, tall_across, along(tall_across, [(1, 0), (2, 3)]))
    sent = order(first_norm)
    from_left = along(sent, [(0, 1), (1, 2), (2, 3)])
    from_right = along(sent, [(1, 0), (2, 1), (3, 2)])
    if aligned:
        feed_gather = Gather(
            [
                jnp.concatenate([tall, out_rows[: block // 2]]),
                jnp.concatenate([tall_other, out_rows[block // 2 :]]),
            ]
        )
        qkv_gather.advance(order)
        arrays, plan = plan_of(
            qkv_gather.result,
            [
                [(0, block, 0, 0, 0, 0), (block, split - block, 1, 0, 0, 0)],
                [
                    (0, 2 * block - split, 1, 0, 0, split - block),
                    (2 * block - split, block, 1, 1, 0, 0),
                ],
            ],
        )
        query_weight, pair_weight = order(*place(arrays, plan, block, [(D, D), (D, 2 * D)]))
        feed_gather.advance(order)
    else:
        weights = lax.all_gather(qkv_rows.reshape(3, block, D), "dp", axis=1, tiled=True)
        query_weight = weights[0]
        pair_weight = jnp.concatenate([weights[1], weights[2]], axis=1)
    hop_right, hop_left = order(from_left, from_right)
    second_right = along(hop_right, [(1, 2), (2, 3)])
    second_left = along(hop_left, [(1, 0), (2, 1)])
    near = jnp.where(rank == 0, hop_left, hop_right)
    if aligned:
        while feed_gather.step < len(feed_gather.bits):
            feed_gather.advance(order)
    attend = lambda chunks, numbers, carried: attend_forward(
        chunks,
        numbers,
        scalars,
        query_weight,
        pair_weight,
        qv_bias[0:1],
        qv_bias[1:2],
        carried,
    )
    key_own, key_near, value_own, value_near, queries, *state = order(
        *attend(order(first_norm, near), (0, 1), None)
    )
    second = order(jnp.where(upper, second_right, second_left))
    third = along(second, [(1, 0), (2, 3)])
    key_second, value_second, *state = attend([second], (2,), (queries, *state))
    key_second, value_second, *state = order(key_second, value_second, *state)
    last = order(jnp.where(middle, hop_left, third))
    if aligned:
        feed_gather.advance(order)
    key_last, value_last, mixed, logs = order(*attend([order(last)], (3,), (queries, *state)))
    if aligned:
        layout = lambda masks, shift: [
            (0, block, 0, masks[0], D, 0),
            (block, block, 1, masks[0], D, 0),
            (2 * block, block, 0, masks[1], D, 0),
            (3 * block, block, 1, masks[1], D, 0),
            (4 * block, block // 2, 2, 0, 0, shift),
        ]
        arrays, plan = plan_of(
            feed_gather.result, [layout((0, 1), 0), layout((2, 3), block // 2)]
        )
    else:
        arrays = [
            lax.all_gather(w_up, ("mp", "dp"), axis=0, tiled=True),
            lax.all_gather(w_down.T, ("mp", "dp"), axis=0, tiled=True),
            lax.all_gather(out_rows, "dp", axis=0, tiled=True),
        ]
        plan = [[(0, array.shape[0], n, None, 0, 0, 0)] for n, array in enumerate(arrays)]
    chunks = [first_norm, near, second, last]
    keys = [key_own, key_near, key_second, key_last]
    values = [value_own, value_near, value_second, value_last]

    output, middle_grad, attended_grad, *parts, deltas, log_rows, sums = middle_call(
        scalars, vectors, tokens, mixed, logs, cotangent, teacher, arrays, plan, block, dp
    )
    scatter = Scatter([(parts[0], parts[1]), (parts[2], parts[3])], (1, 0))
    scatter.advance(order)

    key_grads = [None] * 4
    value_grads = [None] * 4
    firsts = [None] * 4
    query_grad = None
    for n in (3, 2, 1, 0):
        pairs, bits, places = scatter.folds() if n % 2 == 0 else ([], [], [])
        query_grad, key_grads[n], value_grads[n], firsts[n], *folded = attend_backward(
            n,
            queries,
            keys[n],
            values[n],
            order(attended_grad),
            log_rows,
            deltas,
            query_weight,
            pair_weight,
            scalars,
            query_grad,
            n == 0,
            pairs,
            bits,
            places,
        )
        firsts[n] = order(firsts[n])
        if folded:
            scatter.give(folded)
        if n == 3:
            back_last = along(firsts[3], [(0, 1), (3, 2)]).astype(full)
        elif n == 2:
            scatter.advance(order)
            payload = order((firsts[2] + back_last).astype(low))
            back_right = along(payload, [(0, 1), (1, 2)]).astype(full)
            back_left = along(payload, [(3, 2), (2, 1)]).astype(full)
        elif n == 1:
            to_right = jnp.where(
                rank == 0, firsts[1], firsts[3].astype(full) + back_right
            ).astype(low)
            to_left = (firsts[1] + back_left).astype(low)
            to_right, to_left = order(to_right, to_left)
            final_right = along(to_right, [(0, 1), (1, 2), (2, 3)])
            final_left = along(to_left, [(3, 2), (2, 1), (1, 0)])
    scatter.advance(order)
    query_grad, final_right, final_left = order(query_grad, final_right, final_left)
    *halves, bias_sums = qkv_grads(chunks, query_grad, key_grads, value_grads, dp)
    qkv = Steps(scatter_qkv(*halves))
    qkv.advance(order)
    down_own, up_own = scatter.finish(order)
    feed = Steps(scatter_feed(up_own, down_own))
    feed.advance(order)
    qkv.advance(order)
    tokens, first_own = order(tokens, firsts[0])
    input_grad, packed = last_norm(
        tokens,
        first_own,
        final_right,
        final_left,
        middle_grad,
        vectors,
        norm_gains,
        bias_sums,
        sums,
        dp,
    )
    packed, input_grad = order(packed, input_grad)
    small = Steps(sum_small(packed))
    feed.advance(order)
    feed.advance(order)
    small.advance(order)
    qkv.advance(order)
    qkv.advance(order)
    small.advance(order)
    qkv.advance(order)
    small.advance(order)
    feed.advance(order)
    total = small.finish(order)
    qkv_grad = qkv.finish(order)
    up_grad, down_grad, out_grad = feed.finish(order)
    fixed = 16
    chosen = (timesteps[None, :] == jnp.arange(time_table.shape[0])[:, None]).astype(full)
    table_grad = lax.dot_general(
        chosen,
        total[fixed:],
        (((1,), (0,)), ((), ())),
        precision=lax.Precision.HIGHEST,
        preferred_element_type=full,
    )
    return (
        output,
        input_grad,
        table_grad,
        total[0:2],
        total[2:4],
        qkv_grad,
        total[4:6],
        out_grad,
        total[6],
        up_grad,
        total[8 : 8 + FF // D].reshape(FF),
        down_grad,
        total[7],
    )


def solution(mesh):
    rows = P(both, None)
    placed = (
        rows,
        P(),
        P(),
        P(),
        P(),
        P(),
        P(None, "dp", "mp"),
        P(),
        P("mp", "dp"),
        P(),
        P("dp", "mp"),
        P(),
        P("mp", "dp"),
        P(),
        rows,
        rows,
    )
    return jax.shard_map(
        shards,
        mesh=mesh,
        in_specs=placed,
        out_specs=(
            rows,
            rows,
            P(),
            P(),
            P(),
            P(None, "dp", "mp"),
            P(),
            P("mp", "dp"),
            P(),
            P("dp", "mp"),
            P(),
            P("mp", "dp"),
            P(),
        ),
        check_vma=False,
    )
```

```python
import functools

import jax
import jax.numpy as jnp
from jax import lax
from jax.experimental import pallas as pl
from jax.experimental.pallas import tpu as pltpu
from jax.sharding import PartitionSpec as P

D = 768
HEADS = 12
HEAD_DIM = 64
FF = 3072
MAXLEN = 2048
PAIR = 2 * HEAD_DIM
PAIRS = HEADS // 2
VMEM_LIMIT = 58 << 20
SMALL_COST = pl.CostEstimate(flops=1 << 20, bytes_accessed=1 << 16, transcendentals=0)

far_below = -1e30
epsilon = 1e-05
score_scale = HEAD_DIM ** (-0.5)
low = jnp.bfloat16
full = jnp.float32
both = ("dp", "mp")


def norm_stats(values):
    center = values - jnp.mean(values, axis=-1, keepdims=True)
    spread = jnp.mean(center * center, axis=-1, keepdims=True)
    inverse = lax.rsqrt(spread + epsilon)
    return center * inverse, inverse


def dot_of(left_side, right_side, left_dim, right_dim):
    return lax.dot_general(
        left_side,
        right_side,
        (((left_dim,), (right_dim,)), ((), ())),
        preferred_element_type=full,
    )


def first_half(shape):
    return lax.broadcasted_iota(jnp.int32, shape, len(shape) - 1) < HEAD_DIM


def forward_kernel(numbers, first, final, scalars, *refs):
    count = len(numbers)
    chunk_refs = refs[:count]
    wk_ref, wv_ref, value_bias_ref = refs[count : count + 3]
    refs = refs[count + 3 :]
    if first:
        wq_ref, query_bias_ref = refs[:2]
        key_outs, value_outs = refs[2 : 2 + count], refs[2 + count : 2 + 2 * count]
        query_out, top_ref, sum_ref, acc_ref = refs[2 + 2 * count :]
        q_pair = (dot_of(chunk_refs[0][...], wq_ref[...], 1, 0) + query_bias_ref[...]).astype(low)
        q_pair = q_pair * jnp.asarray(score_scale, low)
        query_out[...] = q_pair
    else:
        q_ref, top_in, sum_in, acc_in = refs[:4]
        key_outs, value_outs = refs[4 : 4 + count], refs[4 + count : 4 + 2 * count]
        results = refs[4 + 2 * count :]
        q_pair = q_ref[...]
    weight = jnp.concatenate([wk_ref[...], wv_ref[...]], axis=1)
    keys = []
    values = []
    for n in range(count):
        both_parts = dot_of(chunk_refs[n][...], weight, 1, 0)
        keys.append(both_parts[:, :PAIR].astype(low))
        values.append((both_parts[:, PAIR:] + value_bias_ref[...]).astype(low))
        key_outs[n][...] = keys[n]
        value_outs[n][...] = values[n]
    rows = q_pair.shape[0]
    size = keys[0].shape[0]
    place = lax.broadcasted_iota(jnp.int32, (1, size), 1)
    lower = first_half((rows, PAIR))
    parts = []
    for half in range(2):
        kept = lower if half == 0 else jnp.logical_not(lower)
        q_half = jnp.where(kept, q_pair, jnp.zeros_like(q_pair))
        scores = []
        for n in range(count):
            bias = jnp.where(place + scalars[numbers[n]] * size < scalars[4], 0.0, far_below)
            scores.append(dot_of(q_half, keys[n], 1, 1) + bias)
        highest = functools.reduce(
            jnp.maximum, [jnp.max(score, axis=-1, keepdims=True) for score in scores]
        )
        totals = jnp.zeros_like(highest)
        mixed = jnp.zeros((rows, PAIR), full)
        for n in range(count):
            exp_scores = jnp.exp(scores[n] - highest)
            totals = totals + jnp.sum(exp_scores, axis=-1, keepdims=True)
            mixed = mixed + dot_of(exp_scores.astype(low), values[n], 1, 0)
        parts.append((highest, totals, mixed))
    top = jnp.where(lower, parts[0][0], parts[1][0])
    total = jnp.where(lower, parts[0][1], parts[1][1])
    mixed = jnp.where(lower, parts[0][2], parts[1][2])
    if first:
        top_ref[...] = top
        sum_ref[...] = total
        acc_ref[...] = mixed
    else:
        highest = jnp.maximum(top, top_in[...])
        here = jnp.exp(top - highest)
        before = jnp.exp(top_in[...] - highest)
        total = total * here + sum_in[...] * before
        mixed = mixed * here + acc_in[...] * before
        if final:
            results[0][...] = mixed / total
            results[1][...] = highest + jnp.log(total)
        else:
            results[0][...] = highest
            results[1][...] = total
            results[2][...] = mixed


def attend_forward(chunks, numbers, scalars, query_weight, pair_weight, query_bias, value_bias, carried):
    rows = chunks[0].shape[0]
    count = len(chunks)
    first = carried is None
    final = 3 in numbers
    column = lambda height, c: pl.BlockSpec((height, PAIR), lambda i, n: (0, c * PAIRS + i))
    whole = pl.BlockSpec((rows, D), lambda i, n: (0, 0))
    wide = jax.ShapeDtypeStruct((rows, D), full)
    narrow = jax.ShapeDtypeStruct((rows, D), low)
    extra = (query_weight, query_bias) if first else carried
    results = (narrow,) * first + (wide,) * (2 if final else 3)
    return pl.pallas_call(
        functools.partial(forward_kernel, numbers, first, final),
        out_shape=(narrow,) * (2 * count) + results,
        grid_spec=pltpu.PrefetchScalarGridSpec(
            num_scalar_prefetch=1,
            grid=(PAIRS,),
            in_specs=[whole] * count
            + [column(D, 0), column(D, 1), column(1, 0)]
            + ([column(D, 0), column(1, 0)] if first else [column(rows, 0)] * 4),
            out_specs=[column(rows, 0)] * (2 * count + len(results)),
        ),
        compiler_params=pltpu.CompilerParams(vmem_limit_bytes=VMEM_LIMIT),
        cost_estimate=SMALL_COST,
        name="attend_forward",
    )(scalars, *chunks, pair_weight, pair_weight, value_bias, *extra)


def backward_kernel(
    number,
    first,
    last,
    folds,
    scalars,
    q_ref,
    k_ref,
    v_ref,
    g_ref,
    log_ref,
    delta_ref,
    wk_ref,
    wv_ref,
    *refs
):
    if last:
        wq_ref = refs[0]
        refs = refs[1:]
    if not first:
        dq_in = refs[0]
        refs = refs[1:]
    count = len(folds)
    fold_ins, refs = refs[: 2 * count], refs[2 * count :]
    dq_ref, dk_ref, dv_ref, back_ref = refs[:4]
    fold_outs, accum = refs[4:-1], refs[-1]
    step = pl.program_id(0)
    for n, (lead, bit, at) in enumerate(folds):

        @pl.when(step < lead)
        def _():
            fold_block(
                *fold_ins[2 * n : 2 * n + 2], *fold_outs[2 * n : 2 * n + 2], bit, at
            )

    rows = q_ref.shape[0]
    keys = k_ref.shape[0]
    limit = scalars[4] - scalars[number] * keys
    q_pair = q_ref[...]
    g_pair = g_ref[...]
    k_pair = k_ref[...]
    v_pair = v_ref[...]
    lower = first_half((rows, PAIR))
    nothing = jnp.zeros((rows, PAIR), low)
    two_halves = lambda pair: jnp.concatenate(
        [jnp.where(lower, pair, nothing), jnp.where(lower, nothing, pair)]
    )
    queries = two_halves(q_pair)
    grads_out = two_halves(g_pair)
    row_of = lambda ref: jnp.concatenate([ref[0, 0:1, :], ref[0, 1:2, :]], axis=1)
    place = lax.broadcasted_iota(jnp.int32, (keys, 1), 0)
    bias = jnp.where(place < limit, 0.0, far_below)
    scores = dot_of(k_pair, queries, 1, 1) + bias
    prob_grad = dot_of(v_pair, grads_out, 1, 1)
    probs = jnp.exp(scores - row_of(log_ref))
    score_grad = (probs * (prob_grad - row_of(delta_ref))).astype(low)
    dv_low = dot_of(probs.astype(low), grads_out, 1, 0).astype(low)
    dk_low = dot_of(score_grad, queries, 1, 0).astype(low)
    turned = dot_of(k_pair.T, score_grad, 1, 0)
    upper_rows = lax.broadcasted_iota(jnp.int32, (PAIR, rows), 0) < HEAD_DIM
    dk_ref[...] = dk_low
    dv_ref[...] = dv_low
    grads = [dk_low, dv_low]
    weights = [wk_ref[...], wv_ref[...]]
    dq_all = jnp.where(upper_rows, turned[:, :rows], turned[:, rows:]).T
    if not first:
        dq_all = dq_all + dq_in[...]
    back = dot_of(jnp.concatenate(grads, axis=1), jnp.concatenate(weights, axis=1), 1, 1)
    if last:
        dq_low = (dq_all * score_scale).astype(low)
        dq_ref[...] = dq_low
        back = back + dot_of(dq_low, wq_ref[...], 1, 1)
    else:
        dq_ref[...] = dq_all

    @pl.when(step == 0)
    def _():
        accum[...] = back

    @pl.when(step > 0)
    def _():
        accum[...] += back

    @pl.when(step == PAIRS - 1)
    def _():
        back_ref[...] = accum[...].astype(back_ref.dtype)


def attend_backward(
    number,
    queries,
    keys,
    values,
    grads,
    logs,
    deltas,
    query_weight,
    pair_weight,
    scalars,
    carried,
    last,
    pairs,
    bits,
    places,
):
    rows, total = queries.shape[0], keys.shape[0]
    first = carried is None
    folds = [(keep.shape[0], bit, at) for (keep, _), bit, at in zip(pairs, bits, places)]
    halves = [
        (keep.shape[0], keep.shape[1] // 2) + keep.shape[2:] for keep, _ in pairs for _ in range(2)
    ]

    def by_lead(shape):
        end = shape[0] - 1
        return pl.BlockSpec((1,) + shape[1:], lambda i, n: (jnp.minimum(i, end), 0, 0, 0))

    column = lambda count, c: pl.BlockSpec((count, PAIR), lambda i, n: (0, c * PAIRS + i))
    stats = pl.BlockSpec((1, 2, rows), lambda i, n: (i, 0, 0))
    extra = (query_weight,) * last + (() if first else (carried,))
    extra_specs = [column(D, 0)] * last + ([] if first else [column(rows, 0)])
    return pl.pallas_call(
        functools.partial(backward_kernel, number, first, last, folds),
        out_shape=(
            jax.ShapeDtypeStruct((rows, D), low if last else full),
            jax.ShapeDtypeStruct((total, D), low),
            jax.ShapeDtypeStruct((total, D), low),
            jax.ShapeDtypeStruct((total, D), low if first else full),
            *[jax.ShapeDtypeStruct(shape, low) for shape in halves],
        ),
        grid_spec=pltpu.PrefetchScalarGridSpec(
            num_scalar_prefetch=1,
            grid=(PAIRS,),
            in_specs=[
                column(rows, 0),
                column(total, 0),
                column(total, 0),
                column(rows, 0),
                stats,
                stats,
                column(D, 0),
                column(D, 1),
            ]
            + extra_specs
            + [by_lead(value.shape) for pair in pairs for value in pair],
            out_specs=[
                column(rows, 0),
                column(total, 0),
                column(total, 0),
                pl.BlockSpec((total, D), lambda i, n: (0, 0)),
            ]
            + [by_lead(shape) for shape in halves],
            scratch_shapes=[pltpu.VMEM((total, D), full)],
        ),
        compiler_params=pltpu.CompilerParams(vmem_limit_bytes=VMEM_LIMIT),
        cost_estimate=SMALL_COST,
        name="attend_backward",
    )(
        scalars,
        queries,
        keys,
        values,
        grads,
        logs,
        deltas,
        pair_weight,
        pair_weight,
        *extra,
        *[value for pair in pairs for value in pair],
    )


def swap(value, axis, bit):
    count = lax.axis_size(axis)
    return lax.ppermute(value, axis, [(i, i ^ bit) for i in range(count)])


class Order:
    def __init__(self):
        self.marks = ()

    def __call__(self, *values):
        values = lax.optimization_barrier(values + self.marks)[: len(values)]
        self.marks = values
        return values[0] if len(values) == 1 else values


def outer_bits():
    bits = []
    bit = 2
    while bit < lax.axis_size("dp"):
        bits.append(bit)
        bit *= 2
    return bits


class Gather:
    def __init__(self, parts):
        self.bits = outer_bits()
        half = len(self.bits) // 2
        self.orders = [
            self.bits[half * (n % 2) :] + self.bits[: half * (n % 2)] for n in range(len(parts))
        ]
        self.result = [[([0], part)] for part in parts]
        self.step = 0

    def advance(self, order):
        held = self.result
        if self.step < len(self.bits):
            masks = [[m for mask, _ in pieces for m in mask] for pieces in held]
            blocks = [
                jnp.concatenate([array for _, array in pieces]) if self.step else pieces[0][1]
                for pieces in held
            ]
            blocks = order(*blocks)
            bits = [turn[self.step] for turn in self.orders]
            self.result = [
                [(mask, block), ([m ^ bit for m in mask], swap(block, "dp", bit))]
                for mask, block, bit in zip(masks, blocks, bits)
            ]
        else:
            arrays = order(*[array for pieces in held for _, array in pieces])
            arrays = iter(arrays)
            self.result = []
            for pieces in held:
                kept = [(masks, next(arrays)) for masks, _ in pieces]
                self.result.append(
                    kept + [([m ^ 1 for m in masks], swap(array, "dp", 1)) for masks, array in kept]
                )
        self.step += 1


def canonical_row(me, rank, block, mask, rank_mask, stride, offset):
    if mask is None:
        return offset
    row = (me ^ mask) * block + offset
    if stride:
        if rank_mask >= 2:
            rank_mask = rank_mask ^ ((rank + 1) // 2 % 2)
        row = row + (rank ^ rank_mask) * stride
    return pl.multiple_of(row, 16)


def place_kernel(plan, block, *refs):
    count = len(plan)
    ins = refs[:count]
    outs = refs[count:-1]
    sems = refs[-1]
    me = lax.axis_index("dp")
    rank = lax.axis_index("mp")
    copies = []
    for ref, moves in zip(ins, plan):
        for start, size, which, mask, column, _, offset in moves:
            row = canonical_row(me, rank, block, mask, 0, 0, offset)
            copy = pltpu.make_async_copy(
                ref.at[pl.ds(start, size), :],
                outs[which].at[pl.ds(row, size), pl.ds(column * D, D)],
                sems.at[len(copies)],
            )
            copy.start()
            copies.append(copy)
    for copy in copies:
        copy.wait()


def plan_of(gathered, layouts):
    arrays = []
    plan = []
    for pieces, layout in zip(gathered, layouts):
        rows = sum(size for _, size, *_ in layout)
        for masks, array in pieces:
            moves = []
            for j, mask in enumerate(masks):
                for start, size, which, rank_mask, stride, offset in layout:
                    moves.append((j * rows + start, size, which, mask, rank_mask, stride, offset))
            arrays.append(array)
            plan.append(moves)
    return arrays, plan


def place(arrays, plan, block, shapes):
    return pl.pallas_call(
        functools.partial(place_kernel, plan, block),
        out_shape=[jax.ShapeDtypeStruct(shape, low) for shape in shapes],
        in_specs=[pl.BlockSpec(memory_space=pl.ANY)] * len(arrays),
        out_specs=[pl.BlockSpec(memory_space=pltpu.VMEM)] * len(shapes),
        scratch_shapes=[pltpu.SemaphoreType.DMA((sum(len(moves) for moves in plan),))],
        compiler_params=pltpu.CompilerParams(vmem_limit_bytes=VMEM_LIMIT),
        cost_estimate=SMALL_COST,
        name="place",
    )(*arrays)


def store_split(value, keep, send, index):
    block = keep.shape[2]
    even = lax.axis_index("dp") % 2 == 0
    for outer in range(keep.shape[1]):
        first = value[2 * outer * block : (2 * outer + 1) * block]
        other = value[(2 * outer + 1) * block : (2 * outer + 2) * block]
        keep[index, outer] = jnp.where(even, first, other).astype(low)
        send[index, outer] = jnp.where(even, other, first).astype(low)


def middle_kernel(plan, block, total, *refs):
    limit_ref, vector_ref = refs[:2]
    token_hbm, mixed_hbm, log_hbm, cot_hbm, teach_hbm = refs[2:7]
    pieces = refs[7 : 7 + total]
    (
        out_hbm,
        middle_hbm,
        grad_hbm,
        down_keep,
        down_send,
        up_keep,
        up_send,
        delta_ref,
        log_ref,
        sum_ref,
    ) = refs[7 + total : 17 + total]
    (
        token,
        mixed,
        logs,
        cot,
        teach,
        up,
        down,
        proj,
        right,
        slope,
        second,
        middle,
        final,
        out,
        final_low,
        middle_low,
        grad,
        accum,
        turned,
        stage_keep,
        stage_send,
        in_sems,
        weight_sems,
        out_sems,
        keep_sems,
        send_sems,
    ) = refs[17 + total :]
    hidden = FF // D
    targets = (up, down, proj)
    rows = token.shape[0]
    me = lax.axis_index("dp")
    rank = lax.axis_index("mp")

    def fetch(ref, scratch, n):
        copy = pltpu.make_async_copy(ref, scratch, in_sems.at[n])
        copy.start()
        return copy

    def send(scratch, ref, n):
        copy = pltpu.make_async_copy(scratch, ref, out_sems.at[n])
        copy.start()
        return copy

    gets = [
        fetch(token_hbm, token, 0),
        fetch(mixed_hbm, mixed, 1),
        fetch(log_hbm, logs, 2),
        fetch(cot_hbm, cot, 3),
        fetch(teach_hbm, teach, 4),
    ]
    loads = {0: [], 1: [], 2: []}
    number = 0
    for want in (2, 0, 1):
        for ref, moves in zip(pieces, plan):
            for start, size, which, mask, rank_mask, stride, offset in moves:
                if which != want:
                    continue
                row = canonical_row(me, rank, block, mask, rank_mask, stride, offset)
                copy = pltpu.make_async_copy(
                    ref.at[pl.ds(start, size), :],
                    targets[which].at[pl.ds(row, size), :],
                    weight_sems.at[number],
                )
                copy.start()
                loads[which].append(copy)
                number += 1

    table_row = vector_ref[0:1, :]
    out_bias = vector_ref[1:2, :]
    gain = vector_ref[2:3, :]
    shift = vector_ref[3:4, :]
    down_bias = vector_ref[4:5, :]
    weight = vector_ref[5:6, :]
    gets[0].wait()
    gets[1].wait()
    right[2 * hidden] = mixed[...].astype(low)
    for copy in loads[2]:
        copy.wait()
    state = token[...].astype(full) + table_row + out_bias
    state = state + dot_of(right[2 * hidden], proj[...], 1, 1)
    middle[...] = state
    unit, _ = norm_stats(state)
    second[...] = (unit * gain + shift).astype(low)
    accum[...] = jnp.zeros((rows, D), full)
    for copy in loads[0]:
        copy.wait()
    for copy in loads[1]:
        copy.wait()

    def forward(m, _):
        place = pl.ds(pl.multiple_of(m * D, D), D)
        value = dot_of(second[...], up[place, :], 1, 0) + vector_ref[pl.ds(8 + m, 1), :]
        cumulative = 0.5 + 0.5 * lax.erf(value * (0.5**0.5))
        right[m] = (value * cumulative).astype(low)
        slope[m] = cumulative + value * jnp.exp(-0.5 * value * value) * 0.3989422804014327
        accum[...] += dot_of(right[m], down[place, :], 1, 1)
        return 0

    lax.fori_loop(0, FF // D, forward, 0)
    final_state = middle[...] + accum[...] + down_bias
    out[...] = final_state.astype(low)
    puts = [send(out, out_hbm, 0)]
    gets[3].wait()
    gets[4].wait()
    place = lax.broadcasted_iota(jnp.int32, (rows, 1), 0)
    grads = cot[...].astype(full) + weight * (final_state - teach[...].astype(full))
    grads = jnp.where(place < limit_ref[5], grads, 0.0)
    final[...] = grads
    final_low[...] = grads.astype(low)
    sum_ref[3:4, :] = jnp.sum(grads, axis=0, keepdims=True)
    accum[...] = jnp.zeros((rows, D), full)

    def backward(m, _):
        place = pl.ds(pl.multiple_of(m * D, D), D)
        value = slope[m] * dot_of(final_low[...], down[place, :], 1, 0)
        value = value.astype(low)
        right[hidden + m] = value
        sum_ref[pl.ds(8 + m, 1), :] = jnp.sum(value.astype(full), axis=0, keepdims=True)
        accum[...] += dot_of(value, up[place, :], 1, 1)
        return 0

    lax.fori_loop(0, FF // D, backward, 0)
    unit, inverse = norm_stats(middle[...])
    second_grad = accum[...]
    sum_ref[0:1, :] = jnp.sum(second_grad * unit, axis=0, keepdims=True)
    sum_ref[1:2, :] = jnp.sum(second_grad, axis=0, keepdims=True)
    scaled = second_grad * gain
    mean_scaled = jnp.mean(scaled, axis=-1, keepdims=True)
    mean_unit = jnp.mean(scaled * unit, axis=-1, keepdims=True)
    total_grad = final[...] + inverse * (scaled - mean_scaled - unit * mean_unit)
    middle[...] = total_grad
    puts.append(send(middle, middle_hbm, 1))
    middle_low[...] = total_grad.astype(low)
    sum_ref[2:3, :] = jnp.sum(total_grad, axis=0, keepdims=True)
    attended_grad = dot_of(middle_low[...], proj[...], 1, 0).astype(low)
    grad[...] = attended_grad
    puts.append(send(grad, grad_hbm, 2))
    gets[2].wait()
    head = lax.broadcasted_iota(jnp.int32, (16, D), 0)
    lane = lax.broadcasted_iota(jnp.int32, (16, D), 1)
    member = jnp.where(lane // HEAD_DIM == head, 1.0, 0.0)
    leader = jnp.where(lane == head * HEAD_DIM, 1.0, 0.0)
    exact = functools.partial(
        lax.dot_general,
        dimension_numbers=(((1,), (1,)), ((), ())),
        precision=lax.Precision.HIGHEST,
        preferred_element_type=full,
    )
    deltas = exact(member, attended_grad.astype(full) * mixed[...])
    tops = exact(leader, logs[...])
    for pair in range(PAIRS):
        delta_ref[pair] = deltas[2 * pair : 2 * pair + 2]
        log_ref[pair] = tops[2 * pair : 2 * pair + 2]
    turned[0] = final_low[...].T
    turned[1] = second[...].T
    turned[2] = middle_low[...].T

    def weights(i, _):
        store_split(dot_of(turned[i // hidden], right[i], 1, 0), stage_keep, stage_send, i)

        @pl.when(i < hidden)
        def _():
            pltpu.make_async_copy(stage_keep.at[i], down_keep.at[i], keep_sems.at[i]).start()
            pltpu.make_async_copy(stage_send.at[i], down_send.at[i], send_sems.at[i]).start()

        @pl.when(i >= hidden)
        def _():
            row = i - hidden
            pltpu.make_async_copy(stage_keep.at[i], up_keep.at[row], keep_sems.at[i]).start()
            pltpu.make_async_copy(stage_send.at[i], up_send.at[row], send_sems.at[i]).start()

        return 0

    lax.fori_loop(0, 2 * hidden + 1, weights, 0)
    for copy in puts:
        copy.wait()
    for i in range(2 * hidden + 1):
        if i < hidden:
            keep, gone, row = down_keep, down_send, i
        else:
            keep, gone, row = up_keep, up_send, i - hidden
        pltpu.make_async_copy(stage_keep.at[i], keep.at[row], keep_sems.at[i]).wait()
        pltpu.make_async_copy(stage_send.at[i], gone.at[row], send_sems.at[i]).wait()


def middle_call(limit, vectors, tokens, mixed, logs, cot, teach, arrays, plan, block, dp):
    rows = tokens.shape[0]
    hidden = FF // D
    narrow = jax.ShapeDtypeStruct((rows, D), low)
    wide = jax.ShapeDtypeStruct((rows, D), full)
    shape = (dp // 2, D // dp, D)
    parts = [jax.ShapeDtypeStruct((count,) + shape, low) for count in (hidden, hidden + 1)]
    stats = jax.ShapeDtypeStruct((PAIRS, 2, rows), full)
    anywhere = pl.BlockSpec(memory_space=pl.ANY)
    inside = pl.BlockSpec(memory_space=pltpu.VMEM)
    moves = sum(len(part) for part in plan)
    return pl.pallas_call(
        functools.partial(middle_kernel, plan, block, len(arrays)),
        out_shape=(
            narrow,
            wide,
            narrow,
            parts[0],
            parts[0],
            parts[1],
            parts[1],
            stats,
            stats,
            jax.ShapeDtypeStruct((8 + 8, D), full),
        ),
        in_specs=[pl.BlockSpec(memory_space=pltpu.SMEM), inside]
        + [anywhere] * (5 + len(arrays)),
        out_specs=[anywhere] * 7 + [inside] * 3,
        scratch_shapes=[
            pltpu.VMEM((rows, D), low),
            pltpu.VMEM((rows, D), full),
            pltpu.VMEM((rows, D), full),
            pltpu.VMEM((rows, D), low),
            pltpu.VMEM((rows, D), low),
            pltpu.VMEM((FF, D), low),
            pltpu.VMEM((FF, D), low),
            pltpu.VMEM((D, D), low),
            pltpu.VMEM((2 * hidden + 1, rows, D), low),
            pltpu.VMEM((hidden, rows, D), full),
            pltpu.VMEM((rows, D), low),
            pltpu.VMEM((rows, D), full),
            pltpu.VMEM((rows, D), full),
            pltpu.VMEM((rows, D), low),
            pltpu.VMEM((rows, D), low),
            pltpu.VMEM((rows, D), low),
            pltpu.VMEM((rows, D), low),
            pltpu.VMEM((rows, D), full),
            pltpu.VMEM((3, D, rows), low),
            pltpu.VMEM((2 * hidden + 1,) + shape, low),
            pltpu.VMEM((2 * hidden + 1,) + shape, low),
            pltpu.SemaphoreType.DMA((5,)),
            pltpu.SemaphoreType.DMA((moves,)),
            pltpu.SemaphoreType.DMA((3,)),
            pltpu.SemaphoreType.DMA((2 * hidden + 1,)),
            pltpu.SemaphoreType.DMA((2 * hidden + 1,)),
        ],
        compiler_params=pltpu.CompilerParams(vmem_limit_bytes=VMEM_LIMIT),
        cost_estimate=SMALL_COST,
        name="middle",
    )(limit, vectors, tokens, mixed, logs, cot, teach, *arrays)


def fold_block(keep, got, out_keep, out_send, bit, place):
    step = 1 << place
    mine = (lax.axis_index("dp") // bit) % 2 * step
    for j in range(keep.shape[1] // 2):
        base = (j // step) * 2 * step + j % step
        for out, shift in ((out_keep, mine), (out_send, step - mine)):
            value = keep[0, base + shift].astype(full) + got[0, base + shift].astype(full)
            out[0, j] = value.astype(low)


def fold_kernel(bits, places, *refs):
    count = len(bits)
    for n in range(count):
        fold_block(
            *refs[2 * n : 2 * n + 2],
            *refs[2 * count + 2 * n : 2 * count + 2 * n + 2],
            bits[n],
            places[n],
        )


def fold(pairs, bits, places):
    lead = pairs[0][0].shape[0]
    block = lambda shape: pl.BlockSpec((1,) + shape[1:], lambda i: (i, 0, 0, 0))
    halves = [
        (keep.shape[0], keep.shape[1] // 2) + keep.shape[2:] for keep, _ in pairs for _ in range(2)
    ]
    outs = pl.pallas_call(
        functools.partial(fold_kernel, bits, places),
        out_shape=[jax.ShapeDtypeStruct(shape, low) for shape in halves],
        grid=(lead,),
        in_specs=[block(value.shape) for pair in pairs for value in pair],
        out_specs=[block(shape) for shape in halves],
        compiler_params=pltpu.CompilerParams(vmem_limit_bytes=VMEM_LIMIT),
        cost_estimate=pl.CostEstimate(flops=0, bytes_accessed=16 << 20, transcendentals=0),
        name="fold",
    )(*[value for pair in pairs for value in pair])
    return [(outs[2 * n], outs[2 * n + 1]) for n in range(len(pairs))]


def qkv_grad_kernel(count, *refs):
    sources = refs[: 3 * count + 1]
    outs = refs[3 * count + 1 : 3 * count + 5]
    sum_ref, held, turned, total, stage, in_sems, out_sems = refs[3 * count + 5 :]
    first_use = [0, count] + list(range(1, count)) + list(range(count + 1, 3 * count + 1))
    for n in first_use:
        pltpu.make_async_copy(sources[n], held.at[n], in_sems.at[n]).start()

    def wait(n):
        pltpu.make_async_copy(sources[0], held.at[n], in_sems.at[n]).wait()

    def turn(n, _):
        wait(n)
        turned[n] = held[n].T
        return 0

    lax.fori_loop(0, count, turn, 0)
    sum_ref[...] = jnp.zeros_like(sum_ref)

    def step(i, _):
        c = (i + count - 1) // count
        n = jnp.where(i == 0, 0, (i + count - 1) % count)
        wait(count + i)
        right = held[count + i]
        value = dot_of(turned[n], right, 1, 0)
        total[...] = value + jnp.where(n == 0, jnp.zeros_like(value), total[...])

        @pl.when(c != 1)
        def _():
            row = pl.ds(pl.multiple_of(c * 4, 8), 1)
            sum_ref[row, :] += jnp.sum(right.astype(full), axis=0, keepdims=True)

        @pl.when(i % count == 0)
        def _():
            for part in range(2):
                store_split(
                    total[:, part * D // 2 : (part + 1) * D // 2],
                    stage.at[part],
                    stage.at[2 + part],
                    c,
                )
            for k in range(4):
                pltpu.make_async_copy(
                    stage.at[k, c], outs[k].at[c], out_sems.at[k * 3 + c]
                ).start()

        return 0

    lax.fori_loop(0, 2 * count + 1, step, 0)
    for k in range(4):
        for c in range(3):
            pltpu.make_async_copy(stage.at[k, c], outs[k].at[c], out_sems.at[k * 3 + c]).wait()


def qkv_grads(chunks, query_grad, key_grads, value_grads, dp):
    rows = query_grad.shape[0]
    count = len(chunks)
    shape = (3, dp // 2, D // dp, D // 2)
    anywhere = pl.BlockSpec(memory_space=pl.ANY)
    return pl.pallas_call(
        functools.partial(qkv_grad_kernel, count),
        out_shape=[jax.ShapeDtypeStruct(shape, low)] * 4
        + [jax.ShapeDtypeStruct((16, D), full)],
        in_specs=[anywhere] * (3 * count + 1),
        out_specs=[anywhere] * 4 + [pl.BlockSpec(memory_space=pltpu.VMEM)],
        scratch_shapes=[
            pltpu.VMEM((3 * count + 1, rows, D), low),
            pltpu.VMEM((count, D, rows), low),
            pltpu.VMEM((D, D), full),
            pltpu.VMEM((4,) + shape, low),
            pltpu.SemaphoreType.DMA((3 * count + 1,)),
            pltpu.SemaphoreType.DMA((12,)),
        ],
        compiler_params=pltpu.CompilerParams(vmem_limit_bytes=VMEM_LIMIT),
        cost_estimate=SMALL_COST,
        name="qkv_grads",
    )(*chunks, query_grad, *key_grads, *value_grads)


def last_kernel(
    token_ref,
    first_ref,
    right_ref,
    left_ref,
    middle_ref,
    vector_ref,
    gain_ref,
    bias_ref,
    sum_ref,
    out_ref,
    pack_ref,
):
    @pl.when(pl.program_id(0) == 0)
    def _():
        pack_ref[...] = jnp.zeros_like(pack_ref)
        pack_ref[1:2, :] = sum_ref[0:1, :]
        pack_ref[3:4, :] = sum_ref[1:2, :]
        pack_ref[4:5, :] = bias_ref[0:1, :]
        pack_ref[5:6, :] = bias_ref[8:9, :]
        pack_ref[6:8, :] = sum_ref[2:4, :]
        pack_ref[8 : 8 + FF // D, :] = sum_ref[8 : 8 + FF // D, :]

    unit, inverse = norm_stats(token_ref[...].astype(full) + vector_ref[0:1, :])
    grad = first_ref[...] + right_ref[...].astype(full) + left_ref[...].astype(full)
    scaled = grad * gain_ref[0:1, :]
    mean_scaled = jnp.mean(scaled, axis=-1, keepdims=True)
    mean_unit = jnp.mean(scaled * unit, axis=-1, keepdims=True)
    result = middle_ref[...] + inverse * (scaled - mean_scaled - unit * mean_unit)
    out_ref[...] = result
    pack_ref[0:1, :] += jnp.sum(grad * unit, axis=0, keepdims=True)
    pack_ref[2:3, :] += jnp.sum(grad, axis=0, keepdims=True)
    pack_ref[pl.ds(16 + lax.axis_index("dp"), 1), :] += jnp.sum(result, axis=0, keepdims=True)


def last_norm(tokens, first, right, left, middle_grad, vectors, gains, bias_sums, sums, dp):
    rows = tokens.shape[0]
    part = pl.BlockSpec((rows // 4, D), lambda i: (i, 0))
    whole = lambda value: pl.BlockSpec(value.shape, lambda i: (0, 0))
    small = (vectors, gains, bias_sums, sums)
    return pl.pallas_call(
        last_kernel,
        out_shape=(
            jax.ShapeDtypeStruct((rows, D), full),
            jax.ShapeDtypeStruct((16 + dp, D), full),
        ),
        grid=(4,),
        in_specs=[part] * 5 + [whole(value) for value in small],
        out_specs=[part, pl.BlockSpec((16 + dp, D), lambda i: (0, 0))],
        compiler_params=pltpu.CompilerParams(vmem_limit_bytes=VMEM_LIMIT),
        cost_estimate=SMALL_COST,
        name="last_norm",
    )(tokens, first, right, left, middle_grad, *small)


def two_parts(value, axis, mine):
    keep = lax.dynamic_index_in_dim(value, mine, axis, keepdims=False)
    send = lax.dynamic_index_in_dim(value, 1 - mine, axis, keepdims=False)
    return keep, send.astype(low)


class Scatter:
    def __init__(self, parts, turns):
        self.bits = outer_bits()
        half = len(self.bits) // 2
        self.orders = [
            [1] + self.bits[half * (turn % 2) :] + self.bits[: half * (turn % 2)] for turn in turns
        ]
        self.left = [list(self.bits) for _ in turns]
        self.step = 0
        self.parts = parts

    def sends(self):
        return [send for _, send in self.parts]

    def exchange(self, sends):
        self.pairs = [
            (keep, swap(send, "dp", turn[self.step]))
            for (keep, _), send, turn in zip(self.parts, sends, self.orders)
        ]
        self.step += 1

    def folds(self):
        if self.step > len(self.bits):
            return [], [], []
        bits = [turn[self.step] for turn in self.orders]
        places = []
        for left, bit in zip(self.left, bits):
            places.append(left.index(bit))
            left.remove(bit)
        return self.pairs, bits, places

    def give(self, outs):
        self.parts = [(outs[n], outs[n + 1]) for n in range(0, len(outs), 2)]

    def fold(self):
        outs = []
        for pair, bit, at in zip(*self.folds()):
            outs += fold([pair], [bit], [at])[0]
        self.give(outs)

    def advance(self, order):
        sends = order(*self.sends())
        self.exchange(list(sends) if len(self.parts) > 1 else [sends])

    def finish(self, order):
        while self.step <= len(self.bits):
            self.fold()
            self.advance(order)
        got = order(*[other for _, other in self.pairs])
        return [
            (keep.astype(full) + other.astype(full))[:, 0]
            for (keep, _), other in zip(self.pairs, got)
        ]


def scatter_dp(parts, turns):
    scatter = Scatter(parts, turns)
    while True:
        sends = yield scatter.sends()
        scatter.exchange(sends)
        if scatter.step > len(scatter.bits):
            break
        scatter.parts = fold(*scatter.folds())
    got = yield [other for _, other in scatter.pairs]
    return [
        (keep.astype(full) + other.astype(full))[:, 0]
        for (keep, _), other in zip(scatter.pairs, got)
    ]


def scatter_mp(value):
    rank = lax.axis_index("mp")
    part = lambda index: lax.dynamic_index_in_dim(value, index, keepdims=False)
    sends = yield [part(rank ^ bit).astype(low) for bit in (1, 2, 3)]
    got = yield [swap(send, "mp", bit) for bit, send in zip((1, 2, 3), sends)]
    got = [other.astype(full) for other in got]
    return (part(rank) + got[0]) + (got[1] + got[2])


def halve_mp(value):
    rank = lax.axis_index("mp")
    pairs = value.reshape((2, 2) + value.shape[1:])
    keep, send = two_parts(pairs, 1, rank % 2)
    (send,) = yield [send]
    (got,) = yield [swap(send, "mp", 1)]
    keep, send = two_parts(keep.astype(full) + got.astype(full), 0, rank // 2)
    (send,) = yield [send]
    (got,) = yield [swap(send, "mp", 2)]
    return keep + got.astype(full)


def scatter_feed(up_own, down_own):
    mp = lax.axis_size("mp")
    block = down_own.shape[1]
    out_own = up_own[mp].reshape(block, mp, -1).transpose(1, 0, 2)
    own = yield from halve_mp(
        jnp.concatenate([up_own[:mp], down_own, out_own.reshape(mp, -1, D)], axis=1)
    )
    return own[:block], own[block : 2 * block].T, own[2 * block :].reshape(block, -1).T


def scatter_qkv(keep_left, keep_right, send_left, send_right):
    left_part, right_part = yield from scatter_dp(
        [(keep_left, send_left), (keep_right, send_right)], (0, 1)
    )
    width = D // lax.axis_size("mp")
    parts = [part[..., at : at + width] for part in (left_part, right_part) for at in (0, width)]
    return (yield from scatter_mp(jnp.stack(parts)))


def sum_small(value):
    (value,) = yield [value]
    value = value + swap(value, "dp", 1)
    bits = outer_bits()
    groups = [("dp", bits[n : n + 2]) for n in range(0, len(bits), 2)] + [("mp", [1, 2])]
    for axis, pair in groups:
        (value,) = yield [value]
        if len(pair) == 1:
            value = value + swap(value, axis, pair[0])
        else:
            one, two = pair
            got = [swap(value, axis, mask) for mask in (one, two, one + two)]
            if axis == "mp":
                got = yield got
            value = (value + got[0]) + (got[1] + got[2])
    return value


class Steps:
    def __init__(self, steps):
        self.steps = steps
        self.pending = next(steps)
        self.result = None

    def advance(self, order):
        if self.pending is None:
            return
        sends = order(*self.pending)
        sends = [sends] if len(self.pending) == 1 else list(sends)
        try:
            self.pending = self.steps.send(sends)
        except StopIteration as stop:
            self.pending = None
            self.result = stop.value

    def finish(self, order):
        while self.pending is not None:
            self.advance(order)
        return self.result


def shards(
    tokens_in,
    timesteps,
    lengths,
    time_table,
    norm_gains,
    norm_biases,
    w_qkv,
    qv_bias,
    w_out,
    out_bias,
    w_up,
    up_bias,
    w_down,
    down_bias,
    cotangent,
    teacher,
):
    rank = lax.axis_index("mp")
    data_rank = lax.axis_index("dp")
    mp = lax.axis_size("mp")
    dp = lax.axis_size("dp")
    own_rows = tokens_in.shape[0]
    length = lax.dynamic_index_in_dim(lengths, data_rank, keepdims=False)
    own_time = lax.dynamic_index_in_dim(timesteps, data_rank, keepdims=False)
    odd = rank % 2 == 1
    upper = rank >= 2
    middle = jnp.logical_or(rank == 1, rank == 2)
    order = Order()
    along = lambda value, pairs: lax.ppermute(value, "mp", pairs)

    block = w_qkv.shape[1]
    aligned = block % 32 == 0
    narrow = order(jnp.concatenate([w_qkv.reshape(3 * block, -1), w_out.T]))
    first_swap = swap(narrow, "mp", 1)
    tall = order(jnp.concatenate([w_up, w_down.T]))
    tall_swap = swap(tall, "mp", 1)
    pair = order(
        jnp.concatenate(
            [jnp.where(odd, first_swap, narrow), jnp.where(odd, narrow, first_swap)], axis=1
        )
    )
    second_swap = swap(pair, "mp", 2)
    tokens, lengths, own_time, norm_gains, norm_biases, out_bias, down_bias, up_bias, length = order(
        tokens_in, lengths, own_time, norm_gains, norm_biases, out_bias, down_bias, up_bias, length
    )
    table_row = lax.dynamic_slice_in_dim(time_table, own_time, 1).astype(full)
    unit_one, _ = norm_stats(tokens.astype(full) + table_row)
    first_norm = (unit_one * norm_gains[0] + norm_biases[0]).astype(low)
    loss_weight = lengths.shape[0] * MAXLEN / jnp.sum(lengths).astype(full)
    vectors = jnp.concatenate(
        [
            table_row,
            out_bias[None],
            norm_gains[1:2],
            norm_biases[1:2],
            down_bias[None],
            jnp.full((3, D), loss_weight),
            up_bias.reshape(-1, D),
            jnp.zeros((4, D), full),
        ]
    )
    scalars = jnp.stack(
        [
            rank,
            jnp.where(rank == 0, 1, rank - 1),
            jnp.where(upper, rank - 2, rank + 2),
            jnp.where(middle, rank + 1, 3 - rank),
            length,
            length - rank * own_rows,
        ]
    ).astype(jnp.int32)
    first_norm, vectors, scalars = order(first_norm, vectors, scalars)
    wide = jnp.concatenate(
        [jnp.where(upper, second_swap, pair), jnp.where(upper, pair, second_swap)], axis=1
    )
    qkv_rows, out_rows = wide[: 3 * block], wide[3 * block :]
    if aligned:
        split = 3 * block // 2
        qkv_gather = Gather([qkv_rows[:split], qkv_rows[split:]])
        qkv_gather.advance(order)
    tall = order(jnp.concatenate([tall, tall_swap]))
    tall_across = along(tall, [(1, 2), (2, 1)])

    if aligned:
        while qkv_gather.step < len(qkv_gather.bits):
            qkv_gather.advance(order)
    sent = order(first_norm)
    from_left = along(sent, [(0, 1), (1, 2), (2, 3)])
    from_right = along(sent, [(1, 0), (2, 1), (3, 2)])
    tall_across = order(tall_across)
    tall_other = jnp.where(middle, tall_across, along(tall_across, [(1, 0), (2, 3)]))
    if aligned:
        qkv_gather.advance(order)
    hop_right, hop_left = order(from_left, from_right)
    second_right = along(hop_right, [(1, 2), (2, 3)])
    second_left = along(hop_left, [(1, 0), (2, 1)])
    if aligned:
        arrays, plan = plan_of(
            qkv_gather.result,
            [
                [(0, block, 0, 0, 0, 0), (block, split - block, 1, 0, 0, 0)],
                [
                    (0, 2 * block - split, 1, 0, 0, split - block),
                    (2 * block - split, block, 1, 1, 0, 0),
                ],
            ],
        )
        query_weight, pair_weight = order(*place(arrays, plan, block, [(D, D), (D, 2 * D)]))
        feed_gather = Gather(
            [
                jnp.concatenate([tall, out_rows[: block // 2]]),
                jnp.concatenate([tall_other, out_rows[block // 2 :]]),
            ]
        )
        feed_gather.advance(order)
    else:
        weights = lax.all_gather(qkv_rows.reshape(3, block, D), "dp", axis=1, tiled=True)
        query_weight = weights[0]
        pair_weight = jnp.concatenate([weights[1], weights[2]], axis=1)
    near = jnp.where(rank == 0, hop_left, hop_right)
    attend = lambda chunk, number, carried: order(
        *attend_forward(
            [order(chunk)],
            (number,),
            scalars,
            query_weight,
            pair_weight,
            qv_bias[0:1],
            qv_bias[1:2],
            carried,
        )
    )
    key_own, value_own, queries, *state = attend(first_norm, 0, None)
    if aligned:
        while feed_gather.step < len(feed_gather.bits):
            feed_gather.advance(order)
    key_near, value_near, *state = attend(near, 1, (queries, *state))
    second_right, second_left = order(second_right, second_left)
    second = order(jnp.where(upper, second_right, second_left))
    third = along(second, [(1, 0), (2, 3)])
    key_second, value_second, *state = attend(second, 2, (queries, *state))
    last = order(jnp.where(middle, hop_left, third))
    if aligned:
        feed_gather.advance(order)
    key_last, value_last, mixed, logs = attend(last, 3, (queries, *state))
    if aligned:
        layout = lambda masks, shift: [
            (0, block, 0, masks[0], D, 0),
            (block, block, 1, masks[0], D, 0),
            (2 * block, block, 0, masks[1], D, 0),
            (3 * block, block, 1, masks[1], D, 0),
            (4 * block, block // 2, 2, 0, 0, shift),
        ]
        arrays, plan = plan_of(
            feed_gather.result, [layout((0, 1), 0), layout((2, 3), block // 2)]
        )
    else:
        arrays = [
            lax.all_gather(w_up, ("mp", "dp"), axis=0, tiled=True),
            lax.all_gather(w_down.T, ("mp", "dp"), axis=0, tiled=True),
            lax.all_gather(out_rows, "dp", axis=0, tiled=True),
        ]
        plan = [[(0, array.shape[0], n, None, 0, 0, 0)] for n, array in enumerate(arrays)]
    chunks = [first_norm, near, second, last]
    keys = [key_own, key_near, key_second, key_last]
    values = [value_own, value_near, value_second, value_last]

    output, middle_grad, attended_grad, *parts, deltas, log_rows, sums = middle_call(
        scalars, vectors, tokens, mixed, logs, cotangent, teacher, arrays, plan, block, dp
    )
    scatter = Scatter([(parts[0], parts[1]), (parts[2], parts[3])], (1, 0))
    scatter.advance(order)

    key_grads = [None] * 4
    value_grads = [None] * 4
    firsts = [None] * 4
    query_grad = None
    for n in (3, 2, 1, 0):
        pairs, bits, places = scatter.folds() if n % 2 == 0 else ([], [], [])
        query_grad, key_grads[n], value_grads[n], firsts[n], *folded = attend_backward(
            n,
            queries,
            keys[n],
            values[n],
            order(attended_grad),
            log_rows,
            deltas,
            query_weight,
            pair_weight,
            scalars,
            query_grad,
            n == 0,
            pairs,
            bits,
            places,
        )
        firsts[n] = order(firsts[n])
        if folded:
            scatter.give(folded)
        if n == 3:
            back_last = along(firsts[3], [(0, 1), (3, 2)]).astype(full)
        elif n == 2:
            scatter.advance(order)
            payload = order((firsts[2] + back_last).astype(low))
            back_right = along(payload, [(0, 1), (1, 2)]).astype(full)
            back_left = along(payload, [(3, 2), (2, 1)]).astype(full)
        elif n == 1:
            to_right = jnp.where(
                rank == 0, firsts[1], firsts[3].astype(full) + back_right
            ).astype(low)
            to_left = (firsts[1] + back_left).astype(low)
            to_right, to_left = order(to_right, to_left)
            final_right = along(to_right, [(0, 1), (1, 2), (2, 3)])
            final_left = along(to_left, [(3, 2), (2, 1), (1, 0)])
    scatter.advance(order)
    query_grad, final_right, final_left = order(query_grad, final_right, final_left)
    *halves, bias_sums = qkv_grads(chunks, query_grad, key_grads, value_grads, dp)
    qkv = Steps(scatter_qkv(*halves))
    qkv.advance(order)
    down_own, up_own = scatter.finish(order)
    feed = Steps(scatter_feed(up_own, down_own))
    feed.advance(order)
    qkv.advance(order)
    tokens, first_own = order(tokens, firsts[0])
    input_grad, packed = last_norm(
        tokens,
        first_own,
        final_right,
        final_left,
        middle_grad,
        vectors,
        norm_gains,
        bias_sums,
        sums,
        dp,
    )
    packed, input_grad = order(packed, input_grad)
    small = Steps(sum_small(packed))
    feed.advance(order)
    feed.advance(order)
    small.advance(order)
    qkv.advance(order)
    qkv.advance(order)
    small.advance(order)
    qkv.advance(order)
    small.advance(order)
    feed.advance(order)
    total = small.finish(order)
    qkv_grad = qkv.finish(order)
    up_grad, down_grad, out_grad = feed.finish(order)
    fixed = 16
    chosen = (timesteps[None, :] == jnp.arange(time_table.shape[0])[:, None]).astype(full)
    table_grad = lax.dot_general(
        chosen,
        total[fixed:],
        (((1,), (0,)), ((), ())),
        precision=lax.Precision.HIGHEST,
        preferred_element_type=full,
    )
    return (
        output,
        input_grad,
        table_grad,
        total[0:2],
        total[2:4],
        qkv_grad,
        total[4:6],
        out_grad,
        total[6],
        up_grad,
        total[8 : 8 + FF // D].reshape(FF),
        down_grad,
        total[7],
    )


def solution(mesh):
    rows = P(both, None)
    placed = (
        rows,
        P(),
        P(),
        P(),
        P(),
        P(),
        P(None, "dp", "mp"),
        P(),
        P("mp", "dp"),
        P(),
        P("dp", "mp"),
        P(),
        P("mp", "dp"),
        P(),
        rows,
        rows,
    )
    return jax.shard_map(
        shards,
        mesh=mesh,
        in_specs=placed,
        out_specs=(
            rows,
            rows,
            P(),
            P(),
            P(),
            P(None, "dp", "mp"),
            P(),
            P("mp", "dp"),
            P(),
            P("dp", "mp"),
            P(),
            P("mp", "dp"),
            P(),
        ),
        check_vma=False,
    )
```

```python
import functools

import jax
import jax.numpy as jnp
from jax import lax
from jax.experimental import pallas as pl
from jax.experimental.pallas import tpu as pltpu
from jax.sharding import PartitionSpec as P

D = 768
HEADS = 12
HEAD_DIM = 64
FF = 3072
MAXLEN = 2048
PAIR = 2 * HEAD_DIM
PAIRS = HEADS // 2
VMEM_LIMIT = 58 << 20
SMALL_COST = pl.CostEstimate(flops=1 << 20, bytes_accessed=1 << 16, transcendentals=0)

far_below = -1e30
epsilon = 1e-05
score_scale = HEAD_DIM ** (-0.5)
low = jnp.bfloat16
full = jnp.float32
both = ("dp", "mp")


def norm_stats(values):
    center = values - jnp.mean(values, axis=-1, keepdims=True)
    spread = jnp.mean(center * center, axis=-1, keepdims=True)
    inverse = lax.rsqrt(spread + epsilon)
    return center * inverse, inverse


def dot_of(left_side, right_side, left_dim, right_dim):
    return lax.dot_general(
        left_side,
        right_side,
        (((left_dim,), (right_dim,)), ((), ())),
        preferred_element_type=full,
    )


def first_half(shape):
    return lax.broadcasted_iota(jnp.int32, shape, len(shape) - 1) < HEAD_DIM


def forward_kernel(numbers, first, final, scalars, *refs):
    count = len(numbers)
    chunk_refs = refs[:count]
    wk_ref, wv_ref, value_bias_ref = refs[count : count + 3]
    refs = refs[count + 3 :]
    if first:
        wq_ref, query_bias_ref = refs[:2]
        key_outs, value_outs = refs[2 : 2 + count], refs[2 + count : 2 + 2 * count]
        query_out, top_ref, sum_ref, acc_ref = refs[2 + 2 * count :]
        q_pair = (dot_of(chunk_refs[0][...], wq_ref[...], 1, 0) + query_bias_ref[...]).astype(low)
        q_pair = q_pair * jnp.asarray(score_scale, low)
        query_out[...] = q_pair
    else:
        q_ref, top_in, sum_in, acc_in = refs[:4]
        key_outs, value_outs = refs[4 : 4 + count], refs[4 + count : 4 + 2 * count]
        results = refs[4 + 2 * count :]
        q_pair = q_ref[...]
    weight = jnp.concatenate([wk_ref[...], wv_ref[...]], axis=1)
    keys = []
    values = []
    for n in range(count):
        both_parts = dot_of(chunk_refs[n][...], weight, 1, 0)
        keys.append(both_parts[:, :PAIR].astype(low))
        values.append((both_parts[:, PAIR:] + value_bias_ref[...]).astype(low))
        key_outs[n][...] = keys[n]
        value_outs[n][...] = values[n]
    rows = q_pair.shape[0]
    size = keys[0].shape[0]
    place = lax.broadcasted_iota(jnp.int32, (1, size), 1)
    lower = first_half((rows, PAIR))
    parts = []
    for half in range(2):
        kept = lower if half == 0 else jnp.logical_not(lower)
        q_half = jnp.where(kept, q_pair, jnp.zeros_like(q_pair))
        scores = []
        for n in range(count):
            bias = jnp.where(place + scalars[numbers[n]] * size < scalars[4], 0.0, far_below)
            scores.append(dot_of(q_half, keys[n], 1, 1) + bias)
        highest = functools.reduce(
            jnp.maximum, [jnp.max(score, axis=-1, keepdims=True) for score in scores]
        )
        totals = jnp.zeros_like(highest)
        mixed = jnp.zeros((rows, PAIR), full)
        for n in range(count):
            exp_scores = jnp.exp(scores[n] - highest)
            totals = totals + jnp.sum(exp_scores, axis=-1, keepdims=True)
            mixed = mixed + dot_of(exp_scores.astype(low), values[n], 1, 0)
        parts.append((highest, totals, mixed))
    top = jnp.where(lower, parts[0][0], parts[1][0])
    total = jnp.where(lower, parts[0][1], parts[1][1])
    mixed = jnp.where(lower, parts[0][2], parts[1][2])
    if first:
        top_ref[...] = top
        sum_ref[...] = total
        acc_ref[...] = mixed
    else:
        highest = jnp.maximum(top, top_in[...])
        here = jnp.exp(top - highest)
        before = jnp.exp(top_in[...] - highest)
        total = total * here + sum_in[...] * before
        mixed = mixed * here + acc_in[...] * before
        if final:
            results[0][...] = mixed / total
            results[1][...] = highest + jnp.log(total)
        else:
            results[0][...] = highest
            results[1][...] = total
            results[2][...] = mixed


def attend_forward(chunks, numbers, scalars, query_weight, pair_weight, query_bias, value_bias, carried):
    rows = chunks[0].shape[0]
    count = len(chunks)
    first = carried is None
    final = 3 in numbers
    column = lambda height, c: pl.BlockSpec((height, PAIR), lambda i, n: (0, c * PAIRS + i))
    whole = pl.BlockSpec((rows, D), lambda i, n: (0, 0))
    wide = jax.ShapeDtypeStruct((rows, D), full)
    narrow = jax.ShapeDtypeStruct((rows, D), low)
    extra = (query_weight, query_bias) if first else carried
    results = (narrow,) * first + (wide,) * (2 if final else 3)
    return pl.pallas_call(
        functools.partial(forward_kernel, numbers, first, final),
        out_shape=(narrow,) * (2 * count) + results,
        grid_spec=pltpu.PrefetchScalarGridSpec(
            num_scalar_prefetch=1,
            grid=(PAIRS,),
            in_specs=[whole] * count
            + [column(D, 0), column(D, 1), column(1, 0)]
            + ([column(D, 0), column(1, 0)] if first else [column(rows, 0)] * 4),
            out_specs=[column(rows, 0)] * (2 * count + len(results)),
        ),
        compiler_params=pltpu.CompilerParams(vmem_limit_bytes=VMEM_LIMIT),
        cost_estimate=SMALL_COST,
        name="attend_forward",
    )(scalars, *chunks, pair_weight, pair_weight, value_bias, *extra)


def backward_kernel(
    number,
    first,
    last,
    folds,
    scalars,
    q_ref,
    k_ref,
    v_ref,
    g_ref,
    log_ref,
    delta_ref,
    wk_ref,
    wv_ref,
    *refs
):
    if last:
        wq_ref = refs[0]
        refs = refs[1:]
    if not first:
        dq_in = refs[0]
        refs = refs[1:]
    count = len(folds)
    fold_ins, refs = refs[: 2 * count], refs[2 * count :]
    dq_ref, dk_ref, dv_ref, back_ref = refs[:4]
    fold_outs, accum = refs[4:-1], refs[-1]
    step = pl.program_id(0)
    for n, (lead, bit, at) in enumerate(folds):

        @pl.when(step < lead)
        def _():
            fold_block(
                *fold_ins[2 * n : 2 * n + 2], *fold_outs[2 * n : 2 * n + 2], bit, at
            )

    rows = q_ref.shape[0]
    keys = k_ref.shape[0]
    limit = scalars[4] - scalars[number] * keys
    q_pair = q_ref[...]
    g_pair = g_ref[...]
    k_pair = k_ref[...]
    v_pair = v_ref[...]
    lower = first_half((rows, PAIR))
    nothing = jnp.zeros((rows, PAIR), low)
    two_halves = lambda pair: jnp.concatenate(
        [jnp.where(lower, pair, nothing), jnp.where(lower, nothing, pair)]
    )
    queries = two_halves(q_pair)
    grads_out = two_halves(g_pair)
    row_of = lambda ref: jnp.concatenate([ref[0, 0:1, :], ref[0, 1:2, :]], axis=1)
    place = lax.broadcasted_iota(jnp.int32, (keys, 1), 0)
    bias = jnp.where(place < limit, 0.0, far_below)
    scores = dot_of(k_pair, queries, 1, 1) + bias
    prob_grad = dot_of(v_pair, grads_out, 1, 1)
    probs = jnp.exp(scores - row_of(log_ref))
    score_grad = (probs * (prob_grad - row_of(delta_ref))).astype(low)
    dv_low = dot_of(probs.astype(low), grads_out, 1, 0).astype(low)
    dk_low = dot_of(score_grad, queries, 1, 0).astype(low)
    turned = dot_of(k_pair.T, score_grad, 1, 0)
    upper_rows = lax.broadcasted_iota(jnp.int32, (PAIR, rows), 0) < HEAD_DIM
    dk_ref[...] = dk_low
    dv_ref[...] = dv_low
    grads = [dk_low, dv_low]
    weights = [wk_ref[...], wv_ref[...]]
    dq_all = jnp.where(upper_rows, turned[:, :rows], turned[:, rows:]).T
    if not first:
        dq_all = dq_all + dq_in[...]
    back = dot_of(jnp.concatenate(grads, axis=1), jnp.concatenate(weights, axis=1), 1, 1)
    if last:
        dq_low = (dq_all * score_scale).astype(low)
        dq_ref[...] = dq_low
        back = back + dot_of(dq_low, wq_ref[...], 1, 1)
    else:
        dq_ref[...] = dq_all

    @pl.when(step == 0)
    def _():
        accum[...] = back

    @pl.when(step > 0)
    def _():
        accum[...] += back

    @pl.when(step == PAIRS - 1)
    def _():
        back_ref[...] = accum[...].astype(back_ref.dtype)


def attend_backward(
    number,
    queries,
    keys,
    values,
    grads,
    logs,
    deltas,
    query_weight,
    pair_weight,
    scalars,
    carried,
    last,
    pairs,
    bits,
    places,
):
    rows, total = queries.shape[0], keys.shape[0]
    first = carried is None
    folds = [(keep.shape[0], bit, at) for (keep, _), bit, at in zip(pairs, bits, places)]
    halves = [
        (keep.shape[0], keep.shape[1] // 2) + keep.shape[2:] for keep, _ in pairs for _ in range(2)
    ]

    def by_lead(shape):
        end = shape[0] - 1
        return pl.BlockSpec((1,) + shape[1:], lambda i, n: (jnp.minimum(i, end), 0, 0, 0))

    column = lambda count, c: pl.BlockSpec((count, PAIR), lambda i, n: (0, c * PAIRS + i))
    stats = pl.BlockSpec((1, 2, rows), lambda i, n: (i, 0, 0))
    extra = (query_weight,) * last + (() if first else (carried,))
    extra_specs = [column(D, 0)] * last + ([] if first else [column(rows, 0)])
    return pl.pallas_call(
        functools.partial(backward_kernel, number, first, last, folds),
        out_shape=(
            jax.ShapeDtypeStruct((rows, D), low if last else full),
            jax.ShapeDtypeStruct((total, D), low),
            jax.ShapeDtypeStruct((total, D), low),
            jax.ShapeDtypeStruct((total, D), low if first else full),
            *[jax.ShapeDtypeStruct(shape, low) for shape in halves],
        ),
        grid_spec=pltpu.PrefetchScalarGridSpec(
            num_scalar_prefetch=1,
            grid=(PAIRS,),
            in_specs=[
                column(rows, 0),
                column(total, 0),
                column(total, 0),
                column(rows, 0),
                stats,
                stats,
                column(D, 0),
                column(D, 1),
            ]
            + extra_specs
            + [by_lead(value.shape) for pair in pairs for value in pair],
            out_specs=[
                column(rows, 0),
                column(total, 0),
                column(total, 0),
                pl.BlockSpec((total, D), lambda i, n: (0, 0)),
            ]
            + [by_lead(shape) for shape in halves],
            scratch_shapes=[pltpu.VMEM((total, D), full)],
        ),
        compiler_params=pltpu.CompilerParams(vmem_limit_bytes=VMEM_LIMIT),
        cost_estimate=SMALL_COST,
        name="attend_backward",
    )(
        scalars,
        queries,
        keys,
        values,
        grads,
        logs,
        deltas,
        pair_weight,
        pair_weight,
        *extra,
        *[value for pair in pairs for value in pair],
    )


def swap(value, axis, bit):
    count = lax.axis_size(axis)
    return lax.ppermute(value, axis, [(i, i ^ bit) for i in range(count)])


class Order:
    def __init__(self):
        self.marks = ()

    def __call__(self, *values):
        values = lax.optimization_barrier(values + self.marks)[: len(values)]
        self.marks = values
        return values[0] if len(values) == 1 else values


def outer_bits():
    bits = []
    bit = 2
    while bit < lax.axis_size("dp"):
        bits.append(bit)
        bit *= 2
    return bits


class Gather:
    def __init__(self, parts):
        self.bits = outer_bits()
        half = len(self.bits) // 2
        self.orders = [
            self.bits[half * (n % 2) :] + self.bits[: half * (n % 2)] for n in range(len(parts))
        ]
        self.result = [[([0], part)] for part in parts]
        self.step = 0

    def advance(self, order):
        held = self.result
        if self.step < len(self.bits):
            masks = [[m for mask, _ in pieces for m in mask] for pieces in held]
            blocks = [
                jnp.concatenate([array for _, array in pieces]) if self.step else pieces[0][1]
                for pieces in held
            ]
            blocks = order(*blocks)
            bits = [turn[self.step] for turn in self.orders]
            self.result = [
                [(mask, block), ([m ^ bit for m in mask], swap(block, "dp", bit))]
                for mask, block, bit in zip(masks, blocks, bits)
            ]
        else:
            arrays = order(*[array for pieces in held for _, array in pieces])
            arrays = iter(arrays)
            self.result = []
            for pieces in held:
                kept = [(masks, next(arrays)) for masks, _ in pieces]
                self.result.append(
                    kept + [([m ^ 1 for m in masks], swap(array, "dp", 1)) for masks, array in kept]
                )
        self.step += 1


def canonical_row(me, rank, block, mask, rank_mask, stride, offset):
    if mask is None:
        return offset
    row = (me ^ mask) * block + offset
    if stride:
        if rank_mask >= 2:
            rank_mask = rank_mask ^ ((rank + 1) // 2 % 2)
        row = row + (rank ^ rank_mask) * stride
    return pl.multiple_of(row, 16)


def place_kernel(plan, block, *refs):
    count = len(plan)
    ins = refs[:count]
    outs = refs[count:-1]
    sems = refs[-1]
    me = lax.axis_index("dp")
    rank = lax.axis_index("mp")
    copies = []
    for ref, moves in zip(ins, plan):
        for start, size, which, mask, column, _, offset in moves:
            row = canonical_row(me, rank, block, mask, 0, 0, offset)
            copy = pltpu.make_async_copy(
                ref.at[pl.ds(start, size), :],
                outs[which].at[pl.ds(row, size), pl.ds(column * D, D)],
                sems.at[len(copies)],
            )
            copy.start()
            copies.append(copy)
    for copy in copies:
        copy.wait()


def plan_of(gathered, layouts):
    arrays = []
    plan = []
    for pieces, layout in zip(gathered, layouts):
        rows = sum(size for _, size, *_ in layout)
        for masks, array in pieces:
            moves = []
            for j, mask in enumerate(masks):
                for start, size, which, rank_mask, stride, offset in layout:
                    moves.append((j * rows + start, size, which, mask, rank_mask, stride, offset))
            arrays.append(array)
            plan.append(moves)
    return arrays, plan


def place(arrays, plan, block, shapes):
    return pl.pallas_call(
        functools.partial(place_kernel, plan, block),
        out_shape=[jax.ShapeDtypeStruct(shape, low) for shape in shapes],
        in_specs=[pl.BlockSpec(memory_space=pl.ANY)] * len(arrays),
        out_specs=[pl.BlockSpec(memory_space=pltpu.VMEM)] * len(shapes),
        scratch_shapes=[pltpu.SemaphoreType.DMA((sum(len(moves) for moves in plan),))],
        compiler_params=pltpu.CompilerParams(vmem_limit_bytes=VMEM_LIMIT),
        cost_estimate=SMALL_COST,
        name="place",
    )(*arrays)


def store_split(value, keep, send, index):
    block = keep.shape[2]
    even = lax.axis_index("dp") % 2 == 0
    for outer in range(keep.shape[1]):
        first = value[2 * outer * block : (2 * outer + 1) * block]
        other = value[(2 * outer + 1) * block : (2 * outer + 2) * block]
        keep[index, outer] = jnp.where(even, first, other).astype(low)
        send[index, outer] = jnp.where(even, other, first).astype(low)


def middle_kernel(plan, block, total, *refs):
    limit_ref, vector_ref = refs[:2]
    token_hbm, mixed_hbm, log_hbm, cot_hbm, teach_hbm = refs[2:7]
    pieces = refs[7 : 7 + total]
    (
        out_hbm,
        middle_hbm,
        grad_hbm,
        down_keep,
        down_send,
        up_keep,
        up_send,
        delta_ref,
        log_ref,
        sum_ref,
    ) = refs[7 + total : 17 + total]
    (
        token,
        mixed,
        logs,
        cot,
        teach,
        up,
        down,
        proj,
        right,
        slope,
        second,
        middle,
        final,
        out,
        final_low,
        middle_low,
        grad,
        accum,
        turned,
        stage_keep,
        stage_send,
        in_sems,
        weight_sems,
        out_sems,
        keep_sems,
        send_sems,
    ) = refs[17 + total :]
    hidden = FF // D
    targets = (up, down, proj)
    rows = token.shape[0]
    me = lax.axis_index("dp")
    rank = lax.axis_index("mp")

    def fetch(ref, scratch, n):
        copy = pltpu.make_async_copy(ref, scratch, in_sems.at[n])
        copy.start()
        return copy

    def send(scratch, ref, n):
        copy = pltpu.make_async_copy(scratch, ref, out_sems.at[n])
        copy.start()
        return copy

    gets = [
        fetch(token_hbm, token, 0),
        fetch(mixed_hbm, mixed, 1),
        fetch(log_hbm, logs, 2),
        fetch(cot_hbm, cot, 3),
        fetch(teach_hbm, teach, 4),
    ]
    loads = {0: [], 1: [], 2: []}
    number = 0
    for want in (2, 0, 1):
        for ref, moves in zip(pieces, plan):
            for start, size, which, mask, rank_mask, stride, offset in moves:
                if which != want:
                    continue
                row = canonical_row(me, rank, block, mask, rank_mask, stride, offset)
                copy = pltpu.make_async_copy(
                    ref.at[pl.ds(start, size), :],
                    targets[which].at[pl.ds(row, size), :],
                    weight_sems.at[number],
                )
                copy.start()
                loads[which].append(copy)
                number += 1

    table_row = vector_ref[0:1, :]
    out_bias = vector_ref[1:2, :]
    gain = vector_ref[2:3, :]
    shift = vector_ref[3:4, :]
    down_bias = vector_ref[4:5, :]
    weight = vector_ref[5:6, :]
    gets[0].wait()
    gets[1].wait()
    right[2 * hidden] = mixed[...].astype(low)
    for copy in loads[2]:
        copy.wait()
    state = token[...].astype(full) + table_row + out_bias
    state = state + dot_of(right[2 * hidden], proj[...], 1, 1)
    middle[...] = state
    unit, _ = norm_stats(state)
    second[...] = (unit * gain + shift).astype(low)
    accum[...] = jnp.zeros((rows, D), full)
    for copy in loads[0]:
        copy.wait()
    for copy in loads[1]:
        copy.wait()

    def forward(m, _):
        place = pl.ds(pl.multiple_of(m * D, D), D)
        value = dot_of(second[...], up[place, :], 1, 0) + vector_ref[pl.ds(8 + m, 1), :]
        cumulative = 0.5 + 0.5 * lax.erf(value * (0.5**0.5))
        right[m] = (value * cumulative).astype(low)
        slope[m] = cumulative + value * jnp.exp(-0.5 * value * value) * 0.3989422804014327
        accum[...] += dot_of(right[m], down[place, :], 1, 1)
        return 0

    lax.fori_loop(0, FF // D, forward, 0)
    final_state = middle[...] + accum[...] + down_bias
    out[...] = final_state.astype(low)
    puts = [send(out, out_hbm, 0)]
    gets[3].wait()
    gets[4].wait()
    place = lax.broadcasted_iota(jnp.int32, (rows, 1), 0)
    grads = cot[...].astype(full) + weight * (final_state - teach[...].astype(full))
    grads = jnp.where(place < limit_ref[5], grads, 0.0)
    final[...] = grads
    final_low[...] = grads.astype(low)
    sum_ref[3:4, :] = jnp.sum(grads, axis=0, keepdims=True)
    accum[...] = jnp.zeros((rows, D), full)

    def backward(m, _):
        place = pl.ds(pl.multiple_of(m * D, D), D)
        value = slope[m] * dot_of(final_low[...], down[place, :], 1, 0)
        value = value.astype(low)
        right[hidden + m] = value
        sum_ref[pl.ds(8 + m, 1), :] = jnp.sum(value.astype(full), axis=0, keepdims=True)
        accum[...] += dot_of(value, up[place, :], 1, 1)
        return 0

    lax.fori_loop(0, FF // D, backward, 0)
    unit, inverse = norm_stats(middle[...])
    second_grad = accum[...]
    sum_ref[0:1, :] = jnp.sum(second_grad * unit, axis=0, keepdims=True)
    sum_ref[1:2, :] = jnp.sum(second_grad, axis=0, keepdims=True)
    scaled = second_grad * gain
    mean_scaled = jnp.mean(scaled, axis=-1, keepdims=True)
    mean_unit = jnp.mean(scaled * unit, axis=-1, keepdims=True)
    total_grad = final[...] + inverse * (scaled - mean_scaled - unit * mean_unit)
    middle[...] = total_grad
    puts.append(send(middle, middle_hbm, 1))
    middle_low[...] = total_grad.astype(low)
    sum_ref[2:3, :] = jnp.sum(total_grad, axis=0, keepdims=True)
    attended_grad = dot_of(middle_low[...], proj[...], 1, 0).astype(low)
    grad[...] = attended_grad
    puts.append(send(grad, grad_hbm, 2))
    gets[2].wait()
    head = lax.broadcasted_iota(jnp.int32, (16, D), 0)
    lane = lax.broadcasted_iota(jnp.int32, (16, D), 1)
    member = jnp.where(lane // HEAD_DIM == head, 1.0, 0.0)
    leader = jnp.where(lane == head * HEAD_DIM, 1.0, 0.0)
    exact = functools.partial(
        lax.dot_general,
        dimension_numbers=(((1,), (1,)), ((), ())),
        precision=lax.Precision.HIGHEST,
        preferred_element_type=full,
    )
    deltas = exact(member, attended_grad.astype(full) * mixed[...])
    tops = exact(leader, logs[...])
    for pair in range(PAIRS):
        delta_ref[pair] = deltas[2 * pair : 2 * pair + 2]
        log_ref[pair] = tops[2 * pair : 2 * pair + 2]
    turned[0] = final_low[...].T
    turned[1] = second[...].T
    turned[2] = middle_low[...].T

    def weights(i, _):
        store_split(dot_of(turned[i // hidden], right[i], 1, 0), stage_keep, stage_send, i)

        @pl.when(i < hidden)
        def _():
            pltpu.make_async_copy(stage_keep.at[i], down_keep.at[i], keep_sems.at[i]).start()
            pltpu.make_async_copy(stage_send.at[i], down_send.at[i], send_sems.at[i]).start()

        @pl.when(i >= hidden)
        def _():
            row = i - hidden
            pltpu.make_async_copy(stage_keep.at[i], up_keep.at[row], keep_sems.at[i]).start()
            pltpu.make_async_copy(stage_send.at[i], up_send.at[row], send_sems.at[i]).start()

        return 0

    lax.fori_loop(0, 2 * hidden + 1, weights, 0)
    for copy in puts:
        copy.wait()
    for i in range(2 * hidden + 1):
        if i < hidden:
            keep, gone, row = down_keep, down_send, i
        else:
            keep, gone, row = up_keep, up_send, i - hidden
        pltpu.make_async_copy(stage_keep.at[i], keep.at[row], keep_sems.at[i]).wait()
        pltpu.make_async_copy(stage_send.at[i], gone.at[row], send_sems.at[i]).wait()


def middle_call(limit, vectors, tokens, mixed, logs, cot, teach, arrays, plan, block, dp):
    rows = tokens.shape[0]
    hidden = FF // D
    narrow = jax.ShapeDtypeStruct((rows, D), low)
    wide = jax.ShapeDtypeStruct((rows, D), full)
    shape = (dp // 2, D // dp, D)
    parts = [jax.ShapeDtypeStruct((count,) + shape, low) for count in (hidden, hidden + 1)]
    stats = jax.ShapeDtypeStruct((PAIRS, 2, rows), full)
    anywhere = pl.BlockSpec(memory_space=pl.ANY)
    inside = pl.BlockSpec(memory_space=pltpu.VMEM)
    moves = sum(len(part) for part in plan)
    return pl.pallas_call(
        functools.partial(middle_kernel, plan, block, len(arrays)),
        out_shape=(
            narrow,
            wide,
            narrow,
            parts[0],
            parts[0],
            parts[1],
            parts[1],
            stats,
            stats,
            jax.ShapeDtypeStruct((8 + 8, D), full),
        ),
        in_specs=[pl.BlockSpec(memory_space=pltpu.SMEM), inside]
        + [anywhere] * (5 + len(arrays)),
        out_specs=[anywhere] * 7 + [inside] * 3,
        scratch_shapes=[
            pltpu.VMEM((rows, D), low),
            pltpu.VMEM((rows, D), full),
            pltpu.VMEM((rows, D), full),
            pltpu.VMEM((rows, D), low),
            pltpu.VMEM((rows, D), low),
            pltpu.VMEM((FF, D), low),
            pltpu.VMEM((FF, D), low),
            pltpu.VMEM((D, D), low),
            pltpu.VMEM((2 * hidden + 1, rows, D), low),
            pltpu.VMEM((hidden, rows, D), full),
            pltpu.VMEM((rows, D), low),
            pltpu.VMEM((rows, D), full),
            pltpu.VMEM((rows, D), full),
            pltpu.VMEM((rows, D), low),
            pltpu.VMEM((rows, D), low),
            pltpu.VMEM((rows, D), low),
            pltpu.VMEM((rows, D), low),
            pltpu.VMEM((rows, D), full),
            pltpu.VMEM((3, D, rows), low),
            pltpu.VMEM((2 * hidden + 1,) + shape, low),
            pltpu.VMEM((2 * hidden + 1,) + shape, low),
            pltpu.SemaphoreType.DMA((5,)),
            pltpu.SemaphoreType.DMA((moves,)),
            pltpu.SemaphoreType.DMA((3,)),
            pltpu.SemaphoreType.DMA((2 * hidden + 1,)),
            pltpu.SemaphoreType.DMA((2 * hidden + 1,)),
        ],
        compiler_params=pltpu.CompilerParams(vmem_limit_bytes=VMEM_LIMIT),
        cost_estimate=SMALL_COST,
        name="middle",
    )(limit, vectors, tokens, mixed, logs, cot, teach, *arrays)


def fold_block(keep, got, out_keep, out_send, bit, place):
    step = 1 << place
    mine = (lax.axis_index("dp") // bit) % 2 * step
    for j in range(keep.shape[1] // 2):
        base = (j // step) * 2 * step + j % step
        for out, shift in ((out_keep, mine), (out_send, step - mine)):
            value = keep[0, base + shift].astype(full) + got[0, base + shift].astype(full)
            out[0, j] = value.astype(low)


def fold_kernel(bits, places, *refs):
    count = len(bits)
    for n in range(count):
        fold_block(
            *refs[2 * n : 2 * n + 2],
            *refs[2 * count + 2 * n : 2 * count + 2 * n + 2],
            bits[n],
            places[n],
        )


def fold(pairs, bits, places):
    lead = pairs[0][0].shape[0]
    block = lambda shape: pl.BlockSpec((1,) + shape[1:], lambda i: (i, 0, 0, 0))
    halves = [
        (keep.shape[0], keep.shape[1] // 2) + keep.shape[2:] for keep, _ in pairs for _ in range(2)
    ]
    outs = pl.pallas_call(
        functools.partial(fold_kernel, bits, places),
        out_shape=[jax.ShapeDtypeStruct(shape, low) for shape in halves],
        grid=(lead,),
        in_specs=[block(value.shape) for pair in pairs for value in pair],
        out_specs=[block(shape) for shape in halves],
        compiler_params=pltpu.CompilerParams(vmem_limit_bytes=VMEM_LIMIT),
        cost_estimate=pl.CostEstimate(flops=0, bytes_accessed=16 << 20, transcendentals=0),
        name="fold",
    )(*[value for pair in pairs for value in pair])
    return [(outs[2 * n], outs[2 * n + 1]) for n in range(len(pairs))]


def qkv_grad_kernel(count, *refs):
    sources = refs[: 3 * count + 1]
    outs = refs[3 * count + 1 : 3 * count + 5]
    sum_ref, held, turned, total, stage, in_sems, out_sems = refs[3 * count + 5 :]
    first_use = [0, count] + list(range(1, count)) + list(range(count + 1, 3 * count + 1))
    for n in first_use:
        pltpu.make_async_copy(sources[n], held.at[n], in_sems.at[n]).start()

    def wait(n):
        pltpu.make_async_copy(sources[0], held.at[n], in_sems.at[n]).wait()

    def turn(n, _):
        wait(n)
        turned[n] = held[n].T
        return 0

    lax.fori_loop(0, count, turn, 0)
    sum_ref[...] = jnp.zeros_like(sum_ref)

    def step(i, _):
        c = (i + count - 1) // count
        n = jnp.where(i == 0, 0, (i + count - 1) % count)
        wait(count + i)
        right = held[count + i]
        value = dot_of(turned[n], right, 1, 0)
        total[...] = value + jnp.where(n == 0, jnp.zeros_like(value), total[...])

        @pl.when(c != 1)
        def _():
            row = pl.ds(pl.multiple_of(c * 4, 8), 1)
            sum_ref[row, :] += jnp.sum(right.astype(full), axis=0, keepdims=True)

        @pl.when(i % count == 0)
        def _():
            for part in range(2):
                store_split(
                    total[:, part * D // 2 : (part + 1) * D // 2],
                    stage.at[part],
                    stage.at[2 + part],
                    c,
                )
            for k in range(4):
                pltpu.make_async_copy(
                    stage.at[k, c], outs[k].at[c], out_sems.at[k * 3 + c]
                ).start()

        return 0

    lax.fori_loop(0, 2 * count + 1, step, 0)
    for k in range(4):
        for c in range(3):
            pltpu.make_async_copy(stage.at[k, c], outs[k].at[c], out_sems.at[k * 3 + c]).wait()


def qkv_grads(chunks, query_grad, key_grads, value_grads, dp):
    rows = query_grad.shape[0]
    count = len(chunks)
    shape = (3, dp // 2, D // dp, D // 2)
    anywhere = pl.BlockSpec(memory_space=pl.ANY)
    return pl.pallas_call(
        functools.partial(qkv_grad_kernel, count),
        out_shape=[jax.ShapeDtypeStruct(shape, low)] * 4
        + [jax.ShapeDtypeStruct((16, D), full)],
        in_specs=[anywhere] * (3 * count + 1),
        out_specs=[anywhere] * 4 + [pl.BlockSpec(memory_space=pltpu.VMEM)],
        scratch_shapes=[
            pltpu.VMEM((3 * count + 1, rows, D), low),
            pltpu.VMEM((count, D, rows), low),
            pltpu.VMEM((D, D), full),
            pltpu.VMEM((4,) + shape, low),
            pltpu.SemaphoreType.DMA((3 * count + 1,)),
            pltpu.SemaphoreType.DMA((12,)),
        ],
        compiler_params=pltpu.CompilerParams(vmem_limit_bytes=VMEM_LIMIT),
        cost_estimate=SMALL_COST,
        name="qkv_grads",
    )(*chunks, query_grad, *key_grads, *value_grads)


def last_kernel(
    token_ref,
    first_ref,
    right_ref,
    left_ref,
    middle_ref,
    vector_ref,
    gain_ref,
    bias_ref,
    sum_ref,
    out_ref,
    pack_ref,
):
    @pl.when(pl.program_id(0) == 0)
    def _():
        pack_ref[...] = jnp.zeros_like(pack_ref)
        pack_ref[1:2, :] = sum_ref[0:1, :]
        pack_ref[3:4, :] = sum_ref[1:2, :]
        pack_ref[4:5, :] = bias_ref[0:1, :]
        pack_ref[5:6, :] = bias_ref[8:9, :]
        pack_ref[6:8, :] = sum_ref[2:4, :]
        pack_ref[8 : 8 + FF // D, :] = sum_ref[8 : 8 + FF // D, :]

    unit, inverse = norm_stats(token_ref[...].astype(full) + vector_ref[0:1, :])
    grad = first_ref[...] + right_ref[...].astype(full) + left_ref[...].astype(full)
    scaled = grad * gain_ref[0:1, :]
    mean_scaled = jnp.mean(scaled, axis=-1, keepdims=True)
    mean_unit = jnp.mean(scaled * unit, axis=-1, keepdims=True)
    result = middle_ref[...] + inverse * (scaled - mean_scaled - unit * mean_unit)
    out_ref[...] = result
    pack_ref[0:1, :] += jnp.sum(grad * unit, axis=0, keepdims=True)
    pack_ref[2:3, :] += jnp.sum(grad, axis=0, keepdims=True)
    pack_ref[pl.ds(16 + lax.axis_index("dp"), 1), :] += jnp.sum(result, axis=0, keepdims=True)


def last_norm(tokens, first, right, left, middle_grad, vectors, gains, bias_sums, sums, dp):
    rows = tokens.shape[0]
    part = pl.BlockSpec((rows // 4, D), lambda i: (i, 0))
    whole = lambda value: pl.BlockSpec(value.shape, lambda i: (0, 0))
    small = (vectors, gains, bias_sums, sums)
    return pl.pallas_call(
        last_kernel,
        out_shape=(
            jax.ShapeDtypeStruct((rows, D), full),
            jax.ShapeDtypeStruct((16 + dp, D), full),
        ),
        grid=(4,),
        in_specs=[part] * 5 + [whole(value) for value in small],
        out_specs=[part, pl.BlockSpec((16 + dp, D), lambda i: (0, 0))],
        compiler_params=pltpu.CompilerParams(vmem_limit_bytes=VMEM_LIMIT),
        cost_estimate=SMALL_COST,
        name="last_norm",
    )(tokens, first, right, left, middle_grad, *small)


def two_parts(value, axis, mine):
    keep = lax.dynamic_index_in_dim(value, mine, axis, keepdims=False)
    send = lax.dynamic_index_in_dim(value, 1 - mine, axis, keepdims=False)
    return keep, send.astype(low)


class Scatter:
    def __init__(self, parts, turns):
        self.bits = outer_bits()
        half = len(self.bits) // 2
        self.orders = [
            [1] + self.bits[half * (turn % 2) :] + self.bits[: half * (turn % 2)] for turn in turns
        ]
        self.left = [list(self.bits) for _ in turns]
        self.step = 0
        self.parts = parts

    def sends(self):
        return [send for _, send in self.parts]

    def exchange(self, sends):
        self.pairs = [
            (keep, swap(send, "dp", turn[self.step]))
            for (keep, _), send, turn in zip(self.parts, sends, self.orders)
        ]
        self.step += 1

    def folds(self):
        if self.step > len(self.bits):
            return [], [], []
        bits = [turn[self.step] for turn in self.orders]
        places = []
        for left, bit in zip(self.left, bits):
            places.append(left.index(bit))
            left.remove(bit)
        return self.pairs, bits, places

    def give(self, outs):
        self.parts = [(outs[n], outs[n + 1]) for n in range(0, len(outs), 2)]

    def fold(self):
        outs = []
        for pair, bit, at in zip(*self.folds()):
            outs += fold([pair], [bit], [at])[0]
        self.give(outs)

    def advance(self, order):
        sends = order(*self.sends())
        self.exchange(list(sends) if len(self.parts) > 1 else [sends])

    def finish(self, order):
        while self.step <= len(self.bits):
            self.fold()
            self.advance(order)
        got = order(*[other for _, other in self.pairs])
        return [
            (keep.astype(full) + other.astype(full))[:, 0]
            for (keep, _), other in zip(self.pairs, got)
        ]


def scatter_dp(parts, turns):
    scatter = Scatter(parts, turns)
    while True:
        sends = yield scatter.sends()
        scatter.exchange(sends)
        if scatter.step > len(scatter.bits):
            break
        scatter.parts = fold(*scatter.folds())
    got = yield [other for _, other in scatter.pairs]
    return [
        (keep.astype(full) + other.astype(full))[:, 0]
        for (keep, _), other in zip(scatter.pairs, got)
    ]


def scatter_mp(value):
    rank = lax.axis_index("mp")
    part = lambda index: lax.dynamic_index_in_dim(value, index, keepdims=False)
    sends = yield [part(rank ^ bit).astype(low) for bit in (1, 2, 3)]
    got = yield [swap(send, "mp", bit) for bit, send in zip((1, 2, 3), sends)]
    got = [other.astype(full) for other in got]
    return (part(rank) + got[0]) + (got[1] + got[2])


def halve_mp(value):
    rank = lax.axis_index("mp")
    pairs = value.reshape((2, 2) + value.shape[1:])
    keep, send = two_parts(pairs, 1, rank % 2)
    (send,) = yield [send]
    (got,) = yield [swap(send, "mp", 1)]
    keep, send = two_parts(keep.astype(full) + got.astype(full), 0, rank // 2)
    (send,) = yield [send]
    (got,) = yield [swap(send, "mp", 2)]
    return keep + got.astype(full)


def scatter_feed(up_own, down_own):
    mp = lax.axis_size("mp")
    block = down_own.shape[1]
    out_own = up_own[mp].reshape(block, mp, -1).transpose(1, 0, 2)
    own = yield from halve_mp(
        jnp.concatenate([up_own[:mp], down_own, out_own.reshape(mp, -1, D)], axis=1)
    )
    return own[:block], own[block : 2 * block].T, own[2 * block :].reshape(block, -1).T


def scatter_qkv(keep_left, keep_right, send_left, send_right):
    left_part, right_part = yield from scatter_dp(
        [(keep_left, send_left), (keep_right, send_right)], (0, 1)
    )
    width = D // lax.axis_size("mp")
    parts = [part[..., at : at + width] for part in (left_part, right_part) for at in (0, width)]
    return (yield from scatter_mp(jnp.stack(parts)))


def sum_small(value):
    (value,) = yield [value]
    value = value + swap(value, "dp", 1)
    bits = outer_bits()
    groups = [("dp", bits[n : n + 2]) for n in range(0, len(bits), 2)] + [("mp", [1, 2])]
    for axis, pair in groups:
        (value,) = yield [value]
        if len(pair) == 1:
            value = value + swap(value, axis, pair[0])
        else:
            one, two = pair
            got = [swap(value, axis, mask) for mask in (one, two, one + two)]
            if axis == "mp":
                got = yield got
            value = (value + got[0]) + (got[1] + got[2])
    return value


class Steps:
    def __init__(self, steps):
        self.steps = steps
        self.pending = next(steps)
        self.result = None

    def advance(self, order):
        if self.pending is None:
            return
        sends = order(*self.pending)
        sends = [sends] if len(self.pending) == 1 else list(sends)
        try:
            self.pending = self.steps.send(sends)
        except StopIteration as stop:
            self.pending = None
            self.result = stop.value

    def finish(self, order):
        while self.pending is not None:
            self.advance(order)
        return self.result


def shards(
    tokens_in,
    timesteps,
    lengths,
    time_table,
    norm_gains,
    norm_biases,
    w_qkv,
    qv_bias,
    w_out,
    out_bias,
    w_up,
    up_bias,
    w_down,
    down_bias,
    cotangent,
    teacher,
):
    rank = lax.axis_index("mp")
    data_rank = lax.axis_index("dp")
    mp = lax.axis_size("mp")
    dp = lax.axis_size("dp")
    own_rows = tokens_in.shape[0]
    length = lax.dynamic_index_in_dim(lengths, data_rank, keepdims=False)
    own_time = lax.dynamic_index_in_dim(timesteps, data_rank, keepdims=False)
    odd = rank % 2 == 1
    upper = rank >= 2
    middle = jnp.logical_or(rank == 1, rank == 2)
    order = Order()
    along = lambda value, pairs: lax.ppermute(value, "mp", pairs)

    block = w_qkv.shape[1]
    aligned = block % 32 == 0
    narrow = order(jnp.concatenate([w_qkv.reshape(3 * block, -1), w_out.T]))
    first_swap = swap(narrow, "mp", 1)
    tall = order(jnp.concatenate([w_up, w_down.T]))
    tall_swap = swap(tall, "mp", 1)
    pair = order(
        jnp.concatenate(
            [jnp.where(odd, first_swap, narrow), jnp.where(odd, narrow, first_swap)], axis=1
        )
    )
    second_swap = swap(pair, "mp", 2)
    tokens, lengths, own_time, norm_gains, norm_biases, out_bias, down_bias, up_bias, length = order(
        tokens_in, lengths, own_time, norm_gains, norm_biases, out_bias, down_bias, up_bias, length
    )
    table_row = lax.dynamic_slice_in_dim(time_table, own_time, 1).astype(full)
    unit_one, _ = norm_stats(tokens.astype(full) + table_row)
    first_norm = (unit_one * norm_gains[0] + norm_biases[0]).astype(low)
    loss_weight = lengths.shape[0] * MAXLEN / jnp.sum(lengths).astype(full)
    vectors = jnp.concatenate(
        [
            table_row,
            out_bias[None],
            norm_gains[1:2],
            norm_biases[1:2],
            down_bias[None],
            jnp.full((3, D), loss_weight),
            up_bias.reshape(-1, D),
            jnp.zeros((4, D), full),
        ]
    )
    scalars = jnp.stack(
        [
            rank,
            jnp.where(rank == 0, 1, rank - 1),
            jnp.where(upper, rank - 2, rank + 2),
            jnp.where(middle, rank + 1, 3 - rank),
            length,
            length - rank * own_rows,
        ]
    ).astype(jnp.int32)
    first_norm, vectors, scalars = order(first_norm, vectors, scalars)
    wide = jnp.concatenate(
        [jnp.where(upper, second_swap, pair), jnp.where(upper, pair, second_swap)], axis=1
    )
    qkv_rows, out_rows = wide[: 3 * block], wide[3 * block :]
    if aligned:
        split = 3 * block // 2
        qkv_gather = Gather([qkv_rows[:split], qkv_rows[split:]])
        qkv_gather.advance(order)
    tall = order(jnp.concatenate([tall, tall_swap]))
    tall_across = along(tall, [(1, 2), (2, 1)])

    sent = order(first_norm)
    from_left = along(sent, [(0, 1), (1, 2), (2, 3)])
    from_right = along(sent, [(1, 0), (2, 1), (3, 2)])
    tall_across = order(tall_across)
    tall_far = along(tall_across, [(1, 0), (2, 3)])
    if aligned:
        while qkv_gather.step < len(qkv_gather.bits):
            qkv_gather.advance(order)
        qkv_gather.advance(order)
    hop_right, hop_left = order(from_left, from_right)
    second_right = along(hop_right, [(1, 2), (2, 3)])
    second_left = along(hop_left, [(1, 0), (2, 1)])
    if aligned:
        arrays, plan = plan_of(
            qkv_gather.result,
            [
                [(0, block, 0, 0, 0, 0), (block, split - block, 1, 0, 0, 0)],
                [
                    (0, 2 * block - split, 1, 0, 0, split - block),
                    (2 * block - split, block, 1, 1, 0, 0),
                ],
            ],
        )
        query_weight, pair_weight = order(*place(arrays, plan, block, [(D, D), (D, 2 * D)]))
        tall_other = jnp.where(middle, tall_across, order(tall_far))
        feed_gather = Gather(
            [
                jnp.concatenate([tall, out_rows[: block // 2]]),
                jnp.concatenate([tall_other, out_rows[block // 2 :]]),
            ]
        )
        feed_gather.advance(order)
    else:
        weights = lax.all_gather(qkv_rows.reshape(3, block, D), "dp", axis=1, tiled=True)
        query_weight = weights[0]
        pair_weight = jnp.concatenate([weights[1], weights[2]], axis=1)
    near = jnp.where(rank == 0, hop_left, hop_right)
    attend = lambda parts, numbers, carried: order(
        *attend_forward(
            parts,
            numbers,
            scalars,
            query_weight,
            pair_weight,
            qv_bias[0:1],
            qv_bias[1:2],
            carried,
        )
    )
    key_own, value_own, queries, *state = attend([order(first_norm)], (0,), None)
    second_right, second_left = order(second_right, second_left)
    second = order(jnp.where(upper, second_right, second_left))
    third = along(second, [(1, 0), (2, 3)])
    if aligned:
        while feed_gather.step < len(feed_gather.bits):
            feed_gather.advance(order)
    near, second = order(near, second)
    key_near, key_second, value_near, value_second, *state = attend(
        [near, second], (1, 2), (queries, *state)
    )
    last = order(jnp.where(middle, hop_left, order(third)))
    if aligned:
        feed_gather.advance(order)
    key_last, value_last, mixed, logs = attend([order(last)], (3,), (queries, *state))
    if aligned:
        layout = lambda masks, shift: [
            (0, block, 0, masks[0], D, 0),
            (block, block, 1, masks[0], D, 0),
            (2 * block, block, 0, masks[1], D, 0),
            (3 * block, block, 1, masks[1], D, 0),
            (4 * block, block // 2, 2, 0, 0, shift),
        ]
        arrays, plan = plan_of(
            feed_gather.result, [layout((0, 1), 0), layout((2, 3), block // 2)]
        )
    else:
        arrays = [
            lax.all_gather(w_up, ("mp", "dp"), axis=0, tiled=True),
            lax.all_gather(w_down.T, ("mp", "dp"), axis=0, tiled=True),
            lax.all_gather(out_rows, "dp", axis=0, tiled=True),
        ]
        plan = [[(0, array.shape[0], n, None, 0, 0, 0)] for n, array in enumerate(arrays)]
    chunks = [first_norm, near, second, last]
    keys = [key_own, key_near, key_second, key_last]
    values = [value_own, value_near, value_second, value_last]

    output, middle_grad, attended_grad, *parts, deltas, log_rows, sums = middle_call(
        scalars, vectors, tokens, mixed, logs, cotangent, teacher, arrays, plan, block, dp
    )
    scatter = Scatter([(parts[0], parts[1]), (parts[2], parts[3])], (1, 0))
    scatter.advance(order)

    key_grads = [None] * 4
    value_grads = [None] * 4
    firsts = [None] * 4
    query_grad = None
    for n in (3, 2, 1, 0):
        pairs, bits, places = scatter.folds() if n % 2 == 0 else ([], [], [])
        query_grad, key_grads[n], value_grads[n], firsts[n], *folded = attend_backward(
            n,
            queries,
            keys[n],
            values[n],
            order(attended_grad),
            log_rows,
            deltas,
            query_weight,
            pair_weight,
            scalars,
            query_grad,
            n == 0,
            pairs,
            bits,
            places,
        )
        firsts[n] = order(firsts[n])
        if folded:
            scatter.give(folded)
        if n == 3:
            back_last = along(firsts[3], [(0, 1), (3, 2)]).astype(full)
        elif n == 2:
            scatter.advance(order)
            payload = order((firsts[2] + back_last).astype(low))
            back_right = along(payload, [(0, 1), (1, 2)]).astype(full)
            back_left = along(payload, [(3, 2), (2, 1)]).astype(full)
        elif n == 1:
            to_right = jnp.where(
                rank == 0, firsts[1], firsts[3].astype(full) + back_right
            ).astype(low)
            to_left = (firsts[1] + back_left).astype(low)
            to_right, to_left = order(to_right, to_left)
            final_right = along(to_right, [(0, 1), (1, 2), (2, 3)])
            final_left = along(to_left, [(3, 2), (2, 1), (1, 0)])
    scatter.advance(order)
    query_grad, final_right, final_left = order(query_grad, final_right, final_left)
    *halves, bias_sums = qkv_grads(chunks, query_grad, key_grads, value_grads, dp)
    qkv = Steps(scatter_qkv(*halves))
    qkv.advance(order)
    down_own, up_own = scatter.finish(order)
    feed = Steps(scatter_feed(up_own, down_own))
    feed.advance(order)
    qkv.advance(order)
    tokens, first_own = order(tokens, firsts[0])
    input_grad, packed = last_norm(
        tokens,
        first_own,
        final_right,
        final_left,
        middle_grad,
        vectors,
        norm_gains,
        bias_sums,
        sums,
        dp,
    )
    packed, input_grad = order(packed, input_grad)
    small = Steps(sum_small(packed))
    feed.advance(order)
    feed.advance(order)
    small.advance(order)
    qkv.advance(order)
    qkv.advance(order)
    small.advance(order)
    qkv.advance(order)
    small.advance(order)
    feed.advance(order)
    total = small.finish(order)
    qkv_grad = qkv.finish(order)
    up_grad, down_grad, out_grad = feed.finish(order)
    fixed = 16
    chosen = (timesteps[None, :] == jnp.arange(time_table.shape[0])[:, None]).astype(full)
    table_grad = lax.dot_general(
        chosen,
        total[fixed:],
        (((1,), (0,)), ((), ())),
        precision=lax.Precision.HIGHEST,
        preferred_element_type=full,
    )
    return (
        output,
        input_grad,
        table_grad,
        total[0:2],
        total[2:4],
        qkv_grad,
        total[4:6],
        out_grad,
        total[6],
        up_grad,
        total[8 : 8 + FF // D].reshape(FF),
        down_grad,
        total[7],
    )


def solution(mesh):
    rows = P(both, None)
    placed = (
        rows,
        P(),
        P(),
        P(),
        P(),
        P(),
        P(None, "dp", "mp"),
        P(),
        P("mp", "dp"),
        P(),
        P("dp", "mp"),
        P(),
        P("mp", "dp"),
        P(),
        rows,
        rows,
    )
    return jax.shard_map(
        shards,
        mesh=mesh,
        in_specs=placed,
        out_specs=(
            rows,
            rows,
            P(),
            P(),
            P(),
            P(None, "dp", "mp"),
            P(),
            P("mp", "dp"),
            P(),
            P("dp", "mp"),
            P(),
            P("mp", "dp"),
            P(),
        ),
        check_vma=False,
    )
```

```python
import functools

import jax
import jax.numpy as jnp
from jax import lax
from jax.experimental import pallas as pl
from jax.experimental.pallas import tpu as pltpu
from jax.sharding import PartitionSpec as P

D = 768
HEADS = 12
HEAD_DIM = 64
FF = 3072
MAXLEN = 2048
PAIR = 2 * HEAD_DIM
PAIRS = HEADS // 2
VMEM_LIMIT = 58 << 20
SMALL_COST = pl.CostEstimate(flops=1 << 20, bytes_accessed=1 << 16, transcendentals=0)

far_below = -1e30
epsilon = 1e-05
score_scale = HEAD_DIM ** (-0.5)
low = jnp.bfloat16
full = jnp.float32
both = ("dp", "mp")


def norm_stats(values):
    center = values - jnp.mean(values, axis=-1, keepdims=True)
    spread = jnp.mean(center * center, axis=-1, keepdims=True)
    inverse = lax.rsqrt(spread + epsilon)
    return center * inverse, inverse


def dot_of(left_side, right_side, left_dim, right_dim):
    return lax.dot_general(
        left_side,
        right_side,
        (((left_dim,), (right_dim,)), ((), ())),
        preferred_element_type=full,
    )


def first_half(shape):
    return lax.broadcasted_iota(jnp.int32, shape, len(shape) - 1) < HEAD_DIM


def forward_kernel(numbers, first, final, scalars, *refs):
    count = len(numbers)
    chunk_refs = refs[:count]
    wk_ref, wv_ref, value_bias_ref = refs[count : count + 3]
    refs = refs[count + 3 :]
    if first:
        wq_ref, query_bias_ref = refs[:2]
        key_outs, value_outs = refs[2 : 2 + count], refs[2 + count : 2 + 2 * count]
        query_out, top_ref, sum_ref, acc_ref = refs[2 + 2 * count :]
        q_pair = (dot_of(chunk_refs[0][...], wq_ref[...], 1, 0) + query_bias_ref[...]).astype(low)
        q_pair = q_pair * jnp.asarray(score_scale, low)
        query_out[...] = q_pair
    else:
        q_ref, top_in, sum_in, acc_in = refs[:4]
        key_outs, value_outs = refs[4 : 4 + count], refs[4 + count : 4 + 2 * count]
        results = refs[4 + 2 * count :]
        q_pair = q_ref[...]
    weight = jnp.concatenate([wk_ref[...], wv_ref[...]], axis=1)
    keys = []
    values = []
    for n in range(count):
        both_parts = dot_of(chunk_refs[n][...], weight, 1, 0)
        keys.append(both_parts[:, :PAIR].astype(low))
        values.append((both_parts[:, PAIR:] + value_bias_ref[...]).astype(low))
        key_outs[n][...] = keys[n]
        value_outs[n][...] = values[n]
    rows = q_pair.shape[0]
    size = keys[0].shape[0]
    place = lax.broadcasted_iota(jnp.int32, (1, size), 1)
    lower = first_half((rows, PAIR))
    parts = []
    for half in range(2):
        kept = lower if half == 0 else jnp.logical_not(lower)
        q_half = jnp.where(kept, q_pair, jnp.zeros_like(q_pair))
        scores = []
        for n in range(count):
            bias = jnp.where(place + scalars[numbers[n]] * size < scalars[4], 0.0, far_below)
            scores.append(dot_of(q_half, keys[n], 1, 1) + bias)
        highest = functools.reduce(
            jnp.maximum, [jnp.max(score, axis=-1, keepdims=True) for score in scores]
        )
        totals = jnp.zeros_like(highest)
        mixed = jnp.zeros((rows, PAIR), full)
        for n in range(count):
            exp_scores = jnp.exp(scores[n] - highest)
            totals = totals + jnp.sum(exp_scores, axis=-1, keepdims=True)
            mixed = mixed + dot_of(exp_scores.astype(low), values[n], 1, 0)
        parts.append((highest, totals, mixed))
    top = jnp.where(lower, parts[0][0], parts[1][0])
    total = jnp.where(lower, parts[0][1], parts[1][1])
    mixed = jnp.where(lower, parts[0][2], parts[1][2])
    if first:
        top_ref[...] = top
        sum_ref[...] = total
        acc_ref[...] = mixed
    else:
        highest = jnp.maximum(top, top_in[...])
        here = jnp.exp(top - highest)
        before = jnp.exp(top_in[...] - highest)
        total = total * here + sum_in[...] * before
        mixed = mixed * here + acc_in[...] * before
        if final:
            results[0][...] = mixed / total
            results[1][...] = highest + jnp.log(total)
        else:
            results[0][...] = highest
            results[1][...] = total
            results[2][...] = mixed


def attend_forward(chunks, numbers, scalars, query_weight, pair_weight, query_bias, value_bias, carried):
    rows = chunks[0].shape[0]
    count = len(chunks)
    first = carried is None
    final = 3 in numbers
    column = lambda height, c: pl.BlockSpec((height, PAIR), lambda i, n: (0, c * PAIRS + i))
    whole = pl.BlockSpec((rows, D), lambda i, n: (0, 0))
    wide = jax.ShapeDtypeStruct((rows, D), full)
    narrow = jax.ShapeDtypeStruct((rows, D), low)
    extra = (query_weight, query_bias) if first else carried
    results = (narrow,) * first + (wide,) * (2 if final else 3)
    return pl.pallas_call(
        functools.partial(forward_kernel, numbers, first, final),
        out_shape=(narrow,) * (2 * count) + results,
        grid_spec=pltpu.PrefetchScalarGridSpec(
            num_scalar_prefetch=1,
            grid=(PAIRS,),
            in_specs=[whole] * count
            + [column(D, 0), column(D, 1), column(1, 0)]
            + ([column(D, 0), column(1, 0)] if first else [column(rows, 0)] * 4),
            out_specs=[column(rows, 0)] * (2 * count + len(results)),
        ),
        compiler_params=pltpu.CompilerParams(vmem_limit_bytes=VMEM_LIMIT),
        cost_estimate=SMALL_COST,
        name="attend_forward",
    )(scalars, *chunks, pair_weight, pair_weight, value_bias, *extra)


def backward_kernel(
    number,
    first,
    last,
    folds,
    scalars,
    q_ref,
    k_ref,
    v_ref,
    g_ref,
    log_ref,
    delta_ref,
    wk_ref,
    wv_ref,
    *refs
):
    if last:
        wq_ref = refs[0]
        refs = refs[1:]
    if not first:
        dq_in = refs[0]
        refs = refs[1:]
    count = len(folds)
    fold_ins, refs = refs[: 2 * count], refs[2 * count :]
    dq_ref, dk_ref, dv_ref, back_ref = refs[:4]
    fold_outs, accum = refs[4:-1], refs[-1]
    step = pl.program_id(0)
    for n, (lead, bit, at) in enumerate(folds):

        @pl.when(step < lead)
        def _():
            fold_block(
                *fold_ins[2 * n : 2 * n + 2], *fold_outs[2 * n : 2 * n + 2], bit, at
            )

    rows = q_ref.shape[0]
    keys = k_ref.shape[0]
    limit = scalars[4] - scalars[number] * keys
    q_pair = q_ref[...]
    g_pair = g_ref[...]
    k_pair = k_ref[...]
    v_pair = v_ref[...]
    lower = first_half((rows, PAIR))
    nothing = jnp.zeros((rows, PAIR), low)
    two_halves = lambda pair: jnp.concatenate(
        [jnp.where(lower, pair, nothing), jnp.where(lower, nothing, pair)]
    )
    queries = two_halves(q_pair)
    grads_out = two_halves(g_pair)
    row_of = lambda ref: jnp.concatenate([ref[0, 0:1, :], ref[0, 1:2, :]], axis=1)
    place = lax.broadcasted_iota(jnp.int32, (keys, 1), 0)
    bias = jnp.where(place < limit, 0.0, far_below)
    scores = dot_of(k_pair, queries, 1, 1) + bias
    prob_grad = dot_of(v_pair, grads_out, 1, 1)
    probs = jnp.exp(scores - row_of(log_ref))
    score_grad = (probs * (prob_grad - row_of(delta_ref))).astype(low)
    dv_low = dot_of(probs.astype(low), grads_out, 1, 0).astype(low)
    dk_low = dot_of(score_grad, queries, 1, 0).astype(low)
    turned = dot_of(k_pair.T, score_grad, 1, 0)
    upper_rows = lax.broadcasted_iota(jnp.int32, (PAIR, rows), 0) < HEAD_DIM
    dk_ref[...] = dk_low
    dv_ref[...] = dv_low
    grads = [dk_low, dv_low]
    weights = [wk_ref[...], wv_ref[...]]
    dq_all = jnp.where(upper_rows, turned[:, :rows], turned[:, rows:]).T
    if not first:
        dq_all = dq_all + dq_in[...]
    back = dot_of(jnp.concatenate(grads, axis=1), jnp.concatenate(weights, axis=1), 1, 1)
    if last:
        dq_low = (dq_all * score_scale).astype(low)
        dq_ref[...] = dq_low
        back = back + dot_of(dq_low, wq_ref[...], 1, 1)
    else:
        dq_ref[...] = dq_all

    @pl.when(step == 0)
    def _():
        accum[...] = back

    @pl.when(step > 0)
    def _():
        accum[...] += back

    @pl.when(step == PAIRS - 1)
    def _():
        back_ref[...] = accum[...].astype(back_ref.dtype)


def attend_backward(
    number,
    queries,
    keys,
    values,
    grads,
    logs,
    deltas,
    query_weight,
    pair_weight,
    scalars,
    carried,
    last,
    pairs,
    bits,
    places,
):
    rows, total = queries.shape[0], keys.shape[0]
    first = carried is None
    folds = [(keep.shape[0], bit, at) for (keep, _), bit, at in zip(pairs, bits, places)]
    halves = [
        (keep.shape[0], keep.shape[1] // 2) + keep.shape[2:] for keep, _ in pairs for _ in range(2)
    ]

    def by_lead(shape):
        end = shape[0] - 1
        return pl.BlockSpec((1,) + shape[1:], lambda i, n: (jnp.minimum(i, end), 0, 0, 0))

    column = lambda count, c: pl.BlockSpec((count, PAIR), lambda i, n: (0, c * PAIRS + i))
    stats = pl.BlockSpec((1, 2, rows), lambda i, n: (i, 0, 0))
    extra = (query_weight,) * last + (() if first else (carried,))
    extra_specs = [column(D, 0)] * last + ([] if first else [column(rows, 0)])
    return pl.pallas_call(
        functools.partial(backward_kernel, number, first, last, folds),
        out_shape=(
            jax.ShapeDtypeStruct((rows, D), low if last else full),
            jax.ShapeDtypeStruct((total, D), low),
            jax.ShapeDtypeStruct((total, D), low),
            jax.ShapeDtypeStruct((total, D), low if first else full),
            *[jax.ShapeDtypeStruct(shape, low) for shape in halves],
        ),
        grid_spec=pltpu.PrefetchScalarGridSpec(
            num_scalar_prefetch=1,
            grid=(PAIRS,),
            in_specs=[
                column(rows, 0),
                column(total, 0),
                column(total, 0),
                column(rows, 0),
                stats,
                stats,
                column(D, 0),
                column(D, 1),
            ]
            + extra_specs
            + [by_lead(value.shape) for pair in pairs for value in pair],
            out_specs=[
                column(rows, 0),
                column(total, 0),
                column(total, 0),
                pl.BlockSpec((total, D), lambda i, n: (0, 0)),
            ]
            + [by_lead(shape) for shape in halves],
            scratch_shapes=[pltpu.VMEM((total, D), full)],
        ),
        compiler_params=pltpu.CompilerParams(vmem_limit_bytes=VMEM_LIMIT),
        cost_estimate=SMALL_COST,
        name="attend_backward",
    )(
        scalars,
        queries,
        keys,
        values,
        grads,
        logs,
        deltas,
        pair_weight,
        pair_weight,
        *extra,
        *[value for pair in pairs for value in pair],
    )


def swap(value, axis, bit):
    count = lax.axis_size(axis)
    return lax.ppermute(value, axis, [(i, i ^ bit) for i in range(count)])


class Order:
    def __init__(self):
        self.marks = ()

    def __call__(self, *values):
        values = lax.optimization_barrier(values + self.marks)[: len(values)]
        self.marks = values
        return values[0] if len(values) == 1 else values


def outer_bits():
    bits = []
    bit = 2
    while bit < lax.axis_size("dp"):
        bits.append(bit)
        bit *= 2
    return bits


class Gather:
    def __init__(self, parts):
        self.bits = outer_bits()
        half = len(self.bits) // 2
        self.orders = [
            self.bits[half * (n % 2) :] + self.bits[: half * (n % 2)] for n in range(len(parts))
        ]
        self.result = [[([0], part)] for part in parts]
        self.step = 0
        self.early = []

    def advance(self, order):
        held = self.result
        if self.step < len(self.bits):
            masks = [[m for mask, _ in pieces for m in mask] for pieces in held]
            blocks = [
                jnp.concatenate([array for _, array in pieces]) if self.step else pieces[0][1]
                for pieces in held
            ]
            blocks = order(*blocks)
            bits = [turn[self.step] for turn in self.orders]
            self.result = [
                [(mask, block), ([m ^ bit for m in mask], swap(block, "dp", bit))]
                for mask, block, bit in zip(masks, blocks, bits)
            ]
        else:
            rest = [pieces[1:] if self.early else pieces for pieces in held]
            arrays = iter(order(*[array for pieces in rest for _, array in pieces]))
            self.result = []
            for n, pieces in enumerate(rest):
                kept = [(masks, next(arrays)) for masks, _ in pieces]
                ours = held[n][:1] + kept if self.early else kept
                theirs = [([m ^ 1 for m in masks], swap(array, "dp", 1)) for masks, array in kept]
                self.result.append(ours + self.early[n : n + 1] + theirs)
        self.step += 1

    def send_early(self, order):
        arrays = order(*[pieces[0][1] for pieces in self.result])
        self.early = [
            ([m ^ 1 for m in pieces[0][0]], swap(array, "dp", 1))
            for pieces, array in zip(self.result, arrays)
        ]


def canonical_row(me, rank, block, mask, rank_mask, stride, offset):
    if mask is None:
        return offset
    row = (me ^ mask) * block + offset
    if stride:
        if rank_mask >= 2:
            rank_mask = rank_mask ^ ((rank + 1) // 2 % 2)
        row = row + (rank ^ rank_mask) * stride
    return pl.multiple_of(row, 16)


def place_kernel(plan, block, *refs):
    count = len(plan)
    ins = refs[:count]
    outs = refs[count:-1]
    sems = refs[-1]
    me = lax.axis_index("dp")
    rank = lax.axis_index("mp")
    copies = []
    for ref, moves in zip(ins, plan):
        for start, size, which, mask, column, _, offset in moves:
            row = canonical_row(me, rank, block, mask, 0, 0, offset)
            copy = pltpu.make_async_copy(
                ref.at[pl.ds(start, size), :],
                outs[which].at[pl.ds(row, size), pl.ds(column * D, D)],
                sems.at[len(copies)],
            )
            copy.start()
            copies.append(copy)
    for copy in copies:
        copy.wait()


def plan_of(gathered, layouts):
    arrays = []
    plan = []
    for pieces, layout in zip(gathered, layouts):
        rows = sum(size for _, size, *_ in layout)
        for masks, array in pieces:
            moves = []
            for j, mask in enumerate(masks):
                for start, size, which, rank_mask, stride, offset in layout:
                    moves.append((j * rows + start, size, which, mask, rank_mask, stride, offset))
            arrays.append(array)
            plan.append(moves)
    return arrays, plan


def place(arrays, plan, block, shapes):
    return pl.pallas_call(
        functools.partial(place_kernel, plan, block),
        out_shape=[jax.ShapeDtypeStruct(shape, low) for shape in shapes],
        in_specs=[pl.BlockSpec(memory_space=pl.ANY)] * len(arrays),
        out_specs=[pl.BlockSpec(memory_space=pltpu.VMEM)] * len(shapes),
        scratch_shapes=[pltpu.SemaphoreType.DMA((sum(len(moves) for moves in plan),))],
        compiler_params=pltpu.CompilerParams(vmem_limit_bytes=VMEM_LIMIT),
        cost_estimate=SMALL_COST,
        name="place",
    )(*arrays)


def store_split(value, keep, send, index):
    block = keep.shape[2]
    even = lax.axis_index("dp") % 2 == 0
    for outer in range(keep.shape[1]):
        first = value[2 * outer * block : (2 * outer + 1) * block]
        other = value[(2 * outer + 1) * block : (2 * outer + 2) * block]
        keep[index, outer] = jnp.where(even, first, other).astype(low)
        send[index, outer] = jnp.where(even, other, first).astype(low)


def middle_kernel(plan, block, total, *refs):
    limit_ref, vector_ref = refs[:2]
    token_hbm, mixed_hbm, log_hbm, cot_hbm, teach_hbm = refs[2:7]
    pieces = refs[7 : 7 + total]
    (
        out_hbm,
        middle_hbm,
        grad_hbm,
        down_keep,
        down_send,
        up_keep,
        up_send,
        delta_ref,
        log_ref,
        sum_ref,
    ) = refs[7 + total : 17 + total]
    (
        token,
        mixed,
        logs,
        cot,
        teach,
        up,
        down,
        proj,
        right,
        slope,
        second,
        middle,
        final,
        out,
        final_low,
        middle_low,
        grad,
        accum,
        turned,
        stage_keep,
        stage_send,
        in_sems,
        weight_sems,
        out_sems,
        keep_sems,
        send_sems,
    ) = refs[17 + total :]
    hidden = FF // D
    targets = (up, down, proj)
    rows = token.shape[0]
    me = lax.axis_index("dp")
    rank = lax.axis_index("mp")

    def fetch(ref, scratch, n):
        copy = pltpu.make_async_copy(ref, scratch, in_sems.at[n])
        copy.start()
        return copy

    def send(scratch, ref, n):
        copy = pltpu.make_async_copy(scratch, ref, out_sems.at[n])
        copy.start()
        return copy

    gets = [
        fetch(token_hbm, token, 0),
        fetch(mixed_hbm, mixed, 1),
        fetch(log_hbm, logs, 2),
        fetch(cot_hbm, cot, 3),
        fetch(teach_hbm, teach, 4),
    ]
    loads = {0: [], 1: [], 2: []}
    number = 0
    for want in (2, 0, 1):
        for ref, moves in zip(pieces, plan):
            for start, size, which, mask, rank_mask, stride, offset in moves:
                if which != want:
                    continue
                row = canonical_row(me, rank, block, mask, rank_mask, stride, offset)
                copy = pltpu.make_async_copy(
                    ref.at[pl.ds(start, size), :],
                    targets[which].at[pl.ds(row, size), :],
                    weight_sems.at[number],
                )
                copy.start()
                loads[which].append(copy)
                number += 1

    table_row = vector_ref[0:1, :]
    out_bias = vector_ref[1:2, :]
    gain = vector_ref[2:3, :]
    shift = vector_ref[3:4, :]
    down_bias = vector_ref[4:5, :]
    weight = vector_ref[5:6, :]
    gets[0].wait()
    gets[1].wait()
    right[2 * hidden] = mixed[...].astype(low)
    for copy in loads[2]:
        copy.wait()
    state = token[...].astype(full) + table_row + out_bias
    state = state + dot_of(right[2 * hidden], proj[...], 1, 1)
    middle[...] = state
    unit, _ = norm_stats(state)
    second[...] = (unit * gain + shift).astype(low)
    accum[...] = jnp.zeros((rows, D), full)
    for copy in loads[0]:
        copy.wait()
    for copy in loads[1]:
        copy.wait()

    def forward(m, _):
        place = pl.ds(pl.multiple_of(m * D, D), D)
        value = dot_of(second[...], up[place, :], 1, 0) + vector_ref[pl.ds(8 + m, 1), :]
        cumulative = 0.5 + 0.5 * lax.erf(value * (0.5**0.5))
        right[m] = (value * cumulative).astype(low)
        slope[m] = cumulative + value * jnp.exp(-0.5 * value * value) * 0.3989422804014327
        accum[...] += dot_of(right[m], down[place, :], 1, 1)
        return 0

    lax.fori_loop(0, FF // D, forward, 0)
    final_state = middle[...] + accum[...] + down_bias
    out[...] = final_state.astype(low)
    puts = [send(out, out_hbm, 0)]
    gets[3].wait()
    gets[4].wait()
    place = lax.broadcasted_iota(jnp.int32, (rows, 1), 0)
    grads = cot[...].astype(full) + weight * (final_state - teach[...].astype(full))
    grads = jnp.where(place < limit_ref[5], grads, 0.0)
    final[...] = grads
    final_low[...] = grads.astype(low)
    sum_ref[3:4, :] = jnp.sum(grads, axis=0, keepdims=True)
    accum[...] = jnp.zeros((rows, D), full)

    def backward(m, _):
        place = pl.ds(pl.multiple_of(m * D, D), D)
        value = slope[m] * dot_of(final_low[...], down[place, :], 1, 0)
        value = value.astype(low)
        right[hidden + m] = value
        sum_ref[pl.ds(8 + m, 1), :] = jnp.sum(value.astype(full), axis=0, keepdims=True)
        accum[...] += dot_of(value, up[place, :], 1, 1)
        return 0

    lax.fori_loop(0, FF // D, backward, 0)
    unit, inverse = norm_stats(middle[...])
    second_grad = accum[...]
    sum_ref[0:1, :] = jnp.sum(second_grad * unit, axis=0, keepdims=True)
    sum_ref[1:2, :] = jnp.sum(second_grad, axis=0, keepdims=True)
    scaled = second_grad * gain
    mean_scaled = jnp.mean(scaled, axis=-1, keepdims=True)
    mean_unit = jnp.mean(scaled * unit, axis=-1, keepdims=True)
    total_grad = final[...] + inverse * (scaled - mean_scaled - unit * mean_unit)
    middle[...] = total_grad
    puts.append(send(middle, middle_hbm, 1))
    middle_low[...] = total_grad.astype(low)
    sum_ref[2:3, :] = jnp.sum(total_grad, axis=0, keepdims=True)
    attended_grad = dot_of(middle_low[...], proj[...], 1, 0).astype(low)
    grad[...] = attended_grad
    puts.append(send(grad, grad_hbm, 2))
    gets[2].wait()
    head = lax.broadcasted_iota(jnp.int32, (16, D), 0)
    lane = lax.broadcasted_iota(jnp.int32, (16, D), 1)
    member = jnp.where(lane // HEAD_DIM == head, 1.0, 0.0)
    leader = jnp.where(lane == head * HEAD_DIM, 1.0, 0.0)
    exact = functools.partial(
        lax.dot_general,
        dimension_numbers=(((1,), (1,)), ((), ())),
        precision=lax.Precision.HIGHEST,
        preferred_element_type=full,
    )
    deltas = exact(member, attended_grad.astype(full) * mixed[...])
    tops = exact(leader, logs[...])
    for pair in range(PAIRS):
        delta_ref[pair] = deltas[2 * pair : 2 * pair + 2]
        log_ref[pair] = tops[2 * pair : 2 * pair + 2]
    turned[0] = final_low[...].T
    turned[1] = second[...].T
    turned[2] = middle_low[...].T

    def weights(i, _):
        store_split(dot_of(turned[i // hidden], right[i], 1, 0), stage_keep, stage_send, i)

        @pl.when(i < hidden)
        def _():
            pltpu.make_async_copy(stage_keep.at[i], down_keep.at[i], keep_sems.at[i]).start()
            pltpu.make_async_copy(stage_send.at[i], down_send.at[i], send_sems.at[i]).start()

        @pl.when(i >= hidden)
        def _():
            row = i - hidden
            pltpu.make_async_copy(stage_keep.at[i], up_keep.at[row], keep_sems.at[i]).start()
            pltpu.make_async_copy(stage_send.at[i], up_send.at[row], send_sems.at[i]).start()

        return 0

    lax.fori_loop(0, 2 * hidden + 1, weights, 0)
    for copy in puts:
        copy.wait()
    for i in range(2 * hidden + 1):
        if i < hidden:
            keep, gone, row = down_keep, down_send, i
        else:
            keep, gone, row = up_keep, up_send, i - hidden
        pltpu.make_async_copy(stage_keep.at[i], keep.at[row], keep_sems.at[i]).wait()
        pltpu.make_async_copy(stage_send.at[i], gone.at[row], send_sems.at[i]).wait()


def middle_call(limit, vectors, tokens, mixed, logs, cot, teach, arrays, plan, block, dp):
    rows = tokens.shape[0]
    hidden = FF // D
    narrow = jax.ShapeDtypeStruct((rows, D), low)
    wide = jax.ShapeDtypeStruct((rows, D), full)
    shape = (dp // 2, D // dp, D)
    parts = [jax.ShapeDtypeStruct((count,) + shape, low) for count in (hidden, hidden + 1)]
    stats = jax.ShapeDtypeStruct((PAIRS, 2, rows), full)
    anywhere = pl.BlockSpec(memory_space=pl.ANY)
    inside = pl.BlockSpec(memory_space=pltpu.VMEM)
    moves = sum(len(part) for part in plan)
    return pl.pallas_call(
        functools.partial(middle_kernel, plan, block, len(arrays)),
        out_shape=(
            narrow,
            wide,
            narrow,
            parts[0],
            parts[0],
            parts[1],
            parts[1],
            stats,
            stats,
            jax.ShapeDtypeStruct((8 + 8, D), full),
        ),
        in_specs=[pl.BlockSpec(memory_space=pltpu.SMEM), inside]
        + [anywhere] * (5 + len(arrays)),
        out_specs=[anywhere] * 7 + [inside] * 3,
        scratch_shapes=[
            pltpu.VMEM((rows, D), low),
            pltpu.VMEM((rows, D), full),
            pltpu.VMEM((rows, D), full),
            pltpu.VMEM((rows, D), low),
            pltpu.VMEM((rows, D), low),
            pltpu.VMEM((FF, D), low),
            pltpu.VMEM((FF, D), low),
            pltpu.VMEM((D, D), low),
            pltpu.VMEM((2 * hidden + 1, rows, D), low),
            pltpu.VMEM((hidden, rows, D), full),
            pltpu.VMEM((rows, D), low),
            pltpu.VMEM((rows, D), full),
            pltpu.VMEM((rows, D), full),
            pltpu.VMEM((rows, D), low),
            pltpu.VMEM((rows, D), low),
            pltpu.VMEM((rows, D), low),
            pltpu.VMEM((rows, D), low),
            pltpu.VMEM((rows, D), full),
            pltpu.VMEM((3, D, rows), low),
            pltpu.VMEM((2 * hidden + 1,) + shape, low),
            pltpu.VMEM((2 * hidden + 1,) + shape, low),
            pltpu.SemaphoreType.DMA((5,)),
            pltpu.SemaphoreType.DMA((moves,)),
            pltpu.SemaphoreType.DMA((3,)),
            pltpu.SemaphoreType.DMA((2 * hidden + 1,)),
            pltpu.SemaphoreType.DMA((2 * hidden + 1,)),
        ],
        compiler_params=pltpu.CompilerParams(vmem_limit_bytes=VMEM_LIMIT),
        cost_estimate=SMALL_COST,
        name="middle",
    )(limit, vectors, tokens, mixed, logs, cot, teach, *arrays)


def fold_block(keep, got, out_keep, out_send, bit, place):
    step = 1 << place
    mine = (lax.axis_index("dp") // bit) % 2 * step
    for j in range(keep.shape[1] // 2):
        base = (j // step) * 2 * step + j % step
        for out, shift in ((out_keep, mine), (out_send, step - mine)):
            value = keep[0, base + shift].astype(full) + got[0, base + shift].astype(full)
            out[0, j] = value.astype(low)


def fold_kernel(bits, places, *refs):
    count = len(bits)
    for n in range(count):
        fold_block(
            *refs[2 * n : 2 * n + 2],
            *refs[2 * count + 2 * n : 2 * count + 2 * n + 2],
            bits[n],
            places[n],
        )


def fold(pairs, bits, places):
    lead = pairs[0][0].shape[0]
    block = lambda shape: pl.BlockSpec((1,) + shape[1:], lambda i: (i, 0, 0, 0))
    halves = [
        (keep.shape[0], keep.shape[1] // 2) + keep.shape[2:] for keep, _ in pairs for _ in range(2)
    ]
    outs = pl.pallas_call(
        functools.partial(fold_kernel, bits, places),
        out_shape=[jax.ShapeDtypeStruct(shape, low) for shape in halves],
        grid=(lead,),
        in_specs=[block(value.shape) for pair in pairs for value in pair],
        out_specs=[block(shape) for shape in halves],
        compiler_params=pltpu.CompilerParams(vmem_limit_bytes=VMEM_LIMIT),
        cost_estimate=pl.CostEstimate(flops=0, bytes_accessed=16 << 20, transcendentals=0),
        name="fold",
    )(*[value for pair in pairs for value in pair])
    return [(outs[2 * n], outs[2 * n + 1]) for n in range(len(pairs))]


def qkv_grad_kernel(count, *refs):
    sources = refs[: 3 * count + 1]
    outs = refs[3 * count + 1 : 3 * count + 5]
    sum_ref, held, turned, total, stage, in_sems, out_sems = refs[3 * count + 5 :]
    first_use = [0, count] + list(range(1, count)) + list(range(count + 1, 3 * count + 1))
    for n in first_use:
        pltpu.make_async_copy(sources[n], held.at[n], in_sems.at[n]).start()

    def wait(n):
        pltpu.make_async_copy(sources[0], held.at[n], in_sems.at[n]).wait()

    def turn(n, _):
        wait(n)
        turned[n] = held[n].T
        return 0

    lax.fori_loop(0, count, turn, 0)
    sum_ref[...] = jnp.zeros_like(sum_ref)

    def step(i, _):
        c = (i + count - 1) // count
        n = jnp.where(i == 0, 0, (i + count - 1) % count)
        wait(count + i)
        right = held[count + i]
        value = dot_of(turned[n], right, 1, 0)
        total[...] = value + jnp.where(n == 0, jnp.zeros_like(value), total[...])

        @pl.when(c != 1)
        def _():
            row = pl.ds(pl.multiple_of(c * 4, 8), 1)
            sum_ref[row, :] += jnp.sum(right.astype(full), axis=0, keepdims=True)

        @pl.when(i % count == 0)
        def _():
            for part in range(2):
                store_split(
                    total[:, part * D // 2 : (part + 1) * D // 2],
                    stage.at[part],
                    stage.at[2 + part],
                    c,
                )
            for k in range(4):
                pltpu.make_async_copy(
                    stage.at[k, c], outs[k].at[c], out_sems.at[k * 3 + c]
                ).start()

        return 0

    lax.fori_loop(0, 2 * count + 1, step, 0)
    for k in range(4):
        for c in range(3):
            pltpu.make_async_copy(stage.at[k, c], outs[k].at[c], out_sems.at[k * 3 + c]).wait()


def qkv_grads(chunks, query_grad, key_grads, value_grads, dp):
    rows = query_grad.shape[0]
    count = len(chunks)
    shape = (3, dp // 2, D // dp, D // 2)
    anywhere = pl.BlockSpec(memory_space=pl.ANY)
    return pl.pallas_call(
        functools.partial(qkv_grad_kernel, count),
        out_shape=[jax.ShapeDtypeStruct(shape, low)] * 4
        + [jax.ShapeDtypeStruct((16, D), full)],
        in_specs=[anywhere] * (3 * count + 1),
        out_specs=[anywhere] * 4 + [pl.BlockSpec(memory_space=pltpu.VMEM)],
        scratch_shapes=[
            pltpu.VMEM((3 * count + 1, rows, D), low),
            pltpu.VMEM((count, D, rows), low),
            pltpu.VMEM((D, D), full),
            pltpu.VMEM((4,) + shape, low),
            pltpu.SemaphoreType.DMA((3 * count + 1,)),
            pltpu.SemaphoreType.DMA((12,)),
        ],
        compiler_params=pltpu.CompilerParams(vmem_limit_bytes=VMEM_LIMIT),
        cost_estimate=SMALL_COST,
        name="qkv_grads",
    )(*chunks, query_grad, *key_grads, *value_grads)


def last_kernel(
    token_ref,
    first_ref,
    right_ref,
    left_ref,
    middle_ref,
    vector_ref,
    gain_ref,
    bias_ref,
    sum_ref,
    out_ref,
    pack_ref,
):
    @pl.when(pl.program_id(0) == 0)
    def _():
        pack_ref[...] = jnp.zeros_like(pack_ref)
        pack_ref[1:2, :] = sum_ref[0:1, :]
        pack_ref[3:4, :] = sum_ref[1:2, :]
        pack_ref[4:5, :] = bias_ref[0:1, :]
        pack_ref[5:6, :] = bias_ref[8:9, :]
        pack_ref[6:8, :] = sum_ref[2:4, :]
        pack_ref[8 : 8 + FF // D, :] = sum_ref[8 : 8 + FF // D, :]

    unit, inverse = norm_stats(token_ref[...].astype(full) + vector_ref[0:1, :])
    grad = first_ref[...] + right_ref[...].astype(full) + left_ref[...].astype(full)
    scaled = grad * gain_ref[0:1, :]
    mean_scaled = jnp.mean(scaled, axis=-1, keepdims=True)
    mean_unit = jnp.mean(scaled * unit, axis=-1, keepdims=True)
    result = middle_ref[...] + inverse * (scaled - mean_scaled - unit * mean_unit)
    out_ref[...] = result
    pack_ref[0:1, :] += jnp.sum(grad * unit, axis=0, keepdims=True)
    pack_ref[2:3, :] += jnp.sum(grad, axis=0, keepdims=True)
    pack_ref[pl.ds(16 + lax.axis_index("dp"), 1), :] += jnp.sum(result, axis=0, keepdims=True)


def last_norm(tokens, first, right, left, middle_grad, vectors, gains, bias_sums, sums, dp):
    rows = tokens.shape[0]
    part = pl.BlockSpec((rows // 4, D), lambda i: (i, 0))
    whole = lambda value: pl.BlockSpec(value.shape, lambda i: (0, 0))
    small = (vectors, gains, bias_sums, sums)
    return pl.pallas_call(
        last_kernel,
        out_shape=(
            jax.ShapeDtypeStruct((rows, D), full),
            jax.ShapeDtypeStruct((16 + dp, D), full),
        ),
        grid=(4,),
        in_specs=[part] * 5 + [whole(value) for value in small],
        out_specs=[part, pl.BlockSpec((16 + dp, D), lambda i: (0, 0))],
        compiler_params=pltpu.CompilerParams(vmem_limit_bytes=VMEM_LIMIT),
        cost_estimate=SMALL_COST,
        name="last_norm",
    )(tokens, first, right, left, middle_grad, *small)


def two_parts(value, axis, mine):
    keep = lax.dynamic_index_in_dim(value, mine, axis, keepdims=False)
    send = lax.dynamic_index_in_dim(value, 1 - mine, axis, keepdims=False)
    return keep, send.astype(low)


class Scatter:
    def __init__(self, parts, turns):
        self.bits = outer_bits()
        half = len(self.bits) // 2
        self.orders = [
            [1] + self.bits[half * (turn % 2) :] + self.bits[: half * (turn % 2)] for turn in turns
        ]
        self.left = [list(self.bits) for _ in turns]
        self.step = 0
        self.parts = parts

    def sends(self):
        return [send for _, send in self.parts]

    def exchange(self, sends):
        self.pairs = [
            (keep, swap(send, "dp", turn[self.step]))
            for (keep, _), send, turn in zip(self.parts, sends, self.orders)
        ]
        self.step += 1

    def folds(self):
        if self.step > len(self.bits):
            return [], [], []
        bits = [turn[self.step] for turn in self.orders]
        places = []
        for left, bit in zip(self.left, bits):
            places.append(left.index(bit))
            left.remove(bit)
        return self.pairs, bits, places

    def give(self, outs):
        self.parts = [(outs[n], outs[n + 1]) for n in range(0, len(outs), 2)]

    def fold(self):
        outs = []
        for pair, bit, at in zip(*self.folds()):
            outs += fold([pair], [bit], [at])[0]
        self.give(outs)

    def advance(self, order):
        sends = order(*self.sends())
        self.exchange(list(sends) if len(self.parts) > 1 else [sends])

    def finish(self, order):
        while self.step <= len(self.bits):
            self.fold()
            self.advance(order)
        got = order(*[other for _, other in self.pairs])
        return [
            (keep.astype(full) + other.astype(full))[:, 0]
            for (keep, _), other in zip(self.pairs, got)
        ]


def scatter_dp(parts, turns):
    scatter = Scatter(parts, turns)
    while True:
        sends = yield scatter.sends()
        scatter.exchange(sends)
        if scatter.step > len(scatter.bits):
            break
        scatter.parts = fold(*scatter.folds())
    got = yield [other for _, other in scatter.pairs]
    return [
        (keep.astype(full) + other.astype(full))[:, 0]
        for (keep, _), other in zip(scatter.pairs, got)
    ]


def scatter_mp(value):
    rank = lax.axis_index("mp")
    part = lambda index: lax.dynamic_index_in_dim(value, index, keepdims=False)
    sends = yield [part(rank ^ bit).astype(low) for bit in (1, 2, 3)]
    got = yield [swap(send, "mp", bit) for bit, send in zip((1, 2, 3), sends)]
    got = [other.astype(full) for other in got]
    return (part(rank) + got[0]) + (got[1] + got[2])


def halve_mp(value):
    rank = lax.axis_index("mp")
    pairs = value.reshape((2, 2) + value.shape[1:])
    keep, send = two_parts(pairs, 1, rank % 2)
    (send,) = yield [send]
    (got,) = yield [swap(send, "mp", 1)]
    keep, send = two_parts(keep.astype(full) + got.astype(full), 0, rank // 2)
    (send,) = yield [send]
    (got,) = yield [swap(send, "mp", 2)]
    return keep + got.astype(full)


def scatter_feed(up_own, down_own):
    mp = lax.axis_size("mp")
    block = down_own.shape[1]
    out_own = up_own[mp].reshape(block, mp, -1).transpose(1, 0, 2)
    own = yield from halve_mp(
        jnp.concatenate([up_own[:mp], down_own, out_own.reshape(mp, -1, D)], axis=1)
    )
    return own[:block], own[block : 2 * block].T, own[2 * block :].reshape(block, -1).T


def scatter_qkv(keep_left, keep_right, send_left, send_right):
    left_part, right_part = yield from scatter_dp(
        [(keep_left, send_left), (keep_right, send_right)], (0, 1)
    )
    width = D // lax.axis_size("mp")
    parts = [part[..., at : at + width] for part in (left_part, right_part) for at in (0, width)]
    return (yield from scatter_mp(jnp.stack(parts)))


def sum_small(value):
    (value,) = yield [value]
    value = value + swap(value, "dp", 1)
    bits = outer_bits()
    groups = [("dp", bits[n : n + 2]) for n in range(0, len(bits), 2)] + [("mp", [1, 2])]
    for axis, pair in groups:
        (value,) = yield [value]
        if len(pair) == 1:
            value = value + swap(value, axis, pair[0])
        else:
            one, two = pair
            got = [swap(value, axis, mask) for mask in (one, two, one + two)]
            if axis == "mp":
                got = yield got
            value = (value + got[0]) + (got[1] + got[2])
    return value


class Steps:
    def __init__(self, steps):
        self.steps = steps
        self.pending = next(steps)
        self.result = None

    def advance(self, order):
        if self.pending is None:
            return
        sends = order(*self.pending)
        sends = [sends] if len(self.pending) == 1 else list(sends)
        try:
            self.pending = self.steps.send(sends)
        except StopIteration as stop:
            self.pending = None
            self.result = stop.value

    def finish(self, order):
        while self.pending is not None:
            self.advance(order)
        return self.result


def shards(
    tokens_in,
    timesteps,
    lengths,
    time_table,
    norm_gains,
    norm_biases,
    w_qkv,
    qv_bias,
    w_out,
    out_bias,
    w_up,
    up_bias,
    w_down,
    down_bias,
    cotangent,
    teacher,
):
    rank = lax.axis_index("mp")
    data_rank = lax.axis_index("dp")
    mp = lax.axis_size("mp")
    dp = lax.axis_size("dp")
    own_rows = tokens_in.shape[0]
    length = lax.dynamic_index_in_dim(lengths, data_rank, keepdims=False)
    own_time = lax.dynamic_index_in_dim(timesteps, data_rank, keepdims=False)
    odd = rank % 2 == 1
    upper = rank >= 2
    middle = jnp.logical_or(rank == 1, rank == 2)
    order = Order()
    along = lambda value, pairs: lax.ppermute(value, "mp", pairs)

    block = w_qkv.shape[1]
    aligned = block % 32 == 0
    narrow = order(jnp.concatenate([w_qkv.reshape(3 * block, -1), w_out.T]))
    first_swap = swap(narrow, "mp", 1)
    tall = order(jnp.concatenate([w_up, w_down.T]))
    tall_swap = swap(tall, "mp", 1)
    pair = order(
        jnp.concatenate(
            [jnp.where(odd, first_swap, narrow), jnp.where(odd, narrow, first_swap)], axis=1
        )
    )
    second_swap = swap(pair, "mp", 2)
    tokens, lengths, own_time, norm_gains, norm_biases, out_bias, down_bias, up_bias, length = order(
        tokens_in, lengths, own_time, norm_gains, norm_biases, out_bias, down_bias, up_bias, length
    )
    table_row = lax.dynamic_slice_in_dim(time_table, own_time, 1).astype(full)
    unit_one, _ = norm_stats(tokens.astype(full) + table_row)
    first_norm = (unit_one * norm_gains[0] + norm_biases[0]).astype(low)
    loss_weight = lengths.shape[0] * MAXLEN / jnp.sum(lengths).astype(full)
    vectors = jnp.concatenate(
        [
            table_row,
            out_bias[None],
            norm_gains[1:2],
            norm_biases[1:2],
            down_bias[None],
            jnp.full((3, D), loss_weight),
            up_bias.reshape(-1, D),
            jnp.zeros((4, D), full),
        ]
    )
    scalars = jnp.stack(
        [
            rank,
            jnp.where(rank == 0, 1, rank - 1),
            jnp.where(upper, rank - 2, rank + 2),
            jnp.where(middle, rank + 1, 3 - rank),
            length,
            length - rank * own_rows,
        ]
    ).astype(jnp.int32)
    first_norm, vectors, scalars = order(first_norm, vectors, scalars)
    wide = jnp.concatenate(
        [jnp.where(upper, second_swap, pair), jnp.where(upper, pair, second_swap)], axis=1
    )
    qkv_rows, out_rows = wide[: 3 * block], wide[3 * block :]
    if aligned:
        split = 3 * block // 2
        qkv_gather = Gather([qkv_rows[:split], qkv_rows[split:]])
        qkv_gather.advance(order)
    tall = order(jnp.concatenate([tall, tall_swap]))
    tall_across = along(tall, [(1, 2), (2, 1)])

    sent = order(first_norm)
    from_left = along(sent, [(0, 1), (1, 2), (2, 3)])
    from_right = along(sent, [(1, 0), (2, 1), (3, 2)])
    tall_across = order(tall_across)
    tall_far = along(tall_across, [(1, 0), (2, 3)])
    if aligned:
        while qkv_gather.step < len(qkv_gather.bits):
            qkv_gather.advance(order)
        qkv_gather.advance(order)
    hop_right, hop_left = order(from_left, from_right)
    second_right = along(hop_right, [(1, 2), (2, 3)])
    second_left = along(hop_left, [(1, 0), (2, 1)])
    if aligned:
        arrays, plan = plan_of(
            qkv_gather.result,
            [
                [(0, block, 0, 0, 0, 0), (block, split - block, 1, 0, 0, 0)],
                [
                    (0, 2 * block - split, 1, 0, 0, split - block),
                    (2 * block - split, block, 1, 1, 0, 0),
                ],
            ],
        )
        query_weight, pair_weight = order(*place(arrays, plan, block, [(D, D), (D, 2 * D)]))
        tall_other = jnp.where(middle, tall_across, order(tall_far))
        feed_gather = Gather(
            [
                jnp.concatenate([tall, out_rows[: block // 2]]),
                jnp.concatenate([tall_other, out_rows[block // 2 :]]),
            ]
        )
        feed_gather.advance(order)
    else:
        weights = lax.all_gather(qkv_rows.reshape(3, block, D), "dp", axis=1, tiled=True)
        query_weight = weights[0]
        pair_weight = jnp.concatenate([weights[1], weights[2]], axis=1)
    near = jnp.where(rank == 0, hop_left, hop_right)
    attend = lambda parts, numbers, carried: order(
        *attend_forward(
            parts,
            numbers,
            scalars,
            query_weight,
            pair_weight,
            qv_bias[0:1],
            qv_bias[1:2],
            carried,
        )
    )
    key_own, key_near, value_own, value_near, queries, *state = attend(
        list(order(first_norm, near)), (0, 1), None
    )
    second_right, second_left = order(second_right, second_left)
    second = order(jnp.where(upper, second_right, second_left))
    third = along(second, [(1, 0), (2, 3)])
    if aligned:
        while feed_gather.step < len(feed_gather.bits):
            feed_gather.advance(order)
        feed_gather.send_early(order)
    key_second, value_second, *state = attend([order(second)], (2,), (queries, *state))
    last = order(jnp.where(middle, hop_left, order(third)))
    key_last, value_last, mixed, logs = attend([order(last)], (3,), (queries, *state))
    if aligned:
        feed_gather.advance(order)
        layout = lambda masks, shift: [
            (0, block, 0, masks[0], D, 0),
            (block, block, 1, masks[0], D, 0),
            (2 * block, block, 0, masks[1], D, 0),
            (3 * block, block, 1, masks[1], D, 0),
            (4 * block, block // 2, 2, 0, 0, shift),
        ]
        arrays, plan = plan_of(
            feed_gather.result, [layout((0, 1), 0), layout((2, 3), block // 2)]
        )
    else:
        arrays = [
            lax.all_gather(w_up, ("mp", "dp"), axis=0, tiled=True),
            lax.all_gather(w_down.T, ("mp", "dp"), axis=0, tiled=True),
            lax.all_gather(out_rows, "dp", axis=0, tiled=True),
        ]
        plan = [[(0, array.shape[0], n, None, 0, 0, 0)] for n, array in enumerate(arrays)]
    chunks = [first_norm, near, second, last]
    keys = [key_own, key_near, key_second, key_last]
    values = [value_own, value_near, value_second, value_last]

    output, middle_grad, attended_grad, *parts, deltas, log_rows, sums = middle_call(
        scalars, vectors, tokens, mixed, logs, cotangent, teacher, arrays, plan, block, dp
    )
    scatter = Scatter([(parts[0], parts[1]), (parts[2], parts[3])], (1, 0))
    scatter.advance(order)

    key_grads = [None] * 4
    value_grads = [None] * 4
    firsts = [None] * 4
    query_grad = None
    for n in (3, 2, 1, 0):
        pairs, bits, places = scatter.folds() if n % 2 == 0 else ([], [], [])
        query_grad, key_grads[n], value_grads[n], firsts[n], *folded = attend_backward(
            n,
            queries,
            keys[n],
            values[n],
            order(attended_grad),
            log_rows,
            deltas,
            query_weight,
            pair_weight,
            scalars,
            query_grad,
            n == 0,
            pairs,
            bits,
            places,
        )
        firsts[n] = order(firsts[n])
        if folded:
            scatter.give(folded)
        if n == 3:
            back_last = along(firsts[3], [(0, 1), (3, 2)]).astype(full)
        elif n == 2:
            scatter.advance(order)
            payload = order((firsts[2] + back_last).astype(low))
            back_right = along(payload, [(0, 1), (1, 2)]).astype(full)
            back_left = along(payload, [(3, 2), (2, 1)]).astype(full)
        elif n == 1:
            to_right = jnp.where(
                rank == 0, firsts[1], firsts[3].astype(full) + back_right
            ).astype(low)
            to_left = (firsts[1] + back_left).astype(low)
            to_right, to_left = order(to_right, to_left)
            final_right = along(to_right, [(0, 1), (1, 2), (2, 3)])
            final_left = along(to_left, [(3, 2), (2, 1), (1, 0)])
    scatter.advance(order)
    query_grad, final_right, final_left = order(query_grad, final_right, final_left)
    *halves, bias_sums = qkv_grads(chunks, query_grad, key_grads, value_grads, dp)
    qkv = Steps(scatter_qkv(*halves))
    qkv.advance(order)
    down_own, up_own = scatter.finish(order)
    feed = Steps(scatter_feed(up_own, down_own))
    feed.advance(order)
    qkv.advance(order)
    tokens, first_own = order(tokens, firsts[0])
    input_grad, packed = last_norm(
        tokens,
        first_own,
        final_right,
        final_left,
        middle_grad,
        vectors,
        norm_gains,
        bias_sums,
        sums,
        dp,
    )
    packed, input_grad = order(packed, input_grad)
    small = Steps(sum_small(packed))
    feed.advance(order)
    feed.advance(order)
    small.advance(order)
    qkv.advance(order)
    qkv.advance(order)
    small.advance(order)
    qkv.advance(order)
    small.advance(order)
    total = small.finish(order)
    up_grad, down_grad, out_grad = feed.finish(order)
    qkv_grad = qkv.finish(order)
    fixed = 16
    chosen = (timesteps[None, :] == jnp.arange(time_table.shape[0])[:, None]).astype(full)
    table_grad = lax.dot_general(
        chosen,
        total[fixed:],
        (((1,), (0,)), ((), ())),
        precision=lax.Precision.HIGHEST,
        preferred_element_type=full,
    )
    return (
        output,
        input_grad,
        table_grad,
        total[0:2],
        total[2:4],
        qkv_grad,
        total[4:6],
        out_grad,
        total[6],
        up_grad,
        total[8 : 8 + FF // D].reshape(FF),
        down_grad,
        total[7],
    )


def solution(mesh):
    rows = P(both, None)
    placed = (
        rows,
        P(),
        P(),
        P(),
        P(),
        P(),
        P(None, "dp", "mp"),
        P(),
        P("mp", "dp"),
        P(),
        P("dp", "mp"),
        P(),
        P("mp", "dp"),
        P(),
        rows,
        rows,
    )
    return jax.shard_map(
        shards,
        mesh=mesh,
        in_specs=placed,
        out_specs=(
            rows,
            rows,
            P(),
            P(),
            P(),
            P(None, "dp", "mp"),
            P(),
            P("mp", "dp"),
            P(),
            P("dp", "mp"),
            P(),
            P("mp", "dp"),
            P(),
        ),
        check_vma=False,
    )
```

```python
import functools

import jax
import jax.numpy as jnp
from jax import lax
from jax.experimental import pallas as pl
from jax.experimental.pallas import tpu as pltpu
from jax.sharding import PartitionSpec as P

D = 768
HEADS = 12
HEAD_DIM = 64
FF = 3072
MAXLEN = 2048
PAIR = 2 * HEAD_DIM
PAIRS = HEADS // 2
VMEM_LIMIT = 58 << 20
SMALL_COST = pl.CostEstimate(flops=1 << 20, bytes_accessed=1 << 16, transcendentals=0)

far_below = -1e30
epsilon = 1e-05
score_scale = HEAD_DIM ** (-0.5)
low = jnp.bfloat16
full = jnp.float32
both = ("dp", "mp")


def norm_stats(values):
    center = values - jnp.mean(values, axis=-1, keepdims=True)
    spread = jnp.mean(center * center, axis=-1, keepdims=True)
    inverse = lax.rsqrt(spread + epsilon)
    return center * inverse, inverse


def dot_of(left_side, right_side, left_dim, right_dim):
    return lax.dot_general(
        left_side,
        right_side,
        (((left_dim,), (right_dim,)), ((), ())),
        preferred_element_type=full,
    )


def first_half(shape):
    return lax.broadcasted_iota(jnp.int32, shape, len(shape) - 1) < HEAD_DIM


def forward_kernel(numbers, first, final, scalars, *refs):
    count = len(numbers)
    chunk_refs = refs[:count]
    wk_ref, wv_ref, value_bias_ref = refs[count : count + 3]
    refs = refs[count + 3 :]
    if first:
        wq_ref, query_bias_ref = refs[:2]
        key_outs, value_outs = refs[2 : 2 + count], refs[2 + count : 2 + 2 * count]
        query_out, top_ref, sum_ref, acc_ref = refs[2 + 2 * count :]
        q_pair = (dot_of(chunk_refs[0][...], wq_ref[...], 1, 0) + query_bias_ref[...]).astype(low)
        q_pair = q_pair * jnp.asarray(score_scale, low)
        query_out[...] = q_pair
    else:
        q_ref, top_in, sum_in, acc_in = refs[:4]
        key_outs, value_outs = refs[4 : 4 + count], refs[4 + count : 4 + 2 * count]
        results = refs[4 + 2 * count :]
        q_pair = q_ref[...]
    weight = jnp.concatenate([wk_ref[...], wv_ref[...]], axis=1)
    keys = []
    values = []
    for n in range(count):
        both_parts = dot_of(chunk_refs[n][...], weight, 1, 0)
        keys.append(both_parts[:, :PAIR].astype(low))
        values.append((both_parts[:, PAIR:] + value_bias_ref[...]).astype(low))
        key_outs[n][...] = keys[n]
        value_outs[n][...] = values[n]
    rows = q_pair.shape[0]
    size = keys[0].shape[0]
    place = lax.broadcasted_iota(jnp.int32, (1, size), 1)
    lower = first_half((rows, PAIR))
    parts = []
    for half in range(2):
        kept = lower if half == 0 else jnp.logical_not(lower)
        q_half = jnp.where(kept, q_pair, jnp.zeros_like(q_pair))
        scores = []
        for n in range(count):
            bias = jnp.where(place + scalars[numbers[n]] * size < scalars[4], 0.0, far_below)
            scores.append(dot_of(q_half, keys[n], 1, 1) + bias)
        highest = functools.reduce(
            jnp.maximum, [jnp.max(score, axis=-1, keepdims=True) for score in scores]
        )
        totals = jnp.zeros_like(highest)
        mixed = jnp.zeros((rows, PAIR), full)
        for n in range(count):
            exp_scores = jnp.exp(scores[n] - highest)
            totals = totals + jnp.sum(exp_scores, axis=-1, keepdims=True)
            mixed = mixed + dot_of(exp_scores.astype(low), values[n], 1, 0)
        parts.append((highest, totals, mixed))
    top = jnp.where(lower, parts[0][0], parts[1][0])
    total = jnp.where(lower, parts[0][1], parts[1][1])
    mixed = jnp.where(lower, parts[0][2], parts[1][2])
    if first:
        top_ref[...] = top
        sum_ref[...] = total
        acc_ref[...] = mixed
    else:
        highest = jnp.maximum(top, top_in[...])
        here = jnp.exp(top - highest)
        before = jnp.exp(top_in[...] - highest)
        total = total * here + sum_in[...] * before
        mixed = mixed * here + acc_in[...] * before
        if final:
            results[0][...] = mixed / total
            results[1][...] = highest + jnp.log(total)
        else:
            results[0][...] = highest
            results[1][...] = total
            results[2][...] = mixed


def attend_forward(chunks, numbers, scalars, query_weight, pair_weight, query_bias, value_bias, carried):
    rows = chunks[0].shape[0]
    count = len(chunks)
    first = carried is None
    final = 3 in numbers
    column = lambda height, c: pl.BlockSpec((height, PAIR), lambda i, n: (0, c * PAIRS + i))
    whole = pl.BlockSpec((rows, D), lambda i, n: (0, 0))
    wide = jax.ShapeDtypeStruct((rows, D), full)
    narrow = jax.ShapeDtypeStruct((rows, D), low)
    extra = (query_weight, query_bias) if first else carried
    results = (narrow,) * first + (wide,) * (2 if final else 3)
    return pl.pallas_call(
        functools.partial(forward_kernel, numbers, first, final),
        out_shape=(narrow,) * (2 * count) + results,
        grid_spec=pltpu.PrefetchScalarGridSpec(
            num_scalar_prefetch=1,
            grid=(PAIRS,),
            in_specs=[whole] * count
            + [column(D, 0), column(D, 1), column(1, 0)]
            + ([column(D, 0), column(1, 0)] if first else [column(rows, 0)] * 4),
            out_specs=[column(rows, 0)] * (2 * count + len(results)),
        ),
        compiler_params=pltpu.CompilerParams(vmem_limit_bytes=VMEM_LIMIT),
        cost_estimate=SMALL_COST,
        name="attend_forward",
    )(scalars, *chunks, pair_weight, pair_weight, value_bias, *extra)


def backward_kernel(
    number,
    first,
    last,
    folds,
    scalars,
    q_ref,
    k_ref,
    v_ref,
    g_ref,
    log_ref,
    delta_ref,
    wk_ref,
    wv_ref,
    *refs
):
    if last:
        wq_ref = refs[0]
        refs = refs[1:]
    if not first:
        dq_in = refs[0]
        refs = refs[1:]
    count = len(folds)
    fold_ins, refs = refs[: 2 * count], refs[2 * count :]
    dq_ref, dk_ref, dv_ref, back_ref = refs[:4]
    fold_outs, accum = refs[4:-1], refs[-1]
    step = pl.program_id(0)
    for n, (lead, bit, at) in enumerate(folds):

        @pl.when(step < lead)
        def _():
            fold_block(
                *fold_ins[2 * n : 2 * n + 2], *fold_outs[2 * n : 2 * n + 2], bit, at
            )

    rows = q_ref.shape[0]
    keys = k_ref.shape[0]
    limit = scalars[4] - scalars[number] * keys
    q_pair = q_ref[...]
    g_pair = g_ref[...]
    k_pair = k_ref[...]
    v_pair = v_ref[...]
    lower = first_half((rows, PAIR))
    nothing = jnp.zeros((rows, PAIR), low)
    two_halves = lambda pair: jnp.concatenate(
        [jnp.where(lower, pair, nothing), jnp.where(lower, nothing, pair)]
    )
    queries = two_halves(q_pair)
    grads_out = two_halves(g_pair)
    row_of = lambda ref: jnp.concatenate([ref[0, 0:1, :], ref[0, 1:2, :]], axis=1)
    place = lax.broadcasted_iota(jnp.int32, (keys, 1), 0)
    bias = jnp.where(place < limit, 0.0, far_below)
    scores = dot_of(k_pair, queries, 1, 1) + bias
    prob_grad = dot_of(v_pair, grads_out, 1, 1)
    probs = jnp.exp(scores - row_of(log_ref))
    score_grad = (probs * (prob_grad - row_of(delta_ref))).astype(low)
    dv_low = dot_of(probs.astype(low), grads_out, 1, 0).astype(low)
    dk_low = dot_of(score_grad, queries, 1, 0).astype(low)
    turned = dot_of(k_pair.T, score_grad, 1, 0)
    upper_rows = lax.broadcasted_iota(jnp.int32, (PAIR, rows), 0) < HEAD_DIM
    dk_ref[...] = dk_low
    dv_ref[...] = dv_low
    grads = [dk_low, dv_low]
    weights = [wk_ref[...], wv_ref[...]]
    dq_all = jnp.where(upper_rows, turned[:, :rows], turned[:, rows:]).T
    if not first:
        dq_all = dq_all + dq_in[...]
    back = dot_of(jnp.concatenate(grads, axis=1), jnp.concatenate(weights, axis=1), 1, 1)
    if last:
        dq_low = (dq_all * score_scale).astype(low)
        dq_ref[...] = dq_low
        back = back + dot_of(dq_low, wq_ref[...], 1, 1)
    else:
        dq_ref[...] = dq_all

    @pl.when(step == 0)
    def _():
        accum[...] = back

    @pl.when(step > 0)
    def _():
        accum[...] += back

    @pl.when(step == PAIRS - 1)
    def _():
        back_ref[...] = accum[...].astype(back_ref.dtype)


def attend_backward(
    number,
    queries,
    keys,
    values,
    grads,
    logs,
    deltas,
    query_weight,
    pair_weight,
    scalars,
    carried,
    last,
    pairs,
    bits,
    places,
):
    rows, total = queries.shape[0], keys.shape[0]
    first = carried is None
    folds = [(keep.shape[0], bit, at) for (keep, _), bit, at in zip(pairs, bits, places)]
    halves = [
        (keep.shape[0], keep.shape[1] // 2) + keep.shape[2:] for keep, _ in pairs for _ in range(2)
    ]

    def by_lead(shape):
        end = shape[0] - 1
        return pl.BlockSpec((1,) + shape[1:], lambda i, n: (jnp.minimum(i, end), 0, 0, 0))

    column = lambda count, c: pl.BlockSpec((count, PAIR), lambda i, n: (0, c * PAIRS + i))
    stats = pl.BlockSpec((1, 2, rows), lambda i, n: (i, 0, 0))
    extra = (query_weight,) * last + (() if first else (carried,))
    extra_specs = [column(D, 0)] * last + ([] if first else [column(rows, 0)])
    return pl.pallas_call(
        functools.partial(backward_kernel, number, first, last, folds),
        out_shape=(
            jax.ShapeDtypeStruct((rows, D), low if last else full),
            jax.ShapeDtypeStruct((total, D), low),
            jax.ShapeDtypeStruct((total, D), low),
            jax.ShapeDtypeStruct((total, D), low if first else full),
            *[jax.ShapeDtypeStruct(shape, low) for shape in halves],
        ),
        grid_spec=pltpu.PrefetchScalarGridSpec(
            num_scalar_prefetch=1,
            grid=(PAIRS,),
            in_specs=[
                column(rows, 0),
                column(total, 0),
                column(total, 0),
                column(rows, 0),
                stats,
                stats,
                column(D, 0),
                column(D, 1),
            ]
            + extra_specs
            + [by_lead(value.shape) for pair in pairs for value in pair],
            out_specs=[
                column(rows, 0),
                column(total, 0),
                column(total, 0),
                pl.BlockSpec((total, D), lambda i, n: (0, 0)),
            ]
            + [by_lead(shape) for shape in halves],
            scratch_shapes=[pltpu.VMEM((total, D), full)],
        ),
        compiler_params=pltpu.CompilerParams(vmem_limit_bytes=VMEM_LIMIT),
        cost_estimate=SMALL_COST,
        name="attend_backward",
    )(
        scalars,
        queries,
        keys,
        values,
        grads,
        logs,
        deltas,
        pair_weight,
        pair_weight,
        *extra,
        *[value for pair in pairs for value in pair],
    )


def swap(value, axis, bit):
    count = lax.axis_size(axis)
    return lax.ppermute(value, axis, [(i, i ^ bit) for i in range(count)])


class Order:
    def __init__(self):
        self.marks = ()

    def __call__(self, *values):
        values = lax.optimization_barrier(values + self.marks)[: len(values)]
        self.marks = values
        return values[0] if len(values) == 1 else values


def outer_bits():
    bits = []
    bit = 2
    while bit < lax.axis_size("dp"):
        bits.append(bit)
        bit *= 2
    return bits


class Gather:
    def __init__(self, parts):
        self.bits = outer_bits()
        half = len(self.bits) // 2
        self.orders = [
            self.bits[half * (n % 2) :] + self.bits[: half * (n % 2)] for n in range(len(parts))
        ]
        self.result = [[([0], part)] for part in parts]
        self.step = 0
        self.early = []

    def advance(self, order):
        held = self.result
        if self.step < len(self.bits):
            masks = [[m for mask, _ in pieces for m in mask] for pieces in held]
            blocks = [
                jnp.concatenate([array for _, array in pieces]) if self.step else pieces[0][1]
                for pieces in held
            ]
            blocks = order(*blocks)
            bits = [turn[self.step] for turn in self.orders]
            self.result = [
                [(mask, block), ([m ^ bit for m in mask], swap(block, "dp", bit))]
                for mask, block, bit in zip(masks, blocks, bits)
            ]
        else:
            rest = [pieces[1:] if self.early else pieces for pieces in held]
            arrays = iter(order(*[array for pieces in rest for _, array in pieces]))
            self.result = []
            for n, pieces in enumerate(rest):
                kept = [(masks, next(arrays)) for masks, _ in pieces]
                ours = held[n][:1] + kept if self.early else kept
                theirs = [([m ^ 1 for m in masks], swap(array, "dp", 1)) for masks, array in kept]
                self.result.append(ours + self.early[n : n + 1] + theirs)
        self.step += 1

    def send_early(self, order):
        arrays = order(*[pieces[0][1] for pieces in self.result])
        self.early = [
            ([m ^ 1 for m in pieces[0][0]], swap(array, "dp", 1))
            for pieces, array in zip(self.result, arrays)
        ]


def canonical_row(me, rank, block, mask, rank_mask, stride, offset):
    if mask is None:
        return offset
    row = (me ^ mask) * block + offset
    if stride:
        if rank_mask >= 2:
            rank_mask = rank_mask ^ ((rank + 1) // 2 % 2)
        row = row + (rank ^ rank_mask) * stride
    return pl.multiple_of(row, 16)


def place_kernel(plan, block, *refs):
    count = len(plan)
    ins = refs[:count]
    outs = refs[count:-1]
    sems = refs[-1]
    me = lax.axis_index("dp")
    rank = lax.axis_index("mp")
    copies = []
    for ref, moves in zip(ins, plan):
        for start, size, which, mask, column, _, offset in moves:
            row = canonical_row(me, rank, block, mask, 0, 0, offset)
            copy = pltpu.make_async_copy(
                ref.at[pl.ds(start, size), :],
                outs[which].at[pl.ds(row, size), pl.ds(column * D, D)],
                sems.at[len(copies)],
            )
            copy.start()
            copies.append(copy)
    for copy in copies:
        copy.wait()


def plan_of(gathered, layouts):
    arrays = []
    plan = []
    for pieces, layout in zip(gathered, layouts):
        rows = sum(size for _, size, *_ in layout)
        for masks, array in pieces:
            moves = []
            for j, mask in enumerate(masks):
                for start, size, which, rank_mask, stride, offset in layout:
                    moves.append((j * rows + start, size, which, mask, rank_mask, stride, offset))
            arrays.append(array)
            plan.append(moves)
    return arrays, plan


def place(arrays, plan, block, shapes):
    return pl.pallas_call(
        functools.partial(place_kernel, plan, block),
        out_shape=[jax.ShapeDtypeStruct(shape, low) for shape in shapes],
        in_specs=[pl.BlockSpec(memory_space=pl.ANY)] * len(arrays),
        out_specs=[pl.BlockSpec(memory_space=pltpu.VMEM)] * len(shapes),
        scratch_shapes=[pltpu.SemaphoreType.DMA((sum(len(moves) for moves in plan),))],
        compiler_params=pltpu.CompilerParams(vmem_limit_bytes=VMEM_LIMIT),
        cost_estimate=SMALL_COST,
        name="place",
    )(*arrays)


def store_split(value, keep, send, index):
    block = keep.shape[2]
    even = lax.axis_index("dp") % 2 == 0
    for outer in range(keep.shape[1]):
        first = value[2 * outer * block : (2 * outer + 1) * block]
        other = value[(2 * outer + 1) * block : (2 * outer + 2) * block]
        keep[index, outer] = jnp.where(even, first, other).astype(low)
        send[index, outer] = jnp.where(even, other, first).astype(low)


def middle_kernel(plan, block, total, *refs):
    limit_ref, vector_ref = refs[:2]
    token_hbm, mixed_hbm, log_hbm, cot_hbm, teach_hbm = refs[2:7]
    pieces = refs[7 : 7 + total]
    (
        out_hbm,
        middle_hbm,
        grad_hbm,
        down_keep,
        down_send,
        up_keep,
        up_send,
        delta_ref,
        log_ref,
        sum_ref,
    ) = refs[7 + total : 17 + total]
    (
        token,
        mixed,
        logs,
        cot,
        teach,
        up,
        down,
        proj,
        right,
        slope,
        second,
        middle,
        final,
        out,
        final_low,
        middle_low,
        grad,
        accum,
        turned,
        stage_keep,
        stage_send,
        in_sems,
        weight_sems,
        out_sems,
        keep_sems,
        send_sems,
    ) = refs[17 + total :]
    hidden = FF // D
    targets = (up, down, proj)
    rows = token.shape[0]
    me = lax.axis_index("dp")
    rank = lax.axis_index("mp")

    def fetch(ref, scratch, n):
        copy = pltpu.make_async_copy(ref, scratch, in_sems.at[n])
        copy.start()
        return copy

    def send(scratch, ref, n):
        copy = pltpu.make_async_copy(scratch, ref, out_sems.at[n])
        copy.start()
        return copy

    gets = [
        fetch(token_hbm, token, 0),
        fetch(mixed_hbm, mixed, 1),
        fetch(log_hbm, logs, 2),
        fetch(cot_hbm, cot, 3),
        fetch(teach_hbm, teach, 4),
    ]
    loads = {0: [], 1: [], 2: []}
    number = 0
    for want in (2, 0, 1):
        for ref, moves in zip(pieces, plan):
            for start, size, which, mask, rank_mask, stride, offset in moves:
                if which != want:
                    continue
                row = canonical_row(me, rank, block, mask, rank_mask, stride, offset)
                copy = pltpu.make_async_copy(
                    ref.at[pl.ds(start, size), :],
                    targets[which].at[pl.ds(row, size), :],
                    weight_sems.at[number],
                )
                copy.start()
                loads[which].append(copy)
                number += 1

    table_row = vector_ref[0:1, :]
    out_bias = vector_ref[1:2, :]
    gain = vector_ref[2:3, :]
    shift = vector_ref[3:4, :]
    down_bias = vector_ref[4:5, :]
    weight = vector_ref[5:6, :]
    gets[0].wait()
    gets[1].wait()
    right[2 * hidden] = mixed[...].astype(low)
    for copy in loads[2]:
        copy.wait()
    state = token[...].astype(full) + table_row + out_bias
    state = state + dot_of(right[2 * hidden], proj[...], 1, 1)
    middle[...] = state
    unit, _ = norm_stats(state)
    second[...] = (unit * gain + shift).astype(low)
    accum[...] = jnp.zeros((rows, D), full)
    for copy in loads[0]:
        copy.wait()
    for copy in loads[1]:
        copy.wait()

    def forward(m, _):
        place = pl.ds(pl.multiple_of(m * D, D), D)
        value = dot_of(second[...], up[place, :], 1, 0) + vector_ref[pl.ds(8 + m, 1), :]
        cumulative = 0.5 + 0.5 * lax.erf(value * (0.5**0.5))
        right[m] = (value * cumulative).astype(low)
        slope[m] = cumulative + value * jnp.exp(-0.5 * value * value) * 0.3989422804014327
        accum[...] += dot_of(right[m], down[place, :], 1, 1)
        return 0

    lax.fori_loop(0, FF // D, forward, 0)
    final_state = middle[...] + accum[...] + down_bias
    out[...] = final_state.astype(low)
    puts = [send(out, out_hbm, 0)]
    gets[3].wait()
    gets[4].wait()
    place = lax.broadcasted_iota(jnp.int32, (rows, 1), 0)
    grads = cot[...].astype(full) + weight * (final_state - teach[...].astype(full))
    grads = jnp.where(place < limit_ref[5], grads, 0.0)
    final[...] = grads
    final_low[...] = grads.astype(low)
    sum_ref[3:4, :] = jnp.sum(grads, axis=0, keepdims=True)
    accum[...] = jnp.zeros((rows, D), full)

    def backward(m, _):
        place = pl.ds(pl.multiple_of(m * D, D), D)
        value = slope[m] * dot_of(final_low[...], down[place, :], 1, 0)
        value = value.astype(low)
        right[hidden + m] = value
        sum_ref[pl.ds(8 + m, 1), :] = jnp.sum(value.astype(full), axis=0, keepdims=True)
        accum[...] += dot_of(value, up[place, :], 1, 1)
        return 0

    lax.fori_loop(0, FF // D, backward, 0)
    unit, inverse = norm_stats(middle[...])
    second_grad = accum[...]
    sum_ref[0:1, :] = jnp.sum(second_grad * unit, axis=0, keepdims=True)
    sum_ref[1:2, :] = jnp.sum(second_grad, axis=0, keepdims=True)
    scaled = second_grad * gain
    mean_scaled = jnp.mean(scaled, axis=-1, keepdims=True)
    mean_unit = jnp.mean(scaled * unit, axis=-1, keepdims=True)
    total_grad = final[...] + inverse * (scaled - mean_scaled - unit * mean_unit)
    middle[...] = total_grad
    puts.append(send(middle, middle_hbm, 1))
    middle_low[...] = total_grad.astype(low)
    sum_ref[2:3, :] = jnp.sum(total_grad, axis=0, keepdims=True)
    attended_grad = dot_of(middle_low[...], proj[...], 1, 0).astype(low)
    grad[...] = attended_grad
    puts.append(send(grad, grad_hbm, 2))
    gets[2].wait()
    head = lax.broadcasted_iota(jnp.int32, (16, D), 0)
    lane = lax.broadcasted_iota(jnp.int32, (16, D), 1)
    member = jnp.where(lane // HEAD_DIM == head, 1.0, 0.0)
    leader = jnp.where(lane == head * HEAD_DIM, 1.0, 0.0)
    exact = functools.partial(
        lax.dot_general,
        dimension_numbers=(((1,), (1,)), ((), ())),
        precision=lax.Precision.HIGHEST,
        preferred_element_type=full,
    )
    deltas = exact(member, attended_grad.astype(full) * mixed[...])
    tops = exact(leader, logs[...])
    for pair in range(PAIRS):
        delta_ref[pair] = deltas[2 * pair : 2 * pair + 2]
        log_ref[pair] = tops[2 * pair : 2 * pair + 2]
    turned[0] = final_low[...].T
    turned[1] = second[...].T
    turned[2] = middle_low[...].T

    def weights(i, _):
        store_split(dot_of(turned[i // hidden], right[i], 1, 0), stage_keep, stage_send, i)

        @pl.when(i < hidden)
        def _():
            pltpu.make_async_copy(stage_keep.at[i], down_keep.at[i], keep_sems.at[i]).start()
            pltpu.make_async_copy(stage_send.at[i], down_send.at[i], send_sems.at[i]).start()

        @pl.when(i >= hidden)
        def _():
            row = i - hidden
            pltpu.make_async_copy(stage_keep.at[i], up_keep.at[row], keep_sems.at[i]).start()
            pltpu.make_async_copy(stage_send.at[i], up_send.at[row], send_sems.at[i]).start()

        return 0

    lax.fori_loop(0, 2 * hidden + 1, weights, 0)
    for copy in puts:
        copy.wait()
    for i in range(2 * hidden + 1):
        if i < hidden:
            keep, gone, row = down_keep, down_send, i
        else:
            keep, gone, row = up_keep, up_send, i - hidden
        pltpu.make_async_copy(stage_keep.at[i], keep.at[row], keep_sems.at[i]).wait()
        pltpu.make_async_copy(stage_send.at[i], gone.at[row], send_sems.at[i]).wait()


def middle_call(limit, vectors, tokens, mixed, logs, cot, teach, arrays, plan, block, dp):
    rows = tokens.shape[0]
    hidden = FF // D
    narrow = jax.ShapeDtypeStruct((rows, D), low)
    wide = jax.ShapeDtypeStruct((rows, D), full)
    shape = (dp // 2, D // dp, D)
    parts = [jax.ShapeDtypeStruct((count,) + shape, low) for count in (hidden, hidden + 1)]
    stats = jax.ShapeDtypeStruct((PAIRS, 2, rows), full)
    anywhere = pl.BlockSpec(memory_space=pl.ANY)
    inside = pl.BlockSpec(memory_space=pltpu.VMEM)
    moves = sum(len(part) for part in plan)
    return pl.pallas_call(
        functools.partial(middle_kernel, plan, block, len(arrays)),
        out_shape=(
            narrow,
            wide,
            narrow,
            parts[0],
            parts[0],
            parts[1],
            parts[1],
            stats,
            stats,
            jax.ShapeDtypeStruct((8 + 8, D), full),
        ),
        in_specs=[pl.BlockSpec(memory_space=pltpu.SMEM), inside]
        + [anywhere] * (5 + len(arrays)),
        out_specs=[anywhere] * 7 + [inside] * 3,
        scratch_shapes=[
            pltpu.VMEM((rows, D), low),
            pltpu.VMEM((rows, D), full),
            pltpu.VMEM((rows, D), full),
            pltpu.VMEM((rows, D), low),
            pltpu.VMEM((rows, D), low),
            pltpu.VMEM((FF, D), low),
            pltpu.VMEM((FF, D), low),
            pltpu.VMEM((D, D), low),
            pltpu.VMEM((2 * hidden + 1, rows, D), low),
            pltpu.VMEM((hidden, rows, D), full),
            pltpu.VMEM((rows, D), low),
            pltpu.VMEM((rows, D), full),
            pltpu.VMEM((rows, D), full),
            pltpu.VMEM((rows, D), low),
            pltpu.VMEM((rows, D), low),
            pltpu.VMEM((rows, D), low),
            pltpu.VMEM((rows, D), low),
            pltpu.VMEM((rows, D), full),
            pltpu.VMEM((3, D, rows), low),
            pltpu.VMEM((2 * hidden + 1,) + shape, low),
            pltpu.VMEM((2 * hidden + 1,) + shape, low),
            pltpu.SemaphoreType.DMA((5,)),
            pltpu.SemaphoreType.DMA((moves,)),
            pltpu.SemaphoreType.DMA((3,)),
            pltpu.SemaphoreType.DMA((2 * hidden + 1,)),
            pltpu.SemaphoreType.DMA((2 * hidden + 1,)),
        ],
        compiler_params=pltpu.CompilerParams(vmem_limit_bytes=VMEM_LIMIT),
        cost_estimate=SMALL_COST,
        name="middle",
    )(limit, vectors, tokens, mixed, logs, cot, teach, *arrays)


def fold_block(keep, got, out_keep, out_send, bit, place):
    step = 1 << place
    mine = (lax.axis_index("dp") // bit) % 2 * step
    for j in range(keep.shape[1] // 2):
        base = (j // step) * 2 * step + j % step
        for out, shift in ((out_keep, mine), (out_send, step - mine)):
            value = keep[0, base + shift].astype(full) + got[0, base + shift].astype(full)
            out[0, j] = value.astype(low)


def fold_kernel(bits, places, *refs):
    count = len(bits)
    for n in range(count):
        fold_block(
            *refs[2 * n : 2 * n + 2],
            *refs[2 * count + 2 * n : 2 * count + 2 * n + 2],
            bits[n],
            places[n],
        )


def fold(pairs, bits, places):
    lead = pairs[0][0].shape[0]
    block = lambda shape: pl.BlockSpec((1,) + shape[1:], lambda i: (i, 0, 0, 0))
    halves = [
        (keep.shape[0], keep.shape[1] // 2) + keep.shape[2:] for keep, _ in pairs for _ in range(2)
    ]
    outs = pl.pallas_call(
        functools.partial(fold_kernel, bits, places),
        out_shape=[jax.ShapeDtypeStruct(shape, low) for shape in halves],
        grid=(lead,),
        in_specs=[block(value.shape) for pair in pairs for value in pair],
        out_specs=[block(shape) for shape in halves],
        compiler_params=pltpu.CompilerParams(vmem_limit_bytes=VMEM_LIMIT),
        cost_estimate=pl.CostEstimate(flops=0, bytes_accessed=16 << 20, transcendentals=0),
        name="fold",
    )(*[value for pair in pairs for value in pair])
    return [(outs[2 * n], outs[2 * n + 1]) for n in range(len(pairs))]


def qkv_grad_kernel(count, *refs):
    sources = refs[: 3 * count + 1]
    outs = refs[3 * count + 1 : 3 * count + 5]
    sum_ref, held, turned, total, stage, in_sems, out_sems = refs[3 * count + 5 :]
    first_use = [0, count] + list(range(1, count)) + list(range(count + 1, 3 * count + 1))
    for n in first_use:
        pltpu.make_async_copy(sources[n], held.at[n], in_sems.at[n]).start()

    def wait(n):
        pltpu.make_async_copy(sources[0], held.at[n], in_sems.at[n]).wait()

    def turn(n, _):
        wait(n)
        turned[n] = held[n].T
        return 0

    lax.fori_loop(0, count, turn, 0)
    sum_ref[...] = jnp.zeros_like(sum_ref)

    def step(i, _):
        c = (i + count - 1) // count
        n = jnp.where(i == 0, 0, (i + count - 1) % count)
        wait(count + i)
        right = held[count + i]
        value = dot_of(turned[n], right, 1, 0)
        total[...] = value + jnp.where(n == 0, jnp.zeros_like(value), total[...])

        @pl.when(c != 1)
        def _():
            row = pl.ds(pl.multiple_of(c * 4, 8), 1)
            sum_ref[row, :] += jnp.sum(right.astype(full), axis=0, keepdims=True)

        @pl.when(i % count == 0)
        def _():
            for part in range(2):
                store_split(
                    total[:, part * D // 2 : (part + 1) * D // 2],
                    stage.at[part],
                    stage.at[2 + part],
                    c,
                )
            for k in range(4):
                pltpu.make_async_copy(
                    stage.at[k, c], outs[k].at[c], out_sems.at[k * 3 + c]
                ).start()

        return 0

    lax.fori_loop(0, 2 * count + 1, step, 0)
    for k in range(4):
        for c in range(3):
            pltpu.make_async_copy(stage.at[k, c], outs[k].at[c], out_sems.at[k * 3 + c]).wait()


def qkv_grads(chunks, query_grad, key_grads, value_grads, dp):
    rows = query_grad.shape[0]
    count = len(chunks)
    shape = (3, dp // 2, D // dp, D // 2)
    anywhere = pl.BlockSpec(memory_space=pl.ANY)
    return pl.pallas_call(
        functools.partial(qkv_grad_kernel, count),
        out_shape=[jax.ShapeDtypeStruct(shape, low)] * 4
        + [jax.ShapeDtypeStruct((16, D), full)],
        in_specs=[anywhere] * (3 * count + 1),
        out_specs=[anywhere] * 4 + [pl.BlockSpec(memory_space=pltpu.VMEM)],
        scratch_shapes=[
            pltpu.VMEM((3 * count + 1, rows, D), low),
            pltpu.VMEM((count, D, rows), low),
            pltpu.VMEM((D, D), full),
            pltpu.VMEM((4,) + shape, low),
            pltpu.SemaphoreType.DMA((3 * count + 1,)),
            pltpu.SemaphoreType.DMA((12,)),
        ],
        compiler_params=pltpu.CompilerParams(vmem_limit_bytes=VMEM_LIMIT),
        cost_estimate=SMALL_COST,
        name="qkv_grads",
    )(*chunks, query_grad, *key_grads, *value_grads)


def last_kernel(
    token_ref,
    first_ref,
    right_ref,
    left_ref,
    middle_ref,
    vector_ref,
    gain_ref,
    bias_ref,
    sum_ref,
    out_ref,
    pack_ref,
):
    @pl.when(pl.program_id(0) == 0)
    def _():
        pack_ref[...] = jnp.zeros_like(pack_ref)
        pack_ref[1:2, :] = sum_ref[0:1, :]
        pack_ref[3:4, :] = sum_ref[1:2, :]
        pack_ref[4:5, :] = bias_ref[0:1, :]
        pack_ref[5:6, :] = bias_ref[8:9, :]
        pack_ref[6:8, :] = sum_ref[2:4, :]
        pack_ref[8 : 8 + FF // D, :] = sum_ref[8 : 8 + FF // D, :]

    unit, inverse = norm_stats(token_ref[...].astype(full) + vector_ref[0:1, :])
    grad = first_ref[...] + right_ref[...].astype(full) + left_ref[...].astype(full)
    scaled = grad * gain_ref[0:1, :]
    mean_scaled = jnp.mean(scaled, axis=-1, keepdims=True)
    mean_unit = jnp.mean(scaled * unit, axis=-1, keepdims=True)
    result = middle_ref[...] + inverse * (scaled - mean_scaled - unit * mean_unit)
    out_ref[...] = result
    pack_ref[0:1, :] += jnp.sum(grad * unit, axis=0, keepdims=True)
    pack_ref[2:3, :] += jnp.sum(grad, axis=0, keepdims=True)
    pack_ref[pl.ds(16 + lax.axis_index("dp"), 1), :] += jnp.sum(result, axis=0, keepdims=True)


def last_norm(tokens, first, right, left, middle_grad, vectors, gains, bias_sums, sums, dp):
    rows = tokens.shape[0]
    part = pl.BlockSpec((rows // 4, D), lambda i: (i, 0))
    whole = lambda value: pl.BlockSpec(value.shape, lambda i: (0, 0))
    small = (vectors, gains, bias_sums, sums)
    return pl.pallas_call(
        last_kernel,
        out_shape=(
            jax.ShapeDtypeStruct((rows, D), full),
            jax.ShapeDtypeStruct((16 + dp, D), full),
        ),
        grid=(4,),
        in_specs=[part] * 5 + [whole(value) for value in small],
        out_specs=[part, pl.BlockSpec((16 + dp, D), lambda i: (0, 0))],
        compiler_params=pltpu.CompilerParams(vmem_limit_bytes=VMEM_LIMIT),
        cost_estimate=SMALL_COST,
        name="last_norm",
    )(tokens, first, right, left, middle_grad, *small)


def two_parts(value, axis, mine):
    keep = lax.dynamic_index_in_dim(value, mine, axis, keepdims=False)
    send = lax.dynamic_index_in_dim(value, 1 - mine, axis, keepdims=False)
    return keep, send.astype(low)


class Scatter:
    def __init__(self, parts, turns):
        self.bits = outer_bits()
        half = len(self.bits) // 2
        self.orders = [
            [1] + self.bits[half * (turn % 2) :] + self.bits[: half * (turn % 2)] for turn in turns
        ]
        self.left = [list(self.bits) for _ in turns]
        self.step = 0
        self.parts = parts

    def sends(self):
        return [send for _, send in self.parts]

    def exchange(self, sends):
        self.pairs = [
            (keep, swap(send, "dp", turn[self.step]))
            for (keep, _), send, turn in zip(self.parts, sends, self.orders)
        ]
        self.step += 1

    def folds(self):
        if self.step > len(self.bits):
            return [], [], []
        bits = [turn[self.step] for turn in self.orders]
        places = []
        for left, bit in zip(self.left, bits):
            places.append(left.index(bit))
            left.remove(bit)
        return self.pairs, bits, places

    def give(self, outs):
        self.parts = [(outs[n], outs[n + 1]) for n in range(0, len(outs), 2)]

    def fold(self):
        outs = []
        for pair, bit, at in zip(*self.folds()):
            outs += fold([pair], [bit], [at])[0]
        self.give(outs)

    def advance(self, order):
        sends = order(*self.sends())
        self.exchange(list(sends) if len(self.parts) > 1 else [sends])

    def finish(self, order):
        while self.step <= len(self.bits):
            self.fold()
            self.advance(order)
        got = order(*[other for _, other in self.pairs])
        return [
            (keep.astype(full) + other.astype(full))[:, 0]
            for (keep, _), other in zip(self.pairs, got)
        ]


def scatter_dp(parts, turns):
    scatter = Scatter(parts, turns)
    while True:
        sends = yield scatter.sends()
        scatter.exchange(sends)
        if scatter.step > len(scatter.bits):
            break
        scatter.parts = fold(*scatter.folds())
    got = yield [other for _, other in scatter.pairs]
    return [
        (keep.astype(full) + other.astype(full))[:, 0]
        for (keep, _), other in zip(scatter.pairs, got)
    ]


def scatter_mp(value):
    rank = lax.axis_index("mp")
    part = lambda index: lax.dynamic_index_in_dim(value, index, keepdims=False)
    sends = yield [part(rank ^ bit).astype(low) for bit in (1, 2, 3)]
    got = yield [swap(send, "mp", bit) for bit, send in zip((1, 2, 3), sends)]
    got = [other.astype(full) for other in got]
    return (part(rank) + got[0]) + (got[1] + got[2])


def halve_mp(value):
    rank = lax.axis_index("mp")
    pairs = value.reshape((2, 2) + value.shape[1:])
    keep, send = two_parts(pairs, 1, rank % 2)
    (send,) = yield [send]
    (got,) = yield [swap(send, "mp", 1)]
    keep, send = two_parts(keep.astype(full) + got.astype(full), 0, rank // 2)
    (send,) = yield [send]
    (got,) = yield [swap(send, "mp", 2)]
    return keep + got.astype(full)


def scatter_feed(up_own, down_own):
    mp = lax.axis_size("mp")
    block = down_own.shape[1]
    out_own = up_own[mp].reshape(block, mp, -1).transpose(1, 0, 2)
    own = yield from halve_mp(
        jnp.concatenate([up_own[:mp], down_own, out_own.reshape(mp, -1, D)], axis=1)
    )
    return own[:block], own[block : 2 * block].T, own[2 * block :].reshape(block, -1).T


def scatter_qkv(keep_left, keep_right, send_left, send_right):
    left_part, right_part = yield from scatter_dp(
        [(keep_left, send_left), (keep_right, send_right)], (0, 1)
    )
    width = D // lax.axis_size("mp")
    parts = [part[..., at : at + width] for part in (left_part, right_part) for at in (0, width)]
    return (yield from scatter_mp(jnp.stack(parts)))


def sum_small(value):
    (value,) = yield [value]
    value = value + swap(value, "dp", 1)
    bits = outer_bits()
    groups = [("dp", bits[n : n + 2]) for n in range(0, len(bits), 2)] + [("mp", [1, 2])]
    for axis, pair in groups:
        (value,) = yield [value]
        if len(pair) == 1:
            value = value + swap(value, axis, pair[0])
        else:
            one, two = pair
            got = [swap(value, axis, mask) for mask in (one, two, one + two)]
            if axis == "mp":
                got = yield got
            value = (value + got[0]) + (got[1] + got[2])
    return value


class Steps:
    def __init__(self, steps):
        self.steps = steps
        self.pending = next(steps)
        self.result = None

    def advance(self, order):
        if self.pending is None:
            return
        sends = order(*self.pending)
        sends = [sends] if len(self.pending) == 1 else list(sends)
        try:
            self.pending = self.steps.send(sends)
        except StopIteration as stop:
            self.pending = None
            self.result = stop.value

    def finish(self, order):
        while self.pending is not None:
            self.advance(order)
        return self.result


def shards(
    tokens_in,
    timesteps,
    lengths,
    time_table,
    norm_gains,
    norm_biases,
    w_qkv,
    qv_bias,
    w_out,
    out_bias,
    w_up,
    up_bias,
    w_down,
    down_bias,
    cotangent,
    teacher,
):
    rank = lax.axis_index("mp")
    data_rank = lax.axis_index("dp")
    mp = lax.axis_size("mp")
    dp = lax.axis_size("dp")
    own_rows = tokens_in.shape[0]
    length = lax.dynamic_index_in_dim(lengths, data_rank, keepdims=False)
    own_time = lax.dynamic_index_in_dim(timesteps, data_rank, keepdims=False)
    odd = rank % 2 == 1
    upper = rank >= 2
    middle = jnp.logical_or(rank == 1, rank == 2)
    order = Order()
    along = lambda value, pairs: lax.ppermute(value, "mp", pairs)

    block = w_qkv.shape[1]
    aligned = block % 32 == 0
    narrow = order(jnp.concatenate([w_qkv.reshape(3 * block, -1), w_out.T]))
    first_swap = swap(narrow, "mp", 1)
    tall = order(jnp.concatenate([w_up, w_down.T]))
    tall_swap = swap(tall, "mp", 1)
    pair = order(
        jnp.concatenate(
            [jnp.where(odd, first_swap, narrow), jnp.where(odd, narrow, first_swap)], axis=1
        )
    )
    second_swap = swap(pair, "mp", 2)
    tokens, lengths, own_time, norm_gains, norm_biases, out_bias, down_bias, up_bias, length = order(
        tokens_in, lengths, own_time, norm_gains, norm_biases, out_bias, down_bias, up_bias, length
    )
    table_row = lax.dynamic_slice_in_dim(time_table, own_time, 1).astype(full)
    unit_one, _ = norm_stats(tokens.astype(full) + table_row)
    first_norm = (unit_one * norm_gains[0] + norm_biases[0]).astype(low)
    loss_weight = lengths.shape[0] * MAXLEN / jnp.sum(lengths).astype(full)
    vectors = jnp.concatenate(
        [
            table_row,
            out_bias[None],
            norm_gains[1:2],
            norm_biases[1:2],
            down_bias[None],
            jnp.full((3, D), loss_weight),
            up_bias.reshape(-1, D),
            jnp.zeros((4, D), full),
        ]
    )
    scalars = jnp.stack(
        [
            rank,
            jnp.where(rank == 0, 1, rank - 1),
            jnp.where(upper, rank - 2, rank + 2),
            jnp.where(middle, rank + 1, 3 - rank),
            length,
            length - rank * own_rows,
        ]
    ).astype(jnp.int32)
    first_norm, vectors, scalars = order(first_norm, vectors, scalars)
    wide = jnp.concatenate(
        [jnp.where(upper, second_swap, pair), jnp.where(upper, pair, second_swap)], axis=1
    )
    qkv_rows, out_rows = wide[: 3 * block], wide[3 * block :]
    if aligned:
        split = 3 * block // 2
        qkv_gather = Gather([qkv_rows[:split], qkv_rows[split:]])
        qkv_gather.advance(order)
    tall = order(jnp.concatenate([tall, tall_swap]))
    tall_across = along(tall, [(1, 2), (2, 1)])

    sent = order(first_norm)
    from_left = along(sent, [(0, 1), (1, 2), (2, 3)])
    from_right = along(sent, [(1, 0), (2, 1), (3, 2)])
    tall_across = order(tall_across)
    tall_far = along(tall_across, [(1, 0), (2, 3)])
    if aligned:
        while qkv_gather.step < len(qkv_gather.bits):
            qkv_gather.advance(order)
        qkv_gather.advance(order)
    hop_right, hop_left = order(from_left, from_right)
    second_right = along(hop_right, [(1, 2), (2, 3)])
    second_left = along(hop_left, [(1, 0), (2, 1)])
    if aligned:
        arrays, plan = plan_of(
            qkv_gather.result,
            [
                [(0, block, 0, 0, 0, 0), (block, split - block, 1, 0, 0, 0)],
                [
                    (0, 2 * block - split, 1, 0, 0, split - block),
                    (2 * block - split, block, 1, 1, 0, 0),
                ],
            ],
        )
        query_weight, pair_weight = order(*place(arrays, plan, block, [(D, D), (D, 2 * D)]))
        tall_other = jnp.where(middle, tall_across, order(tall_far))
        feed_gather = Gather(
            [
                jnp.concatenate([tall, out_rows[: block // 2]]),
                jnp.concatenate([tall_other, out_rows[block // 2 :]]),
            ]
        )
        feed_gather.advance(order)
    else:
        weights = lax.all_gather(qkv_rows.reshape(3, block, D), "dp", axis=1, tiled=True)
        query_weight = weights[0]
        pair_weight = jnp.concatenate([weights[1], weights[2]], axis=1)
    near = jnp.where(rank == 0, hop_left, hop_right)
    attend = lambda parts, numbers, carried: order(
        *attend_forward(
            parts,
            numbers,
            scalars,
            query_weight,
            pair_weight,
            qv_bias[0:1],
            qv_bias[1:2],
            carried,
        )
    )
    key_own, value_own, queries, *state = attend([order(first_norm)], (0,), None)
    second_right, second_left = order(second_right, second_left)
    second = order(jnp.where(upper, second_right, second_left))
    third = along(second, [(1, 0), (2, 3)])
    if aligned:
        while feed_gather.step < len(feed_gather.bits):
            feed_gather.advance(order)
        feed_gather.send_early(order)
    near, second = order(near, second)
    key_near, key_second, value_near, value_second, *state = attend(
        [near, second], (1, 2), (queries, *state)
    )
    last = order(jnp.where(middle, hop_left, order(third)))
    key_last, value_last, mixed, logs = attend([order(last)], (3,), (queries, *state))
    if aligned:
        feed_gather.advance(order)
        layout = lambda masks, shift: [
            (0, block, 0, masks[0], D, 0),
            (block, block, 1, masks[0], D, 0),
            (2 * block, block, 0, masks[1], D, 0),
            (3 * block, block, 1, masks[1], D, 0),
            (4 * block, block // 2, 2, 0, 0, shift),
        ]
        arrays, plan = plan_of(
            feed_gather.result, [layout((0, 1), 0), layout((2, 3), block // 2)]
        )
    else:
        arrays = [
            lax.all_gather(w_up, ("mp", "dp"), axis=0, tiled=True),
            lax.all_gather(w_down.T, ("mp", "dp"), axis=0, tiled=True),
            lax.all_gather(out_rows, "dp", axis=0, tiled=True),
        ]
        plan = [[(0, array.shape[0], n, None, 0, 0, 0)] for n, array in enumerate(arrays)]
    chunks = [first_norm, near, second, last]
    keys = [key_own, key_near, key_second, key_last]
    values = [value_own, value_near, value_second, value_last]

    output, middle_grad, attended_grad, *parts, deltas, log_rows, sums = middle_call(
        scalars, vectors, tokens, mixed, logs, cotangent, teacher, arrays, plan, block, dp
    )
    scatter = Scatter([(parts[0], parts[1]), (parts[2], parts[3])], (1, 0))
    scatter.advance(order)

    key_grads = [None] * 4
    value_grads = [None] * 4
    firsts = [None] * 4
    query_grad = None
    for n in (3, 2, 1, 0):
        pairs, bits, places = scatter.folds() if n % 2 == 0 else ([], [], [])
        query_grad, key_grads[n], value_grads[n], firsts[n], *folded = attend_backward(
            n,
            queries,
            keys[n],
            values[n],
            order(attended_grad),
            log_rows,
            deltas,
            query_weight,
            pair_weight,
            scalars,
            query_grad,
            n == 0,
            pairs,
            bits,
            places,
        )
        firsts[n] = order(firsts[n])
        if folded:
            scatter.give(folded)
        if n == 3:
            back_last = along(firsts[3], [(0, 1), (3, 2)]).astype(full)
        elif n == 2:
            scatter.advance(order)
            payload = order((firsts[2] + back_last).astype(low))
            back_right = along(payload, [(0, 1), (1, 2)]).astype(full)
            back_left = along(payload, [(3, 2), (2, 1)]).astype(full)
        elif n == 1:
            to_right = jnp.where(
                rank == 0, firsts[1], firsts[3].astype(full) + back_right
            ).astype(low)
            to_left = (firsts[1] + back_left).astype(low)
            to_right, to_left = order(to_right, to_left)
            final_right = along(to_right, [(0, 1), (1, 2), (2, 3)])
            final_left = along(to_left, [(3, 2), (2, 1), (1, 0)])
    scatter.advance(order)
    query_grad, final_right, final_left = order(query_grad, final_right, final_left)
    *halves, bias_sums = qkv_grads(chunks, query_grad, key_grads, value_grads, dp)
    qkv = Steps(scatter_qkv(*halves))
    qkv.advance(order)
    down_own, up_own = scatter.finish(order)
    feed = Steps(scatter_feed(up_own, down_own))
    feed.advance(order)
    qkv.advance(order)
    tokens, first_own = order(tokens, firsts[0])
    input_grad, packed = last_norm(
        tokens,
        first_own,
        final_right,
        final_left,
        middle_grad,
        vectors,
        norm_gains,
        bias_sums,
        sums,
        dp,
    )
    packed, input_grad = order(packed, input_grad)
    small = Steps(sum_small(packed))
    feed.advance(order)
    feed.advance(order)
    small.advance(order)
    qkv.advance(order)
    qkv.advance(order)
    small.advance(order)
    qkv.advance(order)
    small.advance(order)
    total = small.finish(order)
    up_grad, down_grad, out_grad = feed.finish(order)
    qkv_grad = qkv.finish(order)
    fixed = 16
    chosen = (timesteps[None, :] == jnp.arange(time_table.shape[0])[:, None]).astype(full)
    table_grad = lax.dot_general(
        chosen,
        total[fixed:],
        (((1,), (0,)), ((), ())),
        precision=lax.Precision.HIGHEST,
        preferred_element_type=full,
    )
    return (
        output,
        input_grad,
        table_grad,
        total[0:2],
        total[2:4],
        qkv_grad,
        total[4:6],
        out_grad,
        total[6],
        up_grad,
        total[8 : 8 + FF // D].reshape(FF),
        down_grad,
        total[7],
    )


def solution(mesh):
    rows = P(both, None)
    placed = (
        rows,
        P(),
        P(),
        P(),
        P(),
        P(),
        P(None, "dp", "mp"),
        P(),
        P("mp", "dp"),
        P(),
        P("dp", "mp"),
        P(),
        P("mp", "dp"),
        P(),
        rows,
        rows,
    )
    return jax.shard_map(
        shards,
        mesh=mesh,
        in_specs=placed,
        out_specs=(
            rows,
            rows,
            P(),
            P(),
            P(),
            P(None, "dp", "mp"),
            P(),
            P("mp", "dp"),
            P(),
            P("dp", "mp"),
            P(),
            P("mp", "dp"),
            P(),
        ),
        check_vma=False,
    )
```

```python
import functools

import jax
import jax.numpy as jnp
from jax import lax
from jax.experimental import pallas as pl
from jax.experimental.pallas import tpu as pltpu
from jax.sharding import PartitionSpec as P

D = 768
HEADS = 12
HEAD_DIM = 64
FF = 3072
MAXLEN = 2048
PAIR = 2 * HEAD_DIM
PAIRS = HEADS // 2
VMEM_LIMIT = 58 << 20
SMALL_COST = pl.CostEstimate(flops=1 << 20, bytes_accessed=1 << 16, transcendentals=0)

far_below = -1e30
epsilon = 1e-05
score_scale = HEAD_DIM ** (-0.5)
low = jnp.bfloat16
full = jnp.float32
both = ("dp", "mp")


def norm_stats(values):
    center = values - jnp.mean(values, axis=-1, keepdims=True)
    spread = jnp.mean(center * center, axis=-1, keepdims=True)
    inverse = lax.rsqrt(spread + epsilon)
    return center * inverse, inverse


def dot_of(left_side, right_side, left_dim, right_dim):
    return lax.dot_general(
        left_side,
        right_side,
        (((left_dim,), (right_dim,)), ((), ())),
        preferred_element_type=full,
    )


def first_half(shape):
    return lax.broadcasted_iota(jnp.int32, shape, len(shape) - 1) < HEAD_DIM


def forward_kernel(numbers, first, final, scalars, *refs):
    count = len(numbers)
    chunk_refs = refs[:count]
    wk_ref, wv_ref, value_bias_ref = refs[count : count + 3]
    refs = refs[count + 3 :]
    if first:
        wq_ref, query_bias_ref = refs[:2]
        key_outs, value_outs = refs[2 : 2 + count], refs[2 + count : 2 + 2 * count]
        query_out, top_ref, sum_ref, acc_ref = refs[2 + 2 * count :]
        q_pair = (dot_of(chunk_refs[0][...], wq_ref[...], 1, 0) + query_bias_ref[...]).astype(low)
        q_pair = q_pair * jnp.asarray(score_scale, low)
        query_out[...] = q_pair
    else:
        q_ref, top_in, sum_in, acc_in = refs[:4]
        key_outs, value_outs = refs[4 : 4 + count], refs[4 + count : 4 + 2 * count]
        results = refs[4 + 2 * count :]
        q_pair = q_ref[...]
    weight = jnp.concatenate([wk_ref[...], wv_ref[...]], axis=1)
    keys = []
    values = []
    for n in range(count):
        both_parts = dot_of(chunk_refs[n][...], weight, 1, 0)
        keys.append(both_parts[:, :PAIR].astype(low))
        values.append((both_parts[:, PAIR:] + value_bias_ref[...]).astype(low))
        key_outs[n][...] = keys[n]
        value_outs[n][...] = values[n]
    rows = q_pair.shape[0]
    size = keys[0].shape[0]
    place = lax.broadcasted_iota(jnp.int32, (1, size), 1)
    lower = first_half((rows, PAIR))
    parts = []
    for half in range(2):
        kept = lower if half == 0 else jnp.logical_not(lower)
        q_half = jnp.where(kept, q_pair, jnp.zeros_like(q_pair))
        scores = []
        for n in range(count):
            bias = jnp.where(place + scalars[numbers[n]] * size < scalars[4], 0.0, far_below)
            scores.append(dot_of(q_half, keys[n], 1, 1) + bias)
        highest = functools.reduce(
            jnp.maximum, [jnp.max(score, axis=-1, keepdims=True) for score in scores]
        )
        totals = jnp.zeros_like(highest)
        mixed = jnp.zeros((rows, PAIR), full)
        for n in range(count):
            exp_scores = jnp.exp(scores[n] - highest)
            totals = totals + jnp.sum(exp_scores, axis=-1, keepdims=True)
            mixed = mixed + dot_of(exp_scores.astype(low), values[n], 1, 0)
        parts.append((highest, totals, mixed))
    top = jnp.where(lower, parts[0][0], parts[1][0])
    total = jnp.where(lower, parts[0][1], parts[1][1])
    mixed = jnp.where(lower, parts[0][2], parts[1][2])
    if first:
        top_ref[...] = top
        sum_ref[...] = total
        acc_ref[...] = mixed
    else:
        highest = jnp.maximum(top, top_in[...])
        here = jnp.exp(top - highest)
        before = jnp.exp(top_in[...] - highest)
        total = total * here + sum_in[...] * before
        mixed = mixed * here + acc_in[...] * before
        if final:
            results[0][...] = mixed / total
            results[1][...] = highest + jnp.log(total)
        else:
            results[0][...] = highest
            results[1][...] = total
            results[2][...] = mixed


def attend_forward(chunks, numbers, scalars, query_weight, pair_weight, query_bias, value_bias, carried):
    rows = chunks[0].shape[0]
    count = len(chunks)
    first = carried is None
    final = 3 in numbers
    column = lambda height, c: pl.BlockSpec((height, PAIR), lambda i, n: (0, c * PAIRS + i))
    whole = pl.BlockSpec((rows, D), lambda i, n: (0, 0))
    wide = jax.ShapeDtypeStruct((rows, D), full)
    narrow = jax.ShapeDtypeStruct((rows, D), low)
    extra = (query_weight, query_bias) if first else carried
    results = (narrow,) * first + (wide,) * (2 if final else 3)
    return pl.pallas_call(
        functools.partial(forward_kernel, numbers, first, final),
        out_shape=(narrow,) * (2 * count) + results,
        grid_spec=pltpu.PrefetchScalarGridSpec(
            num_scalar_prefetch=1,
            grid=(PAIRS,),
            in_specs=[whole] * count
            + [column(D, 0), column(D, 1), column(1, 0)]
            + ([column(D, 0), column(1, 0)] if first else [column(rows, 0)] * 4),
            out_specs=[column(rows, 0)] * (2 * count + len(results)),
        ),
        compiler_params=pltpu.CompilerParams(vmem_limit_bytes=VMEM_LIMIT),
        cost_estimate=SMALL_COST,
        name="attend_forward",
    )(scalars, *chunks, pair_weight, pair_weight, value_bias, *extra)


def backward_kernel(
    number,
    first,
    last,
    folds,
    scalars,
    q_ref,
    k_ref,
    v_ref,
    g_ref,
    log_ref,
    delta_ref,
    wk_ref,
    wv_ref,
    *refs
):
    if last:
        wq_ref = refs[0]
        refs = refs[1:]
    if not first:
        dq_in = refs[0]
        refs = refs[1:]
    count = len(folds)
    fold_ins, refs = refs[: 2 * count], refs[2 * count :]
    dq_ref, dk_ref, dv_ref, back_ref = refs[:4]
    fold_outs, accum = refs[4:-1], refs[-1]
    step = pl.program_id(0)
    for n, (lead, bit, at) in enumerate(folds):

        @pl.when(step < lead)
        def _():
            fold_block(
                *fold_ins[2 * n : 2 * n + 2], *fold_outs[2 * n : 2 * n + 2], bit, at
            )

    rows = q_ref.shape[0]
    keys = k_ref.shape[0]
    limit = scalars[4] - scalars[number] * keys
    q_pair = q_ref[...]
    g_pair = g_ref[...]
    k_pair = k_ref[...]
    v_pair = v_ref[...]
    lower = first_half((rows, PAIR))
    nothing = jnp.zeros((rows, PAIR), low)
    two_halves = lambda pair: jnp.concatenate(
        [jnp.where(lower, pair, nothing), jnp.where(lower, nothing, pair)]
    )
    queries = two_halves(q_pair)
    grads_out = two_halves(g_pair)
    row_of = lambda ref: jnp.concatenate([ref[0, 0:1, :], ref[0, 1:2, :]], axis=1)
    place = lax.broadcasted_iota(jnp.int32, (keys, 1), 0)
    bias = jnp.where(place < limit, 0.0, far_below)
    scores = dot_of(k_pair, queries, 1, 1) + bias
    prob_grad = dot_of(v_pair, grads_out, 1, 1)
    probs = jnp.exp(scores - row_of(log_ref))
    score_grad = (probs * (prob_grad - row_of(delta_ref))).astype(low)
    dv_low = dot_of(probs.astype(low), grads_out, 1, 0).astype(low)
    dk_low = dot_of(score_grad, queries, 1, 0).astype(low)
    turned = dot_of(k_pair.T, score_grad, 1, 0)
    upper_rows = lax.broadcasted_iota(jnp.int32, (PAIR, rows), 0) < HEAD_DIM
    dk_ref[...] = dk_low
    dv_ref[...] = dv_low
    grads = [dk_low, dv_low]
    weights = [wk_ref[...], wv_ref[...]]
    dq_all = jnp.where(upper_rows, turned[:, :rows], turned[:, rows:]).T
    if not first:
        dq_all = dq_all + dq_in[...]
    back = dot_of(jnp.concatenate(grads, axis=1), jnp.concatenate(weights, axis=1), 1, 1)
    if last:
        dq_low = (dq_all * score_scale).astype(low)
        dq_ref[...] = dq_low
        back = back + dot_of(dq_low, wq_ref[...], 1, 1)
    else:
        dq_ref[...] = dq_all

    @pl.when(step == 0)
    def _():
        accum[...] = back

    @pl.when(step > 0)
    def _():
        accum[...] += back

    @pl.when(step == PAIRS - 1)
    def _():
        back_ref[...] = accum[...].astype(back_ref.dtype)


def attend_backward(
    number,
    queries,
    keys,
    values,
    grads,
    logs,
    deltas,
    query_weight,
    pair_weight,
    scalars,
    carried,
    last,
    pairs,
    bits,
    places,
):
    rows, total = queries.shape[0], keys.shape[0]
    first = carried is None
    folds = [(keep.shape[0], bit, at) for (keep, _), bit, at in zip(pairs, bits, places)]
    halves = [
        (keep.shape[0], keep.shape[1] // 2) + keep.shape[2:] for keep, _ in pairs for _ in range(2)
    ]

    def by_lead(shape):
        end = shape[0] - 1
        return pl.BlockSpec((1,) + shape[1:], lambda i, n: (jnp.minimum(i, end), 0, 0, 0))

    column = lambda count, c: pl.BlockSpec((count, PAIR), lambda i, n: (0, c * PAIRS + i))
    stats = pl.BlockSpec((1, 2, rows), lambda i, n: (i, 0, 0))
    extra = (query_weight,) * last + (() if first else (carried,))
    extra_specs = [column(D, 0)] * last + ([] if first else [column(rows, 0)])
    return pl.pallas_call(
        functools.partial(backward_kernel, number, first, last, folds),
        out_shape=(
            jax.ShapeDtypeStruct((rows, D), low if last else full),
            jax.ShapeDtypeStruct((total, D), low),
            jax.ShapeDtypeStruct((total, D), low),
            jax.ShapeDtypeStruct((total, D), low if first else full),
            *[jax.ShapeDtypeStruct(shape, low) for shape in halves],
        ),
        grid_spec=pltpu.PrefetchScalarGridSpec(
            num_scalar_prefetch=1,
            grid=(PAIRS,),
            in_specs=[
                column(rows, 0),
                column(total, 0),
                column(total, 0),
                column(rows, 0),
                stats,
                stats,
                column(D, 0),
                column(D, 1),
            ]
            + extra_specs
            + [by_lead(value.shape) for pair in pairs for value in pair],
            out_specs=[
                column(rows, 0),
                column(total, 0),
                column(total, 0),
                pl.BlockSpec((total, D), lambda i, n: (0, 0)),
            ]
            + [by_lead(shape) for shape in halves],
            scratch_shapes=[pltpu.VMEM((total, D), full)],
        ),
        compiler_params=pltpu.CompilerParams(vmem_limit_bytes=VMEM_LIMIT),
        cost_estimate=SMALL_COST,
        name="attend_backward",
    )(
        scalars,
        queries,
        keys,
        values,
        grads,
        logs,
        deltas,
        pair_weight,
        pair_weight,
        *extra,
        *[value for pair in pairs for value in pair],
    )


def swap(value, axis, bit):
    count = lax.axis_size(axis)
    return lax.ppermute(value, axis, [(i, i ^ bit) for i in range(count)])


class Order:
    def __init__(self):
        self.marks = ()

    def __call__(self, *values):
        values = lax.optimization_barrier(values + self.marks)[: len(values)]
        self.marks = values
        return values[0] if len(values) == 1 else values


def outer_bits():
    bits = []
    bit = 2
    while bit < lax.axis_size("dp"):
        bits.append(bit)
        bit *= 2
    return bits


class Gather:
    def __init__(self, parts):
        self.bits = outer_bits()
        half = len(self.bits) // 2
        self.orders = [
            self.bits[half * (n % 2) :] + self.bits[: half * (n % 2)] for n in range(len(parts))
        ]
        self.result = [[([0], part)] for part in parts]
        self.step = 0
        self.early = []

    def advance(self, order):
        held = self.result
        if self.step < len(self.bits):
            masks = [[m for mask, _ in pieces for m in mask] for pieces in held]
            blocks = [
                jnp.concatenate([array for _, array in pieces]) if self.step else pieces[0][1]
                for pieces in held
            ]
            blocks = order(*blocks)
            bits = [turn[self.step] for turn in self.orders]
            self.result = [
                [(mask, block), ([m ^ bit for m in mask], swap(block, "dp", bit))]
                for mask, block, bit in zip(masks, blocks, bits)
            ]
        else:
            rest = [pieces[1:] if self.early else pieces for pieces in held]
            arrays = iter(order(*[array for pieces in rest for _, array in pieces]))
            self.result = []
            for n, pieces in enumerate(rest):
                kept = [(masks, next(arrays)) for masks, _ in pieces]
                ours = held[n][:1] + kept if self.early else kept
                theirs = [([m ^ 1 for m in masks], swap(array, "dp", 1)) for masks, array in kept]
                self.result.append(ours + self.early[n : n + 1] + theirs)
        self.step += 1

    def send_early(self, order):
        arrays = order(*[pieces[0][1] for pieces in self.result])
        self.early = [
            ([m ^ 1 for m in pieces[0][0]], swap(array, "dp", 1))
            for pieces, array in zip(self.result, arrays)
        ]


def canonical_row(me, rank, block, mask, rank_mask, stride, offset):
    if mask is None:
        return offset
    row = (me ^ mask) * block + offset
    if stride:
        if rank_mask >= 2:
            rank_mask = rank_mask ^ ((rank + 1) // 2 % 2)
        row = row + (rank ^ rank_mask) * stride
    return pl.multiple_of(row, 16)


def place_kernel(plan, block, *refs):
    count = len(plan)
    ins = refs[:count]
    outs = refs[count:-1]
    sems = refs[-1]
    me = lax.axis_index("dp")
    rank = lax.axis_index("mp")
    copies = []
    for ref, moves in zip(ins, plan):
        for start, size, which, mask, column, _, offset in moves:
            row = canonical_row(me, rank, block, mask, 0, 0, offset)
            copy = pltpu.make_async_copy(
                ref.at[pl.ds(start, size), :],
                outs[which].at[pl.ds(row, size), pl.ds(column * D, D)],
                sems.at[len(copies)],
            )
            copy.start()
            copies.append(copy)
    for copy in copies:
        copy.wait()


def plan_of(gathered, layouts):
    arrays = []
    plan = []
    for pieces, layout in zip(gathered, layouts):
        rows = sum(size for _, size, *_ in layout)
        for masks, array in pieces:
            moves = []
            for j, mask in enumerate(masks):
                for start, size, which, rank_mask, stride, offset in layout:
                    moves.append((j * rows + start, size, which, mask, rank_mask, stride, offset))
            arrays.append(array)
            plan.append(moves)
    return arrays, plan


def place(arrays, plan, block, shapes):
    return pl.pallas_call(
        functools.partial(place_kernel, plan, block),
        out_shape=[jax.ShapeDtypeStruct(shape, low) for shape in shapes],
        in_specs=[pl.BlockSpec(memory_space=pl.ANY)] * len(arrays),
        out_specs=[pl.BlockSpec(memory_space=pltpu.VMEM)] * len(shapes),
        scratch_shapes=[pltpu.SemaphoreType.DMA((sum(len(moves) for moves in plan),))],
        compiler_params=pltpu.CompilerParams(vmem_limit_bytes=VMEM_LIMIT),
        cost_estimate=SMALL_COST,
        name="place",
    )(*arrays)


def store_split(value, keep, send, index):
    block = keep.shape[2]
    even = lax.axis_index("dp") % 2 == 0
    for outer in range(keep.shape[1]):
        first = value[2 * outer * block : (2 * outer + 1) * block]
        other = value[(2 * outer + 1) * block : (2 * outer + 2) * block]
        keep[index, outer] = jnp.where(even, first, other).astype(low)
        send[index, outer] = jnp.where(even, other, first).astype(low)


def middle_kernel(plan, block, total, *refs):
    limit_ref, vector_ref = refs[:2]
    token_hbm, mixed_hbm, log_hbm, cot_hbm, teach_hbm = refs[2:7]
    pieces = refs[7 : 7 + total]
    (
        out_hbm,
        middle_hbm,
        grad_hbm,
        down_keep,
        down_send,
        up_keep,
        up_send,
        delta_ref,
        log_ref,
        sum_ref,
    ) = refs[7 + total : 17 + total]
    (
        token,
        mixed,
        logs,
        cot,
        teach,
        up,
        down,
        proj,
        right,
        slope,
        second,
        middle,
        final,
        out,
        final_low,
        middle_low,
        grad,
        accum,
        turned,
        stage_keep,
        stage_send,
        in_sems,
        weight_sems,
        out_sems,
        keep_sems,
        send_sems,
    ) = refs[17 + total :]
    hidden = FF // D
    targets = (up, down, proj)
    rows = token.shape[0]
    me = lax.axis_index("dp")
    rank = lax.axis_index("mp")

    def fetch(ref, scratch, n):
        copy = pltpu.make_async_copy(ref, scratch, in_sems.at[n])
        copy.start()
        return copy

    def send(scratch, ref, n):
        copy = pltpu.make_async_copy(scratch, ref, out_sems.at[n])
        copy.start()
        return copy

    gets = [
        fetch(token_hbm, token, 0),
        fetch(mixed_hbm, mixed, 1),
        fetch(log_hbm, logs, 2),
        fetch(cot_hbm, cot, 3),
        fetch(teach_hbm, teach, 4),
    ]
    loads = {0: [], 1: [], 2: []}
    number = 0
    for want in (2, 0, 1):
        for ref, moves in zip(pieces, plan):
            for start, size, which, mask, rank_mask, stride, offset in moves:
                if which != want:
                    continue
                row = canonical_row(me, rank, block, mask, rank_mask, stride, offset)
                copy = pltpu.make_async_copy(
                    ref.at[pl.ds(start, size), :],
                    targets[which].at[pl.ds(row, size), :],
                    weight_sems.at[number],
                )
                copy.start()
                loads[which].append(copy)
                number += 1

    table_row = vector_ref[0:1, :]
    out_bias = vector_ref[1:2, :]
    gain = vector_ref[2:3, :]
    shift = vector_ref[3:4, :]
    down_bias = vector_ref[4:5, :]
    weight = vector_ref[5:6, :]
    gets[0].wait()
    gets[1].wait()
    right[2 * hidden] = mixed[...].astype(low)
    for copy in loads[2]:
        copy.wait()
    state = token[...].astype(full) + table_row + out_bias
    state = state + dot_of(right[2 * hidden], proj[...], 1, 1)
    middle[...] = state
    unit, _ = norm_stats(state)
    second[...] = (unit * gain + shift).astype(low)
    accum[...] = jnp.zeros((rows, D), full)
    for copy in loads[0]:
        copy.wait()
    for copy in loads[1]:
        copy.wait()

    def forward(m, _):
        place = pl.ds(pl.multiple_of(m * D, D), D)
        value = dot_of(second[...], up[place, :], 1, 0) + vector_ref[pl.ds(8 + m, 1), :]
        cumulative = 0.5 + 0.5 * lax.erf(value * (0.5**0.5))
        right[m] = (value * cumulative).astype(low)
        slope[m] = cumulative + value * jnp.exp(-0.5 * value * value) * 0.3989422804014327
        accum[...] += dot_of(right[m], down[place, :], 1, 1)
        return 0

    lax.fori_loop(0, FF // D, forward, 0)
    final_state = middle[...] + accum[...] + down_bias
    out[...] = final_state.astype(low)
    puts = [send(out, out_hbm, 0)]
    gets[3].wait()
    gets[4].wait()
    place = lax.broadcasted_iota(jnp.int32, (rows, 1), 0)
    grads = cot[...].astype(full) + weight * (final_state - teach[...].astype(full))
    grads = jnp.where(place < limit_ref[5], grads, 0.0)
    final[...] = grads
    final_low[...] = grads.astype(low)
    sum_ref[3:4, :] = jnp.sum(grads, axis=0, keepdims=True)
    accum[...] = jnp.zeros((rows, D), full)

    def backward(m, _):
        place = pl.ds(pl.multiple_of(m * D, D), D)
        value = slope[m] * dot_of(final_low[...], down[place, :], 1, 0)
        value = value.astype(low)
        right[hidden + m] = value
        sum_ref[pl.ds(8 + m, 1), :] = jnp.sum(value.astype(full), axis=0, keepdims=True)
        accum[...] += dot_of(value, up[place, :], 1, 1)
        return 0

    lax.fori_loop(0, FF // D, backward, 0)
    unit, inverse = norm_stats(middle[...])
    second_grad = accum[...]
    sum_ref[0:1, :] = jnp.sum(second_grad * unit, axis=0, keepdims=True)
    sum_ref[1:2, :] = jnp.sum(second_grad, axis=0, keepdims=True)
    scaled = second_grad * gain
    mean_scaled = jnp.mean(scaled, axis=-1, keepdims=True)
    mean_unit = jnp.mean(scaled * unit, axis=-1, keepdims=True)
    total_grad = final[...] + inverse * (scaled - mean_scaled - unit * mean_unit)
    middle[...] = total_grad
    puts.append(send(middle, middle_hbm, 1))
    middle_low[...] = total_grad.astype(low)
    sum_ref[2:3, :] = jnp.sum(total_grad, axis=0, keepdims=True)
    attended_grad = dot_of(middle_low[...], proj[...], 1, 0).astype(low)
    grad[...] = attended_grad
    puts.append(send(grad, grad_hbm, 2))
    gets[2].wait()
    head = lax.broadcasted_iota(jnp.int32, (16, D), 0)
    lane = lax.broadcasted_iota(jnp.int32, (16, D), 1)
    member = jnp.where(lane // HEAD_DIM == head, 1.0, 0.0)
    leader = jnp.where(lane == head * HEAD_DIM, 1.0, 0.0)
    exact = functools.partial(
        lax.dot_general,
        dimension_numbers=(((1,), (1,)), ((), ())),
        precision=lax.Precision.HIGHEST,
        preferred_element_type=full,
    )
    deltas = exact(member, attended_grad.astype(full) * mixed[...])
    tops = exact(leader, logs[...])
    for pair in range(PAIRS):
        delta_ref[pair] = deltas[2 * pair : 2 * pair + 2]
        log_ref[pair] = tops[2 * pair : 2 * pair + 2]
    turned[0] = final_low[...].T
    turned[1] = second[...].T
    turned[2] = middle_low[...].T

    def weights(i, _):
        store_split(dot_of(turned[i // hidden], right[i], 1, 0), stage_keep, stage_send, i)

        @pl.when(i < hidden)
        def _():
            pltpu.make_async_copy(stage_keep.at[i], down_keep.at[i], keep_sems.at[i]).start()
            pltpu.make_async_copy(stage_send.at[i], down_send.at[i], send_sems.at[i]).start()

        @pl.when(i >= hidden)
        def _():
            row = i - hidden
            pltpu.make_async_copy(stage_keep.at[i], up_keep.at[row], keep_sems.at[i]).start()
            pltpu.make_async_copy(stage_send.at[i], up_send.at[row], send_sems.at[i]).start()

        return 0

    lax.fori_loop(0, 2 * hidden + 1, weights, 0)
    for copy in puts:
        copy.wait()
    for i in range(2 * hidden + 1):
        if i < hidden:
            keep, gone, row = down_keep, down_send, i
        else:
            keep, gone, row = up_keep, up_send, i - hidden
        pltpu.make_async_copy(stage_keep.at[i], keep.at[row], keep_sems.at[i]).wait()
        pltpu.make_async_copy(stage_send.at[i], gone.at[row], send_sems.at[i]).wait()


def middle_call(limit, vectors, tokens, mixed, logs, cot, teach, arrays, plan, block, dp):
    rows = tokens.shape[0]
    hidden = FF // D
    narrow = jax.ShapeDtypeStruct((rows, D), low)
    wide = jax.ShapeDtypeStruct((rows, D), full)
    shape = (dp // 2, D // dp, D)
    parts = [jax.ShapeDtypeStruct((count,) + shape, low) for count in (hidden, hidden + 1)]
    stats = jax.ShapeDtypeStruct((PAIRS, 2, rows), full)
    anywhere = pl.BlockSpec(memory_space=pl.ANY)
    inside = pl.BlockSpec(memory_space=pltpu.VMEM)
    moves = sum(len(part) for part in plan)
    return pl.pallas_call(
        functools.partial(middle_kernel, plan, block, len(arrays)),
        out_shape=(
            narrow,
            wide,
            narrow,
            parts[0],
            parts[0],
            parts[1],
            parts[1],
            stats,
            stats,
            jax.ShapeDtypeStruct((8 + 8, D), full),
        ),
        in_specs=[pl.BlockSpec(memory_space=pltpu.SMEM), inside]
        + [anywhere] * (5 + len(arrays)),
        out_specs=[anywhere] * 7 + [inside] * 3,
        scratch_shapes=[
            pltpu.VMEM((rows, D), low),
            pltpu.VMEM((rows, D), full),
            pltpu.VMEM((rows, D), full),
            pltpu.VMEM((rows, D), low),
            pltpu.VMEM((rows, D), low),
            pltpu.VMEM((FF, D), low),
            pltpu.VMEM((FF, D), low),
            pltpu.VMEM((D, D), low),
            pltpu.VMEM((2 * hidden + 1, rows, D), low),
            pltpu.VMEM((hidden, rows, D), full),
            pltpu.VMEM((rows, D), low),
            pltpu.VMEM((rows, D), full),
            pltpu.VMEM((rows, D), full),
            pltpu.VMEM((rows, D), low),
            pltpu.VMEM((rows, D), low),
            pltpu.VMEM((rows, D), low),
            pltpu.VMEM((rows, D), low),
            pltpu.VMEM((rows, D), full),
            pltpu.VMEM((3, D, rows), low),
            pltpu.VMEM((2 * hidden + 1,) + shape, low),
            pltpu.VMEM((2 * hidden + 1,) + shape, low),
            pltpu.SemaphoreType.DMA((5,)),
            pltpu.SemaphoreType.DMA((moves,)),
            pltpu.SemaphoreType.DMA((3,)),
            pltpu.SemaphoreType.DMA((2 * hidden + 1,)),
            pltpu.SemaphoreType.DMA((2 * hidden + 1,)),
        ],
        compiler_params=pltpu.CompilerParams(vmem_limit_bytes=VMEM_LIMIT),
        cost_estimate=SMALL_COST,
        name="middle",
    )(limit, vectors, tokens, mixed, logs, cot, teach, *arrays)


def fold_block(keep, got, out_keep, out_send, bit, place):
    step = 1 << place
    mine = (lax.axis_index("dp") // bit) % 2 * step
    for j in range(keep.shape[1] // 2):
        base = (j // step) * 2 * step + j % step
        for out, shift in ((out_keep, mine), (out_send, step - mine)):
            value = keep[0, base + shift].astype(full) + got[0, base + shift].astype(full)
            out[0, j] = value.astype(low)


def fold_kernel(bits, places, *refs):
    count = len(bits)
    for n in range(count):
        fold_block(
            *refs[2 * n : 2 * n + 2],
            *refs[2 * count + 2 * n : 2 * count + 2 * n + 2],
            bits[n],
            places[n],
        )


def fold(pairs, bits, places):
    lead = pairs[0][0].shape[0]
    block = lambda shape: pl.BlockSpec((1,) + shape[1:], lambda i: (i, 0, 0, 0))
    halves = [
        (keep.shape[0], keep.shape[1] // 2) + keep.shape[2:] for keep, _ in pairs for _ in range(2)
    ]
    outs = pl.pallas_call(
        functools.partial(fold_kernel, bits, places),
        out_shape=[jax.ShapeDtypeStruct(shape, low) for shape in halves],
        grid=(lead,),
        in_specs=[block(value.shape) for pair in pairs for value in pair],
        out_specs=[block(shape) for shape in halves],
        compiler_params=pltpu.CompilerParams(vmem_limit_bytes=VMEM_LIMIT),
        cost_estimate=pl.CostEstimate(flops=0, bytes_accessed=16 << 20, transcendentals=0),
        name="fold",
    )(*[value for pair in pairs for value in pair])
    return [(outs[2 * n], outs[2 * n + 1]) for n in range(len(pairs))]


def qkv_grad_kernel(count, *refs):
    sources = refs[: 3 * count + 1]
    outs = refs[3 * count + 1 : 3 * count + 5]
    sum_ref, held, turned, total, stage, in_sems, out_sems = refs[3 * count + 5 :]
    first_use = [0, count] + list(range(1, count)) + list(range(count + 1, 3 * count + 1))
    for n in first_use:
        pltpu.make_async_copy(sources[n], held.at[n], in_sems.at[n]).start()

    def wait(n):
        pltpu.make_async_copy(sources[0], held.at[n], in_sems.at[n]).wait()

    def turn(n, _):
        wait(n)
        turned[n] = held[n].T
        return 0

    lax.fori_loop(0, count, turn, 0)
    sum_ref[...] = jnp.zeros_like(sum_ref)

    def step(i, _):
        c = (i + count - 1) // count
        n = jnp.where(i == 0, 0, (i + count - 1) % count)
        wait(count + i)
        right = held[count + i]
        value = dot_of(turned[n], right, 1, 0)
        total[...] = value + jnp.where(n == 0, jnp.zeros_like(value), total[...])

        @pl.when(c != 1)
        def _():
            row = pl.ds(pl.multiple_of(c * 4, 8), 1)
            sum_ref[row, :] += jnp.sum(right.astype(full), axis=0, keepdims=True)

        @pl.when(i % count == 0)
        def _():
            for part in range(2):
                store_split(
                    total[:, part * D // 2 : (part + 1) * D // 2],
                    stage.at[part],
                    stage.at[2 + part],
                    c,
                )
            for k in range(4):
                pltpu.make_async_copy(
                    stage.at[k, c], outs[k].at[c], out_sems.at[k * 3 + c]
                ).start()

        return 0

    lax.fori_loop(0, 2 * count + 1, step, 0)
    for k in range(4):
        for c in range(3):
            pltpu.make_async_copy(stage.at[k, c], outs[k].at[c], out_sems.at[k * 3 + c]).wait()


def qkv_grads(chunks, query_grad, key_grads, value_grads, dp):
    rows = query_grad.shape[0]
    count = len(chunks)
    shape = (3, dp // 2, D // dp, D // 2)
    anywhere = pl.BlockSpec(memory_space=pl.ANY)
    return pl.pallas_call(
        functools.partial(qkv_grad_kernel, count),
        out_shape=[jax.ShapeDtypeStruct(shape, low)] * 4
        + [jax.ShapeDtypeStruct((16, D), full)],
        in_specs=[anywhere] * (3 * count + 1),
        out_specs=[anywhere] * 4 + [pl.BlockSpec(memory_space=pltpu.VMEM)],
        scratch_shapes=[
            pltpu.VMEM((3 * count + 1, rows, D), low),
            pltpu.VMEM((count, D, rows), low),
            pltpu.VMEM((D, D), full),
            pltpu.VMEM((4,) + shape, low),
            pltpu.SemaphoreType.DMA((3 * count + 1,)),
            pltpu.SemaphoreType.DMA((12,)),
        ],
        compiler_params=pltpu.CompilerParams(vmem_limit_bytes=VMEM_LIMIT),
        cost_estimate=SMALL_COST,
        name="qkv_grads",
    )(*chunks, query_grad, *key_grads, *value_grads)


def last_kernel(
    token_ref,
    first_ref,
    right_ref,
    left_ref,
    middle_ref,
    vector_ref,
    gain_ref,
    bias_ref,
    sum_ref,
    out_ref,
    pack_ref,
):
    @pl.when(pl.program_id(0) == 0)
    def _():
        pack_ref[...] = jnp.zeros_like(pack_ref)
        pack_ref[1:2, :] = sum_ref[0:1, :]
        pack_ref[3:4, :] = sum_ref[1:2, :]
        pack_ref[4:5, :] = bias_ref[0:1, :]
        pack_ref[5:6, :] = bias_ref[8:9, :]
        pack_ref[6:8, :] = sum_ref[2:4, :]
        pack_ref[8 : 8 + FF // D, :] = sum_ref[8 : 8 + FF // D, :]

    unit, inverse = norm_stats(token_ref[...].astype(full) + vector_ref[0:1, :])
    grad = first_ref[...] + right_ref[...].astype(full) + left_ref[...].astype(full)
    scaled = grad * gain_ref[0:1, :]
    mean_scaled = jnp.mean(scaled, axis=-1, keepdims=True)
    mean_unit = jnp.mean(scaled * unit, axis=-1, keepdims=True)
    result = middle_ref[...] + inverse * (scaled - mean_scaled - unit * mean_unit)
    out_ref[...] = result
    pack_ref[0:1, :] += jnp.sum(grad * unit, axis=0, keepdims=True)
    pack_ref[2:3, :] += jnp.sum(grad, axis=0, keepdims=True)
    pack_ref[pl.ds(16 + lax.axis_index("dp"), 1), :] += jnp.sum(result, axis=0, keepdims=True)


def last_norm(tokens, first, right, left, middle_grad, vectors, gains, bias_sums, sums, dp):
    rows = tokens.shape[0]
    part = pl.BlockSpec((rows // 4, D), lambda i: (i, 0))
    whole = lambda value: pl.BlockSpec(value.shape, lambda i: (0, 0))
    small = (vectors, gains, bias_sums, sums)
    return pl.pallas_call(
        last_kernel,
        out_shape=(
            jax.ShapeDtypeStruct((rows, D), full),
            jax.ShapeDtypeStruct((16 + dp, D), full),
        ),
        grid=(4,),
        in_specs=[part] * 5 + [whole(value) for value in small],
        out_specs=[part, pl.BlockSpec((16 + dp, D), lambda i: (0, 0))],
        compiler_params=pltpu.CompilerParams(vmem_limit_bytes=VMEM_LIMIT),
        cost_estimate=SMALL_COST,
        name="last_norm",
    )(tokens, first, right, left, middle_grad, *small)


def two_parts(value, axis, mine):
    keep = lax.dynamic_index_in_dim(value, mine, axis, keepdims=False)
    send = lax.dynamic_index_in_dim(value, 1 - mine, axis, keepdims=False)
    return keep, send.astype(low)


class Scatter:
    def __init__(self, parts, turns):
        self.bits = outer_bits()
        half = len(self.bits) // 2
        self.orders = [
            [1] + self.bits[half * (turn % 2) :] + self.bits[: half * (turn % 2)] for turn in turns
        ]
        self.left = [list(self.bits) for _ in turns]
        self.step = 0
        self.parts = parts

    def sends(self):
        return [send for _, send in self.parts]

    def exchange(self, sends):
        self.pairs = [
            (keep, swap(send, "dp", turn[self.step]))
            for (keep, _), send, turn in zip(self.parts, sends, self.orders)
        ]
        self.step += 1

    def folds(self):
        if self.step > len(self.bits):
            return [], [], []
        bits = [turn[self.step] for turn in self.orders]
        places = []
        for left, bit in zip(self.left, bits):
            places.append(left.index(bit))
            left.remove(bit)
        return self.pairs, bits, places

    def give(self, outs):
        self.parts = [(outs[n], outs[n + 1]) for n in range(0, len(outs), 2)]

    def fold(self):
        outs = []
        for pair, bit, at in zip(*self.folds()):
            outs += fold([pair], [bit], [at])[0]
        self.give(outs)

    def advance(self, order):
        sends = order(*self.sends())
        self.exchange(list(sends) if len(self.parts) > 1 else [sends])

    def finish(self, order):
        while self.step <= len(self.bits):
            self.fold()
            self.advance(order)
        got = order(*[other for _, other in self.pairs])
        return [
            (keep.astype(full) + other.astype(full))[:, 0]
            for (keep, _), other in zip(self.pairs, got)
        ]


def scatter_dp(parts, turns):
    scatter = Scatter(parts, turns)
    while True:
        sends = yield scatter.sends()
        scatter.exchange(sends)
        if scatter.step > len(scatter.bits):
            break
        scatter.parts = fold(*scatter.folds())
    got = yield [other for _, other in scatter.pairs]
    return [
        (keep.astype(full) + other.astype(full))[:, 0]
        for (keep, _), other in zip(scatter.pairs, got)
    ]


def scatter_mp(value):
    rank = lax.axis_index("mp")
    part = lambda index: lax.dynamic_index_in_dim(value, index, keepdims=False)
    sends = yield [part(rank ^ bit).astype(low) for bit in (1, 2, 3)]
    got = yield [swap(send, "mp", bit) for bit, send in zip((1, 2, 3), sends)]
    got = [other.astype(full) for other in got]
    return (part(rank) + got[0]) + (got[1] + got[2])


def halve_mp(value):
    rank = lax.axis_index("mp")
    pairs = value.reshape((2, 2) + value.shape[1:])
    keep, send = two_parts(pairs, 1, rank % 2)
    (send,) = yield [send]
    (got,) = yield [swap(send, "mp", 1)]
    keep, send = two_parts(keep.astype(full) + got.astype(full), 0, rank // 2)
    (send,) = yield [send]
    (got,) = yield [swap(send, "mp", 2)]
    return keep + got.astype(full)


def scatter_feed(up_own, down_own):
    mp = lax.axis_size("mp")
    block = down_own.shape[1]
    out_own = up_own[mp].reshape(block, mp, -1).transpose(1, 0, 2)
    own = yield from halve_mp(
        jnp.concatenate([up_own[:mp], down_own, out_own.reshape(mp, -1, D)], axis=1)
    )
    return own[:block], own[block : 2 * block].T, own[2 * block :].reshape(block, -1).T


def scatter_qkv(keep_left, keep_right, send_left, send_right):
    left_part, right_part = yield from scatter_dp(
        [(keep_left, send_left), (keep_right, send_right)], (0, 1)
    )
    width = D // lax.axis_size("mp")
    parts = [part[..., at : at + width] for part in (left_part, right_part) for at in (0, width)]
    return (yield from scatter_mp(jnp.stack(parts)))


def sum_small(value):
    (value,) = yield [value]
    value = value + swap(value, "dp", 1)
    bits = outer_bits()
    groups = [("dp", bits[n : n + 2]) for n in range(0, len(bits), 2)] + [("mp", [1, 2])]
    for axis, pair in groups:
        (value,) = yield [value]
        if len(pair) == 1:
            value = value + swap(value, axis, pair[0])
        else:
            one, two = pair
            got = [swap(value, axis, mask) for mask in (one, two, one + two)]
            if axis == "mp":
                got = yield got
            value = (value + got[0]) + (got[1] + got[2])
    return value


class Steps:
    def __init__(self, steps):
        self.steps = steps
        self.pending = next(steps)
        self.result = None

    def advance(self, order):
        if self.pending is None:
            return
        sends = order(*self.pending)
        sends = [sends] if len(self.pending) == 1 else list(sends)
        try:
            self.pending = self.steps.send(sends)
        except StopIteration as stop:
            self.pending = None
            self.result = stop.value

    def finish(self, order):
        while self.pending is not None:
            self.advance(order)
        return self.result


def shards(
    tokens_in,
    timesteps,
    lengths,
    time_table,
    norm_gains,
    norm_biases,
    w_qkv,
    qv_bias,
    w_out,
    out_bias,
    w_up,
    up_bias,
    w_down,
    down_bias,
    cotangent,
    teacher,
):
    rank = lax.axis_index("mp")
    data_rank = lax.axis_index("dp")
    mp = lax.axis_size("mp")
    dp = lax.axis_size("dp")
    own_rows = tokens_in.shape[0]
    length = lax.dynamic_index_in_dim(lengths, data_rank, keepdims=False)
    own_time = lax.dynamic_index_in_dim(timesteps, data_rank, keepdims=False)
    odd = rank % 2 == 1
    upper = rank >= 2
    middle = jnp.logical_or(rank == 1, rank == 2)
    order = Order()
    along = lambda value, pairs: lax.ppermute(value, "mp", pairs)

    block = w_qkv.shape[1]
    aligned = block % 32 == 0
    narrow = order(jnp.concatenate([w_qkv.reshape(3 * block, -1), w_out.T]))
    first_swap = swap(narrow, "mp", 1)
    tall = order(jnp.concatenate([w_up, w_down.T]))
    tall_swap = swap(tall, "mp", 1)
    pair = order(
        jnp.concatenate(
            [jnp.where(odd, first_swap, narrow), jnp.where(odd, narrow, first_swap)], axis=1
        )
    )
    second_swap = swap(pair, "mp", 2)
    tokens, lengths, own_time, norm_gains, norm_biases, out_bias, down_bias, up_bias, length = order(
        tokens_in, lengths, own_time, norm_gains, norm_biases, out_bias, down_bias, up_bias, length
    )
    table_row = lax.dynamic_slice_in_dim(time_table, own_time, 1).astype(full)
    unit_one, _ = norm_stats(tokens.astype(full) + table_row)
    first_norm = (unit_one * norm_gains[0] + norm_biases[0]).astype(low)
    loss_weight = lengths.shape[0] * MAXLEN / jnp.sum(lengths).astype(full)
    vectors = jnp.concatenate(
        [
            table_row,
            out_bias[None],
            norm_gains[1:2],
            norm_biases[1:2],
            down_bias[None],
            jnp.full((3, D), loss_weight),
            up_bias.reshape(-1, D),
            jnp.zeros((4, D), full),
        ]
    )
    scalars = jnp.stack(
        [
            rank,
            jnp.where(rank == 0, 1, rank - 1),
            jnp.where(upper, rank - 2, rank + 2),
            jnp.where(middle, rank + 1, 3 - rank),
            length,
            length - rank * own_rows,
        ]
    ).astype(jnp.int32)
    first_norm, vectors, scalars = order(first_norm, vectors, scalars)
    wide = jnp.concatenate(
        [jnp.where(upper, second_swap, pair), jnp.where(upper, pair, second_swap)], axis=1
    )
    qkv_rows, out_rows = wide[: 3 * block], wide[3 * block :]
    if aligned:
        split = 3 * block // 2
        qkv_gather = Gather([qkv_rows[:split], qkv_rows[split:]])
        qkv_gather.advance(order)
    tall = order(jnp.concatenate([tall, tall_swap]))
    tall_across = along(tall, [(1, 2), (2, 1)])

    sent = order(first_norm)
    from_left = along(sent, [(0, 1), (1, 2), (2, 3)])
    from_right = along(sent, [(1, 0), (2, 1), (3, 2)])
    tall_across = order(tall_across)
    tall_far = along(tall_across, [(1, 0), (2, 3)])
    if aligned:
        while qkv_gather.step < len(qkv_gather.bits):
            qkv_gather.advance(order)
        qkv_gather.advance(order)
    hop_right, hop_left = order(from_left, from_right)
    second_right = along(hop_right, [(1, 2), (2, 3)])
    second_left = along(hop_left, [(1, 0), (2, 1)])
    if aligned:
        arrays, plan = plan_of(
            qkv_gather.result,
            [
                [(0, block, 0, 0, 0, 0), (block, split - block, 1, 0, 0, 0)],
                [
                    (0, 2 * block - split, 1, 0, 0, split - block),
                    (2 * block - split, block, 1, 1, 0, 0),
                ],
            ],
        )
        query_weight, pair_weight = order(*place(arrays, plan, block, [(D, D), (D, 2 * D)]))
        tall_other = jnp.where(middle, tall_across, order(tall_far))
        feed_gather = Gather(
            [
                jnp.concatenate([tall, out_rows[: block // 2]]),
                jnp.concatenate([tall_other, out_rows[block // 2 :]]),
            ]
        )
        feed_gather.advance(order)
    else:
        weights = lax.all_gather(qkv_rows.reshape(3, block, D), "dp", axis=1, tiled=True)
        query_weight = weights[0]
        pair_weight = jnp.concatenate([weights[1], weights[2]], axis=1)
    near = jnp.where(rank == 0, hop_left, hop_right)
    attend = lambda parts, numbers, carried: order(
        *attend_forward(
            parts,
            numbers,
            scalars,
            query_weight,
            pair_weight,
            qv_bias[0:1],
            qv_bias[1:2],
            carried,
        )
    )
    key_own, value_own, queries, *state = attend([order(first_norm)], (0,), None)
    second_right, second_left = order(second_right, second_left)
    second = order(jnp.where(upper, second_right, second_left))
    third = along(second, [(1, 0), (2, 3)])
    if aligned:
        while feed_gather.step < len(feed_gather.bits):
            feed_gather.advance(order)
        feed_gather.send_early(order)
    near, second = order(near, second)
    key_near, key_second, value_near, value_second, *state = attend(
        [near, second], (1, 2), (queries, *state)
    )
    last = order(jnp.where(middle, hop_left, order(third)))
    key_last, value_last, mixed, logs = attend([order(last)], (3,), (queries, *state))
    if aligned:
        feed_gather.advance(order)
        layout = lambda masks, shift: [
            (0, block, 0, masks[0], D, 0),
            (block, block, 1, masks[0], D, 0),
            (2 * block, block, 0, masks[1], D, 0),
            (3 * block, block, 1, masks[1], D, 0),
            (4 * block, block // 2, 2, 0, 0, shift),
        ]
        arrays, plan = plan_of(
            feed_gather.result, [layout((0, 1), 0), layout((2, 3), block // 2)]
        )
    else:
        arrays = [
            lax.all_gather(w_up, ("mp", "dp"), axis=0, tiled=True),
            lax.all_gather(w_down.T, ("mp", "dp"), axis=0, tiled=True),
            lax.all_gather(out_rows, "dp", axis=0, tiled=True),
        ]
        plan = [[(0, array.shape[0], n, None, 0, 0, 0)] for n, array in enumerate(arrays)]
    chunks = [first_norm, near, second, last]
    keys = [key_own, key_near, key_second, key_last]
    values = [value_own, value_near, value_second, value_last]

    output, middle_grad, attended_grad, *parts, deltas, log_rows, sums = middle_call(
        scalars, vectors, tokens, mixed, logs, cotangent, teacher, arrays, plan, block, dp
    )
    scatter = Scatter([(parts[0], parts[1]), (parts[2], parts[3])], (1, 0))
    scatter.advance(order)

    key_grads = [None] * 4
    value_grads = [None] * 4
    firsts = [None] * 4
    query_grad = None
    for n in (3, 2, 1, 0):
        pairs, bits, places = scatter.folds() if n % 2 == 0 else ([], [], [])
        query_grad, key_grads[n], value_grads[n], firsts[n], *folded = attend_backward(
            n,
            queries,
            keys[n],
            values[n],
            order(attended_grad),
            log_rows,
            deltas,
            query_weight,
            pair_weight,
            scalars,
            query_grad,
            n == 0,
            pairs,
            bits,
            places,
        )
        firsts[n] = order(firsts[n])
        if folded:
            scatter.give(folded)
        if n == 3:
            back_last = along(firsts[3], [(0, 1), (3, 2)]).astype(full)
        elif n == 2:
            scatter.advance(order)
            payload = order((firsts[2] + back_last).astype(low))
            back_right = along(payload, [(0, 1), (1, 2)]).astype(full)
            back_left = along(payload, [(3, 2), (2, 1)]).astype(full)
        elif n == 1:
            to_right = jnp.where(
                rank == 0, firsts[1], firsts[3].astype(full) + back_right
            ).astype(low)
            to_left = (firsts[1] + back_left).astype(low)
            to_right, to_left = order(to_right, to_left)
            final_right = along(to_right, [(0, 1), (1, 2), (2, 3)])
            final_left = along(to_left, [(3, 2), (2, 1), (1, 0)])
    scatter.advance(order)
    query_grad, final_right, final_left = order(query_grad, final_right, final_left)
    *halves, bias_sums = qkv_grads(chunks, query_grad, key_grads, value_grads, dp)
    qkv = Steps(scatter_qkv(*halves))
    qkv.advance(order)
    down_own, up_own = scatter.finish(order)
    feed = Steps(scatter_feed(up_own, down_own))
    feed.advance(order)
    qkv.advance(order)
    tokens, first_own = order(tokens, firsts[0])
    input_grad, packed = last_norm(
        tokens,
        first_own,
        final_right,
        final_left,
        middle_grad,
        vectors,
        norm_gains,
        bias_sums,
        sums,
        dp,
    )
    packed, input_grad = order(packed, input_grad)
    small = Steps(sum_small(packed))
    feed.advance(order)
    feed.advance(order)
    small.advance(order)
    qkv.advance(order)
    feed.advance(order)
    qkv.advance(order)
    small.advance(order)
    qkv.advance(order)
    small.advance(order)
    total = small.finish(order)
    up_grad, down_grad, out_grad = feed.finish(order)
    qkv_grad = qkv.finish(order)
    fixed = 16
    chosen = (timesteps[None, :] == jnp.arange(time_table.shape[0])[:, None]).astype(full)
    table_grad = lax.dot_general(
        chosen,
        total[fixed:],
        (((1,), (0,)), ((), ())),
        precision=lax.Precision.HIGHEST,
        preferred_element_type=full,
    )
    return (
        output,
        input_grad,
        table_grad,
        total[0:2],
        total[2:4],
        qkv_grad,
        total[4:6],
        out_grad,
        total[6],
        up_grad,
        total[8 : 8 + FF // D].reshape(FF),
        down_grad,
        total[7],
    )


def solution(mesh):
    rows = P(both, None)
    placed = (
        rows,
        P(),
        P(),
        P(),
        P(),
        P(),
        P(None, "dp", "mp"),
        P(),
        P("mp", "dp"),
        P(),
        P("dp", "mp"),
        P(),
        P("mp", "dp"),
        P(),
        rows,
        rows,
    )
    return jax.shard_map(
        shards,
        mesh=mesh,
        in_specs=placed,
        out_specs=(
            rows,
            rows,
            P(),
            P(),
            P(),
            P(None, "dp", "mp"),
            P(),
            P("mp", "dp"),
            P(),
            P("dp", "mp"),
            P(),
            P("mp", "dp"),
            P(),
        ),
        check_vma=False,
    )
```

```python
import functools

import jax
import jax.numpy as jnp
from jax import lax
from jax.experimental import pallas as pl
from jax.experimental.pallas import tpu as pltpu
from jax.sharding import PartitionSpec as P

D = 768
HEADS = 12
HEAD_DIM = 64
FF = 3072
MAXLEN = 2048
PAIR = 2 * HEAD_DIM
PAIRS = HEADS // 2
VMEM_LIMIT = 58 << 20
SMALL_COST = pl.CostEstimate(flops=1 << 20, bytes_accessed=1 << 16, transcendentals=0)

far_below = -1e30
epsilon = 1e-05
score_scale = HEAD_DIM ** (-0.5)
low = jnp.bfloat16
full = jnp.float32
both = ("dp", "mp")


def norm_stats(values):
    center = values - jnp.mean(values, axis=-1, keepdims=True)
    spread = jnp.mean(center * center, axis=-1, keepdims=True)
    inverse = lax.rsqrt(spread + epsilon)
    return center * inverse, inverse


def dot_of(left_side, right_side, left_dim, right_dim):
    return lax.dot_general(
        left_side,
        right_side,
        (((left_dim,), (right_dim,)), ((), ())),
        preferred_element_type=full,
    )


def first_half(shape):
    return lax.broadcasted_iota(jnp.int32, shape, len(shape) - 1) < HEAD_DIM


def forward_kernel(numbers, first, final, scalars, *refs):
    count = len(numbers)
    chunk_refs = refs[:count]
    wk_ref, wv_ref, value_bias_ref = refs[count : count + 3]
    refs = refs[count + 3 :]
    if first:
        wq_ref, query_bias_ref = refs[:2]
        key_outs, value_outs = refs[2 : 2 + count], refs[2 + count : 2 + 2 * count]
        query_out, top_ref, sum_ref, acc_ref = refs[2 + 2 * count :]
        q_pair = (dot_of(chunk_refs[0][...], wq_ref[...], 1, 0) + query_bias_ref[...]).astype(low)
        q_pair = q_pair * jnp.asarray(score_scale, low)
        query_out[...] = q_pair
    else:
        q_ref, top_in, sum_in, acc_in = refs[:4]
        key_outs, value_outs = refs[4 : 4 + count], refs[4 + count : 4 + 2 * count]
        results = refs[4 + 2 * count :]
        q_pair = q_ref[...]
    weight = jnp.concatenate([wk_ref[...], wv_ref[...]], axis=1)
    keys = []
    values = []
    for n in range(count):
        both_parts = dot_of(chunk_refs[n][...], weight, 1, 0)
        keys.append(both_parts[:, :PAIR].astype(low))
        values.append((both_parts[:, PAIR:] + value_bias_ref[...]).astype(low))
        key_outs[n][...] = keys[n]
        value_outs[n][...] = values[n]
    rows = q_pair.shape[0]
    size = keys[0].shape[0]
    place = lax.broadcasted_iota(jnp.int32, (1, size), 1)
    lower = first_half((rows, PAIR))
    parts = []
    for half in range(2):
        kept = lower if half == 0 else jnp.logical_not(lower)
        q_half = jnp.where(kept, q_pair, jnp.zeros_like(q_pair))
        scores = []
        for n in range(count):
            bias = jnp.where(place + scalars[numbers[n]] * size < scalars[4], 0.0, far_below)
            scores.append(dot_of(q_half, keys[n], 1, 1) + bias)
        highest = functools.reduce(
            jnp.maximum, [jnp.max(score, axis=-1, keepdims=True) for score in scores]
        )
        totals = jnp.zeros_like(highest)
        mixed = jnp.zeros((rows, PAIR), full)
        for n in range(count):
            exp_scores = jnp.exp(scores[n] - highest)
            totals = totals + jnp.sum(exp_scores, axis=-1, keepdims=True)
            mixed = mixed + dot_of(exp_scores.astype(low), values[n], 1, 0)
        parts.append((highest, totals, mixed))
    top = jnp.where(lower, parts[0][0], parts[1][0])
    total = jnp.where(lower, parts[0][1], parts[1][1])
    mixed = jnp.where(lower, parts[0][2], parts[1][2])
    if first:
        top_ref[...] = top
        sum_ref[...] = total
        acc_ref[...] = mixed
    else:
        highest = jnp.maximum(top, top_in[...])
        here = jnp.exp(top - highest)
        before = jnp.exp(top_in[...] - highest)
        total = total * here + sum_in[...] * before
        mixed = mixed * here + acc_in[...] * before
        if final:
            results[0][...] = mixed / total
            results[1][...] = highest + jnp.log(total)
        else:
            results[0][...] = highest
            results[1][...] = total
            results[2][...] = mixed


def attend_forward(chunks, numbers, scalars, query_weight, pair_weight, query_bias, value_bias, carried):
    rows = chunks[0].shape[0]
    count = len(chunks)
    first = carried is None
    final = 3 in numbers
    column = lambda height, c: pl.BlockSpec((height, PAIR), lambda i, n: (0, c * PAIRS + i))
    whole = pl.BlockSpec((rows, D), lambda i, n: (0, 0))
    wide = jax.ShapeDtypeStruct((rows, D), full)
    narrow = jax.ShapeDtypeStruct((rows, D), low)
    extra = (query_weight, query_bias) if first else carried
    results = (narrow,) * first + (wide,) * (2 if final else 3)
    return pl.pallas_call(
        functools.partial(forward_kernel, numbers, first, final),
        out_shape=(narrow,) * (2 * count) + results,
        grid_spec=pltpu.PrefetchScalarGridSpec(
            num_scalar_prefetch=1,
            grid=(PAIRS,),
            in_specs=[whole] * count
            + [column(D, 0), column(D, 1), column(1, 0)]
            + ([column(D, 0), column(1, 0)] if first else [column(rows, 0)] * 4),
            out_specs=[column(rows, 0)] * (2 * count + len(results)),
        ),
        compiler_params=pltpu.CompilerParams(vmem_limit_bytes=VMEM_LIMIT),
        cost_estimate=SMALL_COST,
        name="attend_forward",
    )(scalars, *chunks, pair_weight, pair_weight, value_bias, *extra)


def backward_kernel(
    number,
    first,
    last,
    folds,
    scalars,
    q_ref,
    k_ref,
    v_ref,
    g_ref,
    log_ref,
    delta_ref,
    wk_ref,
    wv_ref,
    *refs
):
    if last:
        wq_ref = refs[0]
        refs = refs[1:]
    if not first:
        dq_in = refs[0]
        refs = refs[1:]
    count = len(folds)
    fold_ins, refs = refs[: 2 * count], refs[2 * count :]
    dq_ref, dk_ref, dv_ref, back_ref = refs[:4]
    fold_outs, accum = refs[4:-1], refs[-1]
    step = pl.program_id(0)
    for n, (lead, bit, at) in enumerate(folds):

        @pl.when(step < lead)
        def _():
            fold_block(
                *fold_ins[2 * n : 2 * n + 2], *fold_outs[2 * n : 2 * n + 2], bit, at
            )

    rows = q_ref.shape[0]
    keys = k_ref.shape[0]
    limit = scalars[4] - scalars[number] * keys
    q_pair = q_ref[...]
    g_pair = g_ref[...]
    k_pair = k_ref[...]
    v_pair = v_ref[...]
    lower = first_half((rows, PAIR))
    nothing = jnp.zeros((rows, PAIR), low)
    two_halves = lambda pair: jnp.concatenate(
        [jnp.where(lower, pair, nothing), jnp.where(lower, nothing, pair)]
    )
    queries = two_halves(q_pair)
    grads_out = two_halves(g_pair)
    row_of = lambda ref: jnp.concatenate([ref[0, 0:1, :], ref[0, 1:2, :]], axis=1)
    place = lax.broadcasted_iota(jnp.int32, (keys, 1), 0)
    bias = jnp.where(place < limit, 0.0, far_below)
    scores = dot_of(k_pair, queries, 1, 1) + bias
    prob_grad = dot_of(v_pair, grads_out, 1, 1)
    probs = jnp.exp(scores - row_of(log_ref))
    score_grad = (probs * (prob_grad - row_of(delta_ref))).astype(low)
    dv_low = dot_of(probs.astype(low), grads_out, 1, 0).astype(low)
    dk_low = dot_of(score_grad, queries, 1, 0).astype(low)
    turned = dot_of(k_pair.T, score_grad, 1, 0)
    upper_rows = lax.broadcasted_iota(jnp.int32, (PAIR, rows), 0) < HEAD_DIM
    dk_ref[...] = dk_low
    dv_ref[...] = dv_low
    grads = [dk_low, dv_low]
    weights = [wk_ref[...], wv_ref[...]]
    dq_all = jnp.where(upper_rows, turned[:, :rows], turned[:, rows:]).T
    if not first:
        dq_all = dq_all + dq_in[...]
    back = dot_of(jnp.concatenate(grads, axis=1), jnp.concatenate(weights, axis=1), 1, 1)
    if last:
        dq_low = (dq_all * score_scale).astype(low)
        dq_ref[...] = dq_low
        back = back + dot_of(dq_low, wq_ref[...], 1, 1)
    else:
        dq_ref[...] = dq_all

    @pl.when(step == 0)
    def _():
        accum[...] = back

    @pl.when(step > 0)
    def _():
        accum[...] += back

    @pl.when(step == PAIRS - 1)
    def _():
        back_ref[...] = accum[...].astype(back_ref.dtype)


def attend_backward(
    number,
    queries,
    keys,
    values,
    grads,
    logs,
    deltas,
    query_weight,
    pair_weight,
    scalars,
    carried,
    last,
    pairs,
    bits,
    places,
):
    rows, total = queries.shape[0], keys.shape[0]
    first = carried is None
    folds = [(keep.shape[0], bit, at) for (keep, _), bit, at in zip(pairs, bits, places)]
    halves = [
        (keep.shape[0], keep.shape[1] // 2) + keep.shape[2:] for keep, _ in pairs for _ in range(2)
    ]

    def by_lead(shape):
        end = shape[0] - 1
        return pl.BlockSpec((1,) + shape[1:], lambda i, n: (jnp.minimum(i, end), 0, 0, 0))

    column = lambda count, c: pl.BlockSpec((count, PAIR), lambda i, n: (0, c * PAIRS + i))
    stats = pl.BlockSpec((1, 2, rows), lambda i, n: (i, 0, 0))
    extra = (query_weight,) * last + (() if first else (carried,))
    extra_specs = [column(D, 0)] * last + ([] if first else [column(rows, 0)])
    return pl.pallas_call(
        functools.partial(backward_kernel, number, first, last, folds),
        out_shape=(
            jax.ShapeDtypeStruct((rows, D), low if last else full),
            jax.ShapeDtypeStruct((total, D), low),
            jax.ShapeDtypeStruct((total, D), low),
            jax.ShapeDtypeStruct((total, D), low if first else full),
            *[jax.ShapeDtypeStruct(shape, low) for shape in halves],
        ),
        grid_spec=pltpu.PrefetchScalarGridSpec(
            num_scalar_prefetch=1,
            grid=(PAIRS,),
            in_specs=[
                column(rows, 0),
                column(total, 0),
                column(total, 0),
                column(rows, 0),
                stats,
                stats,
                column(D, 0),
                column(D, 1),
            ]
            + extra_specs
            + [by_lead(value.shape) for pair in pairs for value in pair],
            out_specs=[
                column(rows, 0),
                column(total, 0),
                column(total, 0),
                pl.BlockSpec((total, D), lambda i, n: (0, 0)),
            ]
            + [by_lead(shape) for shape in halves],
            scratch_shapes=[pltpu.VMEM((total, D), full)],
        ),
        compiler_params=pltpu.CompilerParams(vmem_limit_bytes=VMEM_LIMIT),
        cost_estimate=SMALL_COST,
        name="attend_backward",
    )(
        scalars,
        queries,
        keys,
        values,
        grads,
        logs,
        deltas,
        pair_weight,
        pair_weight,
        *extra,
        *[value for pair in pairs for value in pair],
    )


def swap(value, axis, bit):
    count = lax.axis_size(axis)
    return lax.ppermute(value, axis, [(i, i ^ bit) for i in range(count)])


class Order:
    def __init__(self):
        self.marks = ()

    def __call__(self, *values):
        values = lax.optimization_barrier(values + self.marks)[: len(values)]
        self.marks = values
        return values[0] if len(values) == 1 else values


def outer_bits():
    bits = []
    bit = 2
    while bit < lax.axis_size("dp"):
        bits.append(bit)
        bit *= 2
    return bits


class Gather:
    def __init__(self, parts):
        self.bits = outer_bits()
        half = len(self.bits) // 2
        self.orders = [
            self.bits[half * (n % 2) :] + self.bits[: half * (n % 2)] for n in range(len(parts))
        ]
        self.result = [[([0], part)] for part in parts]
        self.step = 0
        self.early = []

    def advance(self, order):
        held = self.result
        if self.step < len(self.bits):
            masks = [[m for mask, _ in pieces for m in mask] for pieces in held]
            blocks = [
                jnp.concatenate([array for _, array in pieces]) if self.step else pieces[0][1]
                for pieces in held
            ]
            blocks = order(*blocks)
            bits = [turn[self.step] for turn in self.orders]
            self.result = [
                [(mask, block), ([m ^ bit for m in mask], swap(block, "dp", bit))]
                for mask, block, bit in zip(masks, blocks, bits)
            ]
        else:
            rest = [pieces[1:] if self.early else pieces for pieces in held]
            arrays = iter(order(*[array for pieces in rest for _, array in pieces]))
            self.result = []
            for n, pieces in enumerate(rest):
                kept = [(masks, next(arrays)) for masks, _ in pieces]
                ours = held[n][:1] + kept if self.early else kept
                theirs = [([m ^ 1 for m in masks], swap(array, "dp", 1)) for masks, array in kept]
                self.result.append(ours + self.early[n : n + 1] + theirs)
        self.step += 1

    def send_early(self, order):
        arrays = order(*[pieces[0][1] for pieces in self.result])
        self.early = [
            ([m ^ 1 for m in pieces[0][0]], swap(array, "dp", 1))
            for pieces, array in zip(self.result, arrays)
        ]


def canonical_row(me, rank, block, mask, rank_mask, stride, offset):
    if mask is None:
        return offset
    row = (me ^ mask) * block + offset
    if stride:
        if rank_mask >= 2:
            rank_mask = rank_mask ^ ((rank + 1) // 2 % 2)
        row = row + (rank ^ rank_mask) * stride
    return pl.multiple_of(row, 16)


def place_kernel(plan, block, *refs):
    count = len(plan)
    ins = refs[:count]
    outs = refs[count:-1]
    sems = refs[-1]
    me = lax.axis_index("dp")
    rank = lax.axis_index("mp")
    copies = []
    for ref, moves in zip(ins, plan):
        for start, size, which, mask, column, _, offset in moves:
            row = canonical_row(me, rank, block, mask, 0, 0, offset)
            copy = pltpu.make_async_copy(
                ref.at[pl.ds(start, size), :],
                outs[which].at[pl.ds(row, size), pl.ds(column * D, D)],
                sems.at[len(copies)],
            )
            copy.start()
            copies.append(copy)
    for copy in copies:
        copy.wait()


def plan_of(gathered, layouts):
    arrays = []
    plan = []
    for pieces, layout in zip(gathered, layouts):
        rows = sum(size for _, size, *_ in layout)
        for masks, array in pieces:
            moves = []
            for j, mask in enumerate(masks):
                for start, size, which, rank_mask, stride, offset in layout:
                    moves.append((j * rows + start, size, which, mask, rank_mask, stride, offset))
            arrays.append(array)
            plan.append(moves)
    return arrays, plan


def place(arrays, plan, block, shapes):
    return pl.pallas_call(
        functools.partial(place_kernel, plan, block),
        out_shape=[jax.ShapeDtypeStruct(shape, low) for shape in shapes],
        in_specs=[pl.BlockSpec(memory_space=pl.ANY)] * len(arrays),
        out_specs=[pl.BlockSpec(memory_space=pltpu.VMEM)] * len(shapes),
        scratch_shapes=[pltpu.SemaphoreType.DMA((sum(len(moves) for moves in plan),))],
        compiler_params=pltpu.CompilerParams(vmem_limit_bytes=VMEM_LIMIT),
        cost_estimate=SMALL_COST,
        name="place",
    )(*arrays)


def store_split(value, keep, send, index):
    block = keep.shape[2]
    even = lax.axis_index("dp") % 2 == 0
    for outer in range(keep.shape[1]):
        first = value[2 * outer * block : (2 * outer + 1) * block]
        other = value[(2 * outer + 1) * block : (2 * outer + 2) * block]
        keep[index, outer] = jnp.where(even, first, other).astype(low)
        send[index, outer] = jnp.where(even, other, first).astype(low)


def middle_kernel(plan, block, total, *refs):
    limit_ref, vector_ref = refs[:2]
    token_hbm, mixed_hbm, log_hbm, cot_hbm, teach_hbm = refs[2:7]
    pieces = refs[7 : 7 + total]
    (
        out_hbm,
        middle_hbm,
        grad_hbm,
        down_keep,
        down_send,
        up_keep,
        up_send,
        delta_ref,
        log_ref,
        sum_ref,
    ) = refs[7 + total : 17 + total]
    (
        token,
        mixed,
        logs,
        cot,
        teach,
        up,
        down,
        proj,
        right,
        slope,
        second,
        middle,
        final,
        out,
        final_low,
        middle_low,
        grad,
        accum,
        turned,
        stage_keep,
        stage_send,
        in_sems,
        weight_sems,
        out_sems,
        keep_sems,
        send_sems,
    ) = refs[17 + total :]
    hidden = FF // D
    targets = (up, down, proj)
    rows = token.shape[0]
    me = lax.axis_index("dp")
    rank = lax.axis_index("mp")

    def fetch(ref, scratch, n):
        copy = pltpu.make_async_copy(ref, scratch, in_sems.at[n])
        copy.start()
        return copy

    def send(scratch, ref, n):
        copy = pltpu.make_async_copy(scratch, ref, out_sems.at[n])
        copy.start()
        return copy

    gets = [
        fetch(token_hbm, token, 0),
        fetch(mixed_hbm, mixed, 1),
        fetch(log_hbm, logs, 2),
        fetch(cot_hbm, cot, 3),
        fetch(teach_hbm, teach, 4),
    ]
    loads = {0: [], 1: [], 2: []}
    number = 0
    for want in (2, 0, 1):
        for ref, moves in zip(pieces, plan):
            for start, size, which, mask, rank_mask, stride, offset in moves:
                if which != want:
                    continue
                row = canonical_row(me, rank, block, mask, rank_mask, stride, offset)
                copy = pltpu.make_async_copy(
                    ref.at[pl.ds(start, size), :],
                    targets[which].at[pl.ds(row, size), :],
                    weight_sems.at[number],
                )
                copy.start()
                loads[which].append(copy)
                number += 1

    table_row = vector_ref[0:1, :]
    out_bias = vector_ref[1:2, :]
    gain = vector_ref[2:3, :]
    shift = vector_ref[3:4, :]
    down_bias = vector_ref[4:5, :]
    weight = vector_ref[5:6, :]
    gets[0].wait()
    gets[1].wait()
    right[2 * hidden] = mixed[...].astype(low)
    for copy in loads[2]:
        copy.wait()
    state = token[...].astype(full) + table_row + out_bias
    state = state + dot_of(right[2 * hidden], proj[...], 1, 1)
    middle[...] = state
    unit, _ = norm_stats(state)
    second[...] = (unit * gain + shift).astype(low)
    accum[...] = jnp.zeros((rows, D), full)
    for copy in loads[0]:
        copy.wait()
    for copy in loads[1]:
        copy.wait()

    def forward(m, _):
        place = pl.ds(pl.multiple_of(m * D, D), D)
        value = dot_of(second[...], up[place, :], 1, 0) + vector_ref[pl.ds(8 + m, 1), :]
        cumulative = 0.5 + 0.5 * lax.erf(value * (0.5**0.5))
        right[m] = (value * cumulative).astype(low)
        slope[m] = cumulative + value * jnp.exp(-0.5 * value * value) * 0.3989422804014327
        accum[...] += dot_of(right[m], down[place, :], 1, 1)
        return 0

    lax.fori_loop(0, FF // D, forward, 0)
    final_state = middle[...] + accum[...] + down_bias
    out[...] = final_state.astype(low)
    puts = [send(out, out_hbm, 0)]
    gets[3].wait()
    gets[4].wait()
    place = lax.broadcasted_iota(jnp.int32, (rows, 1), 0)
    grads = cot[...].astype(full) + weight * (final_state - teach[...].astype(full))
    grads = jnp.where(place < limit_ref[5], grads, 0.0)
    final[...] = grads
    final_low[...] = grads.astype(low)
    sum_ref[3:4, :] = jnp.sum(grads, axis=0, keepdims=True)
    accum[...] = jnp.zeros((rows, D), full)

    def backward(m, _):
        place = pl.ds(pl.multiple_of(m * D, D), D)
        value = slope[m] * dot_of(final_low[...], down[place, :], 1, 0)
        value = value.astype(low)
        right[hidden + m] = value
        sum_ref[pl.ds(8 + m, 1), :] = jnp.sum(value.astype(full), axis=0, keepdims=True)
        accum[...] += dot_of(value, up[place, :], 1, 1)
        return 0

    lax.fori_loop(0, FF // D, backward, 0)
    unit, inverse = norm_stats(middle[...])
    second_grad = accum[...]
    sum_ref[0:1, :] = jnp.sum(second_grad * unit, axis=0, keepdims=True)
    sum_ref[1:2, :] = jnp.sum(second_grad, axis=0, keepdims=True)
    scaled = second_grad * gain
    mean_scaled = jnp.mean(scaled, axis=-1, keepdims=True)
    mean_unit = jnp.mean(scaled * unit, axis=-1, keepdims=True)
    total_grad = final[...] + inverse * (scaled - mean_scaled - unit * mean_unit)
    middle[...] = total_grad
    puts.append(send(middle, middle_hbm, 1))
    middle_low[...] = total_grad.astype(low)
    sum_ref[2:3, :] = jnp.sum(total_grad, axis=0, keepdims=True)
    attended_grad = dot_of(middle_low[...], proj[...], 1, 0).astype(low)
    grad[...] = attended_grad
    puts.append(send(grad, grad_hbm, 2))
    gets[2].wait()
    head = lax.broadcasted_iota(jnp.int32, (16, D), 0)
    lane = lax.broadcasted_iota(jnp.int32, (16, D), 1)
    member = jnp.where(lane // HEAD_DIM == head, 1.0, 0.0)
    leader = jnp.where(lane == head * HEAD_DIM, 1.0, 0.0)
    exact = functools.partial(
        lax.dot_general,
        dimension_numbers=(((1,), (1,)), ((), ())),
        precision=lax.Precision.HIGHEST,
        preferred_element_type=full,
    )
    deltas = exact(member, attended_grad.astype(full) * mixed[...])
    tops = exact(leader, logs[...])
    for pair in range(PAIRS):
        delta_ref[pair] = deltas[2 * pair : 2 * pair + 2]
        log_ref[pair] = tops[2 * pair : 2 * pair + 2]
    turned[0] = final_low[...].T
    turned[1] = second[...].T
    turned[2] = middle_low[...].T

    def weights(i, _):
        store_split(dot_of(turned[i // hidden], right[i], 1, 0), stage_keep, stage_send, i)

        @pl.when(i < hidden)
        def _():
            pltpu.make_async_copy(stage_keep.at[i], down_keep.at[i], keep_sems.at[i]).start()
            pltpu.make_async_copy(stage_send.at[i], down_send.at[i], send_sems.at[i]).start()

        @pl.when(i >= hidden)
        def _():
            row = i - hidden
            pltpu.make_async_copy(stage_keep.at[i], up_keep.at[row], keep_sems.at[i]).start()
            pltpu.make_async_copy(stage_send.at[i], up_send.at[row], send_sems.at[i]).start()

        return 0

    lax.fori_loop(0, 2 * hidden + 1, weights, 0)
    for copy in puts:
        copy.wait()
    for i in range(2 * hidden + 1):
        if i < hidden:
            keep, gone, row = down_keep, down_send, i
        else:
            keep, gone, row = up_keep, up_send, i - hidden
        pltpu.make_async_copy(stage_keep.at[i], keep.at[row], keep_sems.at[i]).wait()
        pltpu.make_async_copy(stage_send.at[i], gone.at[row], send_sems.at[i]).wait()


def middle_call(limit, vectors, tokens, mixed, logs, cot, teach, arrays, plan, block, dp):
    rows = tokens.shape[0]
    hidden = FF // D
    narrow = jax.ShapeDtypeStruct((rows, D), low)
    wide = jax.ShapeDtypeStruct((rows, D), full)
    shape = (dp // 2, D // dp, D)
    parts = [jax.ShapeDtypeStruct((count,) + shape, low) for count in (hidden, hidden + 1)]
    stats = jax.ShapeDtypeStruct((PAIRS, 2, rows), full)
    anywhere = pl.BlockSpec(memory_space=pl.ANY)
    inside = pl.BlockSpec(memory_space=pltpu.VMEM)
    moves = sum(len(part) for part in plan)
    return pl.pallas_call(
        functools.partial(middle_kernel, plan, block, len(arrays)),
        out_shape=(
            narrow,
            wide,
            narrow,
            parts[0],
            parts[0],
            parts[1],
            parts[1],
            stats,
            stats,
            jax.ShapeDtypeStruct((8 + 8, D), full),
        ),
        in_specs=[pl.BlockSpec(memory_space=pltpu.SMEM), inside]
        + [anywhere] * (5 + len(arrays)),
        out_specs=[anywhere] * 7 + [inside] * 3,
        scratch_shapes=[
            pltpu.VMEM((rows, D), low),
            pltpu.VMEM((rows, D), full),
            pltpu.VMEM((rows, D), full),
            pltpu.VMEM((rows, D), low),
            pltpu.VMEM((rows, D), low),
            pltpu.VMEM((FF, D), low),
            pltpu.VMEM((FF, D), low),
            pltpu.VMEM((D, D), low),
            pltpu.VMEM((2 * hidden + 1, rows, D), low),
            pltpu.VMEM((hidden, rows, D), full),
            pltpu.VMEM((rows, D), low),
            pltpu.VMEM((rows, D), full),
            pltpu.VMEM((rows, D), full),
            pltpu.VMEM((rows, D), low),
            pltpu.VMEM((rows, D), low),
            pltpu.VMEM((rows, D), low),
            pltpu.VMEM((rows, D), low),
            pltpu.VMEM((rows, D), full),
            pltpu.VMEM((3, D, rows), low),
            pltpu.VMEM((2 * hidden + 1,) + shape, low),
            pltpu.VMEM((2 * hidden + 1,) + shape, low),
            pltpu.SemaphoreType.DMA((5,)),
            pltpu.SemaphoreType.DMA((moves,)),
            pltpu.SemaphoreType.DMA((3,)),
            pltpu.SemaphoreType.DMA((2 * hidden + 1,)),
            pltpu.SemaphoreType.DMA((2 * hidden + 1,)),
        ],
        compiler_params=pltpu.CompilerParams(vmem_limit_bytes=VMEM_LIMIT),
        cost_estimate=SMALL_COST,
        name="middle",
    )(limit, vectors, tokens, mixed, logs, cot, teach, *arrays)


def fold_block(keep, got, out_keep, out_send, bit, place):
    step = 1 << place
    mine = (lax.axis_index("dp") // bit) % 2 * step
    for j in range(keep.shape[1] // 2):
        base = (j // step) * 2 * step + j % step
        for out, shift in ((out_keep, mine), (out_send, step - mine)):
            value = keep[0, base + shift].astype(full) + got[0, base + shift].astype(full)
            out[0, j] = value.astype(low)


def fold_kernel(bits, places, *refs):
    count = len(bits)
    for n in range(count):
        fold_block(
            *refs[2 * n : 2 * n + 2],
            *refs[2 * count + 2 * n : 2 * count + 2 * n + 2],
            bits[n],
            places[n],
        )


def fold(pairs, bits, places):
    lead = pairs[0][0].shape[0]
    block = lambda shape: pl.BlockSpec((1,) + shape[1:], lambda i: (i, 0, 0, 0))
    halves = [
        (keep.shape[0], keep.shape[1] // 2) + keep.shape[2:] for keep, _ in pairs for _ in range(2)
    ]
    outs = pl.pallas_call(
        functools.partial(fold_kernel, bits, places),
        out_shape=[jax.ShapeDtypeStruct(shape, low) for shape in halves],
        grid=(lead,),
        in_specs=[block(value.shape) for pair in pairs for value in pair],
        out_specs=[block(shape) for shape in halves],
        compiler_params=pltpu.CompilerParams(vmem_limit_bytes=VMEM_LIMIT),
        cost_estimate=pl.CostEstimate(flops=0, bytes_accessed=16 << 20, transcendentals=0),
        name="fold",
    )(*[value for pair in pairs for value in pair])
    return [(outs[2 * n], outs[2 * n + 1]) for n in range(len(pairs))]


def qkv_grad_kernel(count, *refs):
    sources = refs[: 3 * count + 1]
    outs = refs[3 * count + 1 : 3 * count + 5]
    sum_ref, held, turned, total, stage, in_sems, out_sems = refs[3 * count + 5 :]
    first_use = [0, count] + list(range(1, count)) + list(range(count + 1, 3 * count + 1))
    for n in first_use:
        pltpu.make_async_copy(sources[n], held.at[n], in_sems.at[n]).start()

    def wait(n):
        pltpu.make_async_copy(sources[0], held.at[n], in_sems.at[n]).wait()

    def turn(n, _):
        wait(n)
        turned[n] = held[n].T
        return 0

    lax.fori_loop(0, count, turn, 0)
    sum_ref[...] = jnp.zeros_like(sum_ref)

    def step(i, _):
        c = (i + count - 1) // count
        n = jnp.where(i == 0, 0, (i + count - 1) % count)
        wait(count + i)
        right = held[count + i]
        value = dot_of(turned[n], right, 1, 0)
        total[...] = value + jnp.where(n == 0, jnp.zeros_like(value), total[...])

        @pl.when(c != 1)
        def _():
            row = pl.ds(pl.multiple_of(c * 4, 8), 1)
            sum_ref[row, :] += jnp.sum(right.astype(full), axis=0, keepdims=True)

        @pl.when(i % count == 0)
        def _():
            for part in range(2):
                store_split(
                    total[:, part * D // 2 : (part + 1) * D // 2],
                    stage.at[part],
                    stage.at[2 + part],
                    c,
                )
            for k in range(4):
                pltpu.make_async_copy(
                    stage.at[k, c], outs[k].at[c], out_sems.at[k * 3 + c]
                ).start()

        return 0

    lax.fori_loop(0, 2 * count + 1, step, 0)
    for k in range(4):
        for c in range(3):
            pltpu.make_async_copy(stage.at[k, c], outs[k].at[c], out_sems.at[k * 3 + c]).wait()


def qkv_grads(chunks, query_grad, key_grads, value_grads, dp):
    rows = query_grad.shape[0]
    count = len(chunks)
    shape = (3, dp // 2, D // dp, D // 2)
    anywhere = pl.BlockSpec(memory_space=pl.ANY)
    return pl.pallas_call(
        functools.partial(qkv_grad_kernel, count),
        out_shape=[jax.ShapeDtypeStruct(shape, low)] * 4
        + [jax.ShapeDtypeStruct((16, D), full)],
        in_specs=[anywhere] * (3 * count + 1),
        out_specs=[anywhere] * 4 + [pl.BlockSpec(memory_space=pltpu.VMEM)],
        scratch_shapes=[
            pltpu.VMEM((3 * count + 1, rows, D), low),
            pltpu.VMEM((count, D, rows), low),
            pltpu.VMEM((D, D), full),
            pltpu.VMEM((4,) + shape, low),
            pltpu.SemaphoreType.DMA((3 * count + 1,)),
            pltpu.SemaphoreType.DMA((12,)),
        ],
        compiler_params=pltpu.CompilerParams(vmem_limit_bytes=VMEM_LIMIT),
        cost_estimate=SMALL_COST,
        name="qkv_grads",
    )(*chunks, query_grad, *key_grads, *value_grads)


def last_kernel(
    token_ref,
    first_ref,
    right_ref,
    left_ref,
    middle_ref,
    vector_ref,
    gain_ref,
    bias_ref,
    sum_ref,
    out_ref,
    pack_ref,
):
    @pl.when(pl.program_id(0) == 0)
    def _():
        pack_ref[...] = jnp.zeros_like(pack_ref)
        pack_ref[1:2, :] = sum_ref[0:1, :]
        pack_ref[3:4, :] = sum_ref[1:2, :]
        pack_ref[4:5, :] = bias_ref[0:1, :]
        pack_ref[5:6, :] = bias_ref[8:9, :]
        pack_ref[6:8, :] = sum_ref[2:4, :]
        pack_ref[8 : 8 + FF // D, :] = sum_ref[8 : 8 + FF // D, :]

    unit, inverse = norm_stats(token_ref[...].astype(full) + vector_ref[0:1, :])
    grad = first_ref[...] + right_ref[...].astype(full) + left_ref[...].astype(full)
    scaled = grad * gain_ref[0:1, :]
    mean_scaled = jnp.mean(scaled, axis=-1, keepdims=True)
    mean_unit = jnp.mean(scaled * unit, axis=-1, keepdims=True)
    result = middle_ref[...] + inverse * (scaled - mean_scaled - unit * mean_unit)
    out_ref[...] = result
    pack_ref[0:1, :] += jnp.sum(grad * unit, axis=0, keepdims=True)
    pack_ref[2:3, :] += jnp.sum(grad, axis=0, keepdims=True)
    pack_ref[pl.ds(16 + lax.axis_index("dp"), 1), :] += jnp.sum(result, axis=0, keepdims=True)


def last_norm(tokens, first, right, left, middle_grad, vectors, gains, bias_sums, sums, dp):
    rows = tokens.shape[0]
    part = pl.BlockSpec((rows // 4, D), lambda i: (i, 0))
    whole = lambda value: pl.BlockSpec(value.shape, lambda i: (0, 0))
    small = (vectors, gains, bias_sums, sums)
    return pl.pallas_call(
        last_kernel,
        out_shape=(
            jax.ShapeDtypeStruct((rows, D), full),
            jax.ShapeDtypeStruct((16 + dp, D), full),
        ),
        grid=(4,),
        in_specs=[part] * 5 + [whole(value) for value in small],
        out_specs=[part, pl.BlockSpec((16 + dp, D), lambda i: (0, 0))],
        compiler_params=pltpu.CompilerParams(vmem_limit_bytes=VMEM_LIMIT),
        cost_estimate=SMALL_COST,
        name="last_norm",
    )(tokens, first, right, left, middle_grad, *small)


def two_parts(value, axis, mine):
    keep = lax.dynamic_index_in_dim(value, mine, axis, keepdims=False)
    send = lax.dynamic_index_in_dim(value, 1 - mine, axis, keepdims=False)
    return keep, send.astype(low)


class Scatter:
    def __init__(self, parts, turns):
        self.bits = outer_bits()
        half = len(self.bits) // 2
        self.orders = [
            [1] + self.bits[half * (turn % 2) :] + self.bits[: half * (turn % 2)] for turn in turns
        ]
        self.left = [list(self.bits) for _ in turns]
        self.step = 0
        self.parts = parts

    def sends(self):
        return [send for _, send in self.parts]

    def exchange(self, sends):
        self.pairs = [
            (keep, swap(send, "dp", turn[self.step]))
            for (keep, _), send, turn in zip(self.parts, sends, self.orders)
        ]
        self.step += 1

    def folds(self):
        if self.step > len(self.bits):
            return [], [], []
        bits = [turn[self.step] for turn in self.orders]
        places = []
        for left, bit in zip(self.left, bits):
            places.append(left.index(bit))
            left.remove(bit)
        return self.pairs, bits, places

    def give(self, outs):
        self.parts = [(outs[n], outs[n + 1]) for n in range(0, len(outs), 2)]

    def fold(self):
        outs = []
        for pair, bit, at in zip(*self.folds()):
            outs += fold([pair], [bit], [at])[0]
        self.give(outs)

    def advance(self, order):
        sends = order(*self.sends())
        self.exchange(list(sends) if len(self.parts) > 1 else [sends])

    def finish(self, order):
        while self.step <= len(self.bits):
            self.fold()
            self.advance(order)
        got = order(*[other for _, other in self.pairs])
        return [
            (keep.astype(full) + other.astype(full))[:, 0]
            for (keep, _), other in zip(self.pairs, got)
        ]


def scatter_dp(parts, turns):
    scatter = Scatter(parts, turns)
    while True:
        sends = yield scatter.sends()
        scatter.exchange(sends)
        if scatter.step > len(scatter.bits):
            break
        scatter.parts = fold(*scatter.folds())
    got = yield [other for _, other in scatter.pairs]
    return [
        (keep.astype(full) + other.astype(full))[:, 0]
        for (keep, _), other in zip(scatter.pairs, got)
    ]


def scatter_mp(value):
    rank = lax.axis_index("mp")
    part = lambda index: lax.dynamic_index_in_dim(value, index, keepdims=False)
    sends = yield [part(rank ^ bit).astype(low) for bit in (1, 2, 3)]
    got = yield [swap(send, "mp", bit) for bit, send in zip((1, 2, 3), sends)]
    got = [other.astype(full) for other in got]
    return (part(rank) + got[0]) + (got[1] + got[2])


def halve_mp(value):
    rank = lax.axis_index("mp")
    pairs = value.reshape((2, 2) + value.shape[1:])
    keep, send = two_parts(pairs, 1, rank % 2)
    (send,) = yield [send]
    (got,) = yield [swap(send, "mp", 1)]
    keep, send = two_parts(keep.astype(full) + got.astype(full), 0, rank // 2)
    (send,) = yield [send]
    (got,) = yield [swap(send, "mp", 2)]
    return keep + got.astype(full)


def scatter_feed(up_own, down_own):
    mp = lax.axis_size("mp")
    block = down_own.shape[1]
    out_own = up_own[mp].reshape(block, mp, -1).transpose(1, 0, 2)
    own = yield from halve_mp(
        jnp.concatenate([up_own[:mp], down_own, out_own.reshape(mp, -1, D)], axis=1)
    )
    return own[:block], own[block : 2 * block].T, own[2 * block :].reshape(block, -1).T


def scatter_qkv(keep_left, keep_right, send_left, send_right):
    left_part, right_part = yield from scatter_dp(
        [(keep_left, send_left), (keep_right, send_right)], (0, 1)
    )
    width = D // lax.axis_size("mp")
    parts = [part[..., at : at + width] for part in (left_part, right_part) for at in (0, width)]
    return (yield from scatter_mp(jnp.stack(parts)))


def sum_small(value):
    (value,) = yield [value]
    value = value + swap(value, "dp", 1)
    bits = outer_bits()
    groups = [("dp", bits[n : n + 2]) for n in range(0, len(bits), 2)] + [("mp", [1, 2])]
    for axis, pair in groups:
        (value,) = yield [value]
        if len(pair) == 1:
            value = value + swap(value, axis, pair[0])
        else:
            one, two = pair
            got = [swap(value, axis, mask) for mask in (one, two, one + two)]
            if axis == "mp":
                got = yield got
            value = (value + got[0]) + (got[1] + got[2])
    return value


class Steps:
    def __init__(self, steps):
        self.steps = steps
        self.pending = next(steps)
        self.result = None

    def advance(self, order):
        if self.pending is None:
            return
        sends = order(*self.pending)
        sends = [sends] if len(self.pending) == 1 else list(sends)
        try:
            self.pending = self.steps.send(sends)
        except StopIteration as stop:
            self.pending = None
            self.result = stop.value

    def finish(self, order):
        while self.pending is not None:
            self.advance(order)
        return self.result


def shards(
    tokens_in,
    timesteps,
    lengths,
    time_table,
    norm_gains,
    norm_biases,
    w_qkv,
    qv_bias,
    w_out,
    out_bias,
    w_up,
    up_bias,
    w_down,
    down_bias,
    cotangent,
    teacher,
):
    rank = lax.axis_index("mp")
    data_rank = lax.axis_index("dp")
    mp = lax.axis_size("mp")
    dp = lax.axis_size("dp")
    own_rows = tokens_in.shape[0]
    length = lax.dynamic_index_in_dim(lengths, data_rank, keepdims=False)
    own_time = lax.dynamic_index_in_dim(timesteps, data_rank, keepdims=False)
    odd = rank % 2 == 1
    upper = rank >= 2
    middle = jnp.logical_or(rank == 1, rank == 2)
    order = Order()
    along = lambda value, pairs: lax.ppermute(value, "mp", pairs)

    block = w_qkv.shape[1]
    aligned = block % 32 == 0
    narrow = order(jnp.concatenate([w_qkv.reshape(3 * block, -1), w_out.T]))
    first_swap = swap(narrow, "mp", 1)
    tall = order(jnp.concatenate([w_up, w_down.T]))
    tall_swap = swap(tall, "mp", 1)
    pair = order(
        jnp.concatenate(
            [jnp.where(odd, first_swap, narrow), jnp.where(odd, narrow, first_swap)], axis=1
        )
    )
    second_swap = swap(pair, "mp", 2)
    tokens, lengths, own_time, norm_gains, norm_biases, out_bias, down_bias, up_bias, length = order(
        tokens_in, lengths, own_time, norm_gains, norm_biases, out_bias, down_bias, up_bias, length
    )
    table_row = lax.dynamic_slice_in_dim(time_table, own_time, 1).astype(full)
    unit_one, _ = norm_stats(tokens.astype(full) + table_row)
    first_norm = (unit_one * norm_gains[0] + norm_biases[0]).astype(low)
    loss_weight = lengths.shape[0] * MAXLEN / jnp.sum(lengths).astype(full)
    vectors = jnp.concatenate(
        [
            table_row,
            out_bias[None],
            norm_gains[1:2],
            norm_biases[1:2],
            down_bias[None],
            jnp.full((3, D), loss_weight),
            up_bias.reshape(-1, D),
            jnp.zeros((4, D), full),
        ]
    )
    scalars = jnp.stack(
        [
            rank,
            jnp.where(rank == 0, 1, rank - 1),
            jnp.where(upper, rank - 2, rank + 2),
            jnp.where(middle, rank + 1, 3 - rank),
            length,
            length - rank * own_rows,
        ]
    ).astype(jnp.int32)
    first_norm, vectors, scalars = order(first_norm, vectors, scalars)
    wide = jnp.concatenate(
        [jnp.where(upper, second_swap, pair), jnp.where(upper, pair, second_swap)], axis=1
    )
    qkv_rows, out_rows = wide[: 3 * block], wide[3 * block :]
    if aligned:
        split = 3 * block // 2
        qkv_gather = Gather([qkv_rows[:split], qkv_rows[split:]])
        qkv_gather.advance(order)
    tall = order(jnp.concatenate([tall, tall_swap]))
    tall_across = along(tall, [(1, 2), (2, 1)])

    sent = order(first_norm)
    from_left = along(sent, [(0, 1), (1, 2), (2, 3)])
    from_right = along(sent, [(1, 0), (2, 1), (3, 2)])
    tall_across = order(tall_across)
    tall_far = along(tall_across, [(1, 0), (2, 3)])
    if aligned:
        while qkv_gather.step < len(qkv_gather.bits):
            qkv_gather.advance(order)
        qkv_gather.advance(order)
    hop_right, hop_left = order(from_left, from_right)
    second_right = along(hop_right, [(1, 2), (2, 3)])
    second_left = along(hop_left, [(1, 0), (2, 1)])
    if aligned:
        arrays, plan = plan_of(
            qkv_gather.result,
            [
                [(0, block, 0, 0, 0, 0), (block, split - block, 1, 0, 0, 0)],
                [
                    (0, 2 * block - split, 1, 0, 0, split - block),
                    (2 * block - split, block, 1, 1, 0, 0),
                ],
            ],
        )
        query_weight, pair_weight = order(*place(arrays, plan, block, [(D, D), (D, 2 * D)]))
        tall_other = jnp.where(middle, tall_across, order(tall_far))
        feed_gather = Gather(
            [
                jnp.concatenate([tall, out_rows[: block // 2]]),
                jnp.concatenate([tall_other, out_rows[block // 2 :]]),
            ]
        )
        feed_gather.advance(order)
    else:
        weights = lax.all_gather(qkv_rows.reshape(3, block, D), "dp", axis=1, tiled=True)
        query_weight = weights[0]
        pair_weight = jnp.concatenate([weights[1], weights[2]], axis=1)
    near = jnp.where(rank == 0, hop_left, hop_right)
    attend = lambda parts, numbers, carried: order(
        *attend_forward(
            parts,
            numbers,
            scalars,
            query_weight,
            pair_weight,
            qv_bias[0:1],
            qv_bias[1:2],
            carried,
        )
    )
    key_own, value_own, queries, *state = attend([order(first_norm)], (0,), None)
    second_right, second_left = order(second_right, second_left)
    second = order(jnp.where(upper, second_right, second_left))
    third = along(second, [(1, 0), (2, 3)])
    if aligned:
        while feed_gather.step < len(feed_gather.bits):
            feed_gather.advance(order)
        feed_gather.send_early(order)
    near, second = order(near, second)
    key_near, key_second, value_near, value_second, *state = attend(
        [near, second], (1, 2), (queries, *state)
    )
    last = order(jnp.where(middle, hop_left, order(third)))
    key_last, value_last, mixed, logs = attend([order(last)], (3,), (queries, *state))
    if aligned:
        feed_gather.advance(order)
        layout = lambda masks, shift: [
            (0, block, 0, masks[0], D, 0),
            (block, block, 1, masks[0], D, 0),
            (2 * block, block, 0, masks[1], D, 0),
            (3 * block, block, 1, masks[1], D, 0),
            (4 * block, block // 2, 2, 0, 0, shift),
        ]
        arrays, plan = plan_of(
            feed_gather.result, [layout((0, 1), 0), layout((2, 3), block // 2)]
        )
    else:
        arrays = [
            lax.all_gather(w_up, ("mp", "dp"), axis=0, tiled=True),
            lax.all_gather(w_down.T, ("mp", "dp"), axis=0, tiled=True),
            lax.all_gather(out_rows, "dp", axis=0, tiled=True),
        ]
        plan = [[(0, array.shape[0], n, None, 0, 0, 0)] for n, array in enumerate(arrays)]
    chunks = [first_norm, near, second, last]
    keys = [key_own, key_near, key_second, key_last]
    values = [value_own, value_near, value_second, value_last]

    output, middle_grad, attended_grad, *parts, deltas, log_rows, sums = middle_call(
        scalars, vectors, tokens, mixed, logs, cotangent, teacher, arrays, plan, block, dp
    )
    scatter = Scatter([(parts[0], parts[1]), (parts[2], parts[3])], (1, 0))
    scatter.advance(order)

    key_grads = [None] * 4
    value_grads = [None] * 4
    firsts = [None] * 4
    query_grad = None
    for n in (3, 2, 1, 0):
        pairs, bits, places = scatter.folds() if n % 2 == 0 else ([], [], [])
        query_grad, key_grads[n], value_grads[n], firsts[n], *folded = attend_backward(
            n,
            queries,
            keys[n],
            values[n],
            order(attended_grad),
            log_rows,
            deltas,
            query_weight,
            pair_weight,
            scalars,
            query_grad,
            n == 0,
            pairs,
            bits,
            places,
        )
        firsts[n] = order(firsts[n])
        if folded:
            scatter.give(folded)
        if n == 3:
            back_last = along(firsts[3], [(0, 1), (3, 2)]).astype(full)
        elif n == 2:
            scatter.advance(order)
            payload = order((firsts[2] + back_last).astype(low))
            back_right = along(payload, [(0, 1), (1, 2)]).astype(full)
            back_left = along(payload, [(3, 2), (2, 1)]).astype(full)
        elif n == 1:
            to_right = jnp.where(
                rank == 0, firsts[1], firsts[3].astype(full) + back_right
            ).astype(low)
            to_left = (firsts[1] + back_left).astype(low)
            to_right, to_left = order(to_right, to_left)
            final_right = along(to_right, [(0, 1), (1, 2), (2, 3)])
            final_left = along(to_left, [(3, 2), (2, 1), (1, 0)])
    scatter.advance(order)
    query_grad, final_right, final_left = order(query_grad, final_right, final_left)
    *halves, bias_sums = qkv_grads(chunks, query_grad, key_grads, value_grads, dp)
    qkv = Steps(scatter_qkv(*halves))
    qkv.advance(order)
    down_own, up_own = scatter.finish(order)
    feed = Steps(scatter_feed(up_own, down_own))
    feed.advance(order)
    qkv.advance(order)
    tokens, first_own = order(tokens, firsts[0])
    input_grad, packed = last_norm(
        tokens,
        first_own,
        final_right,
        final_left,
        middle_grad,
        vectors,
        norm_gains,
        bias_sums,
        sums,
        dp,
    )
    packed, input_grad = order(packed, input_grad)
    small = Steps(sum_small(packed))
    feed.advance(order)
    feed.advance(order)
    small.advance(order)
    qkv.advance(order)
    feed.advance(order)
    qkv.advance(order)
    small.advance(order)
    qkv.advance(order)
    small.advance(order)
    qkv_grad = qkv.finish(order)
    up_grad, down_grad, out_grad = feed.finish(order)
    total = small.finish(order)
    fixed = 16
    chosen = (timesteps[None, :] == jnp.arange(time_table.shape[0])[:, None]).astype(full)
    table_grad = lax.dot_general(
        chosen,
        total[fixed:],
        (((1,), (0,)), ((), ())),
        precision=lax.Precision.HIGHEST,
        preferred_element_type=full,
    )
    return (
        output,
        input_grad,
        table_grad,
        total[0:2],
        total[2:4],
        qkv_grad,
        total[4:6],
        out_grad,
        total[6],
        up_grad,
        total[8 : 8 + FF // D].reshape(FF),
        down_grad,
        total[7],
    )


def solution(mesh):
    rows = P(both, None)
    placed = (
        rows,
        P(),
        P(),
        P(),
        P(),
        P(),
        P(None, "dp", "mp"),
        P(),
        P("mp", "dp"),
        P(),
        P("dp", "mp"),
        P(),
        P("mp", "dp"),
        P(),
        rows,
        rows,
    )
    return jax.shard_map(
        shards,
        mesh=mesh,
        in_specs=placed,
        out_specs=(
            rows,
            rows,
            P(),
            P(),
            P(),
            P(None, "dp", "mp"),
            P(),
            P("mp", "dp"),
            P(),
            P("dp", "mp"),
            P(),
            P("mp", "dp"),
            P(),
        ),
        check_vma=False,
    )
```

```python
import functools

import jax
import jax.numpy as jnp
from jax import lax
from jax.experimental import pallas as pl
from jax.experimental.pallas import tpu as pltpu
from jax.sharding import PartitionSpec as P

D = 768
HEADS = 12
HEAD_DIM = 64
FF = 3072
MAXLEN = 2048
PAIR = 2 * HEAD_DIM
PAIRS = HEADS // 2
VMEM_LIMIT = 58 << 20
SMALL_COST = pl.CostEstimate(flops=1 << 20, bytes_accessed=1 << 16, transcendentals=0)

far_below = -1e30
epsilon = 1e-05
score_scale = HEAD_DIM ** (-0.5)
low = jnp.bfloat16
full = jnp.float32
both = ("dp", "mp")


def norm_stats(values):
    center = values - jnp.mean(values, axis=-1, keepdims=True)
    spread = jnp.mean(center * center, axis=-1, keepdims=True)
    inverse = lax.rsqrt(spread + epsilon)
    return center * inverse, inverse


def dot_of(left_side, right_side, left_dim, right_dim):
    return lax.dot_general(
        left_side,
        right_side,
        (((left_dim,), (right_dim,)), ((), ())),
        preferred_element_type=full,
    )


def first_half(shape):
    return lax.broadcasted_iota(jnp.int32, shape, len(shape) - 1) < HEAD_DIM


def forward_kernel(numbers, first, final, scalars, *refs):
    count = len(numbers)
    chunk_refs = refs[:count]
    wk_ref, wv_ref, value_bias_ref = refs[count : count + 3]
    refs = refs[count + 3 :]
    if first:
        wq_ref, query_bias_ref = refs[:2]
        key_outs, value_outs = refs[2 : 2 + count], refs[2 + count : 2 + 2 * count]
        query_out, top_ref, sum_ref, acc_ref = refs[2 + 2 * count :]
        q_pair = (dot_of(chunk_refs[0][...], wq_ref[...], 1, 0) + query_bias_ref[...]).astype(low)
        q_pair = q_pair * jnp.asarray(score_scale, low)
        query_out[...] = q_pair
    else:
        q_ref, top_in, sum_in, acc_in = refs[:4]
        key_outs, value_outs = refs[4 : 4 + count], refs[4 + count : 4 + 2 * count]
        results = refs[4 + 2 * count :]
        q_pair = q_ref[...]
    weight = jnp.concatenate([wk_ref[...], wv_ref[...]], axis=1)
    keys = []
    values = []
    for n in range(count):
        both_parts = dot_of(chunk_refs[n][...], weight, 1, 0)
        keys.append(both_parts[:, :PAIR].astype(low))
        values.append((both_parts[:, PAIR:] + value_bias_ref[...]).astype(low))
        key_outs[n][...] = keys[n]
        value_outs[n][...] = values[n]
    rows = q_pair.shape[0]
    size = keys[0].shape[0]
    place = lax.broadcasted_iota(jnp.int32, (1, size), 1)
    lower = first_half((rows, PAIR))
    parts = []
    for half in range(2):
        kept = lower if half == 0 else jnp.logical_not(lower)
        q_half = jnp.where(kept, q_pair, jnp.zeros_like(q_pair))
        scores = []
        for n in range(count):
            bias = jnp.where(place + scalars[numbers[n]] * size < scalars[4], 0.0, far_below)
            scores.append(dot_of(q_half, keys[n], 1, 1) + bias)
        highest = functools.reduce(
            jnp.maximum, [jnp.max(score, axis=-1, keepdims=True) for score in scores]
        )
        totals = jnp.zeros_like(highest)
        mixed = jnp.zeros((rows, PAIR), full)
        for n in range(count):
            exp_scores = jnp.exp(scores[n] - highest)
            totals = totals + jnp.sum(exp_scores, axis=-1, keepdims=True)
            mixed = mixed + dot_of(exp_scores.astype(low), values[n], 1, 0)
        parts.append((highest, totals, mixed))
    top = jnp.where(lower, parts[0][0], parts[1][0])
    total = jnp.where(lower, parts[0][1], parts[1][1])
    mixed = jnp.where(lower, parts[0][2], parts[1][2])
    if first:
        top_ref[...] = top
        sum_ref[...] = total
        acc_ref[...] = mixed
    else:
        highest = jnp.maximum(top, top_in[...])
        here = jnp.exp(top - highest)
        before = jnp.exp(top_in[...] - highest)
        total = total * here + sum_in[...] * before
        mixed = mixed * here + acc_in[...] * before
        if final:
            results[0][...] = mixed / total
            results[1][...] = highest + jnp.log(total)
        else:
            results[0][...] = highest
            results[1][...] = total
            results[2][...] = mixed


def attend_forward(chunks, numbers, scalars, query_weight, pair_weight, query_bias, value_bias, carried):
    rows = chunks[0].shape[0]
    count = len(chunks)
    first = carried is None
    final = 3 in numbers
    column = lambda height, c: pl.BlockSpec((height, PAIR), lambda i, n: (0, c * PAIRS + i))
    whole = pl.BlockSpec((rows, D), lambda i, n: (0, 0))
    wide = jax.ShapeDtypeStruct((rows, D), full)
    narrow = jax.ShapeDtypeStruct((rows, D), low)
    extra = (query_weight, query_bias) if first else carried
    results = (narrow,) * first + (wide,) * (2 if final else 3)
    return pl.pallas_call(
        functools.partial(forward_kernel, numbers, first, final),
        out_shape=(narrow,) * (2 * count) + results,
        grid_spec=pltpu.PrefetchScalarGridSpec(
            num_scalar_prefetch=1,
            grid=(PAIRS,),
            in_specs=[whole] * count
            + [column(D, 0), column(D, 1), column(1, 0)]
            + ([column(D, 0), column(1, 0)] if first else [column(rows, 0)] * 4),
            out_specs=[column(rows, 0)] * (2 * count + len(results)),
        ),
        compiler_params=pltpu.CompilerParams(vmem_limit_bytes=VMEM_LIMIT),
        cost_estimate=SMALL_COST,
        name="attend_forward",
    )(scalars, *chunks, pair_weight, pair_weight, value_bias, *extra)


def backward_kernel(
    number,
    first,
    last,
    folds,
    scalars,
    q_ref,
    k_ref,
    v_ref,
    g_ref,
    log_ref,
    delta_ref,
    wk_ref,
    wv_ref,
    *refs
):
    if last:
        wq_ref = refs[0]
        refs = refs[1:]
    if not first:
        dq_in = refs[0]
        refs = refs[1:]
    count = len(folds)
    fold_ins, refs = refs[: 2 * count], refs[2 * count :]
    dq_ref, dk_ref, dv_ref, back_ref = refs[:4]
    fold_outs, accum = refs[4:-1], refs[-1]
    step = pl.program_id(0)
    for n, (lead, bit, at) in enumerate(folds):

        @pl.when(step < lead)
        def _():
            fold_block(
                *fold_ins[2 * n : 2 * n + 2], *fold_outs[2 * n : 2 * n + 2], bit, at
            )

    rows = q_ref.shape[0]
    keys = k_ref.shape[0]
    limit = scalars[4] - scalars[number] * keys
    q_pair = q_ref[...]
    g_pair = g_ref[...]
    k_pair = k_ref[...]
    v_pair = v_ref[...]
    lower = first_half((rows, PAIR))
    nothing = jnp.zeros((rows, PAIR), low)
    two_halves = lambda pair: jnp.concatenate(
        [jnp.where(lower, pair, nothing), jnp.where(lower, nothing, pair)]
    )
    queries = two_halves(q_pair)
    grads_out = two_halves(g_pair)
    row_of = lambda ref: jnp.concatenate([ref[0, 0:1, :], ref[0, 1:2, :]], axis=1)
    place = lax.broadcasted_iota(jnp.int32, (keys, 1), 0)
    bias = jnp.where(place < limit, 0.0, far_below)
    scores = dot_of(k_pair, queries, 1, 1) + bias
    prob_grad = dot_of(v_pair, grads_out, 1, 1)
    probs = jnp.exp(scores - row_of(log_ref))
    score_grad = (probs * (prob_grad - row_of(delta_ref))).astype(low)
    dv_low = dot_of(probs.astype(low), grads_out, 1, 0).astype(low)
    dk_low = dot_of(score_grad, queries, 1, 0).astype(low)
    turned = dot_of(k_pair.T, score_grad, 1, 0)
    upper_rows = lax.broadcasted_iota(jnp.int32, (PAIR, rows), 0) < HEAD_DIM
    dk_ref[...] = dk_low
    dv_ref[...] = dv_low
    grads = [dk_low, dv_low]
    weights = [wk_ref[...], wv_ref[...]]
    dq_all = jnp.where(upper_rows, turned[:, :rows], turned[:, rows:]).T
    if not first:
        dq_all = dq_all + dq_in[...]
    back = dot_of(jnp.concatenate(grads, axis=1), jnp.concatenate(weights, axis=1), 1, 1)
    if last:
        dq_low = (dq_all * score_scale).astype(low)
        dq_ref[...] = dq_low
        back = back + dot_of(dq_low, wq_ref[...], 1, 1)
    else:
        dq_ref[...] = dq_all

    @pl.when(step == 0)
    def _():
        accum[...] = back

    @pl.when(step > 0)
    def _():
        accum[...] += back

    @pl.when(step == PAIRS - 1)
    def _():
        back_ref[...] = accum[...].astype(back_ref.dtype)


def attend_backward(
    number,
    queries,
    keys,
    values,
    grads,
    logs,
    deltas,
    query_weight,
    pair_weight,
    scalars,
    carried,
    last,
    pairs,
    bits,
    places,
):
    rows, total = queries.shape[0], keys.shape[0]
    first = carried is None
    folds = [(keep.shape[0], bit, at) for (keep, _), bit, at in zip(pairs, bits, places)]
    halves = [
        (keep.shape[0], keep.shape[1] // 2) + keep.shape[2:] for keep, _ in pairs for _ in range(2)
    ]

    def by_lead(shape):
        end = shape[0] - 1
        return pl.BlockSpec((1,) + shape[1:], lambda i, n: (jnp.minimum(i, end), 0, 0, 0))

    column = lambda count, c: pl.BlockSpec((count, PAIR), lambda i, n: (0, c * PAIRS + i))
    stats = pl.BlockSpec((1, 2, rows), lambda i, n: (i, 0, 0))
    extra = (query_weight,) * last + (() if first else (carried,))
    extra_specs = [column(D, 0)] * last + ([] if first else [column(rows, 0)])
    return pl.pallas_call(
        functools.partial(backward_kernel, number, first, last, folds),
        out_shape=(
            jax.ShapeDtypeStruct((rows, D), low if last else full),
            jax.ShapeDtypeStruct((total, D), low),
            jax.ShapeDtypeStruct((total, D), low),
            jax.ShapeDtypeStruct((total, D), low if first else full),
            *[jax.ShapeDtypeStruct(shape, low) for shape in halves],
        ),
        grid_spec=pltpu.PrefetchScalarGridSpec(
            num_scalar_prefetch=1,
            grid=(PAIRS,),
            in_specs=[
                column(rows, 0),
                column(total, 0),
                column(total, 0),
                column(rows, 0),
                stats,
                stats,
                column(D, 0),
                column(D, 1),
            ]
            + extra_specs
            + [by_lead(value.shape) for pair in pairs for value in pair],
            out_specs=[
                column(rows, 0),
                column(total, 0),
                column(total, 0),
                pl.BlockSpec((total, D), lambda i, n: (0, 0)),
            ]
            + [by_lead(shape) for shape in halves],
            scratch_shapes=[pltpu.VMEM((total, D), full)],
        ),
        compiler_params=pltpu.CompilerParams(vmem_limit_bytes=VMEM_LIMIT),
        cost_estimate=SMALL_COST,
        name="attend_backward",
    )(
        scalars,
        queries,
        keys,
        values,
        grads,
        logs,
        deltas,
        pair_weight,
        pair_weight,
        *extra,
        *[value for pair in pairs for value in pair],
    )


def swap(value, axis, bit):
    count = lax.axis_size(axis)
    return lax.ppermute(value, axis, [(i, i ^ bit) for i in range(count)])


class Order:
    def __init__(self):
        self.marks = ()

    def __call__(self, *values):
        values = lax.optimization_barrier(values + self.marks)[: len(values)]
        self.marks = values
        return values[0] if len(values) == 1 else values


def outer_bits():
    bits = []
    bit = 2
    while bit < lax.axis_size("dp"):
        bits.append(bit)
        bit *= 2
    return bits


class Gather:
    def __init__(self, parts):
        self.bits = outer_bits()
        half = len(self.bits) // 2
        self.orders = [
            self.bits[half * (n % 2) :] + self.bits[: half * (n % 2)] for n in range(len(parts))
        ]
        self.result = [[([0], part)] for part in parts]
        self.step = 0
        self.early = []

    def advance(self, order):
        held = self.result
        if self.step < len(self.bits):
            masks = [[m for mask, _ in pieces for m in mask] for pieces in held]
            blocks = [
                jnp.concatenate([array for _, array in pieces]) if self.step else pieces[0][1]
                for pieces in held
            ]
            blocks = order(*blocks)
            bits = [turn[self.step] for turn in self.orders]
            self.result = [
                [(mask, block), ([m ^ bit for m in mask], swap(block, "dp", bit))]
                for mask, block, bit in zip(masks, blocks, bits)
            ]
        else:
            rest = [pieces[1:] if self.early else pieces for pieces in held]
            arrays = iter(order(*[array for pieces in rest for _, array in pieces]))
            self.result = []
            for n, pieces in enumerate(rest):
                kept = [(masks, next(arrays)) for masks, _ in pieces]
                ours = held[n][:1] + kept if self.early else kept
                theirs = [([m ^ 1 for m in masks], swap(array, "dp", 1)) for masks, array in kept]
                self.result.append(ours + self.early[n : n + 1] + theirs)
        self.step += 1

    def send_early(self, order):
        arrays = order(*[pieces[0][1] for pieces in self.result])
        self.early = [
            ([m ^ 1 for m in pieces[0][0]], swap(array, "dp", 1))
            for pieces, array in zip(self.result, arrays)
        ]


def canonical_row(me, rank, block, mask, rank_mask, stride, offset):
    if mask is None:
        return offset
    row = (me ^ mask) * block + offset
    if stride:
        if rank_mask >= 2:
            rank_mask = rank_mask ^ ((rank + 1) // 2 % 2)
        row = row + (rank ^ rank_mask) * stride
    return pl.multiple_of(row, 16)


def place_kernel(plan, block, *refs):
    count = len(plan)
    ins = refs[:count]
    outs = refs[count:-1]
    sems = refs[-1]
    me = lax.axis_index("dp")
    rank = lax.axis_index("mp")
    copies = []
    for ref, moves in zip(ins, plan):
        for start, size, which, mask, column, _, offset in moves:
            row = canonical_row(me, rank, block, mask, 0, 0, offset)
            copy = pltpu.make_async_copy(
                ref.at[pl.ds(start, size), :],
                outs[which].at[pl.ds(row, size), pl.ds(column * D, D)],
                sems.at[len(copies)],
            )
            copy.start()
            copies.append(copy)
    for copy in copies:
        copy.wait()


def plan_of(gathered, layouts):
    arrays = []
    plan = []
    for pieces, layout in zip(gathered, layouts):
        rows = sum(size for _, size, *_ in layout)
        for masks, array in pieces:
            moves = []
            for j, mask in enumerate(masks):
                for start, size, which, rank_mask, stride, offset in layout:
                    moves.append((j * rows + start, size, which, mask, rank_mask, stride, offset))
            arrays.append(array)
            plan.append(moves)
    return arrays, plan


def place(arrays, plan, block, shapes):
    return pl.pallas_call(
        functools.partial(place_kernel, plan, block),
        out_shape=[jax.ShapeDtypeStruct(shape, low) for shape in shapes],
        in_specs=[pl.BlockSpec(memory_space=pl.ANY)] * len(arrays),
        out_specs=[pl.BlockSpec(memory_space=pltpu.VMEM)] * len(shapes),
        scratch_shapes=[pltpu.SemaphoreType.DMA((sum(len(moves) for moves in plan),))],
        compiler_params=pltpu.CompilerParams(vmem_limit_bytes=VMEM_LIMIT),
        cost_estimate=SMALL_COST,
        name="place",
    )(*arrays)


def store_split(value, keep, send, index):
    block = keep.shape[2]
    even = lax.axis_index("dp") % 2 == 0
    for outer in range(keep.shape[1]):
        first = value[2 * outer * block : (2 * outer + 1) * block]
        other = value[(2 * outer + 1) * block : (2 * outer + 2) * block]
        keep[index, outer] = jnp.where(even, first, other).astype(low)
        send[index, outer] = jnp.where(even, other, first).astype(low)


def middle_kernel(plan, block, total, *refs):
    limit_ref, vector_ref = refs[:2]
    token_hbm, mixed_hbm, log_hbm, cot_hbm, teach_hbm = refs[2:7]
    pieces = refs[7 : 7 + total]
    (
        out_hbm,
        middle_hbm,
        grad_hbm,
        down_keep,
        down_send,
        up_keep,
        up_send,
        delta_ref,
        log_ref,
        sum_ref,
    ) = refs[7 + total : 17 + total]
    (
        token,
        mixed,
        logs,
        cot,
        teach,
        up,
        down,
        proj,
        right,
        slope,
        second,
        middle,
        final,
        out,
        final_low,
        middle_low,
        grad,
        accum,
        turned,
        stage_keep,
        stage_send,
        in_sems,
        weight_sems,
        out_sems,
        keep_sems,
        send_sems,
    ) = refs[17 + total :]
    hidden = FF // D
    targets = (up, down, proj)
    rows = token.shape[0]
    me = lax.axis_index("dp")
    rank = lax.axis_index("mp")

    def fetch(ref, scratch, n):
        copy = pltpu.make_async_copy(ref, scratch, in_sems.at[n])
        copy.start()
        return copy

    def send(scratch, ref, n):
        copy = pltpu.make_async_copy(scratch, ref, out_sems.at[n])
        copy.start()
        return copy

    gets = [
        fetch(token_hbm, token, 0),
        fetch(mixed_hbm, mixed, 1),
        fetch(log_hbm, logs, 2),
        fetch(cot_hbm, cot, 3),
        fetch(teach_hbm, teach, 4),
    ]
    loads = {0: [], 1: [], 2: []}
    number = 0
    for want in (2, 0, 1):
        for ref, moves in zip(pieces, plan):
            for start, size, which, mask, rank_mask, stride, offset in moves:
                if which != want:
                    continue
                row = canonical_row(me, rank, block, mask, rank_mask, stride, offset)
                copy = pltpu.make_async_copy(
                    ref.at[pl.ds(start, size), :],
                    targets[which].at[pl.ds(row, size), :],
                    weight_sems.at[number],
                )
                copy.start()
                loads[which].append(copy)
                number += 1

    table_row = vector_ref[0:1, :]
    out_bias = vector_ref[1:2, :]
    gain = vector_ref[2:3, :]
    shift = vector_ref[3:4, :]
    down_bias = vector_ref[4:5, :]
    weight = vector_ref[5:6, :]
    gets[0].wait()
    gets[1].wait()
    right[2 * hidden] = mixed[...].astype(low)
    for copy in loads[2]:
        copy.wait()
    state = token[...].astype(full) + table_row + out_bias
    state = state + dot_of(right[2 * hidden], proj[...], 1, 1)
    middle[...] = state
    unit, _ = norm_stats(state)
    second[...] = (unit * gain + shift).astype(low)
    accum[...] = jnp.zeros((rows, D), full)
    for copy in loads[0]:
        copy.wait()
    for copy in loads[1]:
        copy.wait()

    def forward(m, _):
        place = pl.ds(pl.multiple_of(m * D, D), D)
        half = rows // 2
        spans = [pl.ds(part * half, half) for part in range(2)]
        values = [
            dot_of(second[span, :], up[place, :], 1, 0) + vector_ref[pl.ds(8 + m, 1), :]
            for span in spans
        ]
        for span, value in zip(spans, values):
            cumulative = 0.5 + 0.5 * lax.erf(value * (0.5**0.5))
            active = (value * cumulative).astype(low)
            right[m, span, :] = active
            slope[m, span, :] = (
                cumulative + value * jnp.exp(-0.5 * value * value) * 0.3989422804014327
            )
            accum[span, :] += dot_of(active, down[place, :], 1, 1)
        return 0

    lax.fori_loop(0, FF // D, forward, 0)
    final_state = middle[...] + accum[...] + down_bias
    out[...] = final_state.astype(low)
    puts = [send(out, out_hbm, 0)]
    gets[3].wait()
    gets[4].wait()
    place = lax.broadcasted_iota(jnp.int32, (rows, 1), 0)
    grads = cot[...].astype(full) + weight * (final_state - teach[...].astype(full))
    grads = jnp.where(place < limit_ref[5], grads, 0.0)
    final[...] = grads
    final_low[...] = grads.astype(low)
    sum_ref[3:4, :] = jnp.sum(grads, axis=0, keepdims=True)
    accum[...] = jnp.zeros((rows, D), full)

    def backward(m, _):
        place = pl.ds(pl.multiple_of(m * D, D), D)
        value = slope[m] * dot_of(final_low[...], down[place, :], 1, 0)
        value = value.astype(low)
        right[hidden + m] = value
        sum_ref[pl.ds(8 + m, 1), :] = jnp.sum(value.astype(full), axis=0, keepdims=True)
        accum[...] += dot_of(value, up[place, :], 1, 1)
        return 0

    lax.fori_loop(0, FF // D, backward, 0)
    unit, inverse = norm_stats(middle[...])
    second_grad = accum[...]
    sum_ref[0:1, :] = jnp.sum(second_grad * unit, axis=0, keepdims=True)
    sum_ref[1:2, :] = jnp.sum(second_grad, axis=0, keepdims=True)
    scaled = second_grad * gain
    mean_scaled = jnp.mean(scaled, axis=-1, keepdims=True)
    mean_unit = jnp.mean(scaled * unit, axis=-1, keepdims=True)
    total_grad = final[...] + inverse * (scaled - mean_scaled - unit * mean_unit)
    middle[...] = total_grad
    puts.append(send(middle, middle_hbm, 1))
    middle_low[...] = total_grad.astype(low)
    sum_ref[2:3, :] = jnp.sum(total_grad, axis=0, keepdims=True)
    attended_grad = dot_of(middle_low[...], proj[...], 1, 0).astype(low)
    grad[...] = attended_grad
    puts.append(send(grad, grad_hbm, 2))
    gets[2].wait()
    head = lax.broadcasted_iota(jnp.int32, (16, D), 0)
    lane = lax.broadcasted_iota(jnp.int32, (16, D), 1)
    member = jnp.where(lane // HEAD_DIM == head, 1.0, 0.0)
    leader = jnp.where(lane == head * HEAD_DIM, 1.0, 0.0)
    exact = functools.partial(
        lax.dot_general,
        dimension_numbers=(((1,), (1,)), ((), ())),
        precision=lax.Precision.HIGHEST,
        preferred_element_type=full,
    )
    deltas = exact(member, attended_grad.astype(full) * mixed[...])
    tops = exact(leader, logs[...])
    for pair in range(PAIRS):
        delta_ref[pair] = deltas[2 * pair : 2 * pair + 2]
        log_ref[pair] = tops[2 * pair : 2 * pair + 2]
    turned[0] = final_low[...].T
    turned[1] = second[...].T
    turned[2] = middle_low[...].T

    def weights(i, _):
        store_split(dot_of(turned[i // hidden], right[i], 1, 0), stage_keep, stage_send, i)

        @pl.when(i < hidden)
        def _():
            pltpu.make_async_copy(stage_keep.at[i], down_keep.at[i], keep_sems.at[i]).start()
            pltpu.make_async_copy(stage_send.at[i], down_send.at[i], send_sems.at[i]).start()

        @pl.when(i >= hidden)
        def _():
            row = i - hidden
            pltpu.make_async_copy(stage_keep.at[i], up_keep.at[row], keep_sems.at[i]).start()
            pltpu.make_async_copy(stage_send.at[i], up_send.at[row], send_sems.at[i]).start()

        return 0

    lax.fori_loop(0, 2 * hidden + 1, weights, 0)
    for copy in puts:
        copy.wait()
    for i in range(2 * hidden + 1):
        if i < hidden:
            keep, gone, row = down_keep, down_send, i
        else:
            keep, gone, row = up_keep, up_send, i - hidden
        pltpu.make_async_copy(stage_keep.at[i], keep.at[row], keep_sems.at[i]).wait()
        pltpu.make_async_copy(stage_send.at[i], gone.at[row], send_sems.at[i]).wait()


def middle_call(limit, vectors, tokens, mixed, logs, cot, teach, arrays, plan, block, dp):
    rows = tokens.shape[0]
    hidden = FF // D
    narrow = jax.ShapeDtypeStruct((rows, D), low)
    wide = jax.ShapeDtypeStruct((rows, D), full)
    shape = (dp // 2, D // dp, D)
    parts = [jax.ShapeDtypeStruct((count,) + shape, low) for count in (hidden, hidden + 1)]
    stats = jax.ShapeDtypeStruct((PAIRS, 2, rows), full)
    anywhere = pl.BlockSpec(memory_space=pl.ANY)
    inside = pl.BlockSpec(memory_space=pltpu.VMEM)
    moves = sum(len(part) for part in plan)
    return pl.pallas_call(
        functools.partial(middle_kernel, plan, block, len(arrays)),
        out_shape=(
            narrow,
            wide,
            narrow,
            parts[0],
            parts[0],
            parts[1],
            parts[1],
            stats,
            stats,
            jax.ShapeDtypeStruct((8 + 8, D), full),
        ),
        in_specs=[pl.BlockSpec(memory_space=pltpu.SMEM), inside]
        + [anywhere] * (5 + len(arrays)),
        out_specs=[anywhere] * 7 + [inside] * 3,
        scratch_shapes=[
            pltpu.VMEM((rows, D), low),
            pltpu.VMEM((rows, D), full),
            pltpu.VMEM((rows, D), full),
            pltpu.VMEM((rows, D), low),
            pltpu.VMEM((rows, D), low),
            pltpu.VMEM((FF, D), low),
            pltpu.VMEM((FF, D), low),
            pltpu.VMEM((D, D), low),
            pltpu.VMEM((2 * hidden + 1, rows, D), low),
            pltpu.VMEM((hidden, rows, D), full),
            pltpu.VMEM((rows, D), low),
            pltpu.VMEM((rows, D), full),
            pltpu.VMEM((rows, D), full),
            pltpu.VMEM((rows, D), low),
            pltpu.VMEM((rows, D), low),
            pltpu.VMEM((rows, D), low),
            pltpu.VMEM((rows, D), low),
            pltpu.VMEM((rows, D), full),
            pltpu.VMEM((3, D, rows), low),
            pltpu.VMEM((2 * hidden + 1,) + shape, low),
            pltpu.VMEM((2 * hidden + 1,) + shape, low),
            pltpu.SemaphoreType.DMA((5,)),
            pltpu.SemaphoreType.DMA((moves,)),
            pltpu.SemaphoreType.DMA((3,)),
            pltpu.SemaphoreType.DMA((2 * hidden + 1,)),
            pltpu.SemaphoreType.DMA((2 * hidden + 1,)),
        ],
        compiler_params=pltpu.CompilerParams(vmem_limit_bytes=VMEM_LIMIT),
        cost_estimate=SMALL_COST,
        name="middle",
    )(limit, vectors, tokens, mixed, logs, cot, teach, *arrays)


def fold_block(keep, got, out_keep, out_send, bit, place):
    step = 1 << place
    mine = (lax.axis_index("dp") // bit) % 2 * step
    for j in range(keep.shape[1] // 2):
        base = (j // step) * 2 * step + j % step
        for out, shift in ((out_keep, mine), (out_send, step - mine)):
            value = keep[0, base + shift].astype(full) + got[0, base + shift].astype(full)
            out[0, j] = value.astype(low)


def fold_kernel(bits, places, *refs):
    count = len(bits)
    for n in range(count):
        fold_block(
            *refs[2 * n : 2 * n + 2],
            *refs[2 * count + 2 * n : 2 * count + 2 * n + 2],
            bits[n],
            places[n],
        )


def fold(pairs, bits, places):
    lead = pairs[0][0].shape[0]
    block = lambda shape: pl.BlockSpec((1,) + shape[1:], lambda i: (i, 0, 0, 0))
    halves = [
        (keep.shape[0], keep.shape[1] // 2) + keep.shape[2:] for keep, _ in pairs for _ in range(2)
    ]
    outs = pl.pallas_call(
        functools.partial(fold_kernel, bits, places),
        out_shape=[jax.ShapeDtypeStruct(shape, low) for shape in halves],
        grid=(lead,),
        in_specs=[block(value.shape) for pair in pairs for value in pair],
        out_specs=[block(shape) for shape in halves],
        compiler_params=pltpu.CompilerParams(vmem_limit_bytes=VMEM_LIMIT),
        cost_estimate=pl.CostEstimate(flops=0, bytes_accessed=16 << 20, transcendentals=0),
        name="fold",
    )(*[value for pair in pairs for value in pair])
    return [(outs[2 * n], outs[2 * n + 1]) for n in range(len(pairs))]


def qkv_grad_kernel(count, *refs):
    sources = refs[: 3 * count + 1]
    outs = refs[3 * count + 1 : 3 * count + 5]
    sum_ref, held, turned, total, stage, in_sems, out_sems = refs[3 * count + 5 :]
    first_use = [0, count] + list(range(1, count)) + list(range(count + 1, 3 * count + 1))
    for n in first_use:
        pltpu.make_async_copy(sources[n], held.at[n], in_sems.at[n]).start()

    def wait(n):
        pltpu.make_async_copy(sources[0], held.at[n], in_sems.at[n]).wait()

    def turn(n, _):
        wait(n)
        turned[n] = held[n].T
        return 0

    lax.fori_loop(0, count, turn, 0)
    sum_ref[...] = jnp.zeros_like(sum_ref)

    def step(i, _):
        c = (i + count - 1) // count
        n = jnp.where(i == 0, 0, (i + count - 1) % count)
        wait(count + i)
        right = held[count + i]
        value = dot_of(turned[n], right, 1, 0)
        total[...] = value + jnp.where(n == 0, jnp.zeros_like(value), total[...])

        @pl.when(c != 1)
        def _():
            row = pl.ds(pl.multiple_of(c * 4, 8), 1)
            sum_ref[row, :] += jnp.sum(right.astype(full), axis=0, keepdims=True)

        @pl.when(i % count == 0)
        def _():
            for part in range(2):
                store_split(
                    total[:, part * D // 2 : (part + 1) * D // 2],
                    stage.at[part],
                    stage.at[2 + part],
                    c,
                )
            for k in range(4):
                pltpu.make_async_copy(
                    stage.at[k, c], outs[k].at[c], out_sems.at[k * 3 + c]
                ).start()

        return 0

    lax.fori_loop(0, 2 * count + 1, step, 0)
    for k in range(4):
        for c in range(3):
            pltpu.make_async_copy(stage.at[k, c], outs[k].at[c], out_sems.at[k * 3 + c]).wait()


def qkv_grads(chunks, query_grad, key_grads, value_grads, dp):
    rows = query_grad.shape[0]
    count = len(chunks)
    shape = (3, dp // 2, D // dp, D // 2)
    anywhere = pl.BlockSpec(memory_space=pl.ANY)
    return pl.pallas_call(
        functools.partial(qkv_grad_kernel, count),
        out_shape=[jax.ShapeDtypeStruct(shape, low)] * 4
        + [jax.ShapeDtypeStruct((16, D), full)],
        in_specs=[anywhere] * (3 * count + 1),
        out_specs=[anywhere] * 4 + [pl.BlockSpec(memory_space=pltpu.VMEM)],
        scratch_shapes=[
            pltpu.VMEM((3 * count + 1, rows, D), low),
            pltpu.VMEM((count, D, rows), low),
            pltpu.VMEM((D, D), full),
            pltpu.VMEM((4,) + shape, low),
            pltpu.SemaphoreType.DMA((3 * count + 1,)),
            pltpu.SemaphoreType.DMA((12,)),
        ],
        compiler_params=pltpu.CompilerParams(vmem_limit_bytes=VMEM_LIMIT),
        cost_estimate=SMALL_COST,
        name="qkv_grads",
    )(*chunks, query_grad, *key_grads, *value_grads)


def last_kernel(
    token_ref,
    first_ref,
    right_ref,
    left_ref,
    middle_ref,
    vector_ref,
    gain_ref,
    bias_ref,
    sum_ref,
    out_ref,
    pack_ref,
):
    @pl.when(pl.program_id(0) == 0)
    def _():
        pack_ref[...] = jnp.zeros_like(pack_ref)
        pack_ref[1:2, :] = sum_ref[0:1, :]
        pack_ref[3:4, :] = sum_ref[1:2, :]
        pack_ref[4:5, :] = bias_ref[0:1, :]
        pack_ref[5:6, :] = bias_ref[8:9, :]
        pack_ref[6:8, :] = sum_ref[2:4, :]
        pack_ref[8 : 8 + FF // D, :] = sum_ref[8 : 8 + FF // D, :]

    unit, inverse = norm_stats(token_ref[...].astype(full) + vector_ref[0:1, :])
    grad = first_ref[...] + right_ref[...].astype(full) + left_ref[...].astype(full)
    scaled = grad * gain_ref[0:1, :]
    mean_scaled = jnp.mean(scaled, axis=-1, keepdims=True)
    mean_unit = jnp.mean(scaled * unit, axis=-1, keepdims=True)
    result = middle_ref[...] + inverse * (scaled - mean_scaled - unit * mean_unit)
    out_ref[...] = result
    pack_ref[0:1, :] += jnp.sum(grad * unit, axis=0, keepdims=True)
    pack_ref[2:3, :] += jnp.sum(grad, axis=0, keepdims=True)
    pack_ref[pl.ds(16 + lax.axis_index("dp"), 1), :] += jnp.sum(result, axis=0, keepdims=True)


def last_norm(tokens, first, right, left, middle_grad, vectors, gains, bias_sums, sums, dp):
    rows = tokens.shape[0]
    part = pl.BlockSpec((rows // 4, D), lambda i: (i, 0))
    whole = lambda value: pl.BlockSpec(value.shape, lambda i: (0, 0))
    small = (vectors, gains, bias_sums, sums)
    return pl.pallas_call(
        last_kernel,
        out_shape=(
            jax.ShapeDtypeStruct((rows, D), full),
            jax.ShapeDtypeStruct((16 + dp, D), full),
        ),
        grid=(4,),
        in_specs=[part] * 5 + [whole(value) for value in small],
        out_specs=[part, pl.BlockSpec((16 + dp, D), lambda i: (0, 0))],
        compiler_params=pltpu.CompilerParams(vmem_limit_bytes=VMEM_LIMIT),
        cost_estimate=SMALL_COST,
        name="last_norm",
    )(tokens, first, right, left, middle_grad, *small)


def two_parts(value, axis, mine):
    keep = lax.dynamic_index_in_dim(value, mine, axis, keepdims=False)
    send = lax.dynamic_index_in_dim(value, 1 - mine, axis, keepdims=False)
    return keep, send.astype(low)


class Scatter:
    def __init__(self, parts, turns):
        self.bits = outer_bits()
        half = len(self.bits) // 2
        self.orders = [
            [1] + self.bits[half * (turn % 2) :] + self.bits[: half * (turn % 2)] for turn in turns
        ]
        self.left = [list(self.bits) for _ in turns]
        self.step = 0
        self.parts = parts

    def sends(self):
        return [send for _, send in self.parts]

    def exchange(self, sends):
        self.pairs = [
            (keep, swap(send, "dp", turn[self.step]))
            for (keep, _), send, turn in zip(self.parts, sends, self.orders)
        ]
        self.step += 1

    def folds(self):
        if self.step > len(self.bits):
            return [], [], []
        bits = [turn[self.step] for turn in self.orders]
        places = []
        for left, bit in zip(self.left, bits):
            places.append(left.index(bit))
            left.remove(bit)
        return self.pairs, bits, places

    def give(self, outs):
        self.parts = [(outs[n], outs[n + 1]) for n in range(0, len(outs), 2)]

    def fold(self):
        outs = []
        for pair, bit, at in zip(*self.folds()):
            outs += fold([pair], [bit], [at])[0]
        self.give(outs)

    def advance(self, order):
        sends = order(*self.sends())
        self.exchange(list(sends) if len(self.parts) > 1 else [sends])

    def finish(self, order):
        while self.step <= len(self.bits):
            self.fold()
            self.advance(order)
        got = order(*[other for _, other in self.pairs])
        return [
            (keep.astype(full) + other.astype(full))[:, 0]
            for (keep, _), other in zip(self.pairs, got)
        ]


def scatter_dp(parts, turns):
    scatter = Scatter(parts, turns)
    while True:
        sends = yield scatter.sends()
        scatter.exchange(sends)
        if scatter.step > len(scatter.bits):
            break
        scatter.parts = fold(*scatter.folds())
    got = yield [other for _, other in scatter.pairs]
    return [
        (keep.astype(full) + other.astype(full))[:, 0]
        for (keep, _), other in zip(scatter.pairs, got)
    ]


def scatter_mp(value):
    rank = lax.axis_index("mp")
    part = lambda index: lax.dynamic_index_in_dim(value, index, keepdims=False)
    sends = yield [part(rank ^ bit).astype(low) for bit in (1, 2, 3)]
    got = yield [swap(send, "mp", bit) for bit, send in zip((1, 2, 3), sends)]
    got = [other.astype(full) for other in got]
    return (part(rank) + got[0]) + (got[1] + got[2])


def halve_mp(value):
    rank = lax.axis_index("mp")
    pairs = value.reshape((2, 2) + value.shape[1:])
    keep, send = two_parts(pairs, 1, rank % 2)
    (send,) = yield [send]
    (got,) = yield [swap(send, "mp", 1)]
    keep, send = two_parts(keep.astype(full) + got.astype(full), 0, rank // 2)
    (send,) = yield [send]
    (got,) = yield [swap(send, "mp", 2)]
    return keep + got.astype(full)


def scatter_feed(up_own, down_own):
    mp = lax.axis_size("mp")
    block = down_own.shape[1]
    out_own = up_own[mp].reshape(block, mp, -1).transpose(1, 0, 2)
    own = yield from halve_mp(
        jnp.concatenate([up_own[:mp], down_own, out_own.reshape(mp, -1, D)], axis=1)
    )
    return own[:block], own[block : 2 * block].T, own[2 * block :].reshape(block, -1).T


def scatter_qkv(keep_left, keep_right, send_left, send_right):
    left_part, right_part = yield from scatter_dp(
        [(keep_left, send_left), (keep_right, send_right)], (0, 1)
    )
    width = D // lax.axis_size("mp")
    parts = [part[..., at : at + width] for part in (left_part, right_part) for at in (0, width)]
    return (yield from scatter_mp(jnp.stack(parts)))


def sum_small(value):
    (value,) = yield [value]
    value = value + swap(value, "dp", 1)
    bits = outer_bits()
    groups = [("dp", bits[n : n + 2]) for n in range(0, len(bits), 2)] + [("mp", [1, 2])]
    for axis, pair in groups:
        (value,) = yield [value]
        if len(pair) == 1:
            value = value + swap(value, axis, pair[0])
        else:
            one, two = pair
            got = [swap(value, axis, mask) for mask in (one, two, one + two)]
            if axis == "mp":
                got = yield got
            value = (value + got[0]) + (got[1] + got[2])
    return value


class Steps:
    def __init__(self, steps):
        self.steps = steps
        self.pending = next(steps)
        self.result = None

    def advance(self, order):
        if self.pending is None:
            return
        sends = order(*self.pending)
        sends = [sends] if len(self.pending) == 1 else list(sends)
        try:
            self.pending = self.steps.send(sends)
        except StopIteration as stop:
            self.pending = None
            self.result = stop.value

    def finish(self, order):
        while self.pending is not None:
            self.advance(order)
        return self.result


def shards(
    tokens_in,
    timesteps,
    lengths,
    time_table,
    norm_gains,
    norm_biases,
    w_qkv,
    qv_bias,
    w_out,
    out_bias,
    w_up,
    up_bias,
    w_down,
    down_bias,
    cotangent,
    teacher,
):
    rank = lax.axis_index("mp")
    data_rank = lax.axis_index("dp")
    mp = lax.axis_size("mp")
    dp = lax.axis_size("dp")
    own_rows = tokens_in.shape[0]
    length = lax.dynamic_index_in_dim(lengths, data_rank, keepdims=False)
    own_time = lax.dynamic_index_in_dim(timesteps, data_rank, keepdims=False)
    odd = rank % 2 == 1
    upper = rank >= 2
    middle = jnp.logical_or(rank == 1, rank == 2)
    order = Order()
    along = lambda value, pairs: lax.ppermute(value, "mp", pairs)

    block = w_qkv.shape[1]
    aligned = block % 32 == 0
    narrow = order(jnp.concatenate([w_qkv.reshape(3 * block, -1), w_out.T]))
    first_swap = swap(narrow, "mp", 1)
    tall = order(jnp.concatenate([w_up, w_down.T]))
    tall_swap = swap(tall, "mp", 1)
    pair = order(
        jnp.concatenate(
            [jnp.where(odd, first_swap, narrow), jnp.where(odd, narrow, first_swap)], axis=1
        )
    )
    second_swap = swap(pair, "mp", 2)
    tokens, lengths, own_time, norm_gains, norm_biases, out_bias, down_bias, up_bias, length = order(
        tokens_in, lengths, own_time, norm_gains, norm_biases, out_bias, down_bias, up_bias, length
    )
    table_row = lax.dynamic_slice_in_dim(time_table, own_time, 1).astype(full)
    unit_one, _ = norm_stats(tokens.astype(full) + table_row)
    first_norm = (unit_one * norm_gains[0] + norm_biases[0]).astype(low)
    loss_weight = lengths.shape[0] * MAXLEN / jnp.sum(lengths).astype(full)
    vectors = jnp.concatenate(
        [
            table_row,
            out_bias[None],
            norm_gains[1:2],
            norm_biases[1:2],
            down_bias[None],
            jnp.full((3, D), loss_weight),
            up_bias.reshape(-1, D),
            jnp.zeros((4, D), full),
        ]
    )
    scalars = jnp.stack(
        [
            rank,
            jnp.where(rank == 0, 1, rank - 1),
            jnp.where(upper, rank - 2, rank + 2),
            jnp.where(middle, rank + 1, 3 - rank),
            length,
            length - rank * own_rows,
        ]
    ).astype(jnp.int32)
    first_norm, vectors, scalars = order(first_norm, vectors, scalars)
    wide = jnp.concatenate(
        [jnp.where(upper, second_swap, pair), jnp.where(upper, pair, second_swap)], axis=1
    )
    qkv_rows, out_rows = wide[: 3 * block], wide[3 * block :]
    if aligned:
        split = 3 * block // 2
        qkv_gather = Gather([qkv_rows[:split], qkv_rows[split:]])
        qkv_gather.advance(order)
    tall = order(jnp.concatenate([tall, tall_swap]))
    tall_across = along(tall, [(1, 2), (2, 1)])

    sent = order(first_norm)
    from_left = along(sent, [(0, 1), (1, 2), (2, 3)])
    from_right = along(sent, [(1, 0), (2, 1), (3, 2)])
    tall_across = order(tall_across)
    tall_far = along(tall_across, [(1, 0), (2, 3)])
    if aligned:
        while qkv_gather.step < len(qkv_gather.bits):
            qkv_gather.advance(order)
        qkv_gather.advance(order)
    hop_right, hop_left = order(from_left, from_right)
    second_right = along(hop_right, [(1, 2), (2, 3)])
    second_left = along(hop_left, [(1, 0), (2, 1)])
    if aligned:
        arrays, plan = plan_of(
            qkv_gather.result,
            [
                [(0, block, 0, 0, 0, 0), (block, split - block, 1, 0, 0, 0)],
                [
                    (0, 2 * block - split, 1, 0, 0, split - block),
                    (2 * block - split, block, 1, 1, 0, 0),
                ],
            ],
        )
        query_weight, pair_weight = order(*place(arrays, plan, block, [(D, D), (D, 2 * D)]))
        tall_other = jnp.where(middle, tall_across, order(tall_far))
        feed_gather = Gather(
            [
                jnp.concatenate([tall, out_rows[: block // 2]]),
                jnp.concatenate([tall_other, out_rows[block // 2 :]]),
            ]
        )
        feed_gather.advance(order)
    else:
        weights = lax.all_gather(qkv_rows.reshape(3, block, D), "dp", axis=1, tiled=True)
        query_weight = weights[0]
        pair_weight = jnp.concatenate([weights[1], weights[2]], axis=1)
    near = jnp.where(rank == 0, hop_left, hop_right)
    attend = lambda parts, numbers, carried: order(
        *attend_forward(
            parts,
            numbers,
            scalars,
            query_weight,
            pair_weight,
            qv_bias[0:1],
            qv_bias[1:2],
            carried,
        )
    )
    key_own, value_own, queries, *state = attend([order(first_norm)], (0,), None)
    second_right, second_left = order(second_right, second_left)
    second = order(jnp.where(upper, second_right, second_left))
    third = along(second, [(1, 0), (2, 3)])
    if aligned:
        while feed_gather.step < len(feed_gather.bits):
            feed_gather.advance(order)
        feed_gather.send_early(order)
    near, second = order(near, second)
    key_near, key_second, value_near, value_second, *state = attend(
        [near, second], (1, 2), (queries, *state)
    )
    last = order(jnp.where(middle, hop_left, order(third)))
    key_last, value_last, mixed, logs = attend([order(last)], (3,), (queries, *state))
    if aligned:
        feed_gather.advance(order)
        layout = lambda masks, shift: [
            (0, block, 0, masks[0], D, 0),
            (block, block, 1, masks[0], D, 0),
            (2 * block, block, 0, masks[1], D, 0),
            (3 * block, block, 1, masks[1], D, 0),
            (4 * block, block // 2, 2, 0, 0, shift),
        ]
        arrays, plan = plan_of(
            feed_gather.result, [layout((0, 1), 0), layout((2, 3), block // 2)]
        )
    else:
        arrays = [
            lax.all_gather(w_up, ("mp", "dp"), axis=0, tiled=True),
            lax.all_gather(w_down.T, ("mp", "dp"), axis=0, tiled=True),
            lax.all_gather(out_rows, "dp", axis=0, tiled=True),
        ]
        plan = [[(0, array.shape[0], n, None, 0, 0, 0)] for n, array in enumerate(arrays)]
    chunks = [first_norm, near, second, last]
    keys = [key_own, key_near, key_second, key_last]
    values = [value_own, value_near, value_second, value_last]

    output, middle_grad, attended_grad, *parts, deltas, log_rows, sums = middle_call(
        scalars, vectors, tokens, mixed, logs, cotangent, teacher, arrays, plan, block, dp
    )
    scatter = Scatter([(parts[0], parts[1]), (parts[2], parts[3])], (1, 0))
    scatter.advance(order)

    key_grads = [None] * 4
    value_grads = [None] * 4
    firsts = [None] * 4
    query_grad = None
    for n in (3, 2, 1, 0):
        pairs, bits, places = scatter.folds() if n % 2 == 0 else ([], [], [])
        query_grad, key_grads[n], value_grads[n], firsts[n], *folded = attend_backward(
            n,
            queries,
            keys[n],
            values[n],
            order(attended_grad),
            log_rows,
            deltas,
            query_weight,
            pair_weight,
            scalars,
            query_grad,
            n == 0,
            pairs,
            bits,
            places,
        )
        firsts[n] = order(firsts[n])
        if folded:
            scatter.give(folded)
        if n == 3:
            back_last = along(firsts[3], [(0, 1), (3, 2)]).astype(full)
        elif n == 2:
            scatter.advance(order)
            payload = order((firsts[2] + back_last).astype(low))
            back_right = along(payload, [(0, 1), (1, 2)]).astype(full)
            back_left = along(payload, [(3, 2), (2, 1)]).astype(full)
        elif n == 1:
            to_right = jnp.where(
                rank == 0, firsts[1], firsts[3].astype(full) + back_right
            ).astype(low)
            to_left = (firsts[1] + back_left).astype(low)
            to_right, to_left = order(to_right, to_left)
            final_right = along(to_right, [(0, 1), (1, 2), (2, 3)])
            final_left = along(to_left, [(3, 2), (2, 1), (1, 0)])
    scatter.advance(order)
    query_grad, final_right, final_left = order(query_grad, final_right, final_left)
    *halves, bias_sums = qkv_grads(chunks, query_grad, key_grads, value_grads, dp)
    qkv = Steps(scatter_qkv(*halves))
    qkv.advance(order)
    down_own, up_own = scatter.finish(order)
    feed = Steps(scatter_feed(up_own, down_own))
    feed.advance(order)
    qkv.advance(order)
    tokens, first_own = order(tokens, firsts[0])
    input_grad, packed = last_norm(
        tokens,
        first_own,
        final_right,
        final_left,
        middle_grad,
        vectors,
        norm_gains,
        bias_sums,
        sums,
        dp,
    )
    packed, input_grad = order(packed, input_grad)
    small = Steps(sum_small(packed))
    feed.advance(order)
    feed.advance(order)
    small.advance(order)
    qkv.advance(order)
    feed.advance(order)
    qkv.advance(order)
    small.advance(order)
    qkv.advance(order)
    small.advance(order)
    total = small.finish(order)
    up_grad, down_grad, out_grad = feed.finish(order)
    qkv_grad = qkv.finish(order)
    fixed = 16
    chosen = (timesteps[None, :] == jnp.arange(time_table.shape[0])[:, None]).astype(full)
    table_grad = lax.dot_general(
        chosen,
        total[fixed:],
        (((1,), (0,)), ((), ())),
        precision=lax.Precision.HIGHEST,
        preferred_element_type=full,
    )
    return (
        output,
        input_grad,
        table_grad,
        total[0:2],
        total[2:4],
        qkv_grad,
        total[4:6],
        out_grad,
        total[6],
        up_grad,
        total[8 : 8 + FF // D].reshape(FF),
        down_grad,
        total[7],
    )


def solution(mesh):
    rows = P(both, None)
    placed = (
        rows,
        P(),
        P(),
        P(),
        P(),
        P(),
        P(None, "dp", "mp"),
        P(),
        P("mp", "dp"),
        P(),
        P("dp", "mp"),
        P(),
        P("mp", "dp"),
        P(),
        rows,
        rows,
    )
    return jax.shard_map(
        shards,
        mesh=mesh,
        in_specs=placed,
        out_specs=(
            rows,
            rows,
            P(),
            P(),
            P(),
            P(None, "dp", "mp"),
            P(),
            P("mp", "dp"),
            P(),
            P("dp", "mp"),
            P(),
            P("mp", "dp"),
            P(),
        ),
        check_vma=False,
    )
```

```python
import functools

import jax
import jax.numpy as jnp
from jax import lax
from jax.experimental import pallas as pl
from jax.experimental.pallas import tpu as pltpu
from jax.sharding import PartitionSpec as P

D = 768
HEADS = 12
HEAD_DIM = 64
FF = 3072
MAXLEN = 2048
PAIR = 2 * HEAD_DIM
PAIRS = HEADS // 2
VMEM_LIMIT = 58 << 20
SMALL_COST = pl.CostEstimate(flops=1 << 20, bytes_accessed=1 << 16, transcendentals=0)

far_below = -1e30
epsilon = 1e-05
score_scale = HEAD_DIM ** (-0.5)
low = jnp.bfloat16
full = jnp.float32
both = ("dp", "mp")


def norm_stats(values):
    center = values - jnp.mean(values, axis=-1, keepdims=True)
    spread = jnp.mean(center * center, axis=-1, keepdims=True)
    inverse = lax.rsqrt(spread + epsilon)
    return center * inverse, inverse


def dot_of(left_side, right_side, left_dim, right_dim):
    return lax.dot_general(
        left_side,
        right_side,
        (((left_dim,), (right_dim,)), ((), ())),
        preferred_element_type=full,
    )


def first_half(shape):
    return lax.broadcasted_iota(jnp.int32, shape, len(shape) - 1) < HEAD_DIM


def forward_kernel(numbers, first, final, scalars, *refs):
    count = len(numbers)
    chunk_refs = refs[:count]
    wk_ref, wv_ref, value_bias_ref = refs[count : count + 3]
    refs = refs[count + 3 :]
    if first:
        wq_ref, query_bias_ref = refs[:2]
        key_outs, value_outs = refs[2 : 2 + count], refs[2 + count : 2 + 2 * count]
        query_out, top_ref, sum_ref, acc_ref = refs[2 + 2 * count :]
        q_pair = (dot_of(chunk_refs[0][...], wq_ref[...], 1, 0) + query_bias_ref[...]).astype(low)
        q_pair = q_pair * jnp.asarray(score_scale, low)
        query_out[...] = q_pair
    else:
        q_ref, top_in, sum_in, acc_in = refs[:4]
        key_outs, value_outs = refs[4 : 4 + count], refs[4 + count : 4 + 2 * count]
        results = refs[4 + 2 * count :]
        q_pair = q_ref[...]
    weight = jnp.concatenate([wk_ref[...], wv_ref[...]], axis=1)
    keys = []
    values = []
    for n in range(count):
        both_parts = dot_of(chunk_refs[n][...], weight, 1, 0)
        keys.append(both_parts[:, :PAIR].astype(low))
        values.append((both_parts[:, PAIR:] + value_bias_ref[...]).astype(low))
        key_outs[n][...] = keys[n]
        value_outs[n][...] = values[n]
    rows = q_pair.shape[0]
    size = keys[0].shape[0]
    place = lax.broadcasted_iota(jnp.int32, (1, size), 1)
    lower = first_half((rows, PAIR))
    parts = []
    for half in range(2):
        kept = lower if half == 0 else jnp.logical_not(lower)
        q_half = jnp.where(kept, q_pair, jnp.zeros_like(q_pair))
        scores = []
        for n in range(count):
            bias = jnp.where(place + scalars[numbers[n]] * size < scalars[4], 0.0, far_below)
            scores.append(dot_of(q_half, keys[n], 1, 1) + bias)
        highest = functools.reduce(
            jnp.maximum, [jnp.max(score, axis=-1, keepdims=True) for score in scores]
        )
        totals = jnp.zeros_like(highest)
        mixed = jnp.zeros((rows, PAIR), full)
        for n in range(count):
            exp_scores = jnp.exp(scores[n] - highest)
            totals = totals + jnp.sum(exp_scores, axis=-1, keepdims=True)
            mixed = mixed + dot_of(exp_scores.astype(low), values[n], 1, 0)
        parts.append((highest, totals, mixed))
    top = jnp.where(lower, parts[0][0], parts[1][0])
    total = jnp.where(lower, parts[0][1], parts[1][1])
    mixed = jnp.where(lower, parts[0][2], parts[1][2])
    if first:
        top_ref[...] = top
        sum_ref[...] = total
        acc_ref[...] = mixed
    else:
        highest = jnp.maximum(top, top_in[...])
        here = jnp.exp(top - highest)
        before = jnp.exp(top_in[...] - highest)
        total = total * here + sum_in[...] * before
        mixed = mixed * here + acc_in[...] * before
        if final:
            results[0][...] = mixed / total
            results[1][...] = highest + jnp.log(total)
        else:
            results[0][...] = highest
            results[1][...] = total
            results[2][...] = mixed


def attend_forward(chunks, numbers, scalars, query_weight, pair_weight, query_bias, value_bias, carried):
    rows = chunks[0].shape[0]
    count = len(chunks)
    first = carried is None
    final = 3 in numbers
    column = lambda height, c: pl.BlockSpec((height, PAIR), lambda i, n: (0, c * PAIRS + i))
    whole = pl.BlockSpec((rows, D), lambda i, n: (0, 0))
    wide = jax.ShapeDtypeStruct((rows, D), full)
    narrow = jax.ShapeDtypeStruct((rows, D), low)
    extra = (query_weight, query_bias) if first else carried
    results = (narrow,) * first + (wide,) * (2 if final else 3)
    return pl.pallas_call(
        functools.partial(forward_kernel, numbers, first, final),
        out_shape=(narrow,) * (2 * count) + results,
        grid_spec=pltpu.PrefetchScalarGridSpec(
            num_scalar_prefetch=1,
            grid=(PAIRS,),
            in_specs=[whole] * count
            + [column(D, 0), column(D, 1), column(1, 0)]
            + ([column(D, 0), column(1, 0)] if first else [column(rows, 0)] * 4),
            out_specs=[column(rows, 0)] * (2 * count + len(results)),
        ),
        compiler_params=pltpu.CompilerParams(vmem_limit_bytes=VMEM_LIMIT),
        cost_estimate=SMALL_COST,
        name="attend_forward",
    )(scalars, *chunks, pair_weight, pair_weight, value_bias, *extra)


def backward_kernel(
    number,
    first,
    last,
    folds,
    scalars,
    q_ref,
    k_ref,
    v_ref,
    g_ref,
    log_ref,
    delta_ref,
    wk_ref,
    wv_ref,
    *refs
):
    if last:
        wq_ref = refs[0]
        refs = refs[1:]
    if not first:
        dq_in = refs[0]
        refs = refs[1:]
    count = len(folds)
    fold_ins, refs = refs[: 2 * count], refs[2 * count :]
    dq_ref, dk_ref, dv_ref, back_ref = refs[:4]
    fold_outs, accum = refs[4:-1], refs[-1]
    step = pl.program_id(0)
    for n, (lead, bit, at) in enumerate(folds):

        @pl.when(step < lead)
        def _():
            fold_block(
                *fold_ins[2 * n : 2 * n + 2], *fold_outs[2 * n : 2 * n + 2], bit, at
            )

    rows = q_ref.shape[0]
    keys = k_ref.shape[0]
    limit = scalars[4] - scalars[number] * keys
    q_pair = q_ref[...]
    g_pair = g_ref[...]
    k_pair = k_ref[...]
    v_pair = v_ref[...]
    lower = first_half((rows, PAIR))
    nothing = jnp.zeros((rows, PAIR), low)
    two_halves = lambda pair: jnp.concatenate(
        [jnp.where(lower, pair, nothing), jnp.where(lower, nothing, pair)]
    )
    queries = two_halves(q_pair)
    grads_out = two_halves(g_pair)
    row_of = lambda ref: jnp.concatenate([ref[0, 0:1, :], ref[0, 1:2, :]], axis=1)
    place = lax.broadcasted_iota(jnp.int32, (keys, 1), 0)
    bias = jnp.where(place < limit, 0.0, far_below)
    scores = dot_of(k_pair, queries, 1, 1) + bias
    prob_grad = dot_of(v_pair, grads_out, 1, 1)
    probs = jnp.exp(scores - row_of(log_ref))
    score_grad = (probs * (prob_grad - row_of(delta_ref))).astype(low)
    dv_low = dot_of(probs.astype(low), grads_out, 1, 0).astype(low)
    dk_low = dot_of(score_grad, queries, 1, 0).astype(low)
    turned = dot_of(k_pair.T, score_grad, 1, 0)
    upper_rows = lax.broadcasted_iota(jnp.int32, (PAIR, rows), 0) < HEAD_DIM
    dk_ref[...] = dk_low
    dv_ref[...] = dv_low
    grads = [dk_low, dv_low]
    weights = [wk_ref[...], wv_ref[...]]
    dq_all = jnp.where(upper_rows, turned[:, :rows], turned[:, rows:]).T
    if not first:
        dq_all = dq_all + dq_in[...]
    back = dot_of(jnp.concatenate(grads, axis=1), jnp.concatenate(weights, axis=1), 1, 1)
    if last:
        dq_low = (dq_all * score_scale).astype(low)
        dq_ref[...] = dq_low
        back = back + dot_of(dq_low, wq_ref[...], 1, 1)
    else:
        dq_ref[...] = dq_all

    @pl.when(step == 0)
    def _():
        accum[...] = back

    @pl.when(step > 0)
    def _():
        accum[...] += back

    @pl.when(step == PAIRS - 1)
    def _():
        back_ref[...] = accum[...].astype(back_ref.dtype)


def attend_backward(
    number,
    queries,
    keys,
    values,
    grads,
    logs,
    deltas,
    query_weight,
    pair_weight,
    scalars,
    carried,
    last,
    pairs,
    bits,
    places,
):
    rows, total = queries.shape[0], keys.shape[0]
    first = carried is None
    folds = [(keep.shape[0], bit, at) for (keep, _), bit, at in zip(pairs, bits, places)]
    halves = [
        (keep.shape[0], keep.shape[1] // 2) + keep.shape[2:] for keep, _ in pairs for _ in range(2)
    ]

    def by_lead(shape):
        end = shape[0] - 1
        return pl.BlockSpec((1,) + shape[1:], lambda i, n: (jnp.minimum(i, end), 0, 0, 0))

    column = lambda count, c: pl.BlockSpec((count, PAIR), lambda i, n: (0, c * PAIRS + i))
    stats = pl.BlockSpec((1, 2, rows), lambda i, n: (i, 0, 0))
    extra = (query_weight,) * last + (() if first else (carried,))
    extra_specs = [column(D, 0)] * last + ([] if first else [column(rows, 0)])
    return pl.pallas_call(
        functools.partial(backward_kernel, number, first, last, folds),
        out_shape=(
            jax.ShapeDtypeStruct((rows, D), low if last else full),
            jax.ShapeDtypeStruct((total, D), low),
            jax.ShapeDtypeStruct((total, D), low),
            jax.ShapeDtypeStruct((total, D), low if first else full),
            *[jax.ShapeDtypeStruct(shape, low) for shape in halves],
        ),
        grid_spec=pltpu.PrefetchScalarGridSpec(
            num_scalar_prefetch=1,
            grid=(PAIRS,),
            in_specs=[
                column(rows, 0),
                column(total, 0),
                column(total, 0),
                column(rows, 0),
                stats,
                stats,
                column(D, 0),
                column(D, 1),
            ]
            + extra_specs
            + [by_lead(value.shape) for pair in pairs for value in pair],
            out_specs=[
                column(rows, 0),
                column(total, 0),
                column(total, 0),
                pl.BlockSpec((total, D), lambda i, n: (0, 0)),
            ]
            + [by_lead(shape) for shape in halves],
            scratch_shapes=[pltpu.VMEM((total, D), full)],
        ),
        compiler_params=pltpu.CompilerParams(vmem_limit_bytes=VMEM_LIMIT),
        cost_estimate=SMALL_COST,
        name="attend_backward",
    )(
        scalars,
        queries,
        keys,
        values,
        grads,
        logs,
        deltas,
        pair_weight,
        pair_weight,
        *extra,
        *[value for pair in pairs for value in pair],
    )


def swap(value, axis, bit):
    count = lax.axis_size(axis)
    return lax.ppermute(value, axis, [(i, i ^ bit) for i in range(count)])


class Order:
    def __init__(self):
        self.marks = ()

    def __call__(self, *values):
        values = lax.optimization_barrier(values + self.marks)[: len(values)]
        self.marks = values
        return values[0] if len(values) == 1 else values


def outer_bits():
    bits = []
    bit = 2
    while bit < lax.axis_size("dp"):
        bits.append(bit)
        bit *= 2
    return bits


class Gather:
    def __init__(self, parts):
        self.bits = outer_bits()
        half = len(self.bits) // 2
        self.orders = [
            self.bits[half * (n % 2) :] + self.bits[: half * (n % 2)] for n in range(len(parts))
        ]
        self.result = [[([0], part)] for part in parts]
        self.step = 0
        self.early = []

    def advance(self, order):
        held = self.result
        if self.step < len(self.bits):
            masks = [[m for mask, _ in pieces for m in mask] for pieces in held]
            blocks = [
                jnp.concatenate([array for _, array in pieces]) if self.step else pieces[0][1]
                for pieces in held
            ]
            blocks = order(*blocks)
            bits = [turn[self.step] for turn in self.orders]
            self.result = [
                [(mask, block), ([m ^ bit for m in mask], swap(block, "dp", bit))]
                for mask, block, bit in zip(masks, blocks, bits)
            ]
        else:
            rest = [pieces[1:] if self.early else pieces for pieces in held]
            arrays = iter(order(*[array for pieces in rest for _, array in pieces]))
            self.result = []
            for n, pieces in enumerate(rest):
                kept = [(masks, next(arrays)) for masks, _ in pieces]
                ours = held[n][:1] + kept if self.early else kept
                theirs = [([m ^ 1 for m in masks], swap(array, "dp", 1)) for masks, array in kept]
                self.result.append(ours + self.early[n : n + 1] + theirs)
        self.step += 1

    def send_early(self, order):
        arrays = order(*[pieces[0][1] for pieces in self.result])
        self.early = [
            ([m ^ 1 for m in pieces[0][0]], swap(array, "dp", 1))
            for pieces, array in zip(self.result, arrays)
        ]


def canonical_row(me, rank, block, mask, rank_mask, stride, offset):
    if mask is None:
        return offset
    row = (me ^ mask) * block + offset
    if stride:
        if rank_mask >= 2:
            rank_mask = rank_mask ^ ((rank + 1) // 2 % 2)
        row = row + (rank ^ rank_mask) * stride
    return pl.multiple_of(row, 16)


def place_kernel(plan, block, *refs):
    count = len(plan)
    ins = refs[:count]
    outs = refs[count:-1]
    sems = refs[-1]
    me = lax.axis_index("dp")
    rank = lax.axis_index("mp")
    copies = []
    for ref, moves in zip(ins, plan):
        for start, size, which, mask, column, _, offset in moves:
            row = canonical_row(me, rank, block, mask, 0, 0, offset)
            copy = pltpu.make_async_copy(
                ref.at[pl.ds(start, size), :],
                outs[which].at[pl.ds(row, size), pl.ds(column * D, D)],
                sems.at[len(copies)],
            )
            copy.start()
            copies.append(copy)
    for copy in copies:
        copy.wait()


def plan_of(gathered, layouts):
    arrays = []
    plan = []
    for pieces, layout in zip(gathered, layouts):
        rows = sum(size for _, size, *_ in layout)
        for masks, array in pieces:
            moves = []
            for j, mask in enumerate(masks):
                for start, size, which, rank_mask, stride, offset in layout:
                    moves.append((j * rows + start, size, which, mask, rank_mask, stride, offset))
            arrays.append(array)
            plan.append(moves)
    return arrays, plan


def place(arrays, plan, block, shapes):
    return pl.pallas_call(
        functools.partial(place_kernel, plan, block),
        out_shape=[jax.ShapeDtypeStruct(shape, low) for shape in shapes],
        in_specs=[pl.BlockSpec(memory_space=pl.ANY)] * len(arrays),
        out_specs=[pl.BlockSpec(memory_space=pltpu.VMEM)] * len(shapes),
        scratch_shapes=[pltpu.SemaphoreType.DMA((sum(len(moves) for moves in plan),))],
        compiler_params=pltpu.CompilerParams(vmem_limit_bytes=VMEM_LIMIT),
        cost_estimate=SMALL_COST,
        name="place",
    )(*arrays)


def store_split(value, keep, send, index):
    block = keep.shape[2]
    even = lax.axis_index("dp") % 2 == 0
    for outer in range(keep.shape[1]):
        first = value[2 * outer * block : (2 * outer + 1) * block]
        other = value[(2 * outer + 1) * block : (2 * outer + 2) * block]
        keep[index, outer] = jnp.where(even, first, other).astype(low)
        send[index, outer] = jnp.where(even, other, first).astype(low)


def middle_kernel(plan, block, total, *refs):
    limit_ref, vector_ref = refs[:2]
    token_hbm, mixed_hbm, log_hbm, cot_hbm, teach_hbm = refs[2:7]
    pieces = refs[7 : 7 + total]
    (
        out_hbm,
        middle_hbm,
        grad_hbm,
        down_keep,
        down_send,
        up_keep,
        up_send,
        delta_ref,
        log_ref,
        sum_ref,
    ) = refs[7 + total : 17 + total]
    (
        token,
        mixed,
        logs,
        cot,
        teach,
        up,
        down,
        proj,
        right,
        slope,
        second,
        middle,
        final,
        out,
        final_low,
        middle_low,
        grad,
        accum,
        turned,
        stage_keep,
        stage_send,
        in_sems,
        weight_sems,
        out_sems,
        keep_sems,
        send_sems,
    ) = refs[17 + total :]
    hidden = FF // D
    targets = (up, down, proj)
    rows = token.shape[0]
    me = lax.axis_index("dp")
    rank = lax.axis_index("mp")

    def fetch(ref, scratch, n):
        copy = pltpu.make_async_copy(ref, scratch, in_sems.at[n])
        copy.start()
        return copy

    def send(scratch, ref, n):
        copy = pltpu.make_async_copy(scratch, ref, out_sems.at[n])
        copy.start()
        return copy

    gets = [
        fetch(token_hbm, token, 0),
        fetch(mixed_hbm, mixed, 1),
        fetch(log_hbm, logs, 2),
        fetch(cot_hbm, cot, 3),
        fetch(teach_hbm, teach, 4),
    ]
    loads = {0: [], 1: [], 2: []}
    number = 0
    for want in (2, 0, 1):
        for ref, moves in zip(pieces, plan):
            for start, size, which, mask, rank_mask, stride, offset in moves:
                if which != want:
                    continue
                row = canonical_row(me, rank, block, mask, rank_mask, stride, offset)
                copy = pltpu.make_async_copy(
                    ref.at[pl.ds(start, size), :],
                    targets[which].at[pl.ds(row, size), :],
                    weight_sems.at[number],
                )
                copy.start()
                loads[which].append(copy)
                number += 1

    table_row = vector_ref[0:1, :]
    out_bias = vector_ref[1:2, :]
    gain = vector_ref[2:3, :]
    shift = vector_ref[3:4, :]
    down_bias = vector_ref[4:5, :]
    weight = vector_ref[5:6, :]
    gets[0].wait()
    gets[1].wait()
    right[2 * hidden] = mixed[...].astype(low)
    for copy in loads[2]:
        copy.wait()
    state = token[...].astype(full) + table_row + out_bias
    state = state + dot_of(right[2 * hidden], proj[...], 1, 1)
    middle[...] = state
    unit, _ = norm_stats(state)
    second[...] = (unit * gain + shift).astype(low)
    accum[...] = jnp.zeros((rows, D), full)
    for copy in loads[0]:
        copy.wait()
    for copy in loads[1]:
        copy.wait()

    def forward(m, _):
        place = pl.ds(pl.multiple_of(m * D, D), D)
        half = rows // 2
        spans = [pl.ds(part * half, half) for part in range(2)]
        values = [
            dot_of(second[span, :], up[place, :], 1, 0) + vector_ref[pl.ds(8 + m, 1), :]
            for span in spans
        ]
        for span, value in zip(spans, values):
            cumulative = 0.5 + 0.5 * lax.erf(value * (0.5**0.5))
            active = (value * cumulative).astype(low)
            right[m, span, :] = active
            slope[m, span, :] = (
                cumulative + value * jnp.exp(-0.5 * value * value) * 0.3989422804014327
            )
            accum[span, :] += dot_of(active, down[place, :], 1, 1)
        return 0

    lax.fori_loop(0, FF // D, forward, 0)
    final_state = middle[...] + accum[...] + down_bias
    out[...] = final_state.astype(low)
    puts = [send(out, out_hbm, 0)]
    gets[3].wait()
    gets[4].wait()
    place = lax.broadcasted_iota(jnp.int32, (rows, 1), 0)
    grads = cot[...].astype(full) + weight * (final_state - teach[...].astype(full))
    grads = jnp.where(place < limit_ref[5], grads, 0.0)
    final[...] = grads
    final_low[...] = grads.astype(low)
    sum_ref[3:4, :] = jnp.sum(grads, axis=0, keepdims=True)
    accum[...] = jnp.zeros((rows, D), full)

    def backward(m, _):
        place = pl.ds(pl.multiple_of(m * D, D), D)
        value = slope[m] * dot_of(final_low[...], down[place, :], 1, 0)
        value = value.astype(low)
        right[hidden + m] = value
        sum_ref[pl.ds(8 + m, 1), :] = jnp.sum(value.astype(full), axis=0, keepdims=True)
        accum[...] += dot_of(value, up[place, :], 1, 1)
        return 0

    lax.fori_loop(0, FF // D, backward, 0)
    unit, inverse = norm_stats(middle[...])
    second_grad = accum[...]
    sum_ref[0:1, :] = jnp.sum(second_grad * unit, axis=0, keepdims=True)
    sum_ref[1:2, :] = jnp.sum(second_grad, axis=0, keepdims=True)
    scaled = second_grad * gain
    mean_scaled = jnp.mean(scaled, axis=-1, keepdims=True)
    mean_unit = jnp.mean(scaled * unit, axis=-1, keepdims=True)
    total_grad = final[...] + inverse * (scaled - mean_scaled - unit * mean_unit)
    middle[...] = total_grad
    puts.append(send(middle, middle_hbm, 1))
    middle_low[...] = total_grad.astype(low)
    sum_ref[2:3, :] = jnp.sum(total_grad, axis=0, keepdims=True)
    attended_grad = dot_of(middle_low[...], proj[...], 1, 0).astype(low)
    grad[...] = attended_grad
    puts.append(send(grad, grad_hbm, 2))
    gets[2].wait()
    head = lax.broadcasted_iota(jnp.int32, (16, D), 0)
    lane = lax.broadcasted_iota(jnp.int32, (16, D), 1)
    member = jnp.where(lane // HEAD_DIM == head, 1.0, 0.0)
    leader = jnp.where(lane == head * HEAD_DIM, 1.0, 0.0)
    exact = functools.partial(
        lax.dot_general,
        dimension_numbers=(((1,), (1,)), ((), ())),
        precision=lax.Precision.HIGHEST,
        preferred_element_type=full,
    )
    deltas = exact(member, attended_grad.astype(full) * mixed[...])
    tops = exact(leader, logs[...])
    for pair in range(PAIRS):
        delta_ref[pair] = deltas[2 * pair : 2 * pair + 2]
        log_ref[pair] = tops[2 * pair : 2 * pair + 2]
    turned[0] = final_low[...].T
    turned[1] = second[...].T
    turned[2] = middle_low[...].T

    def weights(i, _):
        store_split(dot_of(turned[i // hidden], right[i], 1, 0), stage_keep, stage_send, i)

        @pl.when(i < hidden)
        def _():
            pltpu.make_async_copy(stage_keep.at[i], down_keep.at[i], keep_sems.at[i]).start()
            pltpu.make_async_copy(stage_send.at[i], down_send.at[i], send_sems.at[i]).start()

        @pl.when(i >= hidden)
        def _():
            row = i - hidden
            pltpu.make_async_copy(stage_keep.at[i], up_keep.at[row], keep_sems.at[i]).start()
            pltpu.make_async_copy(stage_send.at[i], up_send.at[row], send_sems.at[i]).start()

        return 0

    lax.fori_loop(0, 2 * hidden + 1, weights, 0)
    for copy in puts:
        copy.wait()
    for i in range(2 * hidden + 1):
        if i < hidden:
            keep, gone, row = down_keep, down_send, i
        else:
            keep, gone, row = up_keep, up_send, i - hidden
        pltpu.make_async_copy(stage_keep.at[i], keep.at[row], keep_sems.at[i]).wait()
        pltpu.make_async_copy(stage_send.at[i], gone.at[row], send_sems.at[i]).wait()


def middle_call(limit, vectors, tokens, mixed, logs, cot, teach, arrays, plan, block, dp):
    rows = tokens.shape[0]
    hidden = FF // D
    narrow = jax.ShapeDtypeStruct((rows, D), low)
    wide = jax.ShapeDtypeStruct((rows, D), full)
    shape = (dp // 2, D // dp, D)
    parts = [jax.ShapeDtypeStruct((count,) + shape, low) for count in (hidden, hidden + 1)]
    stats = jax.ShapeDtypeStruct((PAIRS, 2, rows), full)
    anywhere = pl.BlockSpec(memory_space=pl.ANY)
    inside = pl.BlockSpec(memory_space=pltpu.VMEM)
    moves = sum(len(part) for part in plan)
    return pl.pallas_call(
        functools.partial(middle_kernel, plan, block, len(arrays)),
        out_shape=(
            narrow,
            wide,
            narrow,
            parts[0],
            parts[0],
            parts[1],
            parts[1],
            stats,
            stats,
            jax.ShapeDtypeStruct((8 + 8, D), full),
        ),
        in_specs=[pl.BlockSpec(memory_space=pltpu.SMEM), inside]
        + [anywhere] * (5 + len(arrays)),
        out_specs=[anywhere] * 7 + [inside] * 3,
        scratch_shapes=[
            pltpu.VMEM((rows, D), low),
            pltpu.VMEM((rows, D), full),
            pltpu.VMEM((rows, D), full),
            pltpu.VMEM((rows, D), low),
            pltpu.VMEM((rows, D), low),
            pltpu.VMEM((FF, D), low),
            pltpu.VMEM((FF, D), low),
            pltpu.VMEM((D, D), low),
            pltpu.VMEM((2 * hidden + 1, rows, D), low),
            pltpu.VMEM((hidden, rows, D), full),
            pltpu.VMEM((rows, D), low),
            pltpu.VMEM((rows, D), full),
            pltpu.VMEM((rows, D), full),
            pltpu.VMEM((rows, D), low),
            pltpu.VMEM((rows, D), low),
            pltpu.VMEM((rows, D), low),
            pltpu.VMEM((rows, D), low),
            pltpu.VMEM((rows, D), full),
            pltpu.VMEM((3, D, rows), low),
            pltpu.VMEM((2 * hidden + 1,) + shape, low),
            pltpu.VMEM((2 * hidden + 1,) + shape, low),
            pltpu.SemaphoreType.DMA((5,)),
            pltpu.SemaphoreType.DMA((moves,)),
            pltpu.SemaphoreType.DMA((3,)),
            pltpu.SemaphoreType.DMA((2 * hidden + 1,)),
            pltpu.SemaphoreType.DMA((2 * hidden + 1,)),
        ],
        compiler_params=pltpu.CompilerParams(vmem_limit_bytes=VMEM_LIMIT),
        cost_estimate=SMALL_COST,
        name="middle",
    )(limit, vectors, tokens, mixed, logs, cot, teach, *arrays)


def fold_block(keep, got, out_keep, out_send, bit, place):
    step = 1 << place
    mine = (lax.axis_index("dp") // bit) % 2 * step
    for j in range(keep.shape[1] // 2):
        base = (j // step) * 2 * step + j % step
        for out, shift in ((out_keep, mine), (out_send, step - mine)):
            value = keep[0, base + shift].astype(full) + got[0, base + shift].astype(full)
            out[0, j] = value.astype(low)


def fold_kernel(bits, places, *refs):
    count = len(bits)
    for n in range(count):
        fold_block(
            *refs[2 * n : 2 * n + 2],
            *refs[2 * count + 2 * n : 2 * count + 2 * n + 2],
            bits[n],
            places[n],
        )


def fold(pairs, bits, places):
    lead = pairs[0][0].shape[0]
    block = lambda shape: pl.BlockSpec((1,) + shape[1:], lambda i: (i, 0, 0, 0))
    halves = [
        (keep.shape[0], keep.shape[1] // 2) + keep.shape[2:] for keep, _ in pairs for _ in range(2)
    ]
    outs = pl.pallas_call(
        functools.partial(fold_kernel, bits, places),
        out_shape=[jax.ShapeDtypeStruct(shape, low) for shape in halves],
        grid=(lead,),
        in_specs=[block(value.shape) for pair in pairs for value in pair],
        out_specs=[block(shape) for shape in halves],
        compiler_params=pltpu.CompilerParams(vmem_limit_bytes=VMEM_LIMIT),
        cost_estimate=pl.CostEstimate(flops=0, bytes_accessed=16 << 20, transcendentals=0),
        name="fold",
    )(*[value for pair in pairs for value in pair])
    return [(outs[2 * n], outs[2 * n + 1]) for n in range(len(pairs))]


def qkv_grad_kernel(count, *refs):
    sources = refs[: 3 * count + 1]
    outs = refs[3 * count + 1 : 3 * count + 5]
    sum_ref, held, *turned, totals, stage, in_sems, out_sems = refs[3 * count + 5 :]
    first_use = [0, count, count + 1, 2 * count + 1]
    for n in range(1, count):
        first_use += [n, count + 1 + n, 2 * count + 1 + n]
    copies = {}
    for n in first_use:
        copies[n] = pltpu.make_async_copy(sources[n], held.at[n], in_sems.at[n])
        copies[n].start()

    def column_sum(n):
        return jnp.sum(held[n].astype(full), axis=0, keepdims=True)

    puts = []

    def store(value, c):
        for part in range(2):
            store_split(
                value[:, part * D // 2 : (part + 1) * D // 2],
                stage.at[part],
                stage.at[2 + part],
                c,
            )
        for k in range(4):
            put = pltpu.make_async_copy(stage.at[k, c], outs[k].at[c], out_sems.at[k * 3 + c])
            put.start()
            puts.append(put)

    sum_ref[...] = jnp.zeros_like(sum_ref)
    copies[0].wait()
    turned[0][...] = held[0].T
    copies[count].wait()
    store(dot_of(turned[0][...], held[count], 1, 0), 0)
    sum_ref[0:1, :] = column_sum(count)
    value_sum = jnp.zeros((1, D), full)
    for n in range(count):
        if n + 1 < count:
            copies[n + 1].wait()
        copies[count + 1 + n].wait()
        copies[2 * count + 1 + n].wait()
        left = turned[n % 2][...]
        if n + 1 < count:
            turned[(n + 1) % 2][...] = held[n + 1].T
        for c in (1, 2):
            value = dot_of(left, held[c * count + 1 + n], 1, 0)
            if n > 0:
                value = value + totals[c - 1]
            if n + 1 < count:
                totals[c - 1] = value
            else:
                store(value, c)
        value_sum = value_sum + column_sum(2 * count + 1 + n)
    sum_ref[8:9, :] = value_sum
    for put in puts:
        put.wait()


def qkv_grads(chunks, query_grad, key_grads, value_grads, dp):
    rows = query_grad.shape[0]
    count = len(chunks)
    shape = (3, dp // 2, D // dp, D // 2)
    anywhere = pl.BlockSpec(memory_space=pl.ANY)
    return pl.pallas_call(
        functools.partial(qkv_grad_kernel, count),
        out_shape=[jax.ShapeDtypeStruct(shape, low)] * 4
        + [jax.ShapeDtypeStruct((16, D), full)],
        in_specs=[anywhere] * (3 * count + 1),
        out_specs=[anywhere] * 4 + [pl.BlockSpec(memory_space=pltpu.VMEM)],
        scratch_shapes=[
            pltpu.VMEM((3 * count + 1, rows, D), low),
            pltpu.VMEM((D, rows), low),
            pltpu.VMEM((D, rows), low),
            pltpu.VMEM((2, D, D), full),
            pltpu.VMEM((4,) + shape, low),
            pltpu.SemaphoreType.DMA((3 * count + 1,)),
            pltpu.SemaphoreType.DMA((12,)),
        ],
        compiler_params=pltpu.CompilerParams(vmem_limit_bytes=VMEM_LIMIT),
        cost_estimate=SMALL_COST,
        name="qkv_grads",
    )(*chunks, query_grad, *key_grads, *value_grads)


def last_kernel(
    token_ref,
    first_ref,
    right_ref,
    left_ref,
    middle_ref,
    vector_ref,
    gain_ref,
    bias_ref,
    sum_ref,
    out_ref,
    pack_ref,
):
    @pl.when(pl.program_id(0) == 0)
    def _():
        pack_ref[...] = jnp.zeros_like(pack_ref)
        pack_ref[1:2, :] = sum_ref[0:1, :]
        pack_ref[3:4, :] = sum_ref[1:2, :]
        pack_ref[4:5, :] = bias_ref[0:1, :]
        pack_ref[5:6, :] = bias_ref[8:9, :]
        pack_ref[6:8, :] = sum_ref[2:4, :]
        pack_ref[8 : 8 + FF // D, :] = sum_ref[8 : 8 + FF // D, :]

    unit, inverse = norm_stats(token_ref[...].astype(full) + vector_ref[0:1, :])
    grad = first_ref[...] + right_ref[...].astype(full) + left_ref[...].astype(full)
    scaled = grad * gain_ref[0:1, :]
    mean_scaled = jnp.mean(scaled, axis=-1, keepdims=True)
    mean_unit = jnp.mean(scaled * unit, axis=-1, keepdims=True)
    result = middle_ref[...] + inverse * (scaled - mean_scaled - unit * mean_unit)
    out_ref[...] = result
    pack_ref[0:1, :] += jnp.sum(grad * unit, axis=0, keepdims=True)
    pack_ref[2:3, :] += jnp.sum(grad, axis=0, keepdims=True)
    pack_ref[pl.ds(16 + lax.axis_index("dp"), 1), :] += jnp.sum(result, axis=0, keepdims=True)


def last_norm(tokens, first, right, left, middle_grad, vectors, gains, bias_sums, sums, dp):
    rows = tokens.shape[0]
    part = pl.BlockSpec((rows // 4, D), lambda i: (i, 0))
    whole = lambda value: pl.BlockSpec(value.shape, lambda i: (0, 0))
    small = (vectors, gains, bias_sums, sums)
    return pl.pallas_call(
        last_kernel,
        out_shape=(
            jax.ShapeDtypeStruct((rows, D), full),
            jax.ShapeDtypeStruct((16 + dp, D), full),
        ),
        grid=(4,),
        in_specs=[part] * 5 + [whole(value) for value in small],
        out_specs=[part, pl.BlockSpec((16 + dp, D), lambda i: (0, 0))],
        compiler_params=pltpu.CompilerParams(vmem_limit_bytes=VMEM_LIMIT),
        cost_estimate=SMALL_COST,
        name="last_norm",
    )(tokens, first, right, left, middle_grad, *small)


def two_parts(value, axis, mine):
    keep = lax.dynamic_index_in_dim(value, mine, axis, keepdims=False)
    send = lax.dynamic_index_in_dim(value, 1 - mine, axis, keepdims=False)
    return keep, send.astype(low)


class Scatter:
    def __init__(self, parts, turns):
        self.bits = outer_bits()
        half = len(self.bits) // 2
        self.orders = [
            [1] + self.bits[half * (turn % 2) :] + self.bits[: half * (turn % 2)] for turn in turns
        ]
        self.left = [list(self.bits) for _ in turns]
        self.step = 0
        self.parts = parts

    def sends(self):
        return [send for _, send in self.parts]

    def exchange(self, sends):
        self.pairs = [
            (keep, swap(send, "dp", turn[self.step]))
            for (keep, _), send, turn in zip(self.parts, sends, self.orders)
        ]
        self.step += 1

    def folds(self):
        if self.step > len(self.bits):
            return [], [], []
        bits = [turn[self.step] for turn in self.orders]
        places = []
        for left, bit in zip(self.left, bits):
            places.append(left.index(bit))
            left.remove(bit)
        return self.pairs, bits, places

    def give(self, outs):
        self.parts = [(outs[n], outs[n + 1]) for n in range(0, len(outs), 2)]

    def fold(self):
        outs = []
        for pair, bit, at in zip(*self.folds()):
            outs += fold([pair], [bit], [at])[0]
        self.give(outs)

    def advance(self, order):
        sends = order(*self.sends())
        self.exchange(list(sends) if len(self.parts) > 1 else [sends])

    def finish(self, order):
        while self.step <= len(self.bits):
            self.fold()
            self.advance(order)
        got = order(*[other for _, other in self.pairs])
        return [
            (keep.astype(full) + other.astype(full))[:, 0]
            for (keep, _), other in zip(self.pairs, got)
        ]


def scatter_dp(parts, turns):
    scatter = Scatter(parts, turns)
    while True:
        sends = yield scatter.sends()
        scatter.exchange(sends)
        if scatter.step > len(scatter.bits):
            break
        scatter.parts = fold(*scatter.folds())
    got = yield [other for _, other in scatter.pairs]
    return [
        (keep.astype(full) + other.astype(full))[:, 0]
        for (keep, _), other in zip(scatter.pairs, got)
    ]


def scatter_mp(value):
    rank = lax.axis_index("mp")
    part = lambda index: lax.dynamic_index_in_dim(value, index, keepdims=False)
    sends = yield [part(rank ^ bit).astype(low) for bit in (1, 2, 3)]
    got = yield [swap(send, "mp", bit) for bit, send in zip((1, 2, 3), sends)]
    got = [other.astype(full) for other in got]
    return (part(rank) + got[0]) + (got[1] + got[2])


def halve_mp(value):
    rank = lax.axis_index("mp")
    pairs = value.reshape((2, 2) + value.shape[1:])
    keep, send = two_parts(pairs, 1, rank % 2)
    (send,) = yield [send]
    (got,) = yield [swap(send, "mp", 1)]
    keep, send = two_parts(keep.astype(full) + got.astype(full), 0, rank // 2)
    (send,) = yield [send]
    (got,) = yield [swap(send, "mp", 2)]
    return keep + got.astype(full)


def scatter_feed(up_own, down_own):
    mp = lax.axis_size("mp")
    block = down_own.shape[1]
    out_own = up_own[mp].reshape(block, mp, -1).transpose(1, 0, 2)
    own = yield from halve_mp(
        jnp.concatenate([up_own[:mp], down_own, out_own.reshape(mp, -1, D)], axis=1)
    )
    return own[:block], own[block : 2 * block].T, own[2 * block :].reshape(block, -1).T


def scatter_qkv(keep_left, keep_right, send_left, send_right):
    left_part, right_part = yield from scatter_dp(
        [(keep_left, send_left), (keep_right, send_right)], (0, 1)
    )
    width = D // lax.axis_size("mp")
    parts = [part[..., at : at + width] for part in (left_part, right_part) for at in (0, width)]
    return (yield from scatter_mp(jnp.stack(parts)))


def sum_small(value):
    (value,) = yield [value]
    value = value + swap(value, "dp", 1)
    bits = outer_bits()
    groups = [("dp", bits[n : n + 2]) for n in range(0, len(bits), 2)] + [("mp", [1, 2])]
    for axis, pair in groups:
        (value,) = yield [value]
        if len(pair) == 1:
            value = value + swap(value, axis, pair[0])
        else:
            one, two = pair
            got = [swap(value, axis, mask) for mask in (one, two, one + two)]
            if axis == "mp":
                got = yield got
            value = (value + got[0]) + (got[1] + got[2])
    return value


class Steps:
    def __init__(self, steps):
        self.steps = steps
        self.pending = next(steps)
        self.result = None

    def advance(self, order):
        if self.pending is None:
            return
        sends = order(*self.pending)
        sends = [sends] if len(self.pending) == 1 else list(sends)
        try:
            self.pending = self.steps.send(sends)
        except StopIteration as stop:
            self.pending = None
            self.result = stop.value

    def finish(self, order):
        while self.pending is not None:
            self.advance(order)
        return self.result


def shards(
    tokens_in,
    timesteps,
    lengths,
    time_table,
    norm_gains,
    norm_biases,
    w_qkv,
    qv_bias,
    w_out,
    out_bias,
    w_up,
    up_bias,
    w_down,
    down_bias,
    cotangent,
    teacher,
):
    rank = lax.axis_index("mp")
    data_rank = lax.axis_index("dp")
    mp = lax.axis_size("mp")
    dp = lax.axis_size("dp")
    own_rows = tokens_in.shape[0]
    length = lax.dynamic_index_in_dim(lengths, data_rank, keepdims=False)
    own_time = lax.dynamic_index_in_dim(timesteps, data_rank, keepdims=False)
    odd = rank % 2 == 1
    upper = rank >= 2
    middle = jnp.logical_or(rank == 1, rank == 2)
    order = Order()
    along = lambda value, pairs: lax.ppermute(value, "mp", pairs)

    block = w_qkv.shape[1]
    aligned = block % 32 == 0
    narrow = order(jnp.concatenate([w_qkv.reshape(3 * block, -1), w_out.T]))
    first_swap = swap(narrow, "mp", 1)
    tall = order(jnp.concatenate([w_up, w_down.T]))
    tall_swap = swap(tall, "mp", 1)
    pair = order(
        jnp.concatenate(
            [jnp.where(odd, first_swap, narrow), jnp.where(odd, narrow, first_swap)], axis=1
        )
    )
    second_swap = swap(pair, "mp", 2)
    tokens, lengths, own_time, norm_gains, norm_biases, out_bias, down_bias, up_bias, length = order(
        tokens_in, lengths, own_time, norm_gains, norm_biases, out_bias, down_bias, up_bias, length
    )
    table_row = lax.dynamic_slice_in_dim(time_table, own_time, 1).astype(full)
    unit_one, _ = norm_stats(tokens.astype(full) + table_row)
    first_norm = (unit_one * norm_gains[0] + norm_biases[0]).astype(low)
    loss_weight = lengths.shape[0] * MAXLEN / jnp.sum(lengths).astype(full)
    vectors = jnp.concatenate(
        [
            table_row,
            out_bias[None],
            norm_gains[1:2],
            norm_biases[1:2],
            down_bias[None],
            jnp.full((3, D), loss_weight),
            up_bias.reshape(-1, D),
            jnp.zeros((4, D), full),
        ]
    )
    scalars = jnp.stack(
        [
            rank,
            jnp.where(rank == 0, 1, rank - 1),
            jnp.where(upper, rank - 2, rank + 2),
            jnp.where(middle, rank + 1, 3 - rank),
            length,
            length - rank * own_rows,
        ]
    ).astype(jnp.int32)
    first_norm, vectors, scalars = order(first_norm, vectors, scalars)
    wide = jnp.concatenate(
        [jnp.where(upper, second_swap, pair), jnp.where(upper, pair, second_swap)], axis=1
    )
    qkv_rows, out_rows = wide[: 3 * block], wide[3 * block :]
    if aligned:
        split = 3 * block // 2
        qkv_gather = Gather([qkv_rows[:split], qkv_rows[split:]])
        qkv_gather.advance(order)
    tall = order(jnp.concatenate([tall, tall_swap]))
    tall_across = along(tall, [(1, 2), (2, 1)])

    sent = order(first_norm)
    from_left = along(sent, [(0, 1), (1, 2), (2, 3)])
    from_right = along(sent, [(1, 0), (2, 1), (3, 2)])
    tall_across = order(tall_across)
    tall_far = along(tall_across, [(1, 0), (2, 3)])
    if aligned:
        while qkv_gather.step < len(qkv_gather.bits):
            qkv_gather.advance(order)
        qkv_gather.advance(order)
    hop_right, hop_left = order(from_left, from_right)
    second_right = along(hop_right, [(1, 2), (2, 3)])
    second_left = along(hop_left, [(1, 0), (2, 1)])
    if aligned:
        arrays, plan = plan_of(
            qkv_gather.result,
            [
                [(0, block, 0, 0, 0, 0), (block, split - block, 1, 0, 0, 0)],
                [
                    (0, 2 * block - split, 1, 0, 0, split - block),
                    (2 * block - split, block, 1, 1, 0, 0),
                ],
            ],
        )
        query_weight, pair_weight = order(*place(arrays, plan, block, [(D, D), (D, 2 * D)]))
        tall_other = jnp.where(middle, tall_across, order(tall_far))
        feed_gather = Gather(
            [
                jnp.concatenate([tall, out_rows[: block // 2]]),
                jnp.concatenate([tall_other, out_rows[block // 2 :]]),
            ]
        )
        feed_gather.advance(order)
    else:
        weights = lax.all_gather(qkv_rows.reshape(3, block, D), "dp", axis=1, tiled=True)
        query_weight = weights[0]
        pair_weight = jnp.concatenate([weights[1], weights[2]], axis=1)
    near = jnp.where(rank == 0, hop_left, hop_right)
    attend = lambda parts, numbers, carried: order(
        *attend_forward(
            parts,
            numbers,
            scalars,
            query_weight,
            pair_weight,
            qv_bias[0:1],
            qv_bias[1:2],
            carried,
        )
    )
    key_own, value_own, queries, *state = attend([order(first_norm)], (0,), None)
    second_right, second_left = order(second_right, second_left)
    second = order(jnp.where(upper, second_right, second_left))
    third = along(second, [(1, 0), (2, 3)])
    if aligned:
        while feed_gather.step < len(feed_gather.bits):
            feed_gather.advance(order)
        feed_gather.send_early(order)
    near, second = order(near, second)
    key_near, key_second, value_near, value_second, *state = attend(
        [near, second], (1, 2), (queries, *state)
    )
    last = order(jnp.where(middle, hop_left, order(third)))
    key_last, value_last, mixed, logs = attend([order(last)], (3,), (queries, *state))
    if aligned:
        feed_gather.advance(order)
        layout = lambda masks, shift: [
            (0, block, 0, masks[0], D, 0),
            (block, block, 1, masks[0], D, 0),
            (2 * block, block, 0, masks[1], D, 0),
            (3 * block, block, 1, masks[1], D, 0),
            (4 * block, block // 2, 2, 0, 0, shift),
        ]
        arrays, plan = plan_of(
            feed_gather.result, [layout((0, 1), 0), layout((2, 3), block // 2)]
        )
    else:
        arrays = [
            lax.all_gather(w_up, ("mp", "dp"), axis=0, tiled=True),
            lax.all_gather(w_down.T, ("mp", "dp"), axis=0, tiled=True),
            lax.all_gather(out_rows, "dp", axis=0, tiled=True),
        ]
        plan = [[(0, array.shape[0], n, None, 0, 0, 0)] for n, array in enumerate(arrays)]
    chunks = [first_norm, near, second, last]
    keys = [key_own, key_near, key_second, key_last]
    values = [value_own, value_near, value_second, value_last]

    output, middle_grad, attended_grad, *parts, deltas, log_rows, sums = middle_call(
        scalars, vectors, tokens, mixed, logs, cotangent, teacher, arrays, plan, block, dp
    )
    scatter = Scatter([(parts[0], parts[1]), (parts[2], parts[3])], (1, 0))
    scatter.advance(order)

    key_grads = [None] * 4
    value_grads = [None] * 4
    firsts = [None] * 4
    query_grad = None
    for n in (3, 2, 1, 0):
        pairs, bits, places = scatter.folds() if n % 2 == 0 else ([], [], [])
        query_grad, key_grads[n], value_grads[n], firsts[n], *folded = attend_backward(
            n,
            queries,
            keys[n],
            values[n],
            order(attended_grad),
            log_rows,
            deltas,
            query_weight,
            pair_weight,
            scalars,
            query_grad,
            n == 0,
            pairs,
            bits,
            places,
        )
        firsts[n] = order(firsts[n])
        if folded:
            scatter.give(folded)
        if n == 3:
            back_last = along(firsts[3], [(0, 1), (3, 2)]).astype(full)
        elif n == 2:
            scatter.advance(order)
            payload = order((firsts[2] + back_last).astype(low))
            back_right = along(payload, [(0, 1), (1, 2)]).astype(full)
            back_left = along(payload, [(3, 2), (2, 1)]).astype(full)
        elif n == 1:
            to_right = jnp.where(
                rank == 0, firsts[1], firsts[3].astype(full) + back_right
            ).astype(low)
            to_left = (firsts[1] + back_left).astype(low)
            to_right, to_left = order(to_right, to_left)
            final_right = along(to_right, [(0, 1), (1, 2), (2, 3)])
            final_left = along(to_left, [(3, 2), (2, 1), (1, 0)])
    scatter.advance(order)
    query_grad, final_right, final_left = order(query_grad, final_right, final_left)
    *halves, bias_sums = qkv_grads(chunks, query_grad, key_grads, value_grads, dp)
    qkv = Steps(scatter_qkv(*halves))
    qkv.advance(order)
    down_own, up_own = scatter.finish(order)
    feed = Steps(scatter_feed(up_own, down_own))
    feed.advance(order)
    qkv.advance(order)
    tokens, first_own = order(tokens, firsts[0])
    input_grad, packed = last_norm(
        tokens,
        first_own,
        final_right,
        final_left,
        middle_grad,
        vectors,
        norm_gains,
        bias_sums,
        sums,
        dp,
    )
    packed, input_grad = order(packed, input_grad)
    small = Steps(sum_small(packed))
    feed.advance(order)
    feed.advance(order)
    small.advance(order)
    qkv.advance(order)
    feed.advance(order)
    qkv.advance(order)
    small.advance(order)
    qkv.advance(order)
    small.advance(order)
    total = small.finish(order)
    up_grad, down_grad, out_grad = feed.finish(order)
    qkv_grad = qkv.finish(order)
    fixed = 16
    chosen = (timesteps[None, :] == jnp.arange(time_table.shape[0])[:, None]).astype(full)
    table_grad = lax.dot_general(
        chosen,
        total[fixed:],
        (((1,), (0,)), ((), ())),
        precision=lax.Precision.HIGHEST,
        preferred_element_type=full,
    )
    return (
        output,
        input_grad,
        table_grad,
        total[0:2],
        total[2:4],
        qkv_grad,
        total[4:6],
        out_grad,
        total[6],
        up_grad,
        total[8 : 8 + FF // D].reshape(FF),
        down_grad,
        total[7],
    )


def solution(mesh):
    rows = P(both, None)
    placed = (
        rows,
        P(),
        P(),
        P(),
        P(),
        P(),
        P(None, "dp", "mp"),
        P(),
        P("mp", "dp"),
        P(),
        P("dp", "mp"),
        P(),
        P("mp", "dp"),
        P(),
        rows,
        rows,
    )
    return jax.shard_map(
        shards,
        mesh=mesh,
        in_specs=placed,
        out_specs=(
            rows,
            rows,
            P(),
            P(),
            P(),
            P(None, "dp", "mp"),
            P(),
            P("mp", "dp"),
            P(),
            P("dp", "mp"),
            P(),
            P("mp", "dp"),
            P(),
        ),
        check_vma=False,
    )
```

```python
import functools

import jax
import jax.numpy as jnp
from jax import lax
from jax.experimental import pallas as pl
from jax.experimental.pallas import tpu as pltpu
from jax.sharding import PartitionSpec as P

D = 768
HEADS = 12
HEAD_DIM = 64
FF = 3072
MAXLEN = 2048
PAIR = 2 * HEAD_DIM
PAIRS = HEADS // 2
VMEM_LIMIT = 58 << 20
SMALL_COST = pl.CostEstimate(flops=1 << 20, bytes_accessed=1 << 16, transcendentals=0)

far_below = -1e30
epsilon = 1e-05
score_scale = HEAD_DIM ** (-0.5)
low = jnp.bfloat16
full = jnp.float32
both = ("dp", "mp")


def norm_stats(values):
    center = values - jnp.mean(values, axis=-1, keepdims=True)
    spread = jnp.mean(center * center, axis=-1, keepdims=True)
    inverse = lax.rsqrt(spread + epsilon)
    return center * inverse, inverse


def dot_of(left_side, right_side, left_dim, right_dim):
    return lax.dot_general(
        left_side,
        right_side,
        (((left_dim,), (right_dim,)), ((), ())),
        preferred_element_type=full,
    )


def first_half(shape):
    return lax.broadcasted_iota(jnp.int32, shape, len(shape) - 1) < HEAD_DIM


def forward_kernel(numbers, first, final, scalars, *refs):
    count = len(numbers)
    chunk_refs = refs[:count]
    wk_ref, wv_ref, value_bias_ref = refs[count : count + 3]
    refs = refs[count + 3 :]
    if first:
        wq_ref, query_bias_ref = refs[:2]
        key_outs, value_outs = refs[2 : 2 + count], refs[2 + count : 2 + 2 * count]
        query_out, top_ref, sum_ref, acc_ref = refs[2 + 2 * count :]
        q_pair = (dot_of(chunk_refs[0][...], wq_ref[...], 1, 0) + query_bias_ref[...]).astype(low)
        q_pair = q_pair * jnp.asarray(score_scale, low)
        query_out[...] = q_pair
    else:
        q_ref, top_in, sum_in, acc_in = refs[:4]
        key_outs, value_outs = refs[4 : 4 + count], refs[4 + count : 4 + 2 * count]
        results = refs[4 + 2 * count :]
        q_pair = q_ref[...]
    weight = jnp.concatenate([wk_ref[...], wv_ref[...]], axis=1)
    keys = []
    values = []
    for n in range(count):
        both_parts = dot_of(chunk_refs[n][...], weight, 1, 0)
        keys.append(both_parts[:, :PAIR].astype(low))
        values.append((both_parts[:, PAIR:] + value_bias_ref[...]).astype(low))
        key_outs[n][...] = keys[n]
        value_outs[n][...] = values[n]
    rows = q_pair.shape[0]
    size = keys[0].shape[0]
    values = [jnp.concatenate([value, jnp.ones((size, PAIR), low)], axis=1) for value in values]
    place = lax.broadcasted_iota(jnp.int32, (1, size), 1)
    lower = first_half((rows, PAIR))
    parts = []
    for half in range(2):
        kept = lower if half == 0 else jnp.logical_not(lower)
        q_half = jnp.where(kept, q_pair, jnp.zeros_like(q_pair))
        scores = []
        for n in range(count):
            bias = jnp.where(place + scalars[numbers[n]] * size < scalars[4], 0.0, far_below)
            scores.append(dot_of(q_half, keys[n], 1, 1) + bias)
        highest = functools.reduce(
            jnp.maximum, [jnp.max(score, axis=-1, keepdims=True) for score in scores]
        )
        weighed = None
        for n in range(count):
            exp_scores = jnp.exp(scores[n] - highest).astype(low)
            part = dot_of(exp_scores, values[n], 1, 0)
            weighed = part if weighed is None else weighed + part
        parts.append((highest, weighed[:, PAIR:], weighed[:, :PAIR]))
    top = jnp.where(lower, parts[0][0], parts[1][0])
    total = jnp.where(lower, parts[0][1], parts[1][1])
    mixed = jnp.where(lower, parts[0][2], parts[1][2])
    if first:
        top_ref[...] = top
        sum_ref[...] = total
        acc_ref[...] = mixed
    else:
        highest = jnp.maximum(top, top_in[...])
        here = jnp.exp(top - highest)
        before = jnp.exp(top_in[...] - highest)
        total = total * here + sum_in[...] * before
        mixed = mixed * here + acc_in[...] * before
        if final:
            results[0][...] = mixed / total
            results[1][...] = highest + jnp.log(total)
        else:
            results[0][...] = highest
            results[1][...] = total
            results[2][...] = mixed


def attend_forward(chunks, numbers, scalars, query_weight, pair_weight, query_bias, value_bias, carried):
    rows = chunks[0].shape[0]
    count = len(chunks)
    first = carried is None
    final = 3 in numbers
    column = lambda height, c: pl.BlockSpec((height, PAIR), lambda i, n: (0, c * PAIRS + i))
    whole = pl.BlockSpec((rows, D), lambda i, n: (0, 0))
    wide = jax.ShapeDtypeStruct((rows, D), full)
    narrow = jax.ShapeDtypeStruct((rows, D), low)
    extra = (query_weight, query_bias) if first else carried
    results = (narrow,) * first + (wide,) * (2 if final else 3)
    return pl.pallas_call(
        functools.partial(forward_kernel, numbers, first, final),
        out_shape=(narrow,) * (2 * count) + results,
        grid_spec=pltpu.PrefetchScalarGridSpec(
            num_scalar_prefetch=1,
            grid=(PAIRS,),
            in_specs=[whole] * count
            + [column(D, 0), column(D, 1), column(1, 0)]
            + ([column(D, 0), column(1, 0)] if first else [column(rows, 0)] * 4),
            out_specs=[column(rows, 0)] * (2 * count + len(results)),
        ),
        compiler_params=pltpu.CompilerParams(vmem_limit_bytes=VMEM_LIMIT),
        cost_estimate=SMALL_COST,
        name="attend_forward",
    )(scalars, *chunks, pair_weight, pair_weight, value_bias, *extra)


def backward_kernel(
    number,
    first,
    last,
    folds,
    scalars,
    q_ref,
    k_ref,
    v_ref,
    g_ref,
    log_ref,
    delta_ref,
    wk_ref,
    wv_ref,
    *refs
):
    if last:
        wq_ref = refs[0]
        refs = refs[1:]
    if not first:
        dq_in = refs[0]
        refs = refs[1:]
    count = len(folds)
    fold_ins, refs = refs[: 2 * count], refs[2 * count :]
    dq_ref, dk_ref, dv_ref, back_ref = refs[:4]
    fold_outs, accum = refs[4:-1], refs[-1]
    step = pl.program_id(0)
    for n, (lead, bit, at) in enumerate(folds):

        @pl.when(step < lead)
        def _():
            fold_block(
                *fold_ins[2 * n : 2 * n + 2], *fold_outs[2 * n : 2 * n + 2], bit, at
            )

    rows = q_ref.shape[0]
    keys = k_ref.shape[0]
    limit = scalars[4] - scalars[number] * keys
    q_pair = q_ref[...]
    g_pair = g_ref[...]
    k_pair = k_ref[...]
    v_pair = v_ref[...]
    lower = first_half((rows, PAIR))
    nothing = jnp.zeros((rows, PAIR), low)
    two_halves = lambda pair: jnp.concatenate(
        [jnp.where(lower, pair, nothing), jnp.where(lower, nothing, pair)]
    )
    queries = two_halves(q_pair)
    grads_out = two_halves(g_pair)
    row_of = lambda ref: jnp.concatenate([ref[0, 0:1, :], ref[0, 1:2, :]], axis=1)
    place = lax.broadcasted_iota(jnp.int32, (keys, 1), 0)
    bias = jnp.where(place < limit, 0.0, far_below)
    scores = dot_of(k_pair, queries, 1, 1) + bias
    prob_grad = dot_of(v_pair, grads_out, 1, 1)
    probs = jnp.exp(scores - row_of(log_ref))
    score_grad = (probs * (prob_grad - row_of(delta_ref))).astype(low)
    dv_low = dot_of(probs.astype(low), grads_out, 1, 0).astype(low)
    dk_low = dot_of(score_grad, queries, 1, 0).astype(low)
    turned = dot_of(k_pair.T, score_grad, 1, 0)
    upper_rows = lax.broadcasted_iota(jnp.int32, (PAIR, rows), 0) < HEAD_DIM
    dk_ref[...] = dk_low
    dv_ref[...] = dv_low
    grads = [dk_low, dv_low]
    weights = [wk_ref[...], wv_ref[...]]
    dq_all = jnp.where(upper_rows, turned[:, :rows], turned[:, rows:]).T
    if not first:
        dq_all = dq_all + dq_in[...]
    back = dot_of(jnp.concatenate(grads, axis=1), jnp.concatenate(weights, axis=1), 1, 1)
    if last:
        dq_low = (dq_all * score_scale).astype(low)
        dq_ref[...] = dq_low
        back = back + dot_of(dq_low, wq_ref[...], 1, 1)
    else:
        dq_ref[...] = dq_all

    @pl.when(step == 0)
    def _():
        accum[...] = back

    @pl.when(step > 0)
    def _():
        accum[...] += back

    @pl.when(step == PAIRS - 1)
    def _():
        back_ref[...] = accum[...].astype(back_ref.dtype)


def attend_backward(
    number,
    queries,
    keys,
    values,
    grads,
    logs,
    deltas,
    query_weight,
    pair_weight,
    scalars,
    carried,
    last,
    pairs,
    bits,
    places,
):
    rows, total = queries.shape[0], keys.shape[0]
    first = carried is None
    folds = [(keep.shape[0], bit, at) for (keep, _), bit, at in zip(pairs, bits, places)]
    halves = [
        (keep.shape[0], keep.shape[1] // 2) + keep.shape[2:] for keep, _ in pairs for _ in range(2)
    ]

    def by_lead(shape):
        end = shape[0] - 1
        return pl.BlockSpec((1,) + shape[1:], lambda i, n: (jnp.minimum(i, end), 0, 0, 0))

    column = lambda count, c: pl.BlockSpec((count, PAIR), lambda i, n: (0, c * PAIRS + i))
    stats = pl.BlockSpec((1, 2, rows), lambda i, n: (i, 0, 0))
    extra = (query_weight,) * last + (() if first else (carried,))
    extra_specs = [column(D, 0)] * last + ([] if first else [column(rows, 0)])
    return pl.pallas_call(
        functools.partial(backward_kernel, number, first, last, folds),
        out_shape=(
            jax.ShapeDtypeStruct((rows, D), low if last else full),
            jax.ShapeDtypeStruct((total, D), low),
            jax.ShapeDtypeStruct((total, D), low),
            jax.ShapeDtypeStruct((total, D), low if first else full),
            *[jax.ShapeDtypeStruct(shape, low) for shape in halves],
        ),
        grid_spec=pltpu.PrefetchScalarGridSpec(
            num_scalar_prefetch=1,
            grid=(PAIRS,),
            in_specs=[
                column(rows, 0),
                column(total, 0),
                column(total, 0),
                column(rows, 0),
                stats,
                stats,
                column(D, 0),
                column(D, 1),
            ]
            + extra_specs
            + [by_lead(value.shape) for pair in pairs for value in pair],
            out_specs=[
                column(rows, 0),
                column(total, 0),
                column(total, 0),
                pl.BlockSpec((total, D), lambda i, n: (0, 0)),
            ]
            + [by_lead(shape) for shape in halves],
            scratch_shapes=[pltpu.VMEM((total, D), full)],
        ),
        compiler_params=pltpu.CompilerParams(vmem_limit_bytes=VMEM_LIMIT),
        cost_estimate=SMALL_COST,
        name="attend_backward",
    )(
        scalars,
        queries,
        keys,
        values,
        grads,
        logs,
        deltas,
        pair_weight,
        pair_weight,
        *extra,
        *[value for pair in pairs for value in pair],
    )


def swap(value, axis, bit):
    count = lax.axis_size(axis)
    return lax.ppermute(value, axis, [(i, i ^ bit) for i in range(count)])


class Order:
    def __init__(self):
        self.marks = ()

    def __call__(self, *values):
        values = lax.optimization_barrier(values + self.marks)[: len(values)]
        self.marks = values
        return values[0] if len(values) == 1 else values


def outer_bits():
    bits = []
    bit = 2
    while bit < lax.axis_size("dp"):
        bits.append(bit)
        bit *= 2
    return bits


class Gather:
    def __init__(self, parts):
        self.bits = outer_bits()
        half = len(self.bits) // 2
        self.orders = [
            self.bits[half * (n % 2) :] + self.bits[: half * (n % 2)] for n in range(len(parts))
        ]
        self.result = [[([0], part)] for part in parts]
        self.step = 0
        self.early = []

    def advance(self, order):
        held = self.result
        if self.step < len(self.bits):
            masks = [[m for mask, _ in pieces for m in mask] for pieces in held]
            blocks = [
                jnp.concatenate([array for _, array in pieces]) if self.step else pieces[0][1]
                for pieces in held
            ]
            blocks = order(*blocks)
            bits = [turn[self.step] for turn in self.orders]
            self.result = [
                [(mask, block), ([m ^ bit for m in mask], swap(block, "dp", bit))]
                for mask, block, bit in zip(masks, blocks, bits)
            ]
        else:
            rest = [pieces[1:] if self.early else pieces for pieces in held]
            arrays = iter(order(*[array for pieces in rest for _, array in pieces]))
            self.result = []
            for n, pieces in enumerate(rest):
                kept = [(masks, next(arrays)) for masks, _ in pieces]
                ours = held[n][:1] + kept if self.early else kept
                theirs = [([m ^ 1 for m in masks], swap(array, "dp", 1)) for masks, array in kept]
                self.result.append(ours + self.early[n : n + 1] + theirs)
        self.step += 1

    def send_early(self, order):
        arrays = order(*[pieces[0][1] for pieces in self.result])
        self.early = [
            ([m ^ 1 for m in pieces[0][0]], swap(array, "dp", 1))
            for pieces, array in zip(self.result, arrays)
        ]


def canonical_row(me, rank, block, mask, rank_mask, stride, offset):
    if mask is None:
        return offset
    row = (me ^ mask) * block + offset
    if stride:
        if rank_mask >= 2:
            rank_mask = rank_mask ^ ((rank + 1) // 2 % 2)
        row = row + (rank ^ rank_mask) * stride
    return pl.multiple_of(row, 16)


def place_kernel(plan, block, *refs):
    count = len(plan)
    ins = refs[:count]
    outs = refs[count:-1]
    sems = refs[-1]
    me = lax.axis_index("dp")
    rank = lax.axis_index("mp")
    copies = []
    for ref, moves in zip(ins, plan):
        for start, size, which, mask, column, _, offset in moves:
            row = canonical_row(me, rank, block, mask, 0, 0, offset)
            copy = pltpu.make_async_copy(
                ref.at[pl.ds(start, size), :],
                outs[which].at[pl.ds(row, size), pl.ds(column * D, D)],
                sems.at[len(copies)],
            )
            copy.start()
            copies.append(copy)
    for copy in copies:
        copy.wait()


def plan_of(gathered, layouts):
    arrays = []
    plan = []
    for pieces, layout in zip(gathered, layouts):
        rows = sum(size for _, size, *_ in layout)
        for masks, array in pieces:
            moves = []
            for j, mask in enumerate(masks):
                for start, size, which, rank_mask, stride, offset in layout:
                    moves.append((j * rows + start, size, which, mask, rank_mask, stride, offset))
            arrays.append(array)
            plan.append(moves)
    return arrays, plan


def place(arrays, plan, block, shapes):
    return pl.pallas_call(
        functools.partial(place_kernel, plan, block),
        out_shape=[jax.ShapeDtypeStruct(shape, low) for shape in shapes],
        in_specs=[pl.BlockSpec(memory_space=pl.ANY)] * len(arrays),
        out_specs=[pl.BlockSpec(memory_space=pltpu.VMEM)] * len(shapes),
        scratch_shapes=[pltpu.SemaphoreType.DMA((sum(len(moves) for moves in plan),))],
        compiler_params=pltpu.CompilerParams(vmem_limit_bytes=VMEM_LIMIT),
        cost_estimate=SMALL_COST,
        name="place",
    )(*arrays)


def store_split(value, keep, send, index):
    block = keep.shape[2]
    even = lax.axis_index("dp") % 2 == 0
    for outer in range(keep.shape[1]):
        first = value[2 * outer * block : (2 * outer + 1) * block]
        other = value[(2 * outer + 1) * block : (2 * outer + 2) * block]
        keep[index, outer] = jnp.where(even, first, other).astype(low)
        send[index, outer] = jnp.where(even, other, first).astype(low)


def middle_kernel(plan, block, total, *refs):
    limit_ref, vector_ref = refs[:2]
    token_hbm, mixed_hbm, log_hbm, cot_hbm, teach_hbm = refs[2:7]
    pieces = refs[7 : 7 + total]
    (
        out_hbm,
        middle_hbm,
        grad_hbm,
        down_keep,
        down_send,
        up_keep,
        up_send,
        delta_ref,
        log_ref,
        sum_ref,
    ) = refs[7 + total : 17 + total]
    (
        token,
        mixed,
        logs,
        cot,
        teach,
        up,
        down,
        proj,
        right,
        slope,
        second,
        middle,
        final,
        out,
        final_low,
        middle_low,
        grad,
        accum,
        turned,
        stage_keep,
        stage_send,
        in_sems,
        weight_sems,
        out_sems,
        keep_sems,
        send_sems,
    ) = refs[17 + total :]
    hidden = FF // D
    targets = (up, down, proj)
    rows = token.shape[0]
    me = lax.axis_index("dp")
    rank = lax.axis_index("mp")

    def fetch(ref, scratch, n):
        copy = pltpu.make_async_copy(ref, scratch, in_sems.at[n])
        copy.start()
        return copy

    def send(scratch, ref, n):
        copy = pltpu.make_async_copy(scratch, ref, out_sems.at[n])
        copy.start()
        return copy

    gets = [
        fetch(token_hbm, token, 0),
        fetch(mixed_hbm, mixed, 1),
        fetch(log_hbm, logs, 2),
        fetch(cot_hbm, cot, 3),
        fetch(teach_hbm, teach, 4),
    ]
    loads = {0: [], 1: [], 2: []}
    number = 0
    for want in (2, 0, 1):
        for ref, moves in zip(pieces, plan):
            for start, size, which, mask, rank_mask, stride, offset in moves:
                if which != want:
                    continue
                row = canonical_row(me, rank, block, mask, rank_mask, stride, offset)
                copy = pltpu.make_async_copy(
                    ref.at[pl.ds(start, size), :],
                    targets[which].at[pl.ds(row, size), :],
                    weight_sems.at[number],
                )
                copy.start()
                loads[which].append(copy)
                number += 1

    table_row = vector_ref[0:1, :]
    out_bias = vector_ref[1:2, :]
    gain = vector_ref[2:3, :]
    shift = vector_ref[3:4, :]
    down_bias = vector_ref[4:5, :]
    weight = vector_ref[5:6, :]
    gets[0].wait()
    gets[1].wait()
    right[2 * hidden] = mixed[...].astype(low)
    for copy in loads[2]:
        copy.wait()
    state = token[...].astype(full) + table_row + out_bias
    state = state + dot_of(right[2 * hidden], proj[...], 1, 1)
    middle[...] = state
    unit, _ = norm_stats(state)
    second[...] = (unit * gain + shift).astype(low)
    accum[...] = jnp.zeros((rows, D), full)
    for copy in loads[0]:
        copy.wait()
    for copy in loads[1]:
        copy.wait()

    def forward(m, _):
        place = pl.ds(pl.multiple_of(m * D, D), D)
        half = rows // 2
        spans = [pl.ds(part * half, half) for part in range(2)]
        values = [
            dot_of(second[span, :], up[place, :], 1, 0) + vector_ref[pl.ds(8 + m, 1), :]
            for span in spans
        ]
        for span, value in zip(spans, values):
            cumulative = 0.5 + 0.5 * lax.erf(value * (0.5**0.5))
            active = (value * cumulative).astype(low)
            right[m, span, :] = active
            slope[m, span, :] = (
                cumulative + value * jnp.exp(-0.5 * value * value) * 0.3989422804014327
            )
            accum[span, :] += dot_of(active, down[place, :], 1, 1)
        return 0

    lax.fori_loop(0, FF // D, forward, 0)
    final_state = middle[...] + accum[...] + down_bias
    out[...] = final_state.astype(low)
    puts = [send(out, out_hbm, 0)]
    gets[3].wait()
    gets[4].wait()
    place = lax.broadcasted_iota(jnp.int32, (rows, 1), 0)
    grads = cot[...].astype(full) + weight * (final_state - teach[...].astype(full))
    grads = jnp.where(place < limit_ref[5], grads, 0.0)
    final[...] = grads
    final_low[...] = grads.astype(low)
    sum_ref[3:4, :] = jnp.sum(grads, axis=0, keepdims=True)
    accum[...] = jnp.zeros((rows, D), full)

    def backward(m, _):
        place = pl.ds(pl.multiple_of(m * D, D), D)
        value = slope[m] * dot_of(final_low[...], down[place, :], 1, 0)
        value = value.astype(low)
        right[hidden + m] = value
        sum_ref[pl.ds(8 + m, 1), :] = jnp.sum(value.astype(full), axis=0, keepdims=True)
        accum[...] += dot_of(value, up[place, :], 1, 1)
        return 0

    lax.fori_loop(0, FF // D, backward, 0)
    unit, inverse = norm_stats(middle[...])
    second_grad = accum[...]
    sum_ref[0:1, :] = jnp.sum(second_grad * unit, axis=0, keepdims=True)
    sum_ref[1:2, :] = jnp.sum(second_grad, axis=0, keepdims=True)
    scaled = second_grad * gain
    mean_scaled = jnp.mean(scaled, axis=-1, keepdims=True)
    mean_unit = jnp.mean(scaled * unit, axis=-1, keepdims=True)
    total_grad = final[...] + inverse * (scaled - mean_scaled - unit * mean_unit)
    middle[...] = total_grad
    puts.append(send(middle, middle_hbm, 1))
    middle_low[...] = total_grad.astype(low)
    sum_ref[2:3, :] = jnp.sum(total_grad, axis=0, keepdims=True)
    attended_grad = dot_of(middle_low[...], proj[...], 1, 0).astype(low)
    grad[...] = attended_grad
    puts.append(send(grad, grad_hbm, 2))
    gets[2].wait()
    head = lax.broadcasted_iota(jnp.int32, (16, D), 0)
    lane = lax.broadcasted_iota(jnp.int32, (16, D), 1)
    member = jnp.where(lane // HEAD_DIM == head, 1.0, 0.0)
    leader = jnp.where(lane == head * HEAD_DIM, 1.0, 0.0)
    exact = functools.partial(
        lax.dot_general,
        dimension_numbers=(((1,), (1,)), ((), ())),
        precision=lax.Precision.HIGHEST,
        preferred_element_type=full,
    )
    deltas = exact(member, attended_grad.astype(full) * mixed[...])
    tops = exact(leader, logs[...])
    for pair in range(PAIRS):
        delta_ref[pair] = deltas[2 * pair : 2 * pair + 2]
        log_ref[pair] = tops[2 * pair : 2 * pair + 2]
    turned[0] = final_low[...].T
    turned[1] = second[...].T
    turned[2] = middle_low[...].T

    def weights(i, _):
        store_split(dot_of(turned[i // hidden], right[i], 1, 0), stage_keep, stage_send, i)

        @pl.when(i < hidden)
        def _():
            pltpu.make_async_copy(stage_keep.at[i], down_keep.at[i], keep_sems.at[i]).start()
            pltpu.make_async_copy(stage_send.at[i], down_send.at[i], send_sems.at[i]).start()

        @pl.when(i >= hidden)
        def _():
            row = i - hidden
            pltpu.make_async_copy(stage_keep.at[i], up_keep.at[row], keep_sems.at[i]).start()
            pltpu.make_async_copy(stage_send.at[i], up_send.at[row], send_sems.at[i]).start()

        return 0

    lax.fori_loop(0, 2 * hidden + 1, weights, 0)
    for copy in puts:
        copy.wait()
    for i in range(2 * hidden + 1):
        if i < hidden:
            keep, gone, row = down_keep, down_send, i
        else:
            keep, gone, row = up_keep, up_send, i - hidden
        pltpu.make_async_copy(stage_keep.at[i], keep.at[row], keep_sems.at[i]).wait()
        pltpu.make_async_copy(stage_send.at[i], gone.at[row], send_sems.at[i]).wait()


def middle_call(limit, vectors, tokens, mixed, logs, cot, teach, arrays, plan, block, dp):
    rows = tokens.shape[0]
    hidden = FF // D
    narrow = jax.ShapeDtypeStruct((rows, D), low)
    wide = jax.ShapeDtypeStruct((rows, D), full)
    shape = (dp // 2, D // dp, D)
    parts = [jax.ShapeDtypeStruct((count,) + shape, low) for count in (hidden, hidden + 1)]
    stats = jax.ShapeDtypeStruct((PAIRS, 2, rows), full)
    anywhere = pl.BlockSpec(memory_space=pl.ANY)
    inside = pl.BlockSpec(memory_space=pltpu.VMEM)
    moves = sum(len(part) for part in plan)
    return pl.pallas_call(
        functools.partial(middle_kernel, plan, block, len(arrays)),
        out_shape=(
            narrow,
            wide,
            narrow,
            parts[0],
            parts[0],
            parts[1],
            parts[1],
            stats,
            stats,
            jax.ShapeDtypeStruct((8 + 8, D), full),
        ),
        in_specs=[pl.BlockSpec(memory_space=pltpu.SMEM), inside]
        + [anywhere] * (5 + len(arrays)),
        out_specs=[anywhere] * 7 + [inside] * 3,
        scratch_shapes=[
            pltpu.VMEM((rows, D), low),
            pltpu.VMEM((rows, D), full),
            pltpu.VMEM((rows, D), full),
            pltpu.VMEM((rows, D), low),
            pltpu.VMEM((rows, D), low),
            pltpu.VMEM((FF, D), low),
            pltpu.VMEM((FF, D), low),
            pltpu.VMEM((D, D), low),
            pltpu.VMEM((2 * hidden + 1, rows, D), low),
            pltpu.VMEM((hidden, rows, D), full),
            pltpu.VMEM((rows, D), low),
            pltpu.VMEM((rows, D), full),
            pltpu.VMEM((rows, D), full),
            pltpu.VMEM((rows, D), low),
            pltpu.VMEM((rows, D), low),
            pltpu.VMEM((rows, D), low),
            pltpu.VMEM((rows, D), low),
            pltpu.VMEM((rows, D), full),
            pltpu.VMEM((3, D, rows), low),
            pltpu.VMEM((2 * hidden + 1,) + shape, low),
            pltpu.VMEM((2 * hidden + 1,) + shape, low),
            pltpu.SemaphoreType.DMA((5,)),
            pltpu.SemaphoreType.DMA((moves,)),
            pltpu.SemaphoreType.DMA((3,)),
            pltpu.SemaphoreType.DMA((2 * hidden + 1,)),
            pltpu.SemaphoreType.DMA((2 * hidden + 1,)),
        ],
        compiler_params=pltpu.CompilerParams(vmem_limit_bytes=VMEM_LIMIT),
        cost_estimate=SMALL_COST,
        name="middle",
    )(limit, vectors, tokens, mixed, logs, cot, teach, *arrays)


def fold_block(keep, got, out_keep, out_send, bit, place):
    step = 1 << place
    mine = (lax.axis_index("dp") // bit) % 2 * step
    for j in range(keep.shape[1] // 2):
        base = (j // step) * 2 * step + j % step
        for out, shift in ((out_keep, mine), (out_send, step - mine)):
            value = keep[0, base + shift].astype(full) + got[0, base + shift].astype(full)
            out[0, j] = value.astype(low)


def fold_kernel(bits, places, *refs):
    count = len(bits)
    for n in range(count):
        fold_block(
            *refs[2 * n : 2 * n + 2],
            *refs[2 * count + 2 * n : 2 * count + 2 * n + 2],
            bits[n],
            places[n],
        )


def fold(pairs, bits, places):
    lead = pairs[0][0].shape[0]
    block = lambda shape: pl.BlockSpec((1,) + shape[1:], lambda i: (i, 0, 0, 0))
    halves = [
        (keep.shape[0], keep.shape[1] // 2) + keep.shape[2:] for keep, _ in pairs for _ in range(2)
    ]
    outs = pl.pallas_call(
        functools.partial(fold_kernel, bits, places),
        out_shape=[jax.ShapeDtypeStruct(shape, low) for shape in halves],
        grid=(lead,),
        in_specs=[block(value.shape) for pair in pairs for value in pair],
        out_specs=[block(shape) for shape in halves],
        compiler_params=pltpu.CompilerParams(vmem_limit_bytes=VMEM_LIMIT),
        cost_estimate=pl.CostEstimate(flops=0, bytes_accessed=16 << 20, transcendentals=0),
        name="fold",
    )(*[value for pair in pairs for value in pair])
    return [(outs[2 * n], outs[2 * n + 1]) for n in range(len(pairs))]


def qkv_grad_kernel(count, *refs):
    sources = refs[: 3 * count + 1]
    outs = refs[3 * count + 1 : 3 * count + 5]
    sum_ref, held, turned, total, stage, in_sems, out_sems = refs[3 * count + 5 :]
    first_use = [0, count] + list(range(1, count)) + list(range(count + 1, 3 * count + 1))
    for n in first_use:
        pltpu.make_async_copy(sources[n], held.at[n], in_sems.at[n]).start()

    def wait(n):
        pltpu.make_async_copy(sources[0], held.at[n], in_sems.at[n]).wait()

    def turn(n, _):
        wait(n)
        turned[n] = held[n].T
        return 0

    lax.fori_loop(0, count, turn, 0)
    sum_ref[...] = jnp.zeros_like(sum_ref)

    def step(i, _):
        c = (i + count - 1) // count
        n = jnp.where(i == 0, 0, (i + count - 1) % count)
        wait(count + i)
        right = held[count + i]
        value = dot_of(turned[n], right, 1, 0)
        total[...] = value + jnp.where(n == 0, jnp.zeros_like(value), total[...])

        @pl.when(c != 1)
        def _():
            row = pl.ds(pl.multiple_of(c * 4, 8), 1)
            sum_ref[row, :] += jnp.sum(right.astype(full), axis=0, keepdims=True)

        @pl.when(i % count == 0)
        def _():
            for part in range(2):
                store_split(
                    total[:, part * D // 2 : (part + 1) * D // 2],
                    stage.at[part],
                    stage.at[2 + part],
                    c,
                )
            for k in range(4):
                pltpu.make_async_copy(
                    stage.at[k, c], outs[k].at[c], out_sems.at[k * 3 + c]
                ).start()

        return 0

    lax.fori_loop(0, 2 * count + 1, step, 0)
    for k in range(4):
        for c in range(3):
            pltpu.make_async_copy(stage.at[k, c], outs[k].at[c], out_sems.at[k * 3 + c]).wait()


def qkv_grads(chunks, query_grad, key_grads, value_grads, dp):
    rows = query_grad.shape[0]
    count = len(chunks)
    shape = (3, dp // 2, D // dp, D // 2)
    anywhere = pl.BlockSpec(memory_space=pl.ANY)
    return pl.pallas_call(
        functools.partial(qkv_grad_kernel, count),
        out_shape=[jax.ShapeDtypeStruct(shape, low)] * 4
        + [jax.ShapeDtypeStruct((16, D), full)],
        in_specs=[anywhere] * (3 * count + 1),
        out_specs=[anywhere] * 4 + [pl.BlockSpec(memory_space=pltpu.VMEM)],
        scratch_shapes=[
            pltpu.VMEM((3 * count + 1, rows, D), low),
            pltpu.VMEM((count, D, rows), low),
            pltpu.VMEM((D, D), full),
            pltpu.VMEM((4,) + shape, low),
            pltpu.SemaphoreType.DMA((3 * count + 1,)),
            pltpu.SemaphoreType.DMA((12,)),
        ],
        compiler_params=pltpu.CompilerParams(vmem_limit_bytes=VMEM_LIMIT),
        cost_estimate=SMALL_COST,
        name="qkv_grads",
    )(*chunks, query_grad, *key_grads, *value_grads)


def last_kernel(
    token_ref,
    first_ref,
    right_ref,
    left_ref,
    middle_ref,
    vector_ref,
    gain_ref,
    bias_ref,
    sum_ref,
    out_ref,
    pack_ref,
):
    @pl.when(pl.program_id(0) == 0)
    def _():
        pack_ref[...] = jnp.zeros_like(pack_ref)
        pack_ref[1:2, :] = sum_ref[0:1, :]
        pack_ref[3:4, :] = sum_ref[1:2, :]
        pack_ref[4:5, :] = bias_ref[0:1, :]
        pack_ref[5:6, :] = bias_ref[8:9, :]
        pack_ref[6:8, :] = sum_ref[2:4, :]
        pack_ref[8 : 8 + FF // D, :] = sum_ref[8 : 8 + FF // D, :]

    unit, inverse = norm_stats(token_ref[...].astype(full) + vector_ref[0:1, :])
    grad = first_ref[...] + right_ref[...].astype(full) + left_ref[...].astype(full)
    scaled = grad * gain_ref[0:1, :]
    mean_scaled = jnp.mean(scaled, axis=-1, keepdims=True)
    mean_unit = jnp.mean(scaled * unit, axis=-1, keepdims=True)
    result = middle_ref[...] + inverse * (scaled - mean_scaled - unit * mean_unit)
    out_ref[...] = result
    pack_ref[0:1, :] += jnp.sum(grad * unit, axis=0, keepdims=True)
    pack_ref[2:3, :] += jnp.sum(grad, axis=0, keepdims=True)
    pack_ref[pl.ds(16 + lax.axis_index("dp"), 1), :] += jnp.sum(result, axis=0, keepdims=True)


def last_norm(tokens, first, right, left, middle_grad, vectors, gains, bias_sums, sums, dp):
    rows = tokens.shape[0]
    part = pl.BlockSpec((rows // 4, D), lambda i: (i, 0))
    whole = lambda value: pl.BlockSpec(value.shape, lambda i: (0, 0))
    small = (vectors, gains, bias_sums, sums)
    return pl.pallas_call(
        last_kernel,
        out_shape=(
            jax.ShapeDtypeStruct((rows, D), full),
            jax.ShapeDtypeStruct((16 + dp, D), full),
        ),
        grid=(4,),
        in_specs=[part] * 5 + [whole(value) for value in small],
        out_specs=[part, pl.BlockSpec((16 + dp, D), lambda i: (0, 0))],
        compiler_params=pltpu.CompilerParams(vmem_limit_bytes=VMEM_LIMIT),
        cost_estimate=SMALL_COST,
        name="last_norm",
    )(tokens, first, right, left, middle_grad, *small)


def two_parts(value, axis, mine):
    keep = lax.dynamic_index_in_dim(value, mine, axis, keepdims=False)
    send = lax.dynamic_index_in_dim(value, 1 - mine, axis, keepdims=False)
    return keep, send.astype(low)


class Scatter:
    def __init__(self, parts, turns):
        self.bits = outer_bits()
        half = len(self.bits) // 2
        self.orders = [
            [1] + self.bits[half * (turn % 2) :] + self.bits[: half * (turn % 2)] for turn in turns
        ]
        self.left = [list(self.bits) for _ in turns]
        self.step = 0
        self.parts = parts

    def sends(self):
        return [send for _, send in self.parts]

    def exchange(self, sends):
        self.pairs = [
            (keep, swap(send, "dp", turn[self.step]))
            for (keep, _), send, turn in zip(self.parts, sends, self.orders)
        ]
        self.step += 1

    def folds(self):
        if self.step > len(self.bits):
            return [], [], []
        bits = [turn[self.step] for turn in self.orders]
        places = []
        for left, bit in zip(self.left, bits):
            places.append(left.index(bit))
            left.remove(bit)
        return self.pairs, bits, places

    def give(self, outs):
        self.parts = [(outs[n], outs[n + 1]) for n in range(0, len(outs), 2)]

    def fold(self):
        outs = []
        for pair, bit, at in zip(*self.folds()):
            outs += fold([pair], [bit], [at])[0]
        self.give(outs)

    def advance(self, order):
        sends = order(*self.sends())
        self.exchange(list(sends) if len(self.parts) > 1 else [sends])

    def finish(self, order):
        while self.step <= len(self.bits):
            self.fold()
            self.advance(order)
        got = order(*[other for _, other in self.pairs])
        return [
            (keep.astype(full) + other.astype(full))[:, 0]
            for (keep, _), other in zip(self.pairs, got)
        ]


def scatter_dp(parts, turns):
    scatter = Scatter(parts, turns)
    while True:
        sends = yield scatter.sends()
        scatter.exchange(sends)
        if scatter.step > len(scatter.bits):
            break
        scatter.parts = fold(*scatter.folds())
    got = yield [other for _, other in scatter.pairs]
    return [
        (keep.astype(full) + other.astype(full))[:, 0]
        for (keep, _), other in zip(scatter.pairs, got)
    ]


def scatter_mp(value):
    rank = lax.axis_index("mp")
    part = lambda index: lax.dynamic_index_in_dim(value, index, keepdims=False)
    sends = yield [part(rank ^ bit).astype(low) for bit in (1, 2, 3)]
    got = yield [swap(send, "mp", bit) for bit, send in zip((1, 2, 3), sends)]
    got = [other.astype(full) for other in got]
    return (part(rank) + got[0]) + (got[1] + got[2])


def halve_mp(value):
    rank = lax.axis_index("mp")
    pairs = value.reshape((2, 2) + value.shape[1:])
    keep, send = two_parts(pairs, 1, rank % 2)
    (send,) = yield [send]
    (got,) = yield [swap(send, "mp", 1)]
    keep, send = two_parts(keep.astype(full) + got.astype(full), 0, rank // 2)
    (send,) = yield [send]
    (got,) = yield [swap(send, "mp", 2)]
    return keep + got.astype(full)


def scatter_feed(up_own, down_own):
    mp = lax.axis_size("mp")
    block = down_own.shape[1]
    out_own = up_own[mp].reshape(block, mp, -1).transpose(1, 0, 2)
    own = yield from halve_mp(
        jnp.concatenate([up_own[:mp], down_own, out_own.reshape(mp, -1, D)], axis=1)
    )
    return own[:block], own[block : 2 * block].T, own[2 * block :].reshape(block, -1).T


def scatter_qkv(keep_left, keep_right, send_left, send_right):
    left_part, right_part = yield from scatter_dp(
        [(keep_left, send_left), (keep_right, send_right)], (0, 1)
    )
    width = D // lax.axis_size("mp")
    parts = [part[..., at : at + width] for part in (left_part, right_part) for at in (0, width)]
    return (yield from scatter_mp(jnp.stack(parts)))


def sum_small(value):
    (value,) = yield [value]
    value = value + swap(value, "dp", 1)
    bits = outer_bits()
    groups = [("dp", bits[n : n + 2]) for n in range(0, len(bits), 2)] + [("mp", [1, 2])]
    for axis, pair in groups:
        (value,) = yield [value]
        if len(pair) == 1:
            value = value + swap(value, axis, pair[0])
        else:
            one, two = pair
            got = [swap(value, axis, mask) for mask in (one, two, one + two)]
            if axis == "mp":
                got = yield got
            value = (value + got[0]) + (got[1] + got[2])
    return value


class Steps:
    def __init__(self, steps):
        self.steps = steps
        self.pending = next(steps)
        self.result = None

    def advance(self, order):
        if self.pending is None:
            return
        sends = order(*self.pending)
        sends = [sends] if len(self.pending) == 1 else list(sends)
        try:
            self.pending = self.steps.send(sends)
        except StopIteration as stop:
            self.pending = None
            self.result = stop.value

    def finish(self, order):
        while self.pending is not None:
            self.advance(order)
        return self.result


def shards(
    tokens_in,
    timesteps,
    lengths,
    time_table,
    norm_gains,
    norm_biases,
    w_qkv,
    qv_bias,
    w_out,
    out_bias,
    w_up,
    up_bias,
    w_down,
    down_bias,
    cotangent,
    teacher,
):
    rank = lax.axis_index("mp")
    data_rank = lax.axis_index("dp")
    mp = lax.axis_size("mp")
    dp = lax.axis_size("dp")
    own_rows = tokens_in.shape[0]
    length = lax.dynamic_index_in_dim(lengths, data_rank, keepdims=False)
    own_time = lax.dynamic_index_in_dim(timesteps, data_rank, keepdims=False)
    odd = rank % 2 == 1
    upper = rank >= 2
    middle = jnp.logical_or(rank == 1, rank == 2)
    order = Order()
    along = lambda value, pairs: lax.ppermute(value, "mp", pairs)

    block = w_qkv.shape[1]
    aligned = block % 32 == 0
    narrow = order(jnp.concatenate([w_qkv.reshape(3 * block, -1), w_out.T]))
    first_swap = swap(narrow, "mp", 1)
    tall = order(jnp.concatenate([w_up, w_down.T]))
    tall_swap = swap(tall, "mp", 1)
    pair = order(
        jnp.concatenate(
            [jnp.where(odd, first_swap, narrow), jnp.where(odd, narrow, first_swap)], axis=1
        )
    )
    second_swap = swap(pair, "mp", 2)
    tokens, lengths, own_time, norm_gains, norm_biases, out_bias, down_bias, up_bias, length = order(
        tokens_in, lengths, own_time, norm_gains, norm_biases, out_bias, down_bias, up_bias, length
    )
    table_row = lax.dynamic_slice_in_dim(time_table, own_time, 1).astype(full)
    unit_one, _ = norm_stats(tokens.astype(full) + table_row)
    first_norm = (unit_one * norm_gains[0] + norm_biases[0]).astype(low)
    loss_weight = lengths.shape[0] * MAXLEN / jnp.sum(lengths).astype(full)
    vectors = jnp.concatenate(
        [
            table_row,
            out_bias[None],
            norm_gains[1:2],
            norm_biases[1:2],
            down_bias[None],
            jnp.full((3, D), loss_weight),
            up_bias.reshape(-1, D),
            jnp.zeros((4, D), full),
        ]
    )
    scalars = jnp.stack(
        [
            rank,
            jnp.where(rank == 0, 1, rank - 1),
            jnp.where(upper, rank - 2, rank + 2),
            jnp.where(middle, rank + 1, 3 - rank),
            length,
            length - rank * own_rows,
        ]
    ).astype(jnp.int32)
    first_norm, vectors, scalars = order(first_norm, vectors, scalars)
    wide = jnp.concatenate(
        [jnp.where(upper, second_swap, pair), jnp.where(upper, pair, second_swap)], axis=1
    )
    qkv_rows, out_rows = wide[: 3 * block], wide[3 * block :]
    if aligned:
        split = 3 * block // 2
        qkv_gather = Gather([qkv_rows[:split], qkv_rows[split:]])
        qkv_gather.advance(order)
    tall = order(jnp.concatenate([tall, tall_swap]))
    tall_across = along(tall, [(1, 2), (2, 1)])

    sent = order(first_norm)
    from_left = along(sent, [(0, 1), (1, 2), (2, 3)])
    from_right = along(sent, [(1, 0), (2, 1), (3, 2)])
    tall_across = order(tall_across)
    tall_far = along(tall_across, [(1, 0), (2, 3)])
    if aligned:
        while qkv_gather.step < len(qkv_gather.bits):
            qkv_gather.advance(order)
        qkv_gather.advance(order)
    hop_right, hop_left = order(from_left, from_right)
    second_right = along(hop_right, [(1, 2), (2, 3)])
    second_left = along(hop_left, [(1, 0), (2, 1)])
    if aligned:
        arrays, plan = plan_of(
            qkv_gather.result,
            [
                [(0, block, 0, 0, 0, 0), (block, split - block, 1, 0, 0, 0)],
                [
                    (0, 2 * block - split, 1, 0, 0, split - block),
                    (2 * block - split, block, 1, 1, 0, 0),
                ],
            ],
        )
        query_weight, pair_weight = order(*place(arrays, plan, block, [(D, D), (D, 2 * D)]))
        tall_other = jnp.where(middle, tall_across, order(tall_far))
        feed_gather = Gather(
            [
                jnp.concatenate([tall, out_rows[: block // 2]]),
                jnp.concatenate([tall_other, out_rows[block // 2 :]]),
            ]
        )
        feed_gather.advance(order)
    else:
        weights = lax.all_gather(qkv_rows.reshape(3, block, D), "dp", axis=1, tiled=True)
        query_weight = weights[0]
        pair_weight = jnp.concatenate([weights[1], weights[2]], axis=1)
    near = jnp.where(rank == 0, hop_left, hop_right)
    attend = lambda parts, numbers, carried: order(
        *attend_forward(
            parts,
            numbers,
            scalars,
            query_weight,
            pair_weight,
            qv_bias[0:1],
            qv_bias[1:2],
            carried,
        )
    )
    key_own, value_own, queries, *state = attend([order(first_norm)], (0,), None)
    second_right, second_left = order(second_right, second_left)
    second = order(jnp.where(upper, second_right, second_left))
    third = along(second, [(1, 0), (2, 3)])
    if aligned:
        while feed_gather.step < len(feed_gather.bits):
            feed_gather.advance(order)
        feed_gather.send_early(order)
    near, second = order(near, second)
    key_near, key_second, value_near, value_second, *state = attend(
        [near, second], (1, 2), (queries, *state)
    )
    last = order(jnp.where(middle, hop_left, order(third)))
    key_last, value_last, mixed, logs = attend([order(last)], (3,), (queries, *state))
    if aligned:
        feed_gather.advance(order)
        layout = lambda masks, shift: [
            (0, block, 0, masks[0], D, 0),
            (block, block, 1, masks[0], D, 0),
            (2 * block, block, 0, masks[1], D, 0),
            (3 * block, block, 1, masks[1], D, 0),
            (4 * block, block // 2, 2, 0, 0, shift),
        ]
        arrays, plan = plan_of(
            feed_gather.result, [layout((0, 1), 0), layout((2, 3), block // 2)]
        )
    else:
        arrays = [
            lax.all_gather(w_up, ("mp", "dp"), axis=0, tiled=True),
            lax.all_gather(w_down.T, ("mp", "dp"), axis=0, tiled=True),
            lax.all_gather(out_rows, "dp", axis=0, tiled=True),
        ]
        plan = [[(0, array.shape[0], n, None, 0, 0, 0)] for n, array in enumerate(arrays)]
    chunks = [first_norm, near, second, last]
    keys = [key_own, key_near, key_second, key_last]
    values = [value_own, value_near, value_second, value_last]

    output, middle_grad, attended_grad, *parts, deltas, log_rows, sums = middle_call(
        scalars, vectors, tokens, mixed, logs, cotangent, teacher, arrays, plan, block, dp
    )
    scatter = Scatter([(parts[0], parts[1]), (parts[2], parts[3])], (1, 0))
    scatter.advance(order)

    key_grads = [None] * 4
    value_grads = [None] * 4
    firsts = [None] * 4
    query_grad = None
    for n in (3, 2, 1, 0):
        pairs, bits, places = scatter.folds() if n % 2 == 0 else ([], [], [])
        query_grad, key_grads[n], value_grads[n], firsts[n], *folded = attend_backward(
            n,
            queries,
            keys[n],
            values[n],
            order(attended_grad),
            log_rows,
            deltas,
            query_weight,
            pair_weight,
            scalars,
            query_grad,
            n == 0,
            pairs,
            bits,
            places,
        )
        firsts[n] = order(firsts[n])
        if folded:
            scatter.give(folded)
        if n == 3:
            back_last = along(firsts[3], [(0, 1), (3, 2)]).astype(full)
        elif n == 2:
            scatter.advance(order)
            payload = order((firsts[2] + back_last).astype(low))
            back_right = along(payload, [(0, 1), (1, 2)]).astype(full)
            back_left = along(payload, [(3, 2), (2, 1)]).astype(full)
        elif n == 1:
            to_right = jnp.where(
                rank == 0, firsts[1], firsts[3].astype(full) + back_right
            ).astype(low)
            to_left = (firsts[1] + back_left).astype(low)
            to_right, to_left = order(to_right, to_left)
            final_right = along(to_right, [(0, 1), (1, 2), (2, 3)])
            final_left = along(to_left, [(3, 2), (2, 1), (1, 0)])
    scatter.advance(order)
    query_grad, final_right, final_left = order(query_grad, final_right, final_left)
    *halves, bias_sums = qkv_grads(chunks, query_grad, key_grads, value_grads, dp)
    qkv = Steps(scatter_qkv(*halves))
    qkv.advance(order)
    down_own, up_own = scatter.finish(order)
    feed = Steps(scatter_feed(up_own, down_own))
    feed.advance(order)
    qkv.advance(order)
    tokens, first_own = order(tokens, firsts[0])
    input_grad, packed = last_norm(
        tokens,
        first_own,
        final_right,
        final_left,
        middle_grad,
        vectors,
        norm_gains,
        bias_sums,
        sums,
        dp,
    )
    packed, input_grad = order(packed, input_grad)
    small = Steps(sum_small(packed))
    feed.advance(order)
    feed.advance(order)
    small.advance(order)
    qkv.advance(order)
    feed.advance(order)
    qkv.advance(order)
    small.advance(order)
    qkv.advance(order)
    small.advance(order)
    total = small.finish(order)
    up_grad, down_grad, out_grad = feed.finish(order)
    qkv_grad = qkv.finish(order)
    fixed = 16
    chosen = (timesteps[None, :] == jnp.arange(time_table.shape[0])[:, None]).astype(full)
    table_grad = lax.dot_general(
        chosen,
        total[fixed:],
        (((1,), (0,)), ((), ())),
        precision=lax.Precision.HIGHEST,
        preferred_element_type=full,
    )
    return (
        output,
        input_grad,
        table_grad,
        total[0:2],
        total[2:4],
        qkv_grad,
        total[4:6],
        out_grad,
        total[6],
        up_grad,
        total[8 : 8 + FF // D].reshape(FF),
        down_grad,
        total[7],
    )


def solution(mesh):
    rows = P(both, None)
    placed = (
        rows,
        P(),
        P(),
        P(),
        P(),
        P(),
        P(None, "dp", "mp"),
        P(),
        P("mp", "dp"),
        P(),
        P("dp", "mp"),
        P(),
        P("mp", "dp"),
        P(),
        rows,
        rows,
    )
    return jax.shard_map(
        shards,
        mesh=mesh,
        in_specs=placed,
        out_specs=(
            rows,
            rows,
            P(),
            P(),
            P(),
            P(None, "dp", "mp"),
            P(),
            P("mp", "dp"),
            P(),
            P("dp", "mp"),
            P(),
            P("mp", "dp"),
            P(),
        ),
        check_vma=False,
    )
```

```python
import functools

import jax
import jax.numpy as jnp
from jax import lax
from jax.experimental import pallas as pl
from jax.experimental.pallas import tpu as pltpu
from jax.sharding import PartitionSpec as P

D = 768
HEADS = 12
HEAD_DIM = 64
FF = 3072
MAXLEN = 2048
PAIR = 2 * HEAD_DIM
PAIRS = HEADS // 2
VMEM_LIMIT = 58 << 20
SMALL_COST = pl.CostEstimate(flops=1 << 20, bytes_accessed=1 << 16, transcendentals=0)

far_below = -1e30
epsilon = 1e-05
score_scale = HEAD_DIM ** (-0.5)
low = jnp.bfloat16
full = jnp.float32
both = ("dp", "mp")


def norm_stats(values):
    center = values - jnp.mean(values, axis=-1, keepdims=True)
    spread = jnp.mean(center * center, axis=-1, keepdims=True)
    inverse = lax.rsqrt(spread + epsilon)
    return center * inverse, inverse


def dot_of(left_side, right_side, left_dim, right_dim):
    return lax.dot_general(
        left_side,
        right_side,
        (((left_dim,), (right_dim,)), ((), ())),
        preferred_element_type=full,
    )


def first_half(shape):
    return lax.broadcasted_iota(jnp.int32, shape, len(shape) - 1) < HEAD_DIM


def forward_kernel(numbers, first, final, scalars, *refs):
    count = len(numbers)
    chunk_refs = refs[:count]
    wk_ref, wv_ref, value_bias_ref = refs[count : count + 3]
    refs = refs[count + 3 :]
    if first:
        wq_ref, query_bias_ref = refs[:2]
        key_outs, value_outs = refs[2 : 2 + count], refs[2 + count : 2 + 2 * count]
        query_out, top_ref, sum_ref, acc_ref = refs[2 + 2 * count :]
        q_pair = (dot_of(chunk_refs[0][...], wq_ref[...], 1, 0) + query_bias_ref[...]).astype(low)
        q_pair = q_pair * jnp.asarray(score_scale, low)
        query_out[...] = q_pair
    else:
        q_ref, top_in, sum_in, acc_in = refs[:4]
        key_outs, value_outs = refs[4 : 4 + count], refs[4 + count : 4 + 2 * count]
        results = refs[4 + 2 * count :]
        q_pair = q_ref[...]
    weight = jnp.concatenate([wk_ref[...], wv_ref[...]], axis=1)
    keys = []
    values = []
    for n in range(count):
        both_parts = dot_of(chunk_refs[n][...], weight, 1, 0)
        keys.append(both_parts[:, :PAIR].astype(low))
        values.append((both_parts[:, PAIR:] + value_bias_ref[...]).astype(low))
        key_outs[n][...] = keys[n]
        value_outs[n][...] = values[n]
    rows = q_pair.shape[0]
    size = keys[0].shape[0]
    place = lax.broadcasted_iota(jnp.int32, (1, size), 1)
    lower = first_half((rows, PAIR))
    parts = []
    for half in range(2):
        kept = lower if half == 0 else jnp.logical_not(lower)
        q_half = jnp.where(kept, q_pair, jnp.zeros_like(q_pair))
        scores = []
        for n in range(count):
            bias = jnp.where(place + scalars[numbers[n]] * size < scalars[4], 0.0, far_below)
            scores.append(dot_of(q_half, keys[n], 1, 1) + bias)
        highest = functools.reduce(
            jnp.maximum, [jnp.max(score, axis=-1, keepdims=True) for score in scores]
        )
        totals = jnp.zeros_like(highest)
        mixed = jnp.zeros((rows, PAIR), full)
        for n in range(count):
            exp_scores = jnp.exp(scores[n] - highest)
            totals = totals + jnp.sum(exp_scores, axis=-1, keepdims=True)
            mixed = mixed + dot_of(exp_scores.astype(low), values[n], 1, 0)
        parts.append((highest, totals, mixed))
    top = jnp.where(lower, parts[0][0], parts[1][0])
    total = jnp.where(lower, parts[0][1], parts[1][1])
    mixed = jnp.where(lower, parts[0][2], parts[1][2])
    if first:
        top_ref[...] = top
        sum_ref[...] = total
        acc_ref[...] = mixed
    else:
        highest = jnp.maximum(top, top_in[...])
        here = jnp.exp(top - highest)
        before = jnp.exp(top_in[...] - highest)
        total = total * here + sum_in[...] * before
        mixed = mixed * here + acc_in[...] * before
        if final:
            results[0][...] = mixed / total
            results[1][...] = highest + jnp.log(total)
        else:
            results[0][...] = highest
            results[1][...] = total
            results[2][...] = mixed


def attend_forward(chunks, numbers, scalars, query_weight, pair_weight, query_bias, value_bias, carried):
    rows = chunks[0].shape[0]
    count = len(chunks)
    first = carried is None
    final = 3 in numbers
    column = lambda height, c: pl.BlockSpec((height, PAIR), lambda i, n: (0, c * PAIRS + i))
    whole = pl.BlockSpec((rows, D), lambda i, n: (0, 0))
    wide = jax.ShapeDtypeStruct((rows, D), full)
    narrow = jax.ShapeDtypeStruct((rows, D), low)
    extra = (query_weight, query_bias) if first else carried
    results = (narrow,) * first + (wide,) * (2 if final else 3)
    return pl.pallas_call(
        functools.partial(forward_kernel, numbers, first, final),
        out_shape=(narrow,) * (2 * count) + results,
        grid_spec=pltpu.PrefetchScalarGridSpec(
            num_scalar_prefetch=1,
            grid=(PAIRS,),
            in_specs=[whole] * count
            + [column(D, 0), column(D, 1), column(1, 0)]
            + ([column(D, 0), column(1, 0)] if first else [column(rows, 0)] * 4),
            out_specs=[column(rows, 0)] * (2 * count + len(results)),
        ),
        compiler_params=pltpu.CompilerParams(vmem_limit_bytes=VMEM_LIMIT),
        cost_estimate=SMALL_COST,
        name="attend_forward",
    )(scalars, *chunks, pair_weight, pair_weight, value_bias, *extra)


def backward_kernel(
    number,
    first,
    last,
    folds,
    scalars,
    q_ref,
    k_ref,
    v_ref,
    g_ref,
    log_ref,
    delta_ref,
    wk_ref,
    wv_ref,
    *refs
):
    if last:
        wq_ref = refs[0]
        refs = refs[1:]
    if not first:
        dq_in = refs[0]
        refs = refs[1:]
    count = len(folds)
    fold_ins, refs = refs[: 2 * count], refs[2 * count :]
    dq_ref, dk_ref, dv_ref, back_ref = refs[:4]
    fold_outs, accum = refs[4:-1], refs[-1]
    step = pl.program_id(0)
    for n, (lead, bit, at) in enumerate(folds):

        @pl.when(step < lead)
        def _():
            fold_block(
                *fold_ins[2 * n : 2 * n + 2], *fold_outs[2 * n : 2 * n + 2], bit, at
            )

    rows = q_ref.shape[0]
    keys = k_ref.shape[0]
    limit = scalars[4] - scalars[number] * keys
    q_pair = q_ref[...]
    g_pair = g_ref[...]
    k_pair = k_ref[...]
    v_pair = v_ref[...]
    lower = first_half((rows, PAIR))
    nothing = jnp.zeros((rows, PAIR), low)
    two_halves = lambda pair: jnp.concatenate(
        [jnp.where(lower, pair, nothing), jnp.where(lower, nothing, pair)]
    )
    queries = two_halves(q_pair)
    grads_out = two_halves(g_pair)
    row_of = lambda ref: jnp.concatenate([ref[0, 0:1, :], ref[0, 1:2, :]], axis=1)
    place = lax.broadcasted_iota(jnp.int32, (keys, 1), 0)
    bias = jnp.where(place < limit, 0.0, far_below)
    scores = dot_of(k_pair, queries, 1, 1) + bias
    prob_grad = dot_of(v_pair, grads_out, 1, 1)
    probs = jnp.exp(scores - row_of(log_ref))
    score_grad = (probs * (prob_grad - row_of(delta_ref))).astype(low)
    dv_low = dot_of(probs.astype(low), grads_out, 1, 0).astype(low)
    dk_low = dot_of(score_grad, queries, 1, 0).astype(low)
    turned = dot_of(k_pair.T, score_grad, 1, 0)
    upper_rows = lax.broadcasted_iota(jnp.int32, (PAIR, rows), 0) < HEAD_DIM
    dk_ref[...] = dk_low
    dv_ref[...] = dv_low
    grads = [dk_low, dv_low]
    weights = [wk_ref[...], wv_ref[...]]
    dq_all = jnp.where(upper_rows, turned[:, :rows], turned[:, rows:]).T
    if not first:
        dq_all = dq_all + dq_in[...]
    back = dot_of(jnp.concatenate(grads, axis=1), jnp.concatenate(weights, axis=1), 1, 1)
    if last:
        dq_low = (dq_all * score_scale).astype(low)
        dq_ref[...] = dq_low
        back = back + dot_of(dq_low, wq_ref[...], 1, 1)
    else:
        dq_ref[...] = dq_all

    @pl.when(step == 0)
    def _():
        accum[...] = back

    @pl.when(step > 0)
    def _():
        accum[...] += back

    @pl.when(step == PAIRS - 1)
    def _():
        back_ref[...] = accum[...].astype(back_ref.dtype)


def attend_backward(
    number,
    queries,
    keys,
    values,
    grads,
    logs,
    deltas,
    query_weight,
    pair_weight,
    scalars,
    carried,
    last,
    pairs,
    bits,
    places,
):
    rows, total = queries.shape[0], keys.shape[0]
    first = carried is None
    folds = [(keep.shape[0], bit, at) for (keep, _), bit, at in zip(pairs, bits, places)]
    halves = [
        (keep.shape[0], keep.shape[1] // 2) + keep.shape[2:] for keep, _ in pairs for _ in range(2)
    ]

    def by_lead(shape):
        end = shape[0] - 1
        return pl.BlockSpec((1,) + shape[1:], lambda i, n: (jnp.minimum(i, end), 0, 0, 0))

    column = lambda count, c: pl.BlockSpec((count, PAIR), lambda i, n: (0, c * PAIRS + i))
    stats = pl.BlockSpec((1, 2, rows), lambda i, n: (i, 0, 0))
    extra = (query_weight,) * last + (() if first else (carried,))
    extra_specs = [column(D, 0)] * last + ([] if first else [column(rows, 0)])
    return pl.pallas_call(
        functools.partial(backward_kernel, number, first, last, folds),
        out_shape=(
            jax.ShapeDtypeStruct((rows, D), low if last else full),
            jax.ShapeDtypeStruct((total, D), low),
            jax.ShapeDtypeStruct((total, D), low),
            jax.ShapeDtypeStruct((total, D), low if first else full),
            *[jax.ShapeDtypeStruct(shape, low) for shape in halves],
        ),
        grid_spec=pltpu.PrefetchScalarGridSpec(
            num_scalar_prefetch=1,
            grid=(PAIRS,),
            in_specs=[
                column(rows, 0),
                column(total, 0),
                column(total, 0),
                column(rows, 0),
                stats,
                stats,
                column(D, 0),
                column(D, 1),
            ]
            + extra_specs
            + [by_lead(value.shape) for pair in pairs for value in pair],
            out_specs=[
                column(rows, 0),
                column(total, 0),
                column(total, 0),
                pl.BlockSpec((total, D), lambda i, n: (0, 0)),
            ]
            + [by_lead(shape) for shape in halves],
            scratch_shapes=[pltpu.VMEM((total, D), full)],
        ),
        compiler_params=pltpu.CompilerParams(vmem_limit_bytes=VMEM_LIMIT),
        cost_estimate=SMALL_COST,
        name="attend_backward",
    )(
        scalars,
        queries,
        keys,
        values,
        grads,
        logs,
        deltas,
        pair_weight,
        pair_weight,
        *extra,
        *[value for pair in pairs for value in pair],
    )


def swap(value, axis, bit):
    count = lax.axis_size(axis)
    return lax.ppermute(value, axis, [(i, i ^ bit) for i in range(count)])


class Order:
    def __init__(self):
        self.marks = ()

    def __call__(self, *values):
        values = lax.optimization_barrier(values + self.marks)[: len(values)]
        self.marks = values
        return values[0] if len(values) == 1 else values


def outer_bits():
    bits = []
    bit = 2
    while bit < lax.axis_size("dp"):
        bits.append(bit)
        bit *= 2
    return bits


class Gather:
    def __init__(self, parts):
        self.bits = outer_bits()
        half = len(self.bits) // 2
        self.orders = [
            self.bits[half * (n % 2) :] + self.bits[: half * (n % 2)] for n in range(len(parts))
        ]
        self.result = [[([0], part)] for part in parts]
        self.step = 0
        self.early = []

    def advance(self, order):
        held = self.result
        if self.step < len(self.bits):
            masks = [[m for mask, _ in pieces for m in mask] for pieces in held]
            blocks = [
                jnp.concatenate([array for _, array in pieces]) if self.step else pieces[0][1]
                for pieces in held
            ]
            blocks = order(*blocks)
            bits = [turn[self.step] for turn in self.orders]
            self.result = [
                [(mask, block), ([m ^ bit for m in mask], swap(block, "dp", bit))]
                for mask, block, bit in zip(masks, blocks, bits)
            ]
        else:
            rest = [pieces[1:] if self.early else pieces for pieces in held]
            arrays = iter(order(*[array for pieces in rest for _, array in pieces]))
            self.result = []
            for n, pieces in enumerate(rest):
                kept = [(masks, next(arrays)) for masks, _ in pieces]
                ours = held[n][:1] + kept if self.early else kept
                theirs = [([m ^ 1 for m in masks], swap(array, "dp", 1)) for masks, array in kept]
                self.result.append(ours + self.early[n : n + 1] + theirs)
        self.step += 1

    def send_early(self, order):
        arrays = order(*[pieces[0][1] for pieces in self.result])
        self.early = [
            ([m ^ 1 for m in pieces[0][0]], swap(array, "dp", 1))
            for pieces, array in zip(self.result, arrays)
        ]


def canonical_row(me, rank, block, mask, rank_mask, stride, offset):
    if mask is None:
        return offset
    row = (me ^ mask) * block + offset
    if stride:
        if rank_mask >= 2:
            rank_mask = rank_mask ^ ((rank + 1) // 2 % 2)
        row = row + (rank ^ rank_mask) * stride
    return pl.multiple_of(row, 16)


def place_kernel(plan, block, *refs):
    count = len(plan)
    ins = refs[:count]
    outs = refs[count:-1]
    sems = refs[-1]
    me = lax.axis_index("dp")
    rank = lax.axis_index("mp")
    copies = []
    for ref, moves in zip(ins, plan):
        for start, size, which, mask, column, _, offset in moves:
            row = canonical_row(me, rank, block, mask, 0, 0, offset)
            copy = pltpu.make_async_copy(
                ref.at[pl.ds(start, size), :],
                outs[which].at[pl.ds(row, size), pl.ds(column * D, D)],
                sems.at[len(copies)],
            )
            copy.start()
            copies.append(copy)
    for copy in copies:
        copy.wait()


def plan_of(gathered, layouts):
    arrays = []
    plan = []
    for pieces, layout in zip(gathered, layouts):
        rows = sum(size for _, size, *_ in layout)
        for masks, array in pieces:
            moves = []
            for j, mask in enumerate(masks):
                for start, size, which, rank_mask, stride, offset in layout:
                    moves.append((j * rows + start, size, which, mask, rank_mask, stride, offset))
            arrays.append(array)
            plan.append(moves)
    return arrays, plan


def place(arrays, plan, block, shapes):
    return pl.pallas_call(
        functools.partial(place_kernel, plan, block),
        out_shape=[jax.ShapeDtypeStruct(shape, low) for shape in shapes],
        in_specs=[pl.BlockSpec(memory_space=pl.ANY)] * len(arrays),
        out_specs=[pl.BlockSpec(memory_space=pltpu.VMEM)] * len(shapes),
        scratch_shapes=[pltpu.SemaphoreType.DMA((sum(len(moves) for moves in plan),))],
        compiler_params=pltpu.CompilerParams(vmem_limit_bytes=VMEM_LIMIT),
        cost_estimate=SMALL_COST,
        name="place",
    )(*arrays)


def store_split(value, keep, send, index, start=0):
    block = keep.shape[2]
    even = lax.axis_index("dp") % 2 == 0
    for outer in range(value.shape[0] // (2 * block)):
        first = value[2 * outer * block : (2 * outer + 1) * block]
        other = value[(2 * outer + 1) * block : (2 * outer + 2) * block]
        keep[index, start + outer] = jnp.where(even, first, other).astype(low)
        send[index, start + outer] = jnp.where(even, other, first).astype(low)


def middle_kernel(plan, block, total, *refs):
    limit_ref, vector_ref = refs[:2]
    token_hbm, mixed_hbm, log_hbm, cot_hbm, teach_hbm = refs[2:7]
    pieces = refs[7 : 7 + total]
    (
        out_hbm,
        middle_hbm,
        grad_hbm,
        down_keep,
        down_send,
        up_keep,
        up_send,
        delta_ref,
        log_ref,
        sum_ref,
    ) = refs[7 + total : 17 + total]
    (
        token,
        mixed,
        logs,
        cot,
        teach,
        up,
        down,
        proj,
        right,
        slope,
        second,
        middle,
        final,
        out,
        final_low,
        middle_low,
        grad,
        accum,
        turned,
        stage_keep,
        stage_send,
        in_sems,
        weight_sems,
        out_sems,
        keep_sems,
        send_sems,
    ) = refs[17 + total :]
    hidden = FF // D
    targets = (up, down, proj)
    rows = token.shape[0]
    me = lax.axis_index("dp")
    rank = lax.axis_index("mp")

    def fetch(ref, scratch, n):
        copy = pltpu.make_async_copy(ref, scratch, in_sems.at[n])
        copy.start()
        return copy

    def send(scratch, ref, n):
        copy = pltpu.make_async_copy(scratch, ref, out_sems.at[n])
        copy.start()
        return copy

    gets = [
        fetch(token_hbm, token, 0),
        fetch(mixed_hbm, mixed, 1),
        fetch(log_hbm, logs, 2),
        fetch(cot_hbm, cot, 3),
        fetch(teach_hbm, teach, 4),
    ]
    loads = {0: [], 1: [], 2: []}
    number = 0
    for want in (2, 0, 1):
        for ref, moves in zip(pieces, plan):
            for start, size, which, mask, rank_mask, stride, offset in moves:
                if which != want:
                    continue
                row = canonical_row(me, rank, block, mask, rank_mask, stride, offset)
                copy = pltpu.make_async_copy(
                    ref.at[pl.ds(start, size), :],
                    targets[which].at[pl.ds(row, size), :],
                    weight_sems.at[number],
                )
                copy.start()
                loads[which].append(copy)
                number += 1

    table_row = vector_ref[0:1, :]
    out_bias = vector_ref[1:2, :]
    gain = vector_ref[2:3, :]
    shift = vector_ref[3:4, :]
    down_bias = vector_ref[4:5, :]
    weight = vector_ref[5:6, :]
    gets[0].wait()
    gets[1].wait()
    right[2 * hidden] = mixed[...].astype(low)
    for copy in loads[2]:
        copy.wait()
    state = token[...].astype(full) + table_row + out_bias
    state = state + dot_of(right[2 * hidden], proj[...], 1, 1)
    middle[...] = state
    unit, _ = norm_stats(state)
    second[...] = (unit * gain + shift).astype(low)
    accum[...] = jnp.zeros((rows, D), full)
    for copy in loads[0]:
        copy.wait()
    for copy in loads[1]:
        copy.wait()

    def forward(m, _):
        place = pl.ds(pl.multiple_of(m * D, D), D)
        half = rows // 2
        spans = [pl.ds(part * half, half) for part in range(2)]
        values = [
            dot_of(second[span, :], up[place, :], 1, 0) + vector_ref[pl.ds(8 + m, 1), :]
            for span in spans
        ]
        for span, value in zip(spans, values):
            cumulative = 0.5 + 0.5 * lax.erf(value * (0.5**0.5))
            active = (value * cumulative).astype(low)
            right[m, span, :] = active
            slope[m, span, :] = (
                cumulative + value * jnp.exp(-0.5 * value * value) * 0.3989422804014327
            )
            accum[span, :] += dot_of(active, down[place, :], 1, 1)
        return 0

    lax.fori_loop(0, FF // D, forward, 0)
    final_state = middle[...] + accum[...] + down_bias
    out[...] = final_state.astype(low)
    puts = [send(out, out_hbm, 0)]
    gets[3].wait()
    gets[4].wait()
    place = lax.broadcasted_iota(jnp.int32, (rows, 1), 0)
    grads = cot[...].astype(full) + weight * (final_state - teach[...].astype(full))
    grads = jnp.where(place < limit_ref[5], grads, 0.0)
    final[...] = grads
    final_low[...] = grads.astype(low)
    sum_ref[3:4, :] = jnp.sum(grads, axis=0, keepdims=True)
    accum[...] = jnp.zeros((rows, D), full)

    def backward(m, _):
        place = pl.ds(pl.multiple_of(m * D, D), D)
        half = rows // 2
        spans = [pl.ds(part * half, half) for part in range(2)]
        values = [dot_of(final_low[span, :], down[place, :], 1, 0) for span in spans]
        sums = []
        for span, value in zip(spans, values):
            value = (slope[m, span, :] * value).astype(low)
            right[hidden + m, span, :] = value
            sums.append(jnp.sum(value.astype(full), axis=0, keepdims=True))
            accum[span, :] += dot_of(value, up[place, :], 1, 1)
        sum_ref[pl.ds(8 + m, 1), :] = sums[0] + sums[1]
        return 0

    lax.fori_loop(0, FF // D, backward, 0)
    unit, inverse = norm_stats(middle[...])
    second_grad = accum[...]
    sum_ref[0:1, :] = jnp.sum(second_grad * unit, axis=0, keepdims=True)
    sum_ref[1:2, :] = jnp.sum(second_grad, axis=0, keepdims=True)
    scaled = second_grad * gain
    mean_scaled = jnp.mean(scaled, axis=-1, keepdims=True)
    mean_unit = jnp.mean(scaled * unit, axis=-1, keepdims=True)
    total_grad = final[...] + inverse * (scaled - mean_scaled - unit * mean_unit)
    middle[...] = total_grad
    puts.append(send(middle, middle_hbm, 1))
    middle_low[...] = total_grad.astype(low)
    sum_ref[2:3, :] = jnp.sum(total_grad, axis=0, keepdims=True)
    attended_grad = dot_of(middle_low[...], proj[...], 1, 0).astype(low)
    grad[...] = attended_grad
    puts.append(send(grad, grad_hbm, 2))
    gets[2].wait()
    head = lax.broadcasted_iota(jnp.int32, (16, D), 0)
    lane = lax.broadcasted_iota(jnp.int32, (16, D), 1)
    member = jnp.where(lane // HEAD_DIM == head, 1.0, 0.0)
    leader = jnp.where(lane == head * HEAD_DIM, 1.0, 0.0)
    exact = functools.partial(
        lax.dot_general,
        dimension_numbers=(((1,), (1,)), ((), ())),
        precision=lax.Precision.HIGHEST,
        preferred_element_type=full,
    )
    deltas = exact(member, attended_grad.astype(full) * mixed[...])
    tops = exact(leader, logs[...])
    for pair in range(PAIRS):
        delta_ref[pair] = deltas[2 * pair : 2 * pair + 2]
        log_ref[pair] = tops[2 * pair : 2 * pair + 2]
    turned[0] = final_low[...].T
    turned[1] = second[...].T
    turned[2] = middle_low[...].T

    def weights(i, _):
        half = D // 2
        values = [
            dot_of(turned[i // hidden, part * half : (part + 1) * half, :], right[i], 1, 0)
            for part in range(2)
        ]
        for part, value in enumerate(values):
            store_split(value, stage_keep, stage_send, i, part * stage_keep.shape[1] // 2)

        @pl.when(i < hidden)
        def _():
            pltpu.make_async_copy(stage_keep.at[i], down_keep.at[i], keep_sems.at[i]).start()
            pltpu.make_async_copy(stage_send.at[i], down_send.at[i], send_sems.at[i]).start()

        @pl.when(i >= hidden)
        def _():
            row = i - hidden
            pltpu.make_async_copy(stage_keep.at[i], up_keep.at[row], keep_sems.at[i]).start()
            pltpu.make_async_copy(stage_send.at[i], up_send.at[row], send_sems.at[i]).start()

        return 0

    lax.fori_loop(0, 2 * hidden + 1, weights, 0)
    for copy in puts:
        copy.wait()
    for i in range(2 * hidden + 1):
        if i < hidden:
            keep, gone, row = down_keep, down_send, i
        else:
            keep, gone, row = up_keep, up_send, i - hidden
        pltpu.make_async_copy(stage_keep.at[i], keep.at[row], keep_sems.at[i]).wait()
        pltpu.make_async_copy(stage_send.at[i], gone.at[row], send_sems.at[i]).wait()


def middle_call(limit, vectors, tokens, mixed, logs, cot, teach, arrays, plan, block, dp):
    rows = tokens.shape[0]
    hidden = FF // D
    narrow = jax.ShapeDtypeStruct((rows, D), low)
    wide = jax.ShapeDtypeStruct((rows, D), full)
    shape = (dp // 2, D // dp, D)
    parts = [jax.ShapeDtypeStruct((count,) + shape, low) for count in (hidden, hidden + 1)]
    stats = jax.ShapeDtypeStruct((PAIRS, 2, rows), full)
    anywhere = pl.BlockSpec(memory_space=pl.ANY)
    inside = pl.BlockSpec(memory_space=pltpu.VMEM)
    moves = sum(len(part) for part in plan)
    return pl.pallas_call(
        functools.partial(middle_kernel, plan, block, len(arrays)),
        out_shape=(
            narrow,
            wide,
            narrow,
            parts[0],
            parts[0],
            parts[1],
            parts[1],
            stats,
            stats,
            jax.ShapeDtypeStruct((8 + 8, D), full),
        ),
        in_specs=[pl.BlockSpec(memory_space=pltpu.SMEM), inside]
        + [anywhere] * (5 + len(arrays)),
        out_specs=[anywhere] * 7 + [inside] * 3,
        scratch_shapes=[
            pltpu.VMEM((rows, D), low),
            pltpu.VMEM((rows, D), full),
            pltpu.VMEM((rows, D), full),
            pltpu.VMEM((rows, D), low),
            pltpu.VMEM((rows, D), low),
            pltpu.VMEM((FF, D), low),
            pltpu.VMEM((FF, D), low),
            pltpu.VMEM((D, D), low),
            pltpu.VMEM((2 * hidden + 1, rows, D), low),
            pltpu.VMEM((hidden, rows, D), full),
            pltpu.VMEM((rows, D), low),
            pltpu.VMEM((rows, D), full),
            pltpu.VMEM((rows, D), full),
            pltpu.VMEM((rows, D), low),
            pltpu.VMEM((rows, D), low),
            pltpu.VMEM((rows, D), low),
            pltpu.VMEM((rows, D), low),
            pltpu.VMEM((rows, D), full),
            pltpu.VMEM((3, D, rows), low),
            pltpu.VMEM((2 * hidden + 1,) + shape, low),
            pltpu.VMEM((2 * hidden + 1,) + shape, low),
            pltpu.SemaphoreType.DMA((5,)),
            pltpu.SemaphoreType.DMA((moves,)),
            pltpu.SemaphoreType.DMA((3,)),
            pltpu.SemaphoreType.DMA((2 * hidden + 1,)),
            pltpu.SemaphoreType.DMA((2 * hidden + 1,)),
        ],
        compiler_params=pltpu.CompilerParams(vmem_limit_bytes=VMEM_LIMIT),
        cost_estimate=SMALL_COST,
        name="middle",
    )(limit, vectors, tokens, mixed, logs, cot, teach, *arrays)


def fold_block(keep, got, out_keep, out_send, bit, place):
    step = 1 << place
    mine = (lax.axis_index("dp") // bit) % 2 * step
    for j in range(keep.shape[1] // 2):
        base = (j // step) * 2 * step + j % step
        for out, shift in ((out_keep, mine), (out_send, step - mine)):
            value = keep[0, base + shift].astype(full) + got[0, base + shift].astype(full)
            out[0, j] = value.astype(low)


def fold_kernel(bits, places, *refs):
    count = len(bits)
    for n in range(count):
        fold_block(
            *refs[2 * n : 2 * n + 2],
            *refs[2 * count + 2 * n : 2 * count + 2 * n + 2],
            bits[n],
            places[n],
        )


def fold(pairs, bits, places):
    lead = pairs[0][0].shape[0]
    block = lambda shape: pl.BlockSpec((1,) + shape[1:], lambda i: (i, 0, 0, 0))
    halves = [
        (keep.shape[0], keep.shape[1] // 2) + keep.shape[2:] for keep, _ in pairs for _ in range(2)
    ]
    outs = pl.pallas_call(
        functools.partial(fold_kernel, bits, places),
        out_shape=[jax.ShapeDtypeStruct(shape, low) for shape in halves],
        grid=(lead,),
        in_specs=[block(value.shape) for pair in pairs for value in pair],
        out_specs=[block(shape) for shape in halves],
        compiler_params=pltpu.CompilerParams(vmem_limit_bytes=VMEM_LIMIT),
        cost_estimate=pl.CostEstimate(flops=0, bytes_accessed=16 << 20, transcendentals=0),
        name="fold",
    )(*[value for pair in pairs for value in pair])
    return [(outs[2 * n], outs[2 * n + 1]) for n in range(len(pairs))]


def qkv_grad_kernel(count, *refs):
    sources = refs[: 3 * count + 1]
    outs = refs[3 * count + 1 : 3 * count + 5]
    sum_ref, held, turned, total, stage, in_sems, out_sems = refs[3 * count + 5 :]
    first_use = [0, count] + list(range(1, count)) + list(range(count + 1, 3 * count + 1))
    for n in first_use:
        pltpu.make_async_copy(sources[n], held.at[n], in_sems.at[n]).start()

    def wait(n):
        pltpu.make_async_copy(sources[0], held.at[n], in_sems.at[n]).wait()

    def turn(n, _):
        wait(n)
        turned[n] = held[n].T
        return 0

    lax.fori_loop(0, count, turn, 0)
    sum_ref[...] = jnp.zeros_like(sum_ref)

    def step(i, _):
        c = (i + count - 1) // count
        n = jnp.where(i == 0, 0, (i + count - 1) % count)
        wait(count + i)
        right = held[count + i]
        value = dot_of(turned[n], right, 1, 0)
        total[...] = value + jnp.where(n == 0, jnp.zeros_like(value), total[...])

        @pl.when(c != 1)
        def _():
            row = pl.ds(pl.multiple_of(c * 4, 8), 1)
            sum_ref[row, :] += jnp.sum(right.astype(full), axis=0, keepdims=True)

        @pl.when(i % count == 0)
        def _():
            for part in range(2):
                store_split(
                    total[:, part * D // 2 : (part + 1) * D // 2],
                    stage.at[part],
                    stage.at[2 + part],
                    c,
                )
            for k in range(4):
                pltpu.make_async_copy(
                    stage.at[k, c], outs[k].at[c], out_sems.at[k * 3 + c]
                ).start()

        return 0

    lax.fori_loop(0, 2 * count + 1, step, 0)
    for k in range(4):
        for c in range(3):
            pltpu.make_async_copy(stage.at[k, c], outs[k].at[c], out_sems.at[k * 3 + c]).wait()


def qkv_grads(chunks, query_grad, key_grads, value_grads, dp):
    rows = query_grad.shape[0]
    count = len(chunks)
    shape = (3, dp // 2, D // dp, D // 2)
    anywhere = pl.BlockSpec(memory_space=pl.ANY)
    return pl.pallas_call(
        functools.partial(qkv_grad_kernel, count),
        out_shape=[jax.ShapeDtypeStruct(shape, low)] * 4
        + [jax.ShapeDtypeStruct((16, D), full)],
        in_specs=[anywhere] * (3 * count + 1),
        out_specs=[anywhere] * 4 + [pl.BlockSpec(memory_space=pltpu.VMEM)],
        scratch_shapes=[
            pltpu.VMEM((3 * count + 1, rows, D), low),
            pltpu.VMEM((count, D, rows), low),
            pltpu.VMEM((D, D), full),
            pltpu.VMEM((4,) + shape, low),
            pltpu.SemaphoreType.DMA((3 * count + 1,)),
            pltpu.SemaphoreType.DMA((12,)),
        ],
        compiler_params=pltpu.CompilerParams(vmem_limit_bytes=VMEM_LIMIT),
        cost_estimate=SMALL_COST,
        name="qkv_grads",
    )(*chunks, query_grad, *key_grads, *value_grads)


def last_kernel(
    token_ref,
    first_ref,
    right_ref,
    left_ref,
    middle_ref,
    vector_ref,
    gain_ref,
    bias_ref,
    sum_ref,
    out_ref,
    pack_ref,
):
    @pl.when(pl.program_id(0) == 0)
    def _():
        pack_ref[...] = jnp.zeros_like(pack_ref)
        pack_ref[1:2, :] = sum_ref[0:1, :]
        pack_ref[3:4, :] = sum_ref[1:2, :]
        pack_ref[4:5, :] = bias_ref[0:1, :]
        pack_ref[5:6, :] = bias_ref[8:9, :]
        pack_ref[6:8, :] = sum_ref[2:4, :]
        pack_ref[8 : 8 + FF // D, :] = sum_ref[8 : 8 + FF // D, :]

    unit, inverse = norm_stats(token_ref[...].astype(full) + vector_ref[0:1, :])
    grad = first_ref[...] + right_ref[...].astype(full) + left_ref[...].astype(full)
    scaled = grad * gain_ref[0:1, :]
    mean_scaled = jnp.mean(scaled, axis=-1, keepdims=True)
    mean_unit = jnp.mean(scaled * unit, axis=-1, keepdims=True)
    result = middle_ref[...] + inverse * (scaled - mean_scaled - unit * mean_unit)
    out_ref[...] = result
    pack_ref[0:1, :] += jnp.sum(grad * unit, axis=0, keepdims=True)
    pack_ref[2:3, :] += jnp.sum(grad, axis=0, keepdims=True)
    pack_ref[pl.ds(16 + lax.axis_index("dp"), 1), :] += jnp.sum(result, axis=0, keepdims=True)


def last_norm(tokens, first, right, left, middle_grad, vectors, gains, bias_sums, sums, dp):
    rows = tokens.shape[0]
    part = pl.BlockSpec((rows // 4, D), lambda i: (i, 0))
    whole = lambda value: pl.BlockSpec(value.shape, lambda i: (0, 0))
    small = (vectors, gains, bias_sums, sums)
    return pl.pallas_call(
        last_kernel,
        out_shape=(
            jax.ShapeDtypeStruct((rows, D), full),
            jax.ShapeDtypeStruct((16 + dp, D), full),
        ),
        grid=(4,),
        in_specs=[part] * 5 + [whole(value) for value in small],
        out_specs=[part, pl.BlockSpec((16 + dp, D), lambda i: (0, 0))],
        compiler_params=pltpu.CompilerParams(vmem_limit_bytes=VMEM_LIMIT),
        cost_estimate=SMALL_COST,
        name="last_norm",
    )(tokens, first, right, left, middle_grad, *small)


def two_parts(value, axis, mine):
    keep = lax.dynamic_index_in_dim(value, mine, axis, keepdims=False)
    send = lax.dynamic_index_in_dim(value, 1 - mine, axis, keepdims=False)
    return keep, send.astype(low)


class Scatter:
    def __init__(self, parts, turns):
        self.bits = outer_bits()
        half = len(self.bits) // 2
        self.orders = [
            [1] + self.bits[half * (turn % 2) :] + self.bits[: half * (turn % 2)] for turn in turns
        ]
        self.left = [list(self.bits) for _ in turns]
        self.step = 0
        self.parts = parts

    def sends(self):
        return [send for _, send in self.parts]

    def exchange(self, sends):
        self.pairs = [
            (keep, swap(send, "dp", turn[self.step]))
            for (keep, _), send, turn in zip(self.parts, sends, self.orders)
        ]
        self.step += 1

    def folds(self):
        if self.step > len(self.bits):
            return [], [], []
        bits = [turn[self.step] for turn in self.orders]
        places = []
        for left, bit in zip(self.left, bits):
            places.append(left.index(bit))
            left.remove(bit)
        return self.pairs, bits, places

    def give(self, outs):
        self.parts = [(outs[n], outs[n + 1]) for n in range(0, len(outs), 2)]

    def fold(self):
        outs = []
        for pair, bit, at in zip(*self.folds()):
            outs += fold([pair], [bit], [at])[0]
        self.give(outs)

    def advance(self, order):
        sends = order(*self.sends())
        self.exchange(list(sends) if len(self.parts) > 1 else [sends])

    def finish(self, order):
        while self.step <= len(self.bits):
            self.fold()
            self.advance(order)
        got = order(*[other for _, other in self.pairs])
        return [
            (keep.astype(full) + other.astype(full))[:, 0]
            for (keep, _), other in zip(self.pairs, got)
        ]


def scatter_dp(parts, turns):
    scatter = Scatter(parts, turns)
    while True:
        sends = yield scatter.sends()
        scatter.exchange(sends)
        if scatter.step > len(scatter.bits):
            break
        scatter.parts = fold(*scatter.folds())
    got = yield [other for _, other in scatter.pairs]
    return [
        (keep.astype(full) + other.astype(full))[:, 0]
        for (keep, _), other in zip(scatter.pairs, got)
    ]


def scatter_mp(value):
    rank = lax.axis_index("mp")
    part = lambda index: lax.dynamic_index_in_dim(value, index, keepdims=False)
    sends = yield [part(rank ^ bit).astype(low) for bit in (1, 2, 3)]
    got = yield [swap(send, "mp", bit) for bit, send in zip((1, 2, 3), sends)]
    got = [other.astype(full) for other in got]
    return (part(rank) + got[0]) + (got[1] + got[2])


def halve_mp(value):
    rank = lax.axis_index("mp")
    pairs = value.reshape((2, 2) + value.shape[1:])
    keep, send = two_parts(pairs, 1, rank % 2)
    (send,) = yield [send]
    (got,) = yield [swap(send, "mp", 1)]
    keep, send = two_parts(keep.astype(full) + got.astype(full), 0, rank // 2)
    (send,) = yield [send]
    (got,) = yield [swap(send, "mp", 2)]
    return keep + got.astype(full)


def scatter_feed(up_own, down_own):
    mp = lax.axis_size("mp")
    block = down_own.shape[1]
    out_own = up_own[mp].reshape(block, mp, -1).transpose(1, 0, 2)
    own = yield from halve_mp(
        jnp.concatenate([up_own[:mp], down_own, out_own.reshape(mp, -1, D)], axis=1)
    )
    return own[:block], own[block : 2 * block].T, own[2 * block :].reshape(block, -1).T


def scatter_qkv(keep_left, keep_right, send_left, send_right):
    left_part, right_part = yield from scatter_dp(
        [(keep_left, send_left), (keep_right, send_right)], (0, 1)
    )
    width = D // lax.axis_size("mp")
    parts = [part[..., at : at + width] for part in (left_part, right_part) for at in (0, width)]
    return (yield from scatter_mp(jnp.stack(parts)))


def sum_small(value):
    (value,) = yield [value]
    value = value + swap(value, "dp", 1)
    bits = outer_bits()
    groups = [("dp", bits[n : n + 2]) for n in range(0, len(bits), 2)] + [("mp", [1, 2])]
    for axis, pair in groups:
        (value,) = yield [value]
        if len(pair) == 1:
            value = value + swap(value, axis, pair[0])
        else:
            one, two = pair
            got = [swap(value, axis, mask) for mask in (one, two, one + two)]
            if axis == "mp":
                got = yield got
            value = (value + got[0]) + (got[1] + got[2])
    return value


class Steps:
    def __init__(self, steps):
        self.steps = steps
        self.pending = next(steps)
        self.result = None

    def advance(self, order):
        if self.pending is None:
            return
        sends = order(*self.pending)
        sends = [sends] if len(self.pending) == 1 else list(sends)
        try:
            self.pending = self.steps.send(sends)
        except StopIteration as stop:
            self.pending = None
            self.result = stop.value

    def finish(self, order):
        while self.pending is not None:
            self.advance(order)
        return self.result


def shards(
    tokens_in,
    timesteps,
    lengths,
    time_table,
    norm_gains,
    norm_biases,
    w_qkv,
    qv_bias,
    w_out,
    out_bias,
    w_up,
    up_bias,
    w_down,
    down_bias,
    cotangent,
    teacher,
):
    rank = lax.axis_index("mp")
    data_rank = lax.axis_index("dp")
    mp = lax.axis_size("mp")
    dp = lax.axis_size("dp")
    own_rows = tokens_in.shape[0]
    length = lax.dynamic_index_in_dim(lengths, data_rank, keepdims=False)
    own_time = lax.dynamic_index_in_dim(timesteps, data_rank, keepdims=False)
    odd = rank % 2 == 1
    upper = rank >= 2
    middle = jnp.logical_or(rank == 1, rank == 2)
    order = Order()
    along = lambda value, pairs: lax.ppermute(value, "mp", pairs)

    block = w_qkv.shape[1]
    aligned = block % 32 == 0
    narrow = order(jnp.concatenate([w_qkv.reshape(3 * block, -1), w_out.T]))
    first_swap = swap(narrow, "mp", 1)
    tall = order(jnp.concatenate([w_up, w_down.T]))
    tall_swap = swap(tall, "mp", 1)
    pair = order(
        jnp.concatenate(
            [jnp.where(odd, first_swap, narrow), jnp.where(odd, narrow, first_swap)], axis=1
        )
    )
    second_swap = swap(pair, "mp", 2)
    tokens, lengths, own_time, norm_gains, norm_biases, out_bias, down_bias, up_bias, length = order(
        tokens_in, lengths, own_time, norm_gains, norm_biases, out_bias, down_bias, up_bias, length
    )
    table_row = lax.dynamic_slice_in_dim(time_table, own_time, 1).astype(full)
    unit_one, _ = norm_stats(tokens.astype(full) + table_row)
    first_norm = (unit_one * norm_gains[0] + norm_biases[0]).astype(low)
    loss_weight = lengths.shape[0] * MAXLEN / jnp.sum(lengths).astype(full)
    vectors = jnp.concatenate(
        [
            table_row,
            out_bias[None],
            norm_gains[1:2],
            norm_biases[1:2],
            down_bias[None],
            jnp.full((3, D), loss_weight),
            up_bias.reshape(-1, D),
            jnp.zeros((4, D), full),
        ]
    )
    scalars = jnp.stack(
        [
            rank,
            jnp.where(rank == 0, 1, rank - 1),
            jnp.where(upper, rank - 2, rank + 2),
            jnp.where(middle, rank + 1, 3 - rank),
            length,
            length - rank * own_rows,
        ]
    ).astype(jnp.int32)
    first_norm, vectors, scalars = order(first_norm, vectors, scalars)
    wide = jnp.concatenate(
        [jnp.where(upper, second_swap, pair), jnp.where(upper, pair, second_swap)], axis=1
    )
    qkv_rows, out_rows = wide[: 3 * block], wide[3 * block :]
    if aligned:
        split = 3 * block // 2
        qkv_gather = Gather([qkv_rows[:split], qkv_rows[split:]])
        qkv_gather.advance(order)
    tall = order(jnp.concatenate([tall, tall_swap]))
    tall_across = along(tall, [(1, 2), (2, 1)])

    sent = order(first_norm)
    from_left = along(sent, [(0, 1), (1, 2), (2, 3)])
    from_right = along(sent, [(1, 0), (2, 1), (3, 2)])
    tall_across = order(tall_across)
    tall_far = along(tall_across, [(1, 0), (2, 3)])
    if aligned:
        while qkv_gather.step < len(qkv_gather.bits):
            qkv_gather.advance(order)
        qkv_gather.advance(order)
    hop_right, hop_left = order(from_left, from_right)
    second_right = along(hop_right, [(1, 2), (2, 3)])
    second_left = along(hop_left, [(1, 0), (2, 1)])
    if aligned:
        arrays, plan = plan_of(
            qkv_gather.result,
            [
                [(0, block, 0, 0, 0, 0), (block, split - block, 1, 0, 0, 0)],
                [
                    (0, 2 * block - split, 1, 0, 0, split - block),
                    (2 * block - split, block, 1, 1, 0, 0),
                ],
            ],
        )
        query_weight, pair_weight = order(*place(arrays, plan, block, [(D, D), (D, 2 * D)]))
        tall_other = jnp.where(middle, tall_across, order(tall_far))
        feed_gather = Gather(
            [
                jnp.concatenate([tall, out_rows[: block // 2]]),
                jnp.concatenate([tall_other, out_rows[block // 2 :]]),
            ]
        )
        feed_gather.advance(order)
    else:
        weights = lax.all_gather(qkv_rows.reshape(3, block, D), "dp", axis=1, tiled=True)
        query_weight = weights[0]
        pair_weight = jnp.concatenate([weights[1], weights[2]], axis=1)
    near = jnp.where(rank == 0, hop_left, hop_right)
    attend = lambda parts, numbers, carried: order(
        *attend_forward(
            parts,
            numbers,
            scalars,
            query_weight,
            pair_weight,
            qv_bias[0:1],
            qv_bias[1:2],
            carried,
        )
    )
    key_own, value_own, queries, *state = attend([order(first_norm)], (0,), None)
    second_right, second_left = order(second_right, second_left)
    second = order(jnp.where(upper, second_right, second_left))
    third = along(second, [(1, 0), (2, 3)])
    if aligned:
        while feed_gather.step < len(feed_gather.bits):
            feed_gather.advance(order)
        feed_gather.send_early(order)
    near, second = order(near, second)
    key_near, key_second, value_near, value_second, *state = attend(
        [near, second], (1, 2), (queries, *state)
    )
    last = order(jnp.where(middle, hop_left, order(third)))
    key_last, value_last, mixed, logs = attend([order(last)], (3,), (queries, *state))
    if aligned:
        feed_gather.advance(order)
        layout = lambda masks, shift: [
            (0, block, 0, masks[0], D, 0),
            (block, block, 1, masks[0], D, 0),
            (2 * block, block, 0, masks[1], D, 0),
            (3 * block, block, 1, masks[1], D, 0),
            (4 * block, block // 2, 2, 0, 0, shift),
        ]
        arrays, plan = plan_of(
            feed_gather.result, [layout((0, 1), 0), layout((2, 3), block // 2)]
        )
    else:
        arrays = [
            lax.all_gather(w_up, ("mp", "dp"), axis=0, tiled=True),
            lax.all_gather(w_down.T, ("mp", "dp"), axis=0, tiled=True),
            lax.all_gather(out_rows, "dp", axis=0, tiled=True),
        ]
        plan = [[(0, array.shape[0], n, None, 0, 0, 0)] for n, array in enumerate(arrays)]
    chunks = [first_norm, near, second, last]
    keys = [key_own, key_near, key_second, key_last]
    values = [value_own, value_near, value_second, value_last]

    output, middle_grad, attended_grad, *parts, deltas, log_rows, sums = middle_call(
        scalars, vectors, tokens, mixed, logs, cotangent, teacher, arrays, plan, block, dp
    )
    scatter = Scatter([(parts[0], parts[1]), (parts[2], parts[3])], (1, 0))
    scatter.advance(order)

    key_grads = [None] * 4
    value_grads = [None] * 4
    firsts = [None] * 4
    query_grad = None
    for n in (3, 2, 1, 0):
        pairs, bits, places = scatter.folds() if n % 2 == 0 else ([], [], [])
        query_grad, key_grads[n], value_grads[n], firsts[n], *folded = attend_backward(
            n,
            queries,
            keys[n],
            values[n],
            order(attended_grad),
            log_rows,
            deltas,
            query_weight,
            pair_weight,
            scalars,
            query_grad,
            n == 0,
            pairs,
            bits,
            places,
        )
        firsts[n] = order(firsts[n])
        if folded:
            scatter.give(folded)
        if n == 3:
            back_last = along(firsts[3], [(0, 1), (3, 2)]).astype(full)
        elif n == 2:
            scatter.advance(order)
            payload = order((firsts[2] + back_last).astype(low))
            back_right = along(payload, [(0, 1), (1, 2)]).astype(full)
            back_left = along(payload, [(3, 2), (2, 1)]).astype(full)
        elif n == 1:
            to_right = jnp.where(
                rank == 0, firsts[1], firsts[3].astype(full) + back_right
            ).astype(low)
            to_left = (firsts[1] + back_left).astype(low)
            to_right, to_left = order(to_right, to_left)
            final_right = along(to_right, [(0, 1), (1, 2), (2, 3)])
            final_left = along(to_left, [(3, 2), (2, 1), (1, 0)])
    scatter.advance(order)
    query_grad, final_right, final_left = order(query_grad, final_right, final_left)
    *halves, bias_sums = qkv_grads(chunks, query_grad, key_grads, value_grads, dp)
    qkv = Steps(scatter_qkv(*halves))
    qkv.advance(order)
    down_own, up_own = scatter.finish(order)
    feed = Steps(scatter_feed(up_own, down_own))
    feed.advance(order)
    qkv.advance(order)
    tokens, first_own = order(tokens, firsts[0])
    input_grad, packed = last_norm(
        tokens,
        first_own,
        final_right,
        final_left,
        middle_grad,
        vectors,
        norm_gains,
        bias_sums,
        sums,
        dp,
    )
    packed, input_grad = order(packed, input_grad)
    small = Steps(sum_small(packed))
    feed.advance(order)
    feed.advance(order)
    small.advance(order)
    qkv.advance(order)
    feed.advance(order)
    qkv.advance(order)
    small.advance(order)
    qkv.advance(order)
    small.advance(order)
    total = small.finish(order)
    up_grad, down_grad, out_grad = feed.finish(order)
    qkv_grad = qkv.finish(order)
    fixed = 16
    chosen = (timesteps[None, :] == jnp.arange(time_table.shape[0])[:, None]).astype(full)
    table_grad = lax.dot_general(
        chosen,
        total[fixed:],
        (((1,), (0,)), ((), ())),
        precision=lax.Precision.HIGHEST,
        preferred_element_type=full,
    )
    return (
        output,
        input_grad,
        table_grad,
        total[0:2],
        total[2:4],
        qkv_grad,
        total[4:6],
        out_grad,
        total[6],
        up_grad,
        total[8 : 8 + FF // D].reshape(FF),
        down_grad,
        total[7],
    )


def solution(mesh):
    rows = P(both, None)
    placed = (
        rows,
        P(),
        P(),
        P(),
        P(),
        P(),
        P(None, "dp", "mp"),
        P(),
        P("mp", "dp"),
        P(),
        P("dp", "mp"),
        P(),
        P("mp", "dp"),
        P(),
        rows,
        rows,
    )
    return jax.shard_map(
        shards,
        mesh=mesh,
        in_specs=placed,
        out_specs=(
            rows,
            rows,
            P(),
            P(),
            P(),
            P(None, "dp", "mp"),
            P(),
            P("mp", "dp"),
            P(),
            P("dp", "mp"),
            P(),
            P("mp", "dp"),
            P(),
        ),
        check_vma=False,
    )
```

```python
import functools

import jax
import jax.numpy as jnp
from jax import lax
from jax.experimental import pallas as pl
from jax.experimental.pallas import tpu as pltpu
from jax.sharding import PartitionSpec as P

D = 768
HEADS = 12
HEAD_DIM = 64
FF = 3072
MAXLEN = 2048
PAIR = 2 * HEAD_DIM
PAIRS = HEADS // 2
VMEM_LIMIT = 58 << 20
SMALL_COST = pl.CostEstimate(flops=1 << 20, bytes_accessed=1 << 16, transcendentals=0)

far_below = -1e30
epsilon = 1e-05
score_scale = HEAD_DIM ** (-0.5)
low = jnp.bfloat16
full = jnp.float32
both = ("dp", "mp")


def norm_stats(values):
    center = values - jnp.mean(values, axis=-1, keepdims=True)
    spread = jnp.mean(center * center, axis=-1, keepdims=True)
    inverse = lax.rsqrt(spread + epsilon)
    return center * inverse, inverse


def dot_of(left_side, right_side, left_dim, right_dim):
    return lax.dot_general(
        left_side,
        right_side,
        (((left_dim,), (right_dim,)), ((), ())),
        preferred_element_type=full,
    )


def first_half(shape):
    return lax.broadcasted_iota(jnp.int32, shape, len(shape) - 1) < HEAD_DIM


def forward_kernel(numbers, first, final, scalars, *refs):
    count = len(numbers)
    chunk_refs = refs[:count]
    wk_ref, wv_ref, value_bias_ref = refs[count : count + 3]
    refs = refs[count + 3 :]
    if first:
        wq_ref, query_bias_ref = refs[:2]
        key_outs, value_outs = refs[2 : 2 + count], refs[2 + count : 2 + 2 * count]
        query_out, top_ref, sum_ref, acc_ref = refs[2 + 2 * count :]
        q_pair = (dot_of(chunk_refs[0][...], wq_ref[...], 1, 0) + query_bias_ref[...]).astype(low)
        q_pair = q_pair * jnp.asarray(score_scale, low)
        query_out[...] = q_pair
    else:
        q_ref, top_in, sum_in, acc_in = refs[:4]
        key_outs, value_outs = refs[4 : 4 + count], refs[4 + count : 4 + 2 * count]
        results = refs[4 + 2 * count :]
        q_pair = q_ref[...]
    weight = jnp.concatenate([wk_ref[...], wv_ref[...]], axis=1)
    keys = []
    values = []
    for n in range(count):
        both_parts = dot_of(chunk_refs[n][...], weight, 1, 0)
        keys.append(both_parts[:, :PAIR].astype(low))
        values.append((both_parts[:, PAIR:] + value_bias_ref[...]).astype(low))
        key_outs[n][...] = keys[n]
        value_outs[n][...] = values[n]
    rows = q_pair.shape[0]
    size = keys[0].shape[0]
    place = lax.broadcasted_iota(jnp.int32, (1, size), 1)
    lower = first_half((rows, PAIR))
    parts = []
    for half in range(2):
        kept = lower if half == 0 else jnp.logical_not(lower)
        q_half = jnp.where(kept, q_pair, jnp.zeros_like(q_pair))
        scores = []
        for n in range(count):
            bias = jnp.where(place + scalars[numbers[n]] * size < scalars[4], 0.0, far_below)
            scores.append(dot_of(q_half, keys[n], 1, 1) + bias)
        highest = functools.reduce(
            jnp.maximum, [jnp.max(score, axis=-1, keepdims=True) for score in scores]
        )
        totals = jnp.zeros_like(highest)
        mixed = jnp.zeros((rows, PAIR), full)
        for n in range(count):
            exp_scores = jnp.exp(scores[n] - highest)
            totals = totals + jnp.sum(exp_scores, axis=-1, keepdims=True)
            mixed = mixed + dot_of(exp_scores.astype(low), values[n], 1, 0)
        parts.append((highest, totals, mixed))
    top = jnp.where(lower, parts[0][0], parts[1][0])
    total = jnp.where(lower, parts[0][1], parts[1][1])
    mixed = jnp.where(lower, parts[0][2], parts[1][2])
    if first:
        top_ref[...] = top
        sum_ref[...] = total
        acc_ref[...] = mixed
    else:
        highest = jnp.maximum(top, top_in[...])
        here = jnp.exp(top - highest)
        before = jnp.exp(top_in[...] - highest)
        total = total * here + sum_in[...] * before
        mixed = mixed * here + acc_in[...] * before
        if final:
            results[0][...] = mixed / total
            results[1][...] = highest + jnp.log(total)
        else:
            results[0][...] = highest
            results[1][...] = total
            results[2][...] = mixed


def attend_forward(chunks, numbers, scalars, query_weight, pair_weight, query_bias, value_bias, carried):
    rows = chunks[0].shape[0]
    count = len(chunks)
    first = carried is None
    final = 3 in numbers
    column = lambda height, c: pl.BlockSpec((height, PAIR), lambda i, n: (0, c * PAIRS + i))
    whole = pl.BlockSpec((rows, D), lambda i, n: (0, 0))
    wide = jax.ShapeDtypeStruct((rows, D), full)
    narrow = jax.ShapeDtypeStruct((rows, D), low)
    extra = (query_weight, query_bias) if first else carried
    results = (narrow,) * first + (wide,) * (2 if final else 3)
    return pl.pallas_call(
        functools.partial(forward_kernel, numbers, first, final),
        out_shape=(narrow,) * (2 * count) + results,
        grid_spec=pltpu.PrefetchScalarGridSpec(
            num_scalar_prefetch=1,
            grid=(PAIRS,),
            in_specs=[whole] * count
            + [column(D, 0), column(D, 1), column(1, 0)]
            + ([column(D, 0), column(1, 0)] if first else [column(rows, 0)] * 4),
            out_specs=[column(rows, 0)] * (2 * count + len(results)),
        ),
        compiler_params=pltpu.CompilerParams(vmem_limit_bytes=VMEM_LIMIT),
        cost_estimate=SMALL_COST,
        name="attend_forward",
    )(scalars, *chunks, pair_weight, pair_weight, value_bias, *extra)


def backward_kernel(
    number,
    first,
    last,
    folds,
    scalars,
    q_ref,
    k_ref,
    v_ref,
    g_ref,
    log_ref,
    delta_ref,
    wk_ref,
    wv_ref,
    *refs
):
    if last:
        wq_ref = refs[0]
        refs = refs[1:]
    if not first:
        dq_in = refs[0]
        refs = refs[1:]
    count = len(folds)
    fold_ins, refs = refs[: 2 * count], refs[2 * count :]
    dq_ref, dk_ref, dv_ref, back_ref = refs[:4]
    fold_outs, accum = refs[4:-1], refs[-1]
    step = pl.program_id(0)
    for n, (lead, bit, at) in enumerate(folds):

        @pl.when(step < lead)
        def _():
            fold_block(
                *fold_ins[2 * n : 2 * n + 2], *fold_outs[2 * n : 2 * n + 2], bit, at
            )

    rows = q_ref.shape[0]
    keys = k_ref.shape[0]
    limit = scalars[4] - scalars[number] * keys
    q_pair = q_ref[...]
    g_pair = g_ref[...]
    k_pair = k_ref[...]
    v_pair = v_ref[...]
    lower = first_half((rows, PAIR))
    nothing = jnp.zeros((rows, PAIR), low)
    two_halves = lambda pair: jnp.concatenate(
        [jnp.where(lower, pair, nothing), jnp.where(lower, nothing, pair)]
    )
    queries = two_halves(q_pair)
    grads_out = two_halves(g_pair)
    row_of = lambda ref: jnp.concatenate([ref[0, 0:1, :], ref[0, 1:2, :]], axis=1)
    place = lax.broadcasted_iota(jnp.int32, (keys, 1), 0)
    bias = jnp.where(place < limit, 0.0, far_below)
    scores = dot_of(k_pair, queries, 1, 1) + bias
    prob_grad = dot_of(v_pair, grads_out, 1, 1)
    probs = jnp.exp(scores - row_of(log_ref))
    score_grad = (probs * (prob_grad - row_of(delta_ref))).astype(low)
    dv_low = dot_of(probs.astype(low), grads_out, 1, 0).astype(low)
    dk_low = dot_of(score_grad, queries, 1, 0).astype(low)
    turned = dot_of(k_pair.T, score_grad, 1, 0)
    upper_rows = lax.broadcasted_iota(jnp.int32, (PAIR, rows), 0) < HEAD_DIM
    dk_ref[...] = dk_low
    dv_ref[...] = dv_low
    grads = [dk_low, dv_low]
    weights = [wk_ref[...], wv_ref[...]]
    dq_all = jnp.where(upper_rows, turned[:, :rows], turned[:, rows:]).T
    if not first:
        dq_all = dq_all + dq_in[...]
    back = dot_of(jnp.concatenate(grads, axis=1), jnp.concatenate(weights, axis=1), 1, 1)
    if last:
        dq_low = (dq_all * score_scale).astype(low)
        dq_ref[...] = dq_low
        back = back + dot_of(dq_low, wq_ref[...], 1, 1)
    else:
        dq_ref[...] = dq_all

    @pl.when(step == 0)
    def _():
        accum[...] = back

    @pl.when(step > 0)
    def _():
        accum[...] += back

    @pl.when(step == PAIRS - 1)
    def _():
        back_ref[...] = accum[...].astype(back_ref.dtype)


def attend_backward(
    number,
    queries,
    keys,
    values,
    grads,
    logs,
    deltas,
    query_weight,
    pair_weight,
    scalars,
    carried,
    last,
    pairs,
    bits,
    places,
):
    rows, total = queries.shape[0], keys.shape[0]
    first = carried is None
    folds = [(keep.shape[0], bit, at) for (keep, _), bit, at in zip(pairs, bits, places)]
    halves = [
        (keep.shape[0], keep.shape[1] // 2) + keep.shape[2:] for keep, _ in pairs for _ in range(2)
    ]

    def by_lead(shape):
        end = shape[0] - 1
        return pl.BlockSpec((1,) + shape[1:], lambda i, n: (jnp.minimum(i, end), 0, 0, 0))

    column = lambda count, c: pl.BlockSpec((count, PAIR), lambda i, n: (0, c * PAIRS + i))
    stats = pl.BlockSpec((1, 2, rows), lambda i, n: (i, 0, 0))
    extra = (query_weight,) * last + (() if first else (carried,))
    extra_specs = [column(D, 0)] * last + ([] if first else [column(rows, 0)])
    return pl.pallas_call(
        functools.partial(backward_kernel, number, first, last, folds),
        out_shape=(
            jax.ShapeDtypeStruct((rows, D), low if last else full),
            jax.ShapeDtypeStruct((total, D), low),
            jax.ShapeDtypeStruct((total, D), low),
            jax.ShapeDtypeStruct((total, D), low if first else full),
            *[jax.ShapeDtypeStruct(shape, low) for shape in halves],
        ),
        grid_spec=pltpu.PrefetchScalarGridSpec(
            num_scalar_prefetch=1,
            grid=(PAIRS,),
            in_specs=[
                column(rows, 0),
                column(total, 0),
                column(total, 0),
                column(rows, 0),
                stats,
                stats,
                column(D, 0),
                column(D, 1),
            ]
            + extra_specs
            + [by_lead(value.shape) for pair in pairs for value in pair],
            out_specs=[
                column(rows, 0),
                column(total, 0),
                column(total, 0),
                pl.BlockSpec((total, D), lambda i, n: (0, 0)),
            ]
            + [by_lead(shape) for shape in halves],
            scratch_shapes=[pltpu.VMEM((total, D), full)],
        ),
        compiler_params=pltpu.CompilerParams(vmem_limit_bytes=VMEM_LIMIT),
        cost_estimate=SMALL_COST,
        name="attend_backward",
    )(
        scalars,
        queries,
        keys,
        values,
        grads,
        logs,
        deltas,
        pair_weight,
        pair_weight,
        *extra,
        *[value for pair in pairs for value in pair],
    )


def swap(value, axis, bit):
    count = lax.axis_size(axis)
    return lax.ppermute(value, axis, [(i, i ^ bit) for i in range(count)])


class Order:
    def __init__(self):
        self.marks = ()

    def __call__(self, *values):
        values = lax.optimization_barrier(values + self.marks)[: len(values)]
        self.marks = values
        return values[0] if len(values) == 1 else values


def outer_bits():
    bits = []
    bit = 2
    while bit < lax.axis_size("dp"):
        bits.append(bit)
        bit *= 2
    return bits


class Gather:
    def __init__(self, parts):
        self.bits = outer_bits()
        half = len(self.bits) // 2
        self.orders = [
            self.bits[half * (n % 2) :] + self.bits[: half * (n % 2)] for n in range(len(parts))
        ]
        self.result = [[([0], part)] for part in parts]
        self.step = 0
        self.early = []

    def advance(self, order):
        held = self.result
        if self.step < len(self.bits):
            masks = [[m for mask, _ in pieces for m in mask] for pieces in held]
            blocks = [
                jnp.concatenate([array for _, array in pieces]) if self.step else pieces[0][1]
                for pieces in held
            ]
            blocks = order(*blocks)
            bits = [turn[self.step] for turn in self.orders]
            self.result = [
                [(mask, block), ([m ^ bit for m in mask], swap(block, "dp", bit))]
                for mask, block, bit in zip(masks, blocks, bits)
            ]
        else:
            rest = [pieces[1:] if self.early else pieces for pieces in held]
            arrays = iter(order(*[array for pieces in rest for _, array in pieces]))
            self.result = []
            for n, pieces in enumerate(rest):
                kept = [(masks, next(arrays)) for masks, _ in pieces]
                ours = held[n][:1] + kept if self.early else kept
                theirs = [([m ^ 1 for m in masks], swap(array, "dp", 1)) for masks, array in kept]
                self.result.append(ours + self.early[n : n + 1] + theirs)
        self.step += 1

    def send_early(self, order):
        arrays = order(*[pieces[0][1] for pieces in self.result])
        self.early = [
            ([m ^ 1 for m in pieces[0][0]], swap(array, "dp", 1))
            for pieces, array in zip(self.result, arrays)
        ]


def canonical_row(me, rank, block, mask, rank_mask, stride, offset):
    if mask is None:
        return offset
    row = (me ^ mask) * block + offset
    if stride:
        if rank_mask >= 2:
            rank_mask = rank_mask ^ ((rank + 1) // 2 % 2)
        row = row + (rank ^ rank_mask) * stride
    return pl.multiple_of(row, 16)


def place_kernel(plan, block, *refs):
    count = len(plan)
    ins = refs[:count]
    outs = refs[count:-1]
    sems = refs[-1]
    me = lax.axis_index("dp")
    rank = lax.axis_index("mp")
    copies = []
    for ref, moves in zip(ins, plan):
        for start, size, which, mask, column, _, offset in moves:
            row = canonical_row(me, rank, block, mask, 0, 0, offset)
            copy = pltpu.make_async_copy(
                ref.at[pl.ds(start, size), :],
                outs[which].at[pl.ds(row, size), pl.ds(column * D, D)],
                sems.at[len(copies)],
            )
            copy.start()
            copies.append(copy)
    for copy in copies:
        copy.wait()


def plan_of(gathered, layouts):
    arrays = []
    plan = []
    for pieces, layout in zip(gathered, layouts):
        rows = sum(size for _, size, *_ in layout)
        for masks, array in pieces:
            moves = []
            for j, mask in enumerate(masks):
                for start, size, which, rank_mask, stride, offset in layout:
                    moves.append((j * rows + start, size, which, mask, rank_mask, stride, offset))
            arrays.append(array)
            plan.append(moves)
    return arrays, plan


def place(arrays, plan, block, shapes):
    return pl.pallas_call(
        functools.partial(place_kernel, plan, block),
        out_shape=[jax.ShapeDtypeStruct(shape, low) for shape in shapes],
        in_specs=[pl.BlockSpec(memory_space=pl.ANY)] * len(arrays),
        out_specs=[pl.BlockSpec(memory_space=pltpu.VMEM)] * len(shapes),
        scratch_shapes=[pltpu.SemaphoreType.DMA((sum(len(moves) for moves in plan),))],
        compiler_params=pltpu.CompilerParams(vmem_limit_bytes=VMEM_LIMIT),
        cost_estimate=SMALL_COST,
        name="place",
    )(*arrays)


def store_split(value, keep, send, index, start=0):
    block = keep.shape[2]
    even = lax.axis_index("dp") % 2 == 0
    for outer in range(value.shape[0] // (2 * block)):
        first = value[2 * outer * block : (2 * outer + 1) * block]
        other = value[(2 * outer + 1) * block : (2 * outer + 2) * block]
        keep[index, start + outer] = jnp.where(even, first, other).astype(low)
        send[index, start + outer] = jnp.where(even, other, first).astype(low)


def middle_kernel(plan, block, total, *refs):
    limit_ref, vector_ref = refs[:2]
    token_hbm, mixed_hbm, log_hbm, cot_hbm, teach_hbm = refs[2:7]
    pieces = refs[7 : 7 + total]
    (
        out_hbm,
        middle_hbm,
        grad_hbm,
        down_keep,
        down_send,
        up_keep,
        up_send,
        delta_ref,
        log_ref,
        sum_ref,
    ) = refs[7 + total : 17 + total]
    (
        token,
        mixed,
        logs,
        cot,
        teach,
        up,
        down,
        proj,
        right,
        slope,
        second,
        middle,
        final,
        out,
        final_low,
        middle_low,
        grad,
        accum,
        turned,
        stage_keep,
        stage_send,
        in_sems,
        weight_sems,
        out_sems,
        keep_sems,
        send_sems,
    ) = refs[17 + total :]
    hidden = FF // D
    targets = (up, down, proj)
    rows = token.shape[0]
    me = lax.axis_index("dp")
    rank = lax.axis_index("mp")

    def fetch(ref, scratch, n):
        copy = pltpu.make_async_copy(ref, scratch, in_sems.at[n])
        copy.start()
        return copy

    def send(scratch, ref, n):
        copy = pltpu.make_async_copy(scratch, ref, out_sems.at[n])
        copy.start()
        return copy

    gets = [
        fetch(token_hbm, token, 0),
        fetch(mixed_hbm, mixed, 1),
        fetch(log_hbm, logs, 2),
        fetch(cot_hbm, cot, 3),
        fetch(teach_hbm, teach, 4),
    ]
    loads = {0: [], 1: [], 2: []}
    number = 0
    for want in (2, 0, 1):
        for ref, moves in zip(pieces, plan):
            for start, size, which, mask, rank_mask, stride, offset in moves:
                if which != want:
                    continue
                row = canonical_row(me, rank, block, mask, rank_mask, stride, offset)
                copy = pltpu.make_async_copy(
                    ref.at[pl.ds(start, size), :],
                    targets[which].at[pl.ds(row, size), :],
                    weight_sems.at[number],
                )
                copy.start()
                loads[which].append(copy)
                number += 1

    table_row = vector_ref[0:1, :]
    out_bias = vector_ref[1:2, :]
    gain = vector_ref[2:3, :]
    shift = vector_ref[3:4, :]
    down_bias = vector_ref[4:5, :]
    weight = vector_ref[5:6, :]
    gets[0].wait()
    gets[1].wait()
    right[2 * hidden] = mixed[...].astype(low)
    for copy in loads[2]:
        copy.wait()
    state = token[...].astype(full) + table_row + out_bias
    state = state + dot_of(right[2 * hidden], proj[...], 1, 1)
    middle[...] = state
    unit, _ = norm_stats(state)
    second[...] = (unit * gain + shift).astype(low)
    accum[...] = jnp.zeros((rows, D), full)
    for copy in loads[0]:
        copy.wait()
    for copy in loads[1]:
        copy.wait()

    def forward(m, _):
        place = pl.ds(pl.multiple_of(m * D, D), D)
        half = rows // 2
        spans = [pl.ds(part * half, half) for part in range(2)]
        values = [
            dot_of(second[span, :], up[place, :], 1, 0) + vector_ref[pl.ds(8 + m, 1), :]
            for span in spans
        ]
        for span, value in zip(spans, values):
            cumulative = 0.5 + 0.5 * lax.erf(value * (0.5**0.5))
            active = (value * cumulative).astype(low)
            right[m, span, :] = active
            slope[m, span, :] = (
                cumulative + value * jnp.exp(-0.5 * value * value) * 0.3989422804014327
            )
            accum[span, :] += dot_of(active, down[place, :], 1, 1)
        return 0

    lax.fori_loop(0, FF // D, forward, 0)
    final_state = middle[...] + accum[...] + down_bias
    out[...] = final_state.astype(low)
    puts = [send(out, out_hbm, 0)]
    gets[3].wait()
    gets[4].wait()
    place = lax.broadcasted_iota(jnp.int32, (rows, 1), 0)
    grads = cot[...].astype(full) + weight * (final_state - teach[...].astype(full))
    grads = jnp.where(place < limit_ref[5], grads, 0.0)
    final[...] = grads
    final_low[...] = grads.astype(low)
    sum_ref[3:4, :] = jnp.sum(grads, axis=0, keepdims=True)
    accum[...] = jnp.zeros((rows, D), full)

    def backward(m, _):
        place = pl.ds(pl.multiple_of(m * D, D), D)
        half = rows // 2
        spans = [pl.ds(part * half, half) for part in range(2)]
        values = [dot_of(final_low[span, :], down[place, :], 1, 0) for span in spans]
        sums = []
        for span, value in zip(spans, values):
            value = (slope[m, span, :] * value).astype(low)
            right[hidden + m, span, :] = value
            sums.append(jnp.sum(value.astype(full), axis=0, keepdims=True))
            accum[span, :] += dot_of(value, up[place, :], 1, 1)
        sum_ref[pl.ds(8 + m, 1), :] = sums[0] + sums[1]
        return 0

    lax.fori_loop(0, FF // D, backward, 0)
    unit, inverse = norm_stats(middle[...])
    second_grad = accum[...]
    sum_ref[0:1, :] = jnp.sum(second_grad * unit, axis=0, keepdims=True)
    sum_ref[1:2, :] = jnp.sum(second_grad, axis=0, keepdims=True)
    scaled = second_grad * gain
    mean_scaled = jnp.mean(scaled, axis=-1, keepdims=True)
    mean_unit = jnp.mean(scaled * unit, axis=-1, keepdims=True)
    total_grad = final[...] + inverse * (scaled - mean_scaled - unit * mean_unit)
    middle[...] = total_grad
    puts.append(send(middle, middle_hbm, 1))
    middle_low[...] = total_grad.astype(low)
    sum_ref[2:3, :] = jnp.sum(total_grad, axis=0, keepdims=True)
    attended_grad = dot_of(middle_low[...], proj[...], 1, 0).astype(low)
    grad[...] = attended_grad
    puts.append(send(grad, grad_hbm, 2))
    gets[2].wait()
    head = lax.broadcasted_iota(jnp.int32, (16, D), 0)
    lane = lax.broadcasted_iota(jnp.int32, (16, D), 1)
    member = jnp.where(lane // HEAD_DIM == head, 1.0, 0.0)
    leader = jnp.where(lane == head * HEAD_DIM, 1.0, 0.0)
    exact = functools.partial(
        lax.dot_general,
        dimension_numbers=(((1,), (1,)), ((), ())),
        precision=lax.Precision.HIGHEST,
        preferred_element_type=full,
    )
    deltas = exact(member, attended_grad.astype(full) * mixed[...])
    tops = exact(leader, logs[...])
    for pair in range(PAIRS):
        delta_ref[pair] = deltas[2 * pair : 2 * pair + 2]
        log_ref[pair] = tops[2 * pair : 2 * pair + 2]
    turned[0] = final_low[...].T
    turned[1] = second[...].T
    turned[2] = middle_low[...].T

    def weights(i, _):
        half = D // 2
        values = [
            dot_of(turned[i // hidden, part * half : (part + 1) * half, :], right[i], 1, 0)
            for part in range(2)
        ]
        for part, value in enumerate(values):
            store_split(value, stage_keep, stage_send, i, part * stage_keep.shape[1] // 2)

        @pl.when(i < hidden)
        def _():
            pltpu.make_async_copy(stage_keep.at[i], down_keep.at[i], keep_sems.at[i]).start()
            pltpu.make_async_copy(stage_send.at[i], down_send.at[i], send_sems.at[i]).start()

        @pl.when(i >= hidden)
        def _():
            row = i - hidden
            pltpu.make_async_copy(stage_keep.at[i], up_keep.at[row], keep_sems.at[i]).start()
            pltpu.make_async_copy(stage_send.at[i], up_send.at[row], send_sems.at[i]).start()

        return 0

    lax.fori_loop(0, 2 * hidden + 1, weights, 0)
    for copy in puts:
        copy.wait()
    for i in range(2 * hidden + 1):
        if i < hidden:
            keep, gone, row = down_keep, down_send, i
        else:
            keep, gone, row = up_keep, up_send, i - hidden
        pltpu.make_async_copy(stage_keep.at[i], keep.at[row], keep_sems.at[i]).wait()
        pltpu.make_async_copy(stage_send.at[i], gone.at[row], send_sems.at[i]).wait()


def middle_call(limit, vectors, tokens, mixed, logs, cot, teach, arrays, plan, block, dp):
    rows = tokens.shape[0]
    hidden = FF // D
    narrow = jax.ShapeDtypeStruct((rows, D), low)
    wide = jax.ShapeDtypeStruct((rows, D), full)
    shape = (dp // 2, D // dp, D)
    parts = [jax.ShapeDtypeStruct((count,) + shape, low) for count in (hidden, hidden + 1)]
    stats = jax.ShapeDtypeStruct((PAIRS, 2, rows), full)
    anywhere = pl.BlockSpec(memory_space=pl.ANY)
    inside = pl.BlockSpec(memory_space=pltpu.VMEM)
    moves = sum(len(part) for part in plan)
    return pl.pallas_call(
        functools.partial(middle_kernel, plan, block, len(arrays)),
        out_shape=(
            narrow,
            wide,
            narrow,
            parts[0],
            parts[0],
            parts[1],
            parts[1],
            stats,
            stats,
            jax.ShapeDtypeStruct((8 + 8, D), full),
        ),
        in_specs=[pl.BlockSpec(memory_space=pltpu.SMEM), inside]
        + [anywhere] * (5 + len(arrays)),
        out_specs=[anywhere] * 7 + [inside] * 3,
        scratch_shapes=[
            pltpu.VMEM((rows, D), low),
            pltpu.VMEM((rows, D), full),
            pltpu.VMEM((rows, D), full),
            pltpu.VMEM((rows, D), low),
            pltpu.VMEM((rows, D), low),
            pltpu.VMEM((FF, D), low),
            pltpu.VMEM((FF, D), low),
            pltpu.VMEM((D, D), low),
            pltpu.VMEM((2 * hidden + 1, rows, D), low),
            pltpu.VMEM((hidden, rows, D), full),
            pltpu.VMEM((rows, D), low),
            pltpu.VMEM((rows, D), full),
            pltpu.VMEM((rows, D), full),
            pltpu.VMEM((rows, D), low),
            pltpu.VMEM((rows, D), low),
            pltpu.VMEM((rows, D), low),
            pltpu.VMEM((rows, D), low),
            pltpu.VMEM((rows, D), full),
            pltpu.VMEM((3, D, rows), low),
            pltpu.VMEM((2 * hidden + 1,) + shape, low),
            pltpu.VMEM((2 * hidden + 1,) + shape, low),
            pltpu.SemaphoreType.DMA((5,)),
            pltpu.SemaphoreType.DMA((moves,)),
            pltpu.SemaphoreType.DMA((3,)),
            pltpu.SemaphoreType.DMA((2 * hidden + 1,)),
            pltpu.SemaphoreType.DMA((2 * hidden + 1,)),
        ],
        compiler_params=pltpu.CompilerParams(vmem_limit_bytes=VMEM_LIMIT),
        cost_estimate=SMALL_COST,
        name="middle",
    )(limit, vectors, tokens, mixed, logs, cot, teach, *arrays)


def fold_block(keep, got, out_keep, out_send, bit, place):
    step = 1 << place
    mine = (lax.axis_index("dp") // bit) % 2 * step
    for j in range(keep.shape[1] // 2):
        base = (j // step) * 2 * step + j % step
        for out, shift in ((out_keep, mine), (out_send, step - mine)):
            value = keep[0, base + shift].astype(full) + got[0, base + shift].astype(full)
            out[0, j] = value.astype(low)


def fold_kernel(bits, places, *refs):
    count = len(bits)
    for n in range(count):
        fold_block(
            *refs[2 * n : 2 * n + 2],
            *refs[2 * count + 2 * n : 2 * count + 2 * n + 2],
            bits[n],
            places[n],
        )


def fold(pairs, bits, places):
    lead = pairs[0][0].shape[0]
    block = lambda shape: pl.BlockSpec((1,) + shape[1:], lambda i: (i, 0, 0, 0))
    halves = [
        (keep.shape[0], keep.shape[1] // 2) + keep.shape[2:] for keep, _ in pairs for _ in range(2)
    ]
    outs = pl.pallas_call(
        functools.partial(fold_kernel, bits, places),
        out_shape=[jax.ShapeDtypeStruct(shape, low) for shape in halves],
        grid=(lead,),
        in_specs=[block(value.shape) for pair in pairs for value in pair],
        out_specs=[block(shape) for shape in halves],
        compiler_params=pltpu.CompilerParams(vmem_limit_bytes=VMEM_LIMIT),
        cost_estimate=pl.CostEstimate(flops=0, bytes_accessed=16 << 20, transcendentals=0),
        name="fold",
    )(*[value for pair in pairs for value in pair])
    return [(outs[2 * n], outs[2 * n + 1]) for n in range(len(pairs))]


def qkv_grad_kernel(count, *refs):
    sources = refs[: 3 * count + 1]
    outs = refs[3 * count + 1 : 3 * count + 5]
    sum_ref, held, *turned, totals, stage, in_sems, out_sems = refs[3 * count + 5 :]
    first_use = [0, count, count + 1, 2 * count + 1]
    for n in range(1, count):
        first_use += [n, count + 1 + n, 2 * count + 1 + n]
    copies = {}
    for n in first_use:
        copies[n] = pltpu.make_async_copy(sources[n], held.at[n], in_sems.at[n])
        copies[n].start()

    def column_sum(n):
        return jnp.sum(held[n].astype(full), axis=0, keepdims=True)

    puts = []

    def store(value, c):
        for part in range(2):
            store_split(
                value[:, part * D // 2 : (part + 1) * D // 2],
                stage.at[part],
                stage.at[2 + part],
                c,
            )
        for k in range(4):
            put = pltpu.make_async_copy(stage.at[k, c], outs[k].at[c], out_sems.at[k * 3 + c])
            put.start()
            puts.append(put)

    sum_ref[...] = jnp.zeros_like(sum_ref)
    copies[0].wait()
    turned[0][...] = held[0].T
    copies[count].wait()
    store(dot_of(turned[0][...], held[count], 1, 0), 0)
    sum_ref[0:1, :] = column_sum(count)
    value_sum = jnp.zeros((1, D), full)
    for n in range(count):
        if n + 1 < count:
            copies[n + 1].wait()
        copies[count + 1 + n].wait()
        copies[2 * count + 1 + n].wait()
        left = turned[n % 2][...]
        if n + 1 < count:
            turned[(n + 1) % 2][...] = held[n + 1].T
        for c in (1, 2):
            value = dot_of(left, held[c * count + 1 + n], 1, 0)
            if n > 0:
                value = value + totals[c - 1]
            if n + 1 < count:
                totals[c - 1] = value
            else:
                store(value, c)
        value_sum = value_sum + column_sum(2 * count + 1 + n)
    sum_ref[8:9, :] = value_sum
    for put in puts:
        put.wait()


def qkv_grads(chunks, query_grad, key_grads, value_grads, dp):
    rows = query_grad.shape[0]
    count = len(chunks)
    shape = (3, dp // 2, D // dp, D // 2)
    anywhere = pl.BlockSpec(memory_space=pl.ANY)
    return pl.pallas_call(
        functools.partial(qkv_grad_kernel, count),
        out_shape=[jax.ShapeDtypeStruct(shape, low)] * 4
        + [jax.ShapeDtypeStruct((16, D), full)],
        in_specs=[anywhere] * (3 * count + 1),
        out_specs=[anywhere] * 4 + [pl.BlockSpec(memory_space=pltpu.VMEM)],
        scratch_shapes=[
            pltpu.VMEM((3 * count + 1, rows, D), low),
            pltpu.VMEM((D, rows), low),
            pltpu.VMEM((D, rows), low),
            pltpu.VMEM((2, D, D), full),
            pltpu.VMEM((4,) + shape, low),
            pltpu.SemaphoreType.DMA((3 * count + 1,)),
            pltpu.SemaphoreType.DMA((12,)),
        ],
        compiler_params=pltpu.CompilerParams(vmem_limit_bytes=VMEM_LIMIT),
        cost_estimate=SMALL_COST,
        name="qkv_grads",
    )(*chunks, query_grad, *key_grads, *value_grads)


def last_kernel(
    token_ref,
    first_ref,
    right_ref,
    left_ref,
    middle_ref,
    vector_ref,
    gain_ref,
    bias_ref,
    sum_ref,
    out_ref,
    pack_ref,
):
    @pl.when(pl.program_id(0) == 0)
    def _():
        pack_ref[...] = jnp.zeros_like(pack_ref)
        pack_ref[1:2, :] = sum_ref[0:1, :]
        pack_ref[3:4, :] = sum_ref[1:2, :]
        pack_ref[4:5, :] = bias_ref[0:1, :]
        pack_ref[5:6, :] = bias_ref[8:9, :]
        pack_ref[6:8, :] = sum_ref[2:4, :]
        pack_ref[8 : 8 + FF // D, :] = sum_ref[8 : 8 + FF // D, :]

    unit, inverse = norm_stats(token_ref[...].astype(full) + vector_ref[0:1, :])
    grad = first_ref[...] + right_ref[...].astype(full) + left_ref[...].astype(full)
    scaled = grad * gain_ref[0:1, :]
    mean_scaled = jnp.mean(scaled, axis=-1, keepdims=True)
    mean_unit = jnp.mean(scaled * unit, axis=-1, keepdims=True)
    result = middle_ref[...] + inverse * (scaled - mean_scaled - unit * mean_unit)
    out_ref[...] = result
    pack_ref[0:1, :] += jnp.sum(grad * unit, axis=0, keepdims=True)
    pack_ref[2:3, :] += jnp.sum(grad, axis=0, keepdims=True)
    pack_ref[pl.ds(16 + lax.axis_index("dp"), 1), :] += jnp.sum(result, axis=0, keepdims=True)


def last_norm(tokens, first, right, left, middle_grad, vectors, gains, bias_sums, sums, dp):
    rows = tokens.shape[0]
    part = pl.BlockSpec((rows // 4, D), lambda i: (i, 0))
    whole = lambda value: pl.BlockSpec(value.shape, lambda i: (0, 0))
    small = (vectors, gains, bias_sums, sums)
    return pl.pallas_call(
        last_kernel,
        out_shape=(
            jax.ShapeDtypeStruct((rows, D), full),
            jax.ShapeDtypeStruct((16 + dp, D), full),
        ),
        grid=(4,),
        in_specs=[part] * 5 + [whole(value) for value in small],
        out_specs=[part, pl.BlockSpec((16 + dp, D), lambda i: (0, 0))],
        compiler_params=pltpu.CompilerParams(vmem_limit_bytes=VMEM_LIMIT),
        cost_estimate=SMALL_COST,
        name="last_norm",
    )(tokens, first, right, left, middle_grad, *small)


def two_parts(value, axis, mine):
    keep = lax.dynamic_index_in_dim(value, mine, axis, keepdims=False)
    send = lax.dynamic_index_in_dim(value, 1 - mine, axis, keepdims=False)
    return keep, send.astype(low)


class Scatter:
    def __init__(self, parts, turns):
        self.bits = outer_bits()
        half = len(self.bits) // 2
        self.orders = [
            [1] + self.bits[half * (turn % 2) :] + self.bits[: half * (turn % 2)] for turn in turns
        ]
        self.left = [list(self.bits) for _ in turns]
        self.step = 0
        self.parts = parts

    def sends(self):
        return [send for _, send in self.parts]

    def exchange(self, sends):
        self.pairs = [
            (keep, swap(send, "dp", turn[self.step]))
            for (keep, _), send, turn in zip(self.parts, sends, self.orders)
        ]
        self.step += 1

    def folds(self):
        if self.step > len(self.bits):
            return [], [], []
        bits = [turn[self.step] for turn in self.orders]
        places = []
        for left, bit in zip(self.left, bits):
            places.append(left.index(bit))
            left.remove(bit)
        return self.pairs, bits, places

    def give(self, outs):
        self.parts = [(outs[n], outs[n + 1]) for n in range(0, len(outs), 2)]

    def fold(self):
        outs = []
        for pair, bit, at in zip(*self.folds()):
            outs += fold([pair], [bit], [at])[0]
        self.give(outs)

    def advance(self, order):
        sends = order(*self.sends())
        self.exchange(list(sends) if len(self.parts) > 1 else [sends])

    def finish(self, order):
        while self.step <= len(self.bits):
            self.fold()
            self.advance(order)
        got = order(*[other for _, other in self.pairs])
        return [
            (keep.astype(full) + other.astype(full))[:, 0]
            for (keep, _), other in zip(self.pairs, got)
        ]


def scatter_dp(parts, turns):
    scatter = Scatter(parts, turns)
    while True:
        sends = yield scatter.sends()
        scatter.exchange(sends)
        if scatter.step > len(scatter.bits):
            break
        scatter.parts = fold(*scatter.folds())
    got = yield [other for _, other in scatter.pairs]
    return [
        (keep.astype(full) + other.astype(full))[:, 0]
        for (keep, _), other in zip(scatter.pairs, got)
    ]


def scatter_mp(value):
    rank = lax.axis_index("mp")
    part = lambda index: lax.dynamic_index_in_dim(value, index, keepdims=False)
    sends = yield [part(rank ^ bit).astype(low) for bit in (1, 2, 3)]
    got = yield [swap(send, "mp", bit) for bit, send in zip((1, 2, 3), sends)]
    got = [other.astype(full) for other in got]
    return (part(rank) + got[0]) + (got[1] + got[2])


def halve_mp(value):
    rank = lax.axis_index("mp")
    pairs = value.reshape((2, 2) + value.shape[1:])
    keep, send = two_parts(pairs, 1, rank % 2)
    (send,) = yield [send]
    (got,) = yield [swap(send, "mp", 1)]
    keep, send = two_parts(keep.astype(full) + got.astype(full), 0, rank // 2)
    (send,) = yield [send]
    (got,) = yield [swap(send, "mp", 2)]
    return keep + got.astype(full)


def scatter_feed(up_own, down_own):
    mp = lax.axis_size("mp")
    block = down_own.shape[1]
    out_own = up_own[mp].reshape(block, mp, -1).transpose(1, 0, 2)
    own = yield from halve_mp(
        jnp.concatenate([up_own[:mp], down_own, out_own.reshape(mp, -1, D)], axis=1)
    )
    return own[:block], own[block : 2 * block].T, own[2 * block :].reshape(block, -1).T


def scatter_qkv(keep_left, keep_right, send_left, send_right):
    left_part, right_part = yield from scatter_dp(
        [(keep_left, send_left), (keep_right, send_right)], (0, 1)
    )
    width = D // lax.axis_size("mp")
    parts = [part[..., at : at + width] for part in (left_part, right_part) for at in (0, width)]
    return (yield from scatter_mp(jnp.stack(parts)))


def sum_small(value):
    (value,) = yield [value]
    value = value + swap(value, "dp", 1)
    bits = outer_bits()
    groups = [("dp", bits[n : n + 2]) for n in range(0, len(bits), 2)] + [("mp", [1, 2])]
    for axis, pair in groups:
        (value,) = yield [value]
        if len(pair) == 1:
            value = value + swap(value, axis, pair[0])
        else:
            one, two = pair
            got = [swap(value, axis, mask) for mask in (one, two, one + two)]
            if axis == "mp":
                got = yield got
            value = (value + got[0]) + (got[1] + got[2])
    return value


class Steps:
    def __init__(self, steps):
        self.steps = steps
        self.pending = next(steps)
        self.result = None

    def advance(self, order):
        if self.pending is None:
            return
        sends = order(*self.pending)
        sends = [sends] if len(self.pending) == 1 else list(sends)
        try:
            self.pending = self.steps.send(sends)
        except StopIteration as stop:
            self.pending = None
            self.result = stop.value

    def finish(self, order):
        while self.pending is not None:
            self.advance(order)
        return self.result


def shards(
    tokens_in,
    timesteps,
    lengths,
    time_table,
    norm_gains,
    norm_biases,
    w_qkv,
    qv_bias,
    w_out,
    out_bias,
    w_up,
    up_bias,
    w_down,
    down_bias,
    cotangent,
    teacher,
):
    rank = lax.axis_index("mp")
    data_rank = lax.axis_index("dp")
    mp = lax.axis_size("mp")
    dp = lax.axis_size("dp")
    own_rows = tokens_in.shape[0]
    length = lax.dynamic_index_in_dim(lengths, data_rank, keepdims=False)
    own_time = lax.dynamic_index_in_dim(timesteps, data_rank, keepdims=False)
    odd = rank % 2 == 1
    upper = rank >= 2
    middle = jnp.logical_or(rank == 1, rank == 2)
    order = Order()
    along = lambda value, pairs: lax.ppermute(value, "mp", pairs)

    block = w_qkv.shape[1]
    aligned = block % 32 == 0
    narrow = order(jnp.concatenate([w_qkv.reshape(3 * block, -1), w_out.T]))
    first_swap = swap(narrow, "mp", 1)
    tall = order(jnp.concatenate([w_up, w_down.T]))
    tall_swap = swap(tall, "mp", 1)
    pair = order(
        jnp.concatenate(
            [jnp.where(odd, first_swap, narrow), jnp.where(odd, narrow, first_swap)], axis=1
        )
    )
    second_swap = swap(pair, "mp", 2)
    tokens, lengths, own_time, norm_gains, norm_biases, out_bias, down_bias, up_bias, length = order(
        tokens_in, lengths, own_time, norm_gains, norm_biases, out_bias, down_bias, up_bias, length
    )
    table_row = lax.dynamic_slice_in_dim(time_table, own_time, 1).astype(full)
    unit_one, _ = norm_stats(tokens.astype(full) + table_row)
    first_norm = (unit_one * norm_gains[0] + norm_biases[0]).astype(low)
    loss_weight = lengths.shape[0] * MAXLEN / jnp.sum(lengths).astype(full)
    vectors = jnp.concatenate(
        [
            table_row,
            out_bias[None],
            norm_gains[1:2],
            norm_biases[1:2],
            down_bias[None],
            jnp.full((3, D), loss_weight),
            up_bias.reshape(-1, D),
            jnp.zeros((4, D), full),
        ]
    )
    scalars = jnp.stack(
        [
            rank,
            jnp.where(rank == 0, 1, rank - 1),
            jnp.where(upper, rank - 2, rank + 2),
            jnp.where(middle, rank + 1, 3 - rank),
            length,
            length - rank * own_rows,
        ]
    ).astype(jnp.int32)
    first_norm, vectors, scalars = order(first_norm, vectors, scalars)
    wide = jnp.concatenate(
        [jnp.where(upper, second_swap, pair), jnp.where(upper, pair, second_swap)], axis=1
    )
    qkv_rows, out_rows = wide[: 3 * block], wide[3 * block :]
    if aligned:
        split = 3 * block // 2
        qkv_gather = Gather([qkv_rows[:split], qkv_rows[split:]])
        qkv_gather.advance(order)
    tall = order(jnp.concatenate([tall, tall_swap]))
    tall_across = along(tall, [(1, 2), (2, 1)])

    sent = order(first_norm)
    from_left = along(sent, [(0, 1), (1, 2), (2, 3)])
    from_right = along(sent, [(1, 0), (2, 1), (3, 2)])
    tall_across = order(tall_across)
    tall_far = along(tall_across, [(1, 0), (2, 3)])
    if aligned:
        while qkv_gather.step < len(qkv_gather.bits):
            qkv_gather.advance(order)
        qkv_gather.advance(order)
    hop_right, hop_left = order(from_left, from_right)
    second_right = along(hop_right, [(1, 2), (2, 3)])
    second_left = along(hop_left, [(1, 0), (2, 1)])
    if aligned:
        arrays, plan = plan_of(
            qkv_gather.result,
            [
                [(0, block, 0, 0, 0, 0), (block, split - block, 1, 0, 0, 0)],
                [
                    (0, 2 * block - split, 1, 0, 0, split - block),
                    (2 * block - split, block, 1, 1, 0, 0),
                ],
            ],
        )
        query_weight, pair_weight = order(*place(arrays, plan, block, [(D, D), (D, 2 * D)]))
        tall_other = jnp.where(middle, tall_across, order(tall_far))
        feed_gather = Gather(
            [
                jnp.concatenate([tall, out_rows[: block // 2]]),
                jnp.concatenate([tall_other, out_rows[block // 2 :]]),
            ]
        )
        feed_gather.advance(order)
    else:
        weights = lax.all_gather(qkv_rows.reshape(3, block, D), "dp", axis=1, tiled=True)
        query_weight = weights[0]
        pair_weight = jnp.concatenate([weights[1], weights[2]], axis=1)
    near = jnp.where(rank == 0, hop_left, hop_right)
    attend = lambda parts, numbers, carried: order(
        *attend_forward(
            parts,
            numbers,
            scalars,
            query_weight,
            pair_weight,
            qv_bias[0:1],
            qv_bias[1:2],
            carried,
        )
    )
    key_own, value_own, queries, *state = attend([order(first_norm)], (0,), None)
    second_right, second_left = order(second_right, second_left)
    second = order(jnp.where(upper, second_right, second_left))
    third = along(second, [(1, 0), (2, 3)])
    if aligned:
        while feed_gather.step < len(feed_gather.bits):
            feed_gather.advance(order)
        feed_gather.send_early(order)
    near, second = order(near, second)
    key_near, key_second, value_near, value_second, *state = attend(
        [near, second], (1, 2), (queries, *state)
    )
    last = order(jnp.where(middle, hop_left, order(third)))
    key_last, value_last, mixed, logs = attend([order(last)], (3,), (queries, *state))
    if aligned:
        feed_gather.advance(order)
        layout = lambda masks, shift: [
            (0, block, 0, masks[0], D, 0),
            (block, block, 1, masks[0], D, 0),
            (2 * block, block, 0, masks[1], D, 0),
            (3 * block, block, 1, masks[1], D, 0),
            (4 * block, block // 2, 2, 0, 0, shift),
        ]
        arrays, plan = plan_of(
            feed_gather.result, [layout((0, 1), 0), layout((2, 3), block // 2)]
        )
    else:
        arrays = [
            lax.all_gather(w_up, ("mp", "dp"), axis=0, tiled=True),
            lax.all_gather(w_down.T, ("mp", "dp"), axis=0, tiled=True),
            lax.all_gather(out_rows, "dp", axis=0, tiled=True),
        ]
        plan = [[(0, array.shape[0], n, None, 0, 0, 0)] for n, array in enumerate(arrays)]
    chunks = [first_norm, near, second, last]
    keys = [key_own, key_near, key_second, key_last]
    values = [value_own, value_near, value_second, value_last]

    output, middle_grad, attended_grad, *parts, deltas, log_rows, sums = middle_call(
        scalars, vectors, tokens, mixed, logs, cotangent, teacher, arrays, plan, block, dp
    )
    scatter = Scatter([(parts[0], parts[1]), (parts[2], parts[3])], (1, 0))
    scatter.advance(order)

    key_grads = [None] * 4
    value_grads = [None] * 4
    firsts = [None] * 4
    query_grad = None
    for n in (3, 2, 1, 0):
        pairs, bits, places = scatter.folds() if n % 2 == 0 else ([], [], [])
        query_grad, key_grads[n], value_grads[n], firsts[n], *folded = attend_backward(
            n,
            queries,
            keys[n],
            values[n],
            order(attended_grad),
            log_rows,
            deltas,
            query_weight,
            pair_weight,
            scalars,
            query_grad,
            n == 0,
            pairs,
            bits,
            places,
        )
        firsts[n] = order(firsts[n])
        if folded:
            scatter.give(folded)
        if n == 3:
            back_last = along(firsts[3], [(0, 1), (3, 2)]).astype(full)
        elif n == 2:
            scatter.advance(order)
            payload = order((firsts[2] + back_last).astype(low))
            back_right = along(payload, [(0, 1), (1, 2)]).astype(full)
            back_left = along(payload, [(3, 2), (2, 1)]).astype(full)
        elif n == 1:
            to_right = jnp.where(
                rank == 0, firsts[1], firsts[3].astype(full) + back_right
            ).astype(low)
            to_left = (firsts[1] + back_left).astype(low)
            to_right, to_left = order(to_right, to_left)
            final_right = along(to_right, [(0, 1), (1, 2), (2, 3)])
            final_left = along(to_left, [(3, 2), (2, 1), (1, 0)])
    scatter.advance(order)
    query_grad, final_right, final_left = order(query_grad, final_right, final_left)
    *halves, bias_sums = qkv_grads(chunks, query_grad, key_grads, value_grads, dp)
    qkv = Steps(scatter_qkv(*halves))
    qkv.advance(order)
    down_own, up_own = scatter.finish(order)
    feed = Steps(scatter_feed(up_own, down_own))
    feed.advance(order)
    qkv.advance(order)
    tokens, first_own = order(tokens, firsts[0])
    input_grad, packed = last_norm(
        tokens,
        first_own,
        final_right,
        final_left,
        middle_grad,
        vectors,
        norm_gains,
        bias_sums,
        sums,
        dp,
    )
    packed, input_grad = order(packed, input_grad)
    small = Steps(sum_small(packed))
    feed.advance(order)
    feed.advance(order)
    small.advance(order)
    qkv.advance(order)
    feed.advance(order)
    qkv.advance(order)
    small.advance(order)
    qkv.advance(order)
    small.advance(order)
    total = small.finish(order)
    up_grad, down_grad, out_grad = feed.finish(order)
    qkv_grad = qkv.finish(order)
    fixed = 16
    chosen = (timesteps[None, :] == jnp.arange(time_table.shape[0])[:, None]).astype(full)
    table_grad = lax.dot_general(
        chosen,
        total[fixed:],
        (((1,), (0,)), ((), ())),
        precision=lax.Precision.HIGHEST,
        preferred_element_type=full,
    )
    return (
        output,
        input_grad,
        table_grad,
        total[0:2],
        total[2:4],
        qkv_grad,
        total[4:6],
        out_grad,
        total[6],
        up_grad,
        total[8 : 8 + FF // D].reshape(FF),
        down_grad,
        total[7],
    )


def solution(mesh):
    rows = P(both, None)
    placed = (
        rows,
        P(),
        P(),
        P(),
        P(),
        P(),
        P(None, "dp", "mp"),
        P(),
        P("mp", "dp"),
        P(),
        P("dp", "mp"),
        P(),
        P("mp", "dp"),
        P(),
        rows,
        rows,
    )
    return jax.shard_map(
        shards,
        mesh=mesh,
        in_specs=placed,
        out_specs=(
            rows,
            rows,
            P(),
            P(),
            P(),
            P(None, "dp", "mp"),
            P(),
            P("mp", "dp"),
            P(),
            P("dp", "mp"),
            P(),
            P("mp", "dp"),
            P(),
        ),
        check_vma=False,
    )
```

```python
import functools

import jax
import jax.numpy as jnp
from jax import lax
from jax.experimental import pallas as pl
from jax.experimental.pallas import tpu as pltpu
from jax.sharding import PartitionSpec as P

D = 768
HEADS = 12
HEAD_DIM = 64
FF = 3072
MAXLEN = 2048
PAIR = 2 * HEAD_DIM
PAIRS = HEADS // 2
VMEM_LIMIT = 58 << 20
SMALL_COST = pl.CostEstimate(flops=1 << 20, bytes_accessed=1 << 16, transcendentals=0)

far_below = -1e30
epsilon = 1e-05
score_scale = HEAD_DIM ** (-0.5)
low = jnp.bfloat16
full = jnp.float32
both = ("dp", "mp")


def norm_stats(values):
    center = values - jnp.mean(values, axis=-1, keepdims=True)
    spread = jnp.mean(center * center, axis=-1, keepdims=True)
    inverse = lax.rsqrt(spread + epsilon)
    return center * inverse, inverse


def dot_of(left_side, right_side, left_dim, right_dim):
    return lax.dot_general(
        left_side,
        right_side,
        (((left_dim,), (right_dim,)), ((), ())),
        preferred_element_type=full,
    )


def first_half(shape):
    return lax.broadcasted_iota(jnp.int32, shape, len(shape) - 1) < HEAD_DIM


def forward_kernel(numbers, first, final, scalars, *refs):
    count = len(numbers)
    chunk_refs = refs[:count]
    wk_ref, wv_ref, value_bias_ref = refs[count : count + 3]
    refs = refs[count + 3 :]
    if first:
        wq_ref, query_bias_ref = refs[:2]
        key_outs, value_outs = refs[2 : 2 + count], refs[2 + count : 2 + 2 * count]
        query_out, top_ref, sum_ref, acc_ref = refs[2 + 2 * count :]
        q_pair = (dot_of(chunk_refs[0][...], wq_ref[...], 1, 0) + query_bias_ref[...]).astype(low)
        q_pair = q_pair * jnp.asarray(score_scale, low)
        query_out[...] = q_pair
    else:
        q_ref, top_in, sum_in, acc_in = refs[:4]
        key_outs, value_outs = refs[4 : 4 + count], refs[4 + count : 4 + 2 * count]
        results = refs[4 + 2 * count :]
        q_pair = q_ref[...]
    weight = jnp.concatenate([wk_ref[...], wv_ref[...]], axis=1)
    keys = []
    values = []
    for n in range(count):
        both_parts = dot_of(chunk_refs[n][...], weight, 1, 0)
        keys.append(both_parts[:, :PAIR].astype(low))
        values.append((both_parts[:, PAIR:] + value_bias_ref[...]).astype(low))
        key_outs[n][...] = keys[n]
        value_outs[n][...] = values[n]
    rows = q_pair.shape[0]
    size = keys[0].shape[0]
    values = [jnp.concatenate([value, jnp.ones((size, PAIR), low)], axis=1) for value in values]
    place = lax.broadcasted_iota(jnp.int32, (1, size), 1)
    lower = first_half((rows, PAIR))
    parts = []
    for half in range(2):
        kept = lower if half == 0 else jnp.logical_not(lower)
        q_half = jnp.where(kept, q_pair, jnp.zeros_like(q_pair))
        scores = []
        for n in range(count):
            bias = jnp.where(place + scalars[numbers[n]] * size < scalars[4], 0.0, far_below)
            scores.append(dot_of(q_half, keys[n], 1, 1) + bias)
        highest = functools.reduce(
            jnp.maximum, [jnp.max(score, axis=-1, keepdims=True) for score in scores]
        )
        weighed = None
        for n in range(count):
            exp_scores = jnp.exp(scores[n] - highest).astype(low)
            part = dot_of(exp_scores, values[n], 1, 0)
            weighed = part if weighed is None else weighed + part
        parts.append((highest, weighed[:, PAIR:], weighed[:, :PAIR]))
    top = jnp.where(lower, parts[0][0], parts[1][0])
    total = jnp.where(lower, parts[0][1], parts[1][1])
    mixed = jnp.where(lower, parts[0][2], parts[1][2])
    if first:
        top_ref[...] = top
        sum_ref[...] = total
        acc_ref[...] = mixed
    else:
        highest = jnp.maximum(top, top_in[...])
        here = jnp.exp(top - highest)
        before = jnp.exp(top_in[...] - highest)
        total = total * here + sum_in[...] * before
        mixed = mixed * here + acc_in[...] * before
        if final:
            results[0][...] = mixed / total
            results[1][...] = highest + jnp.log(total)
        else:
            results[0][...] = highest
            results[1][...] = total
            results[2][...] = mixed


def attend_forward(chunks, numbers, scalars, query_weight, pair_weight, query_bias, value_bias, carried):
    rows = chunks[0].shape[0]
    count = len(chunks)
    first = carried is None
    final = 3 in numbers
    column = lambda height, c: pl.BlockSpec((height, PAIR), lambda i, n: (0, c * PAIRS + i))
    whole = pl.BlockSpec((rows, D), lambda i, n: (0, 0))
    wide = jax.ShapeDtypeStruct((rows, D), full)
    narrow = jax.ShapeDtypeStruct((rows, D), low)
    extra = (query_weight, query_bias) if first else carried
    results = (narrow,) * first + (wide,) * (2 if final else 3)
    return pl.pallas_call(
        functools.partial(forward_kernel, numbers, first, final),
        out_shape=(narrow,) * (2 * count) + results,
        grid_spec=pltpu.PrefetchScalarGridSpec(
            num_scalar_prefetch=1,
            grid=(PAIRS,),
            in_specs=[whole] * count
            + [column(D, 0), column(D, 1), column(1, 0)]
            + ([column(D, 0), column(1, 0)] if first else [column(rows, 0)] * 4),
            out_specs=[column(rows, 0)] * (2 * count + len(results)),
        ),
        compiler_params=pltpu.CompilerParams(vmem_limit_bytes=VMEM_LIMIT),
        cost_estimate=SMALL_COST,
        name="attend_forward",
    )(scalars, *chunks, pair_weight, pair_weight, value_bias, *extra)


def backward_kernel(
    number,
    first,
    last,
    folds,
    scalars,
    q_ref,
    k_ref,
    v_ref,
    g_ref,
    log_ref,
    delta_ref,
    wk_ref,
    wv_ref,
    *refs
):
    if last:
        wq_ref = refs[0]
        refs = refs[1:]
    if not first:
        dq_in = refs[0]
        refs = refs[1:]
    count = len(folds)
    fold_ins, refs = refs[: 2 * count], refs[2 * count :]
    dq_ref, dk_ref, dv_ref, back_ref = refs[:4]
    fold_outs, accum = refs[4:-1], refs[-1]
    step = pl.program_id(0)
    for n, (lead, bit, at) in enumerate(folds):

        @pl.when(step < lead)
        def _():
            fold_block(
                *fold_ins[2 * n : 2 * n + 2], *fold_outs[2 * n : 2 * n + 2], bit, at
            )

    rows = q_ref.shape[0]
    keys = k_ref.shape[0]
    limit = scalars[4] - scalars[number] * keys
    q_pair = q_ref[...]
    g_pair = g_ref[...]
    k_pair = k_ref[...]
    v_pair = v_ref[...]
    lower = first_half((rows, PAIR))
    nothing = jnp.zeros((rows, PAIR), low)
    two_halves = lambda pair: jnp.concatenate(
        [jnp.where(lower, pair, nothing), jnp.where(lower, nothing, pair)]
    )
    queries = two_halves(q_pair)
    grads_out = two_halves(g_pair)
    row_of = lambda ref: jnp.concatenate([ref[0, 0:1, :], ref[0, 1:2, :]], axis=1)
    place = lax.broadcasted_iota(jnp.int32, (keys, 1), 0)
    bias = jnp.where(place < limit, 0.0, far_below)
    scores = dot_of(k_pair, queries, 1, 1) + bias
    prob_grad = dot_of(v_pair, grads_out, 1, 1)
    probs = jnp.exp(scores - row_of(log_ref))
    score_grad = (probs * (prob_grad - row_of(delta_ref))).astype(low)
    dv_low = dot_of(probs.astype(low), grads_out, 1, 0).astype(low)
    dk_low = dot_of(score_grad, queries, 1, 0).astype(low)
    turned = dot_of(k_pair.T, score_grad, 1, 0)
    upper_rows = lax.broadcasted_iota(jnp.int32, (PAIR, rows), 0) < HEAD_DIM
    dk_ref[...] = dk_low
    dv_ref[...] = dv_low
    grads = [dk_low, dv_low]
    weights = [wk_ref[...], wv_ref[...]]
    dq_all = jnp.where(upper_rows, turned[:, :rows], turned[:, rows:]).T
    if not first:
        dq_all = dq_all + dq_in[...]
    back = dot_of(jnp.concatenate(grads, axis=1), jnp.concatenate(weights, axis=1), 1, 1)
    if last:
        dq_low = (dq_all * score_scale).astype(low)
        dq_ref[...] = dq_low
        back = back + dot_of(dq_low, wq_ref[...], 1, 1)
    else:
        dq_ref[...] = dq_all

    @pl.when(step == 0)
    def _():
        accum[...] = back

    @pl.when(step > 0)
    def _():
        accum[...] += back

    @pl.when(step == PAIRS - 1)
    def _():
        back_ref[...] = accum[...].astype(back_ref.dtype)


def attend_backward(
    number,
    queries,
    keys,
    values,
    grads,
    logs,
    deltas,
    query_weight,
    pair_weight,
    scalars,
    carried,
    last,
    pairs,
    bits,
    places,
):
    rows, total = queries.shape[0], keys.shape[0]
    first = carried is None
    folds = [(keep.shape[0], bit, at) for (keep, _), bit, at in zip(pairs, bits, places)]
    halves = [
        (keep.shape[0], keep.shape[1] // 2) + keep.shape[2:] for keep, _ in pairs for _ in range(2)
    ]

    def by_lead(shape):
        end = shape[0] - 1
        return pl.BlockSpec((1,) + shape[1:], lambda i, n: (jnp.minimum(i, end), 0, 0, 0))

    column = lambda count, c: pl.BlockSpec((count, PAIR), lambda i, n: (0, c * PAIRS + i))
    stats = pl.BlockSpec((1, 2, rows), lambda i, n: (i, 0, 0))
    extra = (query_weight,) * last + (() if first else (carried,))
    extra_specs = [column(D, 0)] * last + ([] if first else [column(rows, 0)])
    return pl.pallas_call(
        functools.partial(backward_kernel, number, first, last, folds),
        out_shape=(
            jax.ShapeDtypeStruct((rows, D), low if last else full),
            jax.ShapeDtypeStruct((total, D), low),
            jax.ShapeDtypeStruct((total, D), low),
            jax.ShapeDtypeStruct((total, D), low if first else full),
            *[jax.ShapeDtypeStruct(shape, low) for shape in halves],
        ),
        grid_spec=pltpu.PrefetchScalarGridSpec(
            num_scalar_prefetch=1,
            grid=(PAIRS,),
            in_specs=[
                column(rows, 0),
                column(total, 0),
                column(total, 0),
                column(rows, 0),
                stats,
                stats,
                column(D, 0),
                column(D, 1),
            ]
            + extra_specs
            + [by_lead(value.shape) for pair in pairs for value in pair],
            out_specs=[
                column(rows, 0),
                column(total, 0),
                column(total, 0),
                pl.BlockSpec((total, D), lambda i, n: (0, 0)),
            ]
            + [by_lead(shape) for shape in halves],
            scratch_shapes=[pltpu.VMEM((total, D), full)],
        ),
        compiler_params=pltpu.CompilerParams(vmem_limit_bytes=VMEM_LIMIT),
        cost_estimate=SMALL_COST,
        name="attend_backward",
    )(
        scalars,
        queries,
        keys,
        values,
        grads,
        logs,
        deltas,
        pair_weight,
        pair_weight,
        *extra,
        *[value for pair in pairs for value in pair],
    )


def swap(value, axis, bit):
    count = lax.axis_size(axis)
    return lax.ppermute(value, axis, [(i, i ^ bit) for i in range(count)])


class Order:
    def __init__(self):
        self.marks = ()

    def __call__(self, *values):
        values = lax.optimization_barrier(values + self.marks)[: len(values)]
        self.marks = values
        return values[0] if len(values) == 1 else values


def outer_bits():
    bits = []
    bit = 2
    while bit < lax.axis_size("dp"):
        bits.append(bit)
        bit *= 2
    return bits


class Gather:
    def __init__(self, parts):
        self.bits = outer_bits()
        half = len(self.bits) // 2
        self.orders = [
            self.bits[half * (n % 2) :] + self.bits[: half * (n % 2)] for n in range(len(parts))
        ]
        self.result = [[([0], part)] for part in parts]
        self.step = 0
        self.early = []

    def advance(self, order):
        held = self.result
        if self.step < len(self.bits):
            masks = [[m for mask, _ in pieces for m in mask] for pieces in held]
            blocks = [
                jnp.concatenate([array for _, array in pieces]) if self.step else pieces[0][1]
                for pieces in held
            ]
            blocks = order(*blocks)
            bits = [turn[self.step] for turn in self.orders]
            self.result = [
                [(mask, block), ([m ^ bit for m in mask], swap(block, "dp", bit))]
                for mask, block, bit in zip(masks, blocks, bits)
            ]
        else:
            rest = [pieces[1:] if self.early else pieces for pieces in held]
            arrays = iter(order(*[array for pieces in rest for _, array in pieces]))
            self.result = []
            for n, pieces in enumerate(rest):
                kept = [(masks, next(arrays)) for masks, _ in pieces]
                ours = held[n][:1] + kept if self.early else kept
                theirs = [([m ^ 1 for m in masks], swap(array, "dp", 1)) for masks, array in kept]
                self.result.append(ours + self.early[n : n + 1] + theirs)
        self.step += 1

    def send_early(self, order):
        arrays = order(*[pieces[0][1] for pieces in self.result])
        self.early = [
            ([m ^ 1 for m in pieces[0][0]], swap(array, "dp", 1))
            for pieces, array in zip(self.result, arrays)
        ]


def canonical_row(me, rank, block, mask, rank_mask, stride, offset):
    if mask is None:
        return offset
    row = (me ^ mask) * block + offset
    if stride:
        if rank_mask >= 2:
            rank_mask = rank_mask ^ ((rank + 1) // 2 % 2)
        row = row + (rank ^ rank_mask) * stride
    return pl.multiple_of(row, 16)


def place_kernel(plan, block, *refs):
    count = len(plan)
    ins = refs[:count]
    outs = refs[count:-1]
    sems = refs[-1]
    me = lax.axis_index("dp")
    rank = lax.axis_index("mp")
    copies = []
    for ref, moves in zip(ins, plan):
        for start, size, which, mask, column, _, offset in moves:
            row = canonical_row(me, rank, block, mask, 0, 0, offset)
            copy = pltpu.make_async_copy(
                ref.at[pl.ds(start, size), :],
                outs[which].at[pl.ds(row, size), pl.ds(column * D, D)],
                sems.at[len(copies)],
            )
            copy.start()
            copies.append(copy)
    for copy in copies:
        copy.wait()


def plan_of(gathered, layouts):
    arrays = []
    plan = []
    for pieces, layout in zip(gathered, layouts):
        rows = sum(size for _, size, *_ in layout)
        for masks, array in pieces:
            moves = []
            for j, mask in enumerate(masks):
                for start, size, which, rank_mask, stride, offset in layout:
                    moves.append((j * rows + start, size, which, mask, rank_mask, stride, offset))
            arrays.append(array)
            plan.append(moves)
    return arrays, plan


def place(arrays, plan, block, shapes):
    return pl.pallas_call(
        functools.partial(place_kernel, plan, block),
        out_shape=[jax.ShapeDtypeStruct(shape, low) for shape in shapes],
        in_specs=[pl.BlockSpec(memory_space=pl.ANY)] * len(arrays),
        out_specs=[pl.BlockSpec(memory_space=pltpu.VMEM)] * len(shapes),
        scratch_shapes=[pltpu.SemaphoreType.DMA((sum(len(moves) for moves in plan),))],
        compiler_params=pltpu.CompilerParams(vmem_limit_bytes=VMEM_LIMIT),
        cost_estimate=SMALL_COST,
        name="place",
    )(*arrays)


def store_split(value, keep, send, index, start=0):
    block = keep.shape[2]
    even = lax.axis_index("dp") % 2 == 0
    for outer in range(value.shape[0] // (2 * block)):
        first = value[2 * outer * block : (2 * outer + 1) * block]
        other = value[(2 * outer + 1) * block : (2 * outer + 2) * block]
        keep[index, start + outer] = jnp.where(even, first, other).astype(low)
        send[index, start + outer] = jnp.where(even, other, first).astype(low)


def middle_kernel(plan, block, total, *refs):
    limit_ref, vector_ref = refs[:2]
    token_hbm, mixed_hbm, log_hbm, cot_hbm, teach_hbm = refs[2:7]
    pieces = refs[7 : 7 + total]
    (
        out_hbm,
        middle_hbm,
        grad_hbm,
        down_keep,
        down_send,
        up_keep,
        up_send,
        delta_ref,
        log_ref,
        sum_ref,
    ) = refs[7 + total : 17 + total]
    (
        token,
        mixed,
        logs,
        cot,
        teach,
        up,
        down,
        proj,
        right,
        slope,
        second,
        middle,
        final,
        out,
        final_low,
        middle_low,
        grad,
        accum,
        turned,
        stage_keep,
        stage_send,
        in_sems,
        weight_sems,
        out_sems,
        keep_sems,
        send_sems,
    ) = refs[17 + total :]
    hidden = FF // D
    targets = (up, down, proj)
    rows = token.shape[0]
    me = lax.axis_index("dp")
    rank = lax.axis_index("mp")

    def fetch(ref, scratch, n):
        copy = pltpu.make_async_copy(ref, scratch, in_sems.at[n])
        copy.start()
        return copy

    def send(scratch, ref, n):
        copy = pltpu.make_async_copy(scratch, ref, out_sems.at[n])
        copy.start()
        return copy

    gets = [
        fetch(token_hbm, token, 0),
        fetch(mixed_hbm, mixed, 1),
        fetch(log_hbm, logs, 2),
        fetch(cot_hbm, cot, 3),
        fetch(teach_hbm, teach, 4),
    ]
    loads = {0: [], 1: [], 2: []}
    number = 0
    for want in (2, 0, 1):
        for ref, moves in zip(pieces, plan):
            for start, size, which, mask, rank_mask, stride, offset in moves:
                if which != want:
                    continue
                row = canonical_row(me, rank, block, mask, rank_mask, stride, offset)
                copy = pltpu.make_async_copy(
                    ref.at[pl.ds(start, size), :],
                    targets[which].at[pl.ds(row, size), :],
                    weight_sems.at[number],
                )
                copy.start()
                loads[which].append(copy)
                number += 1

    table_row = vector_ref[0:1, :]
    out_bias = vector_ref[1:2, :]
    gain = vector_ref[2:3, :]
    shift = vector_ref[3:4, :]
    down_bias = vector_ref[4:5, :]
    weight = vector_ref[5:6, :]
    gets[0].wait()
    gets[1].wait()
    right[2 * hidden] = mixed[...].astype(low)
    for copy in loads[2]:
        copy.wait()
    state = token[...].astype(full) + table_row + out_bias
    state = state + dot_of(right[2 * hidden], proj[...], 1, 1)
    middle[...] = state
    unit, _ = norm_stats(state)
    second[...] = (unit * gain + shift).astype(low)
    accum[...] = jnp.zeros((rows, D), full)
    for copy in loads[0]:
        copy.wait()
    for copy in loads[1]:
        copy.wait()

    def forward(m, _):
        place = pl.ds(pl.multiple_of(m * D, D), D)
        half = rows // 2
        spans = [pl.ds(part * half, half) for part in range(2)]
        values = [
            dot_of(second[span, :], up[place, :], 1, 0) + vector_ref[pl.ds(8 + m, 1), :]
            for span in spans
        ]
        for span, value in zip(spans, values):
            cumulative = 0.5 + 0.5 * lax.erf(value * (0.5**0.5))
            active = (value * cumulative).astype(low)
            right[m, span, :] = active
            slope[m, span, :] = (
                cumulative + value * jnp.exp(-0.5 * value * value) * 0.3989422804014327
            )
            accum[span, :] += dot_of(active, down[place, :], 1, 1)
        return 0

    lax.fori_loop(0, FF // D, forward, 0)
    final_state = middle[...] + accum[...] + down_bias
    out[...] = final_state.astype(low)
    puts = [send(out, out_hbm, 0)]
    gets[3].wait()
    gets[4].wait()
    place = lax.broadcasted_iota(jnp.int32, (rows, 1), 0)
    grads = cot[...].astype(full) + weight * (final_state - teach[...].astype(full))
    grads = jnp.where(place < limit_ref[5], grads, 0.0)
    final[...] = grads
    final_low[...] = grads.astype(low)
    sum_ref[3:4, :] = jnp.sum(grads, axis=0, keepdims=True)
    accum[...] = jnp.zeros((rows, D), full)

    def backward(m, _):
        place = pl.ds(pl.multiple_of(m * D, D), D)
        half = rows // 2
        spans = [pl.ds(part * half, half) for part in range(2)]
        values = [dot_of(final_low[span, :], down[place, :], 1, 0) for span in spans]
        sums = []
        for span, value in zip(spans, values):
            value = (slope[m, span, :] * value).astype(low)
            right[hidden + m, span, :] = value
            sums.append(jnp.sum(value.astype(full), axis=0, keepdims=True))
            accum[span, :] += dot_of(value, up[place, :], 1, 1)
        sum_ref[pl.ds(8 + m, 1), :] = sums[0] + sums[1]
        return 0

    lax.fori_loop(0, FF // D, backward, 0)
    unit, inverse = norm_stats(middle[...])
    second_grad = accum[...]
    sum_ref[0:1, :] = jnp.sum(second_grad * unit, axis=0, keepdims=True)
    sum_ref[1:2, :] = jnp.sum(second_grad, axis=0, keepdims=True)
    scaled = second_grad * gain
    mean_scaled = jnp.mean(scaled, axis=-1, keepdims=True)
    mean_unit = jnp.mean(scaled * unit, axis=-1, keepdims=True)
    total_grad = final[...] + inverse * (scaled - mean_scaled - unit * mean_unit)
    middle[...] = total_grad
    puts.append(send(middle, middle_hbm, 1))
    middle_low[...] = total_grad.astype(low)
    sum_ref[2:3, :] = jnp.sum(total_grad, axis=0, keepdims=True)
    attended_grad = dot_of(middle_low[...], proj[...], 1, 0).astype(low)
    grad[...] = attended_grad
    puts.append(send(grad, grad_hbm, 2))
    gets[2].wait()
    head = lax.broadcasted_iota(jnp.int32, (16, D), 0)
    lane = lax.broadcasted_iota(jnp.int32, (16, D), 1)
    member = jnp.where(lane // HEAD_DIM == head, 1.0, 0.0)
    leader = jnp.where(lane == head * HEAD_DIM, 1.0, 0.0)
    exact = functools.partial(
        lax.dot_general,
        dimension_numbers=(((1,), (1,)), ((), ())),
        precision=lax.Precision.HIGHEST,
        preferred_element_type=full,
    )
    deltas = exact(member, attended_grad.astype(full) * mixed[...])
    tops = exact(leader, logs[...])
    for pair in range(PAIRS):
        delta_ref[pair] = deltas[2 * pair : 2 * pair + 2]
        log_ref[pair] = tops[2 * pair : 2 * pair + 2]
    turned[0] = final_low[...].T
    turned[1] = second[...].T
    turned[2] = middle_low[...].T

    def weights(i, _):
        half = D // 2
        values = [
            dot_of(turned[i // hidden, part * half : (part + 1) * half, :], right[i], 1, 0)
            for part in range(2)
        ]
        for part, value in enumerate(values):
            store_split(value, stage_keep, stage_send, i, part * stage_keep.shape[1] // 2)

        @pl.when(i < hidden)
        def _():
            pltpu.make_async_copy(stage_keep.at[i], down_keep.at[i], keep_sems.at[i]).start()
            pltpu.make_async_copy(stage_send.at[i], down_send.at[i], send_sems.at[i]).start()

        @pl.when(i >= hidden)
        def _():
            row = i - hidden
            pltpu.make_async_copy(stage_keep.at[i], up_keep.at[row], keep_sems.at[i]).start()
            pltpu.make_async_copy(stage_send.at[i], up_send.at[row], send_sems.at[i]).start()

        return 0

    lax.fori_loop(0, 2 * hidden + 1, weights, 0)
    for copy in puts:
        copy.wait()
    for i in range(2 * hidden + 1):
        if i < hidden:
            keep, gone, row = down_keep, down_send, i
        else:
            keep, gone, row = up_keep, up_send, i - hidden
        pltpu.make_async_copy(stage_keep.at[i], keep.at[row], keep_sems.at[i]).wait()
        pltpu.make_async_copy(stage_send.at[i], gone.at[row], send_sems.at[i]).wait()


def middle_call(limit, vectors, tokens, mixed, logs, cot, teach, arrays, plan, block, dp):
    rows = tokens.shape[0]
    hidden = FF // D
    narrow = jax.ShapeDtypeStruct((rows, D), low)
    wide = jax.ShapeDtypeStruct((rows, D), full)
    shape = (dp // 2, D // dp, D)
    parts = [jax.ShapeDtypeStruct((count,) + shape, low) for count in (hidden, hidden + 1)]
    stats = jax.ShapeDtypeStruct((PAIRS, 2, rows), full)
    anywhere = pl.BlockSpec(memory_space=pl.ANY)
    inside = pl.BlockSpec(memory_space=pltpu.VMEM)
    moves = sum(len(part) for part in plan)
    return pl.pallas_call(
        functools.partial(middle_kernel, plan, block, len(arrays)),
        out_shape=(
            narrow,
            wide,
            narrow,
            parts[0],
            parts[0],
            parts[1],
            parts[1],
            stats,
            stats,
            jax.ShapeDtypeStruct((8 + 8, D), full),
        ),
        in_specs=[pl.BlockSpec(memory_space=pltpu.SMEM), inside]
        + [anywhere] * (5 + len(arrays)),
        out_specs=[anywhere] * 7 + [inside] * 3,
        scratch_shapes=[
            pltpu.VMEM((rows, D), low),
            pltpu.VMEM((rows, D), full),
            pltpu.VMEM((rows, D), full),
            pltpu.VMEM((rows, D), low),
            pltpu.VMEM((rows, D), low),
            pltpu.VMEM((FF, D), low),
            pltpu.VMEM((FF, D), low),
            pltpu.VMEM((D, D), low),
            pltpu.VMEM((2 * hidden + 1, rows, D), low),
            pltpu.VMEM((hidden, rows, D), full),
            pltpu.VMEM((rows, D), low),
            pltpu.VMEM((rows, D), full),
            pltpu.VMEM((rows, D), full),
            pltpu.VMEM((rows, D), low),
            pltpu.VMEM((rows, D), low),
            pltpu.VMEM((rows, D), low),
            pltpu.VMEM((rows, D), low),
            pltpu.VMEM((rows, D), full),
            pltpu.VMEM((3, D, rows), low),
            pltpu.VMEM((2 * hidden + 1,) + shape, low),
            pltpu.VMEM((2 * hidden + 1,) + shape, low),
            pltpu.SemaphoreType.DMA((5,)),
            pltpu.SemaphoreType.DMA((moves,)),
            pltpu.SemaphoreType.DMA((3,)),
            pltpu.SemaphoreType.DMA((2 * hidden + 1,)),
            pltpu.SemaphoreType.DMA((2 * hidden + 1,)),
        ],
        compiler_params=pltpu.CompilerParams(vmem_limit_bytes=VMEM_LIMIT),
        cost_estimate=SMALL_COST,
        name="middle",
    )(limit, vectors, tokens, mixed, logs, cot, teach, *arrays)


def fold_block(keep, got, out_keep, out_send, bit, place):
    step = 1 << place
    mine = (lax.axis_index("dp") // bit) % 2 * step
    for j in range(keep.shape[1] // 2):
        base = (j // step) * 2 * step + j % step
        for out, shift in ((out_keep, mine), (out_send, step - mine)):
            value = keep[0, base + shift].astype(full) + got[0, base + shift].astype(full)
            out[0, j] = value.astype(low)


def fold_kernel(bits, places, *refs):
    count = len(bits)
    for n in range(count):
        fold_block(
            *refs[2 * n : 2 * n + 2],
            *refs[2 * count + 2 * n : 2 * count + 2 * n + 2],
            bits[n],
            places[n],
        )


def fold(pairs, bits, places):
    lead = pairs[0][0].shape[0]
    block = lambda shape: pl.BlockSpec((1,) + shape[1:], lambda i: (i, 0, 0, 0))
    halves = [
        (keep.shape[0], keep.shape[1] // 2) + keep.shape[2:] for keep, _ in pairs for _ in range(2)
    ]
    outs = pl.pallas_call(
        functools.partial(fold_kernel, bits, places),
        out_shape=[jax.ShapeDtypeStruct(shape, low) for shape in halves],
        grid=(lead,),
        in_specs=[block(value.shape) for pair in pairs for value in pair],
        out_specs=[block(shape) for shape in halves],
        compiler_params=pltpu.CompilerParams(vmem_limit_bytes=VMEM_LIMIT),
        cost_estimate=pl.CostEstimate(flops=0, bytes_accessed=16 << 20, transcendentals=0),
        name="fold",
    )(*[value for pair in pairs for value in pair])
    return [(outs[2 * n], outs[2 * n + 1]) for n in range(len(pairs))]


def qkv_grad_kernel(count, *refs):
    sources = refs[: 3 * count + 1]
    outs = refs[3 * count + 1 : 3 * count + 5]
    sum_ref, held, turned, total, stage, in_sems, out_sems = refs[3 * count + 5 :]
    first_use = [0, count] + list(range(1, count)) + list(range(count + 1, 3 * count + 1))
    for n in first_use:
        pltpu.make_async_copy(sources[n], held.at[n], in_sems.at[n]).start()

    def wait(n):
        pltpu.make_async_copy(sources[0], held.at[n], in_sems.at[n]).wait()

    def turn(n, _):
        wait(n)
        turned[n] = held[n].T
        return 0

    lax.fori_loop(0, count, turn, 0)
    sum_ref[...] = jnp.zeros_like(sum_ref)

    def step(i, _):
        c = (i + count - 1) // count
        n = jnp.where(i == 0, 0, (i + count - 1) % count)
        wait(count + i)
        right = held[count + i]
        value = dot_of(turned[n], right, 1, 0)
        total[...] = value + jnp.where(n == 0, jnp.zeros_like(value), total[...])

        @pl.when(c != 1)
        def _():
            row = pl.ds(pl.multiple_of(c * 4, 8), 1)
            sum_ref[row, :] += jnp.sum(right.astype(full), axis=0, keepdims=True)

        @pl.when(i % count == 0)
        def _():
            for part in range(2):
                store_split(
                    total[:, part * D // 2 : (part + 1) * D // 2],
                    stage.at[part],
                    stage.at[2 + part],
                    c,
                )
            for k in range(4):
                pltpu.make_async_copy(
                    stage.at[k, c], outs[k].at[c], out_sems.at[k * 3 + c]
                ).start()

        return 0

    lax.fori_loop(0, 2 * count + 1, step, 0)
    for k in range(4):
        for c in range(3):
            pltpu.make_async_copy(stage.at[k, c], outs[k].at[c], out_sems.at[k * 3 + c]).wait()


def qkv_grads(chunks, query_grad, key_grads, value_grads, dp):
    rows = query_grad.shape[0]
    count = len(chunks)
    shape = (3, dp // 2, D // dp, D // 2)
    anywhere = pl.BlockSpec(memory_space=pl.ANY)
    return pl.pallas_call(
        functools.partial(qkv_grad_kernel, count),
        out_shape=[jax.ShapeDtypeStruct(shape, low)] * 4
        + [jax.ShapeDtypeStruct((16, D), full)],
        in_specs=[anywhere] * (3 * count + 1),
        out_specs=[anywhere] * 4 + [pl.BlockSpec(memory_space=pltpu.VMEM)],
        scratch_shapes=[
            pltpu.VMEM((3 * count + 1, rows, D), low),
            pltpu.VMEM((count, D, rows), low),
            pltpu.VMEM((D, D), full),
            pltpu.VMEM((4,) + shape, low),
            pltpu.SemaphoreType.DMA((3 * count + 1,)),
            pltpu.SemaphoreType.DMA((12,)),
        ],
        compiler_params=pltpu.CompilerParams(vmem_limit_bytes=VMEM_LIMIT),
        cost_estimate=SMALL_COST,
        name="qkv_grads",
    )(*chunks, query_grad, *key_grads, *value_grads)


def last_kernel(
    token_ref,
    first_ref,
    right_ref,
    left_ref,
    middle_ref,
    vector_ref,
    gain_ref,
    bias_ref,
    sum_ref,
    out_ref,
    pack_ref,
):
    @pl.when(pl.program_id(0) == 0)
    def _():
        pack_ref[...] = jnp.zeros_like(pack_ref)
        pack_ref[1:2, :] = sum_ref[0:1, :]
        pack_ref[3:4, :] = sum_ref[1:2, :]
        pack_ref[4:5, :] = bias_ref[0:1, :]
        pack_ref[5:6, :] = bias_ref[8:9, :]
        pack_ref[6:8, :] = sum_ref[2:4, :]
        pack_ref[8 : 8 + FF // D, :] = sum_ref[8 : 8 + FF // D, :]

    unit, inverse = norm_stats(token_ref[...].astype(full) + vector_ref[0:1, :])
    grad = first_ref[...] + right_ref[...].astype(full) + left_ref[...].astype(full)
    scaled = grad * gain_ref[0:1, :]
    mean_scaled = jnp.mean(scaled, axis=-1, keepdims=True)
    mean_unit = jnp.mean(scaled * unit, axis=-1, keepdims=True)
    result = middle_ref[...] + inverse * (scaled - mean_scaled - unit * mean_unit)
    out_ref[...] = result
    pack_ref[0:1, :] += jnp.sum(grad * unit, axis=0, keepdims=True)
    pack_ref[2:3, :] += jnp.sum(grad, axis=0, keepdims=True)
    pack_ref[pl.ds(16 + lax.axis_index("dp"), 1), :] += jnp.sum(result, axis=0, keepdims=True)


def last_norm(tokens, first, right, left, middle_grad, vectors, gains, bias_sums, sums, dp):
    rows = tokens.shape[0]
    part = pl.BlockSpec((rows // 4, D), lambda i: (i, 0))
    whole = lambda value: pl.BlockSpec(value.shape, lambda i: (0, 0))
    small = (vectors, gains, bias_sums, sums)
    return pl.pallas_call(
        last_kernel,
        out_shape=(
            jax.ShapeDtypeStruct((rows, D), full),
            jax.ShapeDtypeStruct((16 + dp, D), full),
        ),
        grid=(4,),
        in_specs=[part] * 5 + [whole(value) for value in small],
        out_specs=[part, pl.BlockSpec((16 + dp, D), lambda i: (0, 0))],
        compiler_params=pltpu.CompilerParams(vmem_limit_bytes=VMEM_LIMIT),
        cost_estimate=SMALL_COST,
        name="last_norm",
    )(tokens, first, right, left, middle_grad, *small)


def two_parts(value, axis, mine):
    keep = lax.dynamic_index_in_dim(value, mine, axis, keepdims=False)
    send = lax.dynamic_index_in_dim(value, 1 - mine, axis, keepdims=False)
    return keep, send.astype(low)


class Scatter:
    def __init__(self, parts, turns):
        self.bits = outer_bits()
        half = len(self.bits) // 2
        self.orders = [
            [1] + self.bits[half * (turn % 2) :] + self.bits[: half * (turn % 2)] for turn in turns
        ]
        self.left = [list(self.bits) for _ in turns]
        self.step = 0
        self.parts = parts

    def sends(self):
        return [send for _, send in self.parts]

    def exchange(self, sends):
        self.pairs = [
            (keep, swap(send, "dp", turn[self.step]))
            for (keep, _), send, turn in zip(self.parts, sends, self.orders)
        ]
        self.step += 1

    def folds(self):
        if self.step > len(self.bits):
            return [], [], []
        bits = [turn[self.step] for turn in self.orders]
        places = []
        for left, bit in zip(self.left, bits):
            places.append(left.index(bit))
            left.remove(bit)
        return self.pairs, bits, places

    def give(self, outs):
        self.parts = [(outs[n], outs[n + 1]) for n in range(0, len(outs), 2)]

    def fold(self):
        outs = []
        for pair, bit, at in zip(*self.folds()):
            outs += fold([pair], [bit], [at])[0]
        self.give(outs)

    def advance(self, order):
        sends = order(*self.sends())
        self.exchange(list(sends) if len(self.parts) > 1 else [sends])

    def finish(self, order):
        while self.step <= len(self.bits):
            self.fold()
            self.advance(order)
        got = order(*[other for _, other in self.pairs])
        return [
            (keep.astype(full) + other.astype(full))[:, 0]
            for (keep, _), other in zip(self.pairs, got)
        ]


def scatter_dp(parts, turns):
    scatter = Scatter(parts, turns)
    while True:
        sends = yield scatter.sends()
        scatter.exchange(sends)
        if scatter.step > len(scatter.bits):
            break
        scatter.parts = fold(*scatter.folds())
    got = yield [other for _, other in scatter.pairs]
    return [
        (keep.astype(full) + other.astype(full))[:, 0]
        for (keep, _), other in zip(scatter.pairs, got)
    ]


def scatter_mp(value):
    rank = lax.axis_index("mp")
    part = lambda index: lax.dynamic_index_in_dim(value, index, keepdims=False)
    sends = yield [part(rank ^ bit).astype(low) for bit in (1, 2, 3)]
    got = yield [swap(send, "mp", bit) for bit, send in zip((1, 2, 3), sends)]
    got = [other.astype(full) for other in got]
    return (part(rank) + got[0]) + (got[1] + got[2])


def halve_mp(value):
    rank = lax.axis_index("mp")
    pairs = value.reshape((2, 2) + value.shape[1:])
    keep, send = two_parts(pairs, 1, rank % 2)
    (send,) = yield [send]
    (got,) = yield [swap(send, "mp", 1)]
    keep, send = two_parts(keep.astype(full) + got.astype(full), 0, rank // 2)
    (send,) = yield [send]
    (got,) = yield [swap(send, "mp", 2)]
    return keep + got.astype(full)


def scatter_feed(up_own, down_own):
    mp = lax.axis_size("mp")
    block = down_own.shape[1]
    out_own = up_own[mp].reshape(block, mp, -1).transpose(1, 0, 2)
    own = yield from halve_mp(
        jnp.concatenate([up_own[:mp], down_own, out_own.reshape(mp, -1, D)], axis=1)
    )
    return own[:block], own[block : 2 * block].T, own[2 * block :].reshape(block, -1).T


def scatter_qkv(keep_left, keep_right, send_left, send_right):
    left_part, right_part = yield from scatter_dp(
        [(keep_left, send_left), (keep_right, send_right)], (0, 1)
    )
    width = D // lax.axis_size("mp")
    parts = [part[..., at : at + width] for part in (left_part, right_part) for at in (0, width)]
    return (yield from scatter_mp(jnp.stack(parts)))


def sum_small(value):
    (value,) = yield [value]
    value = value + swap(value, "dp", 1)
    bits = outer_bits()
    groups = [("dp", bits[n : n + 2]) for n in range(0, len(bits), 2)] + [("mp", [1, 2])]
    for axis, pair in groups:
        (value,) = yield [value]
        if len(pair) == 1:
            value = value + swap(value, axis, pair[0])
        else:
            one, two = pair
            got = [swap(value, axis, mask) for mask in (one, two, one + two)]
            if axis == "mp":
                got = yield got
            value = (value + got[0]) + (got[1] + got[2])
    return value


class Steps:
    def __init__(self, steps):
        self.steps = steps
        self.pending = next(steps)
        self.result = None

    def advance(self, order):
        if self.pending is None:
            return
        sends = order(*self.pending)
        sends = [sends] if len(self.pending) == 1 else list(sends)
        try:
            self.pending = self.steps.send(sends)
        except StopIteration as stop:
            self.pending = None
            self.result = stop.value

    def finish(self, order):
        while self.pending is not None:
            self.advance(order)
        return self.result


def shards(
    tokens_in,
    timesteps,
    lengths,
    time_table,
    norm_gains,
    norm_biases,
    w_qkv,
    qv_bias,
    w_out,
    out_bias,
    w_up,
    up_bias,
    w_down,
    down_bias,
    cotangent,
    teacher,
):
    rank = lax.axis_index("mp")
    data_rank = lax.axis_index("dp")
    mp = lax.axis_size("mp")
    dp = lax.axis_size("dp")
    own_rows = tokens_in.shape[0]
    length = lax.dynamic_index_in_dim(lengths, data_rank, keepdims=False)
    own_time = lax.dynamic_index_in_dim(timesteps, data_rank, keepdims=False)
    odd = rank % 2 == 1
    upper = rank >= 2
    middle = jnp.logical_or(rank == 1, rank == 2)
    order = Order()
    along = lambda value, pairs: lax.ppermute(value, "mp", pairs)

    block = w_qkv.shape[1]
    aligned = block % 32 == 0
    narrow = order(jnp.concatenate([w_qkv.reshape(3 * block, -1), w_out.T]))
    first_swap = swap(narrow, "mp", 1)
    tall = order(jnp.concatenate([w_up, w_down.T]))
    tall_swap = swap(tall, "mp", 1)
    pair = order(
        jnp.concatenate(
            [jnp.where(odd, first_swap, narrow), jnp.where(odd, narrow, first_swap)], axis=1
        )
    )
    second_swap = swap(pair, "mp", 2)
    tokens, lengths, own_time, norm_gains, norm_biases, out_bias, down_bias, up_bias, length = order(
        tokens_in, lengths, own_time, norm_gains, norm_biases, out_bias, down_bias, up_bias, length
    )
    table_row = lax.dynamic_slice_in_dim(time_table, own_time, 1).astype(full)
    unit_one, _ = norm_stats(tokens.astype(full) + table_row)
    first_norm = (unit_one * norm_gains[0] + norm_biases[0]).astype(low)
    loss_weight = lengths.shape[0] * MAXLEN / jnp.sum(lengths).astype(full)
    vectors = jnp.concatenate(
        [
            table_row,
            out_bias[None],
            norm_gains[1:2],
            norm_biases[1:2],
            down_bias[None],
            jnp.full((3, D), loss_weight),
            up_bias.reshape(-1, D),
            jnp.zeros((4, D), full),
        ]
    )
    scalars = jnp.stack(
        [
            rank,
            jnp.where(rank == 0, 1, rank - 1),
            jnp.where(upper, rank - 2, rank + 2),
            jnp.where(middle, rank + 1, 3 - rank),
            length,
            length - rank * own_rows,
        ]
    ).astype(jnp.int32)
    first_norm, vectors, scalars = order(first_norm, vectors, scalars)
    wide = jnp.concatenate(
        [jnp.where(upper, second_swap, pair), jnp.where(upper, pair, second_swap)], axis=1
    )
    qkv_rows, out_rows = wide[: 3 * block], wide[3 * block :]
    if aligned:
        split = 3 * block // 2
        qkv_gather = Gather([qkv_rows[:split], qkv_rows[split:]])
        qkv_gather.advance(order)
    tall = order(jnp.concatenate([tall, tall_swap]))
    tall_across = along(tall, [(1, 2), (2, 1)])

    sent = order(first_norm)
    from_left = along(sent, [(0, 1), (1, 2), (2, 3)])
    from_right = along(sent, [(1, 0), (2, 1), (3, 2)])
    tall_across = order(tall_across)
    tall_far = along(tall_across, [(1, 0), (2, 3)])
    if aligned:
        while qkv_gather.step < len(qkv_gather.bits):
            qkv_gather.advance(order)
        qkv_gather.advance(order)
    hop_right, hop_left = order(from_left, from_right)
    second_right = along(hop_right, [(1, 2), (2, 3)])
    second_left = along(hop_left, [(1, 0), (2, 1)])
    if aligned:
        arrays, plan = plan_of(
            qkv_gather.result,
            [
                [(0, block, 0, 0, 0, 0), (block, split - block, 1, 0, 0, 0)],
                [
                    (0, 2 * block - split, 1, 0, 0, split - block),
                    (2 * block - split, block, 1, 1, 0, 0),
                ],
            ],
        )
        query_weight, pair_weight = order(*place(arrays, plan, block, [(D, D), (D, 2 * D)]))
        tall_other = jnp.where(middle, tall_across, order(tall_far))
        feed_gather = Gather(
            [
                jnp.concatenate([tall, out_rows[: block // 2]]),
                jnp.concatenate([tall_other, out_rows[block // 2 :]]),
            ]
        )
        feed_gather.advance(order)
    else:
        weights = lax.all_gather(qkv_rows.reshape(3, block, D), "dp", axis=1, tiled=True)
        query_weight = weights[0]
        pair_weight = jnp.concatenate([weights[1], weights[2]], axis=1)
    near = jnp.where(rank == 0, hop_left, hop_right)
    attend = lambda parts, numbers, carried: order(
        *attend_forward(
            parts,
            numbers,
            scalars,
            query_weight,
            pair_weight,
            qv_bias[0:1],
            qv_bias[1:2],
            carried,
        )
    )
    key_own, value_own, queries, *state = attend([order(first_norm)], (0,), None)
    second_right, second_left = order(second_right, second_left)
    second = order(jnp.where(upper, second_right, second_left))
    third = along(second, [(1, 0), (2, 3)])
    if aligned:
        while feed_gather.step < len(feed_gather.bits):
            feed_gather.advance(order)
        feed_gather.send_early(order)
    near, second = order(near, second)
    key_near, key_second, value_near, value_second, *state = attend(
        [near, second], (1, 2), (queries, *state)
    )
    last = order(jnp.where(middle, hop_left, order(third)))
    key_last, value_last, mixed, logs = attend([order(last)], (3,), (queries, *state))
    if aligned:
        feed_gather.advance(order)
        layout = lambda masks, shift: [
            (0, block, 0, masks[0], D, 0),
            (block, block, 1, masks[0], D, 0),
            (2 * block, block, 0, masks[1], D, 0),
            (3 * block, block, 1, masks[1], D, 0),
            (4 * block, block // 2, 2, 0, 0, shift),
        ]
        arrays, plan = plan_of(
            feed_gather.result, [layout((0, 1), 0), layout((2, 3), block // 2)]
        )
    else:
        arrays = [
            lax.all_gather(w_up, ("mp", "dp"), axis=0, tiled=True),
            lax.all_gather(w_down.T, ("mp", "dp"), axis=0, tiled=True),
            lax.all_gather(out_rows, "dp", axis=0, tiled=True),
        ]
        plan = [[(0, array.shape[0], n, None, 0, 0, 0)] for n, array in enumerate(arrays)]
    chunks = [first_norm, near, second, last]
    keys = [key_own, key_near, key_second, key_last]
    values = [value_own, value_near, value_second, value_last]

    output, middle_grad, attended_grad, *parts, deltas, log_rows, sums = middle_call(
        scalars, vectors, tokens, mixed, logs, cotangent, teacher, arrays, plan, block, dp
    )
    scatter = Scatter([(parts[0], parts[1]), (parts[2], parts[3])], (1, 0))
    scatter.advance(order)

    key_grads = [None] * 4
    value_grads = [None] * 4
    firsts = [None] * 4
    query_grad = None
    for n in (3, 2, 1, 0):
        pairs, bits, places = scatter.folds() if n % 2 == 0 else ([], [], [])
        query_grad, key_grads[n], value_grads[n], firsts[n], *folded = attend_backward(
            n,
            queries,
            keys[n],
            values[n],
            order(attended_grad),
            log_rows,
            deltas,
            query_weight,
            pair_weight,
            scalars,
            query_grad,
            n == 0,
            pairs,
            bits,
            places,
        )
        firsts[n] = order(firsts[n])
        if folded:
            scatter.give(folded)
        if n == 3:
            back_last = along(firsts[3], [(0, 1), (3, 2)]).astype(full)
        elif n == 2:
            scatter.advance(order)
            payload = order((firsts[2] + back_last).astype(low))
            back_right = along(payload, [(0, 1), (1, 2)]).astype(full)
            back_left = along(payload, [(3, 2), (2, 1)]).astype(full)
        elif n == 1:
            to_right = jnp.where(
                rank == 0, firsts[1], firsts[3].astype(full) + back_right
            ).astype(low)
            to_left = (firsts[1] + back_left).astype(low)
            to_right, to_left = order(to_right, to_left)
            final_right = along(to_right, [(0, 1), (1, 2), (2, 3)])
            final_left = along(to_left, [(3, 2), (2, 1), (1, 0)])
    scatter.advance(order)
    query_grad, final_right, final_left = order(query_grad, final_right, final_left)
    *halves, bias_sums = qkv_grads(chunks, query_grad, key_grads, value_grads, dp)
    qkv = Steps(scatter_qkv(*halves))
    qkv.advance(order)
    down_own, up_own = scatter.finish(order)
    feed = Steps(scatter_feed(up_own, down_own))
    feed.advance(order)
    qkv.advance(order)
    tokens, first_own = order(tokens, firsts[0])
    input_grad, packed = last_norm(
        tokens,
        first_own,
        final_right,
        final_left,
        middle_grad,
        vectors,
        norm_gains,
        bias_sums,
        sums,
        dp,
    )
    packed, input_grad = order(packed, input_grad)
    small = Steps(sum_small(packed))
    feed.advance(order)
    feed.advance(order)
    small.advance(order)
    qkv.advance(order)
    feed.advance(order)
    qkv.advance(order)
    small.advance(order)
    qkv.advance(order)
    small.advance(order)
    total = small.finish(order)
    up_grad, down_grad, out_grad = feed.finish(order)
    qkv_grad = qkv.finish(order)
    fixed = 16
    chosen = (timesteps[None, :] == jnp.arange(time_table.shape[0])[:, None]).astype(full)
    table_grad = lax.dot_general(
        chosen,
        total[fixed:],
        (((1,), (0,)), ((), ())),
        precision=lax.Precision.HIGHEST,
        preferred_element_type=full,
    )
    return (
        output,
        input_grad,
        table_grad,
        total[0:2],
        total[2:4],
        qkv_grad,
        total[4:6],
        out_grad,
        total[6],
        up_grad,
        total[8 : 8 + FF // D].reshape(FF),
        down_grad,
        total[7],
    )


def solution(mesh):
    rows = P(both, None)
    placed = (
        rows,
        P(),
        P(),
        P(),
        P(),
        P(),
        P(None, "dp", "mp"),
        P(),
        P("mp", "dp"),
        P(),
        P("dp", "mp"),
        P(),
        P("mp", "dp"),
        P(),
        rows,
        rows,
    )
    return jax.shard_map(
        shards,
        mesh=mesh,
        in_specs=placed,
        out_specs=(
            rows,
            rows,
            P(),
            P(),
            P(),
            P(None, "dp", "mp"),
            P(),
            P("mp", "dp"),
            P(),
            P("dp", "mp"),
            P(),
            P("mp", "dp"),
            P(),
        ),
        check_vma=False,
    )
```
